32 devices in a mesh: dp: 4 (over y, core), ctx: 8 (over z, x).
Axes of the slice: x: 2, y: 2, z: 4, core: 2. Of those that a mesh axis runs over, the one named last changes fastest.
Arguments:
- tokens: bfloat16 [8192, 2048], P(('dp', 'ctx')), may hold values from -6 to 6
- lengths: int32 [4, 3], P('dp'), may hold values from 1 to 1536, 2048 in all within a row
- w_qkv: float32 [2048, 6144], P(('dp', 'ctx')), may hold values from -0.125 to 0.125
- b_qkv: float32 [6144], P(('dp', 'ctx')), may hold values from -1.8 to 1.8
- w_out: float32 [2048, 2048], P(('dp', 'ctx')), may hold values from -0.5 to 0.5
- b_out: float32 [2048], P(('dp', 'ctx')), may hold values from -1.8 to 1.8
- w_fc1: float32 [2048, 8192], P(('dp', 'ctx')), may hold values from -0.125 to 0.125
- b_fc1: float32 [8192], P(('dp', 'ctx')), may hold values from -1.8 to 1.8
- w_fc2: float32 [8192, 2048], P(('dp', 'ctx')), may hold values from -0.0625 to 0.0625
- b_fc2: float32 [2048], P(('dp', 'ctx')), may hold values from -1.8 to 1.8
- ln_gain: float32 [2048], P(('dp', 'ctx')), may hold values from 0.5 to 1.5
- ln_shift: float32 [2048], P(('dp', 'ctx')), may hold values from -1.8 to 1.8
- cotangent: bfloat16 [8192, 2048], P(('dp', 'ctx')), may hold values from -6 to 6
Outputs:
- block_out: bfloat16 [8192, 2048], P(('dp', 'ctx'))
- grad_tokens: bfloat16 [8192, 2048], P(('dp', 'ctx'))
- grad_w_qkv: float32 [2048, 6144], P(('dp', 'ctx'))
- grad_b_qkv: float32 [6144], P(('dp', 'ctx'))
- grad_w_out: float32 [2048, 2048], P(('dp', 'ctx'))
- grad_b_out: float32 [2048], P(('dp', 'ctx'))
- grad_w_fc1: float32 [2048, 8192], P(('dp', 'ctx'))
- grad_b_fc1: float32 [8192], P(('dp', 'ctx'))
- grad_w_fc2: float32 [8192, 2048], P(('dp', 'ctx'))
- grad_b_fc2: float32 [2048], P(('dp', 'ctx'))
- grad_ln_gain: float32 [2048], P(('dp', 'ctx'))
- grad_ln_shift: float32 [2048], P(('dp', 'ctx'))
The draws below stay inside these ranges and needn't reach their ends.
Inputs may be any that keep to these rules, and one draw needn't show every extreme that they name: Each row holds the lengths of the sequences of one group in order; they sum to 2048 and the longest is exactly 1536.
All inputs are finite; a program needn't handle non-finite values.
Results may differ from the reference program's by a relative error of at most 0.014.
Values may be sent and summed in bfloat16 or wider, within the bound.
A program may use at most 256 MiB of HBM per device.

```python
import math
import jax
import jax.numpy as jnp
import numpy as np
from jax import lax

D = 2048
HEADS = 32
HEAD_DIM = 64
ROT = 32
FF = 8192
GROUP_TOK = 2048
TOKENS = 8192
MAXLEN = 1536
SEQS = 3
N_DP = 4


def steps_of(own_key, dims, cuts, low, top_value):
    def one(axis_at, shards_of):
        steps = jax.random.uniform(jax.random.fold_in(jax.random.fold_in(own_key, 6), axis_at), (shards_of,), jnp.float32, low / len(cuts), top_value / len(cuts))
        return jnp.repeat(jnp.exp(steps), dims[axis_at] // shards_of).reshape((-1,) + (1,) * (len(dims) - axis_at - 1))

    loudness = one(*cuts[0])
    for cut in cuts[1:]:
        loudness = loudness * one(*cut)
    return loudness


def split_up(count, total, bound, lean):
    portions = [(1 << 20) // math.isqrt(standing ** lean) + 1 for standing in range(2, count + 1)]
    surplus, given = total - bound - (count - 1), [1] * (count - 1)
    while surplus > 0:
        movable = [i for i in range(count - 1) if given[i] < bound]
        pool, remaining = sum([portions[i] for i in movable]), surplus
        for i in movable:
            addition = min(bound - given[i], max(1, remaining * portions[i] // pool), surplus)
            given[i] = given[i] + addition
            surplus = surplus - addition
    return np.array([bound] + given)


def uneven_parts(stream_key, count, total, bound, slope):
    if count == 2:
        one = jax.random.randint(stream_key, (), max(1, total - bound), min(bound, total - 1) + 1)
        return jnp.stack([one, total - one])
    sizes = jnp.asarray(split_up(count, total, bound, slope), jnp.int32)
    twos = (count - 1) // 2
    giver, taker = sizes[1:1 + 2 * twos:2], sizes[2:2 + 2 * twos:2]
    margin = jnp.minimum(giver - 1, bound - taker)
    shifted = jax.random.randint(jax.random.fold_in(stream_key, 1), (twos,), 0, 1 << 20) % (margin + 1)
    sizes = sizes.at[1:1 + 2 * twos:2].set(giver - shifted).at[2:2 + 2 * twos:2].set(taker + shifted)
    return sizes[jax.random.permutation(jax.random.fold_in(stream_key, 2), count)]


def scatter_about(key, shape, scale, limit, shards=(), kind=jnp.bfloat16):
    entries = scale * jax.random.normal(key, shape, jnp.float32)
    if shards:
        entries = entries * steps_of(key, shape, shards, -0.22, 0.18)
    return jnp.clip(entries, -limit, limit).astype(kind)


def setup_inputs(seed: int = 0) -> dict:
    seeds = jax.random.split(jax.random.key(seed), 14)
    return {
        "tokens": scatter_about(seeds[0], (TOKENS, D), 1.0, 6.0, ((0, 32),)),
        "lengths": jax.vmap(lambda own: uneven_parts(own, SEQS, GROUP_TOK, MAXLEN, 0))(jax.random.split(seeds[1], N_DP)).reshape((N_DP, SEQS)).astype(jnp.int32),
        "w_qkv": scatter_about(seeds[2], (D, 3 * D), D ** -0.5, 0.125, ((0, 32),), jnp.float32),
        "b_qkv": scatter_about(seeds[3], (3 * D,), 0.3, 1.8, ((0, 32),), jnp.float32),
        "w_out": scatter_about(seeds[4], (D, D), (D // 16) ** -0.5, 0.5, ((0, 32),), jnp.float32),
        "b_out": scatter_about(seeds[5], (D,), 0.3, 1.8, ((0, 32),), jnp.float32),
        "w_fc1": scatter_about(seeds[6], (D, FF), D ** -0.5, 0.125, ((0, 32),), jnp.float32),
        "b_fc1": scatter_about(seeds[7], (FF,), 0.3, 1.8, ((0, 32),), jnp.float32),
        "w_fc2": scatter_about(seeds[8], (FF, D), FF ** -0.5, 0.0625, ((0, 32),), jnp.float32),
        "b_fc2": scatter_about(seeds[9], (D,), 0.3, 1.8, ((0, 32),), jnp.float32),
        "ln_gain": jnp.clip(1.0 + 0.1 * jax.random.normal(seeds[10], (D,), jnp.float32), 0.5, 1.5),
        "ln_shift": scatter_about(seeds[11], (D,), 0.3, 1.8, ((0, 32),), jnp.float32),
        "cotangent": scatter_about(seeds[12], (TOKENS, D), 1.0, 6.0, ((0, 32),)),
    }


EPS = 1e-05
GELU_COEF = math.sqrt(2.0 / math.pi)
NEGATIVE = -1e+30
HIGH = lax.Precision.HIGHEST

@jax.custom_vjp
def low(v):
    return lax.optimization_barrier(v.astype(jnp.bfloat16)).astype(jnp.float32)

@jax.custom_vjp
def low_back(v):
    return v

def low_keep(v):
    return (low(v), None)

def low_pass(kept, grad):
    return (grad,)

def back_keep(v):
    return (v, None)

def back_low(kept, grad):
    return (low(grad),)
low.defvjp(low_keep, low_pass)
low_back.defvjp(back_keep, back_low)

def matmul(left, right):
    return jnp.dot(left, right, precision=HIGH, preferred_element_type=jnp.float32)

def norm_layer(inputs, gain, shift):
    mean = lax.optimization_barrier(jnp.mean(inputs, axis=-1, keepdims=True))
    centred = inputs - mean
    var = lax.optimization_barrier(jnp.mean(centred * centred, axis=-1, keepdims=True))
    return centred * lax.rsqrt(var + EPS) * gain + shift

def gelu_tanh(pre):
    return 0.5 * pre * (1.0 + jnp.tanh(GELU_COEF * (pre + 0.044715 * pre * pre * pre)))

def rotary_tables(positions):
    half = ROT // 2
    freq = jnp.exp(jnp.arange(half, dtype=jnp.float32) * (-2.0 * math.log(10000.0) / ROT))
    angle = positions.astype(jnp.float32)[:, None] * freq[None, :]
    return (jnp.cos(angle)[:, None, :], jnp.sin(angle)[:, None, :])

def rotate(heads, cosine, sine):
    half = ROT // 2
    first = heads[..., :half]
    second = heads[..., half:ROT]
    return jnp.concatenate([first * cosine - second * sine, second * cosine + first * sine, heads[..., ROT:]], axis=-1)

def segments(lengths_row, rows):
    ends = jnp.cumsum(lengths_row).astype(jnp.int32)
    starts = (ends - lengths_row).astype(jnp.int32)
    seg = lax.optimization_barrier(jnp.sum((rows[:, None] >= ends[None, :]).astype(jnp.int32), axis=1)).astype(jnp.int32)
    onehot = seg[:, None] == jnp.arange(lengths_row.shape[0], dtype=jnp.int32)[None, :]
    first_rows = lax.optimization_barrier(jnp.sum(jnp.where(onehot, starts[None, :], 0), axis=1)).astype(jnp.int32)
    return (seg, (rows - first_rows).astype(jnp.int32))

def attend_block(queries, query_seg, query_rows, keys, values, key_seg, key_rows):
    scores = jnp.einsum('ihd,jhd->hij', queries, keys, precision=HIGH) * (1.0 / math.sqrt(HEAD_DIM))
    scores = low_back(scores)
    allowed = (query_seg[:, None] == key_seg[None, :]) & (key_rows[None, :] <= query_rows[:, None])
    scores = jnp.where(allowed[None], scores, NEGATIVE)
    weights = low(jax.nn.softmax(scores, axis=-1))
    return jnp.einsum('hij,jhd->ihd', weights, values, precision=HIGH)

def attention(queries, keys, values, seg):
    width = min(512, GROUP_TOK)
    count = GROUP_TOK // width
    rows = jnp.arange(GROUP_TOK, dtype=jnp.int32)
    block_fn = jax.checkpoint(attend_block)

    def one_group(item):
        group_q, group_k, group_v, group_seg = item

        def one_block(block_item):
            block_q, block_seg, block_rows = block_item
            return block_fn(block_q, block_seg, block_rows, group_k, group_v, group_seg, rows)
        result = lax.map(one_block, (group_q.reshape(count, width, HEADS, HEAD_DIM), group_seg.reshape(count, width), rows.reshape(count, width)))
        return result.reshape(GROUP_TOK, HEADS, HEAD_DIM)
    return lax.map(one_group, (queries, keys, values, seg))

def forward(inputs, seg, cosine, sine, w_qkv, b_qkv, w_out, b_out, w_fc1, b_fc1, w_fc2, b_fc2, ln_gain, ln_shift):
    hidden = low(norm_layer(inputs, low(ln_gain), low(ln_shift)))
    qkv = low_back(matmul(hidden, low(w_qkv)) + low(b_qkv))
    shape = (TOKENS, HEADS, HEAD_DIM)
    queries = low(rotate(qkv[:, :D].reshape(shape), cosine, sine))
    keys = low(rotate(qkv[:, D:2 * D].reshape(shape), cosine, sine))
    values = low(qkv[:, 2 * D:].reshape(shape))
    group_shape = (N_DP, GROUP_TOK, HEADS, HEAD_DIM)
    attended = attention(queries.reshape(group_shape), keys.reshape(group_shape), values.reshape(group_shape), seg)
    attended = low(low_back(attended.reshape(TOKENS, D)))
    attn_out = matmul(attended, low(w_out)) + low(b_out)
    pre = low_back(matmul(hidden, low(w_fc1)) + low(b_fc1))
    act = low(gelu_tanh(pre))
    return inputs + attn_out + matmul(act, low(w_fc2)) + low(b_fc2)

def reference(tokens, lengths, w_qkv, b_qkv, w_out, b_out, w_fc1, b_fc1, w_fc2, b_fc2, ln_gain, ln_shift, cotangent):
    rows = jnp.arange(GROUP_TOK, dtype=jnp.int32)
    seg, positions = jax.vmap(lambda row: segments(row, rows))(lengths)
    cosine, sine = rotary_tables(positions.reshape(TOKENS))

    def run(inputs, p_qkv, p_bqkv, p_out, p_bout, p_fc1, p_bfc1, p_fc2, p_bfc2, p_gain, p_shift):
        return forward(inputs, seg, cosine, sine, p_qkv, p_bqkv, p_out, p_bout, p_fc1, p_bfc1, p_fc2, p_bfc2, p_gain, p_shift)
    result, pull = jax.vjp(run, tokens.astype(jnp.float32), w_qkv, b_qkv, w_out, b_out, w_fc1, b_fc1, w_fc2, b_fc2, ln_gain, ln_shift)
    grads = pull(cotangent.astype(jnp.float32))
    return (result.astype(jnp.bfloat16), grads[0].astype(jnp.bfloat16), grads[1], grads[2], grads[3], grads[4], grads[5], grads[6], grads[7], grads[8], grads[9], grads[10])
```

```python
import math

import jax
import jax.numpy as jnp
from jax import lax
from jax.sharding import PartitionSpec as P

D = 2048
HEADS = 32
HEAD_DIM = 64
ROT = 32
FF = 8192


EPS = 1e-05
GELU_COEF = math.sqrt(2.0 / math.pi)
NEGATIVE = -1e30


def norm_parts(inputs, gain, shift):
    mean = jnp.mean(inputs, axis=-1, keepdims=True)
    centred = inputs - mean
    var = jnp.mean(centred * centred, axis=-1, keepdims=True)
    scaled = lax.rsqrt(var + EPS)
    normed = centred * scaled
    return (normed, scaled, normed * gain + shift)


def norm_back(d_hidden, normed, scaled, gain32):
    grad_gain = jnp.sum(d_hidden * normed, axis=0)
    grad_shift = jnp.sum(d_hidden, axis=0)
    d_normed = d_hidden * gain32
    d_inputs = scaled * (
        d_normed
        - jnp.mean(d_normed, axis=-1, keepdims=True)
        - normed * jnp.mean(d_normed * normed, axis=-1, keepdims=True)
    )
    return (grad_gain, grad_shift, d_inputs)


def gelu_tanh(pre):
    return 0.5 * pre * (1.0 + jnp.tanh(GELU_COEF * (pre + 0.044715 * pre * pre * pre)))


def gelu_slope(pre):
    tangent = jnp.tanh(GELU_COEF * (pre + 0.044715 * pre * pre * pre))
    return 0.5 * (1.0 + tangent) + 0.5 * pre * (1.0 - tangent * tangent) * GELU_COEF * (
        1.0 + 3.0 * 0.044715 * pre * pre
    )


def rotary_tables(positions):
    half = ROT // 2
    freq = jnp.exp(jnp.arange(half, dtype=jnp.float32) * (-2.0 * math.log(10000.0) / ROT))
    angle = positions.astype(jnp.float32)[:, None] * freq[None, :]
    return (jnp.cos(angle)[:, None, :], jnp.sin(angle)[:, None, :])


def rotate(heads, cosine, sine):
    half = ROT // 2
    first = heads[..., :half]
    second = heads[..., half:ROT]
    return jnp.concatenate(
        [first * cosine - second * sine, second * cosine + first * sine, heads[..., ROT:]], axis=-1
    )


def rotate_back(grads, cosine, sine):
    half = ROT // 2
    first = grads[..., :half]
    second = grads[..., half:ROT]
    return jnp.concatenate(
        [first * cosine + second * sine, second * cosine - first * sine, grads[..., ROT:]], axis=-1
    )


def segment_info(lengths_row, rows):
    ends = jnp.cumsum(lengths_row)
    starts = ends - lengths_row
    seg = jnp.sum((rows[:, None] >= ends[None, :]).astype(jnp.int32), axis=1)
    onehot = seg[:, None] == jnp.arange(lengths_row.shape[0], dtype=jnp.int32)[None, :]
    first_rows = jnp.sum(jnp.where(onehot, starts[None, :], 0), axis=1)
    return (seg, rows - first_rows)


def attend_forward(query, key_all, value_all, query_seg, query_rows, key_seg, key_rows, width):
    count = key_all.shape[0] // width
    rows = query.shape[0]
    heads = query.shape[1]
    score_scale = 1.0 / math.sqrt(HEAD_DIM)

    def absorb(carry, item):
        running_max, denominator, weighted = carry
        key_piece, value_piece, seg_piece, row_piece = item
        allowed = (
            (query_seg[:, None] == seg_piece[None, :]) & (row_piece[None, :] <= query_rows[:, None])
        )[None]
        scores = (
            jnp.einsum("ihd,jhd->hij", query, key_piece, preferred_element_type=jnp.float32)
            * score_scale
        )
        scores = jnp.where(allowed, scores, NEGATIVE)
        new_max = jnp.maximum(running_max, jnp.max(scores, axis=2))
        factor = jnp.exp(running_max - new_max)
        weights = jnp.where(allowed, jnp.exp(scores - new_max[:, :, None]), 0.0)
        denominator = denominator * factor + jnp.sum(weights, axis=2)
        weighted = weighted * factor.T[:, :, None] + jnp.einsum(
            "hij,jhd->ihd",
            weights.astype(jnp.bfloat16),
            value_piece,
            preferred_element_type=jnp.float32,
        )
        return ((new_max, denominator, weighted), None)

    start_carry = (
        jnp.full((heads, rows), NEGATIVE, jnp.float32),
        jnp.zeros((heads, rows), jnp.float32),
        jnp.zeros((rows, heads, HEAD_DIM), jnp.float32),
    )
    items = (
        key_all.reshape(count, width, heads, HEAD_DIM),
        value_all.reshape(count, width, heads, HEAD_DIM),
        key_seg.reshape(count, width),
        key_rows.reshape(count, width),
    )
    (running_max, denominator, weighted), _ = lax.scan(absorb, start_carry, items)
    log_total = running_max + jnp.log(denominator)
    return (weighted / denominator.T[:, :, None], log_total)


def attend_backward(
    query,
    d_attended,
    delta,
    log_total,
    key_all,
    value_all,
    query_seg,
    query_rows,
    key_seg,
    key_rows,
    width,
):
    count = key_all.shape[0] // width
    heads = query.shape[1]
    score_scale = 1.0 / math.sqrt(HEAD_DIM)

    def key_step(d_query, item):
        key_block, value_block, seg_block, row_block = item
        allowed = (
            (query_seg[:, None] == seg_block[None, :]) & (row_block[None, :] <= query_rows[:, None])
        )[None]
        scores = (
            jnp.einsum("ihd,jhd->hij", query, key_block, preferred_element_type=jnp.float32)
            * score_scale
        )
        probs = jnp.where(allowed, jnp.exp(scores - log_total[:, :, None]), 0.0)
        d_probs = jnp.einsum(
            "ihd,jhd->hij", d_attended, value_block, preferred_element_type=jnp.float32
        )
        d_scores = (probs * (d_probs - delta[:, :, None])).astype(jnp.bfloat16)
        d_query = (
            d_query
            + jnp.einsum("hij,jhd->ihd", d_scores, key_block, preferred_element_type=jnp.float32)
            * score_scale
        )
        d_key = (
            jnp.einsum("hij,ihd->jhd", d_scores, query, preferred_element_type=jnp.float32)
            * score_scale
        )
        d_value = jnp.einsum(
            "hij,ihd->jhd",
            probs.astype(jnp.bfloat16),
            d_attended,
            preferred_element_type=jnp.float32,
        )
        return (d_query, (d_key, d_value))

    items = (
        key_all.reshape(count, width, heads, HEAD_DIM),
        value_all.reshape(count, width, heads, HEAD_DIM),
        key_seg.reshape(count, width),
        key_rows.reshape(count, width),
    )
    d_query, (key_terms, value_terms) = lax.scan(
        key_step, jnp.zeros(query.shape, jnp.float32), items
    )
    total = key_all.shape[0]
    return (
        d_query,
        key_terms.reshape(total, heads, HEAD_DIM),
        value_terms.reshape(total, heads, HEAD_DIM),
    )


def causal_forward(query, keys, values, seg, rows, width):
    count = query.shape[0] // width
    results = []
    logs = []
    for block in range(count):
        lower = block * width
        upper = lower + width
        result, log_total = attend_forward(
            query[lower:upper],
            keys[:upper],
            values[:upper],
            seg[lower:upper],
            rows[lower:upper],
            seg[:upper],
            rows[:upper],
            width,
        )
        results.append(result)
        logs.append(log_total)
    return (jnp.concatenate(results, axis=0), jnp.concatenate(logs, axis=1))


def causal_backward(query, d_attended, delta, log_total, keys, values, seg, rows, width):
    total = query.shape[0]
    count = total // width
    query_parts = []
    key_sum = jnp.zeros(keys.shape, jnp.float32)
    value_sum = jnp.zeros(values.shape, jnp.float32)
    for block in range(count):
        lower = block * width
        upper = lower + width
        d_query, key_terms, value_terms = attend_backward(
            query[lower:upper],
            d_attended[lower:upper],
            delta[:, lower:upper],
            log_total[:, lower:upper],
            keys[:upper],
            values[:upper],
            seg[lower:upper],
            rows[lower:upper],
            seg[:upper],
            rows[:upper],
            width,
        )
        query_parts.append(d_query)
        padding = ((0, total - upper), (0, 0), (0, 0))
        key_sum = key_sum + jnp.pad(key_terms, padding)
        value_sum = value_sum + jnp.pad(value_terms, padding)
    return (jnp.concatenate(query_parts, axis=0), key_sum, value_sum)


def block_moves(n_dp, n_ctx):
    count = n_dp * n_ctx
    return [(f, (f % n_dp) * n_ctx + f // n_dp) for f in range(count)]


def fetch_out_rows(w_out):
    n_dp = lax.axis_size("dp")
    n_ctx = lax.axis_size("ctx")
    moved = lax.ppermute(w_out.astype(jnp.bfloat16), ("dp", "ctx"), perm=block_moves(n_dp, n_ctx))
    return lax.all_gather(moved, "dp", axis=0, tiled=True)


def return_out_rows(grad_out_rows):
    n_dp = lax.axis_size("dp")
    n_ctx = lax.axis_size("ctx")
    part = lax.psum_scatter(grad_out_rows, "dp", scatter_dimension=0, tiled=True)
    back = [(b, a) for a, b in block_moves(n_dp, n_ctx)]
    return lax.ppermute(part, ("dp", "ctx"), perm=back)


def fetch_small(b_qkv, b_out, b_fc2, ln_gain, ln_shift, b_fc1):
    pieces = (b_qkv, b_out, b_fc2, ln_gain, ln_shift, b_fc1)
    packed = jnp.concatenate([p.astype(jnp.bfloat16) for p in pieces])
    table = lax.all_gather(packed, ("dp", "ctx"), axis=0, tiled=False)
    result = []
    offset = 0
    for p in pieces:
        result.append(table[:, offset : offset + p.shape[0]])
        offset += p.shape[0]
    return result


def fetch_heads(w_qkv, w_fc1, w_fc2):
    dp_count = lax.axis_size("dp")
    ctx_count = lax.axis_size("ctx")
    rows_piece = w_qkv.shape[0]
    head_width = D // ctx_count
    unit = FF // (dp_count * ctx_count)
    qkv_piece = w_qkv.astype(jnp.bfloat16).reshape(rows_piece, 3, ctx_count, head_width)
    fc1_piece = w_fc1.astype(jnp.bfloat16).reshape(rows_piece, dp_count, ctx_count, unit)
    qkv_sent, fc1_sent = (
        lax.all_to_all(qkv_piece, "ctx", split_axis=2, concat_axis=0, tiled=True),
        lax.all_to_all(fc1_piece, "ctx", split_axis=2, concat_axis=0, tiled=True),
    )
    qkv_cols, fc1_cols, fc2_rows = (
        lax.all_gather(qkv_sent, "dp", axis=0, tiled=True),
        lax.all_gather(fc1_sent, "dp", axis=0, tiled=True),
        lax.all_gather(w_fc2.astype(jnp.bfloat16), "dp", axis=0, tiled=True),
    )
    return (
        qkv_cols.reshape(D, 3 * head_width),
        fc1_cols.reshape(D, dp_count * unit),
        fc2_rows,
    )


def head_plan(
    tokens,
    lengths,
    w_qkv,
    b_qkv,
    w_out,
    b_out,
    w_fc1,
    b_fc1,
    w_fc2,
    b_fc2,
    ln_gain,
    ln_shift,
    cotangent,
):
    rows_here = tokens.shape[0]
    rows_piece = w_qkv.shape[0]
    dp_count = lax.axis_size("dp")
    ctx_count = lax.axis_size("ctx")
    count = dp_count * ctx_count
    group = rows_here * ctx_count
    width = min(512, group)
    head_width = D // ctx_count
    local_heads = HEADS // ctx_count
    unit = FF // (dp_count * ctx_count)
    here = lax.axis_index("ctx")
    group_rows = jnp.arange(group, dtype=jnp.int32)
    seg, positions = segment_info(lengths[0], group_rows)
    cosine, sine = rotary_tables(positions)
    qkv_bias, out_bias, fc2_bias, gain_low, shift_low, fc1_table = fetch_small(
        b_qkv, b_out, b_fc2, ln_gain, ln_shift, b_fc1
    )
    qkv_bias = qkv_bias.reshape(3 * D)
    out_bias = out_bias.reshape(D)
    fc2_bias = fc2_bias.reshape(D)
    gain_low = gain_low.reshape(D)
    shift_low = shift_low.reshape(D)
    fc1_bias = lax.dynamic_index_in_dim(
        fc1_table.reshape(dp_count, ctx_count, unit), here, 1, keepdims=False
    ).reshape(dp_count * unit)
    out_rows = fetch_out_rows(w_out)
    qkv_cols, fc1_cols, fc2_rows = fetch_heads(w_qkv, w_fc1, w_fc2)
    gain32 = gain_low.astype(jnp.float32)
    inputs = tokens.astype(jnp.float32)
    normed, scaled, hidden32 = norm_parts(inputs, gain32, shift_low.astype(jnp.float32))
    hidden = hidden32.astype(jnp.bfloat16)
    hidden_group, dy_group = (
        lax.all_gather(hidden, "ctx", axis=0, tiled=True),
        lax.all_gather(cotangent, "ctx", axis=0, tiled=True),
    )
    bias_cols = lax.dynamic_slice_in_dim(
        qkv_bias.reshape(3, D), here * head_width, head_width, 1
    ).reshape(3 * head_width)
    qkv = jnp.dot(hidden_group, qkv_cols, preferred_element_type=jnp.float32) + bias_cols.astype(
        jnp.float32
    )
    shape = (group, local_heads, HEAD_DIM)
    query = rotate(qkv[:, :head_width].reshape(shape), cosine, sine).astype(jnp.bfloat16)
    keys = rotate(qkv[:, head_width : 2 * head_width].reshape(shape), cosine, sine).astype(
        jnp.bfloat16
    )
    values = qkv[:, 2 * head_width :].reshape(shape).astype(jnp.bfloat16)
    attended32, log_total = causal_forward(query, keys, values, seg, group_rows, width)
    attended = attended32.reshape(group, head_width).astype(jnp.bfloat16)
    pre = jnp.dot(hidden_group, fc1_cols, preferred_element_type=jnp.float32) + fc1_bias.astype(
        jnp.float32
    )
    act = gelu_tanh(pre).astype(jnp.bfloat16)
    branches = lax.psum_scatter(
        (
            jnp.dot(attended, out_rows, preferred_element_type=jnp.float32)
            + jnp.dot(act, fc2_rows, preferred_element_type=jnp.float32)
        ).astype(jnp.bfloat16),
        "ctx",
        scatter_dimension=0,
        tiled=True,
    ).astype(jnp.float32)
    block_out = (
        inputs + branches + out_bias.astype(jnp.float32) + fc2_bias.astype(jnp.float32)
    ).astype(jnp.bfloat16)
    grad_out32 = cotangent.astype(jnp.float32)
    grad_b_fc2 = jnp.sum(grad_out32, axis=0)
    grad_fc2_part = jnp.einsum("tf,td->fd", act, dy_group, preferred_element_type=jnp.float32)
    d_act = jnp.einsum("td,fd->tf", dy_group, fc2_rows, preferred_element_type=jnp.float32)
    d_pre = (d_act * gelu_slope(pre)).astype(jnp.bfloat16)
    grad_fc1_part = jnp.einsum("td,tf->df", hidden_group, d_pre, preferred_element_type=jnp.float32)
    grad_bfc1_part = jnp.sum(d_pre.astype(jnp.float32), axis=0)
    grad_out_rows = jnp.einsum("tc,td->cd", attended, dy_group, preferred_element_type=jnp.float32)
    owned_w_out = return_out_rows(grad_out_rows)
    d_attended = (
        jnp.einsum("td,cd->tc", dy_group, out_rows, preferred_element_type=jnp.float32)
        .astype(jnp.bfloat16)
        .reshape(shape)
    )
    delta = jnp.sum(d_attended.astype(jnp.float32) * attended32, axis=2).T
    d_query, d_keys, d_values = causal_backward(
        query, d_attended, delta, log_total, keys, values, seg, group_rows, width
    )
    d_query = rotate_back(d_query, cosine, sine).reshape(group, head_width)
    d_keys = rotate_back(d_keys, cosine, sine).reshape(group, head_width)
    d_qkv = jnp.concatenate([d_query, d_keys, d_values.reshape(group, head_width)], axis=1).astype(
        jnp.bfloat16
    )
    grad_qkv_part = jnp.einsum("td,tc->dc", hidden_group, d_qkv, preferred_element_type=jnp.float32)
    bias_part = jnp.sum(d_qkv.astype(jnp.float32), axis=0).reshape(3, head_width)
    d_hidden = lax.psum_scatter(
        (
            jnp.einsum("tc,dc->td", d_qkv, qkv_cols, preferred_element_type=jnp.float32)
            + jnp.einsum("tf,df->td", d_pre, fc1_cols, preferred_element_type=jnp.float32)
        ).astype(jnp.bfloat16),
        "ctx",
        scatter_dimension=0,
        tiled=True,
    ).astype(jnp.float32)
    grad_gain, grad_shift, d_inputs = norm_back(d_hidden, normed, scaled, gain32)
    grad_tokens = (grad_out32 + d_inputs).astype(jnp.bfloat16)
    weight_parts = jnp.concatenate([grad_qkv_part, grad_fc1_part], axis=1).astype(jnp.bfloat16)
    owned_parts = lax.psum_scatter(weight_parts, "dp", scatter_dimension=0, tiled=True)
    owned_qkv = owned_parts[:, : 3 * head_width].reshape(-1, 3, 1, head_width)
    owned_fc1 = owned_parts[:, 3 * head_width :].reshape(-1, dp_count, 1, unit)
    owned_fc2 = lax.psum_scatter(
        grad_fc2_part.astype(jnp.bfloat16), "dp", scatter_dimension=0, tiled=True
    ).astype(jnp.float32)
    split_qkv, split_fc1 = (
        lax.all_to_all(owned_qkv, "ctx", split_axis=0, concat_axis=2, tiled=True).astype(
            jnp.float32
        ),
        lax.all_to_all(owned_fc1, "ctx", split_axis=0, concat_axis=2, tiled=True).astype(
            jnp.float32
        ),
    )
    full_bqkv = lax.dynamic_update_slice_in_dim(
        jnp.zeros((3, D), jnp.float32), bias_part, here * head_width, 1
    )
    full_bfc1 = lax.dynamic_update_slice_in_dim(
        jnp.zeros((dp_count, ctx_count, unit), jnp.float32),
        grad_bfc1_part.reshape(dp_count, 1, unit),
        here,
        1,
    )
    small = jnp.concatenate(
        [
            full_bqkv.reshape(count, -1),
            grad_b_fc2.reshape(count, -1),
            grad_gain.reshape(count, -1),
            grad_shift.reshape(count, -1),
            full_bfc1.reshape(count, -1),
        ],
        axis=1,
    )
    owned_small = lax.psum_scatter(small, ("dp", "ctx"), scatter_dimension=0, tiled=True)[0]
    cuts = [0, 3 * D // count, D // count, D // count, D // count, FF // count]
    bounds = [sum(cuts[: i + 1]) for i in range(len(cuts))]
    owned_bqkv, owned_bout, owned_gain, owned_shift, owned_bfc1 = [
        owned_small[bounds[i] : bounds[i + 1]] for i in range(5)
    ]
    return (
        block_out,
        grad_tokens,
        split_qkv.reshape(rows_piece, 3 * D),
        owned_bqkv,
        owned_w_out,
        owned_bout,
        split_fc1.reshape(rows_piece, FF),
        owned_bfc1,
        owned_fc2,
        owned_bout,
        owned_gain,
        owned_shift,
    )


def body(
    tokens,
    lengths,
    w_qkv,
    b_qkv,
    w_out,
    b_out,
    w_fc1,
    b_fc1,
    w_fc2,
    b_fc2,
    ln_gain,
    ln_shift,
    cotangent,
):
    return head_plan(
        tokens,
        lengths,
        w_qkv,
        b_qkv,
        w_out,
        b_out,
        w_fc1,
        b_fc1,
        w_fc2,
        b_fc2,
        ln_gain,
        ln_shift,
        cotangent,
    )


def solution(mesh):
    in_specs = (
        P(("dp", "ctx"), None),
        P("dp", None),
        P(("dp", "ctx"), None),
        P(("dp", "ctx")),
        P(("dp", "ctx"), None),
        P(("dp", "ctx")),
        P(("dp", "ctx"), None),
        P(("dp", "ctx")),
        P(("dp", "ctx"), None),
        P(("dp", "ctx")),
        P(("dp", "ctx")),
        P(("dp", "ctx")),
        P(("dp", "ctx"), None),
    )
    out_specs = (
        P(("dp", "ctx"), None),
        P(("dp", "ctx"), None),
        P(("dp", "ctx"), None),
        P(("dp", "ctx")),
        P(("dp", "ctx"), None),
        P(("dp", "ctx")),
        P(("dp", "ctx"), None),
        P(("dp", "ctx")),
        P(("dp", "ctx"), None),
        P(("dp", "ctx")),
        P(("dp", "ctx")),
        P(("dp", "ctx")),
    )
    return jax.shard_map(body, mesh=mesh, in_specs=in_specs, out_specs=out_specs, check_vma=False)
```

```python
import functools
import math

import jax
import jax.numpy as jnp
from jax import lax
from jax.experimental import pallas as pl
from jax.experimental.pallas import tpu as pltpu
from jax.sharding import PartitionSpec as P

D = 2048
HEADS = 32
HEAD_DIM = 64
ROT = 32
FF = 8192


EPS = 1e-05
GELU_COEF = math.sqrt(2.0 / math.pi)
NEGATIVE = -1e30


def norm_parts(inputs, gain, shift):
    mean = jnp.mean(inputs, axis=-1, keepdims=True)
    centred = inputs - mean
    var = jnp.mean(centred * centred, axis=-1, keepdims=True)
    scaled = lax.rsqrt(var + EPS)
    normed = centred * scaled
    return (normed, scaled, normed * gain + shift)


def norm_back(d_hidden, normed, scaled, gain32):
    grad_gain = jnp.sum(d_hidden * normed, axis=0)
    grad_shift = jnp.sum(d_hidden, axis=0)
    d_normed = d_hidden * gain32
    d_inputs = scaled * (
        d_normed
        - jnp.mean(d_normed, axis=-1, keepdims=True)
        - normed * jnp.mean(d_normed * normed, axis=-1, keepdims=True)
    )
    return (grad_gain, grad_shift, d_inputs)


def gelu_tanh(pre):
    return 0.5 * pre * (1.0 + jnp.tanh(GELU_COEF * (pre + 0.044715 * pre * pre * pre)))


def gelu_slope(pre):
    tangent = jnp.tanh(GELU_COEF * (pre + 0.044715 * pre * pre * pre))
    return 0.5 * (1.0 + tangent) + 0.5 * pre * (1.0 - tangent * tangent) * GELU_COEF * (
        1.0 + 3.0 * 0.044715 * pre * pre
    )


def rotary_tables(positions):
    half = ROT // 2
    freq = jnp.exp(jnp.arange(half, dtype=jnp.float32) * (-2.0 * math.log(10000.0) / ROT))
    angle = positions.astype(jnp.float32)[:, None] * freq[None, :]
    return (jnp.cos(angle)[:, None, :], jnp.sin(angle)[:, None, :])


def rotate(heads, cosine, sine):
    half = ROT // 2
    first = heads[..., :half]
    second = heads[..., half:ROT]
    return jnp.concatenate(
        [first * cosine - second * sine, second * cosine + first * sine, heads[..., ROT:]], axis=-1
    )


def rotate_back(grads, cosine, sine):
    half = ROT // 2
    first = grads[..., :half]
    second = grads[..., half:ROT]
    return jnp.concatenate(
        [first * cosine + second * sine, second * cosine - first * sine, grads[..., ROT:]], axis=-1
    )


def segment_info(lengths_row, rows):
    ends = jnp.cumsum(lengths_row)
    starts = ends - lengths_row
    seg = jnp.sum((rows[:, None] >= ends[None, :]).astype(jnp.int32), axis=1)
    onehot = seg[:, None] == jnp.arange(lengths_row.shape[0], dtype=jnp.int32)[None, :]
    first_rows = jnp.sum(jnp.where(onehot, starts[None, :], 0), axis=1)
    return (seg, rows - first_rows)


TRANS_B = (((1,), (1,)), ((), ()))


def _allowed(segq_ref, segk_ref, i, j, tq, tk):
    rows = i * tq + lax.broadcasted_iota(jnp.int32, (tq, tk), 0)
    cols = j * tk + lax.broadcasted_iota(jnp.int32, (tq, tk), 1)
    return (segq_ref[...] == segk_ref[...]) & (cols <= rows)


def _fwd_kernel(q_ref, k_ref, v_ref, segq_ref, segk_ref, o_ref, lse_ref, m_sc, l_sc, acc_sc, *, tq, tk, scale):
    i = pl.program_id(1)
    j = pl.program_id(2)

    @pl.when(j == 0)
    def _():
        m_sc[...] = jnp.full_like(m_sc, NEGATIVE)
        l_sc[...] = jnp.zeros_like(l_sc)
        acc_sc[...] = jnp.zeros_like(acc_sc)

    @pl.when(j * tk <= i * tq + tq - 1)
    def _():
        q = q_ref[0]
        k = k_ref[0]
        s = lax.dot_general(q, k, TRANS_B, preferred_element_type=jnp.float32) * scale
        allowed = _allowed(segq_ref, segk_ref, i, j, tq, tk)
        s = jnp.where(allowed, s, NEGATIVE)
        m_prev = m_sc[...]
        m_new = jnp.maximum(m_prev, jnp.max(s, axis=1, keepdims=True))
        factor = jnp.exp(m_prev - m_new)
        p = jnp.where(allowed, jnp.exp(s - m_new), 0.0)
        l_sc[...] = l_sc[...] * factor + jnp.sum(p, axis=1, keepdims=True)
        acc_sc[...] = acc_sc[...] * factor + jnp.dot(
            p.astype(jnp.bfloat16), v_ref[0], preferred_element_type=jnp.float32
        )
        m_sc[...] = m_new

    @pl.when(j == pl.num_programs(2) - 1)
    def _():
        total = l_sc[...]
        o_ref[0] = acc_sc[...] / total
        lse_ref[0] = m_sc[...] + jnp.log(total)


def attention_forward(q, k, v, seg, tq=512, tk=512):
    heads, total, dim = q.shape
    nq, nk = total // tq, total // tk
    scale = 1.0 / math.sqrt(dim)
    segq = seg.reshape(total, 1)
    segk = seg.reshape(1, total)

    def kv_map(h, i, j):
        return (h, jnp.minimum(j, (i * tq + tq - 1) // tk), 0)

    def segk_map(h, i, j):
        return (0, jnp.minimum(j, (i * tq + tq - 1) // tk))

    return pl.pallas_call(
        functools.partial(_fwd_kernel, tq=tq, tk=tk, scale=scale),
        out_shape=(
            jax.ShapeDtypeStruct((heads, total, dim), jnp.float32),
            jax.ShapeDtypeStruct((heads, total, 1), jnp.float32),
        ),
        grid=(heads, nq, nk),
        in_specs=[
            pl.BlockSpec((1, tq, dim), lambda h, i, j: (h, i, 0)),
            pl.BlockSpec((1, tk, dim), kv_map),
            pl.BlockSpec((1, tk, dim), kv_map),
            pl.BlockSpec((tq, 1), lambda h, i, j: (i, 0)),
            pl.BlockSpec((1, tk), segk_map),
        ],
        out_specs=[
            pl.BlockSpec((1, tq, dim), lambda h, i, j: (h, i, 0)),
            pl.BlockSpec((1, tq, 1), lambda h, i, j: (h, i, 0)),
        ],
        scratch_shapes=[
            pltpu.VMEM((tq, 1), jnp.float32),
            pltpu.VMEM((tq, 1), jnp.float32),
            pltpu.VMEM((tq, dim), jnp.float32),
        ],
        cost_estimate=pl.CostEstimate(
            flops=2 * heads * total * total * dim,
            transcendentals=heads * total * total // 2,
            bytes_accessed=heads * total * dim * 10,
        ),
    )(q, k, v, segq, segk)


def _bwd_kernel(q_ref, k_ref, v_ref, do_ref, lse_ref, delta_ref, segq_ref, segk_ref, dq_ref, dk_ref, dv_ref, *, tq, tk, scale):
    j = pl.program_id(1)
    i = pl.program_id(2)

    @pl.when((j == 0) & (i == 0))
    def _():
        dq_ref[...] = jnp.zeros_like(dq_ref)

    @pl.when(i == 0)
    def _():
        dk_ref[...] = jnp.zeros_like(dk_ref)
        dv_ref[...] = jnp.zeros_like(dv_ref)

    @pl.when(i * tq + tq - 1 >= j * tk)
    def _():
        q = q_ref[0]
        k = k_ref[0]
        do = do_ref[0]
        s = lax.dot_general(q, k, TRANS_B, preferred_element_type=jnp.float32) * scale
        allowed = _allowed(segq_ref, segk_ref, i, j, tq, tk)
        p = jnp.where(allowed, jnp.exp(s - lse_ref[0]), 0.0)
        dp = lax.dot_general(do, v_ref[0], TRANS_B, preferred_element_type=jnp.float32)
        ds = (p * (dp - delta_ref[0])).astype(jnp.bfloat16)
        dv_ref[0] += lax.dot(p.astype(jnp.bfloat16).T, do, preferred_element_type=jnp.float32)
        dk_ref[0] += lax.dot(ds.T, q, preferred_element_type=jnp.float32) * scale
        rows = pl.ds(pl.multiple_of(i * tq, tq), tq)
        dq_ref[0, rows, :] += lax.dot(ds, k, preferred_element_type=jnp.float32) * scale


def attention_backward(q, k, v, do, lse, delta, seg, tq=512, tk=512):
    heads, total, dim = q.shape
    nq, nk = total // tq, total // tk
    scale = 1.0 / math.sqrt(dim)
    segq = seg.reshape(total, 1)
    segk = seg.reshape(1, total)

    def q_map(h, j, i):
        return (h, jnp.maximum(i, (j * tk) // tq), 0)

    def segq_map(h, j, i):
        return (jnp.maximum(i, (j * tk) // tq), 0)

    return pl.pallas_call(
        functools.partial(_bwd_kernel, tq=tq, tk=tk, scale=scale),
        out_shape=(
            jax.ShapeDtypeStruct((heads, total, dim), jnp.float32),
            jax.ShapeDtypeStruct((heads, total, dim), jnp.float32),
            jax.ShapeDtypeStruct((heads, total, dim), jnp.float32),
        ),
        grid=(heads, nk, nq),
        in_specs=[
            pl.BlockSpec((1, tq, dim), q_map),
            pl.BlockSpec((1, tk, dim), lambda h, j, i: (h, j, 0)),
            pl.BlockSpec((1, tk, dim), lambda h, j, i: (h, j, 0)),
            pl.BlockSpec((1, tq, dim), q_map),
            pl.BlockSpec((1, tq, 1), q_map),
            pl.BlockSpec((1, tq, 1), q_map),
            pl.BlockSpec((tq, 1), segq_map),
            pl.BlockSpec((1, tk), lambda h, j, i: (0, j)),
        ],
        out_specs=[
            pl.BlockSpec((1, total, dim), lambda h, j, i: (h, 0, 0)),
            pl.BlockSpec((1, tk, dim), lambda h, j, i: (h, j, 0)),
            pl.BlockSpec((1, tk, dim), lambda h, j, i: (h, j, 0)),
        ],
        cost_estimate=pl.CostEstimate(
            flops=5 * heads * total * total * dim,
            transcendentals=heads * total * total // 2,
            bytes_accessed=heads * total * dim * 24,
        ),
    )(q, k, v, do, lse, delta, segq, segk)


def block_moves(n_dp, n_ctx):
    count = n_dp * n_ctx
    return [(f, (f % n_dp) * n_ctx + f // n_dp) for f in range(count)]


def fetch_out_rows(w_out):
    n_dp = lax.axis_size("dp")
    n_ctx = lax.axis_size("ctx")
    moved = lax.ppermute(w_out.astype(jnp.bfloat16), ("dp", "ctx"), perm=block_moves(n_dp, n_ctx))
    return lax.all_gather(moved, "dp", axis=0, tiled=True)


def return_out_rows(grad_out_rows):
    n_dp = lax.axis_size("dp")
    n_ctx = lax.axis_size("ctx")
    part = lax.psum_scatter(grad_out_rows, "dp", scatter_dimension=0, tiled=True)
    back = [(b, a) for a, b in block_moves(n_dp, n_ctx)]
    return lax.ppermute(part, ("dp", "ctx"), perm=back)


def fetch_small(b_qkv, b_out, b_fc2, ln_gain, ln_shift, b_fc1):
    pieces = (b_qkv, b_out, b_fc2, ln_gain, ln_shift, b_fc1)
    packed = jnp.concatenate([p.astype(jnp.bfloat16) for p in pieces])
    table = lax.all_gather(packed, ("dp", "ctx"), axis=0, tiled=False)
    result = []
    offset = 0
    for p in pieces:
        result.append(table[:, offset : offset + p.shape[0]])
        offset += p.shape[0]
    return result


def fetch_heads(w_qkv, w_fc1, w_fc2):
    dp_count = lax.axis_size("dp")
    ctx_count = lax.axis_size("ctx")
    rows_piece = w_qkv.shape[0]
    head_width = D // ctx_count
    unit = FF // (dp_count * ctx_count)
    qkv_piece = w_qkv.astype(jnp.bfloat16).reshape(rows_piece, 3, ctx_count, head_width)
    fc1_piece = w_fc1.astype(jnp.bfloat16).reshape(rows_piece, dp_count, ctx_count, unit)
    qkv_sent, fc1_sent = (
        lax.all_to_all(qkv_piece, "ctx", split_axis=2, concat_axis=0, tiled=True),
        lax.all_to_all(fc1_piece, "ctx", split_axis=2, concat_axis=0, tiled=True),
    )
    qkv_cols, fc1_cols, fc2_rows = (
        lax.all_gather(qkv_sent, "dp", axis=0, tiled=True),
        lax.all_gather(fc1_sent, "dp", axis=0, tiled=True),
        lax.all_gather(w_fc2.astype(jnp.bfloat16), "dp", axis=0, tiled=True),
    )
    return (
        qkv_cols.reshape(D, 3 * head_width),
        fc1_cols.reshape(D, dp_count * unit),
        fc2_rows,
    )


def head_plan(
    tokens,
    lengths,
    w_qkv,
    b_qkv,
    w_out,
    b_out,
    w_fc1,
    b_fc1,
    w_fc2,
    b_fc2,
    ln_gain,
    ln_shift,
    cotangent,
):
    rows_here = tokens.shape[0]
    rows_piece = w_qkv.shape[0]
    dp_count = lax.axis_size("dp")
    ctx_count = lax.axis_size("ctx")
    count = dp_count * ctx_count
    group = rows_here * ctx_count
    head_width = D // ctx_count
    local_heads = HEADS // ctx_count
    unit = FF // (dp_count * ctx_count)
    here = lax.axis_index("ctx")
    group_rows = jnp.arange(group, dtype=jnp.int32)
    seg, positions = segment_info(lengths[0], group_rows)
    cosine, sine = rotary_tables(positions)
    qkv_bias, out_bias, fc2_bias, gain_low, shift_low, fc1_table = fetch_small(
        b_qkv, b_out, b_fc2, ln_gain, ln_shift, b_fc1
    )
    qkv_bias = qkv_bias.reshape(3 * D)
    out_bias = out_bias.reshape(D)
    fc2_bias = fc2_bias.reshape(D)
    gain_low = gain_low.reshape(D)
    shift_low = shift_low.reshape(D)
    fc1_bias = lax.dynamic_index_in_dim(
        fc1_table.reshape(dp_count, ctx_count, unit), here, 1, keepdims=False
    ).reshape(dp_count * unit)
    out_rows = fetch_out_rows(w_out)
    qkv_cols, fc1_cols, fc2_rows = fetch_heads(w_qkv, w_fc1, w_fc2)
    gain32 = gain_low.astype(jnp.float32)
    shift32 = shift_low.astype(jnp.float32)
    inputs = tokens.astype(jnp.float32)
    normed, scaled, _ = norm_parts(inputs, gain32, shift32)
    tokens_group, dy_group = (
        lax.all_gather(tokens, "ctx", axis=0, tiled=True),
        lax.all_gather(cotangent, "ctx", axis=0, tiled=True),
    )
    hidden_group = norm_parts(tokens_group.astype(jnp.float32), gain32, shift32)[2].astype(
        jnp.bfloat16
    )
    bias_cols = lax.dynamic_slice_in_dim(
        qkv_bias.reshape(3, D), here * head_width, head_width, 1
    ).reshape(3 * head_width)
    qkv = jnp.dot(hidden_group, qkv_cols, preferred_element_type=jnp.float32) + bias_cols.astype(
        jnp.float32
    )
    shape = (group, local_heads, HEAD_DIM)
    query = rotate(qkv[:, :head_width].reshape(shape), cosine, sine).astype(jnp.bfloat16)
    keys = rotate(qkv[:, head_width : 2 * head_width].reshape(shape), cosine, sine).astype(
        jnp.bfloat16
    )
    values = qkv[:, 2 * head_width :].reshape(shape).astype(jnp.bfloat16)
    q_heads = query.transpose(1, 0, 2)
    k_heads = keys.transpose(1, 0, 2)
    v_heads = values.transpose(1, 0, 2)
    attended_heads, log_total = attention_forward(q_heads, k_heads, v_heads, seg)
    attended = attended_heads.transpose(1, 0, 2).reshape(group, head_width).astype(jnp.bfloat16)
    pre = jnp.dot(hidden_group, fc1_cols, preferred_element_type=jnp.float32) + fc1_bias.astype(
        jnp.float32
    )
    act = gelu_tanh(pre).astype(jnp.bfloat16)
    branches = lax.psum_scatter(
        (
            jnp.dot(attended, out_rows, preferred_element_type=jnp.float32)
            + jnp.dot(act, fc2_rows, preferred_element_type=jnp.float32)
        ).astype(jnp.bfloat16),
        "ctx",
        scatter_dimension=0,
        tiled=True,
    ).astype(jnp.float32)
    block_out = (
        inputs + branches + out_bias.astype(jnp.float32) + fc2_bias.astype(jnp.float32)
    ).astype(jnp.bfloat16)
    grad_out32 = cotangent.astype(jnp.float32)
    grad_b_fc2 = jnp.sum(grad_out32, axis=0)
    grad_fc2_part = jnp.einsum("tf,td->fd", act, dy_group, preferred_element_type=jnp.float32)
    d_act = jnp.einsum("td,fd->tf", dy_group, fc2_rows, preferred_element_type=jnp.float32)
    d_pre = (d_act * gelu_slope(pre)).astype(jnp.bfloat16)
    grad_fc1_part = jnp.einsum("td,tf->df", hidden_group, d_pre, preferred_element_type=jnp.float32)
    grad_bfc1_part = jnp.sum(d_pre.astype(jnp.float32), axis=0)
    grad_out_rows = jnp.einsum("tc,td->cd", attended, dy_group, preferred_element_type=jnp.float32)
    owned_w_out = return_out_rows(grad_out_rows)
    d_attended = (
        jnp.einsum("td,cd->tc", dy_group, out_rows, preferred_element_type=jnp.float32)
        .astype(jnp.bfloat16)
        .reshape(shape)
    )
    d_heads = d_attended.transpose(1, 0, 2)
    delta = jnp.sum(d_heads.astype(jnp.float32) * attended_heads, axis=2, keepdims=True)
    dq_heads, dk_heads, dv_heads = attention_backward(
        q_heads, k_heads, v_heads, d_heads, log_total, delta, seg
    )
    d_query = dq_heads.transpose(1, 0, 2)
    d_keys = dk_heads.transpose(1, 0, 2)
    d_values = dv_heads.transpose(1, 0, 2)
    d_query = rotate_back(d_query, cosine, sine).reshape(group, head_width)
    d_keys = rotate_back(d_keys, cosine, sine).reshape(group, head_width)
    d_qkv = jnp.concatenate([d_query, d_keys, d_values.reshape(group, head_width)], axis=1).astype(
        jnp.bfloat16
    )
    grad_qkv_part = jnp.einsum("td,tc->dc", hidden_group, d_qkv, preferred_element_type=jnp.float32)
    bias_part = jnp.sum(d_qkv.astype(jnp.float32), axis=0).reshape(3, head_width)
    d_hidden = lax.psum_scatter(
        (
            jnp.einsum("tc,dc->td", d_qkv, qkv_cols, preferred_element_type=jnp.float32)
            + jnp.einsum("tf,df->td", d_pre, fc1_cols, preferred_element_type=jnp.float32)
        ).astype(jnp.bfloat16),
        "ctx",
        scatter_dimension=0,
        tiled=True,
    ).astype(jnp.float32)
    grad_gain, grad_shift, d_inputs = norm_back(d_hidden, normed, scaled, gain32)
    grad_tokens = (grad_out32 + d_inputs).astype(jnp.bfloat16)
    weight_parts = jnp.concatenate([grad_qkv_part, grad_fc1_part], axis=1).astype(jnp.bfloat16)
    owned_parts = lax.psum_scatter(weight_parts, "dp", scatter_dimension=0, tiled=True)
    owned_qkv = owned_parts[:, : 3 * head_width].reshape(-1, 3, 1, head_width)
    owned_fc1 = owned_parts[:, 3 * head_width :].reshape(-1, dp_count, 1, unit)
    owned_fc2 = lax.psum_scatter(
        grad_fc2_part.astype(jnp.bfloat16), "dp", scatter_dimension=0, tiled=True
    ).astype(jnp.float32)
    split_qkv, split_fc1 = (
        lax.all_to_all(owned_qkv, "ctx", split_axis=0, concat_axis=2, tiled=True).astype(
            jnp.float32
        ),
        lax.all_to_all(owned_fc1, "ctx", split_axis=0, concat_axis=2, tiled=True).astype(
            jnp.float32
        ),
    )
    full_bqkv = lax.dynamic_update_slice_in_dim(
        jnp.zeros((3, D), jnp.float32), bias_part, here * head_width, 1
    )
    full_bfc1 = lax.dynamic_update_slice_in_dim(
        jnp.zeros((dp_count, ctx_count, unit), jnp.float32),
        grad_bfc1_part.reshape(dp_count, 1, unit),
        here,
        1,
    )
    small = jnp.concatenate(
        [
            full_bqkv.reshape(count, -1),
            grad_b_fc2.reshape(count, -1),
            grad_gain.reshape(count, -1),
            grad_shift.reshape(count, -1),
            full_bfc1.reshape(count, -1),
        ],
        axis=1,
    )
    width_small = small.shape[1]
    over_dp = lax.psum_scatter(
        small.reshape(dp_count, ctx_count * width_small), "dp", scatter_dimension=0, tiled=True
    )
    owned_small = lax.psum_scatter(
        over_dp.reshape(ctx_count, width_small), "ctx", scatter_dimension=0, tiled=True
    )[0]
    cuts = [0, 3 * D // count, D // count, D // count, D // count, FF // count]
    bounds = [sum(cuts[: i + 1]) for i in range(len(cuts))]
    owned_bqkv, owned_bout, owned_gain, owned_shift, owned_bfc1 = [
        owned_small[bounds[i] : bounds[i + 1]] for i in range(5)
    ]
    return (
        block_out,
        grad_tokens,
        split_qkv.reshape(rows_piece, 3 * D),
        owned_bqkv,
        owned_w_out,
        owned_bout,
        split_fc1.reshape(rows_piece, FF),
        owned_bfc1,
        owned_fc2,
        owned_bout,
        owned_gain,
        owned_shift,
    )


def body(
    tokens,
    lengths,
    w_qkv,
    b_qkv,
    w_out,
    b_out,
    w_fc1,
    b_fc1,
    w_fc2,
    b_fc2,
    ln_gain,
    ln_shift,
    cotangent,
):
    return head_plan(
        tokens,
        lengths,
        w_qkv,
        b_qkv,
        w_out,
        b_out,
        w_fc1,
        b_fc1,
        w_fc2,
        b_fc2,
        ln_gain,
        ln_shift,
        cotangent,
    )


def solution(mesh):
    in_specs = (
        P(("dp", "ctx"), None),
        P("dp", None),
        P(("dp", "ctx"), None),
        P(("dp", "ctx")),
        P(("dp", "ctx"), None),
        P(("dp", "ctx")),
        P(("dp", "ctx"), None),
        P(("dp", "ctx")),
        P(("dp", "ctx"), None),
        P(("dp", "ctx")),
        P(("dp", "ctx")),
        P(("dp", "ctx")),
        P(("dp", "ctx"), None),
    )
    out_specs = (
        P(("dp", "ctx"), None),
        P(("dp", "ctx"), None),
        P(("dp", "ctx"), None),
        P(("dp", "ctx")),
        P(("dp", "ctx"), None),
        P(("dp", "ctx")),
        P(("dp", "ctx"), None),
        P(("dp", "ctx")),
        P(("dp", "ctx"), None),
        P(("dp", "ctx")),
        P(("dp", "ctx")),
        P(("dp", "ctx")),
    )
    return jax.shard_map(body, mesh=mesh, in_specs=in_specs, out_specs=out_specs, check_vma=False)
```

```python
import functools
import math

import jax
import jax.numpy as jnp
from jax import lax
from jax.experimental import pallas as pl
from jax.experimental.pallas import tpu as pltpu
from jax.sharding import PartitionSpec as P

D = 2048
HEADS = 32
HEAD_DIM = 64
ROT = 32
FF = 8192


EPS = 1e-05
GELU_COEF = math.sqrt(2.0 / math.pi)
NEGATIVE = -1e30


def norm_parts(inputs, gain, shift):
    mean = jnp.mean(inputs, axis=-1, keepdims=True)
    centred = inputs - mean
    var = jnp.mean(centred * centred, axis=-1, keepdims=True)
    scaled = lax.rsqrt(var + EPS)
    normed = centred * scaled
    return (normed, scaled, normed * gain + shift)


def norm_back(d_hidden, normed, scaled, gain32):
    grad_gain = jnp.sum(d_hidden * normed, axis=0)
    grad_shift = jnp.sum(d_hidden, axis=0)
    d_normed = d_hidden * gain32
    d_inputs = scaled * (
        d_normed
        - jnp.mean(d_normed, axis=-1, keepdims=True)
        - normed * jnp.mean(d_normed * normed, axis=-1, keepdims=True)
    )
    return (grad_gain, grad_shift, d_inputs)


def gelu_tanh(pre):
    return 0.5 * pre * (1.0 + jnp.tanh(GELU_COEF * (pre + 0.044715 * pre * pre * pre)))


def gelu_slope(pre):
    tangent = jnp.tanh(GELU_COEF * (pre + 0.044715 * pre * pre * pre))
    return 0.5 * (1.0 + tangent) + 0.5 * pre * (1.0 - tangent * tangent) * GELU_COEF * (
        1.0 + 3.0 * 0.044715 * pre * pre
    )


def rotary_tables(positions):
    half = ROT // 2
    freq = jnp.exp(jnp.arange(half, dtype=jnp.float32) * (-2.0 * math.log(10000.0) / ROT))
    angle = positions.astype(jnp.float32)[:, None] * freq[None, :]
    return (jnp.cos(angle)[:, None, :], jnp.sin(angle)[:, None, :])


def rotate(heads, cosine, sine):
    half = ROT // 2
    first = heads[..., :half]
    second = heads[..., half:ROT]
    return jnp.concatenate(
        [first * cosine - second * sine, second * cosine + first * sine, heads[..., ROT:]], axis=-1
    )


def rotate_back(grads, cosine, sine):
    half = ROT // 2
    first = grads[..., :half]
    second = grads[..., half:ROT]
    return jnp.concatenate(
        [first * cosine + second * sine, second * cosine - first * sine, grads[..., ROT:]], axis=-1
    )


def segment_info(lengths_row, rows):
    ends = jnp.cumsum(lengths_row)
    starts = ends - lengths_row
    seg = jnp.sum((rows[:, None] >= ends[None, :]).astype(jnp.int32), axis=1)
    onehot = seg[:, None] == jnp.arange(lengths_row.shape[0], dtype=jnp.int32)[None, :]
    first_rows = jnp.sum(jnp.where(onehot, starts[None, :], 0), axis=1)
    return (seg, rows - first_rows)


TRANS_B = (((1,), (1,)), ((), ()))


def _allowed(segq_ref, segk_ref, i, j, tq, tk):
    rows = i * tq + lax.broadcasted_iota(jnp.int32, (tq, tk), 0)
    cols = j * tk + lax.broadcasted_iota(jnp.int32, (tq, tk), 1)
    return (segq_ref[...] == segk_ref[...]) & (cols <= rows)


def _fwd_kernel(q_ref, k_ref, v_ref, segq_ref, segk_ref, o_ref, lse_ref, m_sc, l_sc, acc_sc, *, tq, tk, scale):
    i = pl.program_id(1)
    j = pl.program_id(2)

    @pl.when(j == 0)
    def _():
        m_sc[...] = jnp.full_like(m_sc, NEGATIVE)
        l_sc[...] = jnp.zeros_like(l_sc)
        acc_sc[...] = jnp.zeros_like(acc_sc)

    @pl.when(j * tk <= i * tq + tq - 1)
    def _():
        q = q_ref[0]
        k = k_ref[0]
        s = lax.dot_general(q, k, TRANS_B, preferred_element_type=jnp.float32) * scale
        allowed = _allowed(segq_ref, segk_ref, i, j, tq, tk)
        s = jnp.where(allowed, s, NEGATIVE)
        m_prev = m_sc[...]
        m_new = jnp.maximum(m_prev, jnp.max(s, axis=1, keepdims=True))
        factor = jnp.exp(m_prev - m_new)
        p = jnp.where(allowed, jnp.exp(s - m_new), 0.0)
        l_sc[...] = l_sc[...] * factor + jnp.sum(p, axis=1, keepdims=True)
        acc_sc[...] = acc_sc[...] * factor + jnp.dot(
            p.astype(jnp.bfloat16), v_ref[0], preferred_element_type=jnp.float32
        )
        m_sc[...] = m_new

    @pl.when(j == pl.num_programs(2) - 1)
    def _():
        total = l_sc[...]
        o_ref[0] = acc_sc[...] / total
        lse_ref[0] = m_sc[...] + jnp.log(total)


def attention_forward(q, k, v, seg, tq=512, tk=512):
    heads, total, dim = q.shape
    nq, nk = total // tq, total // tk
    scale = 1.0 / math.sqrt(dim)
    segq = seg.reshape(total, 1)
    segk = seg.reshape(1, total)

    def kv_map(h, i, j):
        return (h, jnp.minimum(j, (i * tq + tq - 1) // tk), 0)

    def segk_map(h, i, j):
        return (0, jnp.minimum(j, (i * tq + tq - 1) // tk))

    return pl.pallas_call(
        functools.partial(_fwd_kernel, tq=tq, tk=tk, scale=scale),
        out_shape=(
            jax.ShapeDtypeStruct((heads, total, dim), jnp.float32),
            jax.ShapeDtypeStruct((heads, total, 1), jnp.float32),
        ),
        grid=(heads, nq, nk),
        in_specs=[
            pl.BlockSpec((1, tq, dim), lambda h, i, j: (h, i, 0)),
            pl.BlockSpec((1, tk, dim), kv_map),
            pl.BlockSpec((1, tk, dim), kv_map),
            pl.BlockSpec((tq, 1), lambda h, i, j: (i, 0)),
            pl.BlockSpec((1, tk), segk_map),
        ],
        out_specs=[
            pl.BlockSpec((1, tq, dim), lambda h, i, j: (h, i, 0)),
            pl.BlockSpec((1, tq, 1), lambda h, i, j: (h, i, 0)),
        ],
        scratch_shapes=[
            pltpu.VMEM((tq, 1), jnp.float32),
            pltpu.VMEM((tq, 1), jnp.float32),
            pltpu.VMEM((tq, dim), jnp.float32),
        ],
        cost_estimate=pl.CostEstimate(
            flops=2 * heads * total * total * dim,
            transcendentals=heads * total * total // 2,
            bytes_accessed=heads * total * dim * 10,
        ),
    )(q, k, v, segq, segk)


def _bwd_kernel(q_ref, k_ref, v_ref, do_ref, lse_ref, delta_ref, segq_ref, segk_ref, dq_ref, dk_ref, dv_ref, *, tq, tk, scale):
    j = pl.program_id(1)
    i = pl.program_id(2)

    @pl.when((j == 0) & (i == 0))
    def _():
        dq_ref[...] = jnp.zeros_like(dq_ref)

    @pl.when(i == 0)
    def _():
        dk_ref[...] = jnp.zeros_like(dk_ref)
        dv_ref[...] = jnp.zeros_like(dv_ref)

    @pl.when(i * tq + tq - 1 >= j * tk)
    def _():
        q = q_ref[0]
        k = k_ref[0]
        do = do_ref[0]
        s = lax.dot_general(q, k, TRANS_B, preferred_element_type=jnp.float32) * scale
        allowed = _allowed(segq_ref, segk_ref, i, j, tq, tk)
        p = jnp.where(allowed, jnp.exp(s - lse_ref[0]), 0.0)
        dp = lax.dot_general(do, v_ref[0], TRANS_B, preferred_element_type=jnp.float32)
        ds = (p * (dp - delta_ref[0])).astype(jnp.bfloat16)
        dv_ref[0] += lax.dot(p.astype(jnp.bfloat16).T, do, preferred_element_type=jnp.float32)
        dk_ref[0] += lax.dot(ds.T, q, preferred_element_type=jnp.float32) * scale
        rows = pl.ds(pl.multiple_of(i * tq, tq), tq)
        dq_ref[0, rows, :] += lax.dot(ds, k, preferred_element_type=jnp.float32) * scale


def attention_backward(q, k, v, do, lse, delta, seg, tq=512, tk=512):
    heads, total, dim = q.shape
    nq, nk = total // tq, total // tk
    scale = 1.0 / math.sqrt(dim)
    segq = seg.reshape(total, 1)
    segk = seg.reshape(1, total)

    def q_map(h, j, i):
        return (h, jnp.maximum(i, (j * tk) // tq), 0)

    def segq_map(h, j, i):
        return (jnp.maximum(i, (j * tk) // tq), 0)

    return pl.pallas_call(
        functools.partial(_bwd_kernel, tq=tq, tk=tk, scale=scale),
        out_shape=(
            jax.ShapeDtypeStruct((heads, total, dim), jnp.float32),
            jax.ShapeDtypeStruct((heads, total, dim), jnp.float32),
            jax.ShapeDtypeStruct((heads, total, dim), jnp.float32),
        ),
        grid=(heads, nk, nq),
        in_specs=[
            pl.BlockSpec((1, tq, dim), q_map),
            pl.BlockSpec((1, tk, dim), lambda h, j, i: (h, j, 0)),
            pl.BlockSpec((1, tk, dim), lambda h, j, i: (h, j, 0)),
            pl.BlockSpec((1, tq, dim), q_map),
            pl.BlockSpec((1, tq, 1), q_map),
            pl.BlockSpec((1, tq, 1), q_map),
            pl.BlockSpec((tq, 1), segq_map),
            pl.BlockSpec((1, tk), lambda h, j, i: (0, j)),
        ],
        out_specs=[
            pl.BlockSpec((1, total, dim), lambda h, j, i: (h, 0, 0)),
            pl.BlockSpec((1, tk, dim), lambda h, j, i: (h, j, 0)),
            pl.BlockSpec((1, tk, dim), lambda h, j, i: (h, j, 0)),
        ],
        cost_estimate=pl.CostEstimate(
            flops=5 * heads * total * total * dim,
            transcendentals=heads * total * total // 2,
            bytes_accessed=heads * total * dim * 24,
        ),
    )(q, k, v, do, lse, delta, segq, segk)


MESH_ID = pl.DeviceIdType.MESH


class Ring:
    def __init__(self, size, a_stride, b_stride):
        self.size = size
        self.half = size // 2
        self.a_stride = a_stride
        self.b_stride = b_stride

    def position(self, c):
        a = (c // self.a_stride) % self.half
        b = (c // self.b_stride) % 2
        return a + b * (2 * self.half - 1 - 2 * a)

    def device(self, pos):
        pos = pos % self.size
        b = pos // self.half
        a = pos + b * (2 * self.half - 1 - 2 * pos)
        return a * self.a_stride + b * self.b_stride


def ring_of(mesh):
    size = mesh.shape["ctx"]
    devices = list(mesh.devices.reshape(-1, size)[0])
    try:
        coords = [tuple(d.coords) for d in devices]
    except AttributeError:
        coords = None
    if coords and size % 2 == 0 and size >= 4:
        for b_stride in range(1, size):
            for a_stride in range(1, size):
                ring = Ring(size, a_stride, b_stride)
                order = [ring.device(p) for p in range(size)]
                if sorted(order) != list(range(size)):
                    continue
                hops = [
                    sum(abs(x - y) for x, y in zip(coords[order[p]], coords[order[(p + 1) % size]]))
                    for p in range(size)
                ]
                if max(hops) == 1:
                    return ring
    return Ring(size, 2, 1) if size % 2 == 0 and size >= 4 else None


def _barrier(g, left, right):
    barrier = pltpu.get_barrier_semaphore()
    for other in (left, right):
        pl.semaphore_signal(barrier, 1, device_id=(g, other), device_id_type=MESH_ID)
    pl.semaphore_wait(barrier, 2)


def _gather_kernel(x_ref, y_ref, own_sem, send_sem, recv_sem, *, ring, rows):
    n = ring.size
    half = rows // 2
    g = lax.axis_index("dp")
    c = lax.axis_index("ctx")
    pos = ring.position(c)
    right = ring.device(pos + 1)
    left = ring.device(pos + n - 1)
    own = pltpu.make_async_copy(x_ref, y_ref.at[pl.ds(c * rows, rows)], own_sem)
    own.start()
    _barrier(g, left, right)

    def link(direction, step, origin, source):
        offset = origin * rows + direction * half
        return pltpu.make_async_remote_copy(
            src_ref=source,
            dst_ref=y_ref.at[pl.ds(offset, half)],
            send_sem=send_sem.at[direction, step],
            recv_sem=recv_sem.at[direction, step],
            device_id=(g, right if direction == 0 else left),
            device_id_type=MESH_ID,
        )

    sent = []
    for step in range(n - 1):
        origins = (ring.device(pos - step + n), ring.device(pos + step))
        for direction in (0, 1):
            origin = origins[direction]
            if step == 0:
                source = x_ref.at[pl.ds(direction * half, half)]
            else:
                link(direction, step - 1, origin, None if False else y_ref.at[pl.ds(origin * rows + direction * half, half)]).wait_recv()
                source = y_ref.at[pl.ds(origin * rows + direction * half, half)]
            copy = link(direction, step, origin, source)
            copy.start()
            sent.append(copy)
    last = n - 2
    for direction, origin in ((0, ring.device(pos - last - 1 + n)), (1, ring.device(pos + last + 1))):
        link(direction, last, origin, y_ref.at[pl.ds(origin * rows + direction * half, half)]).wait_recv()
    for copy in sent:
        copy.wait_send()
    own.wait()


def ring_all_gather(x, ring, collective_id):
    rows, cols = x.shape
    n = ring.size
    return pl.pallas_call(
        functools.partial(_gather_kernel, ring=ring, rows=rows),
        out_shape=jax.ShapeDtypeStruct((n * rows, cols), x.dtype),
        in_specs=[pl.BlockSpec(memory_space=pl.ANY)],
        out_specs=pl.BlockSpec(memory_space=pl.ANY),
        scratch_shapes=[
            pltpu.SemaphoreType.DMA(()),
            pltpu.SemaphoreType.DMA((2, n - 1)),
            pltpu.SemaphoreType.DMA((2, n - 1)),
        ],
        compiler_params=pltpu.CompilerParams(collective_id=collective_id, has_side_effects=True),
    )(x)


def _scatter_kernel(p_ref, out_ref, recv_buf, send_buf, send_sem, recv_sem, *, ring, rows):
    n = ring.size
    half = rows // 2
    g = lax.axis_index("dp")
    c = lax.axis_index("ctx")
    pos = ring.position(c)
    right = ring.device(pos + 1)
    left = ring.device(pos + n - 1)
    _barrier(g, left, right)

    def link(direction, step):
        return pltpu.make_async_remote_copy(
            src_ref=send_buf.at[direction, step],
            dst_ref=recv_buf.at[direction, step],
            send_sem=send_sem.at[direction, step],
            recv_sem=recv_sem.at[direction, step],
            device_id=(g, right if direction == 0 else left),
            device_id_type=MESH_ID,
        )

    sent = []
    for step in range(n - 1):
        targets = (ring.device(pos - 1 - step + 2 * n), ring.device(pos + 1 + step))
        for direction in (0, 1):
            start = pl.multiple_of(targets[direction] * rows + direction * half, half)
            total = p_ref[pl.ds(start, half), :].astype(jnp.float32)
            if step > 0:
                link(direction, step - 1).wait_recv()
                total = total + recv_buf[direction, step - 1].astype(jnp.float32)
            send_buf[direction, step] = total.astype(send_buf.dtype)
            copy = link(direction, step)
            copy.start()
            sent.append(copy)
    for direction in (0, 1):
        link(direction, n - 2).wait_recv()
        start = pl.multiple_of(c * rows + direction * half, half)
        out_ref[pl.ds(direction * half, half), :] = (
            p_ref[pl.ds(start, half), :].astype(jnp.float32)
            + recv_buf[direction, n - 2].astype(jnp.float32)
        ).astype(out_ref.dtype)
    for copy in sent:
        copy.wait_send()


def ring_reduce_scatter(p, ring, collective_id, out_dtype=jnp.float32, wire=jnp.bfloat16):
    total_rows, cols = p.shape
    n = ring.size
    rows = total_rows // n
    half = rows // 2
    return pl.pallas_call(
        functools.partial(_scatter_kernel, ring=ring, rows=rows),
        out_shape=jax.ShapeDtypeStruct((rows, cols), out_dtype),
        in_specs=[pl.BlockSpec(memory_space=pltpu.VMEM)],
        out_specs=pl.BlockSpec(memory_space=pltpu.VMEM),
        scratch_shapes=[
            pltpu.VMEM((2, n - 1, half, cols), wire),
            pltpu.VMEM((2, n - 1, half, cols), wire),
            pltpu.SemaphoreType.DMA((2, n - 1)),
            pltpu.SemaphoreType.DMA((2, n - 1)),
        ],
        compiler_params=pltpu.CompilerParams(
            collective_id=collective_id, has_side_effects=True, vmem_limit_bytes=60 * 1024 * 1024
        ),
    )(p)


def block_moves(n_dp, n_ctx):
    count = n_dp * n_ctx
    return [(f, (f % n_dp) * n_ctx + f // n_dp) for f in range(count)]


def fetch_out_rows(w_out):
    n_dp = lax.axis_size("dp")
    n_ctx = lax.axis_size("ctx")
    moved = lax.ppermute(w_out.astype(jnp.bfloat16), ("dp", "ctx"), perm=block_moves(n_dp, n_ctx))
    return lax.all_gather(moved, "dp", axis=0, tiled=True)


def return_out_rows(grad_out_rows):
    n_dp = lax.axis_size("dp")
    n_ctx = lax.axis_size("ctx")
    part = lax.psum_scatter(grad_out_rows, "dp", scatter_dimension=0, tiled=True)
    back = [(b, a) for a, b in block_moves(n_dp, n_ctx)]
    return lax.ppermute(part, ("dp", "ctx"), perm=back)


def fetch_small(b_qkv, b_out, b_fc2, ln_gain, ln_shift, b_fc1):
    pieces = (b_qkv, b_out, b_fc2, ln_gain, ln_shift, b_fc1)
    packed = jnp.concatenate([p.astype(jnp.bfloat16) for p in pieces])
    table = lax.all_gather(packed, ("dp", "ctx"), axis=0, tiled=False)
    result = []
    offset = 0
    for p in pieces:
        result.append(table[:, offset : offset + p.shape[0]])
        offset += p.shape[0]
    return result


def fetch_heads(w_qkv, w_fc1, w_fc2):
    dp_count = lax.axis_size("dp")
    ctx_count = lax.axis_size("ctx")
    rows_piece = w_qkv.shape[0]
    head_width = D // ctx_count
    unit = FF // (dp_count * ctx_count)
    qkv_piece = w_qkv.astype(jnp.bfloat16).reshape(rows_piece, 3, ctx_count, head_width)
    fc1_piece = w_fc1.astype(jnp.bfloat16).reshape(rows_piece, dp_count, ctx_count, unit)
    qkv_sent, fc1_sent = (
        lax.all_to_all(qkv_piece, "ctx", split_axis=2, concat_axis=0, tiled=True),
        lax.all_to_all(fc1_piece, "ctx", split_axis=2, concat_axis=0, tiled=True),
    )
    qkv_cols, fc1_cols, fc2_rows = (
        lax.all_gather(qkv_sent, "dp", axis=0, tiled=True),
        lax.all_gather(fc1_sent, "dp", axis=0, tiled=True),
        lax.all_gather(w_fc2.astype(jnp.bfloat16), "dp", axis=0, tiled=True),
    )
    return (
        qkv_cols.reshape(D, 3 * head_width),
        fc1_cols.reshape(D, dp_count * unit),
        fc2_rows,
    )


def head_plan(
    ring,
    tokens,
    lengths,
    w_qkv,
    b_qkv,
    w_out,
    b_out,
    w_fc1,
    b_fc1,
    w_fc2,
    b_fc2,
    ln_gain,
    ln_shift,
    cotangent,
):
    rows_here = tokens.shape[0]
    rows_piece = w_qkv.shape[0]
    dp_count = lax.axis_size("dp")
    ctx_count = lax.axis_size("ctx")
    count = dp_count * ctx_count
    group = rows_here * ctx_count
    head_width = D // ctx_count
    local_heads = HEADS // ctx_count
    unit = FF // (dp_count * ctx_count)
    here = lax.axis_index("ctx")
    group_rows = jnp.arange(group, dtype=jnp.int32)
    seg, positions = segment_info(lengths[0], group_rows)
    cosine, sine = rotary_tables(positions)
    qkv_bias, out_bias, fc2_bias, gain_low, shift_low, fc1_table = fetch_small(
        b_qkv, b_out, b_fc2, ln_gain, ln_shift, b_fc1
    )
    qkv_bias = qkv_bias.reshape(3 * D)
    out_bias = out_bias.reshape(D)
    fc2_bias = fc2_bias.reshape(D)
    gain_low = gain_low.reshape(D)
    shift_low = shift_low.reshape(D)
    fc1_bias = lax.dynamic_index_in_dim(
        fc1_table.reshape(dp_count, ctx_count, unit), here, 1, keepdims=False
    ).reshape(dp_count * unit)
    out_rows = fetch_out_rows(w_out)
    qkv_cols, fc1_cols, fc2_rows = fetch_heads(w_qkv, w_fc1, w_fc2)
    gain32 = gain_low.astype(jnp.float32)
    shift32 = shift_low.astype(jnp.float32)
    inputs = tokens.astype(jnp.float32)
    normed, scaled, _ = norm_parts(inputs, gain32, shift32)
    tokens_group = ring_all_gather(tokens, ring, 0)
    dy_group = ring_all_gather(cotangent, ring, 1)
    hidden_group = norm_parts(tokens_group.astype(jnp.float32), gain32, shift32)[2].astype(
        jnp.bfloat16
    )
    bias_cols = lax.dynamic_slice_in_dim(
        qkv_bias.reshape(3, D), here * head_width, head_width, 1
    ).reshape(3 * head_width)
    qkv = jnp.dot(hidden_group, qkv_cols, preferred_element_type=jnp.float32) + bias_cols.astype(
        jnp.float32
    )
    shape = (group, local_heads, HEAD_DIM)
    query = rotate(qkv[:, :head_width].reshape(shape), cosine, sine).astype(jnp.bfloat16)
    keys = rotate(qkv[:, head_width : 2 * head_width].reshape(shape), cosine, sine).astype(
        jnp.bfloat16
    )
    values = qkv[:, 2 * head_width :].reshape(shape).astype(jnp.bfloat16)
    q_heads = query.transpose(1, 0, 2)
    k_heads = keys.transpose(1, 0, 2)
    v_heads = values.transpose(1, 0, 2)
    attended_heads, log_total = attention_forward(q_heads, k_heads, v_heads, seg)
    attended = attended_heads.transpose(1, 0, 2).reshape(group, head_width).astype(jnp.bfloat16)
    pre = jnp.dot(hidden_group, fc1_cols, preferred_element_type=jnp.float32) + fc1_bias.astype(
        jnp.float32
    )
    act = gelu_tanh(pre).astype(jnp.bfloat16)
    branches = ring_reduce_scatter(
        jnp.dot(attended, out_rows, preferred_element_type=jnp.float32)
        + jnp.dot(act, fc2_rows, preferred_element_type=jnp.float32),
        ring,
        2,
    )
    block_out = (
        inputs + branches + out_bias.astype(jnp.float32) + fc2_bias.astype(jnp.float32)
    ).astype(jnp.bfloat16)
    grad_out32 = cotangent.astype(jnp.float32)
    grad_b_fc2 = jnp.sum(grad_out32, axis=0)
    grad_fc2_part = jnp.einsum("tf,td->fd", act, dy_group, preferred_element_type=jnp.float32)
    d_act = jnp.einsum("td,fd->tf", dy_group, fc2_rows, preferred_element_type=jnp.float32)
    d_pre = (d_act * gelu_slope(pre)).astype(jnp.bfloat16)
    grad_fc1_part = jnp.einsum("td,tf->df", hidden_group, d_pre, preferred_element_type=jnp.float32)
    grad_bfc1_part = jnp.sum(d_pre.astype(jnp.float32), axis=0)
    grad_out_rows = jnp.einsum("tc,td->cd", attended, dy_group, preferred_element_type=jnp.float32)
    owned_w_out = return_out_rows(grad_out_rows)
    d_attended = (
        jnp.einsum("td,cd->tc", dy_group, out_rows, preferred_element_type=jnp.float32)
        .astype(jnp.bfloat16)
        .reshape(shape)
    )
    d_heads = d_attended.transpose(1, 0, 2)
    delta = jnp.sum(d_heads.astype(jnp.float32) * attended_heads, axis=2, keepdims=True)
    dq_heads, dk_heads, dv_heads = attention_backward(
        q_heads, k_heads, v_heads, d_heads, log_total, delta, seg
    )
    d_query = dq_heads.transpose(1, 0, 2)
    d_keys = dk_heads.transpose(1, 0, 2)
    d_values = dv_heads.transpose(1, 0, 2)
    d_query = rotate_back(d_query, cosine, sine).reshape(group, head_width)
    d_keys = rotate_back(d_keys, cosine, sine).reshape(group, head_width)
    d_qkv = jnp.concatenate([d_query, d_keys, d_values.reshape(group, head_width)], axis=1).astype(
        jnp.bfloat16
    )
    grad_qkv_part = jnp.einsum("td,tc->dc", hidden_group, d_qkv, preferred_element_type=jnp.float32)
    bias_part = jnp.sum(d_qkv.astype(jnp.float32), axis=0).reshape(3, head_width)
    d_hidden = ring_reduce_scatter(
        jnp.einsum("tc,dc->td", d_qkv, qkv_cols, preferred_element_type=jnp.float32)
        + jnp.einsum("tf,df->td", d_pre, fc1_cols, preferred_element_type=jnp.float32),
        ring,
        3,
    )
    grad_gain, grad_shift, d_inputs = norm_back(d_hidden, normed, scaled, gain32)
    grad_tokens = (grad_out32 + d_inputs).astype(jnp.bfloat16)
    weight_parts = jnp.concatenate([grad_qkv_part, grad_fc1_part], axis=1).astype(jnp.bfloat16)
    owned_parts = lax.psum_scatter(weight_parts, "dp", scatter_dimension=0, tiled=True)
    owned_qkv = owned_parts[:, : 3 * head_width].reshape(-1, 3, 1, head_width)
    owned_fc1 = owned_parts[:, 3 * head_width :].reshape(-1, dp_count, 1, unit)
    owned_fc2 = lax.psum_scatter(
        grad_fc2_part.astype(jnp.bfloat16), "dp", scatter_dimension=0, tiled=True
    ).astype(jnp.float32)
    split_qkv, split_fc1 = (
        lax.all_to_all(owned_qkv, "ctx", split_axis=0, concat_axis=2, tiled=True).astype(
            jnp.float32
        ),
        lax.all_to_all(owned_fc1, "ctx", split_axis=0, concat_axis=2, tiled=True).astype(
            jnp.float32
        ),
    )
    full_bqkv = lax.dynamic_update_slice_in_dim(
        jnp.zeros((3, D), jnp.float32), bias_part, here * head_width, 1
    )
    full_bfc1 = lax.dynamic_update_slice_in_dim(
        jnp.zeros((dp_count, ctx_count, unit), jnp.float32),
        grad_bfc1_part.reshape(dp_count, 1, unit),
        here,
        1,
    )
    small = jnp.concatenate(
        [
            full_bqkv.reshape(count, -1),
            grad_b_fc2.reshape(count, -1),
            grad_gain.reshape(count, -1),
            grad_shift.reshape(count, -1),
            full_bfc1.reshape(count, -1),
        ],
        axis=1,
    )
    width_small = small.shape[1]
    over_dp = lax.psum_scatter(
        small.reshape(dp_count, ctx_count * width_small), "dp", scatter_dimension=0, tiled=True
    )
    owned_small = lax.psum_scatter(
        over_dp.reshape(ctx_count, width_small), "ctx", scatter_dimension=0, tiled=True
    )[0]
    cuts = [0, 3 * D // count, D // count, D // count, D // count, FF // count]
    bounds = [sum(cuts[: i + 1]) for i in range(len(cuts))]
    owned_bqkv, owned_bout, owned_gain, owned_shift, owned_bfc1 = [
        owned_small[bounds[i] : bounds[i + 1]] for i in range(5)
    ]
    return (
        block_out,
        grad_tokens,
        split_qkv.reshape(rows_piece, 3 * D),
        owned_bqkv,
        owned_w_out,
        owned_bout,
        split_fc1.reshape(rows_piece, FF),
        owned_bfc1,
        owned_fc2,
        owned_bout,
        owned_gain,
        owned_shift,
    )


def body(
    ring,
    tokens,
    lengths,
    w_qkv,
    b_qkv,
    w_out,
    b_out,
    w_fc1,
    b_fc1,
    w_fc2,
    b_fc2,
    ln_gain,
    ln_shift,
    cotangent,
):
    return head_plan(
        ring,
        tokens,
        lengths,
        w_qkv,
        b_qkv,
        w_out,
        b_out,
        w_fc1,
        b_fc1,
        w_fc2,
        b_fc2,
        ln_gain,
        ln_shift,
        cotangent,
    )


def solution(mesh):
    in_specs = (
        P(("dp", "ctx"), None),
        P("dp", None),
        P(("dp", "ctx"), None),
        P(("dp", "ctx")),
        P(("dp", "ctx"), None),
        P(("dp", "ctx")),
        P(("dp", "ctx"), None),
        P(("dp", "ctx")),
        P(("dp", "ctx"), None),
        P(("dp", "ctx")),
        P(("dp", "ctx")),
        P(("dp", "ctx")),
        P(("dp", "ctx"), None),
    )
    out_specs = (
        P(("dp", "ctx"), None),
        P(("dp", "ctx"), None),
        P(("dp", "ctx"), None),
        P(("dp", "ctx")),
        P(("dp", "ctx"), None),
        P(("dp", "ctx")),
        P(("dp", "ctx"), None),
        P(("dp", "ctx")),
        P(("dp", "ctx"), None),
        P(("dp", "ctx")),
        P(("dp", "ctx")),
        P(("dp", "ctx")),
    )
    ring = ring_of(mesh)
    return jax.shard_map(functools.partial(body, ring), mesh=mesh, in_specs=in_specs, out_specs=out_specs, check_vma=False)
```

```python
import functools
import math

import jax
import jax.numpy as jnp
from jax import lax
from jax.experimental import pallas as pl
from jax.experimental.pallas import tpu as pltpu
from jax.sharding import PartitionSpec as P

D = 2048
HEADS = 32
HEAD_DIM = 64
ROT = 32
FF = 8192


EPS = 1e-05
GELU_COEF = math.sqrt(2.0 / math.pi)
NEGATIVE = -1e30


def norm_parts(inputs, gain, shift):
    mean = jnp.mean(inputs, axis=-1, keepdims=True)
    centred = inputs - mean
    var = jnp.mean(centred * centred, axis=-1, keepdims=True)
    scaled = lax.rsqrt(var + EPS)
    normed = centred * scaled
    return (normed, scaled, normed * gain + shift)


def norm_back(d_hidden, normed, scaled, gain32):
    grad_gain = jnp.sum(d_hidden * normed, axis=0)
    grad_shift = jnp.sum(d_hidden, axis=0)
    d_normed = d_hidden * gain32
    d_inputs = scaled * (
        d_normed
        - jnp.mean(d_normed, axis=-1, keepdims=True)
        - normed * jnp.mean(d_normed * normed, axis=-1, keepdims=True)
    )
    return (grad_gain, grad_shift, d_inputs)


def gelu_tanh(pre):
    return 0.5 * pre * (1.0 + jnp.tanh(GELU_COEF * (pre + 0.044715 * pre * pre * pre)))


def gelu_slope(pre):
    tangent = jnp.tanh(GELU_COEF * (pre + 0.044715 * pre * pre * pre))
    return 0.5 * (1.0 + tangent) + 0.5 * pre * (1.0 - tangent * tangent) * GELU_COEF * (
        1.0 + 3.0 * 0.044715 * pre * pre
    )


def rotary_tables(positions):
    half = ROT // 2
    freq = jnp.exp(jnp.arange(half, dtype=jnp.float32) * (-2.0 * math.log(10000.0) / ROT))
    angle = positions.astype(jnp.float32)[:, None] * freq[None, :]
    return (jnp.cos(angle)[:, None, :], jnp.sin(angle)[:, None, :])


def rotate(heads, cosine, sine):
    half = ROT // 2
    first = heads[..., :half]
    second = heads[..., half:ROT]
    return jnp.concatenate(
        [first * cosine - second * sine, second * cosine + first * sine, heads[..., ROT:]], axis=-1
    )


def rotate_back(grads, cosine, sine):
    half = ROT // 2
    first = grads[..., :half]
    second = grads[..., half:ROT]
    return jnp.concatenate(
        [first * cosine + second * sine, second * cosine - first * sine, grads[..., ROT:]], axis=-1
    )


def segment_info(lengths_row, rows):
    ends = jnp.cumsum(lengths_row)
    starts = ends - lengths_row
    seg = jnp.sum((rows[:, None] >= ends[None, :]).astype(jnp.int32), axis=1)
    onehot = seg[:, None] == jnp.arange(lengths_row.shape[0], dtype=jnp.int32)[None, :]
    first_rows = jnp.sum(jnp.where(onehot, starts[None, :], 0), axis=1)
    return (seg, rows - first_rows)


TRANS_B = (((1,), (1,)), ((), ()))


def _allowed(segq_ref, segk_ref, i, j, tq, tk):
    rows = i * tq + lax.broadcasted_iota(jnp.int32, (tq, tk), 0)
    cols = j * tk + lax.broadcasted_iota(jnp.int32, (tq, tk), 1)
    return (segq_ref[...] == segk_ref[...]) & (cols <= rows)


def _fwd_kernel(q_ref, k_ref, v_ref, segq_ref, segk_ref, o_ref, lse_ref, m_sc, l_sc, acc_sc, *, tq, tk, scale):
    i = pl.program_id(1)
    j = pl.program_id(2)

    @pl.when(j == 0)
    def _():
        m_sc[...] = jnp.full_like(m_sc, NEGATIVE)
        l_sc[...] = jnp.zeros_like(l_sc)
        acc_sc[...] = jnp.zeros_like(acc_sc)

    @pl.when(j * tk <= i * tq + tq - 1)
    def _():
        q = q_ref[0]
        k = k_ref[0]
        s = lax.dot_general(q, k, TRANS_B, preferred_element_type=jnp.float32) * scale
        allowed = _allowed(segq_ref, segk_ref, i, j, tq, tk)
        s = jnp.where(allowed, s, NEGATIVE)
        m_prev = m_sc[...]
        m_new = jnp.maximum(m_prev, jnp.max(s, axis=1, keepdims=True))
        factor = jnp.exp(m_prev - m_new)
        p = jnp.where(allowed, jnp.exp(s - m_new), 0.0)
        l_sc[...] = l_sc[...] * factor + jnp.sum(p, axis=1, keepdims=True)
        acc_sc[...] = acc_sc[...] * factor + jnp.dot(
            p.astype(jnp.bfloat16), v_ref[0], preferred_element_type=jnp.float32
        )
        m_sc[...] = m_new

    @pl.when(j == pl.num_programs(2) - 1)
    def _():
        total = l_sc[...]
        o_ref[0] = acc_sc[...] / total
        lse_ref[0] = m_sc[...] + jnp.log(total)


def attention_forward(q, k, v, seg, tq=512, tk=512):
    heads, total, dim = q.shape
    nq, nk = total // tq, total // tk
    scale = 1.0 / math.sqrt(dim)
    segq = seg.reshape(total, 1)
    segk = seg.reshape(1, total)

    def kv_map(h, i, j):
        return (h, jnp.minimum(j, (i * tq + tq - 1) // tk), 0)

    def segk_map(h, i, j):
        return (0, jnp.minimum(j, (i * tq + tq - 1) // tk))

    return pl.pallas_call(
        functools.partial(_fwd_kernel, tq=tq, tk=tk, scale=scale),
        out_shape=(
            jax.ShapeDtypeStruct((heads, total, dim), jnp.float32),
            jax.ShapeDtypeStruct((heads, total, 1), jnp.float32),
        ),
        grid=(heads, nq, nk),
        in_specs=[
            pl.BlockSpec((1, tq, dim), lambda h, i, j: (h, i, 0)),
            pl.BlockSpec((1, tk, dim), kv_map),
            pl.BlockSpec((1, tk, dim), kv_map),
            pl.BlockSpec((tq, 1), lambda h, i, j: (i, 0)),
            pl.BlockSpec((1, tk), segk_map),
        ],
        out_specs=[
            pl.BlockSpec((1, tq, dim), lambda h, i, j: (h, i, 0)),
            pl.BlockSpec((1, tq, 1), lambda h, i, j: (h, i, 0)),
        ],
        scratch_shapes=[
            pltpu.VMEM((tq, 1), jnp.float32),
            pltpu.VMEM((tq, 1), jnp.float32),
            pltpu.VMEM((tq, dim), jnp.float32),
        ],
        cost_estimate=pl.CostEstimate(
            flops=2 * heads * total * total * dim,
            transcendentals=heads * total * total // 2,
            bytes_accessed=heads * total * dim * 10,
        ),
    )(q, k, v, segq, segk)


def _bwd_kernel(q_ref, k_ref, v_ref, do_ref, lse_ref, delta_ref, segq_ref, segk_ref, dq_ref, dk_ref, dv_ref, *, tq, tk, scale):
    j = pl.program_id(1)
    i = pl.program_id(2)

    @pl.when((j == 0) & (i == 0))
    def _():
        dq_ref[...] = jnp.zeros_like(dq_ref)

    @pl.when(i == 0)
    def _():
        dk_ref[...] = jnp.zeros_like(dk_ref)
        dv_ref[...] = jnp.zeros_like(dv_ref)

    @pl.when(i * tq + tq - 1 >= j * tk)
    def _():
        q = q_ref[0]
        k = k_ref[0]
        do = do_ref[0]
        s = lax.dot_general(q, k, TRANS_B, preferred_element_type=jnp.float32) * scale
        allowed = _allowed(segq_ref, segk_ref, i, j, tq, tk)
        p = jnp.where(allowed, jnp.exp(s - lse_ref[0]), 0.0)
        dp = lax.dot_general(do, v_ref[0], TRANS_B, preferred_element_type=jnp.float32)
        ds = (p * (dp - delta_ref[0])).astype(jnp.bfloat16)
        dv_ref[0] += lax.dot(p.astype(jnp.bfloat16).T, do, preferred_element_type=jnp.float32)
        dk_ref[0] += lax.dot(ds.T, q, preferred_element_type=jnp.float32) * scale
        rows = pl.ds(pl.multiple_of(i * tq, tq), tq)
        dq_ref[0, rows, :] += lax.dot(ds, k, preferred_element_type=jnp.float32) * scale


def attention_backward(q, k, v, do, lse, delta, seg, tq=512, tk=512):
    heads, total, dim = q.shape
    nq, nk = total // tq, total // tk
    scale = 1.0 / math.sqrt(dim)
    segq = seg.reshape(total, 1)
    segk = seg.reshape(1, total)

    def q_map(h, j, i):
        return (h, jnp.maximum(i, (j * tk) // tq), 0)

    def segq_map(h, j, i):
        return (jnp.maximum(i, (j * tk) // tq), 0)

    return pl.pallas_call(
        functools.partial(_bwd_kernel, tq=tq, tk=tk, scale=scale),
        out_shape=(
            jax.ShapeDtypeStruct((heads, total, dim), jnp.float32),
            jax.ShapeDtypeStruct((heads, total, dim), jnp.float32),
            jax.ShapeDtypeStruct((heads, total, dim), jnp.float32),
        ),
        grid=(heads, nk, nq),
        in_specs=[
            pl.BlockSpec((1, tq, dim), q_map),
            pl.BlockSpec((1, tk, dim), lambda h, j, i: (h, j, 0)),
            pl.BlockSpec((1, tk, dim), lambda h, j, i: (h, j, 0)),
            pl.BlockSpec((1, tq, dim), q_map),
            pl.BlockSpec((1, tq, 1), q_map),
            pl.BlockSpec((1, tq, 1), q_map),
            pl.BlockSpec((tq, 1), segq_map),
            pl.BlockSpec((1, tk), lambda h, j, i: (0, j)),
        ],
        out_specs=[
            pl.BlockSpec((1, total, dim), lambda h, j, i: (h, 0, 0)),
            pl.BlockSpec((1, tk, dim), lambda h, j, i: (h, j, 0)),
            pl.BlockSpec((1, tk, dim), lambda h, j, i: (h, j, 0)),
        ],
        cost_estimate=pl.CostEstimate(
            flops=5 * heads * total * total * dim,
            transcendentals=heads * total * total // 2,
            bytes_accessed=heads * total * dim * 24,
        ),
    )(q, k, v, do, lse, delta, segq, segk)


MESH_ID = pl.DeviceIdType.MESH


class Ring:
    def __init__(self, size, a_stride, b_stride):
        self.size = size
        self.half = size // 2
        self.a_stride = a_stride
        self.b_stride = b_stride

    def position(self, c):
        a = (c // self.a_stride) % self.half
        b = (c // self.b_stride) % 2
        return a + b * (2 * self.half - 1 - 2 * a)

    def device(self, pos):
        pos = pos % self.size
        b = pos // self.half
        a = pos + b * (2 * self.half - 1 - 2 * pos)
        return a * self.a_stride + b * self.b_stride


def ring_of(mesh):
    size = mesh.shape["ctx"]
    devices = list(mesh.devices.reshape(-1, size)[0])
    try:
        coords = [tuple(d.coords) for d in devices]
    except AttributeError:
        coords = None
    if coords and size % 2 == 0 and size >= 4:
        for b_stride in range(1, size):
            for a_stride in range(1, size):
                ring = Ring(size, a_stride, b_stride)
                order = [ring.device(p) for p in range(size)]
                if sorted(order) != list(range(size)):
                    continue
                hops = [
                    sum(abs(x - y) for x, y in zip(coords[order[p]], coords[order[(p + 1) % size]]))
                    for p in range(size)
                ]
                if max(hops) == 1:
                    return ring
    return Ring(size, 2, 1) if size % 2 == 0 and size >= 4 else None


def _barrier(g, left, right):
    barrier = pltpu.get_barrier_semaphore()
    for other in (left, right):
        pl.semaphore_signal(barrier, 1, device_id=(g, other), device_id_type=MESH_ID)
    pl.semaphore_wait(barrier, 2)


def _gather_kernel(x_ref, y_ref, own_sem, send_sem, recv_sem, *, ring, rows):
    n = ring.size
    half = rows // 2
    g = lax.axis_index("dp")
    c = lax.axis_index("ctx")
    pos = ring.position(c)
    right = ring.device(pos + 1)
    left = ring.device(pos + n - 1)
    own = pltpu.make_async_copy(x_ref, y_ref.at[pl.ds(c * rows, rows)], own_sem)
    own.start()
    _barrier(g, left, right)

    def link(direction, step, origin, source):
        offset = origin * rows + direction * half
        return pltpu.make_async_remote_copy(
            src_ref=source,
            dst_ref=y_ref.at[pl.ds(offset, half)],
            send_sem=send_sem.at[direction, step],
            recv_sem=recv_sem.at[direction, step],
            device_id=(g, right if direction == 0 else left),
            device_id_type=MESH_ID,
        )

    sent = []
    for step in range(n - 1):
        origins = (ring.device(pos - step + n), ring.device(pos + step))
        for direction in (0, 1):
            origin = origins[direction]
            if step == 0:
                source = x_ref.at[pl.ds(direction * half, half)]
            else:
                link(direction, step - 1, origin, None if False else y_ref.at[pl.ds(origin * rows + direction * half, half)]).wait_recv()
                source = y_ref.at[pl.ds(origin * rows + direction * half, half)]
            copy = link(direction, step, origin, source)
            copy.start()
            sent.append(copy)
    last = n - 2
    for direction, origin in ((0, ring.device(pos - last - 1 + n)), (1, ring.device(pos + last + 1))):
        link(direction, last, origin, y_ref.at[pl.ds(origin * rows + direction * half, half)]).wait_recv()
    for copy in sent:
        copy.wait_send()
    own.wait()


def ring_all_gather(x, ring, collective_id):
    rows, cols = x.shape
    n = ring.size
    return pl.pallas_call(
        functools.partial(_gather_kernel, ring=ring, rows=rows),
        out_shape=jax.ShapeDtypeStruct((n * rows, cols), x.dtype),
        in_specs=[pl.BlockSpec(memory_space=pl.ANY)],
        out_specs=pl.BlockSpec(memory_space=pl.ANY),
        scratch_shapes=[
            pltpu.SemaphoreType.DMA(()),
            pltpu.SemaphoreType.DMA((2, n - 1)),
            pltpu.SemaphoreType.DMA((2, n - 1)),
        ],
        compiler_params=pltpu.CompilerParams(collective_id=collective_id, has_side_effects=True),
    )(x)


def _scatter_kernel(p_ref, out_ref, recv_buf, send_buf, send_sem, recv_sem, *, ring, rows):
    n = ring.size
    half = rows // 2
    g = lax.axis_index("dp")
    c = lax.axis_index("ctx")
    pos = ring.position(c)
    right = ring.device(pos + 1)
    left = ring.device(pos + n - 1)
    _barrier(g, left, right)

    def link(direction, step):
        return pltpu.make_async_remote_copy(
            src_ref=send_buf.at[direction, step],
            dst_ref=recv_buf.at[direction, step],
            send_sem=send_sem.at[direction, step],
            recv_sem=recv_sem.at[direction, step],
            device_id=(g, right if direction == 0 else left),
            device_id_type=MESH_ID,
        )

    sent = []
    for step in range(n - 1):
        targets = (ring.device(pos - 1 - step + 2 * n), ring.device(pos + 1 + step))
        for direction in (0, 1):
            start = pl.multiple_of(targets[direction] * rows + direction * half, half)
            total = p_ref[pl.ds(start, half), :].astype(jnp.float32)
            if step > 0:
                link(direction, step - 1).wait_recv()
                total = total + recv_buf[direction, step - 1].astype(jnp.float32)
            send_buf[direction, step] = total.astype(send_buf.dtype)
            copy = link(direction, step)
            copy.start()
            sent.append(copy)
    for direction in (0, 1):
        link(direction, n - 2).wait_recv()
        start = pl.multiple_of(c * rows + direction * half, half)
        out_ref[pl.ds(direction * half, half), :] = (
            p_ref[pl.ds(start, half), :].astype(jnp.float32)
            + recv_buf[direction, n - 2].astype(jnp.float32)
        ).astype(out_ref.dtype)
    for copy in sent:
        copy.wait_send()


def ring_reduce_scatter(p, ring, collective_id, out_dtype=jnp.float32, wire=jnp.bfloat16):
    total_rows, cols = p.shape
    n = ring.size
    rows = total_rows // n
    half = rows // 2
    return pl.pallas_call(
        functools.partial(_scatter_kernel, ring=ring, rows=rows),
        out_shape=jax.ShapeDtypeStruct((rows, cols), out_dtype),
        in_specs=[pl.BlockSpec(memory_space=pltpu.VMEM)],
        out_specs=pl.BlockSpec(memory_space=pltpu.VMEM),
        scratch_shapes=[
            pltpu.VMEM((2, n - 1, half, cols), wire),
            pltpu.VMEM((2, n - 1, half, cols), wire),
            pltpu.SemaphoreType.DMA((2, n - 1)),
            pltpu.SemaphoreType.DMA((2, n - 1)),
        ],
        compiler_params=pltpu.CompilerParams(
            collective_id=collective_id, has_side_effects=True, vmem_limit_bytes=60 * 1024 * 1024
        ),
    )(p)


def _exchange_kernel(x_ref, out_ref, own_sem, send_sem, recv_sem, *, everyone):
    n = x_ref.shape[0]
    g = lax.axis_index("dp")
    c = lax.axis_index("ctx")
    n_ctx = lax.axis_size("ctx")
    me = g * n_ctx + c if everyone else c

    def address(member):
        if everyone:
            return (member // n_ctx, member % n_ctx)
        return (g, member)

    own = pltpu.make_async_copy(x_ref.at[me], out_ref.at[me], own_sem)
    own.start()
    barrier = pltpu.get_barrier_semaphore()
    for offset in range(1, n):
        pl.semaphore_signal(
            barrier, 1, device_id=address((me + offset) % n), device_id_type=MESH_ID
        )
    pl.semaphore_wait(barrier, n - 1)

    def link(offset, source, target):
        return pltpu.make_async_remote_copy(
            src_ref=x_ref.at[target],
            dst_ref=out_ref.at[source],
            send_sem=send_sem.at[offset],
            recv_sem=recv_sem.at[offset],
            device_id=address(target),
            device_id_type=MESH_ID,
        )

    sent = []
    for offset in range(1, n):
        copy = link(offset, me, (me + offset) % n)
        copy.start()
        sent.append(copy)
    for offset in range(1, n):
        link(offset, (me + n - offset) % n, me).wait_recv()
    for copy in sent:
        copy.wait_send()
    own.wait()


def exchange(x, everyone, collective_id):
    n = x.shape[0]
    space = pltpu.VMEM
    return pl.pallas_call(
        functools.partial(_exchange_kernel, everyone=everyone),
        out_shape=jax.ShapeDtypeStruct(x.shape, x.dtype),
        in_specs=[pl.BlockSpec(memory_space=space)],
        out_specs=pl.BlockSpec(memory_space=space),
        scratch_shapes=[
            pltpu.SemaphoreType.DMA(()),
            pltpu.SemaphoreType.DMA((n,)),
            pltpu.SemaphoreType.DMA((n,)),
        ],
        compiler_params=pltpu.CompilerParams(collective_id=collective_id, has_side_effects=True),
    )(x)


def block_moves(n_dp, n_ctx):
    count = n_dp * n_ctx
    return [(f, (f % n_dp) * n_ctx + f // n_dp) for f in range(count)]


def fetch_out_rows(w_out):
    n_dp = lax.axis_size("dp")
    n_ctx = lax.axis_size("ctx")
    moved = lax.ppermute(w_out.astype(jnp.bfloat16), ("dp", "ctx"), perm=block_moves(n_dp, n_ctx))
    return lax.all_gather(moved, "dp", axis=0, tiled=True)


def return_out_rows(grad_out_rows):
    n_dp = lax.axis_size("dp")
    n_ctx = lax.axis_size("ctx")
    part = lax.psum_scatter(grad_out_rows, "dp", scatter_dimension=0, tiled=True)
    back = [(b, a) for a, b in block_moves(n_dp, n_ctx)]
    return lax.ppermute(part, ("dp", "ctx"), perm=back)


def pack_rows(vector, lanes):
    size = vector.shape[0]
    total = -(-size // (16 * lanes)) * 16 * lanes
    return jnp.pad(vector, (0, total - size)).reshape(-1, lanes)


def fetch_small(b_qkv, b_out, b_fc2, ln_gain, ln_shift, b_fc1):
    pieces = (b_qkv, b_out, b_fc2, ln_gain, ln_shift, b_fc1)
    count = lax.axis_size("dp") * lax.axis_size("ctx")
    packed = pack_rows(jnp.concatenate([p.astype(jnp.bfloat16) for p in pieces]), 128)
    table = exchange(jnp.broadcast_to(packed[None], (count,) + packed.shape), True, 4)
    table = table.reshape(count, -1)
    result = []
    offset = 0
    for p in pieces:
        result.append(table[:, offset : offset + p.shape[0]])
        offset += p.shape[0]
    return result


def reduce_small(small):
    count, width = small.shape
    packed = jax.vmap(lambda row: pack_rows(row, 128))(small)
    received = exchange(packed, True, 7)
    return jnp.sum(received, axis=0).reshape(-1)[:width]


def fetch_heads(w_qkv, w_fc1, w_fc2):
    dp_count = lax.axis_size("dp")
    ctx_count = lax.axis_size("ctx")
    rows_piece = w_qkv.shape[0]
    head_width = D // ctx_count
    unit = FF // (dp_count * ctx_count)
    qkv_piece = w_qkv.astype(jnp.bfloat16).reshape(rows_piece, 3, ctx_count, head_width)
    fc1_piece = w_fc1.astype(jnp.bfloat16).reshape(rows_piece, dp_count, ctx_count, unit)
    pieces = jnp.concatenate(
        [
            qkv_piece.transpose(2, 0, 1, 3).reshape(ctx_count, rows_piece, 3 * head_width),
            fc1_piece.transpose(2, 0, 1, 3).reshape(ctx_count, rows_piece, dp_count * unit),
        ],
        axis=2,
    )
    sent = exchange(pieces, False, 5).reshape(ctx_count * rows_piece, -1)
    cols, fc2_rows = (
        lax.all_gather(sent, "dp", axis=0, tiled=True),
        lax.all_gather(w_fc2.astype(jnp.bfloat16), "dp", axis=0, tiled=True),
    )
    return (cols, fc2_rows)


def return_heads(owned_parts):
    dp_count = lax.axis_size("dp")
    ctx_count = lax.axis_size("ctx")
    head_width = D // ctx_count
    unit = FF // (dp_count * ctx_count)
    rows_piece = owned_parts.shape[0] // ctx_count
    got = exchange(owned_parts.reshape(ctx_count, rows_piece, -1), False, 6)
    qkv = got[:, :, : 3 * head_width].reshape(ctx_count, rows_piece, 3, head_width)
    fc1 = got[:, :, 3 * head_width :].reshape(ctx_count, rows_piece, dp_count, unit)
    return (
        qkv.transpose(1, 2, 0, 3).reshape(rows_piece, 3 * D).astype(jnp.float32),
        fc1.transpose(1, 2, 0, 3).reshape(rows_piece, FF).astype(jnp.float32),
    )


def head_plan(
    ring,
    tokens,
    lengths,
    w_qkv,
    b_qkv,
    w_out,
    b_out,
    w_fc1,
    b_fc1,
    w_fc2,
    b_fc2,
    ln_gain,
    ln_shift,
    cotangent,
):
    rows_here = tokens.shape[0]
    rows_piece = w_qkv.shape[0]
    dp_count = lax.axis_size("dp")
    ctx_count = lax.axis_size("ctx")
    count = dp_count * ctx_count
    group = rows_here * ctx_count
    head_width = D // ctx_count
    local_heads = HEADS // ctx_count
    unit = FF // (dp_count * ctx_count)
    here = lax.axis_index("ctx")
    group_rows = jnp.arange(group, dtype=jnp.int32)
    seg, positions = segment_info(lengths[0], group_rows)
    cosine, sine = rotary_tables(positions)
    qkv_bias, out_bias, fc2_bias, gain_low, shift_low, fc1_table = fetch_small(
        b_qkv, b_out, b_fc2, ln_gain, ln_shift, b_fc1
    )
    qkv_bias = qkv_bias.reshape(3 * D)
    out_bias = out_bias.reshape(D)
    fc2_bias = fc2_bias.reshape(D)
    gain_low = gain_low.reshape(D)
    shift_low = shift_low.reshape(D)
    fc1_bias = lax.dynamic_index_in_dim(
        fc1_table.reshape(dp_count, ctx_count, unit), here, 1, keepdims=False
    ).reshape(dp_count * unit)
    out_rows = fetch_out_rows(w_out)
    cols, fc2_rows = fetch_heads(w_qkv, w_fc1, w_fc2)
    gain32 = gain_low.astype(jnp.float32)
    shift32 = shift_low.astype(jnp.float32)
    inputs = tokens.astype(jnp.float32)
    normed, scaled, _ = norm_parts(inputs, gain32, shift32)
    tokens_group = ring_all_gather(tokens, ring, 0)
    dy_group = ring_all_gather(cotangent, ring, 1)
    hidden_group = norm_parts(tokens_group.astype(jnp.float32), gain32, shift32)[2].astype(
        jnp.bfloat16
    )
    bias_cols = lax.dynamic_slice_in_dim(
        qkv_bias.reshape(3, D), here * head_width, head_width, 1
    ).reshape(3 * head_width)
    both = jnp.dot(hidden_group, cols, preferred_element_type=jnp.float32) + jnp.concatenate(
        [bias_cols, fc1_bias]
    ).astype(jnp.float32)
    qkv = both[:, : 3 * head_width]
    pre = both[:, 3 * head_width :]
    shape = (group, local_heads, HEAD_DIM)
    query = rotate(qkv[:, :head_width].reshape(shape), cosine, sine).astype(jnp.bfloat16)
    keys = rotate(qkv[:, head_width : 2 * head_width].reshape(shape), cosine, sine).astype(
        jnp.bfloat16
    )
    values = qkv[:, 2 * head_width :].reshape(shape).astype(jnp.bfloat16)
    q_heads = query.transpose(1, 0, 2)
    k_heads = keys.transpose(1, 0, 2)
    v_heads = values.transpose(1, 0, 2)
    attended_heads, log_total = attention_forward(q_heads, k_heads, v_heads, seg)
    attended = attended_heads.transpose(1, 0, 2).reshape(group, head_width).astype(jnp.bfloat16)
    act = gelu_tanh(pre).astype(jnp.bfloat16)
    branches = ring_reduce_scatter(
        jnp.dot(attended, out_rows, preferred_element_type=jnp.float32)
        + jnp.dot(act, fc2_rows, preferred_element_type=jnp.float32),
        ring,
        2,
    )
    block_out = (
        inputs + branches + out_bias.astype(jnp.float32) + fc2_bias.astype(jnp.float32)
    ).astype(jnp.bfloat16)
    grad_out32 = cotangent.astype(jnp.float32)
    grad_b_fc2 = jnp.sum(grad_out32, axis=0)
    grad_fc2_part = jnp.einsum("tf,td->fd", act, dy_group, preferred_element_type=jnp.float32)
    d_act = jnp.einsum("td,fd->tf", dy_group, fc2_rows, preferred_element_type=jnp.float32)
    d_pre = (d_act * gelu_slope(pre)).astype(jnp.bfloat16)
    grad_bfc1_part = jnp.sum(d_pre.astype(jnp.float32), axis=0)
    grad_out_rows = jnp.einsum("tc,td->cd", attended, dy_group, preferred_element_type=jnp.float32)
    owned_w_out = return_out_rows(grad_out_rows)
    d_attended = (
        jnp.einsum("td,cd->tc", dy_group, out_rows, preferred_element_type=jnp.float32)
        .astype(jnp.bfloat16)
        .reshape(shape)
    )
    d_heads = d_attended.transpose(1, 0, 2)
    delta = jnp.sum(d_heads.astype(jnp.float32) * attended_heads, axis=2, keepdims=True)
    dq_heads, dk_heads, dv_heads = attention_backward(
        q_heads, k_heads, v_heads, d_heads, log_total, delta, seg
    )
    d_query = dq_heads.transpose(1, 0, 2)
    d_keys = dk_heads.transpose(1, 0, 2)
    d_values = dv_heads.transpose(1, 0, 2)
    d_query = rotate_back(d_query, cosine, sine).reshape(group, head_width)
    d_keys = rotate_back(d_keys, cosine, sine).reshape(group, head_width)
    d_qkv = jnp.concatenate([d_query, d_keys, d_values.reshape(group, head_width)], axis=1).astype(
        jnp.bfloat16
    )
    d_both = jnp.concatenate([d_qkv, d_pre], axis=1)
    bias_part = jnp.sum(d_qkv.astype(jnp.float32), axis=0).reshape(3, head_width)
    d_hidden = ring_reduce_scatter(
        jnp.einsum("tc,dc->td", d_both, cols, preferred_element_type=jnp.float32), ring, 3
    )
    grad_gain, grad_shift, d_inputs = norm_back(d_hidden, normed, scaled, gain32)
    grad_tokens = (grad_out32 + d_inputs).astype(jnp.bfloat16)
    weight_parts = jnp.einsum(
        "td,tc->dc", hidden_group, d_both, preferred_element_type=jnp.float32
    ).astype(jnp.bfloat16)
    owned_parts = lax.psum_scatter(weight_parts, "dp", scatter_dimension=0, tiled=True)
    split_qkv, split_fc1 = return_heads(owned_parts)
    owned_fc2 = lax.psum_scatter(
        grad_fc2_part.astype(jnp.bfloat16), "dp", scatter_dimension=0, tiled=True
    ).astype(jnp.float32)
    full_bqkv = lax.dynamic_update_slice_in_dim(
        jnp.zeros((3, D), jnp.float32), bias_part, here * head_width, 1
    )
    full_bfc1 = lax.dynamic_update_slice_in_dim(
        jnp.zeros((dp_count, ctx_count, unit), jnp.float32),
        grad_bfc1_part.reshape(dp_count, 1, unit),
        here,
        1,
    )
    small = jnp.concatenate(
        [
            full_bqkv.reshape(count, -1),
            grad_b_fc2.reshape(count, -1),
            grad_gain.reshape(count, -1),
            grad_shift.reshape(count, -1),
            full_bfc1.reshape(count, -1),
        ],
        axis=1,
    )
    owned_small = reduce_small(small)
    cuts = [0, 3 * D // count, D // count, D // count, D // count, FF // count]
    bounds = [sum(cuts[: i + 1]) for i in range(len(cuts))]
    owned_bqkv, owned_bout, owned_gain, owned_shift, owned_bfc1 = [
        owned_small[bounds[i] : bounds[i + 1]] for i in range(5)
    ]
    return (
        block_out,
        grad_tokens,
        split_qkv.reshape(rows_piece, 3 * D),
        owned_bqkv,
        owned_w_out,
        owned_bout,
        split_fc1.reshape(rows_piece, FF),
        owned_bfc1,
        owned_fc2,
        owned_bout,
        owned_gain,
        owned_shift,
    )


def body(
    ring,
    tokens,
    lengths,
    w_qkv,
    b_qkv,
    w_out,
    b_out,
    w_fc1,
    b_fc1,
    w_fc2,
    b_fc2,
    ln_gain,
    ln_shift,
    cotangent,
):
    return head_plan(
        ring,
        tokens,
        lengths,
        w_qkv,
        b_qkv,
        w_out,
        b_out,
        w_fc1,
        b_fc1,
        w_fc2,
        b_fc2,
        ln_gain,
        ln_shift,
        cotangent,
    )


def solution(mesh):
    in_specs = (
        P(("dp", "ctx"), None),
        P("dp", None),
        P(("dp", "ctx"), None),
        P(("dp", "ctx")),
        P(("dp", "ctx"), None),
        P(("dp", "ctx")),
        P(("dp", "ctx"), None),
        P(("dp", "ctx")),
        P(("dp", "ctx"), None),
        P(("dp", "ctx")),
        P(("dp", "ctx")),
        P(("dp", "ctx")),
        P(("dp", "ctx"), None),
    )
    out_specs = (
        P(("dp", "ctx"), None),
        P(("dp", "ctx"), None),
        P(("dp", "ctx"), None),
        P(("dp", "ctx")),
        P(("dp", "ctx"), None),
        P(("dp", "ctx")),
        P(("dp", "ctx"), None),
        P(("dp", "ctx")),
        P(("dp", "ctx"), None),
        P(("dp", "ctx")),
        P(("dp", "ctx")),
        P(("dp", "ctx")),
    )
    ring = ring_of(mesh)
    return jax.shard_map(functools.partial(body, ring), mesh=mesh, in_specs=in_specs, out_specs=out_specs, check_vma=False)
```

```python
import functools
import math

import jax
import jax.numpy as jnp
from jax import lax
from jax.experimental import pallas as pl
from jax.experimental.pallas import tpu as pltpu
from jax.sharding import PartitionSpec as P

D = 2048
HEADS = 32
HEAD_DIM = 64
ROT = 32
FF = 8192


EPS = 1e-05
GELU_COEF = math.sqrt(2.0 / math.pi)
NEGATIVE = -1e30


def norm_parts(inputs, gain, shift):
    mean = jnp.mean(inputs, axis=-1, keepdims=True)
    centred = inputs - mean
    var = jnp.mean(centred * centred, axis=-1, keepdims=True)
    scaled = lax.rsqrt(var + EPS)
    normed = centred * scaled
    return (normed, scaled, normed * gain + shift)


def norm_back(d_hidden, normed, scaled, gain32):
    grad_gain = jnp.sum(d_hidden * normed, axis=0)
    grad_shift = jnp.sum(d_hidden, axis=0)
    d_normed = d_hidden * gain32
    d_inputs = scaled * (
        d_normed
        - jnp.mean(d_normed, axis=-1, keepdims=True)
        - normed * jnp.mean(d_normed * normed, axis=-1, keepdims=True)
    )
    return (grad_gain, grad_shift, d_inputs)


def gelu_tanh(pre):
    return 0.5 * pre * (1.0 + jnp.tanh(GELU_COEF * (pre + 0.044715 * pre * pre * pre)))


def gelu_slope(pre):
    tangent = jnp.tanh(GELU_COEF * (pre + 0.044715 * pre * pre * pre))
    return 0.5 * (1.0 + tangent) + 0.5 * pre * (1.0 - tangent * tangent) * GELU_COEF * (
        1.0 + 3.0 * 0.044715 * pre * pre
    )


def rotary_tables(positions):
    half = ROT // 2
    freq = jnp.exp(jnp.arange(half, dtype=jnp.float32) * (-2.0 * math.log(10000.0) / ROT))
    angle = positions.astype(jnp.float32)[:, None] * freq[None, :]
    return (jnp.cos(angle)[:, None, :], jnp.sin(angle)[:, None, :])


def rotate(heads, cosine, sine):
    half = ROT // 2
    first = heads[..., :half]
    second = heads[..., half:ROT]
    return jnp.concatenate(
        [first * cosine - second * sine, second * cosine + first * sine, heads[..., ROT:]], axis=-1
    )


def rotate_back(grads, cosine, sine):
    half = ROT // 2
    first = grads[..., :half]
    second = grads[..., half:ROT]
    return jnp.concatenate(
        [first * cosine + second * sine, second * cosine - first * sine, grads[..., ROT:]], axis=-1
    )


def segment_info(lengths_row, rows):
    ends = jnp.cumsum(lengths_row)
    starts = ends - lengths_row
    seg = jnp.sum((rows[:, None] >= ends[None, :]).astype(jnp.int32), axis=1)
    onehot = seg[:, None] == jnp.arange(lengths_row.shape[0], dtype=jnp.int32)[None, :]
    first_rows = jnp.sum(jnp.where(onehot, starts[None, :], 0), axis=1)
    return (seg, rows - first_rows)


TRANS_B = (((1,), (1,)), ((), ()))


def _allowed(segq_ref, segk_ref, i, j, tq, tk):
    rows = i * tq + lax.broadcasted_iota(jnp.int32, (tq, tk), 0)
    cols = j * tk + lax.broadcasted_iota(jnp.int32, (tq, tk), 1)
    return (segq_ref[...] == segk_ref[...]) & (cols <= rows)


def _fwd_kernel(q_ref, k_ref, v_ref, segq_ref, segk_ref, o_ref, lse_ref, m_sc, l_sc, acc_sc, *, tq, tk, scale):
    i = pl.program_id(1)
    j = pl.program_id(2)

    @pl.when(j == 0)
    def _():
        m_sc[...] = jnp.full_like(m_sc, NEGATIVE)
        l_sc[...] = jnp.zeros_like(l_sc)
        acc_sc[...] = jnp.zeros_like(acc_sc)

    @pl.when(j * tk <= i * tq + tq - 1)
    def _():
        q = q_ref[0]
        k = k_ref[0]
        s = lax.dot_general(q, k, TRANS_B, preferred_element_type=jnp.float32) * scale
        allowed = _allowed(segq_ref, segk_ref, i, j, tq, tk)
        s = jnp.where(allowed, s, NEGATIVE)
        m_prev = m_sc[...]
        m_new = jnp.maximum(m_prev, jnp.max(s, axis=1, keepdims=True))
        factor = jnp.exp(m_prev - m_new)
        p = jnp.where(allowed, jnp.exp(s - m_new), 0.0)
        l_sc[...] = l_sc[...] * factor + jnp.sum(p, axis=1, keepdims=True)
        acc_sc[...] = acc_sc[...] * factor + jnp.dot(
            p.astype(jnp.bfloat16), v_ref[0], preferred_element_type=jnp.float32
        )
        m_sc[...] = m_new

    @pl.when(j == pl.num_programs(2) - 1)
    def _():
        total = l_sc[...]
        o_ref[0] = acc_sc[...] / total
        lse_ref[0] = m_sc[...] + jnp.log(total)


def attention_forward(q, k, v, seg, tq=512, tk=512):
    heads, total, dim = q.shape
    nq, nk = total // tq, total // tk
    scale = 1.0 / math.sqrt(dim)
    segq = seg.reshape(total, 1)
    segk = seg.reshape(1, total)

    def kv_map(h, i, j):
        return (h, jnp.minimum(j, (i * tq + tq - 1) // tk), 0)

    def segk_map(h, i, j):
        return (0, jnp.minimum(j, (i * tq + tq - 1) // tk))

    return pl.pallas_call(
        functools.partial(_fwd_kernel, tq=tq, tk=tk, scale=scale),
        out_shape=(
            jax.ShapeDtypeStruct((heads, total, dim), jnp.float32),
            jax.ShapeDtypeStruct((heads, total, 1), jnp.float32),
        ),
        grid=(heads, nq, nk),
        in_specs=[
            pl.BlockSpec((1, tq, dim), lambda h, i, j: (h, i, 0)),
            pl.BlockSpec((1, tk, dim), kv_map),
            pl.BlockSpec((1, tk, dim), kv_map),
            pl.BlockSpec((tq, 1), lambda h, i, j: (i, 0)),
            pl.BlockSpec((1, tk), segk_map),
        ],
        out_specs=[
            pl.BlockSpec((1, tq, dim), lambda h, i, j: (h, i, 0)),
            pl.BlockSpec((1, tq, 1), lambda h, i, j: (h, i, 0)),
        ],
        scratch_shapes=[
            pltpu.VMEM((tq, 1), jnp.float32),
            pltpu.VMEM((tq, 1), jnp.float32),
            pltpu.VMEM((tq, dim), jnp.float32),
        ],
        cost_estimate=pl.CostEstimate(
            flops=2 * heads * total * total * dim,
            transcendentals=heads * total * total // 2,
            bytes_accessed=heads * total * dim * 10,
        ),
    )(q, k, v, segq, segk)


def _bwd_kernel(q_ref, k_ref, v_ref, do_ref, lse_ref, delta_ref, segq_ref, segk_ref, dq_ref, dk_ref, dv_ref, *, tq, tk, scale):
    j = pl.program_id(1)
    i = pl.program_id(2)

    @pl.when((j == 0) & (i == 0))
    def _():
        dq_ref[...] = jnp.zeros_like(dq_ref)

    @pl.when(i == 0)
    def _():
        dk_ref[...] = jnp.zeros_like(dk_ref)
        dv_ref[...] = jnp.zeros_like(dv_ref)

    @pl.when(i * tq + tq - 1 >= j * tk)
    def _():
        q = q_ref[0]
        k = k_ref[0]
        do = do_ref[0]
        s = lax.dot_general(q, k, TRANS_B, preferred_element_type=jnp.float32) * scale
        allowed = _allowed(segq_ref, segk_ref, i, j, tq, tk)
        p = jnp.where(allowed, jnp.exp(s - lse_ref[0]), 0.0)
        dp = lax.dot_general(do, v_ref[0], TRANS_B, preferred_element_type=jnp.float32)
        ds = (p * (dp - delta_ref[0])).astype(jnp.bfloat16)
        dv_ref[0] += lax.dot(p.astype(jnp.bfloat16).T, do, preferred_element_type=jnp.float32)
        dk_ref[0] += lax.dot(ds.T, q, preferred_element_type=jnp.float32) * scale
        rows = pl.ds(pl.multiple_of(i * tq, tq), tq)
        dq_ref[0, rows, :] += lax.dot(ds, k, preferred_element_type=jnp.float32) * scale


def attention_backward(q, k, v, do, lse, delta, seg, tq=512, tk=512):
    heads, total, dim = q.shape
    nq, nk = total // tq, total // tk
    scale = 1.0 / math.sqrt(dim)
    segq = seg.reshape(total, 1)
    segk = seg.reshape(1, total)

    def q_map(h, j, i):
        return (h, jnp.maximum(i, (j * tk) // tq), 0)

    def segq_map(h, j, i):
        return (jnp.maximum(i, (j * tk) // tq), 0)

    return pl.pallas_call(
        functools.partial(_bwd_kernel, tq=tq, tk=tk, scale=scale),
        out_shape=(
            jax.ShapeDtypeStruct((heads, total, dim), jnp.float32),
            jax.ShapeDtypeStruct((heads, total, dim), jnp.float32),
            jax.ShapeDtypeStruct((heads, total, dim), jnp.float32),
        ),
        grid=(heads, nk, nq),
        in_specs=[
            pl.BlockSpec((1, tq, dim), q_map),
            pl.BlockSpec((1, tk, dim), lambda h, j, i: (h, j, 0)),
            pl.BlockSpec((1, tk, dim), lambda h, j, i: (h, j, 0)),
            pl.BlockSpec((1, tq, dim), q_map),
            pl.BlockSpec((1, tq, 1), q_map),
            pl.BlockSpec((1, tq, 1), q_map),
            pl.BlockSpec((tq, 1), segq_map),
            pl.BlockSpec((1, tk), lambda h, j, i: (0, j)),
        ],
        out_specs=[
            pl.BlockSpec((1, total, dim), lambda h, j, i: (h, 0, 0)),
            pl.BlockSpec((1, tk, dim), lambda h, j, i: (h, j, 0)),
            pl.BlockSpec((1, tk, dim), lambda h, j, i: (h, j, 0)),
        ],
        cost_estimate=pl.CostEstimate(
            flops=5 * heads * total * total * dim,
            transcendentals=heads * total * total // 2,
            bytes_accessed=heads * total * dim * 24,
        ),
    )(q, k, v, do, lse, delta, segq, segk)


MESH_ID = pl.DeviceIdType.MESH


class Ring:
    def __init__(self, size, a_stride, b_stride):
        self.size = size
        self.half = size // 2
        self.a_stride = a_stride
        self.b_stride = b_stride

    def position(self, c):
        a = (c // self.a_stride) % self.half
        b = (c // self.b_stride) % 2
        return a + b * (2 * self.half - 1 - 2 * a)

    def device(self, pos):
        pos = pos % self.size
        b = pos // self.half
        a = pos + b * (2 * self.half - 1 - 2 * pos)
        return a * self.a_stride + b * self.b_stride


def ring_of(mesh):
    size = mesh.shape["ctx"]
    devices = list(mesh.devices.reshape(-1, size)[0])
    try:
        coords = [tuple(d.coords) for d in devices]
    except AttributeError:
        coords = None
    if coords and size % 2 == 0 and size >= 4:
        for b_stride in range(1, size):
            for a_stride in range(1, size):
                ring = Ring(size, a_stride, b_stride)
                order = [ring.device(p) for p in range(size)]
                if sorted(order) != list(range(size)):
                    continue
                hops = [
                    sum(abs(x - y) for x, y in zip(coords[order[p]], coords[order[(p + 1) % size]]))
                    for p in range(size)
                ]
                if max(hops) == 1:
                    return ring
    return Ring(size, 2, 1) if size % 2 == 0 and size >= 4 else None


def _barrier(g, left, right):
    barrier = pltpu.get_barrier_semaphore()
    for other in (left, right):
        pl.semaphore_signal(barrier, 1, device_id=(g, other), device_id_type=MESH_ID)
    pl.semaphore_wait(barrier, 2)


def _gather_kernel(x_ref, y_ref, own_sem, send_sem, recv_sem, *, ring, rows):
    n = ring.size
    half = rows // 2
    g = lax.axis_index("dp")
    c = lax.axis_index("ctx")
    pos = ring.position(c)
    right = ring.device(pos + 1)
    left = ring.device(pos + n - 1)
    own = pltpu.make_async_copy(x_ref, y_ref.at[pl.ds(c * rows, rows)], own_sem)
    own.start()
    _barrier(g, left, right)

    def link(direction, step, origin, source):
        offset = origin * rows + direction * half
        return pltpu.make_async_remote_copy(
            src_ref=source,
            dst_ref=y_ref.at[pl.ds(offset, half)],
            send_sem=send_sem.at[direction, step],
            recv_sem=recv_sem.at[direction, step],
            device_id=(g, right if direction == 0 else left),
            device_id_type=MESH_ID,
        )

    sent = []
    for step in range(n - 1):
        origins = (ring.device(pos - step + n), ring.device(pos + step))
        for direction in (0, 1):
            origin = origins[direction]
            if step == 0:
                source = x_ref.at[pl.ds(direction * half, half)]
            else:
                link(direction, step - 1, origin, None if False else y_ref.at[pl.ds(origin * rows + direction * half, half)]).wait_recv()
                source = y_ref.at[pl.ds(origin * rows + direction * half, half)]
            copy = link(direction, step, origin, source)
            copy.start()
            sent.append(copy)
    last = n - 2
    for direction, origin in ((0, ring.device(pos - last - 1 + n)), (1, ring.device(pos + last + 1))):
        link(direction, last, origin, y_ref.at[pl.ds(origin * rows + direction * half, half)]).wait_recv()
    for copy in sent:
        copy.wait_send()
    own.wait()


def ring_all_gather(x, ring, collective_id):
    rows, cols = x.shape
    n = ring.size
    return pl.pallas_call(
        functools.partial(_gather_kernel, ring=ring, rows=rows),
        out_shape=jax.ShapeDtypeStruct((n * rows, cols), x.dtype),
        in_specs=[pl.BlockSpec(memory_space=pl.ANY)],
        out_specs=pl.BlockSpec(memory_space=pl.ANY),
        scratch_shapes=[
            pltpu.SemaphoreType.DMA(()),
            pltpu.SemaphoreType.DMA((2, n - 1)),
            pltpu.SemaphoreType.DMA((2, n - 1)),
        ],
        compiler_params=pltpu.CompilerParams(collective_id=collective_id, has_side_effects=True),
    )(x)


def _scatter_kernel(p_ref, out_ref, recv_buf, send_buf, send_sem, recv_sem, *, ring, rows):
    n = ring.size
    half = rows // 2
    g = lax.axis_index("dp")
    c = lax.axis_index("ctx")
    pos = ring.position(c)
    right = ring.device(pos + 1)
    left = ring.device(pos + n - 1)
    _barrier(g, left, right)

    def link(direction, step):
        return pltpu.make_async_remote_copy(
            src_ref=send_buf.at[direction, step],
            dst_ref=recv_buf.at[direction, step],
            send_sem=send_sem.at[direction, step],
            recv_sem=recv_sem.at[direction, step],
            device_id=(g, right if direction == 0 else left),
            device_id_type=MESH_ID,
        )

    sent = []
    for step in range(n - 1):
        targets = (ring.device(pos - 1 - step + 2 * n), ring.device(pos + 1 + step))
        for direction in (0, 1):
            start = pl.multiple_of(targets[direction] * rows + direction * half, half)
            total = p_ref[pl.ds(start, half), :].astype(jnp.float32)
            if step > 0:
                link(direction, step - 1).wait_recv()
                total = total + recv_buf[direction, step - 1].astype(jnp.float32)
            send_buf[direction, step] = total.astype(send_buf.dtype)
            copy = link(direction, step)
            copy.start()
            sent.append(copy)
    for direction in (0, 1):
        link(direction, n - 2).wait_recv()
        start = pl.multiple_of(c * rows + direction * half, half)
        out_ref[pl.ds(direction * half, half), :] = (
            p_ref[pl.ds(start, half), :].astype(jnp.float32)
            + recv_buf[direction, n - 2].astype(jnp.float32)
        ).astype(out_ref.dtype)
    for copy in sent:
        copy.wait_send()


def ring_reduce_scatter(p, ring, collective_id, out_dtype=jnp.float32, wire=jnp.bfloat16):
    total_rows, cols = p.shape
    n = ring.size
    rows = total_rows // n
    half = rows // 2
    return pl.pallas_call(
        functools.partial(_scatter_kernel, ring=ring, rows=rows),
        out_shape=jax.ShapeDtypeStruct((rows, cols), out_dtype),
        in_specs=[pl.BlockSpec(memory_space=pltpu.VMEM)],
        out_specs=pl.BlockSpec(memory_space=pltpu.VMEM),
        scratch_shapes=[
            pltpu.VMEM((2, n - 1, half, cols), wire),
            pltpu.VMEM((2, n - 1, half, cols), wire),
            pltpu.SemaphoreType.DMA((2, n - 1)),
            pltpu.SemaphoreType.DMA((2, n - 1)),
        ],
        compiler_params=pltpu.CompilerParams(
            collective_id=collective_id, has_side_effects=True, vmem_limit_bytes=60 * 1024 * 1024
        ),
    )(p)


def _exchange_kernel(x_ref, out_ref, own_sem, send_sem, recv_sem, *, group):
    n = x_ref.shape[0]
    g = lax.axis_index("dp")
    c = lax.axis_index("ctx")
    n_ctx = lax.axis_size("ctx")
    me = {"all": g * n_ctx + c, "ctx": c, "dp": g}[group]

    def address(member):
        if group == "all":
            return (member // n_ctx, member % n_ctx)
        if group == "ctx":
            return (g, member)
        return (member, c)

    own = pltpu.make_async_copy(x_ref.at[me], out_ref.at[me], own_sem)
    own.start()
    barrier = pltpu.get_barrier_semaphore()
    for offset in range(1, n):
        pl.semaphore_signal(
            barrier, 1, device_id=address((me + offset) % n), device_id_type=MESH_ID
        )
    pl.semaphore_wait(barrier, n - 1)

    def link(offset, source, target):
        return pltpu.make_async_remote_copy(
            src_ref=x_ref.at[target],
            dst_ref=out_ref.at[source],
            send_sem=send_sem.at[offset],
            recv_sem=recv_sem.at[offset],
            device_id=address(target),
            device_id_type=MESH_ID,
        )

    sent = []
    for offset in range(1, n):
        copy = link(offset, me, (me + offset) % n)
        copy.start()
        sent.append(copy)
    for offset in range(1, n):
        link(offset, (me + n - offset) % n, me).wait_recv()
    for copy in sent:
        copy.wait_send()
    own.wait()


def exchange(x, group, collective_id):
    n = x.shape[0]
    space = pltpu.VMEM
    return pl.pallas_call(
        functools.partial(_exchange_kernel, group=group),
        out_shape=jax.ShapeDtypeStruct(x.shape, x.dtype),
        in_specs=[pl.BlockSpec(memory_space=space)],
        out_specs=pl.BlockSpec(memory_space=space),
        scratch_shapes=[
            pltpu.SemaphoreType.DMA(()),
            pltpu.SemaphoreType.DMA((n,)),
            pltpu.SemaphoreType.DMA((n,)),
        ],
        compiler_params=pltpu.CompilerParams(collective_id=collective_id, has_side_effects=True),
    )(x)


def block_moves(n_dp, n_ctx):
    count = n_dp * n_ctx
    return [(f, (f % n_dp) * n_ctx + f // n_dp) for f in range(count)]


def fetch_out_rows(w_out):
    n_dp = lax.axis_size("dp")
    n_ctx = lax.axis_size("ctx")
    moved = lax.ppermute(w_out.astype(jnp.bfloat16), ("dp", "ctx"), perm=block_moves(n_dp, n_ctx))
    return lax.all_gather(moved, "dp", axis=0, tiled=True)


def return_out_rows(grad_out_rows):
    n_dp = lax.axis_size("dp")
    n_ctx = lax.axis_size("ctx")
    part = lax.psum_scatter(grad_out_rows, "dp", scatter_dimension=0, tiled=True)
    back = [(b, a) for a, b in block_moves(n_dp, n_ctx)]
    return lax.ppermute(part, ("dp", "ctx"), perm=back)


def pack_rows(vector, lanes):
    size = vector.shape[0]
    total = -(-size // (16 * lanes)) * 16 * lanes
    return jnp.pad(vector, (0, total - size)).reshape(-1, lanes)


def fetch_small(b_qkv, b_out, b_fc2, ln_gain, ln_shift, b_fc1):
    pieces = (b_qkv, b_out, b_fc2, ln_gain, ln_shift, b_fc1)
    n_dp = lax.axis_size("dp")
    n_ctx = lax.axis_size("ctx")
    packed = pack_rows(jnp.concatenate([p.astype(jnp.bfloat16) for p in pieces]), 128)
    over_dp = exchange(jnp.broadcast_to(packed[None], (n_dp,) + packed.shape), "dp", 4)
    over_all = exchange(jnp.broadcast_to(over_dp[None], (n_ctx,) + over_dp.shape), "ctx", 8)
    table = over_all.transpose(1, 0, 2, 3).reshape(n_dp * n_ctx, -1)
    result = []
    offset = 0
    for p in pieces:
        result.append(table[:, offset : offset + p.shape[0]])
        offset += p.shape[0]
    return result


def reduce_small(small):
    n_dp = lax.axis_size("dp")
    n_ctx = lax.axis_size("ctx")
    count, width = small.shape
    packed = jax.vmap(lambda row: pack_rows(row, 128))(small)
    packed = packed.reshape((n_dp, n_ctx) + packed.shape[1:]).transpose(1, 0, 2, 3)
    over_ctx = jnp.sum(exchange(packed, "ctx", 7), axis=0)
    over_dp = jnp.sum(exchange(over_ctx, "dp", 9), axis=0)
    return over_dp.reshape(-1)[:width]


def fetch_heads(w_qkv, w_fc1, w_fc2):
    dp_count = lax.axis_size("dp")
    ctx_count = lax.axis_size("ctx")
    rows_piece = w_qkv.shape[0]
    head_width = D // ctx_count
    unit = FF // (dp_count * ctx_count)
    qkv_piece = w_qkv.astype(jnp.bfloat16).reshape(rows_piece, 3, ctx_count, head_width)
    fc1_piece = w_fc1.astype(jnp.bfloat16).reshape(rows_piece, dp_count, ctx_count, unit)
    pieces = jnp.concatenate(
        [
            qkv_piece.transpose(2, 0, 1, 3).reshape(ctx_count, rows_piece, 3 * head_width),
            fc1_piece.transpose(2, 0, 1, 3).reshape(ctx_count, rows_piece, dp_count * unit),
        ],
        axis=2,
    )
    sent = exchange(pieces, "ctx", 5).reshape(ctx_count * rows_piece, -1)
    cols, fc2_rows = (
        lax.all_gather(sent, "dp", axis=0, tiled=True),
        lax.all_gather(w_fc2.astype(jnp.bfloat16), "dp", axis=0, tiled=True),
    )
    return (cols, fc2_rows)


def return_heads(owned_parts):
    dp_count = lax.axis_size("dp")
    ctx_count = lax.axis_size("ctx")
    head_width = D // ctx_count
    unit = FF // (dp_count * ctx_count)
    rows_piece = owned_parts.shape[0] // ctx_count
    got = exchange(owned_parts.reshape(ctx_count, rows_piece, -1), "ctx", 6)
    qkv = got[:, :, : 3 * head_width].reshape(ctx_count, rows_piece, 3, head_width)
    fc1 = got[:, :, 3 * head_width :].reshape(ctx_count, rows_piece, dp_count, unit)
    return (
        qkv.transpose(1, 2, 0, 3).reshape(rows_piece, 3 * D).astype(jnp.float32),
        fc1.transpose(1, 2, 0, 3).reshape(rows_piece, FF).astype(jnp.float32),
    )


def head_plan(
    ring,
    tokens,
    lengths,
    w_qkv,
    b_qkv,
    w_out,
    b_out,
    w_fc1,
    b_fc1,
    w_fc2,
    b_fc2,
    ln_gain,
    ln_shift,
    cotangent,
):
    rows_here = tokens.shape[0]
    rows_piece = w_qkv.shape[0]
    dp_count = lax.axis_size("dp")
    ctx_count = lax.axis_size("ctx")
    count = dp_count * ctx_count
    group = rows_here * ctx_count
    head_width = D // ctx_count
    local_heads = HEADS // ctx_count
    unit = FF // (dp_count * ctx_count)
    here = lax.axis_index("ctx")
    group_rows = jnp.arange(group, dtype=jnp.int32)
    seg, positions = segment_info(lengths[0], group_rows)
    cosine, sine = rotary_tables(positions)
    qkv_bias, out_bias, fc2_bias, gain_low, shift_low, fc1_table = fetch_small(
        b_qkv, b_out, b_fc2, ln_gain, ln_shift, b_fc1
    )
    qkv_bias = qkv_bias.reshape(3 * D)
    out_bias = out_bias.reshape(D)
    fc2_bias = fc2_bias.reshape(D)
    gain_low = gain_low.reshape(D)
    shift_low = shift_low.reshape(D)
    fc1_bias = lax.dynamic_index_in_dim(
        fc1_table.reshape(dp_count, ctx_count, unit), here, 1, keepdims=False
    ).reshape(dp_count * unit)
    out_rows = fetch_out_rows(w_out)
    cols, fc2_rows = fetch_heads(w_qkv, w_fc1, w_fc2)
    gain32 = gain_low.astype(jnp.float32)
    shift32 = shift_low.astype(jnp.float32)
    inputs = tokens.astype(jnp.float32)
    normed, scaled, _ = norm_parts(inputs, gain32, shift32)
    tokens_group = ring_all_gather(tokens, ring, 0)
    dy_group = lax.all_gather(cotangent, "ctx", axis=0, tiled=True)
    hidden_group = norm_parts(tokens_group.astype(jnp.float32), gain32, shift32)[2].astype(
        jnp.bfloat16
    )
    bias_cols = lax.dynamic_slice_in_dim(
        qkv_bias.reshape(3, D), here * head_width, head_width, 1
    ).reshape(3 * head_width)
    both = jnp.dot(hidden_group, cols, preferred_element_type=jnp.float32) + jnp.concatenate(
        [bias_cols, fc1_bias]
    ).astype(jnp.float32)
    qkv = both[:, : 3 * head_width]
    pre = both[:, 3 * head_width :]
    shape = (group, local_heads, HEAD_DIM)
    query = rotate(qkv[:, :head_width].reshape(shape), cosine, sine).astype(jnp.bfloat16)
    keys = rotate(qkv[:, head_width : 2 * head_width].reshape(shape), cosine, sine).astype(
        jnp.bfloat16
    )
    values = qkv[:, 2 * head_width :].reshape(shape).astype(jnp.bfloat16)
    q_heads = query.transpose(1, 0, 2)
    k_heads = keys.transpose(1, 0, 2)
    v_heads = values.transpose(1, 0, 2)
    attended_heads, log_total = attention_forward(q_heads, k_heads, v_heads, seg)
    attended = attended_heads.transpose(1, 0, 2).reshape(group, head_width).astype(jnp.bfloat16)
    act = gelu_tanh(pre).astype(jnp.bfloat16)
    branches = ring_reduce_scatter(
        jnp.dot(attended, out_rows, preferred_element_type=jnp.float32)
        + jnp.dot(act, fc2_rows, preferred_element_type=jnp.float32),
        ring,
        2,
    )
    block_out = (
        inputs + branches + out_bias.astype(jnp.float32) + fc2_bias.astype(jnp.float32)
    ).astype(jnp.bfloat16)
    grad_out32 = cotangent.astype(jnp.float32)
    grad_b_fc2 = jnp.sum(grad_out32, axis=0)
    grad_fc2_part = jnp.einsum("tf,td->fd", act, dy_group, preferred_element_type=jnp.float32)
    d_act = jnp.einsum("td,fd->tf", dy_group, fc2_rows, preferred_element_type=jnp.float32)
    d_pre = (d_act * gelu_slope(pre)).astype(jnp.bfloat16)
    grad_bfc1_part = jnp.sum(d_pre.astype(jnp.float32), axis=0)
    grad_out_rows = jnp.einsum("tc,td->cd", attended, dy_group, preferred_element_type=jnp.float32)
    owned_w_out = return_out_rows(grad_out_rows)
    d_attended = (
        jnp.einsum("td,cd->tc", dy_group, out_rows, preferred_element_type=jnp.float32)
        .astype(jnp.bfloat16)
        .reshape(shape)
    )
    d_heads = d_attended.transpose(1, 0, 2)
    delta = jnp.sum(d_heads.astype(jnp.float32) * attended_heads, axis=2, keepdims=True)
    dq_heads, dk_heads, dv_heads = attention_backward(
        q_heads, k_heads, v_heads, d_heads, log_total, delta, seg
    )
    d_query = dq_heads.transpose(1, 0, 2)
    d_keys = dk_heads.transpose(1, 0, 2)
    d_values = dv_heads.transpose(1, 0, 2)
    d_query = rotate_back(d_query, cosine, sine).reshape(group, head_width)
    d_keys = rotate_back(d_keys, cosine, sine).reshape(group, head_width)
    d_qkv = jnp.concatenate([d_query, d_keys, d_values.reshape(group, head_width)], axis=1).astype(
        jnp.bfloat16
    )
    d_both = jnp.concatenate([d_qkv, d_pre], axis=1)
    bias_part = jnp.sum(d_qkv.astype(jnp.float32), axis=0).reshape(3, head_width)
    d_hidden = ring_reduce_scatter(
        jnp.einsum("tc,dc->td", d_both, cols, preferred_element_type=jnp.float32), ring, 3
    )
    grad_gain, grad_shift, d_inputs = norm_back(d_hidden, normed, scaled, gain32)
    grad_tokens = (grad_out32 + d_inputs).astype(jnp.bfloat16)
    weight_parts = jnp.einsum(
        "td,tc->dc", hidden_group, d_both, preferred_element_type=jnp.float32
    ).astype(jnp.bfloat16)
    owned_parts = lax.psum_scatter(weight_parts, "dp", scatter_dimension=0, tiled=True)
    split_qkv, split_fc1 = return_heads(owned_parts)
    owned_fc2 = lax.psum_scatter(
        grad_fc2_part.astype(jnp.bfloat16), "dp", scatter_dimension=0, tiled=True
    ).astype(jnp.float32)
    full_bqkv = lax.dynamic_update_slice_in_dim(
        jnp.zeros((3, D), jnp.float32), bias_part, here * head_width, 1
    )
    full_bfc1 = lax.dynamic_update_slice_in_dim(
        jnp.zeros((dp_count, ctx_count, unit), jnp.float32),
        grad_bfc1_part.reshape(dp_count, 1, unit),
        here,
        1,
    )
    small = jnp.concatenate(
        [
            full_bqkv.reshape(count, -1),
            grad_b_fc2.reshape(count, -1),
            grad_gain.reshape(count, -1),
            grad_shift.reshape(count, -1),
            full_bfc1.reshape(count, -1),
        ],
        axis=1,
    )
    owned_small = reduce_small(small)
    cuts = [0, 3 * D // count, D // count, D // count, D // count, FF // count]
    bounds = [sum(cuts[: i + 1]) for i in range(len(cuts))]
    owned_bqkv, owned_bout, owned_gain, owned_shift, owned_bfc1 = [
        owned_small[bounds[i] : bounds[i + 1]] for i in range(5)
    ]
    return (
        block_out,
        grad_tokens,
        split_qkv.reshape(rows_piece, 3 * D),
        owned_bqkv,
        owned_w_out,
        owned_bout,
        split_fc1.reshape(rows_piece, FF),
        owned_bfc1,
        owned_fc2,
        owned_bout,
        owned_gain,
        owned_shift,
    )


def body(
    ring,
    tokens,
    lengths,
    w_qkv,
    b_qkv,
    w_out,
    b_out,
    w_fc1,
    b_fc1,
    w_fc2,
    b_fc2,
    ln_gain,
    ln_shift,
    cotangent,
):
    return head_plan(
        ring,
        tokens,
        lengths,
        w_qkv,
        b_qkv,
        w_out,
        b_out,
        w_fc1,
        b_fc1,
        w_fc2,
        b_fc2,
        ln_gain,
        ln_shift,
        cotangent,
    )


def solution(mesh):
    in_specs = (
        P(("dp", "ctx"), None),
        P("dp", None),
        P(("dp", "ctx"), None),
        P(("dp", "ctx")),
        P(("dp", "ctx"), None),
        P(("dp", "ctx")),
        P(("dp", "ctx"), None),
        P(("dp", "ctx")),
        P(("dp", "ctx"), None),
        P(("dp", "ctx")),
        P(("dp", "ctx")),
        P(("dp", "ctx")),
        P(("dp", "ctx"), None),
    )
    out_specs = (
        P(("dp", "ctx"), None),
        P(("dp", "ctx"), None),
        P(("dp", "ctx"), None),
        P(("dp", "ctx")),
        P(("dp", "ctx"), None),
        P(("dp", "ctx")),
        P(("dp", "ctx"), None),
        P(("dp", "ctx")),
        P(("dp", "ctx"), None),
        P(("dp", "ctx")),
        P(("dp", "ctx")),
        P(("dp", "ctx")),
    )
    ring = ring_of(mesh)
    return jax.shard_map(functools.partial(body, ring), mesh=mesh, in_specs=in_specs, out_specs=out_specs, check_vma=False)
```

```python
import functools
import math

import jax
import jax.numpy as jnp
from jax import lax
from jax.experimental import pallas as pl
from jax.experimental.pallas import tpu as pltpu
from jax.sharding import PartitionSpec as P

D = 2048
HEADS = 32
HEAD_DIM = 64
ROT = 32
FF = 8192


EPS = 1e-05
GELU_COEF = math.sqrt(2.0 / math.pi)
NEGATIVE = -1e30


def norm_parts(inputs, gain, shift):
    mean = jnp.mean(inputs, axis=-1, keepdims=True)
    centred = inputs - mean
    var = jnp.mean(centred * centred, axis=-1, keepdims=True)
    scaled = lax.rsqrt(var + EPS)
    normed = centred * scaled
    return (normed, scaled, normed * gain + shift)


def norm_back(d_hidden, normed, scaled, gain32):
    grad_gain = jnp.sum(d_hidden * normed, axis=0)
    grad_shift = jnp.sum(d_hidden, axis=0)
    d_normed = d_hidden * gain32
    d_inputs = scaled * (
        d_normed
        - jnp.mean(d_normed, axis=-1, keepdims=True)
        - normed * jnp.mean(d_normed * normed, axis=-1, keepdims=True)
    )
    return (grad_gain, grad_shift, d_inputs)


def gelu_tanh(pre):
    return 0.5 * pre * (1.0 + jnp.tanh(GELU_COEF * (pre + 0.044715 * pre * pre * pre)))


def gelu_slope(pre):
    tangent = jnp.tanh(GELU_COEF * (pre + 0.044715 * pre * pre * pre))
    return 0.5 * (1.0 + tangent) + 0.5 * pre * (1.0 - tangent * tangent) * GELU_COEF * (
        1.0 + 3.0 * 0.044715 * pre * pre
    )


def rotary_tables(positions):
    half = ROT // 2
    freq = jnp.exp(jnp.arange(half, dtype=jnp.float32) * (-2.0 * math.log(10000.0) / ROT))
    angle = positions.astype(jnp.float32)[:, None] * freq[None, :]
    return (jnp.cos(angle)[:, None, :], jnp.sin(angle)[:, None, :])


def rotate(heads, cosine, sine):
    half = ROT // 2
    first = heads[..., :half]
    second = heads[..., half:ROT]
    return jnp.concatenate(
        [first * cosine - second * sine, second * cosine + first * sine, heads[..., ROT:]], axis=-1
    )


def rotate_back(grads, cosine, sine):
    half = ROT // 2
    first = grads[..., :half]
    second = grads[..., half:ROT]
    return jnp.concatenate(
        [first * cosine + second * sine, second * cosine - first * sine, grads[..., ROT:]], axis=-1
    )


def segment_info(lengths_row, rows):
    ends = jnp.cumsum(lengths_row)
    starts = ends - lengths_row
    seg = jnp.sum((rows[:, None] >= ends[None, :]).astype(jnp.int32), axis=1)
    onehot = seg[:, None] == jnp.arange(lengths_row.shape[0], dtype=jnp.int32)[None, :]
    first_rows = jnp.sum(jnp.where(onehot, starts[None, :], 0), axis=1)
    return (seg, rows - first_rows)


TRANS_B = (((1,), (1,)), ((), ()))


def _allowed(segq_ref, segk_ref, i, j, tq, tk):
    rows = i * tq + lax.broadcasted_iota(jnp.int32, (tq, tk), 0)
    cols = j * tk + lax.broadcasted_iota(jnp.int32, (tq, tk), 1)
    return (segq_ref[...] == segk_ref[...]) & (cols <= rows)


def _fwd_kernel(q_ref, k_ref, v_ref, segq_ref, segk_ref, o_ref, lse_ref, m_sc, l_sc, acc_sc, *, tq, tk, scale):
    i = pl.program_id(1)
    j = pl.program_id(2)

    @pl.when(j == 0)
    def _():
        m_sc[...] = jnp.full_like(m_sc, NEGATIVE)
        l_sc[...] = jnp.zeros_like(l_sc)
        acc_sc[...] = jnp.zeros_like(acc_sc)

    @pl.when(j * tk <= i * tq + tq - 1)
    def _():
        q = q_ref[0]
        k = k_ref[0]
        s = lax.dot_general(q, k, TRANS_B, preferred_element_type=jnp.float32) * scale
        allowed = _allowed(segq_ref, segk_ref, i, j, tq, tk)
        s = jnp.where(allowed, s, NEGATIVE)
        m_prev = m_sc[...]
        m_new = jnp.maximum(m_prev, jnp.max(s, axis=1, keepdims=True))
        factor = jnp.exp(m_prev - m_new)
        p = jnp.where(allowed, jnp.exp(s - m_new), 0.0)
        l_sc[...] = l_sc[...] * factor + jnp.sum(p, axis=1, keepdims=True)
        acc_sc[...] = acc_sc[...] * factor + jnp.dot(
            p.astype(jnp.bfloat16), v_ref[0], preferred_element_type=jnp.float32
        )
        m_sc[...] = m_new

    @pl.when(j == pl.num_programs(2) - 1)
    def _():
        total = l_sc[...]
        o_ref[0] = acc_sc[...] / total
        lse_ref[0] = m_sc[...] + jnp.log(total)


def attention_forward(q, k, v, seg, tq=512, tk=512):
    heads, total, dim = q.shape
    nq, nk = total // tq, total // tk
    scale = 1.0 / math.sqrt(dim)
    segq = seg.reshape(total, 1)
    segk = seg.reshape(1, total)

    def kv_map(h, i, j):
        return (h, jnp.minimum(j, (i * tq + tq - 1) // tk), 0)

    def segk_map(h, i, j):
        return (0, jnp.minimum(j, (i * tq + tq - 1) // tk))

    return pl.pallas_call(
        functools.partial(_fwd_kernel, tq=tq, tk=tk, scale=scale),
        out_shape=(
            jax.ShapeDtypeStruct((heads, total, dim), jnp.float32),
            jax.ShapeDtypeStruct((heads, total, 1), jnp.float32),
        ),
        grid=(heads, nq, nk),
        in_specs=[
            pl.BlockSpec((1, tq, dim), lambda h, i, j: (h, i, 0)),
            pl.BlockSpec((1, tk, dim), kv_map),
            pl.BlockSpec((1, tk, dim), kv_map),
            pl.BlockSpec((tq, 1), lambda h, i, j: (i, 0)),
            pl.BlockSpec((1, tk), segk_map),
        ],
        out_specs=[
            pl.BlockSpec((1, tq, dim), lambda h, i, j: (h, i, 0)),
            pl.BlockSpec((1, tq, 1), lambda h, i, j: (h, i, 0)),
        ],
        scratch_shapes=[
            pltpu.VMEM((tq, 1), jnp.float32),
            pltpu.VMEM((tq, 1), jnp.float32),
            pltpu.VMEM((tq, dim), jnp.float32),
        ],
        cost_estimate=pl.CostEstimate(
            flops=2 * heads * total * total * dim,
            transcendentals=heads * total * total // 2,
            bytes_accessed=heads * total * dim * 10,
        ),
    )(q, k, v, segq, segk)


def _bwd_kernel(q_ref, k_ref, v_ref, do_ref, lse_ref, delta_ref, segq_ref, segk_ref, dq_ref, dk_ref, dv_ref, *, tq, tk, scale):
    j = pl.program_id(1)
    i = pl.program_id(2)

    @pl.when((j == 0) & (i == 0))
    def _():
        dq_ref[...] = jnp.zeros_like(dq_ref)

    @pl.when(i == 0)
    def _():
        dk_ref[...] = jnp.zeros_like(dk_ref)
        dv_ref[...] = jnp.zeros_like(dv_ref)

    @pl.when(i * tq + tq - 1 >= j * tk)
    def _():
        q = q_ref[0]
        k = k_ref[0]
        do = do_ref[0]
        s = lax.dot_general(q, k, TRANS_B, preferred_element_type=jnp.float32) * scale
        allowed = _allowed(segq_ref, segk_ref, i, j, tq, tk)
        p = jnp.where(allowed, jnp.exp(s - lse_ref[0]), 0.0)
        dp = lax.dot_general(do, v_ref[0], TRANS_B, preferred_element_type=jnp.float32)
        ds = (p * (dp - delta_ref[0])).astype(jnp.bfloat16)
        dv_ref[0] += lax.dot(p.astype(jnp.bfloat16).T, do, preferred_element_type=jnp.float32)
        dk_ref[0] += lax.dot(ds.T, q, preferred_element_type=jnp.float32) * scale
        rows = pl.ds(pl.multiple_of(i * tq, tq), tq)
        dq_ref[0, rows, :] += lax.dot(ds, k, preferred_element_type=jnp.float32) * scale


def attention_backward(q, k, v, do, lse, delta, seg, tq=512, tk=512):
    heads, total, dim = q.shape
    nq, nk = total // tq, total // tk
    scale = 1.0 / math.sqrt(dim)
    segq = seg.reshape(total, 1)
    segk = seg.reshape(1, total)

    def q_map(h, j, i):
        return (h, jnp.maximum(i, (j * tk) // tq), 0)

    def segq_map(h, j, i):
        return (jnp.maximum(i, (j * tk) // tq), 0)

    return pl.pallas_call(
        functools.partial(_bwd_kernel, tq=tq, tk=tk, scale=scale),
        out_shape=(
            jax.ShapeDtypeStruct((heads, total, dim), jnp.float32),
            jax.ShapeDtypeStruct((heads, total, dim), jnp.float32),
            jax.ShapeDtypeStruct((heads, total, dim), jnp.float32),
        ),
        grid=(heads, nk, nq),
        in_specs=[
            pl.BlockSpec((1, tq, dim), q_map),
            pl.BlockSpec((1, tk, dim), lambda h, j, i: (h, j, 0)),
            pl.BlockSpec((1, tk, dim), lambda h, j, i: (h, j, 0)),
            pl.BlockSpec((1, tq, dim), q_map),
            pl.BlockSpec((1, tq, 1), q_map),
            pl.BlockSpec((1, tq, 1), q_map),
            pl.BlockSpec((tq, 1), segq_map),
            pl.BlockSpec((1, tk), lambda h, j, i: (0, j)),
        ],
        out_specs=[
            pl.BlockSpec((1, total, dim), lambda h, j, i: (h, 0, 0)),
            pl.BlockSpec((1, tk, dim), lambda h, j, i: (h, j, 0)),
            pl.BlockSpec((1, tk, dim), lambda h, j, i: (h, j, 0)),
        ],
        cost_estimate=pl.CostEstimate(
            flops=5 * heads * total * total * dim,
            transcendentals=heads * total * total // 2,
            bytes_accessed=heads * total * dim * 24,
        ),
    )(q, k, v, do, lse, delta, segq, segk)


MESH_ID = pl.DeviceIdType.MESH


class Ring:
    def __init__(self, size, a_stride, b_stride):
        self.size = size
        self.half = size // 2
        self.a_stride = a_stride
        self.b_stride = b_stride

    def position(self, c):
        a = (c // self.a_stride) % self.half
        b = (c // self.b_stride) % 2
        return a + b * (2 * self.half - 1 - 2 * a)

    def device(self, pos):
        pos = pos % self.size
        b = pos // self.half
        a = pos + b * (2 * self.half - 1 - 2 * pos)
        return a * self.a_stride + b * self.b_stride


def ring_of(mesh):
    size = mesh.shape["ctx"]
    devices = list(mesh.devices.reshape(-1, size)[0])
    try:
        coords = [tuple(d.coords) for d in devices]
    except AttributeError:
        coords = None
    if coords and size % 2 == 0 and size >= 4:
        for b_stride in range(1, size):
            for a_stride in range(1, size):
                ring = Ring(size, a_stride, b_stride)
                order = [ring.device(p) for p in range(size)]
                if sorted(order) != list(range(size)):
                    continue
                hops = [
                    sum(abs(x - y) for x, y in zip(coords[order[p]], coords[order[(p + 1) % size]]))
                    for p in range(size)
                ]
                if max(hops) == 1:
                    return ring
    return Ring(size, 2, 1) if size % 2 == 0 and size >= 4 else None


def _barrier(g, left, right):
    barrier = pltpu.get_barrier_semaphore()
    for other in (left, right):
        pl.semaphore_signal(barrier, 1, device_id=(g, other), device_id_type=MESH_ID)
    pl.semaphore_wait(barrier, 2)


def _gather_kernel(x_ref, y_ref, own_sem, send_sem, recv_sem, *, ring, rows):
    n = ring.size
    half = rows // 2
    g = lax.axis_index("dp")
    c = lax.axis_index("ctx")
    pos = ring.position(c)
    right = ring.device(pos + 1)
    left = ring.device(pos + n - 1)
    own = pltpu.make_async_copy(x_ref, y_ref.at[pl.ds(c * rows, rows)], own_sem)
    own.start()
    _barrier(g, left, right)

    def link(direction, step, origin, source):
        offset = origin * rows + direction * half
        return pltpu.make_async_remote_copy(
            src_ref=source,
            dst_ref=y_ref.at[pl.ds(offset, half)],
            send_sem=send_sem.at[direction, step],
            recv_sem=recv_sem.at[direction, step],
            device_id=(g, right if direction == 0 else left),
            device_id_type=MESH_ID,
        )

    sent = []
    for step in range(n - 1):
        origins = (ring.device(pos - step + n), ring.device(pos + step))
        for direction in (0, 1):
            origin = origins[direction]
            if step == 0:
                source = x_ref.at[pl.ds(direction * half, half)]
            else:
                link(direction, step - 1, origin, None if False else y_ref.at[pl.ds(origin * rows + direction * half, half)]).wait_recv()
                source = y_ref.at[pl.ds(origin * rows + direction * half, half)]
            copy = link(direction, step, origin, source)
            copy.start()
            sent.append(copy)
    last = n - 2
    for direction, origin in ((0, ring.device(pos - last - 1 + n)), (1, ring.device(pos + last + 1))):
        link(direction, last, origin, y_ref.at[pl.ds(origin * rows + direction * half, half)]).wait_recv()
    for copy in sent:
        copy.wait_send()
    own.wait()


def ring_all_gather(x, ring, collective_id):
    rows, cols = x.shape
    n = ring.size
    return pl.pallas_call(
        functools.partial(_gather_kernel, ring=ring, rows=rows),
        out_shape=jax.ShapeDtypeStruct((n * rows, cols), x.dtype),
        in_specs=[pl.BlockSpec(memory_space=pl.ANY)],
        out_specs=pl.BlockSpec(memory_space=pl.ANY),
        scratch_shapes=[
            pltpu.SemaphoreType.DMA(()),
            pltpu.SemaphoreType.DMA((2, n - 1)),
            pltpu.SemaphoreType.DMA((2, n - 1)),
        ],
        compiler_params=pltpu.CompilerParams(collective_id=collective_id, has_side_effects=True),
    )(x)


def _scatter_kernel(p_ref, out_ref, recv_buf, send_buf, send_sem, recv_sem, *, ring, rows):
    n = ring.size
    half = rows // 2
    g = lax.axis_index("dp")
    c = lax.axis_index("ctx")
    pos = ring.position(c)
    right = ring.device(pos + 1)
    left = ring.device(pos + n - 1)
    _barrier(g, left, right)

    def link(direction, step):
        return pltpu.make_async_remote_copy(
            src_ref=send_buf.at[direction, step],
            dst_ref=recv_buf.at[direction, step],
            send_sem=send_sem.at[direction, step],
            recv_sem=recv_sem.at[direction, step],
            device_id=(g, right if direction == 0 else left),
            device_id_type=MESH_ID,
        )

    sent = []
    for step in range(n - 1):
        targets = (ring.device(pos - 1 - step + 2 * n), ring.device(pos + 1 + step))
        for direction in (0, 1):
            start = pl.multiple_of(targets[direction] * rows + direction * half, half)
            total = p_ref[pl.ds(start, half), :].astype(jnp.float32)
            if step > 0:
                link(direction, step - 1).wait_recv()
                total = total + recv_buf[direction, step - 1].astype(jnp.float32)
            send_buf[direction, step] = total.astype(send_buf.dtype)
            copy = link(direction, step)
            copy.start()
            sent.append(copy)
    for direction in (0, 1):
        link(direction, n - 2).wait_recv()
        start = pl.multiple_of(c * rows + direction * half, half)
        out_ref[pl.ds(direction * half, half), :] = (
            p_ref[pl.ds(start, half), :].astype(jnp.float32)
            + recv_buf[direction, n - 2].astype(jnp.float32)
        ).astype(out_ref.dtype)
    for copy in sent:
        copy.wait_send()


def ring_reduce_scatter(p, ring, collective_id, out_dtype=jnp.float32, wire=jnp.bfloat16):
    total_rows, cols = p.shape
    n = ring.size
    rows = total_rows // n
    half = rows // 2
    return pl.pallas_call(
        functools.partial(_scatter_kernel, ring=ring, rows=rows),
        out_shape=jax.ShapeDtypeStruct((rows, cols), out_dtype),
        in_specs=[pl.BlockSpec(memory_space=pltpu.VMEM)],
        out_specs=pl.BlockSpec(memory_space=pltpu.VMEM),
        scratch_shapes=[
            pltpu.VMEM((2, n - 1, half, cols), wire),
            pltpu.VMEM((2, n - 1, half, cols), wire),
            pltpu.SemaphoreType.DMA((2, n - 1)),
            pltpu.SemaphoreType.DMA((2, n - 1)),
        ],
        compiler_params=pltpu.CompilerParams(
            collective_id=collective_id, has_side_effects=True, vmem_limit_bytes=60 * 1024 * 1024
        ),
    )(p)


def _exchange_kernel(x_ref, out_ref, own_sem, send_sem, recv_sem, *, group):
    n = x_ref.shape[0]
    g = lax.axis_index("dp")
    c = lax.axis_index("ctx")
    n_ctx = lax.axis_size("ctx")
    me = {"all": g * n_ctx + c, "ctx": c, "dp": g}[group]

    def address(member):
        if group == "all":
            return (member // n_ctx, member % n_ctx)
        if group == "ctx":
            return (g, member)
        return (member, c)

    own = pltpu.make_async_copy(x_ref.at[me], out_ref.at[me], own_sem)
    own.start()
    barrier = pltpu.get_barrier_semaphore()
    for offset in range(1, n):
        pl.semaphore_signal(
            barrier, 1, device_id=address((me + offset) % n), device_id_type=MESH_ID
        )
    pl.semaphore_wait(barrier, n - 1)

    def link(offset, source, target):
        return pltpu.make_async_remote_copy(
            src_ref=x_ref.at[target],
            dst_ref=out_ref.at[source],
            send_sem=send_sem.at[offset],
            recv_sem=recv_sem.at[offset],
            device_id=address(target),
            device_id_type=MESH_ID,
        )

    sent = []
    for offset in range(1, n):
        copy = link(offset, me, (me + offset) % n)
        copy.start()
        sent.append(copy)
    for offset in range(1, n):
        link(offset, (me + n - offset) % n, me).wait_recv()
    for copy in sent:
        copy.wait_send()
    own.wait()


def exchange(x, group, collective_id):
    n = x.shape[0]
    space = pltpu.VMEM
    return pl.pallas_call(
        functools.partial(_exchange_kernel, group=group),
        out_shape=jax.ShapeDtypeStruct(x.shape, x.dtype),
        in_specs=[pl.BlockSpec(memory_space=space)],
        out_specs=pl.BlockSpec(memory_space=space),
        scratch_shapes=[
            pltpu.SemaphoreType.DMA(()),
            pltpu.SemaphoreType.DMA((n,)),
            pltpu.SemaphoreType.DMA((n,)),
        ],
        compiler_params=pltpu.CompilerParams(collective_id=collective_id, has_side_effects=True),
    )(x)


def block_moves(n_dp, n_ctx):
    count = n_dp * n_ctx
    return [(f, (f % n_dp) * n_ctx + f // n_dp) for f in range(count)]


def fetch_out_rows(w_out):
    n_dp = lax.axis_size("dp")
    n_ctx = lax.axis_size("ctx")
    moved = lax.ppermute(w_out.astype(jnp.bfloat16), ("dp", "ctx"), perm=block_moves(n_dp, n_ctx))
    return lax.all_gather(moved, "dp", axis=0, tiled=True)


def return_out_rows(grad_out_rows):
    n_dp = lax.axis_size("dp")
    n_ctx = lax.axis_size("ctx")
    part = lax.psum_scatter(grad_out_rows, "dp", scatter_dimension=0, tiled=True)
    back = [(b, a) for a, b in block_moves(n_dp, n_ctx)]
    return lax.ppermute(part, ("dp", "ctx"), perm=back)


def pack_rows(vector, lanes):
    size = vector.shape[0]
    total = -(-size // (16 * lanes)) * 16 * lanes
    return jnp.pad(vector, (0, total - size)).reshape(-1, lanes)


def fetch_small(b_qkv, b_out, b_fc2, ln_gain, ln_shift, b_fc1):
    pieces = (b_qkv, b_out, b_fc2, ln_gain, ln_shift, b_fc1)
    n_dp = lax.axis_size("dp")
    n_ctx = lax.axis_size("ctx")
    packed = pack_rows(jnp.concatenate([p.astype(jnp.bfloat16) for p in pieces]), 128)
    over_dp = exchange(jnp.broadcast_to(packed[None], (n_dp,) + packed.shape), "dp", 4)
    over_all = exchange(jnp.broadcast_to(over_dp[None], (n_ctx,) + over_dp.shape), "ctx", 8)
    table = over_all.transpose(1, 0, 2, 3).reshape(n_dp * n_ctx, -1)
    result = []
    offset = 0
    for p in pieces:
        result.append(table[:, offset : offset + p.shape[0]])
        offset += p.shape[0]
    return result


def reduce_small(small):
    n_dp = lax.axis_size("dp")
    n_ctx = lax.axis_size("ctx")
    count, width = small.shape
    packed = jax.vmap(lambda row: pack_rows(row, 128))(small)
    packed = packed.reshape((n_dp, n_ctx) + packed.shape[1:]).transpose(1, 0, 2, 3)
    over_ctx = jnp.sum(exchange(packed, "ctx", 7), axis=0)
    over_dp = jnp.sum(exchange(over_ctx, "dp", 9), axis=0)
    return over_dp.reshape(-1)[:width]


def fetch_heads(w_qkv, w_fc1, w_fc2):
    dp_count = lax.axis_size("dp")
    ctx_count = lax.axis_size("ctx")
    rows_piece = w_qkv.shape[0]
    head_width = D // ctx_count
    unit = FF // (dp_count * ctx_count)
    qkv_piece = w_qkv.astype(jnp.bfloat16).reshape(rows_piece, 3, ctx_count, head_width)
    fc1_piece = w_fc1.astype(jnp.bfloat16).reshape(rows_piece, dp_count, ctx_count, unit)
    pieces = jnp.concatenate(
        [
            qkv_piece.transpose(2, 0, 1, 3).reshape(ctx_count, rows_piece, 3 * head_width),
            fc1_piece.transpose(2, 0, 1, 3).reshape(ctx_count, rows_piece, dp_count * unit),
        ],
        axis=2,
    )
    sent = exchange(pieces, "ctx", 5).reshape(ctx_count * rows_piece, -1)
    cols, fc2_rows = (
        lax.all_gather(sent, "dp", axis=0, tiled=True),
        lax.all_gather(w_fc2.astype(jnp.bfloat16), "dp", axis=0, tiled=True),
    )
    return (cols, fc2_rows)


def return_heads(owned_parts):
    dp_count = lax.axis_size("dp")
    ctx_count = lax.axis_size("ctx")
    head_width = D // ctx_count
    unit = FF // (dp_count * ctx_count)
    rows_piece = owned_parts.shape[0] // ctx_count
    got = exchange(owned_parts.reshape(ctx_count, rows_piece, -1), "ctx", 6)
    qkv = got[:, :, : 3 * head_width].reshape(ctx_count, rows_piece, 3, head_width)
    fc1 = got[:, :, 3 * head_width :].reshape(ctx_count, rows_piece, dp_count, unit)
    return (
        qkv.transpose(1, 2, 0, 3).reshape(rows_piece, 3 * D).astype(jnp.float32),
        fc1.transpose(1, 2, 0, 3).reshape(rows_piece, FF).astype(jnp.float32),
    )


def head_plan(
    ring,
    tokens,
    lengths,
    w_qkv,
    b_qkv,
    w_out,
    b_out,
    w_fc1,
    b_fc1,
    w_fc2,
    b_fc2,
    ln_gain,
    ln_shift,
    cotangent,
):
    rows_here = tokens.shape[0]
    rows_piece = w_qkv.shape[0]
    dp_count = lax.axis_size("dp")
    ctx_count = lax.axis_size("ctx")
    count = dp_count * ctx_count
    group = rows_here * ctx_count
    head_width = D // ctx_count
    local_heads = HEADS // ctx_count
    unit = FF // (dp_count * ctx_count)
    here = lax.axis_index("ctx")
    group_rows = jnp.arange(group, dtype=jnp.int32)
    seg, positions = segment_info(lengths[0], group_rows)
    cosine, sine = rotary_tables(positions)
    qkv_bias, out_bias, fc2_bias, gain_low, shift_low, fc1_table = fetch_small(
        b_qkv, b_out, b_fc2, ln_gain, ln_shift, b_fc1
    )
    qkv_bias = qkv_bias.reshape(3 * D)
    out_bias = out_bias.reshape(D)
    fc2_bias = fc2_bias.reshape(D)
    gain_low = gain_low.reshape(D)
    shift_low = shift_low.reshape(D)
    fc1_bias = lax.dynamic_index_in_dim(
        fc1_table.reshape(dp_count, ctx_count, unit), here, 1, keepdims=False
    ).reshape(dp_count * unit)
    out_rows = fetch_out_rows(w_out)
    cols, fc2_rows = fetch_heads(w_qkv, w_fc1, w_fc2)
    gain32 = gain_low.astype(jnp.float32)
    shift32 = shift_low.astype(jnp.float32)
    inputs = tokens.astype(jnp.float32)
    normed, scaled, _ = norm_parts(inputs, gain32, shift32)
    tokens_group = ring_all_gather(tokens, ring, 0)
    dy_group = lax.all_gather(cotangent, "ctx", axis=0, tiled=True)
    hidden_group = norm_parts(tokens_group.astype(jnp.float32), gain32, shift32)[2].astype(
        jnp.bfloat16
    )
    bias_cols = lax.dynamic_slice_in_dim(
        qkv_bias.reshape(3, D), here * head_width, head_width, 1
    ).reshape(3 * head_width)
    both = jnp.dot(hidden_group, cols, preferred_element_type=jnp.float32) + jnp.concatenate(
        [bias_cols, fc1_bias]
    ).astype(jnp.float32)
    qkv = both[:, : 3 * head_width]
    pre = both[:, 3 * head_width :]
    shape = (group, local_heads, HEAD_DIM)
    query = rotate(qkv[:, :head_width].reshape(shape), cosine, sine).astype(jnp.bfloat16)
    keys = rotate(qkv[:, head_width : 2 * head_width].reshape(shape), cosine, sine).astype(
        jnp.bfloat16
    )
    values = qkv[:, 2 * head_width :].reshape(shape).astype(jnp.bfloat16)
    q_heads = query.transpose(1, 0, 2)
    k_heads = keys.transpose(1, 0, 2)
    v_heads = values.transpose(1, 0, 2)
    attended_heads, log_total = attention_forward(q_heads, k_heads, v_heads, seg)
    attended = attended_heads.transpose(1, 0, 2).reshape(group, head_width).astype(jnp.bfloat16)
    act = gelu_tanh(pre).astype(jnp.bfloat16)
    partial = (
        jnp.dot(attended, out_rows, preferred_element_type=jnp.float32)
        + jnp.dot(act, fc2_rows, preferred_element_type=jnp.float32)
    ).astype(jnp.bfloat16)
    partial, q_heads = lax.optimization_barrier((partial, q_heads))
    branches = lax.psum_scatter(partial, "ctx", scatter_dimension=0, tiled=True).astype(
        jnp.float32
    )
    block_out = (
        inputs + branches + out_bias.astype(jnp.float32) + fc2_bias.astype(jnp.float32)
    ).astype(jnp.bfloat16)
    grad_out32 = cotangent.astype(jnp.float32)
    grad_b_fc2 = jnp.sum(grad_out32, axis=0)
    grad_fc2_part = jnp.einsum("tf,td->fd", act, dy_group, preferred_element_type=jnp.float32)
    d_act = jnp.einsum("td,fd->tf", dy_group, fc2_rows, preferred_element_type=jnp.float32)
    d_pre = (d_act * gelu_slope(pre)).astype(jnp.bfloat16)
    grad_bfc1_part = jnp.sum(d_pre.astype(jnp.float32), axis=0)
    grad_out_rows = jnp.einsum("tc,td->cd", attended, dy_group, preferred_element_type=jnp.float32)
    branches, grad_out_rows, grad_fc2_part = lax.optimization_barrier(
        (branches, grad_out_rows, grad_fc2_part)
    )
    owned_w_out = return_out_rows(grad_out_rows)
    d_attended = (
        jnp.einsum("td,cd->tc", dy_group, out_rows, preferred_element_type=jnp.float32)
        .astype(jnp.bfloat16)
        .reshape(shape)
    )
    d_heads = d_attended.transpose(1, 0, 2)
    delta = jnp.sum(d_heads.astype(jnp.float32) * attended_heads, axis=2, keepdims=True)
    dq_heads, dk_heads, dv_heads = attention_backward(
        q_heads, k_heads, v_heads, d_heads, log_total, delta, seg
    )
    d_query = dq_heads.transpose(1, 0, 2)
    d_keys = dk_heads.transpose(1, 0, 2)
    d_values = dv_heads.transpose(1, 0, 2)
    d_query = rotate_back(d_query, cosine, sine).reshape(group, head_width)
    d_keys = rotate_back(d_keys, cosine, sine).reshape(group, head_width)
    d_qkv = jnp.concatenate([d_query, d_keys, d_values.reshape(group, head_width)], axis=1).astype(
        jnp.bfloat16
    )
    d_both = jnp.concatenate([d_qkv, d_pre], axis=1)
    bias_part = jnp.sum(d_qkv.astype(jnp.float32), axis=0).reshape(3, head_width)
    d_hidden = ring_reduce_scatter(
        jnp.einsum("tc,dc->td", d_both, cols, preferred_element_type=jnp.float32), ring, 3
    )
    grad_gain, grad_shift, d_inputs = norm_back(d_hidden, normed, scaled, gain32)
    grad_tokens = (grad_out32 + d_inputs).astype(jnp.bfloat16)
    weight_parts = jnp.einsum(
        "td,tc->dc", hidden_group, d_both, preferred_element_type=jnp.float32
    ).astype(jnp.bfloat16)
    owned_parts = lax.psum_scatter(weight_parts, "dp", scatter_dimension=0, tiled=True)
    split_qkv, split_fc1 = return_heads(owned_parts)
    owned_fc2 = lax.psum_scatter(
        grad_fc2_part.astype(jnp.bfloat16), "dp", scatter_dimension=0, tiled=True
    ).astype(jnp.float32)
    full_bqkv = lax.dynamic_update_slice_in_dim(
        jnp.zeros((3, D), jnp.float32), bias_part, here * head_width, 1
    )
    full_bfc1 = lax.dynamic_update_slice_in_dim(
        jnp.zeros((dp_count, ctx_count, unit), jnp.float32),
        grad_bfc1_part.reshape(dp_count, 1, unit),
        here,
        1,
    )
    small = jnp.concatenate(
        [
            full_bqkv.reshape(count, -1),
            grad_b_fc2.reshape(count, -1),
            grad_gain.reshape(count, -1),
            grad_shift.reshape(count, -1),
            full_bfc1.reshape(count, -1),
        ],
        axis=1,
    )
    owned_small = reduce_small(small)
    cuts = [0, 3 * D // count, D // count, D // count, D // count, FF // count]
    bounds = [sum(cuts[: i + 1]) for i in range(len(cuts))]
    owned_bqkv, owned_bout, owned_gain, owned_shift, owned_bfc1 = [
        owned_small[bounds[i] : bounds[i + 1]] for i in range(5)
    ]
    return (
        block_out,
        grad_tokens,
        split_qkv.reshape(rows_piece, 3 * D),
        owned_bqkv,
        owned_w_out,
        owned_bout,
        split_fc1.reshape(rows_piece, FF),
        owned_bfc1,
        owned_fc2,
        owned_bout,
        owned_gain,
        owned_shift,
    )


def body(
    ring,
    tokens,
    lengths,
    w_qkv,
    b_qkv,
    w_out,
    b_out,
    w_fc1,
    b_fc1,
    w_fc2,
    b_fc2,
    ln_gain,
    ln_shift,
    cotangent,
):
    return head_plan(
        ring,
        tokens,
        lengths,
        w_qkv,
        b_qkv,
        w_out,
        b_out,
        w_fc1,
        b_fc1,
        w_fc2,
        b_fc2,
        ln_gain,
        ln_shift,
        cotangent,
    )


def solution(mesh):
    in_specs = (
        P(("dp", "ctx"), None),
        P("dp", None),
        P(("dp", "ctx"), None),
        P(("dp", "ctx")),
        P(("dp", "ctx"), None),
        P(("dp", "ctx")),
        P(("dp", "ctx"), None),
        P(("dp", "ctx")),
        P(("dp", "ctx"), None),
        P(("dp", "ctx")),
        P(("dp", "ctx")),
        P(("dp", "ctx")),
        P(("dp", "ctx"), None),
    )
    out_specs = (
        P(("dp", "ctx"), None),
        P(("dp", "ctx"), None),
        P(("dp", "ctx"), None),
        P(("dp", "ctx")),
        P(("dp", "ctx"), None),
        P(("dp", "ctx")),
        P(("dp", "ctx"), None),
        P(("dp", "ctx")),
        P(("dp", "ctx"), None),
        P(("dp", "ctx")),
        P(("dp", "ctx")),
        P(("dp", "ctx")),
    )
    ring = ring_of(mesh)
    return jax.shard_map(functools.partial(body, ring), mesh=mesh, in_specs=in_specs, out_specs=out_specs, check_vma=False)
```

```python
import functools
import math

import jax
import jax.numpy as jnp
from jax import lax
from jax.experimental import pallas as pl
from jax.experimental.pallas import tpu as pltpu
from jax.sharding import PartitionSpec as P

D = 2048
HEADS = 32
HEAD_DIM = 64
ROT = 32
FF = 8192


EPS = 1e-05
GELU_COEF = math.sqrt(2.0 / math.pi)
NEGATIVE = -1e30


def norm_parts(inputs, gain, shift):
    mean = jnp.mean(inputs, axis=-1, keepdims=True)
    centred = inputs - mean
    var = jnp.mean(centred * centred, axis=-1, keepdims=True)
    scaled = lax.rsqrt(var + EPS)
    normed = centred * scaled
    return (normed, scaled, normed * gain + shift)


def norm_back(d_hidden, normed, scaled, gain32):
    grad_gain = jnp.sum(d_hidden * normed, axis=0)
    grad_shift = jnp.sum(d_hidden, axis=0)
    d_normed = d_hidden * gain32
    d_inputs = scaled * (
        d_normed
        - jnp.mean(d_normed, axis=-1, keepdims=True)
        - normed * jnp.mean(d_normed * normed, axis=-1, keepdims=True)
    )
    return (grad_gain, grad_shift, d_inputs)


def gelu_tanh(pre):
    return 0.5 * pre * (1.0 + jnp.tanh(GELU_COEF * (pre + 0.044715 * pre * pre * pre)))


def gelu_slope(pre):
    tangent = jnp.tanh(GELU_COEF * (pre + 0.044715 * pre * pre * pre))
    return 0.5 * (1.0 + tangent) + 0.5 * pre * (1.0 - tangent * tangent) * GELU_COEF * (
        1.0 + 3.0 * 0.044715 * pre * pre
    )


def rotary_tables(positions):
    half = ROT // 2
    freq = jnp.exp(jnp.arange(half, dtype=jnp.float32) * (-2.0 * math.log(10000.0) / ROT))
    angle = positions.astype(jnp.float32)[:, None] * freq[None, :]
    return (jnp.cos(angle)[:, None, :], jnp.sin(angle)[:, None, :])


def rotate(heads, cosine, sine):
    half = ROT // 2
    first = heads[..., :half]
    second = heads[..., half:ROT]
    return jnp.concatenate(
        [first * cosine - second * sine, second * cosine + first * sine, heads[..., ROT:]], axis=-1
    )


def rotate_back(grads, cosine, sine):
    half = ROT // 2
    first = grads[..., :half]
    second = grads[..., half:ROT]
    return jnp.concatenate(
        [first * cosine + second * sine, second * cosine - first * sine, grads[..., ROT:]], axis=-1
    )


def segment_info(lengths_row, rows):
    ends = jnp.cumsum(lengths_row)
    starts = ends - lengths_row
    seg = jnp.sum((rows[:, None] >= ends[None, :]).astype(jnp.int32), axis=1)
    onehot = seg[:, None] == jnp.arange(lengths_row.shape[0], dtype=jnp.int32)[None, :]
    first_rows = jnp.sum(jnp.where(onehot, starts[None, :], 0), axis=1)
    return (seg, rows - first_rows)


TRANS_B = (((1,), (1,)), ((), ()))


def _allowed(segq_ref, segk_ref, i, j, tq, tk):
    rows = i * tq + lax.broadcasted_iota(jnp.int32, (tq, tk), 0)
    cols = j * tk + lax.broadcasted_iota(jnp.int32, (tq, tk), 1)
    return (segq_ref[...] == segk_ref[...]) & (cols <= rows)


def _fwd_kernel(q_ref, k_ref, v_ref, segq_ref, segk_ref, o_ref, lse_ref, m_sc, l_sc, acc_sc, *, tq, tk, scale):
    i = pl.program_id(1)
    j = pl.program_id(2)

    @pl.when(j == 0)
    def _():
        m_sc[...] = jnp.full_like(m_sc, NEGATIVE)
        l_sc[...] = jnp.zeros_like(l_sc)
        acc_sc[...] = jnp.zeros_like(acc_sc)

    @pl.when(j * tk <= i * tq + tq - 1)
    def _():
        q = q_ref[0]
        k = k_ref[0]
        s = lax.dot_general(q, k, TRANS_B, preferred_element_type=jnp.float32) * scale
        allowed = _allowed(segq_ref, segk_ref, i, j, tq, tk)
        s = jnp.where(allowed, s, NEGATIVE)
        m_prev = m_sc[...]
        m_new = jnp.maximum(m_prev, jnp.max(s, axis=1, keepdims=True))
        factor = jnp.exp(m_prev - m_new)
        p = jnp.where(allowed, jnp.exp(s - m_new), 0.0)
        l_sc[...] = l_sc[...] * factor + jnp.sum(p, axis=1, keepdims=True)
        acc_sc[...] = acc_sc[...] * factor + jnp.dot(
            p.astype(jnp.bfloat16), v_ref[0], preferred_element_type=jnp.float32
        )
        m_sc[...] = m_new

    @pl.when(j == pl.num_programs(2) - 1)
    def _():
        total = l_sc[...]
        o_ref[0] = acc_sc[...] / total
        lse_ref[0] = m_sc[...] + jnp.log(total)


def attention_forward(q, k, v, seg, tq=512, tk=512):
    heads, total, dim = q.shape
    nq, nk = total // tq, total // tk
    scale = 1.0 / math.sqrt(dim)
    segq = seg.reshape(total, 1)
    segk = seg.reshape(1, total)

    def kv_map(h, i, j):
        return (h, jnp.minimum(j, (i * tq + tq - 1) // tk), 0)

    def segk_map(h, i, j):
        return (0, jnp.minimum(j, (i * tq + tq - 1) // tk))

    return pl.pallas_call(
        functools.partial(_fwd_kernel, tq=tq, tk=tk, scale=scale),
        out_shape=(
            jax.ShapeDtypeStruct((heads, total, dim), jnp.float32),
            jax.ShapeDtypeStruct((heads, total, 1), jnp.float32),
        ),
        grid=(heads, nq, nk),
        in_specs=[
            pl.BlockSpec((1, tq, dim), lambda h, i, j: (h, i, 0)),
            pl.BlockSpec((1, tk, dim), kv_map),
            pl.BlockSpec((1, tk, dim), kv_map),
            pl.BlockSpec((tq, 1), lambda h, i, j: (i, 0)),
            pl.BlockSpec((1, tk), segk_map),
        ],
        out_specs=[
            pl.BlockSpec((1, tq, dim), lambda h, i, j: (h, i, 0)),
            pl.BlockSpec((1, tq, 1), lambda h, i, j: (h, i, 0)),
        ],
        scratch_shapes=[
            pltpu.VMEM((tq, 1), jnp.float32),
            pltpu.VMEM((tq, 1), jnp.float32),
            pltpu.VMEM((tq, dim), jnp.float32),
        ],
        cost_estimate=pl.CostEstimate(
            flops=2 * heads * total * total * dim,
            transcendentals=heads * total * total // 2,
            bytes_accessed=heads * total * dim * 10,
        ),
    )(q, k, v, segq, segk)


def _bwd_kernel(q_ref, k_ref, v_ref, do_ref, lse_ref, delta_ref, segq_ref, segk_ref, dq_ref, dk_ref, dv_ref, *, tq, tk, scale):
    j = pl.program_id(1)
    i = pl.program_id(2)

    @pl.when((j == 0) & (i == 0))
    def _():
        dq_ref[...] = jnp.zeros_like(dq_ref)

    @pl.when(i == 0)
    def _():
        dk_ref[...] = jnp.zeros_like(dk_ref)
        dv_ref[...] = jnp.zeros_like(dv_ref)

    @pl.when(i * tq + tq - 1 >= j * tk)
    def _():
        q = q_ref[0]
        k = k_ref[0]
        do = do_ref[0]
        s = lax.dot_general(q, k, TRANS_B, preferred_element_type=jnp.float32) * scale
        allowed = _allowed(segq_ref, segk_ref, i, j, tq, tk)
        p = jnp.where(allowed, jnp.exp(s - lse_ref[0]), 0.0)
        dp = lax.dot_general(do, v_ref[0], TRANS_B, preferred_element_type=jnp.float32)
        ds = (p * (dp - delta_ref[0])).astype(jnp.bfloat16)
        dv_ref[0] += lax.dot(p.astype(jnp.bfloat16).T, do, preferred_element_type=jnp.float32)
        dk_ref[0] += lax.dot(ds.T, q, preferred_element_type=jnp.float32) * scale
        rows = pl.ds(pl.multiple_of(i * tq, tq), tq)
        dq_ref[0, rows, :] += lax.dot(ds, k, preferred_element_type=jnp.float32) * scale


def attention_backward(q, k, v, do, lse, delta, seg, tq=512, tk=512):
    heads, total, dim = q.shape
    nq, nk = total // tq, total // tk
    scale = 1.0 / math.sqrt(dim)
    segq = seg.reshape(total, 1)
    segk = seg.reshape(1, total)

    def q_map(h, j, i):
        return (h, jnp.maximum(i, (j * tk) // tq), 0)

    def segq_map(h, j, i):
        return (jnp.maximum(i, (j * tk) // tq), 0)

    return pl.pallas_call(
        functools.partial(_bwd_kernel, tq=tq, tk=tk, scale=scale),
        out_shape=(
            jax.ShapeDtypeStruct((heads, total, dim), jnp.float32),
            jax.ShapeDtypeStruct((heads, total, dim), jnp.float32),
            jax.ShapeDtypeStruct((heads, total, dim), jnp.float32),
        ),
        grid=(heads, nk, nq),
        in_specs=[
            pl.BlockSpec((1, tq, dim), q_map),
            pl.BlockSpec((1, tk, dim), lambda h, j, i: (h, j, 0)),
            pl.BlockSpec((1, tk, dim), lambda h, j, i: (h, j, 0)),
            pl.BlockSpec((1, tq, dim), q_map),
            pl.BlockSpec((1, tq, 1), q_map),
            pl.BlockSpec((1, tq, 1), q_map),
            pl.BlockSpec((tq, 1), segq_map),
            pl.BlockSpec((1, tk), lambda h, j, i: (0, j)),
        ],
        out_specs=[
            pl.BlockSpec((1, total, dim), lambda h, j, i: (h, 0, 0)),
            pl.BlockSpec((1, tk, dim), lambda h, j, i: (h, j, 0)),
            pl.BlockSpec((1, tk, dim), lambda h, j, i: (h, j, 0)),
        ],
        cost_estimate=pl.CostEstimate(
            flops=5 * heads * total * total * dim,
            transcendentals=heads * total * total // 2,
            bytes_accessed=heads * total * dim * 24,
        ),
    )(q, k, v, do, lse, delta, segq, segk)


MESH_ID = pl.DeviceIdType.MESH


class Ring:
    def __init__(self, size, a_stride, b_stride):
        self.size = size
        self.half = size // 2
        self.a_stride = a_stride
        self.b_stride = b_stride

    def position(self, c):
        a = (c // self.a_stride) % self.half
        b = (c // self.b_stride) % 2
        return a + b * (2 * self.half - 1 - 2 * a)

    def device(self, pos):
        pos = pos % self.size
        b = pos // self.half
        a = pos + b * (2 * self.half - 1 - 2 * pos)
        return a * self.a_stride + b * self.b_stride


def ring_of(mesh):
    size = mesh.shape["ctx"]
    devices = list(mesh.devices.reshape(-1, size)[0])
    try:
        coords = [tuple(d.coords) for d in devices]
    except AttributeError:
        coords = None
    if coords and size % 2 == 0 and size >= 4:
        for b_stride in range(1, size):
            for a_stride in range(1, size):
                ring = Ring(size, a_stride, b_stride)
                order = [ring.device(p) for p in range(size)]
                if sorted(order) != list(range(size)):
                    continue
                hops = [
                    sum(abs(x - y) for x, y in zip(coords[order[p]], coords[order[(p + 1) % size]]))
                    for p in range(size)
                ]
                if max(hops) == 1:
                    return ring
    return Ring(size, 2, 1) if size % 2 == 0 and size >= 4 else None


def _barrier(g, left, right):
    barrier = pltpu.get_barrier_semaphore()
    for other in (left, right):
        pl.semaphore_signal(barrier, 1, device_id=(g, other), device_id_type=MESH_ID)
    pl.semaphore_wait(barrier, 2)


def _gather_kernel(x_ref, y_ref, own_sem, send_sem, recv_sem, *, ring, rows):
    n = ring.size
    half = rows // 2
    g = lax.axis_index("dp")
    c = lax.axis_index("ctx")
    pos = ring.position(c)
    right = ring.device(pos + 1)
    left = ring.device(pos + n - 1)
    own = pltpu.make_async_copy(x_ref, y_ref.at[pl.ds(c * rows, rows)], own_sem)
    own.start()
    _barrier(g, left, right)

    def link(direction, step, origin, source):
        offset = origin * rows + direction * half
        return pltpu.make_async_remote_copy(
            src_ref=source,
            dst_ref=y_ref.at[pl.ds(offset, half)],
            send_sem=send_sem.at[direction, step],
            recv_sem=recv_sem.at[direction, step],
            device_id=(g, right if direction == 0 else left),
            device_id_type=MESH_ID,
        )

    sent = []
    for step in range(n - 1):
        origins = (ring.device(pos - step + n), ring.device(pos + step))
        for direction in (0, 1):
            origin = origins[direction]
            if step == 0:
                source = x_ref.at[pl.ds(direction * half, half)]
            else:
                link(direction, step - 1, origin, None if False else y_ref.at[pl.ds(origin * rows + direction * half, half)]).wait_recv()
                source = y_ref.at[pl.ds(origin * rows + direction * half, half)]
            copy = link(direction, step, origin, source)
            copy.start()
            sent.append(copy)
    last = n - 2
    for direction, origin in ((0, ring.device(pos - last - 1 + n)), (1, ring.device(pos + last + 1))):
        link(direction, last, origin, y_ref.at[pl.ds(origin * rows + direction * half, half)]).wait_recv()
    for copy in sent:
        copy.wait_send()
    own.wait()


def ring_all_gather(x, ring, collective_id):
    rows, cols = x.shape
    n = ring.size
    return pl.pallas_call(
        functools.partial(_gather_kernel, ring=ring, rows=rows),
        out_shape=jax.ShapeDtypeStruct((n * rows, cols), x.dtype),
        in_specs=[pl.BlockSpec(memory_space=pl.ANY)],
        out_specs=pl.BlockSpec(memory_space=pl.ANY),
        scratch_shapes=[
            pltpu.SemaphoreType.DMA(()),
            pltpu.SemaphoreType.DMA((2, n - 1)),
            pltpu.SemaphoreType.DMA((2, n - 1)),
        ],
        compiler_params=pltpu.CompilerParams(collective_id=collective_id, has_side_effects=True),
    )(x)


def _scatter_kernel(p_ref, out_ref, recv_buf, send_buf, send_sem, recv_sem, *, ring, rows):
    n = ring.size
    half = rows // 2
    g = lax.axis_index("dp")
    c = lax.axis_index("ctx")
    pos = ring.position(c)
    right = ring.device(pos + 1)
    left = ring.device(pos + n - 1)
    _barrier(g, left, right)

    def link(direction, step):
        return pltpu.make_async_remote_copy(
            src_ref=send_buf.at[direction, step],
            dst_ref=recv_buf.at[direction, step],
            send_sem=send_sem.at[direction, step],
            recv_sem=recv_sem.at[direction, step],
            device_id=(g, right if direction == 0 else left),
            device_id_type=MESH_ID,
        )

    sent = []
    for step in range(n - 1):
        targets = (ring.device(pos - 1 - step + 2 * n), ring.device(pos + 1 + step))
        for direction in (0, 1):
            start = pl.multiple_of(targets[direction] * rows + direction * half, half)
            total = p_ref[pl.ds(start, half), :].astype(jnp.float32)
            if step > 0:
                link(direction, step - 1).wait_recv()
                total = total + recv_buf[direction, step - 1].astype(jnp.float32)
            send_buf[direction, step] = total.astype(send_buf.dtype)
            copy = link(direction, step)
            copy.start()
            sent.append(copy)
    for direction in (0, 1):
        link(direction, n - 2).wait_recv()
        start = pl.multiple_of(c * rows + direction * half, half)
        out_ref[pl.ds(direction * half, half), :] = (
            p_ref[pl.ds(start, half), :].astype(jnp.float32)
            + recv_buf[direction, n - 2].astype(jnp.float32)
        ).astype(out_ref.dtype)
    for copy in sent:
        copy.wait_send()


def ring_reduce_scatter(p, ring, collective_id, out_dtype=jnp.float32, wire=jnp.bfloat16):
    total_rows, cols = p.shape
    n = ring.size
    rows = total_rows // n
    half = rows // 2
    return pl.pallas_call(
        functools.partial(_scatter_kernel, ring=ring, rows=rows),
        out_shape=jax.ShapeDtypeStruct((rows, cols), out_dtype),
        in_specs=[pl.BlockSpec(memory_space=pltpu.VMEM)],
        out_specs=pl.BlockSpec(memory_space=pltpu.VMEM),
        scratch_shapes=[
            pltpu.VMEM((2, n - 1, half, cols), wire),
            pltpu.VMEM((2, n - 1, half, cols), wire),
            pltpu.SemaphoreType.DMA((2, n - 1)),
            pltpu.SemaphoreType.DMA((2, n - 1)),
        ],
        compiler_params=pltpu.CompilerParams(
            collective_id=collective_id, has_side_effects=True, vmem_limit_bytes=60 * 1024 * 1024
        ),
    )(p)


def _exchange_kernel(x_ref, out_ref, own_sem, send_sem, recv_sem, *, group):
    n = x_ref.shape[0]
    g = lax.axis_index("dp")
    c = lax.axis_index("ctx")
    n_ctx = lax.axis_size("ctx")
    me = {"all": g * n_ctx + c, "ctx": c, "dp": g}[group]

    def address(member):
        if group == "all":
            return (member // n_ctx, member % n_ctx)
        if group == "ctx":
            return (g, member)
        return (member, c)

    own = pltpu.make_async_copy(x_ref.at[me], out_ref.at[me], own_sem)
    own.start()
    barrier = pltpu.get_barrier_semaphore()
    for offset in range(1, n):
        pl.semaphore_signal(
            barrier, 1, device_id=address((me + offset) % n), device_id_type=MESH_ID
        )
    pl.semaphore_wait(barrier, n - 1)

    def link(offset, source, target):
        return pltpu.make_async_remote_copy(
            src_ref=x_ref.at[target],
            dst_ref=out_ref.at[source],
            send_sem=send_sem.at[offset],
            recv_sem=recv_sem.at[offset],
            device_id=address(target),
            device_id_type=MESH_ID,
        )

    sent = []
    for offset in range(1, n):
        copy = link(offset, me, (me + offset) % n)
        copy.start()
        sent.append(copy)
    for offset in range(1, n):
        link(offset, (me + n - offset) % n, me).wait_recv()
    for copy in sent:
        copy.wait_send()
    own.wait()


def exchange(x, group, collective_id):
    n = x.shape[0]
    space = pltpu.VMEM
    return pl.pallas_call(
        functools.partial(_exchange_kernel, group=group),
        out_shape=jax.ShapeDtypeStruct(x.shape, x.dtype),
        in_specs=[pl.BlockSpec(memory_space=space)],
        out_specs=pl.BlockSpec(memory_space=space),
        scratch_shapes=[
            pltpu.SemaphoreType.DMA(()),
            pltpu.SemaphoreType.DMA((n,)),
            pltpu.SemaphoreType.DMA((n,)),
        ],
        compiler_params=pltpu.CompilerParams(collective_id=collective_id, has_side_effects=True),
    )(x)


def block_moves(n_dp, n_ctx):
    count = n_dp * n_ctx
    return [(f, (f % n_dp) * n_ctx + f // n_dp) for f in range(count)]


def fetch_out_rows(w_out):
    n_dp = lax.axis_size("dp")
    n_ctx = lax.axis_size("ctx")
    moved = lax.ppermute(w_out.astype(jnp.bfloat16), ("dp", "ctx"), perm=block_moves(n_dp, n_ctx))
    return lax.all_gather(moved, "dp", axis=0, tiled=True)


def return_out_rows(grad_out_rows):
    n_dp = lax.axis_size("dp")
    n_ctx = lax.axis_size("ctx")
    part = lax.psum_scatter(grad_out_rows, "dp", scatter_dimension=0, tiled=True)
    back = [(b, a) for a, b in block_moves(n_dp, n_ctx)]
    return lax.ppermute(part, ("dp", "ctx"), perm=back)


def pack_rows(vector, lanes):
    size = vector.shape[0]
    total = -(-size // (16 * lanes)) * 16 * lanes
    return jnp.pad(vector, (0, total - size)).reshape(-1, lanes)


def fetch_small(b_qkv, b_out, b_fc2, ln_gain, ln_shift, b_fc1):
    pieces = (b_qkv, b_out, b_fc2, ln_gain, ln_shift, b_fc1)
    n_dp = lax.axis_size("dp")
    n_ctx = lax.axis_size("ctx")
    packed = pack_rows(jnp.concatenate([p.astype(jnp.bfloat16) for p in pieces]), 128)
    over_dp = exchange(jnp.broadcast_to(packed[None], (n_dp,) + packed.shape), "dp", 4)
    over_all = exchange(jnp.broadcast_to(over_dp[None], (n_ctx,) + over_dp.shape), "ctx", 8)
    table = over_all.transpose(1, 0, 2, 3).reshape(n_dp * n_ctx, -1)
    result = []
    offset = 0
    for p in pieces:
        result.append(table[:, offset : offset + p.shape[0]])
        offset += p.shape[0]
    return result


def reduce_small(small):
    n_dp = lax.axis_size("dp")
    n_ctx = lax.axis_size("ctx")
    count, width = small.shape
    packed = jax.vmap(lambda row: pack_rows(row, 128))(small)
    packed = packed.reshape((n_dp, n_ctx) + packed.shape[1:]).transpose(1, 0, 2, 3)
    over_ctx = jnp.sum(exchange(packed, "ctx", 7), axis=0)
    over_dp = jnp.sum(exchange(over_ctx, "dp", 9), axis=0)
    return over_dp.reshape(-1)[:width]


def fetch_heads(w_qkv, w_fc1, w_fc2, tokens):
    dp_count = lax.axis_size("dp")
    ctx_count = lax.axis_size("ctx")
    rows_piece = w_qkv.shape[0]
    head_width = D // ctx_count
    unit = FF // (dp_count * ctx_count)
    qkv_piece = w_qkv.astype(jnp.bfloat16).reshape(rows_piece, 3, ctx_count, head_width)
    fc1_piece = w_fc1.astype(jnp.bfloat16).reshape(rows_piece, dp_count, ctx_count, unit)
    pieces = jnp.concatenate(
        [
            qkv_piece.transpose(2, 0, 1, 3).reshape(ctx_count, rows_piece, 3 * head_width),
            fc1_piece.transpose(2, 0, 1, 3).reshape(ctx_count, rows_piece, dp_count * unit),
        ],
        axis=2,
    )
    sent = exchange(pieces, "ctx", 5).reshape(ctx_count * rows_piece, -1)
    sent, tokens = lax.optimization_barrier((sent, tokens))
    cols, fc2_rows = (
        lax.all_gather(sent, "dp", axis=0, tiled=True),
        lax.all_gather(w_fc2.astype(jnp.bfloat16), "dp", axis=0, tiled=True),
    )
    return (cols, fc2_rows, tokens)


def return_heads(owned_parts):
    dp_count = lax.axis_size("dp")
    ctx_count = lax.axis_size("ctx")
    head_width = D // ctx_count
    unit = FF // (dp_count * ctx_count)
    rows_piece = owned_parts.shape[0] // ctx_count
    got = exchange(owned_parts.reshape(ctx_count, rows_piece, -1), "ctx", 6)
    qkv = got[:, :, : 3 * head_width].reshape(ctx_count, rows_piece, 3, head_width)
    fc1 = got[:, :, 3 * head_width :].reshape(ctx_count, rows_piece, dp_count, unit)
    return (
        qkv.transpose(1, 2, 0, 3).reshape(rows_piece, 3 * D).astype(jnp.float32),
        fc1.transpose(1, 2, 0, 3).reshape(rows_piece, FF).astype(jnp.float32),
    )


def head_plan(
    ring,
    tokens,
    lengths,
    w_qkv,
    b_qkv,
    w_out,
    b_out,
    w_fc1,
    b_fc1,
    w_fc2,
    b_fc2,
    ln_gain,
    ln_shift,
    cotangent,
):
    rows_here = tokens.shape[0]
    rows_piece = w_qkv.shape[0]
    dp_count = lax.axis_size("dp")
    ctx_count = lax.axis_size("ctx")
    count = dp_count * ctx_count
    group = rows_here * ctx_count
    head_width = D // ctx_count
    local_heads = HEADS // ctx_count
    unit = FF // (dp_count * ctx_count)
    here = lax.axis_index("ctx")
    group_rows = jnp.arange(group, dtype=jnp.int32)
    seg, positions = segment_info(lengths[0], group_rows)
    cosine, sine = rotary_tables(positions)
    qkv_bias, out_bias, fc2_bias, gain_low, shift_low, fc1_table = fetch_small(
        b_qkv, b_out, b_fc2, ln_gain, ln_shift, b_fc1
    )
    qkv_bias = qkv_bias.reshape(3 * D)
    out_bias = out_bias.reshape(D)
    fc2_bias = fc2_bias.reshape(D)
    gain_low = gain_low.reshape(D)
    shift_low = shift_low.reshape(D)
    fc1_bias = lax.dynamic_index_in_dim(
        fc1_table.reshape(dp_count, ctx_count, unit), here, 1, keepdims=False
    ).reshape(dp_count * unit)
    out_rows = fetch_out_rows(w_out)
    cols, fc2_rows, tokens = fetch_heads(w_qkv, w_fc1, w_fc2, tokens)
    gain32 = gain_low.astype(jnp.float32)
    shift32 = shift_low.astype(jnp.float32)
    inputs = tokens.astype(jnp.float32)
    normed, scaled, _ = norm_parts(inputs, gain32, shift32)
    tokens_group = ring_all_gather(tokens, ring, 0)
    late_dy, tokens_group = lax.optimization_barrier((cotangent, tokens_group))
    dy_group = lax.all_gather(late_dy, "ctx", axis=0, tiled=True)
    hidden_group = norm_parts(tokens_group.astype(jnp.float32), gain32, shift32)[2].astype(
        jnp.bfloat16
    )
    bias_cols = lax.dynamic_slice_in_dim(
        qkv_bias.reshape(3, D), here * head_width, head_width, 1
    ).reshape(3 * head_width)
    both = jnp.dot(hidden_group, cols, preferred_element_type=jnp.float32) + jnp.concatenate(
        [bias_cols, fc1_bias]
    ).astype(jnp.float32)
    qkv = both[:, : 3 * head_width]
    pre = both[:, 3 * head_width :]
    shape = (group, local_heads, HEAD_DIM)
    query = rotate(qkv[:, :head_width].reshape(shape), cosine, sine).astype(jnp.bfloat16)
    keys = rotate(qkv[:, head_width : 2 * head_width].reshape(shape), cosine, sine).astype(
        jnp.bfloat16
    )
    values = qkv[:, 2 * head_width :].reshape(shape).astype(jnp.bfloat16)
    q_heads = query.transpose(1, 0, 2)
    k_heads = keys.transpose(1, 0, 2)
    v_heads = values.transpose(1, 0, 2)
    attended_heads, log_total = attention_forward(q_heads, k_heads, v_heads, seg)
    attended = attended_heads.transpose(1, 0, 2).reshape(group, head_width).astype(jnp.bfloat16)
    act = gelu_tanh(pre).astype(jnp.bfloat16)
    branches = ring_reduce_scatter(
        jnp.dot(attended, out_rows, preferred_element_type=jnp.float32)
        + jnp.dot(act, fc2_rows, preferred_element_type=jnp.float32),
        ring,
        2,
    )
    block_out = (
        inputs + branches + out_bias.astype(jnp.float32) + fc2_bias.astype(jnp.float32)
    ).astype(jnp.bfloat16)
    grad_out32 = cotangent.astype(jnp.float32)
    grad_b_fc2 = jnp.sum(grad_out32, axis=0)
    grad_fc2_part = jnp.einsum("tf,td->fd", act, dy_group, preferred_element_type=jnp.float32)
    d_act = jnp.einsum("td,fd->tf", dy_group, fc2_rows, preferred_element_type=jnp.float32)
    d_pre = (d_act * gelu_slope(pre)).astype(jnp.bfloat16)
    grad_bfc1_part = jnp.sum(d_pre.astype(jnp.float32), axis=0)
    grad_out_rows = jnp.einsum("tc,td->cd", attended, dy_group, preferred_element_type=jnp.float32)
    owned_w_out = return_out_rows(grad_out_rows)
    d_attended = (
        jnp.einsum("td,cd->tc", dy_group, out_rows, preferred_element_type=jnp.float32)
        .astype(jnp.bfloat16)
        .reshape(shape)
    )
    d_heads = d_attended.transpose(1, 0, 2)
    delta = jnp.sum(d_heads.astype(jnp.float32) * attended_heads, axis=2, keepdims=True)
    dq_heads, dk_heads, dv_heads = attention_backward(
        q_heads, k_heads, v_heads, d_heads, log_total, delta, seg
    )
    d_query = dq_heads.transpose(1, 0, 2)
    d_keys = dk_heads.transpose(1, 0, 2)
    d_values = dv_heads.transpose(1, 0, 2)
    d_query = rotate_back(d_query, cosine, sine).reshape(group, head_width)
    d_keys = rotate_back(d_keys, cosine, sine).reshape(group, head_width)
    d_qkv = jnp.concatenate([d_query, d_keys, d_values.reshape(group, head_width)], axis=1).astype(
        jnp.bfloat16
    )
    d_both = jnp.concatenate([d_qkv, d_pre], axis=1)
    bias_part = jnp.sum(d_qkv.astype(jnp.float32), axis=0).reshape(3, head_width)
    d_hidden = ring_reduce_scatter(
        jnp.einsum("tc,dc->td", d_both, cols, preferred_element_type=jnp.float32), ring, 3
    )
    grad_gain, grad_shift, d_inputs = norm_back(d_hidden, normed, scaled, gain32)
    grad_tokens = (grad_out32 + d_inputs).astype(jnp.bfloat16)
    weight_parts = jnp.einsum(
        "td,tc->dc", hidden_group, d_both, preferred_element_type=jnp.float32
    ).astype(jnp.bfloat16)
    owned_parts = lax.psum_scatter(weight_parts, "dp", scatter_dimension=0, tiled=True)
    split_qkv, split_fc1 = return_heads(owned_parts)
    owned_fc2 = lax.psum_scatter(
        grad_fc2_part.astype(jnp.bfloat16), "dp", scatter_dimension=0, tiled=True
    ).astype(jnp.float32)
    full_bqkv = lax.dynamic_update_slice_in_dim(
        jnp.zeros((3, D), jnp.float32), bias_part, here * head_width, 1
    )
    full_bfc1 = lax.dynamic_update_slice_in_dim(
        jnp.zeros((dp_count, ctx_count, unit), jnp.float32),
        grad_bfc1_part.reshape(dp_count, 1, unit),
        here,
        1,
    )
    small = jnp.concatenate(
        [
            full_bqkv.reshape(count, -1),
            grad_b_fc2.reshape(count, -1),
            grad_gain.reshape(count, -1),
            grad_shift.reshape(count, -1),
            full_bfc1.reshape(count, -1),
        ],
        axis=1,
    )
    owned_small = reduce_small(small)
    cuts = [0, 3 * D // count, D // count, D // count, D // count, FF // count]
    bounds = [sum(cuts[: i + 1]) for i in range(len(cuts))]
    owned_bqkv, owned_bout, owned_gain, owned_shift, owned_bfc1 = [
        owned_small[bounds[i] : bounds[i + 1]] for i in range(5)
    ]
    return (
        block_out,
        grad_tokens,
        split_qkv.reshape(rows_piece, 3 * D),
        owned_bqkv,
        owned_w_out,
        owned_bout,
        split_fc1.reshape(rows_piece, FF),
        owned_bfc1,
        owned_fc2,
        owned_bout,
        owned_gain,
        owned_shift,
    )


def body(
    ring,
    tokens,
    lengths,
    w_qkv,
    b_qkv,
    w_out,
    b_out,
    w_fc1,
    b_fc1,
    w_fc2,
    b_fc2,
    ln_gain,
    ln_shift,
    cotangent,
):
    return head_plan(
        ring,
        tokens,
        lengths,
        w_qkv,
        b_qkv,
        w_out,
        b_out,
        w_fc1,
        b_fc1,
        w_fc2,
        b_fc2,
        ln_gain,
        ln_shift,
        cotangent,
    )


def solution(mesh):
    in_specs = (
        P(("dp", "ctx"), None),
        P("dp", None),
        P(("dp", "ctx"), None),
        P(("dp", "ctx")),
        P(("dp", "ctx"), None),
        P(("dp", "ctx")),
        P(("dp", "ctx"), None),
        P(("dp", "ctx")),
        P(("dp", "ctx"), None),
        P(("dp", "ctx")),
        P(("dp", "ctx")),
        P(("dp", "ctx")),
        P(("dp", "ctx"), None),
    )
    out_specs = (
        P(("dp", "ctx"), None),
        P(("dp", "ctx"), None),
        P(("dp", "ctx"), None),
        P(("dp", "ctx")),
        P(("dp", "ctx"), None),
        P(("dp", "ctx")),
        P(("dp", "ctx"), None),
        P(("dp", "ctx")),
        P(("dp", "ctx"), None),
        P(("dp", "ctx")),
        P(("dp", "ctx")),
        P(("dp", "ctx")),
    )
    ring = ring_of(mesh)
    return jax.shard_map(functools.partial(body, ring), mesh=mesh, in_specs=in_specs, out_specs=out_specs, check_vma=False)
```

```python
import functools
import math

import jax
import jax.numpy as jnp
from jax import lax
from jax.experimental import pallas as pl
from jax.experimental.pallas import tpu as pltpu
from jax.sharding import PartitionSpec as P

D = 2048
HEADS = 32
HEAD_DIM = 64
ROT = 32
FF = 8192


EPS = 1e-05
GELU_COEF = math.sqrt(2.0 / math.pi)
NEGATIVE = -1e30


def norm_parts(inputs, gain, shift):
    mean = jnp.mean(inputs, axis=-1, keepdims=True)
    centred = inputs - mean
    var = jnp.mean(centred * centred, axis=-1, keepdims=True)
    scaled = lax.rsqrt(var + EPS)
    normed = centred * scaled
    return (normed, scaled, normed * gain + shift)


def norm_back(d_hidden, normed, scaled, gain32):
    grad_gain = jnp.sum(d_hidden * normed, axis=0)
    grad_shift = jnp.sum(d_hidden, axis=0)
    d_normed = d_hidden * gain32
    d_inputs = scaled * (
        d_normed
        - jnp.mean(d_normed, axis=-1, keepdims=True)
        - normed * jnp.mean(d_normed * normed, axis=-1, keepdims=True)
    )
    return (grad_gain, grad_shift, d_inputs)


def gelu_tanh(pre):
    return 0.5 * pre * (1.0 + jnp.tanh(GELU_COEF * (pre + 0.044715 * pre * pre * pre)))


def gelu_slope(pre):
    tangent = jnp.tanh(GELU_COEF * (pre + 0.044715 * pre * pre * pre))
    return 0.5 * (1.0 + tangent) + 0.5 * pre * (1.0 - tangent * tangent) * GELU_COEF * (
        1.0 + 3.0 * 0.044715 * pre * pre
    )


def rotary_tables(positions):
    half = ROT // 2
    freq = jnp.exp(jnp.arange(half, dtype=jnp.float32) * (-2.0 * math.log(10000.0) / ROT))
    angle = positions.astype(jnp.float32)[:, None] * freq[None, :]
    return (jnp.cos(angle)[:, None, :], jnp.sin(angle)[:, None, :])


def rotate(heads, cosine, sine):
    half = ROT // 2
    first = heads[..., :half]
    second = heads[..., half:ROT]
    return jnp.concatenate(
        [first * cosine - second * sine, second * cosine + first * sine, heads[..., ROT:]], axis=-1
    )


def rotate_back(grads, cosine, sine):
    half = ROT // 2
    first = grads[..., :half]
    second = grads[..., half:ROT]
    return jnp.concatenate(
        [first * cosine + second * sine, second * cosine - first * sine, grads[..., ROT:]], axis=-1
    )


def segment_info(lengths_row, rows):
    ends = jnp.cumsum(lengths_row)
    starts = ends - lengths_row
    seg = jnp.sum((rows[:, None] >= ends[None, :]).astype(jnp.int32), axis=1)
    onehot = seg[:, None] == jnp.arange(lengths_row.shape[0], dtype=jnp.int32)[None, :]
    first_rows = jnp.sum(jnp.where(onehot, starts[None, :], 0), axis=1)
    return (seg, rows - first_rows)


TRANS_B = (((1,), (1,)), ((), ()))


def _allowed(segq_ref, segk_ref, i, j, tq, tk, causal):
    same = segq_ref[...] == segk_ref[...]
    if not causal:
        return same
    rows = i * tq + lax.broadcasted_iota(jnp.int32, (tq, tk), 0)
    cols = j * tk + lax.broadcasted_iota(jnp.int32, (tq, tk), 1)
    return same & (cols <= rows)


def _fwd_kernel(q_ref, k_ref, v_ref, segq_ref, segk_ref, o_ref, lse_ref, m_sc, l_sc, acc_sc, *, tq, tk, scale):
    i = pl.program_id(1)
    j = pl.program_id(2)

    @pl.when(j == 0)
    def _():
        m_sc[...] = jnp.full_like(m_sc, NEGATIVE)
        l_sc[...] = jnp.zeros_like(l_sc)
        acc_sc[...] = jnp.zeros_like(acc_sc)

    def absorb(causal):
        q = q_ref[0]
        k = k_ref[0]
        s = lax.dot_general(q, k, TRANS_B, preferred_element_type=jnp.float32) * scale
        s = jnp.where(_allowed(segq_ref, segk_ref, i, j, tq, tk, causal), s, -jnp.inf)
        m_prev = m_sc[...]
        m_new = jnp.maximum(m_prev, jnp.max(s, axis=1, keepdims=True))
        factor = jnp.exp(m_prev - m_new)
        p = jnp.exp(s - m_new)
        l_sc[...] = l_sc[...] * factor + jnp.sum(p, axis=1, keepdims=True)
        acc_sc[...] = acc_sc[...] * factor + jnp.dot(
            p.astype(jnp.bfloat16), v_ref[0], preferred_element_type=jnp.float32
        )
        m_sc[...] = m_new

    below = (j + 1) * tk <= i * tq
    near = jnp.logical_and(jnp.logical_not(below), j * tk <= i * tq + tq - 1)

    @pl.when(below)
    def _():
        absorb(False)

    @pl.when(near)
    def _():
        absorb(True)

    @pl.when(j == pl.num_programs(2) - 1)
    def _():
        total = l_sc[...]
        o_ref[0] = acc_sc[...] / total
        lse_ref[0] = m_sc[...] + jnp.log(total)


def attention_forward(q, k, v, seg, tq=512, tk=512):
    heads, total, dim = q.shape
    nq, nk = total // tq, total // tk
    scale = 1.0 / math.sqrt(dim)
    segq = seg.reshape(total, 1)
    segk = seg.reshape(1, total)

    def kv_map(h, i, j):
        return (h, jnp.minimum(j, (i * tq + tq - 1) // tk), 0)

    def segk_map(h, i, j):
        return (0, jnp.minimum(j, (i * tq + tq - 1) // tk))

    return pl.pallas_call(
        functools.partial(_fwd_kernel, tq=tq, tk=tk, scale=scale),
        out_shape=(
            jax.ShapeDtypeStruct((heads, total, dim), jnp.float32),
            jax.ShapeDtypeStruct((heads, total, 1), jnp.float32),
        ),
        grid=(heads, nq, nk),
        in_specs=[
            pl.BlockSpec((1, tq, dim), lambda h, i, j: (h, i, 0)),
            pl.BlockSpec((1, tk, dim), kv_map),
            pl.BlockSpec((1, tk, dim), kv_map),
            pl.BlockSpec((tq, 1), lambda h, i, j: (i, 0)),
            pl.BlockSpec((1, tk), segk_map),
        ],
        out_specs=[
            pl.BlockSpec((1, tq, dim), lambda h, i, j: (h, i, 0)),
            pl.BlockSpec((1, tq, 1), lambda h, i, j: (h, i, 0)),
        ],
        scratch_shapes=[
            pltpu.VMEM((tq, 1), jnp.float32),
            pltpu.VMEM((tq, 1), jnp.float32),
            pltpu.VMEM((tq, dim), jnp.float32),
        ],
        cost_estimate=pl.CostEstimate(
            flops=2 * heads * total * total * dim,
            transcendentals=heads * total * total // 2,
            bytes_accessed=heads * total * dim * 10,
        ),
    )(q, k, v, segq, segk)


def _bwd_kernel(q_ref, k_ref, v_ref, do_ref, lse_ref, delta_ref, segq_ref, segk_ref, dq_ref, dk_ref, dv_ref, *, tq, tk, scale):
    j = pl.program_id(1)
    i = pl.program_id(2)

    @pl.when((j == 0) & (i == 0))
    def _():
        dq_ref[...] = jnp.zeros_like(dq_ref)

    @pl.when(i == 0)
    def _():
        dk_ref[...] = jnp.zeros_like(dk_ref)
        dv_ref[...] = jnp.zeros_like(dv_ref)

    def absorb(causal):
        q = q_ref[0]
        k = k_ref[0]
        do = do_ref[0]
        s = lax.dot_general(q, k, TRANS_B, preferred_element_type=jnp.float32) * scale
        s = jnp.where(_allowed(segq_ref, segk_ref, i, j, tq, tk, causal), s, -jnp.inf)
        p = jnp.exp(s - lse_ref[0])
        dp = lax.dot_general(do, v_ref[0], TRANS_B, preferred_element_type=jnp.float32)
        ds = (p * (dp - delta_ref[0])).astype(jnp.bfloat16)
        dv_ref[0] += lax.dot(p.astype(jnp.bfloat16).T, do, preferred_element_type=jnp.float32)
        dk_ref[0] += lax.dot(ds.T, q, preferred_element_type=jnp.float32) * scale
        rows = pl.ds(pl.multiple_of(i * tq, tq), tq)
        dq_ref[0, rows, :] += lax.dot(ds, k, preferred_element_type=jnp.float32) * scale

    below = (j + 1) * tk <= i * tq
    near = jnp.logical_and(jnp.logical_not(below), i * tq + tq - 1 >= j * tk)

    @pl.when(below)
    def _():
        absorb(False)

    @pl.when(near)
    def _():
        absorb(True)


def attention_backward(q, k, v, do, lse, delta, seg, tq=512, tk=512):
    heads, total, dim = q.shape
    nq, nk = total // tq, total // tk
    scale = 1.0 / math.sqrt(dim)
    segq = seg.reshape(total, 1)
    segk = seg.reshape(1, total)

    def q_map(h, j, i):
        return (h, jnp.maximum(i, (j * tk) // tq), 0)

    def segq_map(h, j, i):
        return (jnp.maximum(i, (j * tk) // tq), 0)

    return pl.pallas_call(
        functools.partial(_bwd_kernel, tq=tq, tk=tk, scale=scale),
        out_shape=(
            jax.ShapeDtypeStruct((heads, total, dim), jnp.float32),
            jax.ShapeDtypeStruct((heads, total, dim), jnp.float32),
            jax.ShapeDtypeStruct((heads, total, dim), jnp.float32),
        ),
        grid=(heads, nk, nq),
        in_specs=[
            pl.BlockSpec((1, tq, dim), q_map),
            pl.BlockSpec((1, tk, dim), lambda h, j, i: (h, j, 0)),
            pl.BlockSpec((1, tk, dim), lambda h, j, i: (h, j, 0)),
            pl.BlockSpec((1, tq, dim), q_map),
            pl.BlockSpec((1, tq, 1), q_map),
            pl.BlockSpec((1, tq, 1), q_map),
            pl.BlockSpec((tq, 1), segq_map),
            pl.BlockSpec((1, tk), lambda h, j, i: (0, j)),
        ],
        out_specs=[
            pl.BlockSpec((1, total, dim), lambda h, j, i: (h, 0, 0)),
            pl.BlockSpec((1, tk, dim), lambda h, j, i: (h, j, 0)),
            pl.BlockSpec((1, tk, dim), lambda h, j, i: (h, j, 0)),
        ],
        cost_estimate=pl.CostEstimate(
            flops=5 * heads * total * total * dim,
            transcendentals=heads * total * total // 2,
            bytes_accessed=heads * total * dim * 24,
        ),
    )(q, k, v, do, lse, delta, segq, segk)


MESH_ID = pl.DeviceIdType.MESH


class Ring:
    def __init__(self, size, a_stride, b_stride):
        self.size = size
        self.half = size // 2
        self.a_stride = a_stride
        self.b_stride = b_stride

    def position(self, c):
        a = (c // self.a_stride) % self.half
        b = (c // self.b_stride) % 2
        return a + b * (2 * self.half - 1 - 2 * a)

    def device(self, pos):
        pos = pos % self.size
        b = pos // self.half
        a = pos + b * (2 * self.half - 1 - 2 * pos)
        return a * self.a_stride + b * self.b_stride


def ring_of(mesh):
    size = mesh.shape["ctx"]
    devices = list(mesh.devices.reshape(-1, size)[0])
    try:
        coords = [tuple(d.coords) for d in devices]
    except AttributeError:
        coords = None
    if coords and size % 2 == 0 and size >= 4:
        for b_stride in range(1, size):
            for a_stride in range(1, size):
                ring = Ring(size, a_stride, b_stride)
                order = [ring.device(p) for p in range(size)]
                if sorted(order) != list(range(size)):
                    continue
                hops = [
                    sum(abs(x - y) for x, y in zip(coords[order[p]], coords[order[(p + 1) % size]]))
                    for p in range(size)
                ]
                if max(hops) == 1:
                    return ring
    return Ring(size, 2, 1) if size % 2 == 0 and size >= 4 else None


def _barrier(g, left, right):
    barrier = pltpu.get_barrier_semaphore()
    for other in (left, right):
        pl.semaphore_signal(barrier, 1, device_id=(g, other), device_id_type=MESH_ID)
    pl.semaphore_wait(barrier, 2)


def _gather_kernel(x_ref, y_ref, own_sem, send_sem, recv_sem, *, ring, rows):
    n = ring.size
    half = rows // 2
    g = lax.axis_index("dp")
    c = lax.axis_index("ctx")
    pos = ring.position(c)
    right = ring.device(pos + 1)
    left = ring.device(pos + n - 1)
    own = pltpu.make_async_copy(x_ref, y_ref.at[pl.ds(c * rows, rows)], own_sem)
    own.start()
    _barrier(g, left, right)

    def link(direction, step, origin, source):
        offset = origin * rows + direction * half
        return pltpu.make_async_remote_copy(
            src_ref=source,
            dst_ref=y_ref.at[pl.ds(offset, half)],
            send_sem=send_sem.at[direction, step],
            recv_sem=recv_sem.at[direction, step],
            device_id=(g, right if direction == 0 else left),
            device_id_type=MESH_ID,
        )

    sent = []
    for step in range(n - 1):
        origins = (ring.device(pos - step + n), ring.device(pos + step))
        for direction in (0, 1):
            origin = origins[direction]
            if step == 0:
                source = x_ref.at[pl.ds(direction * half, half)]
            else:
                link(direction, step - 1, origin, None if False else y_ref.at[pl.ds(origin * rows + direction * half, half)]).wait_recv()
                source = y_ref.at[pl.ds(origin * rows + direction * half, half)]
            copy = link(direction, step, origin, source)
            copy.start()
            sent.append(copy)
    last = n - 2
    for direction, origin in ((0, ring.device(pos - last - 1 + n)), (1, ring.device(pos + last + 1))):
        link(direction, last, origin, y_ref.at[pl.ds(origin * rows + direction * half, half)]).wait_recv()
    for copy in sent:
        copy.wait_send()
    own.wait()


def ring_all_gather(x, ring, collective_id):
    rows, cols = x.shape
    n = ring.size
    return pl.pallas_call(
        functools.partial(_gather_kernel, ring=ring, rows=rows),
        out_shape=jax.ShapeDtypeStruct((n * rows, cols), x.dtype),
        in_specs=[pl.BlockSpec(memory_space=pl.ANY)],
        out_specs=pl.BlockSpec(memory_space=pl.ANY),
        scratch_shapes=[
            pltpu.SemaphoreType.DMA(()),
            pltpu.SemaphoreType.DMA((2, n - 1)),
            pltpu.SemaphoreType.DMA((2, n - 1)),
        ],
        compiler_params=pltpu.CompilerParams(collective_id=collective_id, has_side_effects=True),
    )(x)


def _scatter_kernel(p_ref, out_ref, recv_buf, send_buf, send_sem, recv_sem, *, ring, rows):
    n = ring.size
    half = rows // 2
    g = lax.axis_index("dp")
    c = lax.axis_index("ctx")
    pos = ring.position(c)
    right = ring.device(pos + 1)
    left = ring.device(pos + n - 1)
    _barrier(g, left, right)

    def link(direction, step):
        return pltpu.make_async_remote_copy(
            src_ref=send_buf.at[direction, step],
            dst_ref=recv_buf.at[direction, step],
            send_sem=send_sem.at[direction, step],
            recv_sem=recv_sem.at[direction, step],
            device_id=(g, right if direction == 0 else left),
            device_id_type=MESH_ID,
        )

    sent = []
    for step in range(n - 1):
        targets = (ring.device(pos - 1 - step + 2 * n), ring.device(pos + 1 + step))
        for direction in (0, 1):
            start = pl.multiple_of(targets[direction] * rows + direction * half, half)
            total = p_ref[pl.ds(start, half), :].astype(jnp.float32)
            if step > 0:
                link(direction, step - 1).wait_recv()
                total = total + recv_buf[direction, step - 1].astype(jnp.float32)
            send_buf[direction, step] = total.astype(send_buf.dtype)
            copy = link(direction, step)
            copy.start()
            sent.append(copy)
    for direction in (0, 1):
        link(direction, n - 2).wait_recv()
        start = pl.multiple_of(c * rows + direction * half, half)
        out_ref[pl.ds(direction * half, half), :] = (
            p_ref[pl.ds(start, half), :].astype(jnp.float32)
            + recv_buf[direction, n - 2].astype(jnp.float32)
        ).astype(out_ref.dtype)
    for copy in sent:
        copy.wait_send()


def ring_reduce_scatter(p, ring, collective_id, out_dtype=jnp.float32, wire=jnp.bfloat16):
    total_rows, cols = p.shape
    n = ring.size
    rows = total_rows // n
    half = rows // 2
    return pl.pallas_call(
        functools.partial(_scatter_kernel, ring=ring, rows=rows),
        out_shape=jax.ShapeDtypeStruct((rows, cols), out_dtype),
        in_specs=[pl.BlockSpec(memory_space=pltpu.VMEM)],
        out_specs=pl.BlockSpec(memory_space=pltpu.VMEM),
        scratch_shapes=[
            pltpu.VMEM((2, n - 1, half, cols), wire),
            pltpu.VMEM((2, n - 1, half, cols), wire),
            pltpu.SemaphoreType.DMA((2, n - 1)),
            pltpu.SemaphoreType.DMA((2, n - 1)),
        ],
        compiler_params=pltpu.CompilerParams(
            collective_id=collective_id, has_side_effects=True, vmem_limit_bytes=60 * 1024 * 1024
        ),
    )(p)


def _exchange_kernel(x_ref, out_ref, own_sem, send_sem, recv_sem, *, group):
    n = x_ref.shape[0]
    g = lax.axis_index("dp")
    c = lax.axis_index("ctx")
    n_ctx = lax.axis_size("ctx")
    me = {"all": g * n_ctx + c, "ctx": c, "dp": g}[group]

    def address(member):
        if group == "all":
            return (member // n_ctx, member % n_ctx)
        if group == "ctx":
            return (g, member)
        return (member, c)

    own = pltpu.make_async_copy(x_ref.at[me], out_ref.at[me], own_sem)
    own.start()
    barrier = pltpu.get_barrier_semaphore()
    for offset in range(1, n):
        pl.semaphore_signal(
            barrier, 1, device_id=address((me + offset) % n), device_id_type=MESH_ID
        )
    pl.semaphore_wait(barrier, n - 1)

    def link(offset, source, target):
        return pltpu.make_async_remote_copy(
            src_ref=x_ref.at[target],
            dst_ref=out_ref.at[source],
            send_sem=send_sem.at[offset],
            recv_sem=recv_sem.at[offset],
            device_id=address(target),
            device_id_type=MESH_ID,
        )

    sent = []
    for offset in range(1, n):
        copy = link(offset, me, (me + offset) % n)
        copy.start()
        sent.append(copy)
    for offset in range(1, n):
        link(offset, (me + n - offset) % n, me).wait_recv()
    for copy in sent:
        copy.wait_send()
    own.wait()


def exchange(x, group, collective_id):
    n = x.shape[0]
    space = pltpu.VMEM
    return pl.pallas_call(
        functools.partial(_exchange_kernel, group=group),
        out_shape=jax.ShapeDtypeStruct(x.shape, x.dtype),
        in_specs=[pl.BlockSpec(memory_space=space)],
        out_specs=pl.BlockSpec(memory_space=space),
        scratch_shapes=[
            pltpu.SemaphoreType.DMA(()),
            pltpu.SemaphoreType.DMA((n,)),
            pltpu.SemaphoreType.DMA((n,)),
        ],
        compiler_params=pltpu.CompilerParams(collective_id=collective_id, has_side_effects=True),
    )(x)


def block_moves(n_dp, n_ctx):
    count = n_dp * n_ctx
    return [(f, (f % n_dp) * n_ctx + f // n_dp) for f in range(count)]


def fetch_out_rows(w_out):
    n_dp = lax.axis_size("dp")
    n_ctx = lax.axis_size("ctx")
    moved = lax.ppermute(w_out.astype(jnp.bfloat16), ("dp", "ctx"), perm=block_moves(n_dp, n_ctx))
    return lax.all_gather(moved, "dp", axis=0, tiled=True)


def return_out_rows(grad_out_rows):
    n_dp = lax.axis_size("dp")
    n_ctx = lax.axis_size("ctx")
    part = lax.psum_scatter(grad_out_rows, "dp", scatter_dimension=0, tiled=True)
    back = [(b, a) for a, b in block_moves(n_dp, n_ctx)]
    return lax.ppermute(part, ("dp", "ctx"), perm=back)


def pack_rows(vector, lanes):
    size = vector.shape[0]
    total = -(-size // (16 * lanes)) * 16 * lanes
    return jnp.pad(vector, (0, total - size)).reshape(-1, lanes)


def fetch_small(b_qkv, b_out, b_fc2, ln_gain, ln_shift, b_fc1):
    pieces = (b_qkv, b_out, b_fc2, ln_gain, ln_shift, b_fc1)
    n_dp = lax.axis_size("dp")
    n_ctx = lax.axis_size("ctx")
    packed = pack_rows(jnp.concatenate([p.astype(jnp.bfloat16) for p in pieces]), 128)
    over_dp = exchange(jnp.broadcast_to(packed[None], (n_dp,) + packed.shape), "dp", 4)
    over_all = exchange(jnp.broadcast_to(over_dp[None], (n_ctx,) + over_dp.shape), "ctx", 8)
    table = over_all.transpose(1, 0, 2, 3).reshape(n_dp * n_ctx, -1)
    result = []
    offset = 0
    for p in pieces:
        result.append(table[:, offset : offset + p.shape[0]])
        offset += p.shape[0]
    return result


def reduce_small(small):
    n_dp = lax.axis_size("dp")
    n_ctx = lax.axis_size("ctx")
    count, width = small.shape
    packed = jax.vmap(lambda row: pack_rows(row, 128))(small)
    packed = packed.reshape((n_dp, n_ctx) + packed.shape[1:]).transpose(1, 0, 2, 3)
    over_ctx = jnp.sum(exchange(packed, "ctx", 7), axis=0)
    over_dp = jnp.sum(exchange(over_ctx, "dp", 9), axis=0)
    return over_dp.reshape(-1)[:width]


def fetch_heads(w_qkv, w_fc1, w_fc2, tokens):
    dp_count = lax.axis_size("dp")
    ctx_count = lax.axis_size("ctx")
    rows_piece = w_qkv.shape[0]
    head_width = D // ctx_count
    unit = FF // (dp_count * ctx_count)
    qkv_piece = w_qkv.astype(jnp.bfloat16).reshape(rows_piece, 3, ctx_count, head_width)
    fc1_piece = w_fc1.astype(jnp.bfloat16).reshape(rows_piece, dp_count, ctx_count, unit)
    pieces = jnp.concatenate(
        [
            qkv_piece.transpose(2, 0, 1, 3).reshape(ctx_count, rows_piece, 3 * head_width),
            fc1_piece.transpose(2, 0, 1, 3).reshape(ctx_count, rows_piece, dp_count * unit),
        ],
        axis=2,
    )
    sent = exchange(pieces, "ctx", 5).reshape(ctx_count * rows_piece, -1)
    sent, tokens = lax.optimization_barrier((sent, tokens))
    cols, fc2_rows = (
        lax.all_gather(sent, "dp", axis=0, tiled=True),
        lax.all_gather(w_fc2.astype(jnp.bfloat16), "dp", axis=0, tiled=True),
    )
    return (cols, fc2_rows, tokens)


def return_heads(owned_parts):
    dp_count = lax.axis_size("dp")
    ctx_count = lax.axis_size("ctx")
    head_width = D // ctx_count
    unit = FF // (dp_count * ctx_count)
    rows_piece = owned_parts.shape[0] // ctx_count
    got = exchange(owned_parts.reshape(ctx_count, rows_piece, -1), "ctx", 6)
    qkv = got[:, :, : 3 * head_width].reshape(ctx_count, rows_piece, 3, head_width)
    fc1 = got[:, :, 3 * head_width :].reshape(ctx_count, rows_piece, dp_count, unit)
    return (
        qkv.transpose(1, 2, 0, 3).reshape(rows_piece, 3 * D).astype(jnp.float32),
        fc1.transpose(1, 2, 0, 3).reshape(rows_piece, FF).astype(jnp.float32),
    )


def head_plan(
    ring,
    tokens,
    lengths,
    w_qkv,
    b_qkv,
    w_out,
    b_out,
    w_fc1,
    b_fc1,
    w_fc2,
    b_fc2,
    ln_gain,
    ln_shift,
    cotangent,
):
    rows_here = tokens.shape[0]
    rows_piece = w_qkv.shape[0]
    dp_count = lax.axis_size("dp")
    ctx_count = lax.axis_size("ctx")
    count = dp_count * ctx_count
    group = rows_here * ctx_count
    head_width = D // ctx_count
    local_heads = HEADS // ctx_count
    unit = FF // (dp_count * ctx_count)
    here = lax.axis_index("ctx")
    group_rows = jnp.arange(group, dtype=jnp.int32)
    seg, positions = segment_info(lengths[0], group_rows)
    cosine, sine = rotary_tables(positions)
    qkv_bias, out_bias, fc2_bias, gain_low, shift_low, fc1_table = fetch_small(
        b_qkv, b_out, b_fc2, ln_gain, ln_shift, b_fc1
    )
    qkv_bias = qkv_bias.reshape(3 * D)
    out_bias = out_bias.reshape(D)
    fc2_bias = fc2_bias.reshape(D)
    gain_low = gain_low.reshape(D)
    shift_low = shift_low.reshape(D)
    fc1_bias = lax.dynamic_index_in_dim(
        fc1_table.reshape(dp_count, ctx_count, unit), here, 1, keepdims=False
    ).reshape(dp_count * unit)
    out_rows = fetch_out_rows(w_out)
    cols, fc2_rows, tokens = fetch_heads(w_qkv, w_fc1, w_fc2, tokens)
    gain32 = gain_low.astype(jnp.float32)
    shift32 = shift_low.astype(jnp.float32)
    inputs = tokens.astype(jnp.float32)
    normed, scaled, _ = norm_parts(inputs, gain32, shift32)
    tokens_group = ring_all_gather(tokens, ring, 0)
    late_dy, tokens_group = lax.optimization_barrier((cotangent, tokens_group))
    dy_group = lax.all_gather(late_dy, "ctx", axis=0, tiled=True)
    hidden_group = norm_parts(tokens_group.astype(jnp.float32), gain32, shift32)[2].astype(
        jnp.bfloat16
    )
    bias_cols = lax.dynamic_slice_in_dim(
        qkv_bias.reshape(3, D), here * head_width, head_width, 1
    ).reshape(3 * head_width)
    both = jnp.dot(hidden_group, cols, preferred_element_type=jnp.float32) + jnp.concatenate(
        [bias_cols, fc1_bias]
    ).astype(jnp.float32)
    qkv = both[:, : 3 * head_width]
    pre = both[:, 3 * head_width :]
    shape = (group, local_heads, HEAD_DIM)
    query = rotate(qkv[:, :head_width].reshape(shape), cosine, sine).astype(jnp.bfloat16)
    keys = rotate(qkv[:, head_width : 2 * head_width].reshape(shape), cosine, sine).astype(
        jnp.bfloat16
    )
    values = qkv[:, 2 * head_width :].reshape(shape).astype(jnp.bfloat16)
    q_heads = query.transpose(1, 0, 2)
    k_heads = keys.transpose(1, 0, 2)
    v_heads = values.transpose(1, 0, 2)
    attended_heads, log_total = attention_forward(q_heads, k_heads, v_heads, seg)
    attended = attended_heads.transpose(1, 0, 2).reshape(group, head_width).astype(jnp.bfloat16)
    act = gelu_tanh(pre).astype(jnp.bfloat16)
    branches = ring_reduce_scatter(
        jnp.dot(attended, out_rows, preferred_element_type=jnp.float32)
        + jnp.dot(act, fc2_rows, preferred_element_type=jnp.float32),
        ring,
        2,
    )
    block_out = (
        inputs + branches + out_bias.astype(jnp.float32) + fc2_bias.astype(jnp.float32)
    ).astype(jnp.bfloat16)
    grad_out32 = cotangent.astype(jnp.float32)
    grad_b_fc2 = jnp.sum(grad_out32, axis=0)
    grad_fc2_part = jnp.einsum("tf,td->fd", act, dy_group, preferred_element_type=jnp.float32)
    d_act = jnp.einsum("td,fd->tf", dy_group, fc2_rows, preferred_element_type=jnp.float32)
    d_pre = (d_act * gelu_slope(pre)).astype(jnp.bfloat16)
    grad_bfc1_part = jnp.sum(d_pre.astype(jnp.float32), axis=0)
    grad_out_rows = jnp.einsum("tc,td->cd", attended, dy_group, preferred_element_type=jnp.float32)
    owned_w_out = return_out_rows(grad_out_rows)
    d_attended = (
        jnp.einsum("td,cd->tc", dy_group, out_rows, preferred_element_type=jnp.float32)
        .astype(jnp.bfloat16)
        .reshape(shape)
    )
    d_heads = d_attended.transpose(1, 0, 2)
    delta = jnp.sum(d_heads.astype(jnp.float32) * attended_heads, axis=2, keepdims=True)
    dq_heads, dk_heads, dv_heads = attention_backward(
        q_heads, k_heads, v_heads, d_heads, log_total, delta, seg
    )
    d_query = dq_heads.transpose(1, 0, 2)
    d_keys = dk_heads.transpose(1, 0, 2)
    d_values = dv_heads.transpose(1, 0, 2)
    d_query = rotate_back(d_query, cosine, sine).reshape(group, head_width)
    d_keys = rotate_back(d_keys, cosine, sine).reshape(group, head_width)
    d_qkv = jnp.concatenate([d_query, d_keys, d_values.reshape(group, head_width)], axis=1).astype(
        jnp.bfloat16
    )
    d_both = jnp.concatenate([d_qkv, d_pre], axis=1)
    bias_part = jnp.sum(d_qkv.astype(jnp.float32), axis=0).reshape(3, head_width)
    d_hidden = ring_reduce_scatter(
        jnp.einsum("tc,dc->td", d_both, cols, preferred_element_type=jnp.float32), ring, 3
    )
    grad_gain, grad_shift, d_inputs = norm_back(d_hidden, normed, scaled, gain32)
    grad_tokens = (grad_out32 + d_inputs).astype(jnp.bfloat16)
    weight_parts = jnp.einsum(
        "td,tc->dc", hidden_group, d_both, preferred_element_type=jnp.float32
    ).astype(jnp.bfloat16)
    owned_parts = lax.psum_scatter(weight_parts, "dp", scatter_dimension=0, tiled=True)
    split_qkv, split_fc1 = return_heads(owned_parts)
    owned_fc2 = lax.psum_scatter(
        grad_fc2_part.astype(jnp.bfloat16), "dp", scatter_dimension=0, tiled=True
    ).astype(jnp.float32)
    full_bqkv = lax.dynamic_update_slice_in_dim(
        jnp.zeros((3, D), jnp.float32), bias_part, here * head_width, 1
    )
    full_bfc1 = lax.dynamic_update_slice_in_dim(
        jnp.zeros((dp_count, ctx_count, unit), jnp.float32),
        grad_bfc1_part.reshape(dp_count, 1, unit),
        here,
        1,
    )
    small = jnp.concatenate(
        [
            full_bqkv.reshape(count, -1),
            grad_b_fc2.reshape(count, -1),
            grad_gain.reshape(count, -1),
            grad_shift.reshape(count, -1),
            full_bfc1.reshape(count, -1),
        ],
        axis=1,
    )
    owned_small = reduce_small(small)
    cuts = [0, 3 * D // count, D // count, D // count, D // count, FF // count]
    bounds = [sum(cuts[: i + 1]) for i in range(len(cuts))]
    owned_bqkv, owned_bout, owned_gain, owned_shift, owned_bfc1 = [
        owned_small[bounds[i] : bounds[i + 1]] for i in range(5)
    ]
    return (
        block_out,
        grad_tokens,
        split_qkv.reshape(rows_piece, 3 * D),
        owned_bqkv,
        owned_w_out,
        owned_bout,
        split_fc1.reshape(rows_piece, FF),
        owned_bfc1,
        owned_fc2,
        owned_bout,
        owned_gain,
        owned_shift,
    )


def body(
    ring,
    tokens,
    lengths,
    w_qkv,
    b_qkv,
    w_out,
    b_out,
    w_fc1,
    b_fc1,
    w_fc2,
    b_fc2,
    ln_gain,
    ln_shift,
    cotangent,
):
    return head_plan(
        ring,
        tokens,
        lengths,
        w_qkv,
        b_qkv,
        w_out,
        b_out,
        w_fc1,
        b_fc1,
        w_fc2,
        b_fc2,
        ln_gain,
        ln_shift,
        cotangent,
    )


def solution(mesh):
    in_specs = (
        P(("dp", "ctx"), None),
        P("dp", None),
        P(("dp", "ctx"), None),
        P(("dp", "ctx")),
        P(("dp", "ctx"), None),
        P(("dp", "ctx")),
        P(("dp", "ctx"), None),
        P(("dp", "ctx")),
        P(("dp", "ctx"), None),
        P(("dp", "ctx")),
        P(("dp", "ctx")),
        P(("dp", "ctx")),
        P(("dp", "ctx"), None),
    )
    out_specs = (
        P(("dp", "ctx"), None),
        P(("dp", "ctx"), None),
        P(("dp", "ctx"), None),
        P(("dp", "ctx")),
        P(("dp", "ctx"), None),
        P(("dp", "ctx")),
        P(("dp", "ctx"), None),
        P(("dp", "ctx")),
        P(("dp", "ctx"), None),
        P(("dp", "ctx")),
        P(("dp", "ctx")),
        P(("dp", "ctx")),
    )
    ring = ring_of(mesh)
    return jax.shard_map(functools.partial(body, ring), mesh=mesh, in_specs=in_specs, out_specs=out_specs, check_vma=False)
```

```python
import functools
import math

import jax
import jax.numpy as jnp
from jax import lax
from jax.experimental import pallas as pl
from jax.experimental.pallas import tpu as pltpu
from jax.sharding import PartitionSpec as P

D = 2048
HEADS = 32
HEAD_DIM = 64
ROT = 32
FF = 8192


EPS = 1e-05
GELU_COEF = math.sqrt(2.0 / math.pi)
NEGATIVE = -1e30


def norm_parts(inputs, gain, shift):
    mean = jnp.mean(inputs, axis=-1, keepdims=True)
    centred = inputs - mean
    var = jnp.mean(centred * centred, axis=-1, keepdims=True)
    scaled = lax.rsqrt(var + EPS)
    normed = centred * scaled
    return (normed, scaled, normed * gain + shift)


def norm_back(d_hidden, normed, scaled, gain32):
    grad_gain = jnp.sum(d_hidden * normed, axis=0)
    grad_shift = jnp.sum(d_hidden, axis=0)
    d_normed = d_hidden * gain32
    d_inputs = scaled * (
        d_normed
        - jnp.mean(d_normed, axis=-1, keepdims=True)
        - normed * jnp.mean(d_normed * normed, axis=-1, keepdims=True)
    )
    return (grad_gain, grad_shift, d_inputs)


def gelu_tanh(pre):
    return 0.5 * pre * (1.0 + jnp.tanh(GELU_COEF * (pre + 0.044715 * pre * pre * pre)))


def gelu_slope(pre):
    tangent = jnp.tanh(GELU_COEF * (pre + 0.044715 * pre * pre * pre))
    return 0.5 * (1.0 + tangent) + 0.5 * pre * (1.0 - tangent * tangent) * GELU_COEF * (
        1.0 + 3.0 * 0.044715 * pre * pre
    )


def rotary_tables(positions):
    half = ROT // 2
    freq = jnp.exp(jnp.arange(half, dtype=jnp.float32) * (-2.0 * math.log(10000.0) / ROT))
    angle = positions.astype(jnp.float32)[:, None] * freq[None, :]
    return (jnp.cos(angle)[:, None, :], jnp.sin(angle)[:, None, :])


def rotate(heads, cosine, sine):
    half = ROT // 2
    first = heads[..., :half]
    second = heads[..., half:ROT]
    return jnp.concatenate(
        [first * cosine - second * sine, second * cosine + first * sine, heads[..., ROT:]], axis=-1
    )


def rotate_back(grads, cosine, sine):
    half = ROT // 2
    first = grads[..., :half]
    second = grads[..., half:ROT]
    return jnp.concatenate(
        [first * cosine + second * sine, second * cosine - first * sine, grads[..., ROT:]], axis=-1
    )


def segment_info(lengths_row, rows):
    ends = jnp.cumsum(lengths_row)
    starts = ends - lengths_row
    seg = jnp.sum((rows[:, None] >= ends[None, :]).astype(jnp.int32), axis=1)
    onehot = seg[:, None] == jnp.arange(lengths_row.shape[0], dtype=jnp.int32)[None, :]
    first_rows = jnp.sum(jnp.where(onehot, starts[None, :], 0), axis=1)
    return (seg, rows - first_rows)


TRANS_B = (((1,), (1,)), ((), ()))


def _allowed(segq_ref, segk_ref, i, j, tq, tk, causal):
    same = segq_ref[...] == segk_ref[...]
    if not causal:
        return same
    rows = i * tq + lax.broadcasted_iota(jnp.int32, (tq, tk), 0)
    cols = j * tk + lax.broadcasted_iota(jnp.int32, (tq, tk), 1)
    return same & (cols <= rows)


def _fwd_kernel(q_ref, k_ref, v_ref, segq_ref, segk_ref, o_ref, lse_ref, m_sc, l_sc, acc_sc, *, tq, tk, scale):
    i = pl.program_id(1)
    j = pl.program_id(2)

    @pl.when(j == 0)
    def _():
        m_sc[...] = jnp.full_like(m_sc, NEGATIVE)
        l_sc[...] = jnp.zeros_like(l_sc)
        acc_sc[...] = jnp.zeros_like(acc_sc)

    def absorb(causal):
        q = q_ref[0]
        k = k_ref[0]
        s = lax.dot_general(q, k, TRANS_B, preferred_element_type=jnp.float32) * scale
        s = jnp.where(_allowed(segq_ref, segk_ref, i, j, tq, tk, causal), s, -jnp.inf)
        m_prev = m_sc[...]
        m_new = jnp.maximum(m_prev, jnp.max(s, axis=1, keepdims=True))
        factor = jnp.exp(m_prev - m_new)
        p = jnp.exp(s - m_new)
        l_sc[...] = l_sc[...] * factor + jnp.sum(p, axis=1, keepdims=True)
        acc_sc[...] = acc_sc[...] * factor + jnp.dot(
            p.astype(jnp.bfloat16), v_ref[0], preferred_element_type=jnp.float32
        )
        m_sc[...] = m_new

    below = (j + 1) * tk <= i * tq
    near = jnp.logical_and(jnp.logical_not(below), j * tk <= i * tq + tq - 1)

    @pl.when(below)
    def _():
        absorb(False)

    @pl.when(near)
    def _():
        absorb(True)

    @pl.when(j == pl.num_programs(2) - 1)
    def _():
        total = l_sc[...]
        o_ref[0] = acc_sc[...] / total
        lse_ref[0] = m_sc[...] + jnp.log(total)


def attention_forward(q, k, v, seg, tq=512, tk=512):
    heads, total, dim = q.shape
    nq, nk = total // tq, total // tk
    scale = 1.0 / math.sqrt(dim)
    segq = seg.reshape(total, 1)
    segk = seg.reshape(1, total)

    def kv_map(h, i, j):
        return (h, jnp.minimum(j, (i * tq + tq - 1) // tk), 0)

    def segk_map(h, i, j):
        return (0, jnp.minimum(j, (i * tq + tq - 1) // tk))

    return pl.pallas_call(
        functools.partial(_fwd_kernel, tq=tq, tk=tk, scale=scale),
        out_shape=(
            jax.ShapeDtypeStruct((heads, total, dim), jnp.float32),
            jax.ShapeDtypeStruct((heads, total, 1), jnp.float32),
        ),
        grid=(heads, nq, nk),
        in_specs=[
            pl.BlockSpec((1, tq, dim), lambda h, i, j: (h, i, 0)),
            pl.BlockSpec((1, tk, dim), kv_map),
            pl.BlockSpec((1, tk, dim), kv_map),
            pl.BlockSpec((tq, 1), lambda h, i, j: (i, 0)),
            pl.BlockSpec((1, tk), segk_map),
        ],
        out_specs=[
            pl.BlockSpec((1, tq, dim), lambda h, i, j: (h, i, 0)),
            pl.BlockSpec((1, tq, 1), lambda h, i, j: (h, i, 0)),
        ],
        scratch_shapes=[
            pltpu.VMEM((tq, 1), jnp.float32),
            pltpu.VMEM((tq, 1), jnp.float32),
            pltpu.VMEM((tq, dim), jnp.float32),
        ],
        cost_estimate=pl.CostEstimate(
            flops=2 * heads * total * total * dim,
            transcendentals=heads * total * total // 2,
            bytes_accessed=heads * total * dim * 10,
        ),
    )(q, k, v, segq, segk)


def _bwd_kernel(q_ref, k_ref, v_ref, do_ref, lse_ref, delta_ref, segq_ref, segk_ref, dq_ref, dk_ref, dv_ref, *, tq, tk, scale):
    j = pl.program_id(1)
    i = pl.program_id(2)

    @pl.when((j == 0) & (i == 0))
    def _():
        dq_ref[...] = jnp.zeros_like(dq_ref)

    @pl.when(i == 0)
    def _():
        dk_ref[...] = jnp.zeros_like(dk_ref)
        dv_ref[...] = jnp.zeros_like(dv_ref)

    def absorb(causal):
        q = q_ref[0]
        k = k_ref[0]
        do = do_ref[0]
        s = lax.dot_general(q, k, TRANS_B, preferred_element_type=jnp.float32) * scale
        s = jnp.where(_allowed(segq_ref, segk_ref, i, j, tq, tk, causal), s, -jnp.inf)
        p = jnp.exp(s - lse_ref[0])
        dp = lax.dot_general(do, v_ref[0], TRANS_B, preferred_element_type=jnp.float32)
        ds = (p * (dp - delta_ref[0])).astype(jnp.bfloat16)
        dv_ref[0] += lax.dot(p.astype(jnp.bfloat16).T, do, preferred_element_type=jnp.float32)
        dk_ref[0] += lax.dot(ds.T, q, preferred_element_type=jnp.float32) * scale
        rows = pl.ds(pl.multiple_of(i * tq, tq), tq)
        dq_ref[0, rows, :] += lax.dot(ds, k, preferred_element_type=jnp.float32) * scale

    below = (j + 1) * tk <= i * tq
    near = jnp.logical_and(jnp.logical_not(below), i * tq + tq - 1 >= j * tk)

    @pl.when(below)
    def _():
        absorb(False)

    @pl.when(near)
    def _():
        absorb(True)


def attention_backward(q, k, v, do, lse, delta, seg, tq=512, tk=512):
    heads, total, dim = q.shape
    nq, nk = total // tq, total // tk
    scale = 1.0 / math.sqrt(dim)
    segq = seg.reshape(total, 1)
    segk = seg.reshape(1, total)

    def q_map(h, j, i):
        return (h, jnp.maximum(i, (j * tk) // tq), 0)

    def segq_map(h, j, i):
        return (jnp.maximum(i, (j * tk) // tq), 0)

    return pl.pallas_call(
        functools.partial(_bwd_kernel, tq=tq, tk=tk, scale=scale),
        out_shape=(
            jax.ShapeDtypeStruct((heads, total, dim), jnp.float32),
            jax.ShapeDtypeStruct((heads, total, dim), jnp.float32),
            jax.ShapeDtypeStruct((heads, total, dim), jnp.float32),
        ),
        grid=(heads, nk, nq),
        in_specs=[
            pl.BlockSpec((1, tq, dim), q_map),
            pl.BlockSpec((1, tk, dim), lambda h, j, i: (h, j, 0)),
            pl.BlockSpec((1, tk, dim), lambda h, j, i: (h, j, 0)),
            pl.BlockSpec((1, tq, dim), q_map),
            pl.BlockSpec((1, tq, 1), q_map),
            pl.BlockSpec((1, tq, 1), q_map),
            pl.BlockSpec((tq, 1), segq_map),
            pl.BlockSpec((1, tk), lambda h, j, i: (0, j)),
        ],
        out_specs=[
            pl.BlockSpec((1, total, dim), lambda h, j, i: (h, 0, 0)),
            pl.BlockSpec((1, tk, dim), lambda h, j, i: (h, j, 0)),
            pl.BlockSpec((1, tk, dim), lambda h, j, i: (h, j, 0)),
        ],
        cost_estimate=pl.CostEstimate(
            flops=5 * heads * total * total * dim,
            transcendentals=heads * total * total // 2,
            bytes_accessed=heads * total * dim * 24,
        ),
    )(q, k, v, do, lse, delta, segq, segk)


MESH_ID = pl.DeviceIdType.MESH


class Ring:
    def __init__(self, size, a_stride, b_stride):
        self.size = size
        self.half = size // 2
        self.a_stride = a_stride
        self.b_stride = b_stride

    def position(self, c):
        a = (c // self.a_stride) % self.half
        b = (c // self.b_stride) % 2
        return a + b * (2 * self.half - 1 - 2 * a)

    def device(self, pos):
        pos = pos % self.size
        b = pos // self.half
        a = pos + b * (2 * self.half - 1 - 2 * pos)
        return a * self.a_stride + b * self.b_stride


def ring_of(mesh):
    size = mesh.shape["ctx"]
    devices = list(mesh.devices.reshape(-1, size)[0])
    try:
        coords = [tuple(d.coords) for d in devices]
    except AttributeError:
        coords = None
    if coords and size % 2 == 0 and size >= 4:
        for b_stride in range(1, size):
            for a_stride in range(1, size):
                ring = Ring(size, a_stride, b_stride)
                order = [ring.device(p) for p in range(size)]
                if sorted(order) != list(range(size)):
                    continue
                hops = [
                    sum(abs(x - y) for x, y in zip(coords[order[p]], coords[order[(p + 1) % size]]))
                    for p in range(size)
                ]
                if max(hops) == 1:
                    return ring
    return Ring(size, 2, 1) if size % 2 == 0 and size >= 4 else None


def _barrier(g, left, right):
    barrier = pltpu.get_barrier_semaphore()
    for other in (left, right):
        pl.semaphore_signal(barrier, 1, device_id=(g, other), device_id_type=MESH_ID)
    pl.semaphore_wait(barrier, 2)


def _gather_kernel(x_ref, y_ref, own_sem, send_sem, recv_sem, *, ring, rows):
    n = ring.size
    half = rows // 2
    g = lax.axis_index("dp")
    c = lax.axis_index("ctx")
    pos = ring.position(c)
    right = ring.device(pos + 1)
    left = ring.device(pos + n - 1)
    own = pltpu.make_async_copy(x_ref, y_ref.at[pl.ds(c * rows, rows)], own_sem)
    own.start()
    _barrier(g, left, right)

    def link(direction, step, origin, source):
        offset = origin * rows + direction * half
        return pltpu.make_async_remote_copy(
            src_ref=source,
            dst_ref=y_ref.at[pl.ds(offset, half)],
            send_sem=send_sem.at[direction, step],
            recv_sem=recv_sem.at[direction, step],
            device_id=(g, right if direction == 0 else left),
            device_id_type=MESH_ID,
        )

    sent = []
    for step in range(n - 1):
        origins = (ring.device(pos - step + n), ring.device(pos + step))
        for direction in (0, 1):
            origin = origins[direction]
            if step == 0:
                source = x_ref.at[pl.ds(direction * half, half)]
            else:
                link(direction, step - 1, origin, None if False else y_ref.at[pl.ds(origin * rows + direction * half, half)]).wait_recv()
                source = y_ref.at[pl.ds(origin * rows + direction * half, half)]
            copy = link(direction, step, origin, source)
            copy.start()
            sent.append(copy)
    last = n - 2
    for direction, origin in ((0, ring.device(pos - last - 1 + n)), (1, ring.device(pos + last + 1))):
        link(direction, last, origin, y_ref.at[pl.ds(origin * rows + direction * half, half)]).wait_recv()
    for copy in sent:
        copy.wait_send()
    own.wait()


def ring_all_gather(x, ring, collective_id):
    rows, cols = x.shape
    n = ring.size
    return pl.pallas_call(
        functools.partial(_gather_kernel, ring=ring, rows=rows),
        out_shape=jax.ShapeDtypeStruct((n * rows, cols), x.dtype),
        in_specs=[pl.BlockSpec(memory_space=pl.ANY)],
        out_specs=pl.BlockSpec(memory_space=pl.ANY),
        scratch_shapes=[
            pltpu.SemaphoreType.DMA(()),
            pltpu.SemaphoreType.DMA((2, n - 1)),
            pltpu.SemaphoreType.DMA((2, n - 1)),
        ],
        compiler_params=pltpu.CompilerParams(collective_id=collective_id, has_side_effects=True),
    )(x)


def _scatter_kernel(p_ref, out_ref, recv_buf, send_buf, send_sem, recv_sem, *, ring, rows):
    n = ring.size
    half = rows // 2
    g = lax.axis_index("dp")
    c = lax.axis_index("ctx")
    pos = ring.position(c)
    right = ring.device(pos + 1)
    left = ring.device(pos + n - 1)
    _barrier(g, left, right)

    def link(direction, step):
        return pltpu.make_async_remote_copy(
            src_ref=send_buf.at[direction, step],
            dst_ref=recv_buf.at[direction, step],
            send_sem=send_sem.at[direction, step],
            recv_sem=recv_sem.at[direction, step],
            device_id=(g, right if direction == 0 else left),
            device_id_type=MESH_ID,
        )

    sent = []
    for step in range(n - 1):
        targets = (ring.device(pos - 1 - step + 2 * n), ring.device(pos + 1 + step))
        for direction in (0, 1):
            start = pl.multiple_of(targets[direction] * rows + direction * half, half)
            total = p_ref[pl.ds(start, half), :].astype(jnp.float32)
            if step > 0:
                link(direction, step - 1).wait_recv()
                total = total + recv_buf[direction, step - 1].astype(jnp.float32)
            send_buf[direction, step] = total.astype(send_buf.dtype)
            copy = link(direction, step)
            copy.start()
            sent.append(copy)
    for direction in (0, 1):
        link(direction, n - 2).wait_recv()
        start = pl.multiple_of(c * rows + direction * half, half)
        out_ref[pl.ds(direction * half, half), :] = (
            p_ref[pl.ds(start, half), :].astype(jnp.float32)
            + recv_buf[direction, n - 2].astype(jnp.float32)
        ).astype(out_ref.dtype)
    for copy in sent:
        copy.wait_send()


def ring_reduce_scatter(p, ring, collective_id, out_dtype=jnp.float32, wire=jnp.bfloat16):
    total_rows, cols = p.shape
    n = ring.size
    rows = total_rows // n
    half = rows // 2
    return pl.pallas_call(
        functools.partial(_scatter_kernel, ring=ring, rows=rows),
        out_shape=jax.ShapeDtypeStruct((rows, cols), out_dtype),
        in_specs=[pl.BlockSpec(memory_space=pltpu.VMEM)],
        out_specs=pl.BlockSpec(memory_space=pltpu.VMEM),
        scratch_shapes=[
            pltpu.VMEM((2, n - 1, half, cols), wire),
            pltpu.VMEM((2, n - 1, half, cols), wire),
            pltpu.SemaphoreType.DMA((2, n - 1)),
            pltpu.SemaphoreType.DMA((2, n - 1)),
        ],
        compiler_params=pltpu.CompilerParams(
            collective_id=collective_id, has_side_effects=True, vmem_limit_bytes=60 * 1024 * 1024
        ),
    )(p)


def _exchange_kernel(x_ref, out_ref, own_sem, send_sem, recv_sem, *, group):
    n = x_ref.shape[0]
    g = lax.axis_index("dp")
    c = lax.axis_index("ctx")
    n_ctx = lax.axis_size("ctx")
    me = {"all": g * n_ctx + c, "ctx": c, "dp": g}[group]

    def address(member):
        if group == "all":
            return (member // n_ctx, member % n_ctx)
        if group == "ctx":
            return (g, member)
        return (member, c)

    own = pltpu.make_async_copy(x_ref.at[me], out_ref.at[me], own_sem)
    own.start()
    barrier = pltpu.get_barrier_semaphore()
    for offset in range(1, n):
        pl.semaphore_signal(
            barrier, 1, device_id=address((me + offset) % n), device_id_type=MESH_ID
        )
    pl.semaphore_wait(barrier, n - 1)

    def link(offset, source, target):
        return pltpu.make_async_remote_copy(
            src_ref=x_ref.at[target],
            dst_ref=out_ref.at[source],
            send_sem=send_sem.at[offset],
            recv_sem=recv_sem.at[offset],
            device_id=address(target),
            device_id_type=MESH_ID,
        )

    sent = []
    for offset in range(1, n):
        copy = link(offset, me, (me + offset) % n)
        copy.start()
        sent.append(copy)
    for offset in range(1, n):
        link(offset, (me + n - offset) % n, me).wait_recv()
    for copy in sent:
        copy.wait_send()
    own.wait()


def exchange(x, group, collective_id):
    n = x.shape[0]
    space = pltpu.VMEM
    return pl.pallas_call(
        functools.partial(_exchange_kernel, group=group),
        out_shape=jax.ShapeDtypeStruct(x.shape, x.dtype),
        in_specs=[pl.BlockSpec(memory_space=space)],
        out_specs=pl.BlockSpec(memory_space=space),
        scratch_shapes=[
            pltpu.SemaphoreType.DMA(()),
            pltpu.SemaphoreType.DMA((n,)),
            pltpu.SemaphoreType.DMA((n,)),
        ],
        compiler_params=pltpu.CompilerParams(collective_id=collective_id, has_side_effects=True),
    )(x)


def block_moves(n_dp, n_ctx):
    count = n_dp * n_ctx
    return [(f, (f % n_dp) * n_ctx + f // n_dp) for f in range(count)]


def fetch_out_rows(w_out):
    n_dp = lax.axis_size("dp")
    n_ctx = lax.axis_size("ctx")
    moved = lax.ppermute(w_out.astype(jnp.bfloat16), ("dp", "ctx"), perm=block_moves(n_dp, n_ctx))
    return lax.all_gather(moved, "dp", axis=0, tiled=True)


def return_out_rows(grad_out_rows):
    n_dp = lax.axis_size("dp")
    n_ctx = lax.axis_size("ctx")
    part = lax.psum_scatter(grad_out_rows, "dp", scatter_dimension=0, tiled=True)
    back = [(b, a) for a, b in block_moves(n_dp, n_ctx)]
    return lax.ppermute(part, ("dp", "ctx"), perm=back)


def pack_rows(vector, lanes):
    size = vector.shape[0]
    total = -(-size // (16 * lanes)) * 16 * lanes
    return jnp.pad(vector, (0, total - size)).reshape(-1, lanes)


def fetch_small(b_qkv, b_out, b_fc2, ln_gain, ln_shift, b_fc1):
    pieces = (b_qkv, b_out, b_fc2, ln_gain, ln_shift, b_fc1)
    n_dp = lax.axis_size("dp")
    n_ctx = lax.axis_size("ctx")
    packed = pack_rows(jnp.concatenate([p.astype(jnp.bfloat16) for p in pieces]), 128)
    over_dp = exchange(jnp.broadcast_to(packed[None], (n_dp,) + packed.shape), "dp", 4)
    over_all = exchange(jnp.broadcast_to(over_dp[None], (n_ctx,) + over_dp.shape), "ctx", 8)
    table = over_all.transpose(1, 0, 2, 3).reshape(n_dp * n_ctx, -1)
    result = []
    offset = 0
    for p in pieces:
        result.append(table[:, offset : offset + p.shape[0]])
        offset += p.shape[0]
    return result


def reduce_small(small):
    n_dp = lax.axis_size("dp")
    n_ctx = lax.axis_size("ctx")
    count, width = small.shape
    packed = jax.vmap(lambda row: pack_rows(row, 128))(small)
    packed = packed.reshape((n_dp, n_ctx) + packed.shape[1:]).transpose(1, 0, 2, 3)
    over_ctx = jnp.sum(exchange(packed, "ctx", 7), axis=0)
    over_dp = jnp.sum(exchange(over_ctx, "dp", 9), axis=0)
    return over_dp.reshape(-1)[:width]


def fetch_heads(w_qkv, w_fc1, w_fc2, tokens):
    dp_count = lax.axis_size("dp")
    ctx_count = lax.axis_size("ctx")
    rows_piece = w_qkv.shape[0]
    head_width = D // ctx_count
    unit = FF // (dp_count * ctx_count)
    qkv_piece = w_qkv.astype(jnp.bfloat16).reshape(rows_piece, 3, ctx_count, head_width)
    fc1_piece = w_fc1.astype(jnp.bfloat16).reshape(rows_piece, dp_count, ctx_count, unit)
    pieces = jnp.concatenate(
        [
            qkv_piece.transpose(2, 0, 1, 3).reshape(ctx_count, rows_piece, 3 * head_width),
            fc1_piece.transpose(2, 0, 1, 3).reshape(ctx_count, rows_piece, dp_count * unit),
        ],
        axis=2,
    )
    sent = exchange(pieces, "ctx", 5).reshape(ctx_count * rows_piece, -1)
    sent, tokens = lax.optimization_barrier((sent, tokens))
    cols, fc2_rows = (
        lax.all_gather(sent, "dp", axis=0, tiled=True),
        lax.all_gather(w_fc2.astype(jnp.bfloat16), "dp", axis=0, tiled=True),
    )
    return (cols, fc2_rows, tokens)


def return_heads(owned_parts):
    dp_count = lax.axis_size("dp")
    ctx_count = lax.axis_size("ctx")
    head_width = D // ctx_count
    unit = FF // (dp_count * ctx_count)
    rows_piece = owned_parts.shape[0] // ctx_count
    got = exchange(owned_parts.reshape(ctx_count, rows_piece, -1), "ctx", 6)
    qkv = got[:, :, : 3 * head_width].reshape(ctx_count, rows_piece, 3, head_width)
    fc1 = got[:, :, 3 * head_width :].reshape(ctx_count, rows_piece, dp_count, unit)
    return (
        qkv.transpose(1, 2, 0, 3).reshape(rows_piece, 3 * D).astype(jnp.float32),
        fc1.transpose(1, 2, 0, 3).reshape(rows_piece, FF).astype(jnp.float32),
    )


def head_plan(
    ring,
    tokens,
    lengths,
    w_qkv,
    b_qkv,
    w_out,
    b_out,
    w_fc1,
    b_fc1,
    w_fc2,
    b_fc2,
    ln_gain,
    ln_shift,
    cotangent,
):
    rows_here = tokens.shape[0]
    rows_piece = w_qkv.shape[0]
    dp_count = lax.axis_size("dp")
    ctx_count = lax.axis_size("ctx")
    count = dp_count * ctx_count
    group = rows_here * ctx_count
    head_width = D // ctx_count
    local_heads = HEADS // ctx_count
    unit = FF // (dp_count * ctx_count)
    here = lax.axis_index("ctx")
    group_rows = jnp.arange(group, dtype=jnp.int32)
    seg, positions = segment_info(lengths[0], group_rows)
    cosine, sine = rotary_tables(positions)
    qkv_bias, out_bias, fc2_bias, gain_low, shift_low, fc1_table = fetch_small(
        b_qkv, b_out, b_fc2, ln_gain, ln_shift, b_fc1
    )
    qkv_bias = qkv_bias.reshape(3 * D)
    out_bias = out_bias.reshape(D)
    fc2_bias = fc2_bias.reshape(D)
    gain_low = gain_low.reshape(D)
    shift_low = shift_low.reshape(D)
    fc1_bias = lax.dynamic_index_in_dim(
        fc1_table.reshape(dp_count, ctx_count, unit), here, 1, keepdims=False
    ).reshape(dp_count * unit)
    out_rows = fetch_out_rows(w_out)
    cols, fc2_rows, tokens = fetch_heads(w_qkv, w_fc1, w_fc2, tokens)
    gain32 = gain_low.astype(jnp.float32)
    shift32 = shift_low.astype(jnp.float32)
    inputs = tokens.astype(jnp.float32)
    normed, scaled, _ = norm_parts(inputs, gain32, shift32)
    tokens_group = ring_all_gather(tokens, ring, 0)
    late_dy, tokens_group = lax.optimization_barrier((cotangent, tokens_group))
    dy_group = lax.all_gather(late_dy, "ctx", axis=0, tiled=True)
    hidden_group = norm_parts(tokens_group.astype(jnp.float32), gain32, shift32)[2].astype(
        jnp.bfloat16
    )
    bias_cols = lax.dynamic_slice_in_dim(
        qkv_bias.reshape(3, D), here * head_width, head_width, 1
    ).reshape(3 * head_width)
    both = jnp.dot(hidden_group, cols, preferred_element_type=jnp.float32) + jnp.concatenate(
        [bias_cols, fc1_bias]
    ).astype(jnp.float32)
    qkv = both[:, : 3 * head_width]
    pre = both[:, 3 * head_width :]
    shape = (group, local_heads, HEAD_DIM)
    query = rotate(qkv[:, :head_width].reshape(shape), cosine, sine).astype(jnp.bfloat16)
    keys = rotate(qkv[:, head_width : 2 * head_width].reshape(shape), cosine, sine).astype(
        jnp.bfloat16
    )
    values = qkv[:, 2 * head_width :].reshape(shape).astype(jnp.bfloat16)
    q_heads = query.transpose(1, 0, 2)
    k_heads = keys.transpose(1, 0, 2)
    v_heads = values.transpose(1, 0, 2)
    attended_heads, log_total = attention_forward(q_heads, k_heads, v_heads, seg)
    attended = attended_heads.transpose(1, 0, 2).reshape(group, head_width).astype(jnp.bfloat16)
    act = gelu_tanh(pre).astype(jnp.bfloat16)
    branches = ring_reduce_scatter(
        jnp.dot(attended, out_rows, preferred_element_type=jnp.float32)
        + jnp.dot(act, fc2_rows, preferred_element_type=jnp.float32),
        ring,
        2,
    )
    block_out = (
        inputs + branches + out_bias.astype(jnp.float32) + fc2_bias.astype(jnp.float32)
    ).astype(jnp.bfloat16)
    grad_out32 = cotangent.astype(jnp.float32)
    grad_b_fc2 = jnp.sum(grad_out32, axis=0)
    grad_fc2_part = jnp.einsum("tf,td->fd", act, dy_group, preferred_element_type=jnp.float32)
    d_act = jnp.einsum("td,fd->tf", dy_group, fc2_rows, preferred_element_type=jnp.float32)
    d_pre = (d_act * gelu_slope(pre)).astype(jnp.bfloat16)
    grad_bfc1_part = jnp.sum(d_pre.astype(jnp.float32), axis=0)
    grad_out_rows = jnp.einsum("tc,td->cd", attended, dy_group, preferred_element_type=jnp.float32)
    owned_w_out = return_out_rows(grad_out_rows)
    d_attended = (
        jnp.einsum("td,cd->tc", dy_group, out_rows, preferred_element_type=jnp.float32)
        .astype(jnp.bfloat16)
        .reshape(shape)
    )
    d_heads = d_attended.transpose(1, 0, 2)
    delta = jnp.sum(d_heads.astype(jnp.float32) * attended_heads, axis=2, keepdims=True)
    dq_heads, dk_heads, dv_heads = attention_backward(
        q_heads, k_heads, v_heads, d_heads, log_total, delta, seg
    )
    d_query = dq_heads.transpose(1, 0, 2)
    d_keys = dk_heads.transpose(1, 0, 2)
    d_values = dv_heads.transpose(1, 0, 2)
    d_query = rotate_back(d_query, cosine, sine).reshape(group, head_width)
    d_keys = rotate_back(d_keys, cosine, sine).reshape(group, head_width)
    d_qkv = jnp.concatenate([d_query, d_keys, d_values.reshape(group, head_width)], axis=1).astype(
        jnp.bfloat16
    )
    d_both = jnp.concatenate([d_qkv, d_pre], axis=1)
    bias_part = jnp.sum(d_qkv.astype(jnp.float32), axis=0).reshape(3, head_width)
    d_hidden = ring_reduce_scatter(
        jnp.einsum("tc,dc->td", d_both, cols, preferred_element_type=jnp.float32), ring, 3
    )
    weight_parts = jnp.einsum(
        "td,tc->dc", hidden_group, d_both, preferred_element_type=jnp.float32
    ).astype(jnp.bfloat16)
    owned_parts = lax.psum_scatter(weight_parts, "dp", scatter_dimension=0, tiled=True)
    split_qkv, split_fc1 = return_heads(owned_parts)
    d_hidden, split_qkv, split_fc1 = lax.optimization_barrier((d_hidden, split_qkv, split_fc1))
    grad_gain, grad_shift, d_inputs = norm_back(d_hidden, normed, scaled, gain32)
    grad_tokens = (grad_out32 + d_inputs).astype(jnp.bfloat16)
    owned_fc2 = lax.psum_scatter(
        grad_fc2_part.astype(jnp.bfloat16), "dp", scatter_dimension=0, tiled=True
    ).astype(jnp.float32)
    full_bqkv = lax.dynamic_update_slice_in_dim(
        jnp.zeros((3, D), jnp.float32), bias_part, here * head_width, 1
    )
    full_bfc1 = lax.dynamic_update_slice_in_dim(
        jnp.zeros((dp_count, ctx_count, unit), jnp.float32),
        grad_bfc1_part.reshape(dp_count, 1, unit),
        here,
        1,
    )
    small = jnp.concatenate(
        [
            full_bqkv.reshape(count, -1),
            grad_b_fc2.reshape(count, -1),
            grad_gain.reshape(count, -1),
            grad_shift.reshape(count, -1),
            full_bfc1.reshape(count, -1),
        ],
        axis=1,
    )
    owned_small = reduce_small(small)
    cuts = [0, 3 * D // count, D // count, D // count, D // count, FF // count]
    bounds = [sum(cuts[: i + 1]) for i in range(len(cuts))]
    owned_bqkv, owned_bout, owned_gain, owned_shift, owned_bfc1 = [
        owned_small[bounds[i] : bounds[i + 1]] for i in range(5)
    ]
    return (
        block_out,
        grad_tokens,
        split_qkv.reshape(rows_piece, 3 * D),
        owned_bqkv,
        owned_w_out,
        owned_bout,
        split_fc1.reshape(rows_piece, FF),
        owned_bfc1,
        owned_fc2,
        owned_bout,
        owned_gain,
        owned_shift,
    )


def body(
    ring,
    tokens,
    lengths,
    w_qkv,
    b_qkv,
    w_out,
    b_out,
    w_fc1,
    b_fc1,
    w_fc2,
    b_fc2,
    ln_gain,
    ln_shift,
    cotangent,
):
    return head_plan(
        ring,
        tokens,
        lengths,
        w_qkv,
        b_qkv,
        w_out,
        b_out,
        w_fc1,
        b_fc1,
        w_fc2,
        b_fc2,
        ln_gain,
        ln_shift,
        cotangent,
    )


def solution(mesh):
    in_specs = (
        P(("dp", "ctx"), None),
        P("dp", None),
        P(("dp", "ctx"), None),
        P(("dp", "ctx")),
        P(("dp", "ctx"), None),
        P(("dp", "ctx")),
        P(("dp", "ctx"), None),
        P(("dp", "ctx")),
        P(("dp", "ctx"), None),
        P(("dp", "ctx")),
        P(("dp", "ctx")),
        P(("dp", "ctx")),
        P(("dp", "ctx"), None),
    )
    out_specs = (
        P(("dp", "ctx"), None),
        P(("dp", "ctx"), None),
        P(("dp", "ctx"), None),
        P(("dp", "ctx")),
        P(("dp", "ctx"), None),
        P(("dp", "ctx")),
        P(("dp", "ctx"), None),
        P(("dp", "ctx")),
        P(("dp", "ctx"), None),
        P(("dp", "ctx")),
        P(("dp", "ctx")),
        P(("dp", "ctx")),
    )
    ring = ring_of(mesh)
    return jax.shard_map(functools.partial(body, ring), mesh=mesh, in_specs=in_specs, out_specs=out_specs, check_vma=False)
```

```python
import functools
import math

import jax
import jax.numpy as jnp
from jax import lax
from jax.experimental import pallas as pl
from jax.experimental.pallas import tpu as pltpu
from jax.sharding import PartitionSpec as P

D = 2048
HEADS = 32
HEAD_DIM = 64
ROT = 32
FF = 8192


EPS = 1e-05
GELU_COEF = math.sqrt(2.0 / math.pi)
NEGATIVE = -1e30


def norm_parts(inputs, gain, shift):
    mean = jnp.mean(inputs, axis=-1, keepdims=True)
    centred = inputs - mean
    var = jnp.mean(centred * centred, axis=-1, keepdims=True)
    scaled = lax.rsqrt(var + EPS)
    normed = centred * scaled
    return (normed, scaled, normed * gain + shift)


def norm_back(d_hidden, normed, scaled, gain32):
    grad_gain = jnp.sum(d_hidden * normed, axis=0)
    grad_shift = jnp.sum(d_hidden, axis=0)
    d_normed = d_hidden * gain32
    d_inputs = scaled * (
        d_normed
        - jnp.mean(d_normed, axis=-1, keepdims=True)
        - normed * jnp.mean(d_normed * normed, axis=-1, keepdims=True)
    )
    return (grad_gain, grad_shift, d_inputs)


def gelu_tanh(pre):
    return 0.5 * pre * (1.0 + jnp.tanh(GELU_COEF * (pre + 0.044715 * pre * pre * pre)))


def gelu_slope(pre):
    tangent = jnp.tanh(GELU_COEF * (pre + 0.044715 * pre * pre * pre))
    return 0.5 * (1.0 + tangent) + 0.5 * pre * (1.0 - tangent * tangent) * GELU_COEF * (
        1.0 + 3.0 * 0.044715 * pre * pre
    )


def rotary_tables(positions):
    half = ROT // 2
    freq = jnp.exp(jnp.arange(half, dtype=jnp.float32) * (-2.0 * math.log(10000.0) / ROT))
    angle = positions.astype(jnp.float32)[:, None] * freq[None, :]
    return (jnp.cos(angle)[:, None, :], jnp.sin(angle)[:, None, :])


def rotate(heads, cosine, sine):
    half = ROT // 2
    first = heads[..., :half]
    second = heads[..., half:ROT]
    return jnp.concatenate(
        [first * cosine - second * sine, second * cosine + first * sine, heads[..., ROT:]], axis=-1
    )


def rotate_back(grads, cosine, sine):
    half = ROT // 2
    first = grads[..., :half]
    second = grads[..., half:ROT]
    return jnp.concatenate(
        [first * cosine + second * sine, second * cosine - first * sine, grads[..., ROT:]], axis=-1
    )


def segment_info(lengths_row, rows):
    ends = jnp.cumsum(lengths_row)
    starts = ends - lengths_row
    seg = jnp.sum((rows[:, None] >= ends[None, :]).astype(jnp.int32), axis=1)
    onehot = seg[:, None] == jnp.arange(lengths_row.shape[0], dtype=jnp.int32)[None, :]
    first_rows = jnp.sum(jnp.where(onehot, starts[None, :], 0), axis=1)
    return (seg, rows - first_rows)


TRANS_B = (((1,), (1,)), ((), ()))


def _allowed(segq_ref, segk_ref, i, j, tq, tk, causal):
    same = segq_ref[...] == segk_ref[...]
    if not causal:
        return same
    rows = i * tq + lax.broadcasted_iota(jnp.int32, (tq, tk), 0)
    cols = j * tk + lax.broadcasted_iota(jnp.int32, (tq, tk), 1)
    return same & (cols <= rows)


def _fwd_kernel(q_ref, k_ref, v_ref, segq_ref, segk_ref, o_ref, lse_ref, m_sc, l_sc, acc_sc, *, tq, tk, scale):
    i = pl.program_id(1)
    j = pl.program_id(2)

    @pl.when(j == 0)
    def _():
        m_sc[...] = jnp.full_like(m_sc, NEGATIVE)
        l_sc[...] = jnp.zeros_like(l_sc)
        acc_sc[...] = jnp.zeros_like(acc_sc)

    def absorb(causal):
        q = q_ref[0]
        k = k_ref[0]
        s = lax.dot_general(q, k, TRANS_B, preferred_element_type=jnp.float32) * scale
        s = jnp.where(_allowed(segq_ref, segk_ref, i, j, tq, tk, causal), s, -jnp.inf)
        m_prev = m_sc[...]
        m_new = jnp.maximum(m_prev, jnp.max(s, axis=1, keepdims=True))
        factor = jnp.exp(m_prev - m_new)
        p = jnp.exp(s - m_new)
        l_sc[...] = l_sc[...] * factor + jnp.sum(p, axis=1, keepdims=True)
        acc_sc[...] = acc_sc[...] * factor + jnp.dot(
            p.astype(jnp.bfloat16), v_ref[0], preferred_element_type=jnp.float32
        )
        m_sc[...] = m_new

    below = (j + 1) * tk <= i * tq
    near = jnp.logical_and(jnp.logical_not(below), j * tk <= i * tq + tq - 1)

    @pl.when(below)
    def _():
        absorb(False)

    @pl.when(near)
    def _():
        absorb(True)

    @pl.when(j == pl.num_programs(2) - 1)
    def _():
        total = l_sc[...]
        o_ref[0] = acc_sc[...] / total
        lse_ref[0] = m_sc[...] + jnp.log(total)


def attention_forward(q, k, v, seg, tq=512, tk=512):
    heads, total, dim = q.shape
    nq, nk = total // tq, total // tk
    scale = 1.0 / math.sqrt(dim)
    segq = seg.reshape(total, 1)
    segk = seg.reshape(1, total)

    def kv_map(h, i, j):
        return (h, jnp.minimum(j, (i * tq + tq - 1) // tk), 0)

    def segk_map(h, i, j):
        return (0, jnp.minimum(j, (i * tq + tq - 1) // tk))

    return pl.pallas_call(
        functools.partial(_fwd_kernel, tq=tq, tk=tk, scale=scale),
        out_shape=(
            jax.ShapeDtypeStruct((heads, total, dim), jnp.float32),
            jax.ShapeDtypeStruct((heads, total, 1), jnp.float32),
        ),
        grid=(heads, nq, nk),
        in_specs=[
            pl.BlockSpec((1, tq, dim), lambda h, i, j: (h, i, 0)),
            pl.BlockSpec((1, tk, dim), kv_map),
            pl.BlockSpec((1, tk, dim), kv_map),
            pl.BlockSpec((tq, 1), lambda h, i, j: (i, 0)),
            pl.BlockSpec((1, tk), segk_map),
        ],
        out_specs=[
            pl.BlockSpec((1, tq, dim), lambda h, i, j: (h, i, 0)),
            pl.BlockSpec((1, tq, 1), lambda h, i, j: (h, i, 0)),
        ],
        scratch_shapes=[
            pltpu.VMEM((tq, 1), jnp.float32),
            pltpu.VMEM((tq, 1), jnp.float32),
            pltpu.VMEM((tq, dim), jnp.float32),
        ],
        cost_estimate=pl.CostEstimate(
            flops=2 * heads * total * total * dim,
            transcendentals=heads * total * total // 2,
            bytes_accessed=heads * total * dim * 10,
        ),
    )(q, k, v, segq, segk)


def _bwd_kernel(q_ref, k_ref, v_ref, do_ref, lse_ref, delta_ref, segq_ref, segk_ref, dq_ref, dk_ref, dv_ref, *, tq, tk, scale):
    j = pl.program_id(1)
    i = pl.program_id(2)

    @pl.when((j == 0) & (i == 0))
    def _():
        dq_ref[...] = jnp.zeros_like(dq_ref)

    @pl.when(i == 0)
    def _():
        dk_ref[...] = jnp.zeros_like(dk_ref)
        dv_ref[...] = jnp.zeros_like(dv_ref)

    def absorb(causal):
        q = q_ref[0]
        k = k_ref[0]
        do = do_ref[0]
        s = lax.dot_general(q, k, TRANS_B, preferred_element_type=jnp.float32) * scale
        s = jnp.where(_allowed(segq_ref, segk_ref, i, j, tq, tk, causal), s, -jnp.inf)
        p = jnp.exp(s - lse_ref[0])
        dp = lax.dot_general(do, v_ref[0], TRANS_B, preferred_element_type=jnp.float32)
        ds = (p * (dp - delta_ref[0])).astype(jnp.bfloat16)
        dv_ref[0] += lax.dot(p.astype(jnp.bfloat16).T, do, preferred_element_type=jnp.float32)
        dk_ref[0] += lax.dot(ds.T, q, preferred_element_type=jnp.float32) * scale
        rows = pl.ds(pl.multiple_of(i * tq, tq), tq)
        dq_ref[0, rows, :] += lax.dot(ds, k, preferred_element_type=jnp.float32) * scale

    below = (j + 1) * tk <= i * tq
    near = jnp.logical_and(jnp.logical_not(below), i * tq + tq - 1 >= j * tk)

    @pl.when(below)
    def _():
        absorb(False)

    @pl.when(near)
    def _():
        absorb(True)


def attention_backward(q, k, v, do, lse, delta, seg, tq=512, tk=512):
    heads, total, dim = q.shape
    nq, nk = total // tq, total // tk
    scale = 1.0 / math.sqrt(dim)
    segq = seg.reshape(total, 1)
    segk = seg.reshape(1, total)

    def q_map(h, j, i):
        return (h, jnp.maximum(i, (j * tk) // tq), 0)

    def segq_map(h, j, i):
        return (jnp.maximum(i, (j * tk) // tq), 0)

    return pl.pallas_call(
        functools.partial(_bwd_kernel, tq=tq, tk=tk, scale=scale),
        out_shape=(
            jax.ShapeDtypeStruct((heads, total, dim), jnp.float32),
            jax.ShapeDtypeStruct((heads, total, dim), jnp.float32),
            jax.ShapeDtypeStruct((heads, total, dim), jnp.float32),
        ),
        grid=(heads, nk, nq),
        in_specs=[
            pl.BlockSpec((1, tq, dim), q_map),
            pl.BlockSpec((1, tk, dim), lambda h, j, i: (h, j, 0)),
            pl.BlockSpec((1, tk, dim), lambda h, j, i: (h, j, 0)),
            pl.BlockSpec((1, tq, dim), q_map),
            pl.BlockSpec((1, tq, 1), q_map),
            pl.BlockSpec((1, tq, 1), q_map),
            pl.BlockSpec((tq, 1), segq_map),
            pl.BlockSpec((1, tk), lambda h, j, i: (0, j)),
        ],
        out_specs=[
            pl.BlockSpec((1, total, dim), lambda h, j, i: (h, 0, 0)),
            pl.BlockSpec((1, tk, dim), lambda h, j, i: (h, j, 0)),
            pl.BlockSpec((1, tk, dim), lambda h, j, i: (h, j, 0)),
        ],
        cost_estimate=pl.CostEstimate(
            flops=5 * heads * total * total * dim,
            transcendentals=heads * total * total // 2,
            bytes_accessed=heads * total * dim * 24,
        ),
    )(q, k, v, do, lse, delta, segq, segk)


MESH_ID = pl.DeviceIdType.MESH


class Ring:
    def __init__(self, size, a_stride, b_stride):
        self.size = size
        self.half = size // 2
        self.a_stride = a_stride
        self.b_stride = b_stride

    def position(self, c):
        a = (c // self.a_stride) % self.half
        b = (c // self.b_stride) % 2
        return a + b * (2 * self.half - 1 - 2 * a)

    def device(self, pos):
        pos = pos % self.size
        b = pos // self.half
        a = pos + b * (2 * self.half - 1 - 2 * pos)
        return a * self.a_stride + b * self.b_stride


def ring_of(mesh):
    size = mesh.shape["ctx"]
    devices = list(mesh.devices.reshape(-1, size)[0])
    try:
        coords = [tuple(d.coords) for d in devices]
    except AttributeError:
        coords = None
    if coords and size % 2 == 0 and size >= 4:
        for b_stride in range(1, size):
            for a_stride in range(1, size):
                ring = Ring(size, a_stride, b_stride)
                order = [ring.device(p) for p in range(size)]
                if sorted(order) != list(range(size)):
                    continue
                hops = [
                    sum(abs(x - y) for x, y in zip(coords[order[p]], coords[order[(p + 1) % size]]))
                    for p in range(size)
                ]
                if max(hops) == 1:
                    return ring
    return Ring(size, 2, 1) if size % 2 == 0 and size >= 4 else None


def _barrier(g, left, right):
    barrier = pltpu.get_barrier_semaphore()
    for other in (left, right):
        pl.semaphore_signal(barrier, 1, device_id=(g, other), device_id_type=MESH_ID)
    pl.semaphore_wait(barrier, 2)


def _gather_kernel(x_ref, y_ref, own_sem, send_sem, recv_sem, *, ring, rows):
    n = ring.size
    half = rows // 2
    g = lax.axis_index("dp")
    c = lax.axis_index("ctx")
    pos = ring.position(c)
    right = ring.device(pos + 1)
    left = ring.device(pos + n - 1)
    own = pltpu.make_async_copy(x_ref, y_ref.at[pl.ds(c * rows, rows)], own_sem)
    own.start()
    _barrier(g, left, right)

    def link(direction, step, origin, source):
        offset = origin * rows + direction * half
        return pltpu.make_async_remote_copy(
            src_ref=source,
            dst_ref=y_ref.at[pl.ds(offset, half)],
            send_sem=send_sem.at[direction, step],
            recv_sem=recv_sem.at[direction, step],
            device_id=(g, right if direction == 0 else left),
            device_id_type=MESH_ID,
        )

    sent = []
    for step in range(n - 1):
        origins = (ring.device(pos - step + n), ring.device(pos + step))
        for direction in (0, 1):
            origin = origins[direction]
            if step == 0:
                source = x_ref.at[pl.ds(direction * half, half)]
            else:
                link(direction, step - 1, origin, None if False else y_ref.at[pl.ds(origin * rows + direction * half, half)]).wait_recv()
                source = y_ref.at[pl.ds(origin * rows + direction * half, half)]
            copy = link(direction, step, origin, source)
            copy.start()
            sent.append(copy)
    last = n - 2
    for direction, origin in ((0, ring.device(pos - last - 1 + n)), (1, ring.device(pos + last + 1))):
        link(direction, last, origin, y_ref.at[pl.ds(origin * rows + direction * half, half)]).wait_recv()
    for copy in sent:
        copy.wait_send()
    own.wait()


def ring_all_gather(x, ring, collective_id):
    rows, cols = x.shape
    n = ring.size
    return pl.pallas_call(
        functools.partial(_gather_kernel, ring=ring, rows=rows),
        out_shape=jax.ShapeDtypeStruct((n * rows, cols), x.dtype),
        in_specs=[pl.BlockSpec(memory_space=pl.ANY)],
        out_specs=pl.BlockSpec(memory_space=pl.ANY),
        scratch_shapes=[
            pltpu.SemaphoreType.DMA(()),
            pltpu.SemaphoreType.DMA((2, n - 1)),
            pltpu.SemaphoreType.DMA((2, n - 1)),
        ],
        compiler_params=pltpu.CompilerParams(collective_id=collective_id, has_side_effects=True),
    )(x)


def _scatter_kernel(p_ref, out_ref, recv_buf, send_buf, send_sem, recv_sem, *, ring, rows):
    n = ring.size
    half = rows // 2
    g = lax.axis_index("dp")
    c = lax.axis_index("ctx")
    pos = ring.position(c)
    right = ring.device(pos + 1)
    left = ring.device(pos + n - 1)
    _barrier(g, left, right)

    def link(direction, step):
        return pltpu.make_async_remote_copy(
            src_ref=send_buf.at[direction, step],
            dst_ref=recv_buf.at[direction, step],
            send_sem=send_sem.at[direction, step],
            recv_sem=recv_sem.at[direction, step],
            device_id=(g, right if direction == 0 else left),
            device_id_type=MESH_ID,
        )

    sent = []
    for step in range(n - 1):
        targets = (ring.device(pos - 1 - step + 2 * n), ring.device(pos + 1 + step))
        for direction in (0, 1):
            start = pl.multiple_of(targets[direction] * rows + direction * half, half)
            total = p_ref[pl.ds(start, half), :].astype(jnp.float32)
            if step > 0:
                link(direction, step - 1).wait_recv()
                total = total + recv_buf[direction, step - 1].astype(jnp.float32)
            send_buf[direction, step] = total.astype(send_buf.dtype)
            copy = link(direction, step)
            copy.start()
            sent.append(copy)
    for direction in (0, 1):
        link(direction, n - 2).wait_recv()
        start = pl.multiple_of(c * rows + direction * half, half)
        out_ref[pl.ds(direction * half, half), :] = (
            p_ref[pl.ds(start, half), :].astype(jnp.float32)
            + recv_buf[direction, n - 2].astype(jnp.float32)
        ).astype(out_ref.dtype)
    for copy in sent:
        copy.wait_send()


def ring_reduce_scatter(p, ring, collective_id, out_dtype=jnp.float32, wire=jnp.bfloat16):
    total_rows, cols = p.shape
    n = ring.size
    rows = total_rows // n
    half = rows // 2
    return pl.pallas_call(
        functools.partial(_scatter_kernel, ring=ring, rows=rows),
        out_shape=jax.ShapeDtypeStruct((rows, cols), out_dtype),
        in_specs=[pl.BlockSpec(memory_space=pltpu.VMEM)],
        out_specs=pl.BlockSpec(memory_space=pltpu.VMEM),
        scratch_shapes=[
            pltpu.VMEM((2, n - 1, half, cols), wire),
            pltpu.VMEM((2, n - 1, half, cols), wire),
            pltpu.SemaphoreType.DMA((2, n - 1)),
            pltpu.SemaphoreType.DMA((2, n - 1)),
        ],
        compiler_params=pltpu.CompilerParams(
            collective_id=collective_id, has_side_effects=True, vmem_limit_bytes=60 * 1024 * 1024
        ),
    )(p)


def _exchange_kernel(x_ref, out_ref, own_sem, send_sem, recv_sem, *, group):
    n = x_ref.shape[0]
    g = lax.axis_index("dp")
    c = lax.axis_index("ctx")
    n_ctx = lax.axis_size("ctx")
    me = {"all": g * n_ctx + c, "ctx": c, "dp": g}[group]

    def address(member):
        if group == "all":
            return (member // n_ctx, member % n_ctx)
        if group == "ctx":
            return (g, member)
        return (member, c)

    own = pltpu.make_async_copy(x_ref.at[me], out_ref.at[me], own_sem)
    own.start()
    barrier = pltpu.get_barrier_semaphore()
    for offset in range(1, n):
        pl.semaphore_signal(
            barrier, 1, device_id=address((me + offset) % n), device_id_type=MESH_ID
        )
    pl.semaphore_wait(barrier, n - 1)

    def link(offset, source, target):
        return pltpu.make_async_remote_copy(
            src_ref=x_ref.at[target],
            dst_ref=out_ref.at[source],
            send_sem=send_sem.at[offset],
            recv_sem=recv_sem.at[offset],
            device_id=address(target),
            device_id_type=MESH_ID,
        )

    sent = []
    for offset in range(1, n):
        copy = link(offset, me, (me + offset) % n)
        copy.start()
        sent.append(copy)
    for offset in range(1, n):
        link(offset, (me + n - offset) % n, me).wait_recv()
    for copy in sent:
        copy.wait_send()
    own.wait()


def exchange(x, group, collective_id):
    n = x.shape[0]
    space = pltpu.VMEM
    return pl.pallas_call(
        functools.partial(_exchange_kernel, group=group),
        out_shape=jax.ShapeDtypeStruct(x.shape, x.dtype),
        in_specs=[pl.BlockSpec(memory_space=space)],
        out_specs=pl.BlockSpec(memory_space=space),
        scratch_shapes=[
            pltpu.SemaphoreType.DMA(()),
            pltpu.SemaphoreType.DMA((n,)),
            pltpu.SemaphoreType.DMA((n,)),
        ],
        compiler_params=pltpu.CompilerParams(collective_id=collective_id, has_side_effects=True),
    )(x)


def block_moves(n_dp, n_ctx):
    count = n_dp * n_ctx
    return [(f, (f % n_dp) * n_ctx + f // n_dp) for f in range(count)]


def fetch_out_rows(w_out):
    n_dp = lax.axis_size("dp")
    n_ctx = lax.axis_size("ctx")
    moved = lax.ppermute(w_out.astype(jnp.bfloat16), ("dp", "ctx"), perm=block_moves(n_dp, n_ctx))
    return lax.all_gather(moved, "dp", axis=0, tiled=True)


def return_out_rows(grad_out_rows):
    n_dp = lax.axis_size("dp")
    n_ctx = lax.axis_size("ctx")
    part = lax.psum_scatter(grad_out_rows, "dp", scatter_dimension=0, tiled=True)
    back = [(b, a) for a, b in block_moves(n_dp, n_ctx)]
    return lax.ppermute(part, ("dp", "ctx"), perm=back)


def pack_rows(vector, lanes):
    size = vector.shape[0]
    total = -(-size // (16 * lanes)) * 16 * lanes
    return jnp.pad(vector, (0, total - size)).reshape(-1, lanes)


def fetch_small(b_qkv, b_out, b_fc2, ln_gain, ln_shift, b_fc1):
    pieces = (b_qkv, b_out, b_fc2, ln_gain, ln_shift, b_fc1)
    n_dp = lax.axis_size("dp")
    n_ctx = lax.axis_size("ctx")
    packed = pack_rows(jnp.concatenate([p.astype(jnp.bfloat16) for p in pieces]), 128)
    over_dp = exchange(jnp.broadcast_to(packed[None], (n_dp,) + packed.shape), "dp", 4)
    over_all = exchange(jnp.broadcast_to(over_dp[None], (n_ctx,) + over_dp.shape), "ctx", 8)
    table = over_all.transpose(1, 0, 2, 3).reshape(n_dp * n_ctx, -1)
    result = []
    offset = 0
    for p in pieces:
        result.append(table[:, offset : offset + p.shape[0]])
        offset += p.shape[0]
    return result


def reduce_small(over_ctx):
    width = over_ctx.shape[1]
    packed = jax.vmap(lambda row: pack_rows(row, 128))(over_ctx)
    over_dp = jnp.sum(exchange(packed, "dp", 9), axis=0)
    return over_dp.reshape(-1)[:width]


def fetch_heads(w_qkv, w_fc1, w_fc2, tokens):
    dp_count = lax.axis_size("dp")
    ctx_count = lax.axis_size("ctx")
    rows_piece = w_qkv.shape[0]
    head_width = D // ctx_count
    unit = FF // (dp_count * ctx_count)
    qkv_piece = w_qkv.astype(jnp.bfloat16).reshape(rows_piece, 3, ctx_count, head_width)
    fc1_piece = w_fc1.astype(jnp.bfloat16).reshape(rows_piece, dp_count, ctx_count, unit)
    pieces = jnp.concatenate(
        [
            qkv_piece.transpose(2, 0, 1, 3).reshape(ctx_count, rows_piece, 3 * head_width),
            fc1_piece.transpose(2, 0, 1, 3).reshape(ctx_count, rows_piece, dp_count * unit),
        ],
        axis=2,
    )
    sent = exchange(pieces, "ctx", 5).reshape(ctx_count * rows_piece, -1)
    sent, tokens = lax.optimization_barrier((sent, tokens))
    cols, fc2_rows = (
        lax.all_gather(sent, "dp", axis=0, tiled=True),
        lax.all_gather(w_fc2.astype(jnp.bfloat16), "dp", axis=0, tiled=True),
    )
    return (cols, fc2_rows, tokens)


def split_wide(values):
    high = values.astype(jnp.bfloat16)
    low_part = (values - high.astype(jnp.float32)).astype(jnp.bfloat16)
    return jnp.concatenate([high, low_part], axis=-1)


def join_wide(values):
    half = values.shape[-1] // 2
    return values[..., :half].astype(jnp.float32) + values[..., half:].astype(jnp.float32)


def return_heads(owned_parts, small):
    dp_count = lax.axis_size("dp")
    ctx_count = lax.axis_size("ctx")
    head_width = D // ctx_count
    unit = FF // (dp_count * ctx_count)
    rows_piece = owned_parts.shape[0] // ctx_count
    width = owned_parts.shape[1]
    small_width = small.shape[1]
    small_by_ctx = small.reshape(dp_count, ctx_count, small_width).transpose(1, 0, 2)
    coded = split_wide(small_by_ctx.reshape(ctx_count, -1))
    extra = -(-coded.shape[1] // (8 * width)) * 8
    coded = jnp.pad(coded, ((0, 0), (0, extra * width - coded.shape[1])))
    payload = jnp.concatenate(
        [owned_parts.reshape(ctx_count, rows_piece, width), coded.reshape(ctx_count, extra, width)],
        axis=1,
    )
    got = exchange(payload, "ctx", 6)
    small_got = got[:, rows_piece:, :].reshape(ctx_count, -1)[:, : 2 * dp_count * small_width]
    over_ctx = jnp.sum(join_wide(small_got), axis=0).reshape(dp_count, small_width)
    got = got[:, :rows_piece, :]
    qkv = got[:, :, : 3 * head_width].reshape(ctx_count, rows_piece, 3, head_width)
    fc1 = got[:, :, 3 * head_width :].reshape(ctx_count, rows_piece, dp_count, unit)
    return (
        qkv.transpose(1, 2, 0, 3).reshape(rows_piece, 3 * D).astype(jnp.float32),
        fc1.transpose(1, 2, 0, 3).reshape(rows_piece, FF).astype(jnp.float32),
        over_ctx,
    )


def head_plan(
    ring,
    tokens,
    lengths,
    w_qkv,
    b_qkv,
    w_out,
    b_out,
    w_fc1,
    b_fc1,
    w_fc2,
    b_fc2,
    ln_gain,
    ln_shift,
    cotangent,
):
    rows_here = tokens.shape[0]
    rows_piece = w_qkv.shape[0]
    dp_count = lax.axis_size("dp")
    ctx_count = lax.axis_size("ctx")
    count = dp_count * ctx_count
    group = rows_here * ctx_count
    head_width = D // ctx_count
    local_heads = HEADS // ctx_count
    unit = FF // (dp_count * ctx_count)
    here = lax.axis_index("ctx")
    group_rows = jnp.arange(group, dtype=jnp.int32)
    seg, positions = segment_info(lengths[0], group_rows)
    cosine, sine = rotary_tables(positions)
    qkv_bias, out_bias, fc2_bias, gain_low, shift_low, fc1_table = fetch_small(
        b_qkv, b_out, b_fc2, ln_gain, ln_shift, b_fc1
    )
    qkv_bias = qkv_bias.reshape(3 * D)
    out_bias = out_bias.reshape(D)
    fc2_bias = fc2_bias.reshape(D)
    gain_low = gain_low.reshape(D)
    shift_low = shift_low.reshape(D)
    fc1_bias = lax.dynamic_index_in_dim(
        fc1_table.reshape(dp_count, ctx_count, unit), here, 1, keepdims=False
    ).reshape(dp_count * unit)
    out_rows = fetch_out_rows(w_out)
    cols, fc2_rows, tokens = fetch_heads(w_qkv, w_fc1, w_fc2, tokens)
    gain32 = gain_low.astype(jnp.float32)
    shift32 = shift_low.astype(jnp.float32)
    inputs = tokens.astype(jnp.float32)
    normed, scaled, _ = norm_parts(inputs, gain32, shift32)
    tokens_group = ring_all_gather(tokens, ring, 0)
    late_dy, tokens_group = lax.optimization_barrier((cotangent, tokens_group))
    dy_group = lax.all_gather(late_dy, "ctx", axis=0, tiled=True)
    hidden_group = norm_parts(tokens_group.astype(jnp.float32), gain32, shift32)[2].astype(
        jnp.bfloat16
    )
    bias_cols = lax.dynamic_slice_in_dim(
        qkv_bias.reshape(3, D), here * head_width, head_width, 1
    ).reshape(3 * head_width)
    both = jnp.dot(hidden_group, cols, preferred_element_type=jnp.float32) + jnp.concatenate(
        [bias_cols, fc1_bias]
    ).astype(jnp.float32)
    qkv = both[:, : 3 * head_width]
    pre = both[:, 3 * head_width :]
    shape = (group, local_heads, HEAD_DIM)
    query = rotate(qkv[:, :head_width].reshape(shape), cosine, sine).astype(jnp.bfloat16)
    keys = rotate(qkv[:, head_width : 2 * head_width].reshape(shape), cosine, sine).astype(
        jnp.bfloat16
    )
    values = qkv[:, 2 * head_width :].reshape(shape).astype(jnp.bfloat16)
    q_heads = query.transpose(1, 0, 2)
    k_heads = keys.transpose(1, 0, 2)
    v_heads = values.transpose(1, 0, 2)
    attended_heads, log_total = attention_forward(q_heads, k_heads, v_heads, seg)
    attended = attended_heads.transpose(1, 0, 2).reshape(group, head_width).astype(jnp.bfloat16)
    act = gelu_tanh(pre).astype(jnp.bfloat16)
    branches = ring_reduce_scatter(
        jnp.dot(attended, out_rows, preferred_element_type=jnp.float32)
        + jnp.dot(act, fc2_rows, preferred_element_type=jnp.float32),
        ring,
        2,
    )
    block_out = (
        inputs + branches + out_bias.astype(jnp.float32) + fc2_bias.astype(jnp.float32)
    ).astype(jnp.bfloat16)
    grad_out32 = cotangent.astype(jnp.float32)
    grad_b_fc2 = jnp.sum(grad_out32, axis=0)
    grad_fc2_part = jnp.einsum("tf,td->fd", act, dy_group, preferred_element_type=jnp.float32)
    d_act = jnp.einsum("td,fd->tf", dy_group, fc2_rows, preferred_element_type=jnp.float32)
    d_pre = (d_act * gelu_slope(pre)).astype(jnp.bfloat16)
    grad_bfc1_part = jnp.sum(d_pre.astype(jnp.float32), axis=0)
    grad_out_rows = jnp.einsum("tc,td->cd", attended, dy_group, preferred_element_type=jnp.float32)
    owned_w_out = return_out_rows(grad_out_rows)
    d_attended = (
        jnp.einsum("td,cd->tc", dy_group, out_rows, preferred_element_type=jnp.float32)
        .astype(jnp.bfloat16)
        .reshape(shape)
    )
    d_heads = d_attended.transpose(1, 0, 2)
    delta = jnp.sum(d_heads.astype(jnp.float32) * attended_heads, axis=2, keepdims=True)
    dq_heads, dk_heads, dv_heads = attention_backward(
        q_heads, k_heads, v_heads, d_heads, log_total, delta, seg
    )
    d_query = dq_heads.transpose(1, 0, 2)
    d_keys = dk_heads.transpose(1, 0, 2)
    d_values = dv_heads.transpose(1, 0, 2)
    d_query = rotate_back(d_query, cosine, sine).reshape(group, head_width)
    d_keys = rotate_back(d_keys, cosine, sine).reshape(group, head_width)
    d_qkv = jnp.concatenate([d_query, d_keys, d_values.reshape(group, head_width)], axis=1).astype(
        jnp.bfloat16
    )
    d_both = jnp.concatenate([d_qkv, d_pre], axis=1)
    bias_part = jnp.sum(d_qkv.astype(jnp.float32), axis=0).reshape(3, head_width)
    d_hidden = ring_reduce_scatter(
        jnp.einsum("tc,dc->td", d_both, cols, preferred_element_type=jnp.float32), ring, 3
    )
    grad_gain, grad_shift, d_inputs = norm_back(d_hidden, normed, scaled, gain32)
    grad_tokens = (grad_out32 + d_inputs).astype(jnp.bfloat16)
    owned_fc2 = lax.psum_scatter(
        grad_fc2_part.astype(jnp.bfloat16), "dp", scatter_dimension=0, tiled=True
    ).astype(jnp.float32)
    full_bqkv = lax.dynamic_update_slice_in_dim(
        jnp.zeros((3, D), jnp.float32), bias_part, here * head_width, 1
    )
    full_bfc1 = lax.dynamic_update_slice_in_dim(
        jnp.zeros((dp_count, ctx_count, unit), jnp.float32),
        grad_bfc1_part.reshape(dp_count, 1, unit),
        here,
        1,
    )
    small = jnp.concatenate(
        [
            full_bqkv.reshape(count, -1),
            grad_b_fc2.reshape(count, -1),
            grad_gain.reshape(count, -1),
            grad_shift.reshape(count, -1),
            full_bfc1.reshape(count, -1),
        ],
        axis=1,
    )
    weight_parts = jnp.einsum(
        "td,tc->dc", hidden_group, d_both, preferred_element_type=jnp.float32
    ).astype(jnp.bfloat16)
    owned_parts = lax.psum_scatter(weight_parts, "dp", scatter_dimension=0, tiled=True)
    split_qkv, split_fc1, over_ctx = return_heads(owned_parts, small)
    owned_small = reduce_small(over_ctx)
    cuts = [0, 3 * D // count, D // count, D // count, D // count, FF // count]
    bounds = [sum(cuts[: i + 1]) for i in range(len(cuts))]
    owned_bqkv, owned_bout, owned_gain, owned_shift, owned_bfc1 = [
        owned_small[bounds[i] : bounds[i + 1]] for i in range(5)
    ]
    return (
        block_out,
        grad_tokens,
        split_qkv.reshape(rows_piece, 3 * D),
        owned_bqkv,
        owned_w_out,
        owned_bout,
        split_fc1.reshape(rows_piece, FF),
        owned_bfc1,
        owned_fc2,
        owned_bout,
        owned_gain,
        owned_shift,
    )


def body(
    ring,
    tokens,
    lengths,
    w_qkv,
    b_qkv,
    w_out,
    b_out,
    w_fc1,
    b_fc1,
    w_fc2,
    b_fc2,
    ln_gain,
    ln_shift,
    cotangent,
):
    return head_plan(
        ring,
        tokens,
        lengths,
        w_qkv,
        b_qkv,
        w_out,
        b_out,
        w_fc1,
        b_fc1,
        w_fc2,
        b_fc2,
        ln_gain,
        ln_shift,
        cotangent,
    )


def solution(mesh):
    in_specs = (
        P(("dp", "ctx"), None),
        P("dp", None),
        P(("dp", "ctx"), None),
        P(("dp", "ctx")),
        P(("dp", "ctx"), None),
        P(("dp", "ctx")),
        P(("dp", "ctx"), None),
        P(("dp", "ctx")),
        P(("dp", "ctx"), None),
        P(("dp", "ctx")),
        P(("dp", "ctx")),
        P(("dp", "ctx")),
        P(("dp", "ctx"), None),
    )
    out_specs = (
        P(("dp", "ctx"), None),
        P(("dp", "ctx"), None),
        P(("dp", "ctx"), None),
        P(("dp", "ctx")),
        P(("dp", "ctx"), None),
        P(("dp", "ctx")),
        P(("dp", "ctx"), None),
        P(("dp", "ctx")),
        P(("dp", "ctx"), None),
        P(("dp", "ctx")),
        P(("dp", "ctx")),
        P(("dp", "ctx")),
    )
    ring = ring_of(mesh)
    return jax.shard_map(functools.partial(body, ring), mesh=mesh, in_specs=in_specs, out_specs=out_specs, check_vma=False)
```

```python
import functools
import math

import jax
import jax.numpy as jnp
from jax import lax
from jax.experimental import pallas as pl
from jax.experimental.pallas import tpu as pltpu
from jax.sharding import PartitionSpec as P

D = 2048
HEADS = 32
HEAD_DIM = 64
ROT = 32
FF = 8192


EPS = 1e-05
GELU_COEF = math.sqrt(2.0 / math.pi)
NEGATIVE = -1e30


def norm_parts(inputs, gain, shift):
    mean = jnp.mean(inputs, axis=-1, keepdims=True)
    centred = inputs - mean
    var = jnp.mean(centred * centred, axis=-1, keepdims=True)
    scaled = lax.rsqrt(var + EPS)
    normed = centred * scaled
    return (normed, scaled, normed * gain + shift)


def norm_back(d_hidden, normed, scaled, gain32):
    grad_gain = jnp.sum(d_hidden * normed, axis=0)
    grad_shift = jnp.sum(d_hidden, axis=0)
    d_normed = d_hidden * gain32
    d_inputs = scaled * (
        d_normed
        - jnp.mean(d_normed, axis=-1, keepdims=True)
        - normed * jnp.mean(d_normed * normed, axis=-1, keepdims=True)
    )
    return (grad_gain, grad_shift, d_inputs)


def gelu_tanh(pre):
    return 0.5 * pre * (1.0 + jnp.tanh(GELU_COEF * (pre + 0.044715 * pre * pre * pre)))


def gelu_slope(pre):
    tangent = jnp.tanh(GELU_COEF * (pre + 0.044715 * pre * pre * pre))
    return 0.5 * (1.0 + tangent) + 0.5 * pre * (1.0 - tangent * tangent) * GELU_COEF * (
        1.0 + 3.0 * 0.044715 * pre * pre
    )


def rotary_tables(positions):
    half = ROT // 2
    freq = jnp.exp(jnp.arange(half, dtype=jnp.float32) * (-2.0 * math.log(10000.0) / ROT))
    angle = positions.astype(jnp.float32)[:, None] * freq[None, :]
    return (jnp.cos(angle)[:, None, :], jnp.sin(angle)[:, None, :])


def rotate(heads, cosine, sine):
    half = ROT // 2
    first = heads[..., :half]
    second = heads[..., half:ROT]
    return jnp.concatenate(
        [first * cosine - second * sine, second * cosine + first * sine, heads[..., ROT:]], axis=-1
    )


def rotate_back(grads, cosine, sine):
    half = ROT // 2
    first = grads[..., :half]
    second = grads[..., half:ROT]
    return jnp.concatenate(
        [first * cosine + second * sine, second * cosine - first * sine, grads[..., ROT:]], axis=-1
    )


def segment_info(lengths_row, rows):
    ends = jnp.cumsum(lengths_row)
    starts = ends - lengths_row
    seg = jnp.sum((rows[:, None] >= ends[None, :]).astype(jnp.int32), axis=1)
    onehot = seg[:, None] == jnp.arange(lengths_row.shape[0], dtype=jnp.int32)[None, :]
    first_rows = jnp.sum(jnp.where(onehot, starts[None, :], 0), axis=1)
    return (seg, rows - first_rows)


TRANS_B = (((1,), (1,)), ((), ()))


def _allowed(segq_ref, segk_ref, i, j, tq, tk, causal):
    same = segq_ref[...] == segk_ref[...]
    if not causal:
        return same
    rows = i * tq + lax.broadcasted_iota(jnp.int32, (tq, tk), 0)
    cols = j * tk + lax.broadcasted_iota(jnp.int32, (tq, tk), 1)
    return same & (cols <= rows)


def _fwd_kernel(qi_ref, kj_ref, q_ref, k_ref, v_ref, segq_ref, segk_ref, o_ref, lse_ref, m_sc, l_sc, acc_sc, *, tq, tk, scale):
    t = pl.program_id(1)
    i = qi_ref[t]
    j = kj_ref[t]

    @pl.when(j == 0)
    def _():
        m_sc[...] = jnp.full_like(m_sc, NEGATIVE)
        l_sc[...] = jnp.zeros_like(l_sc)
        acc_sc[...] = jnp.zeros_like(acc_sc)

    def absorb(causal):
        q = q_ref[0]
        k = k_ref[0]
        s = lax.dot_general(q, k, TRANS_B, preferred_element_type=jnp.float32) * scale
        s = jnp.where(_allowed(segq_ref, segk_ref, i, j, tq, tk, causal), s, -jnp.inf)
        m_prev = m_sc[...]
        m_new = jnp.maximum(m_prev, jnp.max(s, axis=1, keepdims=True))
        factor = jnp.exp(m_prev - m_new)
        p = jnp.exp(s - m_new)
        l_sc[...] = l_sc[...] * factor + jnp.sum(p, axis=1, keepdims=True)
        acc_sc[...] = acc_sc[...] * factor + jnp.dot(
            p.astype(jnp.bfloat16), v_ref[0], preferred_element_type=jnp.float32
        )
        m_sc[...] = m_new

    @pl.when(j < i)
    def _():
        absorb(False)

    @pl.when(j == i)
    def _():
        absorb(True)
        total = l_sc[...]
        o_ref[0] = acc_sc[...] / total
        lse_ref[0] = m_sc[...] + jnp.log(total)


def _schedule(count, queries_outer):
    if queries_outer:
        pairs = [(i, j) for i in range(count) for j in range(i + 1)]
    else:
        pairs = [(i, j) for j in range(count) for i in range(j, count)]
    return (
        jnp.asarray([p[0] for p in pairs], jnp.int32),
        jnp.asarray([p[1] for p in pairs], jnp.int32),
    )


def attention_forward(q, k, v, seg, block=512):
    heads, total, dim = q.shape
    count = total // block
    scale = 1.0 / math.sqrt(dim)
    segq = seg.reshape(total, 1)
    segk = seg.reshape(1, total)
    qi, kj = _schedule(count, True)
    steps = qi.shape[0]

    return pl.pallas_call(
        functools.partial(_fwd_kernel, tq=block, tk=block, scale=scale),
        out_shape=(
            jax.ShapeDtypeStruct((heads, total, dim), jnp.float32),
            jax.ShapeDtypeStruct((heads, total, 1), jnp.float32),
        ),
        grid_spec=pltpu.PrefetchScalarGridSpec(
            num_scalar_prefetch=2,
            grid=(heads, steps),
            in_specs=[
                pl.BlockSpec((1, block, dim), lambda h, t, qi, kj: (h, qi[t], 0)),
                pl.BlockSpec((1, block, dim), lambda h, t, qi, kj: (h, kj[t], 0)),
                pl.BlockSpec((1, block, dim), lambda h, t, qi, kj: (h, kj[t], 0)),
                pl.BlockSpec((block, 1), lambda h, t, qi, kj: (qi[t], 0)),
                pl.BlockSpec((1, block), lambda h, t, qi, kj: (0, kj[t])),
            ],
            out_specs=[
                pl.BlockSpec((1, block, dim), lambda h, t, qi, kj: (h, qi[t], 0)),
                pl.BlockSpec((1, block, 1), lambda h, t, qi, kj: (h, qi[t], 0)),
            ],
            scratch_shapes=[
                pltpu.VMEM((block, 1), jnp.float32),
                pltpu.VMEM((block, 1), jnp.float32),
                pltpu.VMEM((block, dim), jnp.float32),
            ],
        ),
        cost_estimate=pl.CostEstimate(
            flops=2 * heads * total * total * dim,
            transcendentals=heads * total * total // 2,
            bytes_accessed=heads * total * dim * 10,
        ),
    )(qi, kj, q, k, v, segq, segk)


def _bwd_kernel(qi_ref, kj_ref, q_ref, k_ref, v_ref, do_ref, lse_ref, delta_ref, segq_ref, segk_ref, dq_ref, dk_ref, dv_ref, *, tq, tk, scale):
    t = pl.program_id(1)
    i = qi_ref[t]
    j = kj_ref[t]

    @pl.when(t == 0)
    def _():
        dq_ref[...] = jnp.zeros_like(dq_ref)

    @pl.when(i == j)
    def _():
        dk_ref[...] = jnp.zeros_like(dk_ref)
        dv_ref[...] = jnp.zeros_like(dv_ref)

    def absorb(causal):
        q = q_ref[0]
        k = k_ref[0]
        do = do_ref[0]
        s = lax.dot_general(q, k, TRANS_B, preferred_element_type=jnp.float32) * scale
        s = jnp.where(_allowed(segq_ref, segk_ref, i, j, tq, tk, causal), s, -jnp.inf)
        p = jnp.exp(s - lse_ref[0])
        dp = lax.dot_general(do, v_ref[0], TRANS_B, preferred_element_type=jnp.float32)
        ds = (p * (dp - delta_ref[0])).astype(jnp.bfloat16)
        dv_ref[0] += lax.dot(p.astype(jnp.bfloat16).T, do, preferred_element_type=jnp.float32)
        dk_ref[0] += lax.dot(ds.T, q, preferred_element_type=jnp.float32) * scale
        rows = pl.ds(pl.multiple_of(i * tq, tq), tq)
        dq_ref[0, rows, :] += lax.dot(ds, k, preferred_element_type=jnp.float32) * scale

    @pl.when(j < i)
    def _():
        absorb(False)

    @pl.when(j == i)
    def _():
        absorb(True)


def attention_backward(q, k, v, do, lse, delta, seg, block=512):
    heads, total, dim = q.shape
    count = total // block
    scale = 1.0 / math.sqrt(dim)
    segq = seg.reshape(total, 1)
    segk = seg.reshape(1, total)
    qi, kj = _schedule(count, False)
    steps = qi.shape[0]

    def q_map(h, t, qi, kj):
        return (h, qi[t], 0)

    def k_map(h, t, qi, kj):
        return (h, kj[t], 0)

    return pl.pallas_call(
        functools.partial(_bwd_kernel, tq=block, tk=block, scale=scale),
        out_shape=(
            jax.ShapeDtypeStruct((heads, total, dim), jnp.float32),
            jax.ShapeDtypeStruct((heads, total, dim), jnp.float32),
            jax.ShapeDtypeStruct((heads, total, dim), jnp.float32),
        ),
        grid_spec=pltpu.PrefetchScalarGridSpec(
            num_scalar_prefetch=2,
            grid=(heads, steps),
            in_specs=[
                pl.BlockSpec((1, block, dim), q_map),
                pl.BlockSpec((1, block, dim), k_map),
                pl.BlockSpec((1, block, dim), k_map),
                pl.BlockSpec((1, block, dim), q_map),
                pl.BlockSpec((1, block, 1), q_map),
                pl.BlockSpec((1, block, 1), q_map),
                pl.BlockSpec((block, 1), lambda h, t, qi, kj: (qi[t], 0)),
                pl.BlockSpec((1, block), lambda h, t, qi, kj: (0, kj[t])),
            ],
            out_specs=[
                pl.BlockSpec((1, total, dim), lambda h, t, qi, kj: (h, 0, 0)),
                pl.BlockSpec((1, block, dim), k_map),
                pl.BlockSpec((1, block, dim), k_map),
            ],
        ),
        cost_estimate=pl.CostEstimate(
            flops=5 * heads * total * total * dim,
            transcendentals=heads * total * total // 2,
            bytes_accessed=heads * total * dim * 24,
        ),
    )(qi, kj, q, k, v, do, lse, delta, segq, segk)


MESH_ID = pl.DeviceIdType.MESH


class Ring:
    def __init__(self, size, a_stride, b_stride):
        self.size = size
        self.half = size // 2
        self.a_stride = a_stride
        self.b_stride = b_stride

    def position(self, c):
        a = (c // self.a_stride) % self.half
        b = (c // self.b_stride) % 2
        return a + b * (2 * self.half - 1 - 2 * a)

    def device(self, pos):
        pos = pos % self.size
        b = pos // self.half
        a = pos + b * (2 * self.half - 1 - 2 * pos)
        return a * self.a_stride + b * self.b_stride


def ring_of(mesh):
    size = mesh.shape["ctx"]
    devices = list(mesh.devices.reshape(-1, size)[0])
    try:
        coords = [tuple(d.coords) for d in devices]
    except AttributeError:
        coords = None
    if coords and size % 2 == 0 and size >= 4:
        for b_stride in range(1, size):
            for a_stride in range(1, size):
                ring = Ring(size, a_stride, b_stride)
                order = [ring.device(p) for p in range(size)]
                if sorted(order) != list(range(size)):
                    continue
                hops = [
                    sum(abs(x - y) for x, y in zip(coords[order[p]], coords[order[(p + 1) % size]]))
                    for p in range(size)
                ]
                if max(hops) == 1:
                    return ring
    return Ring(size, 2, 1) if size % 2 == 0 and size >= 4 else None


def _barrier(g, left, right):
    barrier = pltpu.get_barrier_semaphore()
    for other in (left, right):
        pl.semaphore_signal(barrier, 1, device_id=(g, other), device_id_type=MESH_ID)
    pl.semaphore_wait(barrier, 2)


def _gather_kernel(x_ref, y_ref, own_sem, send_sem, recv_sem, *, ring, rows):
    n = ring.size
    half = rows // 2
    g = lax.axis_index("dp")
    c = lax.axis_index("ctx")
    pos = ring.position(c)
    right = ring.device(pos + 1)
    left = ring.device(pos + n - 1)
    own = pltpu.make_async_copy(x_ref, y_ref.at[pl.ds(c * rows, rows)], own_sem)
    own.start()
    _barrier(g, left, right)

    def link(direction, step, origin, source):
        offset = origin * rows + direction * half
        return pltpu.make_async_remote_copy(
            src_ref=source,
            dst_ref=y_ref.at[pl.ds(offset, half)],
            send_sem=send_sem.at[direction, step],
            recv_sem=recv_sem.at[direction, step],
            device_id=(g, right if direction == 0 else left),
            device_id_type=MESH_ID,
        )

    sent = []
    for step in range(n - 1):
        origins = (ring.device(pos - step + n), ring.device(pos + step))
        for direction in (0, 1):
            origin = origins[direction]
            if step == 0:
                source = x_ref.at[pl.ds(direction * half, half)]
            else:
                link(direction, step - 1, origin, None if False else y_ref.at[pl.ds(origin * rows + direction * half, half)]).wait_recv()
                source = y_ref.at[pl.ds(origin * rows + direction * half, half)]
            copy = link(direction, step, origin, source)
            copy.start()
            sent.append(copy)
    last = n - 2
    for direction, origin in ((0, ring.device(pos - last - 1 + n)), (1, ring.device(pos + last + 1))):
        link(direction, last, origin, y_ref.at[pl.ds(origin * rows + direction * half, half)]).wait_recv()
    for copy in sent:
        copy.wait_send()
    own.wait()


def ring_all_gather(x, ring, collective_id):
    rows, cols = x.shape
    n = ring.size
    return pl.pallas_call(
        functools.partial(_gather_kernel, ring=ring, rows=rows),
        out_shape=jax.ShapeDtypeStruct((n * rows, cols), x.dtype),
        in_specs=[pl.BlockSpec(memory_space=pl.ANY)],
        out_specs=pl.BlockSpec(memory_space=pl.ANY),
        scratch_shapes=[
            pltpu.SemaphoreType.DMA(()),
            pltpu.SemaphoreType.DMA((2, n - 1)),
            pltpu.SemaphoreType.DMA((2, n - 1)),
        ],
        compiler_params=pltpu.CompilerParams(collective_id=collective_id, has_side_effects=True),
    )(x)


def _scatter_kernel(p_ref, out_ref, recv_buf, send_buf, send_sem, recv_sem, *, ring, rows):
    n = ring.size
    half = rows // 2
    g = lax.axis_index("dp")
    c = lax.axis_index("ctx")
    pos = ring.position(c)
    right = ring.device(pos + 1)
    left = ring.device(pos + n - 1)
    _barrier(g, left, right)

    def link(direction, step):
        return pltpu.make_async_remote_copy(
            src_ref=send_buf.at[direction, step],
            dst_ref=recv_buf.at[direction, step],
            send_sem=send_sem.at[direction, step],
            recv_sem=recv_sem.at[direction, step],
            device_id=(g, right if direction == 0 else left),
            device_id_type=MESH_ID,
        )

    sent = []
    for step in range(n - 1):
        targets = (ring.device(pos - 1 - step + 2 * n), ring.device(pos + 1 + step))
        for direction in (0, 1):
            start = pl.multiple_of(targets[direction] * rows + direction * half, half)
            total = p_ref[pl.ds(start, half), :].astype(jnp.float32)
            if step > 0:
                link(direction, step - 1).wait_recv()
                total = total + recv_buf[direction, step - 1].astype(jnp.float32)
            send_buf[direction, step] = total.astype(send_buf.dtype)
            copy = link(direction, step)
            copy.start()
            sent.append(copy)
    for direction in (0, 1):
        link(direction, n - 2).wait_recv()
        start = pl.multiple_of(c * rows + direction * half, half)
        out_ref[pl.ds(direction * half, half), :] = (
            p_ref[pl.ds(start, half), :].astype(jnp.float32)
            + recv_buf[direction, n - 2].astype(jnp.float32)
        ).astype(out_ref.dtype)
    for copy in sent:
        copy.wait_send()


def ring_reduce_scatter(p, ring, collective_id, out_dtype=jnp.float32, wire=jnp.bfloat16):
    total_rows, cols = p.shape
    n = ring.size
    rows = total_rows // n
    half = rows // 2
    return pl.pallas_call(
        functools.partial(_scatter_kernel, ring=ring, rows=rows),
        out_shape=jax.ShapeDtypeStruct((rows, cols), out_dtype),
        in_specs=[pl.BlockSpec(memory_space=pltpu.VMEM)],
        out_specs=pl.BlockSpec(memory_space=pltpu.VMEM),
        scratch_shapes=[
            pltpu.VMEM((2, n - 1, half, cols), wire),
            pltpu.VMEM((2, n - 1, half, cols), wire),
            pltpu.SemaphoreType.DMA((2, n - 1)),
            pltpu.SemaphoreType.DMA((2, n - 1)),
        ],
        compiler_params=pltpu.CompilerParams(
            collective_id=collective_id, has_side_effects=True, vmem_limit_bytes=60 * 1024 * 1024
        ),
    )(p)


def _exchange_kernel(x_ref, out_ref, own_sem, send_sem, recv_sem, *, group):
    n = x_ref.shape[0]
    g = lax.axis_index("dp")
    c = lax.axis_index("ctx")
    n_ctx = lax.axis_size("ctx")
    me = {"all": g * n_ctx + c, "ctx": c, "dp": g}[group]

    def address(member):
        if group == "all":
            return (member // n_ctx, member % n_ctx)
        if group == "ctx":
            return (g, member)
        return (member, c)

    own = pltpu.make_async_copy(x_ref.at[me], out_ref.at[me], own_sem)
    own.start()
    barrier = pltpu.get_barrier_semaphore()
    for offset in range(1, n):
        pl.semaphore_signal(
            barrier, 1, device_id=address((me + offset) % n), device_id_type=MESH_ID
        )
    pl.semaphore_wait(barrier, n - 1)

    def link(offset, source, target):
        return pltpu.make_async_remote_copy(
            src_ref=x_ref.at[target],
            dst_ref=out_ref.at[source],
            send_sem=send_sem.at[offset],
            recv_sem=recv_sem.at[offset],
            device_id=address(target),
            device_id_type=MESH_ID,
        )

    sent = []
    for offset in range(1, n):
        copy = link(offset, me, (me + offset) % n)
        copy.start()
        sent.append(copy)
    for offset in range(1, n):
        link(offset, (me + n - offset) % n, me).wait_recv()
    for copy in sent:
        copy.wait_send()
    own.wait()


def exchange(x, group, collective_id):
    n = x.shape[0]
    space = pltpu.VMEM
    return pl.pallas_call(
        functools.partial(_exchange_kernel, group=group),
        out_shape=jax.ShapeDtypeStruct(x.shape, x.dtype),
        in_specs=[pl.BlockSpec(memory_space=space)],
        out_specs=pl.BlockSpec(memory_space=space),
        scratch_shapes=[
            pltpu.SemaphoreType.DMA(()),
            pltpu.SemaphoreType.DMA((n,)),
            pltpu.SemaphoreType.DMA((n,)),
        ],
        compiler_params=pltpu.CompilerParams(collective_id=collective_id, has_side_effects=True),
    )(x)


def block_moves(n_dp, n_ctx):
    count = n_dp * n_ctx
    return [(f, (f % n_dp) * n_ctx + f // n_dp) for f in range(count)]


def fetch_out_rows(w_out):
    n_dp = lax.axis_size("dp")
    n_ctx = lax.axis_size("ctx")
    moved = lax.ppermute(w_out.astype(jnp.bfloat16), ("dp", "ctx"), perm=block_moves(n_dp, n_ctx))
    return lax.all_gather(moved, "dp", axis=0, tiled=True)


def return_out_rows(grad_out_rows):
    n_dp = lax.axis_size("dp")
    n_ctx = lax.axis_size("ctx")
    part = lax.psum_scatter(grad_out_rows, "dp", scatter_dimension=0, tiled=True)
    back = [(b, a) for a, b in block_moves(n_dp, n_ctx)]
    return lax.ppermute(part, ("dp", "ctx"), perm=back)


def pack_rows(vector, lanes):
    size = vector.shape[0]
    total = -(-size // (16 * lanes)) * 16 * lanes
    return jnp.pad(vector, (0, total - size)).reshape(-1, lanes)


def fetch_small(b_qkv, b_out, b_fc2, ln_gain, ln_shift, b_fc1):
    pieces = (b_qkv, b_out, b_fc2, ln_gain, ln_shift, b_fc1)
    n_dp = lax.axis_size("dp")
    n_ctx = lax.axis_size("ctx")
    packed = pack_rows(jnp.concatenate([p.astype(jnp.bfloat16) for p in pieces]), 128)
    over_dp = exchange(jnp.broadcast_to(packed[None], (n_dp,) + packed.shape), "dp", 4)
    over_all = exchange(jnp.broadcast_to(over_dp[None], (n_ctx,) + over_dp.shape), "ctx", 8)
    table = over_all.transpose(1, 0, 2, 3).reshape(n_dp * n_ctx, -1)
    result = []
    offset = 0
    for p in pieces:
        result.append(table[:, offset : offset + p.shape[0]])
        offset += p.shape[0]
    return result


def reduce_small(small):
    n_dp = lax.axis_size("dp")
    n_ctx = lax.axis_size("ctx")
    count, width = small.shape
    packed = jax.vmap(lambda row: pack_rows(row, 128))(small)
    packed = packed.reshape((n_dp, n_ctx) + packed.shape[1:]).transpose(1, 0, 2, 3)
    over_ctx = jnp.sum(exchange(packed, "ctx", 7), axis=0)
    over_dp = jnp.sum(exchange(over_ctx, "dp", 9), axis=0)
    return over_dp.reshape(-1)[:width]


def fetch_heads(w_qkv, w_fc1, w_fc2, tokens):
    dp_count = lax.axis_size("dp")
    ctx_count = lax.axis_size("ctx")
    rows_piece = w_qkv.shape[0]
    head_width = D // ctx_count
    unit = FF // (dp_count * ctx_count)
    qkv_piece = w_qkv.astype(jnp.bfloat16).reshape(rows_piece, 3, ctx_count, head_width)
    fc1_piece = w_fc1.astype(jnp.bfloat16).reshape(rows_piece, dp_count, ctx_count, unit)
    pieces = jnp.concatenate(
        [
            qkv_piece.transpose(2, 0, 1, 3).reshape(ctx_count, rows_piece, 3 * head_width),
            fc1_piece.transpose(2, 0, 1, 3).reshape(ctx_count, rows_piece, dp_count * unit),
        ],
        axis=2,
    )
    sent = exchange(pieces, "ctx", 5).reshape(ctx_count * rows_piece, -1)
    sent, tokens = lax.optimization_barrier((sent, tokens))
    cols, fc2_rows = (
        lax.all_gather(sent, "dp", axis=0, tiled=True),
        lax.all_gather(w_fc2.astype(jnp.bfloat16), "dp", axis=0, tiled=True),
    )
    return (cols, fc2_rows, tokens)


def return_heads(owned_parts):
    dp_count = lax.axis_size("dp")
    ctx_count = lax.axis_size("ctx")
    head_width = D // ctx_count
    unit = FF // (dp_count * ctx_count)
    rows_piece = owned_parts.shape[0] // ctx_count
    got = exchange(owned_parts.reshape(ctx_count, rows_piece, -1), "ctx", 6)
    qkv = got[:, :, : 3 * head_width].reshape(ctx_count, rows_piece, 3, head_width)
    fc1 = got[:, :, 3 * head_width :].reshape(ctx_count, rows_piece, dp_count, unit)
    return (
        qkv.transpose(1, 2, 0, 3).reshape(rows_piece, 3 * D).astype(jnp.float32),
        fc1.transpose(1, 2, 0, 3).reshape(rows_piece, FF).astype(jnp.float32),
    )


def head_plan(
    ring,
    tokens,
    lengths,
    w_qkv,
    b_qkv,
    w_out,
    b_out,
    w_fc1,
    b_fc1,
    w_fc2,
    b_fc2,
    ln_gain,
    ln_shift,
    cotangent,
):
    rows_here = tokens.shape[0]
    rows_piece = w_qkv.shape[0]
    dp_count = lax.axis_size("dp")
    ctx_count = lax.axis_size("ctx")
    count = dp_count * ctx_count
    group = rows_here * ctx_count
    head_width = D // ctx_count
    local_heads = HEADS // ctx_count
    unit = FF // (dp_count * ctx_count)
    here = lax.axis_index("ctx")
    group_rows = jnp.arange(group, dtype=jnp.int32)
    seg, positions = segment_info(lengths[0], group_rows)
    cosine, sine = rotary_tables(positions)
    qkv_bias, out_bias, fc2_bias, gain_low, shift_low, fc1_table = fetch_small(
        b_qkv, b_out, b_fc2, ln_gain, ln_shift, b_fc1
    )
    qkv_bias = qkv_bias.reshape(3 * D)
    out_bias = out_bias.reshape(D)
    fc2_bias = fc2_bias.reshape(D)
    gain_low = gain_low.reshape(D)
    shift_low = shift_low.reshape(D)
    fc1_bias = lax.dynamic_index_in_dim(
        fc1_table.reshape(dp_count, ctx_count, unit), here, 1, keepdims=False
    ).reshape(dp_count * unit)
    out_rows = fetch_out_rows(w_out)
    cols, fc2_rows, tokens = fetch_heads(w_qkv, w_fc1, w_fc2, tokens)
    gain32 = gain_low.astype(jnp.float32)
    shift32 = shift_low.astype(jnp.float32)
    inputs = tokens.astype(jnp.float32)
    normed, scaled, _ = norm_parts(inputs, gain32, shift32)
    tokens_group = ring_all_gather(tokens, ring, 0)
    late_dy, tokens_group = lax.optimization_barrier((cotangent, tokens_group))
    dy_group = lax.all_gather(late_dy, "ctx", axis=0, tiled=True)
    hidden_group = norm_parts(tokens_group.astype(jnp.float32), gain32, shift32)[2].astype(
        jnp.bfloat16
    )
    bias_cols = lax.dynamic_slice_in_dim(
        qkv_bias.reshape(3, D), here * head_width, head_width, 1
    ).reshape(3 * head_width)
    both = jnp.dot(hidden_group, cols, preferred_element_type=jnp.float32) + jnp.concatenate(
        [bias_cols, fc1_bias]
    ).astype(jnp.float32)
    qkv = both[:, : 3 * head_width]
    pre = both[:, 3 * head_width :]
    shape = (group, local_heads, HEAD_DIM)
    query = rotate(qkv[:, :head_width].reshape(shape), cosine, sine).astype(jnp.bfloat16)
    keys = rotate(qkv[:, head_width : 2 * head_width].reshape(shape), cosine, sine).astype(
        jnp.bfloat16
    )
    values = qkv[:, 2 * head_width :].reshape(shape).astype(jnp.bfloat16)
    q_heads = query.transpose(1, 0, 2)
    k_heads = keys.transpose(1, 0, 2)
    v_heads = values.transpose(1, 0, 2)
    attended_heads, log_total = attention_forward(q_heads, k_heads, v_heads, seg)
    attended = attended_heads.transpose(1, 0, 2).reshape(group, head_width).astype(jnp.bfloat16)
    act = gelu_tanh(pre).astype(jnp.bfloat16)
    branches = ring_reduce_scatter(
        jnp.dot(attended, out_rows, preferred_element_type=jnp.float32)
        + jnp.dot(act, fc2_rows, preferred_element_type=jnp.float32),
        ring,
        2,
    )
    block_out = (
        inputs + branches + out_bias.astype(jnp.float32) + fc2_bias.astype(jnp.float32)
    ).astype(jnp.bfloat16)
    grad_out32 = cotangent.astype(jnp.float32)
    grad_b_fc2 = jnp.sum(grad_out32, axis=0)
    grad_fc2_part = jnp.einsum("tf,td->fd", act, dy_group, preferred_element_type=jnp.float32)
    d_act = jnp.einsum("td,fd->tf", dy_group, fc2_rows, preferred_element_type=jnp.float32)
    d_pre = (d_act * gelu_slope(pre)).astype(jnp.bfloat16)
    grad_bfc1_part = jnp.sum(d_pre.astype(jnp.float32), axis=0)
    grad_out_rows = jnp.einsum("tc,td->cd", attended, dy_group, preferred_element_type=jnp.float32)
    owned_w_out = return_out_rows(grad_out_rows)
    d_attended = (
        jnp.einsum("td,cd->tc", dy_group, out_rows, preferred_element_type=jnp.float32)
        .astype(jnp.bfloat16)
        .reshape(shape)
    )
    d_heads = d_attended.transpose(1, 0, 2)
    delta = jnp.sum(d_heads.astype(jnp.float32) * attended_heads, axis=2, keepdims=True)
    dq_heads, dk_heads, dv_heads = attention_backward(
        q_heads, k_heads, v_heads, d_heads, log_total, delta, seg
    )
    d_query = dq_heads.transpose(1, 0, 2)
    d_keys = dk_heads.transpose(1, 0, 2)
    d_values = dv_heads.transpose(1, 0, 2)
    d_query = rotate_back(d_query, cosine, sine).reshape(group, head_width)
    d_keys = rotate_back(d_keys, cosine, sine).reshape(group, head_width)
    d_qkv = jnp.concatenate([d_query, d_keys, d_values.reshape(group, head_width)], axis=1).astype(
        jnp.bfloat16
    )
    d_both = jnp.concatenate([d_qkv, d_pre], axis=1)
    bias_part = jnp.sum(d_qkv.astype(jnp.float32), axis=0).reshape(3, head_width)
    d_hidden = ring_reduce_scatter(
        jnp.einsum("tc,dc->td", d_both, cols, preferred_element_type=jnp.float32), ring, 3
    )
    weight_parts = jnp.einsum(
        "td,tc->dc", hidden_group, d_both, preferred_element_type=jnp.float32
    ).astype(jnp.bfloat16)
    owned_parts = lax.psum_scatter(weight_parts, "dp", scatter_dimension=0, tiled=True)
    split_qkv, split_fc1 = return_heads(owned_parts)
    d_hidden, split_qkv, split_fc1 = lax.optimization_barrier((d_hidden, split_qkv, split_fc1))
    grad_gain, grad_shift, d_inputs = norm_back(d_hidden, normed, scaled, gain32)
    grad_tokens = (grad_out32 + d_inputs).astype(jnp.bfloat16)
    owned_fc2 = lax.psum_scatter(
        grad_fc2_part.astype(jnp.bfloat16), "dp", scatter_dimension=0, tiled=True
    ).astype(jnp.float32)
    full_bqkv = lax.dynamic_update_slice_in_dim(
        jnp.zeros((3, D), jnp.float32), bias_part, here * head_width, 1
    )
    full_bfc1 = lax.dynamic_update_slice_in_dim(
        jnp.zeros((dp_count, ctx_count, unit), jnp.float32),
        grad_bfc1_part.reshape(dp_count, 1, unit),
        here,
        1,
    )
    small = jnp.concatenate(
        [
            full_bqkv.reshape(count, -1),
            grad_b_fc2.reshape(count, -1),
            grad_gain.reshape(count, -1),
            grad_shift.reshape(count, -1),
            full_bfc1.reshape(count, -1),
        ],
        axis=1,
    )
    owned_small = reduce_small(small)
    cuts = [0, 3 * D // count, D // count, D // count, D // count, FF // count]
    bounds = [sum(cuts[: i + 1]) for i in range(len(cuts))]
    owned_bqkv, owned_bout, owned_gain, owned_shift, owned_bfc1 = [
        owned_small[bounds[i] : bounds[i + 1]] for i in range(5)
    ]
    return (
        block_out,
        grad_tokens,
        split_qkv.reshape(rows_piece, 3 * D),
        owned_bqkv,
        owned_w_out,
        owned_bout,
        split_fc1.reshape(rows_piece, FF),
        owned_bfc1,
        owned_fc2,
        owned_bout,
        owned_gain,
        owned_shift,
    )


def body(
    ring,
    tokens,
    lengths,
    w_qkv,
    b_qkv,
    w_out,
    b_out,
    w_fc1,
    b_fc1,
    w_fc2,
    b_fc2,
    ln_gain,
    ln_shift,
    cotangent,
):
    return head_plan(
        ring,
        tokens,
        lengths,
        w_qkv,
        b_qkv,
        w_out,
        b_out,
        w_fc1,
        b_fc1,
        w_fc2,
        b_fc2,
        ln_gain,
        ln_shift,
        cotangent,
    )


def solution(mesh):
    in_specs = (
        P(("dp", "ctx"), None),
        P("dp", None),
        P(("dp", "ctx"), None),
        P(("dp", "ctx")),
        P(("dp", "ctx"), None),
        P(("dp", "ctx")),
        P(("dp", "ctx"), None),
        P(("dp", "ctx")),
        P(("dp", "ctx"), None),
        P(("dp", "ctx")),
        P(("dp", "ctx")),
        P(("dp", "ctx")),
        P(("dp", "ctx"), None),
    )
    out_specs = (
        P(("dp", "ctx"), None),
        P(("dp", "ctx"), None),
        P(("dp", "ctx"), None),
        P(("dp", "ctx")),
        P(("dp", "ctx"), None),
        P(("dp", "ctx")),
        P(("dp", "ctx"), None),
        P(("dp", "ctx")),
        P(("dp", "ctx"), None),
        P(("dp", "ctx")),
        P(("dp", "ctx")),
        P(("dp", "ctx")),
    )
    ring = ring_of(mesh)
    return jax.shard_map(functools.partial(body, ring), mesh=mesh, in_specs=in_specs, out_specs=out_specs, check_vma=False)
```

```python
import functools
import math

import jax
import jax.numpy as jnp
from jax import lax
from jax.experimental import pallas as pl
from jax.experimental.pallas import tpu as pltpu
from jax.sharding import PartitionSpec as P

D = 2048
HEADS = 32
HEAD_DIM = 64
ROT = 32
FF = 8192


EPS = 1e-05
GELU_COEF = math.sqrt(2.0 / math.pi)
NEGATIVE = -1e30


def norm_parts(inputs, gain, shift):
    mean = jnp.mean(inputs, axis=-1, keepdims=True)
    centred = inputs - mean
    var = jnp.mean(centred * centred, axis=-1, keepdims=True)
    scaled = lax.rsqrt(var + EPS)
    normed = centred * scaled
    return (normed, scaled, normed * gain + shift)


def norm_back(d_hidden, normed, scaled, gain32):
    grad_gain = jnp.sum(d_hidden * normed, axis=0)
    grad_shift = jnp.sum(d_hidden, axis=0)
    d_normed = d_hidden * gain32
    d_inputs = scaled * (
        d_normed
        - jnp.mean(d_normed, axis=-1, keepdims=True)
        - normed * jnp.mean(d_normed * normed, axis=-1, keepdims=True)
    )
    return (grad_gain, grad_shift, d_inputs)


def gelu_tanh(pre):
    return 0.5 * pre * (1.0 + jnp.tanh(GELU_COEF * (pre + 0.044715 * pre * pre * pre)))


def gelu_slope(pre):
    tangent = jnp.tanh(GELU_COEF * (pre + 0.044715 * pre * pre * pre))
    return 0.5 * (1.0 + tangent) + 0.5 * pre * (1.0 - tangent * tangent) * GELU_COEF * (
        1.0 + 3.0 * 0.044715 * pre * pre
    )


def rotary_tables(positions):
    half = ROT // 2
    freq = jnp.exp(jnp.arange(half, dtype=jnp.float32) * (-2.0 * math.log(10000.0) / ROT))
    angle = positions.astype(jnp.float32)[:, None] * freq[None, :]
    return (jnp.cos(angle)[:, None, :], jnp.sin(angle)[:, None, :])


def rotate(heads, cosine, sine):
    half = ROT // 2
    first = heads[..., :half]
    second = heads[..., half:ROT]
    return jnp.concatenate(
        [first * cosine - second * sine, second * cosine + first * sine, heads[..., ROT:]], axis=-1
    )


def rotate_back(grads, cosine, sine):
    half = ROT // 2
    first = grads[..., :half]
    second = grads[..., half:ROT]
    return jnp.concatenate(
        [first * cosine + second * sine, second * cosine - first * sine, grads[..., ROT:]], axis=-1
    )


def segment_info(lengths_row, rows):
    ends = jnp.cumsum(lengths_row)
    starts = ends - lengths_row
    seg = jnp.sum((rows[:, None] >= ends[None, :]).astype(jnp.int32), axis=1)
    onehot = seg[:, None] == jnp.arange(lengths_row.shape[0], dtype=jnp.int32)[None, :]
    first_rows = jnp.sum(jnp.where(onehot, starts[None, :], 0), axis=1)
    return (seg, rows - first_rows)


TRANS_B = (((1,), (1,)), ((), ()))


def _allowed(segq_ref, segk_ref, i, j, tq, tk, causal):
    same = segq_ref[...] == segk_ref[...]
    if not causal:
        return same
    rows = i * tq + lax.broadcasted_iota(jnp.int32, (tq, tk), 0)
    cols = j * tk + lax.broadcasted_iota(jnp.int32, (tq, tk), 1)
    return same & (cols <= rows)


def _fwd_kernel(qi_ref, kj_ref, q_ref, k_ref, v_ref, segq_ref, segk_ref, o_ref, lse_ref, m_sc, l_sc, acc_sc, *, tq, tk, scale):
    t = pl.program_id(1)
    i = qi_ref[t]
    j = kj_ref[t]

    @pl.when(j == 0)
    def _():
        m_sc[...] = jnp.full_like(m_sc, NEGATIVE)
        l_sc[...] = jnp.zeros_like(l_sc)
        acc_sc[...] = jnp.zeros_like(acc_sc)

    def absorb(causal):
        q = q_ref[0]
        k = k_ref[0]
        s = lax.dot_general(q, k, TRANS_B, preferred_element_type=jnp.float32) * scale
        s = jnp.where(_allowed(segq_ref, segk_ref, i, j, tq, tk, causal), s, -jnp.inf)
        m_prev = m_sc[...]
        m_new = jnp.maximum(m_prev, jnp.max(s, axis=1, keepdims=True))
        factor = jnp.exp(m_prev - m_new)
        p = jnp.exp(s - m_new)
        l_sc[...] = l_sc[...] * factor + jnp.sum(p, axis=1, keepdims=True)
        acc_sc[...] = acc_sc[...] * factor + jnp.dot(
            p.astype(jnp.bfloat16), v_ref[0], preferred_element_type=jnp.float32
        )
        m_sc[...] = m_new

    @pl.when(j < i)
    def _():
        absorb(False)

    @pl.when(j == i)
    def _():
        absorb(True)
        total = l_sc[...]
        o_ref[0] = acc_sc[...] / total
        lse_ref[0] = m_sc[...] + jnp.log(total)


def _schedule(count, queries_outer):
    if queries_outer:
        pairs = [(i, j) for i in range(count) for j in range(i + 1)]
    else:
        pairs = [(i, j) for j in range(count) for i in range(j, count)]
    return (
        jnp.asarray([p[0] for p in pairs], jnp.int32),
        jnp.asarray([p[1] for p in pairs], jnp.int32),
    )


def attention_forward(q, k, v, seg, block=512):
    heads, total, dim = q.shape
    count = total // block
    scale = 1.0 / math.sqrt(dim)
    segq = seg.reshape(total, 1)
    segk = seg.reshape(1, total)
    qi, kj = _schedule(count, True)
    steps = qi.shape[0]

    return pl.pallas_call(
        functools.partial(_fwd_kernel, tq=block, tk=block, scale=scale),
        out_shape=(
            jax.ShapeDtypeStruct((heads, total, dim), jnp.float32),
            jax.ShapeDtypeStruct((heads, total, 1), jnp.float32),
        ),
        grid_spec=pltpu.PrefetchScalarGridSpec(
            num_scalar_prefetch=2,
            grid=(heads, steps),
            in_specs=[
                pl.BlockSpec((1, block, dim), lambda h, t, qi, kj: (h, qi[t], 0)),
                pl.BlockSpec((1, block, dim), lambda h, t, qi, kj: (h, kj[t], 0)),
                pl.BlockSpec((1, block, dim), lambda h, t, qi, kj: (h, kj[t], 0)),
                pl.BlockSpec((block, 1), lambda h, t, qi, kj: (qi[t], 0)),
                pl.BlockSpec((1, block), lambda h, t, qi, kj: (0, kj[t])),
            ],
            out_specs=[
                pl.BlockSpec((1, block, dim), lambda h, t, qi, kj: (h, qi[t], 0)),
                pl.BlockSpec((1, block, 1), lambda h, t, qi, kj: (h, qi[t], 0)),
            ],
            scratch_shapes=[
                pltpu.VMEM((block, 1), jnp.float32),
                pltpu.VMEM((block, 1), jnp.float32),
                pltpu.VMEM((block, dim), jnp.float32),
            ],
        ),
        cost_estimate=pl.CostEstimate(
            flops=2 * heads * total * total * dim,
            transcendentals=heads * total * total // 2,
            bytes_accessed=heads * total * dim * 10,
        ),
    )(qi, kj, q, k, v, segq, segk)


def _bwd_kernel(qi_ref, kj_ref, q_ref, k_ref, v_ref, do_ref, lse_ref, delta_ref, segq_ref, segk_ref, dq_ref, dk_ref, dv_ref, *, tq, tk, scale):
    t = pl.program_id(1)
    i = qi_ref[t]
    j = kj_ref[t]

    @pl.when(t == 0)
    def _():
        dq_ref[...] = jnp.zeros_like(dq_ref)

    @pl.when(i == j)
    def _():
        dk_ref[...] = jnp.zeros_like(dk_ref)
        dv_ref[...] = jnp.zeros_like(dv_ref)

    def absorb(causal):
        q = q_ref[0]
        k = k_ref[0]
        do = do_ref[0]
        s = lax.dot_general(q, k, TRANS_B, preferred_element_type=jnp.float32) * scale
        s = jnp.where(_allowed(segq_ref, segk_ref, i, j, tq, tk, causal), s, -jnp.inf)
        p = jnp.exp(s - lse_ref[0])
        dp = lax.dot_general(do, v_ref[0], TRANS_B, preferred_element_type=jnp.float32)
        ds = (p * (dp - delta_ref[0])).astype(jnp.bfloat16)
        dv_ref[0] += lax.dot(p.astype(jnp.bfloat16).T, do, preferred_element_type=jnp.float32)
        dk_ref[0] += lax.dot(ds.T, q, preferred_element_type=jnp.float32) * scale
        rows = pl.ds(pl.multiple_of(i * tq, tq), tq)
        dq_ref[0, rows, :] += lax.dot(ds, k, preferred_element_type=jnp.float32) * scale

    @pl.when(j < i)
    def _():
        absorb(False)

    @pl.when(j == i)
    def _():
        absorb(True)


def attention_backward(q, k, v, do, lse, delta, seg, block=512):
    heads, total, dim = q.shape
    count = total // block
    scale = 1.0 / math.sqrt(dim)
    segq = seg.reshape(total, 1)
    segk = seg.reshape(1, total)
    qi, kj = _schedule(count, False)
    steps = qi.shape[0]

    def q_map(h, t, qi, kj):
        return (h, qi[t], 0)

    def k_map(h, t, qi, kj):
        return (h, kj[t], 0)

    return pl.pallas_call(
        functools.partial(_bwd_kernel, tq=block, tk=block, scale=scale),
        out_shape=(
            jax.ShapeDtypeStruct((heads, total, dim), jnp.float32),
            jax.ShapeDtypeStruct((heads, total, dim), jnp.float32),
            jax.ShapeDtypeStruct((heads, total, dim), jnp.float32),
        ),
        grid_spec=pltpu.PrefetchScalarGridSpec(
            num_scalar_prefetch=2,
            grid=(heads, steps),
            in_specs=[
                pl.BlockSpec((1, block, dim), q_map),
                pl.BlockSpec((1, block, dim), k_map),
                pl.BlockSpec((1, block, dim), k_map),
                pl.BlockSpec((1, block, dim), q_map),
                pl.BlockSpec((1, block, 1), q_map),
                pl.BlockSpec((1, block, 1), q_map),
                pl.BlockSpec((block, 1), lambda h, t, qi, kj: (qi[t], 0)),
                pl.BlockSpec((1, block), lambda h, t, qi, kj: (0, kj[t])),
            ],
            out_specs=[
                pl.BlockSpec((1, total, dim), lambda h, t, qi, kj: (h, 0, 0)),
                pl.BlockSpec((1, block, dim), k_map),
                pl.BlockSpec((1, block, dim), k_map),
            ],
        ),
        cost_estimate=pl.CostEstimate(
            flops=5 * heads * total * total * dim,
            transcendentals=heads * total * total // 2,
            bytes_accessed=heads * total * dim * 24,
        ),
    )(qi, kj, q, k, v, do, lse, delta, segq, segk)


MESH_ID = pl.DeviceIdType.MESH


class Ring:
    def __init__(self, size, a_stride, b_stride):
        self.size = size
        self.half = size // 2
        self.a_stride = a_stride
        self.b_stride = b_stride

    def position(self, c):
        a = (c // self.a_stride) % self.half
        b = (c // self.b_stride) % 2
        return a + b * (2 * self.half - 1 - 2 * a)

    def device(self, pos):
        pos = pos % self.size
        b = pos // self.half
        a = pos + b * (2 * self.half - 1 - 2 * pos)
        return a * self.a_stride + b * self.b_stride


def ring_of(mesh):
    size = mesh.shape["ctx"]
    devices = list(mesh.devices.reshape(-1, size)[0])
    try:
        coords = [tuple(d.coords) for d in devices]
    except AttributeError:
        coords = None
    if coords and size % 2 == 0 and size >= 4:
        for b_stride in range(1, size):
            for a_stride in range(1, size):
                ring = Ring(size, a_stride, b_stride)
                order = [ring.device(p) for p in range(size)]
                if sorted(order) != list(range(size)):
                    continue
                hops = [
                    sum(abs(x - y) for x, y in zip(coords[order[p]], coords[order[(p + 1) % size]]))
                    for p in range(size)
                ]
                if max(hops) == 1:
                    return ring
    return Ring(size, 2, 1) if size % 2 == 0 and size >= 4 else None


def _barrier(g, left, right):
    barrier = pltpu.get_barrier_semaphore()
    for other in (left, right):
        pl.semaphore_signal(barrier, 1, device_id=(g, other), device_id_type=MESH_ID)
    pl.semaphore_wait(barrier, 2)


def _gather_kernel(x_ref, y_ref, own_sem, send_sem, recv_sem, *, ring, rows):
    n = ring.size
    half = rows // 2
    g = lax.axis_index("dp")
    c = lax.axis_index("ctx")
    pos = ring.position(c)
    right = ring.device(pos + 1)
    left = ring.device(pos + n - 1)
    own = pltpu.make_async_copy(x_ref, y_ref.at[pl.ds(c * rows, rows)], own_sem)
    own.start()
    _barrier(g, left, right)

    def link(direction, step, origin, source):
        offset = origin * rows + direction * half
        return pltpu.make_async_remote_copy(
            src_ref=source,
            dst_ref=y_ref.at[pl.ds(offset, half)],
            send_sem=send_sem.at[direction, step],
            recv_sem=recv_sem.at[direction, step],
            device_id=(g, right if direction == 0 else left),
            device_id_type=MESH_ID,
        )

    sent = []
    for step in range(n - 1):
        origins = (ring.device(pos - step + n), ring.device(pos + step))
        for direction in (0, 1):
            origin = origins[direction]
            if step == 0:
                source = x_ref.at[pl.ds(direction * half, half)]
            else:
                link(direction, step - 1, origin, None if False else y_ref.at[pl.ds(origin * rows + direction * half, half)]).wait_recv()
                source = y_ref.at[pl.ds(origin * rows + direction * half, half)]
            copy = link(direction, step, origin, source)
            copy.start()
            sent.append(copy)
    last = n - 2
    for direction, origin in ((0, ring.device(pos - last - 1 + n)), (1, ring.device(pos + last + 1))):
        link(direction, last, origin, y_ref.at[pl.ds(origin * rows + direction * half, half)]).wait_recv()
    for copy in sent:
        copy.wait_send()
    own.wait()


def ring_all_gather(x, ring, collective_id):
    rows, cols = x.shape
    n = ring.size
    return pl.pallas_call(
        functools.partial(_gather_kernel, ring=ring, rows=rows),
        out_shape=jax.ShapeDtypeStruct((n * rows, cols), x.dtype),
        in_specs=[pl.BlockSpec(memory_space=pl.ANY)],
        out_specs=pl.BlockSpec(memory_space=pl.ANY),
        scratch_shapes=[
            pltpu.SemaphoreType.DMA(()),
            pltpu.SemaphoreType.DMA((2, n - 1)),
            pltpu.SemaphoreType.DMA((2, n - 1)),
        ],
        compiler_params=pltpu.CompilerParams(collective_id=collective_id, has_side_effects=True),
    )(x)


def _scatter_kernel(p_ref, out_ref, recv_buf, send_buf, send_sem, recv_sem, *, ring, rows, parts):
    n = ring.size
    half = rows // 2
    piece = half // parts
    g = lax.axis_index("dp")
    c = lax.axis_index("ctx")
    pos = ring.position(c)
    right = ring.device(pos + 1)
    left = ring.device(pos + n - 1)
    _barrier(g, left, right)

    def link(direction, step, part):
        window = pl.ds(part * piece, piece)
        return pltpu.make_async_remote_copy(
            src_ref=send_buf.at[direction, step, window],
            dst_ref=recv_buf.at[direction, step, window],
            send_sem=send_sem.at[direction, step, part],
            recv_sem=recv_sem.at[direction, step, part],
            device_id=(g, right if direction == 0 else left),
            device_id_type=MESH_ID,
        )

    sent = []
    for step in range(n - 1):
        targets = (ring.device(pos - 1 - step + 2 * n), ring.device(pos + 1 + step))
        for part in range(parts):
            for direction in (0, 1):
                start = pl.multiple_of(
                    targets[direction] * rows + direction * half + part * piece, piece
                )
                window = pl.ds(part * piece, piece)
                total = p_ref[pl.ds(start, piece), :].astype(jnp.float32)
                if step > 0:
                    link(direction, step - 1, part).wait_recv()
                    total = total + recv_buf[direction, step - 1, window].astype(jnp.float32)
                send_buf[direction, step, window] = total.astype(send_buf.dtype)
                copy = link(direction, step, part)
                copy.start()
                sent.append(copy)
    for part in range(parts):
        for direction in (0, 1):
            link(direction, n - 2, part).wait_recv()
            start = pl.multiple_of(c * rows + direction * half + part * piece, piece)
            window = pl.ds(part * piece, piece)
            out_ref[pl.ds(direction * half + part * piece, piece), :] = (
                p_ref[pl.ds(start, piece), :].astype(jnp.float32)
                + recv_buf[direction, n - 2, window].astype(jnp.float32)
            ).astype(out_ref.dtype)
    for copy in sent:
        copy.wait_send()


def ring_reduce_scatter(p, ring, collective_id, out_dtype=jnp.float32, wire=jnp.bfloat16, parts=2):
    total_rows, cols = p.shape
    n = ring.size
    rows = total_rows // n
    half = rows // 2
    return pl.pallas_call(
        functools.partial(_scatter_kernel, ring=ring, rows=rows, parts=parts),
        out_shape=jax.ShapeDtypeStruct((rows, cols), out_dtype),
        in_specs=[pl.BlockSpec(memory_space=pltpu.VMEM)],
        out_specs=pl.BlockSpec(memory_space=pltpu.VMEM),
        scratch_shapes=[
            pltpu.VMEM((2, n - 1, half, cols), wire),
            pltpu.VMEM((2, n - 1, half, cols), wire),
            pltpu.SemaphoreType.DMA((2, n - 1, parts)),
            pltpu.SemaphoreType.DMA((2, n - 1, parts)),
        ],
        compiler_params=pltpu.CompilerParams(
            collective_id=collective_id, has_side_effects=True, vmem_limit_bytes=60 * 1024 * 1024
        ),
    )(p)


def _exchange_kernel(x_ref, out_ref, own_sem, send_sem, recv_sem, *, group):
    n = x_ref.shape[0]
    g = lax.axis_index("dp")
    c = lax.axis_index("ctx")
    n_ctx = lax.axis_size("ctx")
    me = {"all": g * n_ctx + c, "ctx": c, "dp": g}[group]

    def address(member):
        if group == "all":
            return (member // n_ctx, member % n_ctx)
        if group == "ctx":
            return (g, member)
        return (member, c)

    own = pltpu.make_async_copy(x_ref.at[me], out_ref.at[me], own_sem)
    own.start()
    barrier = pltpu.get_barrier_semaphore()
    for offset in range(1, n):
        pl.semaphore_signal(
            barrier, 1, device_id=address((me + offset) % n), device_id_type=MESH_ID
        )
    pl.semaphore_wait(barrier, n - 1)

    def link(offset, source, target):
        return pltpu.make_async_remote_copy(
            src_ref=x_ref.at[target],
            dst_ref=out_ref.at[source],
            send_sem=send_sem.at[offset],
            recv_sem=recv_sem.at[offset],
            device_id=address(target),
            device_id_type=MESH_ID,
        )

    sent = []
    for offset in range(1, n):
        copy = link(offset, me, (me + offset) % n)
        copy.start()
        sent.append(copy)
    for offset in range(1, n):
        link(offset, (me + n - offset) % n, me).wait_recv()
    for copy in sent:
        copy.wait_send()
    own.wait()


def exchange(x, group, collective_id):
    n = x.shape[0]
    space = pltpu.VMEM
    return pl.pallas_call(
        functools.partial(_exchange_kernel, group=group),
        out_shape=jax.ShapeDtypeStruct(x.shape, x.dtype),
        in_specs=[pl.BlockSpec(memory_space=space)],
        out_specs=pl.BlockSpec(memory_space=space),
        scratch_shapes=[
            pltpu.SemaphoreType.DMA(()),
            pltpu.SemaphoreType.DMA((n,)),
            pltpu.SemaphoreType.DMA((n,)),
        ],
        compiler_params=pltpu.CompilerParams(collective_id=collective_id, has_side_effects=True),
    )(x)


def block_moves(n_dp, n_ctx):
    count = n_dp * n_ctx
    return [(f, (f % n_dp) * n_ctx + f // n_dp) for f in range(count)]


def fetch_out_rows(w_out):
    n_dp = lax.axis_size("dp")
    n_ctx = lax.axis_size("ctx")
    moved = lax.ppermute(w_out.astype(jnp.bfloat16), ("dp", "ctx"), perm=block_moves(n_dp, n_ctx))
    return lax.all_gather(moved, "dp", axis=0, tiled=True)


def return_out_rows(grad_out_rows):
    n_dp = lax.axis_size("dp")
    n_ctx = lax.axis_size("ctx")
    part = lax.psum_scatter(grad_out_rows, "dp", scatter_dimension=0, tiled=True)
    back = [(b, a) for a, b in block_moves(n_dp, n_ctx)]
    return lax.ppermute(part, ("dp", "ctx"), perm=back)


def pack_rows(vector, lanes):
    size = vector.shape[0]
    total = -(-size // (16 * lanes)) * 16 * lanes
    return jnp.pad(vector, (0, total - size)).reshape(-1, lanes)


def fetch_small(b_qkv, b_out, b_fc2, ln_gain, ln_shift, b_fc1):
    pieces = (b_qkv, b_out, b_fc2, ln_gain, ln_shift, b_fc1)
    n_dp = lax.axis_size("dp")
    n_ctx = lax.axis_size("ctx")
    packed = pack_rows(jnp.concatenate([p.astype(jnp.bfloat16) for p in pieces]), 128)
    over_dp = exchange(jnp.broadcast_to(packed[None], (n_dp,) + packed.shape), "dp", 4)
    over_all = exchange(jnp.broadcast_to(over_dp[None], (n_ctx,) + over_dp.shape), "ctx", 8)
    table = over_all.transpose(1, 0, 2, 3).reshape(n_dp * n_ctx, -1)
    result = []
    offset = 0
    for p in pieces:
        result.append(table[:, offset : offset + p.shape[0]])
        offset += p.shape[0]
    return result


def reduce_small(small):
    n_dp = lax.axis_size("dp")
    n_ctx = lax.axis_size("ctx")
    count, width = small.shape
    packed = jax.vmap(lambda row: pack_rows(row, 128))(small)
    packed = packed.reshape((n_dp, n_ctx) + packed.shape[1:]).transpose(1, 0, 2, 3)
    over_ctx = jnp.sum(exchange(packed, "ctx", 7), axis=0)
    over_dp = jnp.sum(exchange(over_ctx, "dp", 9), axis=0)
    return over_dp.reshape(-1)[:width]


def fetch_heads(w_qkv, w_fc1, w_fc2, tokens):
    dp_count = lax.axis_size("dp")
    ctx_count = lax.axis_size("ctx")
    rows_piece = w_qkv.shape[0]
    head_width = D // ctx_count
    unit = FF // (dp_count * ctx_count)
    qkv_piece = w_qkv.astype(jnp.bfloat16).reshape(rows_piece, 3, ctx_count, head_width)
    fc1_piece = w_fc1.astype(jnp.bfloat16).reshape(rows_piece, dp_count, ctx_count, unit)
    pieces = jnp.concatenate(
        [
            qkv_piece.transpose(2, 0, 1, 3).reshape(ctx_count, rows_piece, 3 * head_width),
            fc1_piece.transpose(2, 0, 1, 3).reshape(ctx_count, rows_piece, dp_count * unit),
        ],
        axis=2,
    )
    sent = exchange(pieces, "ctx", 5).reshape(ctx_count * rows_piece, -1)
    sent, tokens = lax.optimization_barrier((sent, tokens))
    cols, fc2_rows = (
        lax.all_gather(sent, "dp", axis=0, tiled=True),
        lax.all_gather(w_fc2.astype(jnp.bfloat16), "dp", axis=0, tiled=True),
    )
    return (cols, fc2_rows, tokens)


def return_heads(owned_parts):
    dp_count = lax.axis_size("dp")
    ctx_count = lax.axis_size("ctx")
    head_width = D // ctx_count
    unit = FF // (dp_count * ctx_count)
    rows_piece = owned_parts.shape[0] // ctx_count
    got = exchange(owned_parts.reshape(ctx_count, rows_piece, -1), "ctx", 6)
    qkv = got[:, :, : 3 * head_width].reshape(ctx_count, rows_piece, 3, head_width)
    fc1 = got[:, :, 3 * head_width :].reshape(ctx_count, rows_piece, dp_count, unit)
    return (
        qkv.transpose(1, 2, 0, 3).reshape(rows_piece, 3 * D).astype(jnp.float32),
        fc1.transpose(1, 2, 0, 3).reshape(rows_piece, FF).astype(jnp.float32),
    )


def head_plan(
    ring,
    tokens,
    lengths,
    w_qkv,
    b_qkv,
    w_out,
    b_out,
    w_fc1,
    b_fc1,
    w_fc2,
    b_fc2,
    ln_gain,
    ln_shift,
    cotangent,
):
    rows_here = tokens.shape[0]
    rows_piece = w_qkv.shape[0]
    dp_count = lax.axis_size("dp")
    ctx_count = lax.axis_size("ctx")
    count = dp_count * ctx_count
    group = rows_here * ctx_count
    head_width = D // ctx_count
    local_heads = HEADS // ctx_count
    unit = FF // (dp_count * ctx_count)
    here = lax.axis_index("ctx")
    group_rows = jnp.arange(group, dtype=jnp.int32)
    seg, positions = segment_info(lengths[0], group_rows)
    cosine, sine = rotary_tables(positions)
    qkv_bias, out_bias, fc2_bias, gain_low, shift_low, fc1_table = fetch_small(
        b_qkv, b_out, b_fc2, ln_gain, ln_shift, b_fc1
    )
    qkv_bias = qkv_bias.reshape(3 * D)
    out_bias = out_bias.reshape(D)
    fc2_bias = fc2_bias.reshape(D)
    gain_low = gain_low.reshape(D)
    shift_low = shift_low.reshape(D)
    fc1_bias = lax.dynamic_index_in_dim(
        fc1_table.reshape(dp_count, ctx_count, unit), here, 1, keepdims=False
    ).reshape(dp_count * unit)
    out_rows = fetch_out_rows(w_out)
    cols, fc2_rows, tokens = fetch_heads(w_qkv, w_fc1, w_fc2, tokens)
    gain32 = gain_low.astype(jnp.float32)
    shift32 = shift_low.astype(jnp.float32)
    inputs = tokens.astype(jnp.float32)
    normed, scaled, _ = norm_parts(inputs, gain32, shift32)
    tokens_group = ring_all_gather(tokens, ring, 0)
    late_dy, tokens_group = lax.optimization_barrier((cotangent, tokens_group))
    dy_group = lax.all_gather(late_dy, "ctx", axis=0, tiled=True)
    hidden_group = norm_parts(tokens_group.astype(jnp.float32), gain32, shift32)[2].astype(
        jnp.bfloat16
    )
    bias_cols = lax.dynamic_slice_in_dim(
        qkv_bias.reshape(3, D), here * head_width, head_width, 1
    ).reshape(3 * head_width)
    both = jnp.dot(hidden_group, cols, preferred_element_type=jnp.float32) + jnp.concatenate(
        [bias_cols, fc1_bias]
    ).astype(jnp.float32)
    qkv = both[:, : 3 * head_width]
    pre = both[:, 3 * head_width :]
    shape = (group, local_heads, HEAD_DIM)
    query = rotate(qkv[:, :head_width].reshape(shape), cosine, sine).astype(jnp.bfloat16)
    keys = rotate(qkv[:, head_width : 2 * head_width].reshape(shape), cosine, sine).astype(
        jnp.bfloat16
    )
    values = qkv[:, 2 * head_width :].reshape(shape).astype(jnp.bfloat16)
    q_heads = query.transpose(1, 0, 2)
    k_heads = keys.transpose(1, 0, 2)
    v_heads = values.transpose(1, 0, 2)
    attended_heads, log_total = attention_forward(q_heads, k_heads, v_heads, seg)
    attended = attended_heads.transpose(1, 0, 2).reshape(group, head_width).astype(jnp.bfloat16)
    act = gelu_tanh(pre).astype(jnp.bfloat16)
    branches = ring_reduce_scatter(
        jnp.dot(attended, out_rows, preferred_element_type=jnp.float32)
        + jnp.dot(act, fc2_rows, preferred_element_type=jnp.float32),
        ring,
        2,
    )
    block_out = (
        inputs + branches + out_bias.astype(jnp.float32) + fc2_bias.astype(jnp.float32)
    ).astype(jnp.bfloat16)
    grad_out32 = cotangent.astype(jnp.float32)
    grad_b_fc2 = jnp.sum(grad_out32, axis=0)
    grad_fc2_part = jnp.einsum("tf,td->fd", act, dy_group, preferred_element_type=jnp.float32)
    d_act = jnp.einsum("td,fd->tf", dy_group, fc2_rows, preferred_element_type=jnp.float32)
    d_pre = (d_act * gelu_slope(pre)).astype(jnp.bfloat16)
    grad_bfc1_part = jnp.sum(d_pre.astype(jnp.float32), axis=0)
    grad_out_rows = jnp.einsum("tc,td->cd", attended, dy_group, preferred_element_type=jnp.float32)
    owned_w_out = return_out_rows(grad_out_rows)
    d_attended = (
        jnp.einsum("td,cd->tc", dy_group, out_rows, preferred_element_type=jnp.float32)
        .astype(jnp.bfloat16)
        .reshape(shape)
    )
    d_heads = d_attended.transpose(1, 0, 2)
    delta = jnp.sum(d_heads.astype(jnp.float32) * attended_heads, axis=2, keepdims=True)
    dq_heads, dk_heads, dv_heads = attention_backward(
        q_heads, k_heads, v_heads, d_heads, log_total, delta, seg
    )
    d_query = dq_heads.transpose(1, 0, 2)
    d_keys = dk_heads.transpose(1, 0, 2)
    d_values = dv_heads.transpose(1, 0, 2)
    d_query = rotate_back(d_query, cosine, sine).reshape(group, head_width)
    d_keys = rotate_back(d_keys, cosine, sine).reshape(group, head_width)
    d_qkv = jnp.concatenate([d_query, d_keys, d_values.reshape(group, head_width)], axis=1).astype(
        jnp.bfloat16
    )
    d_both = jnp.concatenate([d_qkv, d_pre], axis=1)
    bias_part = jnp.sum(d_qkv.astype(jnp.float32), axis=0).reshape(3, head_width)
    d_hidden = ring_reduce_scatter(
        jnp.einsum("tc,dc->td", d_both, cols, preferred_element_type=jnp.float32), ring, 3
    )
    weight_parts = jnp.einsum(
        "td,tc->dc", hidden_group, d_both, preferred_element_type=jnp.float32
    ).astype(jnp.bfloat16)
    owned_parts = lax.psum_scatter(weight_parts, "dp", scatter_dimension=0, tiled=True)
    split_qkv, split_fc1 = return_heads(owned_parts)
    d_hidden, split_qkv, split_fc1 = lax.optimization_barrier((d_hidden, split_qkv, split_fc1))
    grad_gain, grad_shift, d_inputs = norm_back(d_hidden, normed, scaled, gain32)
    grad_tokens = (grad_out32 + d_inputs).astype(jnp.bfloat16)
    owned_fc2 = lax.psum_scatter(
        grad_fc2_part.astype(jnp.bfloat16), "dp", scatter_dimension=0, tiled=True
    ).astype(jnp.float32)
    full_bqkv = lax.dynamic_update_slice_in_dim(
        jnp.zeros((3, D), jnp.float32), bias_part, here * head_width, 1
    )
    full_bfc1 = lax.dynamic_update_slice_in_dim(
        jnp.zeros((dp_count, ctx_count, unit), jnp.float32),
        grad_bfc1_part.reshape(dp_count, 1, unit),
        here,
        1,
    )
    small = jnp.concatenate(
        [
            full_bqkv.reshape(count, -1),
            grad_b_fc2.reshape(count, -1),
            grad_gain.reshape(count, -1),
            grad_shift.reshape(count, -1),
            full_bfc1.reshape(count, -1),
        ],
        axis=1,
    )
    owned_small = reduce_small(small)
    cuts = [0, 3 * D // count, D // count, D // count, D // count, FF // count]
    bounds = [sum(cuts[: i + 1]) for i in range(len(cuts))]
    owned_bqkv, owned_bout, owned_gain, owned_shift, owned_bfc1 = [
        owned_small[bounds[i] : bounds[i + 1]] for i in range(5)
    ]
    return (
        block_out,
        grad_tokens,
        split_qkv.reshape(rows_piece, 3 * D),
        owned_bqkv,
        owned_w_out,
        owned_bout,
        split_fc1.reshape(rows_piece, FF),
        owned_bfc1,
        owned_fc2,
        owned_bout,
        owned_gain,
        owned_shift,
    )


def body(
    ring,
    tokens,
    lengths,
    w_qkv,
    b_qkv,
    w_out,
    b_out,
    w_fc1,
    b_fc1,
    w_fc2,
    b_fc2,
    ln_gain,
    ln_shift,
    cotangent,
):
    return head_plan(
        ring,
        tokens,
        lengths,
        w_qkv,
        b_qkv,
        w_out,
        b_out,
        w_fc1,
        b_fc1,
        w_fc2,
        b_fc2,
        ln_gain,
        ln_shift,
        cotangent,
    )


def solution(mesh):
    in_specs = (
        P(("dp", "ctx"), None),
        P("dp", None),
        P(("dp", "ctx"), None),
        P(("dp", "ctx")),
        P(("dp", "ctx"), None),
        P(("dp", "ctx")),
        P(("dp", "ctx"), None),
        P(("dp", "ctx")),
        P(("dp", "ctx"), None),
        P(("dp", "ctx")),
        P(("dp", "ctx")),
        P(("dp", "ctx")),
        P(("dp", "ctx"), None),
    )
    out_specs = (
        P(("dp", "ctx"), None),
        P(("dp", "ctx"), None),
        P(("dp", "ctx"), None),
        P(("dp", "ctx")),
        P(("dp", "ctx"), None),
        P(("dp", "ctx")),
        P(("dp", "ctx"), None),
        P(("dp", "ctx")),
        P(("dp", "ctx"), None),
        P(("dp", "ctx")),
        P(("dp", "ctx")),
        P(("dp", "ctx")),
    )
    ring = ring_of(mesh)
    return jax.shard_map(functools.partial(body, ring), mesh=mesh, in_specs=in_specs, out_specs=out_specs, check_vma=False)
```

```python
import functools
import math

import jax
import jax.numpy as jnp
from jax import lax
from jax.experimental import pallas as pl
from jax.experimental.pallas import tpu as pltpu
from jax.sharding import PartitionSpec as P

D = 2048
HEADS = 32
HEAD_DIM = 64
ROT = 32
FF = 8192


EPS = 1e-05
GELU_COEF = math.sqrt(2.0 / math.pi)
NEGATIVE = -1e30


def norm_parts(inputs, gain, shift):
    mean = jnp.mean(inputs, axis=-1, keepdims=True)
    centred = inputs - mean
    var = jnp.mean(centred * centred, axis=-1, keepdims=True)
    scaled = lax.rsqrt(var + EPS)
    normed = centred * scaled
    return (normed, scaled, normed * gain + shift)


def norm_back(d_hidden, normed, scaled, gain32):
    grad_gain = jnp.sum(d_hidden * normed, axis=0)
    grad_shift = jnp.sum(d_hidden, axis=0)
    d_normed = d_hidden * gain32
    d_inputs = scaled * (
        d_normed
        - jnp.mean(d_normed, axis=-1, keepdims=True)
        - normed * jnp.mean(d_normed * normed, axis=-1, keepdims=True)
    )
    return (grad_gain, grad_shift, d_inputs)


def gelu_tanh(pre):
    return 0.5 * pre * (1.0 + jnp.tanh(GELU_COEF * (pre + 0.044715 * pre * pre * pre)))


def gelu_slope(pre):
    tangent = jnp.tanh(GELU_COEF * (pre + 0.044715 * pre * pre * pre))
    return 0.5 * (1.0 + tangent) + 0.5 * pre * (1.0 - tangent * tangent) * GELU_COEF * (
        1.0 + 3.0 * 0.044715 * pre * pre
    )


def rotary_tables(positions):
    half = ROT // 2
    freq = jnp.exp(jnp.arange(half, dtype=jnp.float32) * (-2.0 * math.log(10000.0) / ROT))
    angle = positions.astype(jnp.float32)[:, None] * freq[None, :]
    return (jnp.cos(angle)[:, None, :], jnp.sin(angle)[:, None, :])


def rotate(heads, cosine, sine):
    half = ROT // 2
    first = heads[..., :half]
    second = heads[..., half:ROT]
    return jnp.concatenate(
        [first * cosine - second * sine, second * cosine + first * sine, heads[..., ROT:]], axis=-1
    )


def rotate_back(grads, cosine, sine):
    half = ROT // 2
    first = grads[..., :half]
    second = grads[..., half:ROT]
    return jnp.concatenate(
        [first * cosine + second * sine, second * cosine - first * sine, grads[..., ROT:]], axis=-1
    )


def segment_info(lengths_row, rows):
    ends = jnp.cumsum(lengths_row)
    starts = ends - lengths_row
    seg = jnp.sum((rows[:, None] >= ends[None, :]).astype(jnp.int32), axis=1)
    onehot = seg[:, None] == jnp.arange(lengths_row.shape[0], dtype=jnp.int32)[None, :]
    first_rows = jnp.sum(jnp.where(onehot, starts[None, :], 0), axis=1)
    return (seg, rows - first_rows)


TRANS_B = (((1,), (1,)), ((), ()))


def _allowed(segq_ref, segk_ref, i, j, tq, tk, causal):
    same = segq_ref[...] == segk_ref[...]
    if not causal:
        return same
    rows = i * tq + lax.broadcasted_iota(jnp.int32, (tq, tk), 0)
    cols = j * tk + lax.broadcasted_iota(jnp.int32, (tq, tk), 1)
    return same & (cols <= rows)


def _fwd_kernel(qi_ref, kj_ref, q_ref, k_ref, v_ref, segq_ref, segk_ref, o_ref, lse_ref, m_sc, acc_sc, *, tq, tk, scale):
    t = pl.program_id(1)
    i = qi_ref[t]
    j = kj_ref[t]
    dim = o_ref.shape[2]

    @pl.when(j == 0)
    def _():
        m_sc[...] = jnp.full_like(m_sc, NEGATIVE)
        acc_sc[...] = jnp.zeros_like(acc_sc)

    def absorb(causal):
        q = q_ref[0]
        k = k_ref[0]
        s = lax.dot_general(q, k, TRANS_B, preferred_element_type=jnp.float32) * scale
        s = jnp.where(_allowed(segq_ref, segk_ref, i, j, tq, tk, causal), s, -jnp.inf)
        m_prev = m_sc[...]
        m_new = jnp.maximum(m_prev, jnp.max(s, axis=1, keepdims=True))
        factor = jnp.exp(m_prev - m_new)
        p = jnp.exp(s - m_new)
        acc_sc[...] = acc_sc[...] * factor + jnp.dot(
            p.astype(jnp.bfloat16), v_ref[0], preferred_element_type=jnp.float32
        )
        m_sc[...] = m_new

    @pl.when(j < i)
    def _():
        absorb(False)

    @pl.when(j == i)
    def _():
        absorb(True)
        acc = acc_sc[...]
        total = acc[:, dim : dim + 1]
        o_ref[0] = acc[:, :dim] / total
        lse_ref[0] = m_sc[...] + jnp.log(total)


def _schedule(count, queries_outer):
    if queries_outer:
        pairs = [(i, j) for i in range(count) for j in range(i + 1)]
    else:
        pairs = [(i, j) for j in range(count) for i in range(j, count)]
    return (
        jnp.asarray([p[0] for p in pairs], jnp.int32),
        jnp.asarray([p[1] for p in pairs], jnp.int32),
    )


def attention_forward(q, k, v, seg, block=512):
    heads, total, dim = q.shape
    count = total // block
    scale = 1.0 / math.sqrt(dim)
    segq = seg.reshape(total, 1)
    segk = seg.reshape(1, total)
    qi, kj = _schedule(count, True)
    steps = qi.shape[0]
    lanes = 2 * dim
    v_ext = jnp.concatenate(
        [v, jnp.ones((heads, total, 1), v.dtype), jnp.zeros((heads, total, lanes - dim - 1), v.dtype)],
        axis=2,
    )

    return pl.pallas_call(
        functools.partial(_fwd_kernel, tq=block, tk=block, scale=scale),
        out_shape=(
            jax.ShapeDtypeStruct((heads, total, dim), jnp.float32),
            jax.ShapeDtypeStruct((heads, total, 1), jnp.float32),
        ),
        grid_spec=pltpu.PrefetchScalarGridSpec(
            num_scalar_prefetch=2,
            grid=(heads, steps),
            in_specs=[
                pl.BlockSpec((1, block, dim), lambda h, t, qi, kj: (h, qi[t], 0)),
                pl.BlockSpec((1, block, dim), lambda h, t, qi, kj: (h, kj[t], 0)),
                pl.BlockSpec((1, block, lanes), lambda h, t, qi, kj: (h, kj[t], 0)),
                pl.BlockSpec((block, 1), lambda h, t, qi, kj: (qi[t], 0)),
                pl.BlockSpec((1, block), lambda h, t, qi, kj: (0, kj[t])),
            ],
            out_specs=[
                pl.BlockSpec((1, block, dim), lambda h, t, qi, kj: (h, qi[t], 0)),
                pl.BlockSpec((1, block, 1), lambda h, t, qi, kj: (h, qi[t], 0)),
            ],
            scratch_shapes=[
                pltpu.VMEM((block, 1), jnp.float32),
                pltpu.VMEM((block, lanes), jnp.float32),
            ],
        ),
        cost_estimate=pl.CostEstimate(
            flops=2 * heads * total * total * dim,
            transcendentals=heads * total * total // 2,
            bytes_accessed=heads * total * dim * 10,
        ),
    )(qi, kj, q, k, v_ext, segq, segk)


def _bwd_kernel(qi_ref, kj_ref, q_ref, k_ref, v_ref, do_ref, lse_ref, delta_ref, segq_ref, segk_ref, dq_ref, dk_ref, dv_ref, *, tq, tk, scale):
    t = pl.program_id(1)
    i = qi_ref[t]
    j = kj_ref[t]

    @pl.when(t == 0)
    def _():
        dq_ref[...] = jnp.zeros_like(dq_ref)

    @pl.when(i == j)
    def _():
        dk_ref[...] = jnp.zeros_like(dk_ref)
        dv_ref[...] = jnp.zeros_like(dv_ref)

    def absorb(causal):
        q = q_ref[0]
        k = k_ref[0]
        do = do_ref[0]
        s = lax.dot_general(q, k, TRANS_B, preferred_element_type=jnp.float32) * scale
        s = jnp.where(_allowed(segq_ref, segk_ref, i, j, tq, tk, causal), s, -jnp.inf)
        p = jnp.exp(s - lse_ref[0])
        dp = lax.dot_general(do, v_ref[0], TRANS_B, preferred_element_type=jnp.float32)
        ds = (p * (dp - delta_ref[0])).astype(jnp.bfloat16)
        dv_ref[0] += lax.dot(p.astype(jnp.bfloat16).T, do, preferred_element_type=jnp.float32)
        dk_ref[0] += lax.dot(ds.T, q, preferred_element_type=jnp.float32) * scale
        rows = pl.ds(pl.multiple_of(i * tq, tq), tq)
        dq_ref[0, rows, :] += lax.dot(ds, k, preferred_element_type=jnp.float32) * scale

    @pl.when(j < i)
    def _():
        absorb(False)

    @pl.when(j == i)
    def _():
        absorb(True)


def attention_backward(q, k, v, do, lse, delta, seg, block=512):
    heads, total, dim = q.shape
    count = total // block
    scale = 1.0 / math.sqrt(dim)
    segq = seg.reshape(total, 1)
    segk = seg.reshape(1, total)
    qi, kj = _schedule(count, False)
    steps = qi.shape[0]

    def q_map(h, t, qi, kj):
        return (h, qi[t], 0)

    def k_map(h, t, qi, kj):
        return (h, kj[t], 0)

    return pl.pallas_call(
        functools.partial(_bwd_kernel, tq=block, tk=block, scale=scale),
        out_shape=(
            jax.ShapeDtypeStruct((heads, total, dim), jnp.float32),
            jax.ShapeDtypeStruct((heads, total, dim), jnp.float32),
            jax.ShapeDtypeStruct((heads, total, dim), jnp.float32),
        ),
        grid_spec=pltpu.PrefetchScalarGridSpec(
            num_scalar_prefetch=2,
            grid=(heads, steps),
            in_specs=[
                pl.BlockSpec((1, block, dim), q_map),
                pl.BlockSpec((1, block, dim), k_map),
                pl.BlockSpec((1, block, dim), k_map),
                pl.BlockSpec((1, block, dim), q_map),
                pl.BlockSpec((1, block, 1), q_map),
                pl.BlockSpec((1, block, 1), q_map),
                pl.BlockSpec((block, 1), lambda h, t, qi, kj: (qi[t], 0)),
                pl.BlockSpec((1, block), lambda h, t, qi, kj: (0, kj[t])),
            ],
            out_specs=[
                pl.BlockSpec((1, total, dim), lambda h, t, qi, kj: (h, 0, 0)),
                pl.BlockSpec((1, block, dim), k_map),
                pl.BlockSpec((1, block, dim), k_map),
            ],
        ),
        cost_estimate=pl.CostEstimate(
            flops=5 * heads * total * total * dim,
            transcendentals=heads * total * total // 2,
            bytes_accessed=heads * total * dim * 24,
        ),
    )(qi, kj, q, k, v, do, lse, delta, segq, segk)


MESH_ID = pl.DeviceIdType.MESH


class Ring:
    def __init__(self, size, a_stride, b_stride):
        self.size = size
        self.half = size // 2
        self.a_stride = a_stride
        self.b_stride = b_stride

    def position(self, c):
        a = (c // self.a_stride) % self.half
        b = (c // self.b_stride) % 2
        return a + b * (2 * self.half - 1 - 2 * a)

    def device(self, pos):
        pos = pos % self.size
        b = pos // self.half
        a = pos + b * (2 * self.half - 1 - 2 * pos)
        return a * self.a_stride + b * self.b_stride


def ring_of(mesh):
    size = mesh.shape["ctx"]
    devices = list(mesh.devices.reshape(-1, size)[0])
    try:
        coords = [tuple(d.coords) for d in devices]
    except AttributeError:
        coords = None
    if coords and size % 2 == 0 and size >= 4:
        for b_stride in range(1, size):
            for a_stride in range(1, size):
                ring = Ring(size, a_stride, b_stride)
                order = [ring.device(p) for p in range(size)]
                if sorted(order) != list(range(size)):
                    continue
                hops = [
                    sum(abs(x - y) for x, y in zip(coords[order[p]], coords[order[(p + 1) % size]]))
                    for p in range(size)
                ]
                if max(hops) == 1:
                    return ring
    return Ring(size, 2, 1) if size % 2 == 0 and size >= 4 else None


def _barrier(g, left, right):
    barrier = pltpu.get_barrier_semaphore()
    for other in (left, right):
        pl.semaphore_signal(barrier, 1, device_id=(g, other), device_id_type=MESH_ID)
    pl.semaphore_wait(barrier, 2)


def _gather_kernel(x_ref, y_ref, own_sem, send_sem, recv_sem, *, ring, rows):
    n = ring.size
    half = rows // 2
    g = lax.axis_index("dp")
    c = lax.axis_index("ctx")
    pos = ring.position(c)
    right = ring.device(pos + 1)
    left = ring.device(pos + n - 1)
    own = pltpu.make_async_copy(x_ref, y_ref.at[pl.ds(c * rows, rows)], own_sem)
    own.start()
    _barrier(g, left, right)

    def link(direction, step, origin, source):
        offset = origin * rows + direction * half
        return pltpu.make_async_remote_copy(
            src_ref=source,
            dst_ref=y_ref.at[pl.ds(offset, half)],
            send_sem=send_sem.at[direction, step],
            recv_sem=recv_sem.at[direction, step],
            device_id=(g, right if direction == 0 else left),
            device_id_type=MESH_ID,
        )

    sent = []
    for step in range(n - 1):
        origins = (ring.device(pos - step + n), ring.device(pos + step))
        for direction in (0, 1):
            origin = origins[direction]
            if step == 0:
                source = x_ref.at[pl.ds(direction * half, half)]
            else:
                link(direction, step - 1, origin, None if False else y_ref.at[pl.ds(origin * rows + direction * half, half)]).wait_recv()
                source = y_ref.at[pl.ds(origin * rows + direction * half, half)]
            copy = link(direction, step, origin, source)
            copy.start()
            sent.append(copy)
    last = n - 2
    for direction, origin in ((0, ring.device(pos - last - 1 + n)), (1, ring.device(pos + last + 1))):
        link(direction, last, origin, y_ref.at[pl.ds(origin * rows + direction * half, half)]).wait_recv()
    for copy in sent:
        copy.wait_send()
    own.wait()


def ring_all_gather(x, ring, collective_id):
    rows, cols = x.shape
    n = ring.size
    return pl.pallas_call(
        functools.partial(_gather_kernel, ring=ring, rows=rows),
        out_shape=jax.ShapeDtypeStruct((n * rows, cols), x.dtype),
        in_specs=[pl.BlockSpec(memory_space=pl.ANY)],
        out_specs=pl.BlockSpec(memory_space=pl.ANY),
        scratch_shapes=[
            pltpu.SemaphoreType.DMA(()),
            pltpu.SemaphoreType.DMA((2, n - 1)),
            pltpu.SemaphoreType.DMA((2, n - 1)),
        ],
        compiler_params=pltpu.CompilerParams(collective_id=collective_id, has_side_effects=True),
    )(x)


def _scatter_kernel(p_ref, out_ref, recv_buf, send_buf, send_sem, recv_sem, *, ring, rows, parts):
    n = ring.size
    half = rows // 2
    piece = half // parts
    g = lax.axis_index("dp")
    c = lax.axis_index("ctx")
    pos = ring.position(c)
    right = ring.device(pos + 1)
    left = ring.device(pos + n - 1)
    _barrier(g, left, right)

    def link(direction, step, part):
        window = pl.ds(part * piece, piece)
        return pltpu.make_async_remote_copy(
            src_ref=send_buf.at[direction, step, window],
            dst_ref=recv_buf.at[direction, step, window],
            send_sem=send_sem.at[direction, step, part],
            recv_sem=recv_sem.at[direction, step, part],
            device_id=(g, right if direction == 0 else left),
            device_id_type=MESH_ID,
        )

    sent = []
    for step in range(n - 1):
        targets = (ring.device(pos - 1 - step + 2 * n), ring.device(pos + 1 + step))
        for part in range(parts):
            for direction in (0, 1):
                start = pl.multiple_of(
                    targets[direction] * rows + direction * half + part * piece, piece
                )
                window = pl.ds(part * piece, piece)
                total = p_ref[pl.ds(start, piece), :].astype(jnp.float32)
                if step > 0:
                    link(direction, step - 1, part).wait_recv()
                    total = total + recv_buf[direction, step - 1, window].astype(jnp.float32)
                send_buf[direction, step, window] = total.astype(send_buf.dtype)
                copy = link(direction, step, part)
                copy.start()
                sent.append(copy)
    for part in range(parts):
        for direction in (0, 1):
            link(direction, n - 2, part).wait_recv()
            start = pl.multiple_of(c * rows + direction * half + part * piece, piece)
            window = pl.ds(part * piece, piece)
            out_ref[pl.ds(direction * half + part * piece, piece), :] = (
                p_ref[pl.ds(start, piece), :].astype(jnp.float32)
                + recv_buf[direction, n - 2, window].astype(jnp.float32)
            ).astype(out_ref.dtype)
    for copy in sent:
        copy.wait_send()


def ring_reduce_scatter(p, ring, collective_id, out_dtype=jnp.float32, wire=jnp.bfloat16, parts=2):
    total_rows, cols = p.shape
    n = ring.size
    rows = total_rows // n
    half = rows // 2
    return pl.pallas_call(
        functools.partial(_scatter_kernel, ring=ring, rows=rows, parts=parts),
        out_shape=jax.ShapeDtypeStruct((rows, cols), out_dtype),
        in_specs=[pl.BlockSpec(memory_space=pltpu.VMEM)],
        out_specs=pl.BlockSpec(memory_space=pltpu.VMEM),
        scratch_shapes=[
            pltpu.VMEM((2, n - 1, half, cols), wire),
            pltpu.VMEM((2, n - 1, half, cols), wire),
            pltpu.SemaphoreType.DMA((2, n - 1, parts)),
            pltpu.SemaphoreType.DMA((2, n - 1, parts)),
        ],
        compiler_params=pltpu.CompilerParams(
            collective_id=collective_id, has_side_effects=True, vmem_limit_bytes=60 * 1024 * 1024
        ),
    )(p)


def _exchange_kernel(x_ref, out_ref, own_sem, send_sem, recv_sem, *, group):
    n = x_ref.shape[0]
    g = lax.axis_index("dp")
    c = lax.axis_index("ctx")
    n_ctx = lax.axis_size("ctx")
    me = {"all": g * n_ctx + c, "ctx": c, "dp": g}[group]

    def address(member):
        if group == "all":
            return (member // n_ctx, member % n_ctx)
        if group == "ctx":
            return (g, member)
        return (member, c)

    own = pltpu.make_async_copy(x_ref.at[me], out_ref.at[me], own_sem)
    own.start()
    barrier = pltpu.get_barrier_semaphore()
    for offset in range(1, n):
        pl.semaphore_signal(
            barrier, 1, device_id=address((me + offset) % n), device_id_type=MESH_ID
        )
    pl.semaphore_wait(barrier, n - 1)

    def link(offset, source, target):
        return pltpu.make_async_remote_copy(
            src_ref=x_ref.at[target],
            dst_ref=out_ref.at[source],
            send_sem=send_sem.at[offset],
            recv_sem=recv_sem.at[offset],
            device_id=address(target),
            device_id_type=MESH_ID,
        )

    sent = []
    for offset in range(1, n):
        copy = link(offset, me, (me + offset) % n)
        copy.start()
        sent.append(copy)
    for offset in range(1, n):
        link(offset, (me + n - offset) % n, me).wait_recv()
    for copy in sent:
        copy.wait_send()
    own.wait()


def exchange(x, group, collective_id):
    n = x.shape[0]
    space = pltpu.VMEM
    return pl.pallas_call(
        functools.partial(_exchange_kernel, group=group),
        out_shape=jax.ShapeDtypeStruct(x.shape, x.dtype),
        in_specs=[pl.BlockSpec(memory_space=space)],
        out_specs=pl.BlockSpec(memory_space=space),
        scratch_shapes=[
            pltpu.SemaphoreType.DMA(()),
            pltpu.SemaphoreType.DMA((n,)),
            pltpu.SemaphoreType.DMA((n,)),
        ],
        compiler_params=pltpu.CompilerParams(collective_id=collective_id, has_side_effects=True),
    )(x)


def block_moves(n_dp, n_ctx):
    count = n_dp * n_ctx
    return [(f, (f % n_dp) * n_ctx + f // n_dp) for f in range(count)]


def fetch_out_rows(w_out):
    n_dp = lax.axis_size("dp")
    n_ctx = lax.axis_size("ctx")
    moved = lax.ppermute(w_out.astype(jnp.bfloat16), ("dp", "ctx"), perm=block_moves(n_dp, n_ctx))
    return lax.all_gather(moved, "dp", axis=0, tiled=True)


def return_out_rows(grad_out_rows):
    n_dp = lax.axis_size("dp")
    n_ctx = lax.axis_size("ctx")
    part = lax.psum_scatter(grad_out_rows, "dp", scatter_dimension=0, tiled=True)
    back = [(b, a) for a, b in block_moves(n_dp, n_ctx)]
    return lax.ppermute(part, ("dp", "ctx"), perm=back)


def pack_rows(vector, lanes):
    size = vector.shape[0]
    total = -(-size // (16 * lanes)) * 16 * lanes
    return jnp.pad(vector, (0, total - size)).reshape(-1, lanes)


def fetch_small(b_qkv, b_out, b_fc2, ln_gain, ln_shift, b_fc1):
    pieces = (b_qkv, b_out, b_fc2, ln_gain, ln_shift, b_fc1)
    n_dp = lax.axis_size("dp")
    n_ctx = lax.axis_size("ctx")
    packed = pack_rows(jnp.concatenate([p.astype(jnp.bfloat16) for p in pieces]), 128)
    over_dp = exchange(jnp.broadcast_to(packed[None], (n_dp,) + packed.shape), "dp", 4)
    over_all = exchange(jnp.broadcast_to(over_dp[None], (n_ctx,) + over_dp.shape), "ctx", 8)
    table = over_all.transpose(1, 0, 2, 3).reshape(n_dp * n_ctx, -1)
    result = []
    offset = 0
    for p in pieces:
        result.append(table[:, offset : offset + p.shape[0]])
        offset += p.shape[0]
    return result


def reduce_small(small):
    n_dp = lax.axis_size("dp")
    n_ctx = lax.axis_size("ctx")
    count, width = small.shape
    packed = jax.vmap(lambda row: pack_rows(row, 128))(small)
    packed = packed.reshape((n_dp, n_ctx) + packed.shape[1:]).transpose(1, 0, 2, 3)
    over_ctx = jnp.sum(exchange(packed, "ctx", 7), axis=0)
    over_dp = jnp.sum(exchange(over_ctx, "dp", 9), axis=0)
    return over_dp.reshape(-1)[:width]


def fetch_heads(w_qkv, w_fc1, w_fc2, tokens):
    dp_count = lax.axis_size("dp")
    ctx_count = lax.axis_size("ctx")
    rows_piece = w_qkv.shape[0]
    head_width = D // ctx_count
    unit = FF // (dp_count * ctx_count)
    qkv_piece = w_qkv.astype(jnp.bfloat16).reshape(rows_piece, 3, ctx_count, head_width)
    fc1_piece = w_fc1.astype(jnp.bfloat16).reshape(rows_piece, dp_count, ctx_count, unit)
    pieces = jnp.concatenate(
        [
            qkv_piece.transpose(2, 0, 1, 3).reshape(ctx_count, rows_piece, 3 * head_width),
            fc1_piece.transpose(2, 0, 1, 3).reshape(ctx_count, rows_piece, dp_count * unit),
        ],
        axis=2,
    )
    sent = exchange(pieces, "ctx", 5).reshape(ctx_count * rows_piece, -1)
    sent, tokens = lax.optimization_barrier((sent, tokens))
    cols, fc2_rows = (
        lax.all_gather(sent, "dp", axis=0, tiled=True),
        lax.all_gather(w_fc2.astype(jnp.bfloat16), "dp", axis=0, tiled=True),
    )
    return (cols, fc2_rows, tokens)


def return_heads(owned_parts):
    dp_count = lax.axis_size("dp")
    ctx_count = lax.axis_size("ctx")
    head_width = D // ctx_count
    unit = FF // (dp_count * ctx_count)
    rows_piece = owned_parts.shape[0] // ctx_count
    got = exchange(owned_parts.reshape(ctx_count, rows_piece, -1), "ctx", 6)
    qkv = got[:, :, : 3 * head_width].reshape(ctx_count, rows_piece, 3, head_width)
    fc1 = got[:, :, 3 * head_width :].reshape(ctx_count, rows_piece, dp_count, unit)
    return (
        qkv.transpose(1, 2, 0, 3).reshape(rows_piece, 3 * D).astype(jnp.float32),
        fc1.transpose(1, 2, 0, 3).reshape(rows_piece, FF).astype(jnp.float32),
    )


def head_plan(
    ring,
    tokens,
    lengths,
    w_qkv,
    b_qkv,
    w_out,
    b_out,
    w_fc1,
    b_fc1,
    w_fc2,
    b_fc2,
    ln_gain,
    ln_shift,
    cotangent,
):
    rows_here = tokens.shape[0]
    rows_piece = w_qkv.shape[0]
    dp_count = lax.axis_size("dp")
    ctx_count = lax.axis_size("ctx")
    count = dp_count * ctx_count
    group = rows_here * ctx_count
    head_width = D // ctx_count
    local_heads = HEADS // ctx_count
    unit = FF // (dp_count * ctx_count)
    here = lax.axis_index("ctx")
    group_rows = jnp.arange(group, dtype=jnp.int32)
    seg, positions = segment_info(lengths[0], group_rows)
    cosine, sine = rotary_tables(positions)
    qkv_bias, out_bias, fc2_bias, gain_low, shift_low, fc1_table = fetch_small(
        b_qkv, b_out, b_fc2, ln_gain, ln_shift, b_fc1
    )
    qkv_bias = qkv_bias.reshape(3 * D)
    out_bias = out_bias.reshape(D)
    fc2_bias = fc2_bias.reshape(D)
    gain_low = gain_low.reshape(D)
    shift_low = shift_low.reshape(D)
    fc1_bias = lax.dynamic_index_in_dim(
        fc1_table.reshape(dp_count, ctx_count, unit), here, 1, keepdims=False
    ).reshape(dp_count * unit)
    out_rows = fetch_out_rows(w_out)
    cols, fc2_rows, tokens = fetch_heads(w_qkv, w_fc1, w_fc2, tokens)
    gain32 = gain_low.astype(jnp.float32)
    shift32 = shift_low.astype(jnp.float32)
    inputs = tokens.astype(jnp.float32)
    normed, scaled, _ = norm_parts(inputs, gain32, shift32)
    tokens_group = ring_all_gather(tokens, ring, 0)
    late_dy, tokens_group = lax.optimization_barrier((cotangent, tokens_group))
    dy_group = lax.all_gather(late_dy, "ctx", axis=0, tiled=True)
    hidden_group = norm_parts(tokens_group.astype(jnp.float32), gain32, shift32)[2].astype(
        jnp.bfloat16
    )
    bias_cols = lax.dynamic_slice_in_dim(
        qkv_bias.reshape(3, D), here * head_width, head_width, 1
    ).reshape(3 * head_width)
    both = jnp.dot(hidden_group, cols, preferred_element_type=jnp.float32) + jnp.concatenate(
        [bias_cols, fc1_bias]
    ).astype(jnp.float32)
    qkv = both[:, : 3 * head_width]
    pre = both[:, 3 * head_width :]
    shape = (group, local_heads, HEAD_DIM)
    query = rotate(qkv[:, :head_width].reshape(shape), cosine, sine).astype(jnp.bfloat16)
    keys = rotate(qkv[:, head_width : 2 * head_width].reshape(shape), cosine, sine).astype(
        jnp.bfloat16
    )
    values = qkv[:, 2 * head_width :].reshape(shape).astype(jnp.bfloat16)
    q_heads = query.transpose(1, 0, 2)
    k_heads = keys.transpose(1, 0, 2)
    v_heads = values.transpose(1, 0, 2)
    attended_heads, log_total = attention_forward(q_heads, k_heads, v_heads, seg)
    attended = attended_heads.transpose(1, 0, 2).reshape(group, head_width).astype(jnp.bfloat16)
    act = gelu_tanh(pre).astype(jnp.bfloat16)
    branches = ring_reduce_scatter(
        jnp.dot(attended, out_rows, preferred_element_type=jnp.float32)
        + jnp.dot(act, fc2_rows, preferred_element_type=jnp.float32),
        ring,
        2,
    )
    block_out = (
        inputs + branches + out_bias.astype(jnp.float32) + fc2_bias.astype(jnp.float32)
    ).astype(jnp.bfloat16)
    grad_out32 = cotangent.astype(jnp.float32)
    grad_b_fc2 = jnp.sum(grad_out32, axis=0)
    grad_fc2_part = jnp.einsum("tf,td->fd", act, dy_group, preferred_element_type=jnp.float32)
    d_act = jnp.einsum("td,fd->tf", dy_group, fc2_rows, preferred_element_type=jnp.float32)
    d_pre = (d_act * gelu_slope(pre)).astype(jnp.bfloat16)
    grad_bfc1_part = jnp.sum(d_pre.astype(jnp.float32), axis=0)
    grad_out_rows = jnp.einsum("tc,td->cd", attended, dy_group, preferred_element_type=jnp.float32)
    owned_w_out = return_out_rows(grad_out_rows)
    d_attended = (
        jnp.einsum("td,cd->tc", dy_group, out_rows, preferred_element_type=jnp.float32)
        .astype(jnp.bfloat16)
        .reshape(shape)
    )
    d_heads = d_attended.transpose(1, 0, 2)
    delta = jnp.sum(d_heads.astype(jnp.float32) * attended_heads, axis=2, keepdims=True)
    dq_heads, dk_heads, dv_heads = attention_backward(
        q_heads, k_heads, v_heads, d_heads, log_total, delta, seg
    )
    d_query = dq_heads.transpose(1, 0, 2)
    d_keys = dk_heads.transpose(1, 0, 2)
    d_values = dv_heads.transpose(1, 0, 2)
    d_query = rotate_back(d_query, cosine, sine).reshape(group, head_width)
    d_keys = rotate_back(d_keys, cosine, sine).reshape(group, head_width)
    d_qkv = jnp.concatenate([d_query, d_keys, d_values.reshape(group, head_width)], axis=1).astype(
        jnp.bfloat16
    )
    d_both = jnp.concatenate([d_qkv, d_pre], axis=1)
    bias_part = jnp.sum(d_qkv.astype(jnp.float32), axis=0).reshape(3, head_width)
    d_hidden = ring_reduce_scatter(
        jnp.einsum("tc,dc->td", d_both, cols, preferred_element_type=jnp.float32), ring, 3
    )
    weight_parts = jnp.einsum(
        "td,tc->dc", hidden_group, d_both, preferred_element_type=jnp.float32
    ).astype(jnp.bfloat16)
    owned_parts = lax.psum_scatter(weight_parts, "dp", scatter_dimension=0, tiled=True)
    split_qkv, split_fc1 = return_heads(owned_parts)
    d_hidden, split_qkv, split_fc1 = lax.optimization_barrier((d_hidden, split_qkv, split_fc1))
    grad_gain, grad_shift, d_inputs = norm_back(d_hidden, normed, scaled, gain32)
    grad_tokens = (grad_out32 + d_inputs).astype(jnp.bfloat16)
    owned_fc2 = lax.psum_scatter(
        grad_fc2_part.astype(jnp.bfloat16), "dp", scatter_dimension=0, tiled=True
    ).astype(jnp.float32)
    full_bqkv = lax.dynamic_update_slice_in_dim(
        jnp.zeros((3, D), jnp.float32), bias_part, here * head_width, 1
    )
    full_bfc1 = lax.dynamic_update_slice_in_dim(
        jnp.zeros((dp_count, ctx_count, unit), jnp.float32),
        grad_bfc1_part.reshape(dp_count, 1, unit),
        here,
        1,
    )
    small = jnp.concatenate(
        [
            full_bqkv.reshape(count, -1),
            grad_b_fc2.reshape(count, -1),
            grad_gain.reshape(count, -1),
            grad_shift.reshape(count, -1),
            full_bfc1.reshape(count, -1),
        ],
        axis=1,
    )
    owned_small = reduce_small(small)
    cuts = [0, 3 * D // count, D // count, D // count, D // count, FF // count]
    bounds = [sum(cuts[: i + 1]) for i in range(len(cuts))]
    owned_bqkv, owned_bout, owned_gain, owned_shift, owned_bfc1 = [
        owned_small[bounds[i] : bounds[i + 1]] for i in range(5)
    ]
    return (
        block_out,
        grad_tokens,
        split_qkv.reshape(rows_piece, 3 * D),
        owned_bqkv,
        owned_w_out,
        owned_bout,
        split_fc1.reshape(rows_piece, FF),
        owned_bfc1,
        owned_fc2,
        owned_bout,
        owned_gain,
        owned_shift,
    )


def body(
    ring,
    tokens,
    lengths,
    w_qkv,
    b_qkv,
    w_out,
    b_out,
    w_fc1,
    b_fc1,
    w_fc2,
    b_fc2,
    ln_gain,
    ln_shift,
    cotangent,
):
    return head_plan(
        ring,
        tokens,
        lengths,
        w_qkv,
        b_qkv,
        w_out,
        b_out,
        w_fc1,
        b_fc1,
        w_fc2,
        b_fc2,
        ln_gain,
        ln_shift,
        cotangent,
    )


def solution(mesh):
    in_specs = (
        P(("dp", "ctx"), None),
        P("dp", None),
        P(("dp", "ctx"), None),
        P(("dp", "ctx")),
        P(("dp", "ctx"), None),
        P(("dp", "ctx")),
        P(("dp", "ctx"), None),
        P(("dp", "ctx")),
        P(("dp", "ctx"), None),
        P(("dp", "ctx")),
        P(("dp", "ctx")),
        P(("dp", "ctx")),
        P(("dp", "ctx"), None),
    )
    out_specs = (
        P(("dp", "ctx"), None),
        P(("dp", "ctx"), None),
        P(("dp", "ctx"), None),
        P(("dp", "ctx")),
        P(("dp", "ctx"), None),
        P(("dp", "ctx")),
        P(("dp", "ctx"), None),
        P(("dp", "ctx")),
        P(("dp", "ctx"), None),
        P(("dp", "ctx")),
        P(("dp", "ctx")),
        P(("dp", "ctx")),
    )
    ring = ring_of(mesh)
    return jax.shard_map(functools.partial(body, ring), mesh=mesh, in_specs=in_specs, out_specs=out_specs, check_vma=False)
```

```python
import functools
import math

import jax
import jax.numpy as jnp
from jax import lax
from jax.experimental import pallas as pl
from jax.experimental.pallas import tpu as pltpu
from jax.sharding import PartitionSpec as P

D = 2048
HEADS = 32
HEAD_DIM = 64
ROT = 32
FF = 8192


EPS = 1e-05
GELU_COEF = math.sqrt(2.0 / math.pi)
NEGATIVE = -1e30


def norm_parts(inputs, gain, shift):
    mean = jnp.mean(inputs, axis=-1, keepdims=True)
    centred = inputs - mean
    var = jnp.mean(centred * centred, axis=-1, keepdims=True)
    scaled = lax.rsqrt(var + EPS)
    normed = centred * scaled
    return (normed, scaled, normed * gain + shift)


def norm_back(d_hidden, normed, scaled, gain32):
    grad_gain = jnp.sum(d_hidden * normed, axis=0)
    grad_shift = jnp.sum(d_hidden, axis=0)
    d_normed = d_hidden * gain32
    d_inputs = scaled * (
        d_normed
        - jnp.mean(d_normed, axis=-1, keepdims=True)
        - normed * jnp.mean(d_normed * normed, axis=-1, keepdims=True)
    )
    return (grad_gain, grad_shift, d_inputs)


def gelu_tanh(pre):
    return 0.5 * pre * (1.0 + jnp.tanh(GELU_COEF * (pre + 0.044715 * pre * pre * pre)))


def gelu_slope(pre):
    tangent = jnp.tanh(GELU_COEF * (pre + 0.044715 * pre * pre * pre))
    return 0.5 * (1.0 + tangent) + 0.5 * pre * (1.0 - tangent * tangent) * GELU_COEF * (
        1.0 + 3.0 * 0.044715 * pre * pre
    )


def rotary_tables(positions):
    half = ROT // 2
    freq = jnp.exp(jnp.arange(half, dtype=jnp.float32) * (-2.0 * math.log(10000.0) / ROT))
    angle = positions.astype(jnp.float32)[:, None] * freq[None, :]
    return (jnp.cos(angle)[:, None, :], jnp.sin(angle)[:, None, :])


def rotate(heads, cosine, sine):
    half = ROT // 2
    first = heads[..., :half]
    second = heads[..., half:ROT]
    return jnp.concatenate(
        [first * cosine - second * sine, second * cosine + first * sine, heads[..., ROT:]], axis=-1
    )


def rotate_back(grads, cosine, sine):
    half = ROT // 2
    first = grads[..., :half]
    second = grads[..., half:ROT]
    return jnp.concatenate(
        [first * cosine + second * sine, second * cosine - first * sine, grads[..., ROT:]], axis=-1
    )


def segment_info(lengths_row, rows):
    ends = jnp.cumsum(lengths_row)
    starts = ends - lengths_row
    seg = jnp.sum((rows[:, None] >= ends[None, :]).astype(jnp.int32), axis=1)
    onehot = seg[:, None] == jnp.arange(lengths_row.shape[0], dtype=jnp.int32)[None, :]
    first_rows = jnp.sum(jnp.where(onehot, starts[None, :], 0), axis=1)
    return (seg, rows - first_rows)


TRANS_B = (((1,), (1,)), ((), ()))


def _allowed(segq_ref, segk_ref, i, j, tq, tk, causal):
    same = segq_ref[...] == segk_ref[...]
    if not causal:
        return same
    rows = i * tq + lax.broadcasted_iota(jnp.int32, (tq, tk), 0)
    cols = j * tk + lax.broadcasted_iota(jnp.int32, (tq, tk), 1)
    return same & (cols <= rows)


def _fwd_kernel(qi_ref, kj_ref, q_ref, k_ref, v_ref, segq_ref, segk_ref, o_ref, lse_ref, m_sc, acc_sc, *, tq, tk, scale):
    t = pl.program_id(1)
    i = qi_ref[t]
    j = kj_ref[t]
    dim = o_ref.shape[2]

    @pl.when(j == 0)
    def _():
        m_sc[...] = jnp.full_like(m_sc, NEGATIVE)
        acc_sc[...] = jnp.zeros_like(acc_sc)

    def absorb(causal):
        q = q_ref[0]
        k = k_ref[0]
        s = lax.dot_general(q, k, TRANS_B, preferred_element_type=jnp.float32) * scale
        s = jnp.where(_allowed(segq_ref, segk_ref, i, j, tq, tk, causal), s, -jnp.inf)
        m_prev = m_sc[...]
        m_new = jnp.maximum(m_prev, jnp.max(s, axis=1, keepdims=True))
        factor = jnp.exp(m_prev - m_new)
        p = jnp.exp(s - m_new)
        acc_sc[...] = acc_sc[...] * factor + jnp.dot(
            p.astype(jnp.bfloat16), v_ref[0], preferred_element_type=jnp.float32
        )
        m_sc[...] = m_new

    @pl.when(j < i)
    def _():
        absorb(False)

    @pl.when(j == i)
    def _():
        absorb(True)
        acc = acc_sc[...]
        total = acc[:, dim : dim + 1]
        o_ref[0] = acc[:, :dim] / total
        lse_ref[0] = m_sc[...] + jnp.log(total)


def _schedule(count, queries_outer):
    if queries_outer:
        pairs = [(i, j) for i in range(count) for j in range(i + 1)]
    else:
        pairs = [(i, j) for j in range(count) for i in range(j, count)]
    return (
        jnp.asarray([p[0] for p in pairs], jnp.int32),
        jnp.asarray([p[1] for p in pairs], jnp.int32),
    )


def attention_forward(q, k, v, seg, block=512):
    heads, total, dim = q.shape
    count = total // block
    scale = 1.0 / math.sqrt(dim)
    segq = seg.reshape(total, 1)
    segk = seg.reshape(1, total)
    qi, kj = _schedule(count, True)
    steps = qi.shape[0]
    lanes = 2 * dim
    v_ext = jnp.concatenate(
        [v, jnp.ones((heads, total, 1), v.dtype), jnp.zeros((heads, total, lanes - dim - 1), v.dtype)],
        axis=2,
    )

    return pl.pallas_call(
        functools.partial(_fwd_kernel, tq=block, tk=block, scale=scale),
        out_shape=(
            jax.ShapeDtypeStruct((heads, total, dim), jnp.float32),
            jax.ShapeDtypeStruct((heads, total, 1), jnp.float32),
        ),
        grid_spec=pltpu.PrefetchScalarGridSpec(
            num_scalar_prefetch=2,
            grid=(heads, steps),
            in_specs=[
                pl.BlockSpec((1, block, dim), lambda h, t, qi, kj: (h, qi[t], 0)),
                pl.BlockSpec((1, block, dim), lambda h, t, qi, kj: (h, kj[t], 0)),
                pl.BlockSpec((1, block, lanes), lambda h, t, qi, kj: (h, kj[t], 0)),
                pl.BlockSpec((block, 1), lambda h, t, qi, kj: (qi[t], 0)),
                pl.BlockSpec((1, block), lambda h, t, qi, kj: (0, kj[t])),
            ],
            out_specs=[
                pl.BlockSpec((1, block, dim), lambda h, t, qi, kj: (h, qi[t], 0)),
                pl.BlockSpec((1, block, 1), lambda h, t, qi, kj: (h, qi[t], 0)),
            ],
            scratch_shapes=[
                pltpu.VMEM((block, 1), jnp.float32),
                pltpu.VMEM((block, lanes), jnp.float32),
            ],
        ),
        cost_estimate=pl.CostEstimate(
            flops=2 * heads * total * total * dim,
            transcendentals=heads * total * total // 2,
            bytes_accessed=heads * total * dim * 10,
        ),
    )(qi, kj, q, k, v_ext, segq, segk)


def _bwd_kernel(qi_ref, kj_ref, q_ref, k_ref, v_ref, do_ref, lse_ref, delta_ref, segq_ref, segk_ref, dq_ref, dk_ref, dv_ref, dk_sc, dv_sc, *, tq, tk, scale, count):
    t = pl.program_id(1)
    i = qi_ref[t]
    j = kj_ref[t]

    @pl.when(t == 0)
    def _():
        dq_ref[...] = jnp.zeros_like(dq_ref)

    @pl.when(i == j)
    def _():
        dk_sc[...] = jnp.zeros_like(dk_sc)
        dv_sc[...] = jnp.zeros_like(dv_sc)

    def absorb(causal):
        q = q_ref[0]
        k = k_ref[0]
        do = do_ref[0]
        s = lax.dot_general(q, k, TRANS_B, preferred_element_type=jnp.float32) * scale
        s = jnp.where(_allowed(segq_ref, segk_ref, i, j, tq, tk, causal), s, -jnp.inf)
        p = jnp.exp(s - lse_ref[0])
        dp = lax.dot_general(do, v_ref[0], TRANS_B, preferred_element_type=jnp.float32)
        ds = (p * (dp - delta_ref[0])).astype(jnp.bfloat16)
        dv_sc[...] += jnp.dot(do.T, p.astype(jnp.bfloat16), preferred_element_type=jnp.float32)
        dk_sc[...] += jnp.dot(q.T, ds, preferred_element_type=jnp.float32)
        rows = pl.ds(pl.multiple_of(i * tq, tq), tq)
        dq_ref[0, rows, :] += lax.dot(ds, k, preferred_element_type=jnp.float32) * scale

    @pl.when(j < i)
    def _():
        absorb(False)

    @pl.when(j == i)
    def _():
        absorb(True)

    @pl.when(i == count - 1)
    def _():
        dk_ref[0] = dk_sc[...].T * scale
        dv_ref[0] = dv_sc[...].T


def attention_backward(q, k, v, do, lse, delta, seg, block=512):
    heads, total, dim = q.shape
    count = total // block
    scale = 1.0 / math.sqrt(dim)
    segq = seg.reshape(total, 1)
    segk = seg.reshape(1, total)
    qi, kj = _schedule(count, False)
    steps = qi.shape[0]

    def q_map(h, t, qi, kj):
        return (h, qi[t], 0)

    def k_map(h, t, qi, kj):
        return (h, kj[t], 0)

    return pl.pallas_call(
        functools.partial(_bwd_kernel, tq=block, tk=block, scale=scale, count=count),
        out_shape=(
            jax.ShapeDtypeStruct((heads, total, dim), jnp.float32),
            jax.ShapeDtypeStruct((heads, total, dim), jnp.float32),
            jax.ShapeDtypeStruct((heads, total, dim), jnp.float32),
        ),
        grid_spec=pltpu.PrefetchScalarGridSpec(
            num_scalar_prefetch=2,
            grid=(heads, steps),
            in_specs=[
                pl.BlockSpec((1, block, dim), q_map),
                pl.BlockSpec((1, block, dim), k_map),
                pl.BlockSpec((1, block, dim), k_map),
                pl.BlockSpec((1, block, dim), q_map),
                pl.BlockSpec((1, block, 1), q_map),
                pl.BlockSpec((1, block, 1), q_map),
                pl.BlockSpec((block, 1), lambda h, t, qi, kj: (qi[t], 0)),
                pl.BlockSpec((1, block), lambda h, t, qi, kj: (0, kj[t])),
            ],
            out_specs=[
                pl.BlockSpec((1, total, dim), lambda h, t, qi, kj: (h, 0, 0)),
                pl.BlockSpec((1, block, dim), k_map),
                pl.BlockSpec((1, block, dim), k_map),
            ],
            scratch_shapes=[
                pltpu.VMEM((dim, block), jnp.float32),
                pltpu.VMEM((dim, block), jnp.float32),
            ],
        ),
        cost_estimate=pl.CostEstimate(
            flops=5 * heads * total * total * dim,
            transcendentals=heads * total * total // 2,
            bytes_accessed=heads * total * dim * 24,
        ),
    )(qi, kj, q, k, v, do, lse, delta, segq, segk)


MESH_ID = pl.DeviceIdType.MESH


class Ring:
    def __init__(self, size, a_stride, b_stride):
        self.size = size
        self.half = size // 2
        self.a_stride = a_stride
        self.b_stride = b_stride

    def position(self, c):
        a = (c // self.a_stride) % self.half
        b = (c // self.b_stride) % 2
        return a + b * (2 * self.half - 1 - 2 * a)

    def device(self, pos):
        pos = pos % self.size
        b = pos // self.half
        a = pos + b * (2 * self.half - 1 - 2 * pos)
        return a * self.a_stride + b * self.b_stride


def ring_of(mesh):
    size = mesh.shape["ctx"]
    devices = list(mesh.devices.reshape(-1, size)[0])
    try:
        coords = [tuple(d.coords) for d in devices]
    except AttributeError:
        coords = None
    if coords and size % 2 == 0 and size >= 4:
        for b_stride in range(1, size):
            for a_stride in range(1, size):
                ring = Ring(size, a_stride, b_stride)
                order = [ring.device(p) for p in range(size)]
                if sorted(order) != list(range(size)):
                    continue
                hops = [
                    sum(abs(x - y) for x, y in zip(coords[order[p]], coords[order[(p + 1) % size]]))
                    for p in range(size)
                ]
                if max(hops) == 1:
                    return ring
    return Ring(size, 2, 1) if size % 2 == 0 and size >= 4 else None


def _barrier(g, left, right):
    barrier = pltpu.get_barrier_semaphore()
    for other in (left, right):
        pl.semaphore_signal(barrier, 1, device_id=(g, other), device_id_type=MESH_ID)
    pl.semaphore_wait(barrier, 2)


def _gather_kernel(x_ref, y_ref, own_sem, send_sem, recv_sem, *, ring, rows):
    n = ring.size
    half = rows // 2
    g = lax.axis_index("dp")
    c = lax.axis_index("ctx")
    pos = ring.position(c)
    right = ring.device(pos + 1)
    left = ring.device(pos + n - 1)
    own = pltpu.make_async_copy(x_ref, y_ref.at[pl.ds(c * rows, rows)], own_sem)
    own.start()
    _barrier(g, left, right)

    def link(direction, step, origin, source):
        offset = origin * rows + direction * half
        return pltpu.make_async_remote_copy(
            src_ref=source,
            dst_ref=y_ref.at[pl.ds(offset, half)],
            send_sem=send_sem.at[direction, step],
            recv_sem=recv_sem.at[direction, step],
            device_id=(g, right if direction == 0 else left),
            device_id_type=MESH_ID,
        )

    sent = []
    for step in range(n - 1):
        origins = (ring.device(pos - step + n), ring.device(pos + step))
        for direction in (0, 1):
            origin = origins[direction]
            if step == 0:
                source = x_ref.at[pl.ds(direction * half, half)]
            else:
                link(direction, step - 1, origin, None if False else y_ref.at[pl.ds(origin * rows + direction * half, half)]).wait_recv()
                source = y_ref.at[pl.ds(origin * rows + direction * half, half)]
            copy = link(direction, step, origin, source)
            copy.start()
            sent.append(copy)
    last = n - 2
    for direction, origin in ((0, ring.device(pos - last - 1 + n)), (1, ring.device(pos + last + 1))):
        link(direction, last, origin, y_ref.at[pl.ds(origin * rows + direction * half, half)]).wait_recv()
    for copy in sent:
        copy.wait_send()
    own.wait()


def ring_all_gather(x, ring, collective_id):
    rows, cols = x.shape
    n = ring.size
    return pl.pallas_call(
        functools.partial(_gather_kernel, ring=ring, rows=rows),
        out_shape=jax.ShapeDtypeStruct((n * rows, cols), x.dtype),
        in_specs=[pl.BlockSpec(memory_space=pl.ANY)],
        out_specs=pl.BlockSpec(memory_space=pl.ANY),
        scratch_shapes=[
            pltpu.SemaphoreType.DMA(()),
            pltpu.SemaphoreType.DMA((2, n - 1)),
            pltpu.SemaphoreType.DMA((2, n - 1)),
        ],
        compiler_params=pltpu.CompilerParams(collective_id=collective_id, has_side_effects=True),
    )(x)


def _scatter_kernel(p_ref, out_ref, recv_buf, send_buf, send_sem, recv_sem, *, ring, rows, parts):
    n = ring.size
    half = rows // 2
    piece = half // parts
    g = lax.axis_index("dp")
    c = lax.axis_index("ctx")
    pos = ring.position(c)
    right = ring.device(pos + 1)
    left = ring.device(pos + n - 1)
    _barrier(g, left, right)

    def link(direction, step, part):
        window = pl.ds(part * piece, piece)
        return pltpu.make_async_remote_copy(
            src_ref=send_buf.at[direction, step, window],
            dst_ref=recv_buf.at[direction, step, window],
            send_sem=send_sem.at[direction, step, part],
            recv_sem=recv_sem.at[direction, step, part],
            device_id=(g, right if direction == 0 else left),
            device_id_type=MESH_ID,
        )

    sent = []
    for step in range(n - 1):
        targets = (ring.device(pos - 1 - step + 2 * n), ring.device(pos + 1 + step))
        for part in range(parts):
            for direction in (0, 1):
                start = pl.multiple_of(
                    targets[direction] * rows + direction * half + part * piece, piece
                )
                window = pl.ds(part * piece, piece)
                total = p_ref[pl.ds(start, piece), :].astype(jnp.float32)
                if step > 0:
                    link(direction, step - 1, part).wait_recv()
                    total = total + recv_buf[direction, step - 1, window].astype(jnp.float32)
                send_buf[direction, step, window] = total.astype(send_buf.dtype)
                copy = link(direction, step, part)
                copy.start()
                sent.append(copy)
    for part in range(parts):
        for direction in (0, 1):
            link(direction, n - 2, part).wait_recv()
            start = pl.multiple_of(c * rows + direction * half + part * piece, piece)
            window = pl.ds(part * piece, piece)
            out_ref[pl.ds(direction * half + part * piece, piece), :] = (
                p_ref[pl.ds(start, piece), :].astype(jnp.float32)
                + recv_buf[direction, n - 2, window].astype(jnp.float32)
            ).astype(out_ref.dtype)
    for copy in sent:
        copy.wait_send()


def ring_reduce_scatter(p, ring, collective_id, out_dtype=jnp.float32, wire=jnp.bfloat16, parts=2):
    total_rows, cols = p.shape
    n = ring.size
    rows = total_rows // n
    half = rows // 2
    return pl.pallas_call(
        functools.partial(_scatter_kernel, ring=ring, rows=rows, parts=parts),
        out_shape=jax.ShapeDtypeStruct((rows, cols), out_dtype),
        in_specs=[pl.BlockSpec(memory_space=pltpu.VMEM)],
        out_specs=pl.BlockSpec(memory_space=pltpu.VMEM),
        scratch_shapes=[
            pltpu.VMEM((2, n - 1, half, cols), wire),
            pltpu.VMEM((2, n - 1, half, cols), wire),
            pltpu.SemaphoreType.DMA((2, n - 1, parts)),
            pltpu.SemaphoreType.DMA((2, n - 1, parts)),
        ],
        compiler_params=pltpu.CompilerParams(
            collective_id=collective_id, has_side_effects=True, vmem_limit_bytes=60 * 1024 * 1024
        ),
    )(p)


def _exchange_kernel(x_ref, out_ref, own_sem, send_sem, recv_sem, *, group):
    n = x_ref.shape[0]
    g = lax.axis_index("dp")
    c = lax.axis_index("ctx")
    n_ctx = lax.axis_size("ctx")
    me = {"all": g * n_ctx + c, "ctx": c, "dp": g}[group]

    def address(member):
        if group == "all":
            return (member // n_ctx, member % n_ctx)
        if group == "ctx":
            return (g, member)
        return (member, c)

    own = pltpu.make_async_copy(x_ref.at[me], out_ref.at[me], own_sem)
    own.start()
    barrier = pltpu.get_barrier_semaphore()
    for offset in range(1, n):
        pl.semaphore_signal(
            barrier, 1, device_id=address((me + offset) % n), device_id_type=MESH_ID
        )
    pl.semaphore_wait(barrier, n - 1)

    def link(offset, source, target):
        return pltpu.make_async_remote_copy(
            src_ref=x_ref.at[target],
            dst_ref=out_ref.at[source],
            send_sem=send_sem.at[offset],
            recv_sem=recv_sem.at[offset],
            device_id=address(target),
            device_id_type=MESH_ID,
        )

    sent = []
    for offset in range(1, n):
        copy = link(offset, me, (me + offset) % n)
        copy.start()
        sent.append(copy)
    for offset in range(1, n):
        link(offset, (me + n - offset) % n, me).wait_recv()
    for copy in sent:
        copy.wait_send()
    own.wait()


def exchange(x, group, collective_id):
    n = x.shape[0]
    space = pltpu.VMEM
    return pl.pallas_call(
        functools.partial(_exchange_kernel, group=group),
        out_shape=jax.ShapeDtypeStruct(x.shape, x.dtype),
        in_specs=[pl.BlockSpec(memory_space=space)],
        out_specs=pl.BlockSpec(memory_space=space),
        scratch_shapes=[
            pltpu.SemaphoreType.DMA(()),
            pltpu.SemaphoreType.DMA((n,)),
            pltpu.SemaphoreType.DMA((n,)),
        ],
        compiler_params=pltpu.CompilerParams(collective_id=collective_id, has_side_effects=True),
    )(x)


def block_moves(n_dp, n_ctx):
    count = n_dp * n_ctx
    return [(f, (f % n_dp) * n_ctx + f // n_dp) for f in range(count)]


def fetch_out_rows(w_out):
    n_dp = lax.axis_size("dp")
    n_ctx = lax.axis_size("ctx")
    moved = lax.ppermute(w_out.astype(jnp.bfloat16), ("dp", "ctx"), perm=block_moves(n_dp, n_ctx))
    return lax.all_gather(moved, "dp", axis=0, tiled=True)


def return_out_rows(grad_out_rows):
    n_dp = lax.axis_size("dp")
    n_ctx = lax.axis_size("ctx")
    part = lax.psum_scatter(grad_out_rows, "dp", scatter_dimension=0, tiled=True)
    back = [(b, a) for a, b in block_moves(n_dp, n_ctx)]
    return lax.ppermute(part, ("dp", "ctx"), perm=back)


def pack_rows(vector, lanes):
    size = vector.shape[0]
    total = -(-size // (16 * lanes)) * 16 * lanes
    return jnp.pad(vector, (0, total - size)).reshape(-1, lanes)


def fetch_small(b_qkv, b_out, b_fc2, ln_gain, ln_shift, b_fc1):
    pieces = (b_qkv, b_out, b_fc2, ln_gain, ln_shift, b_fc1)
    n_dp = lax.axis_size("dp")
    n_ctx = lax.axis_size("ctx")
    packed = pack_rows(jnp.concatenate([p.astype(jnp.bfloat16) for p in pieces]), 128)
    over_dp = exchange(jnp.broadcast_to(packed[None], (n_dp,) + packed.shape), "dp", 4)
    over_all = exchange(jnp.broadcast_to(over_dp[None], (n_ctx,) + over_dp.shape), "ctx", 8)
    table = over_all.transpose(1, 0, 2, 3).reshape(n_dp * n_ctx, -1)
    result = []
    offset = 0
    for p in pieces:
        result.append(table[:, offset : offset + p.shape[0]])
        offset += p.shape[0]
    return result


def reduce_small(small):
    n_dp = lax.axis_size("dp")
    n_ctx = lax.axis_size("ctx")
    count, width = small.shape
    packed = jax.vmap(lambda row: pack_rows(row, 128))(small)
    packed = packed.reshape((n_dp, n_ctx) + packed.shape[1:]).transpose(1, 0, 2, 3)
    over_ctx = jnp.sum(exchange(packed, "ctx", 7), axis=0)
    over_dp = jnp.sum(exchange(over_ctx, "dp", 9), axis=0)
    return over_dp.reshape(-1)[:width]


def fetch_heads(w_qkv, w_fc1, w_fc2, tokens):
    dp_count = lax.axis_size("dp")
    ctx_count = lax.axis_size("ctx")
    rows_piece = w_qkv.shape[0]
    head_width = D // ctx_count
    unit = FF // (dp_count * ctx_count)
    qkv_piece = w_qkv.astype(jnp.bfloat16).reshape(rows_piece, 3, ctx_count, head_width)
    fc1_piece = w_fc1.astype(jnp.bfloat16).reshape(rows_piece, dp_count, ctx_count, unit)
    pieces = jnp.concatenate(
        [
            qkv_piece.transpose(2, 0, 1, 3).reshape(ctx_count, rows_piece, 3 * head_width),
            fc1_piece.transpose(2, 0, 1, 3).reshape(ctx_count, rows_piece, dp_count * unit),
        ],
        axis=2,
    )
    sent = exchange(pieces, "ctx", 5).reshape(ctx_count * rows_piece, -1)
    sent, tokens = lax.optimization_barrier((sent, tokens))
    cols, fc2_rows = (
        lax.all_gather(sent, "dp", axis=0, tiled=True),
        lax.all_gather(w_fc2.astype(jnp.bfloat16), "dp", axis=0, tiled=True),
    )
    return (cols, fc2_rows, tokens)


def return_heads(owned_parts):
    dp_count = lax.axis_size("dp")
    ctx_count = lax.axis_size("ctx")
    head_width = D // ctx_count
    unit = FF // (dp_count * ctx_count)
    rows_piece = owned_parts.shape[0] // ctx_count
    got = exchange(owned_parts.reshape(ctx_count, rows_piece, -1), "ctx", 6)
    qkv = got[:, :, : 3 * head_width].reshape(ctx_count, rows_piece, 3, head_width)
    fc1 = got[:, :, 3 * head_width :].reshape(ctx_count, rows_piece, dp_count, unit)
    return (
        qkv.transpose(1, 2, 0, 3).reshape(rows_piece, 3 * D).astype(jnp.float32),
        fc1.transpose(1, 2, 0, 3).reshape(rows_piece, FF).astype(jnp.float32),
    )


def head_plan(
    ring,
    tokens,
    lengths,
    w_qkv,
    b_qkv,
    w_out,
    b_out,
    w_fc1,
    b_fc1,
    w_fc2,
    b_fc2,
    ln_gain,
    ln_shift,
    cotangent,
):
    rows_here = tokens.shape[0]
    rows_piece = w_qkv.shape[0]
    dp_count = lax.axis_size("dp")
    ctx_count = lax.axis_size("ctx")
    count = dp_count * ctx_count
    group = rows_here * ctx_count
    head_width = D // ctx_count
    local_heads = HEADS // ctx_count
    unit = FF // (dp_count * ctx_count)
    here = lax.axis_index("ctx")
    group_rows = jnp.arange(group, dtype=jnp.int32)
    seg, positions = segment_info(lengths[0], group_rows)
    cosine, sine = rotary_tables(positions)
    qkv_bias, out_bias, fc2_bias, gain_low, shift_low, fc1_table = fetch_small(
        b_qkv, b_out, b_fc2, ln_gain, ln_shift, b_fc1
    )
    qkv_bias = qkv_bias.reshape(3 * D)
    out_bias = out_bias.reshape(D)
    fc2_bias = fc2_bias.reshape(D)
    gain_low = gain_low.reshape(D)
    shift_low = shift_low.reshape(D)
    fc1_bias = lax.dynamic_index_in_dim(
        fc1_table.reshape(dp_count, ctx_count, unit), here, 1, keepdims=False
    ).reshape(dp_count * unit)
    out_rows = fetch_out_rows(w_out)
    cols, fc2_rows, tokens = fetch_heads(w_qkv, w_fc1, w_fc2, tokens)
    gain32 = gain_low.astype(jnp.float32)
    shift32 = shift_low.astype(jnp.float32)
    inputs = tokens.astype(jnp.float32)
    normed, scaled, _ = norm_parts(inputs, gain32, shift32)
    tokens_group = ring_all_gather(tokens, ring, 0)
    late_dy, tokens_group = lax.optimization_barrier((cotangent, tokens_group))
    dy_group = lax.all_gather(late_dy, "ctx", axis=0, tiled=True)
    hidden_group = norm_parts(tokens_group.astype(jnp.float32), gain32, shift32)[2].astype(
        jnp.bfloat16
    )
    bias_cols = lax.dynamic_slice_in_dim(
        qkv_bias.reshape(3, D), here * head_width, head_width, 1
    ).reshape(3 * head_width)
    both = jnp.dot(hidden_group, cols, preferred_element_type=jnp.float32) + jnp.concatenate(
        [bias_cols, fc1_bias]
    ).astype(jnp.float32)
    qkv = both[:, : 3 * head_width]
    pre = both[:, 3 * head_width :]
    shape = (group, local_heads, HEAD_DIM)
    query = rotate(qkv[:, :head_width].reshape(shape), cosine, sine).astype(jnp.bfloat16)
    keys = rotate(qkv[:, head_width : 2 * head_width].reshape(shape), cosine, sine).astype(
        jnp.bfloat16
    )
    values = qkv[:, 2 * head_width :].reshape(shape).astype(jnp.bfloat16)
    q_heads = query.transpose(1, 0, 2)
    k_heads = keys.transpose(1, 0, 2)
    v_heads = values.transpose(1, 0, 2)
    attended_heads, log_total = attention_forward(q_heads, k_heads, v_heads, seg)
    attended = attended_heads.transpose(1, 0, 2).reshape(group, head_width).astype(jnp.bfloat16)
    act = gelu_tanh(pre).astype(jnp.bfloat16)
    branches = ring_reduce_scatter(
        jnp.dot(attended, out_rows, preferred_element_type=jnp.float32)
        + jnp.dot(act, fc2_rows, preferred_element_type=jnp.float32),
        ring,
        2,
    )
    block_out = (
        inputs + branches + out_bias.astype(jnp.float32) + fc2_bias.astype(jnp.float32)
    ).astype(jnp.bfloat16)
    grad_out32 = cotangent.astype(jnp.float32)
    grad_b_fc2 = jnp.sum(grad_out32, axis=0)
    grad_fc2_part = jnp.einsum("tf,td->fd", act, dy_group, preferred_element_type=jnp.float32)
    d_act = jnp.einsum("td,fd->tf", dy_group, fc2_rows, preferred_element_type=jnp.float32)
    d_pre = (d_act * gelu_slope(pre)).astype(jnp.bfloat16)
    grad_bfc1_part = jnp.sum(d_pre.astype(jnp.float32), axis=0)
    grad_out_rows = jnp.einsum("tc,td->cd", attended, dy_group, preferred_element_type=jnp.float32)
    owned_w_out = return_out_rows(grad_out_rows)
    d_attended = (
        jnp.einsum("td,cd->tc", dy_group, out_rows, preferred_element_type=jnp.float32)
        .astype(jnp.bfloat16)
        .reshape(shape)
    )
    d_heads = d_attended.transpose(1, 0, 2)
    delta = jnp.sum(d_heads.astype(jnp.float32) * attended_heads, axis=2, keepdims=True)
    dq_heads, dk_heads, dv_heads = attention_backward(
        q_heads, k_heads, v_heads, d_heads, log_total, delta, seg
    )
    d_query = dq_heads.transpose(1, 0, 2)
    d_keys = dk_heads.transpose(1, 0, 2)
    d_values = dv_heads.transpose(1, 0, 2)
    d_query = rotate_back(d_query, cosine, sine).reshape(group, head_width)
    d_keys = rotate_back(d_keys, cosine, sine).reshape(group, head_width)
    d_qkv = jnp.concatenate([d_query, d_keys, d_values.reshape(group, head_width)], axis=1).astype(
        jnp.bfloat16
    )
    d_both = jnp.concatenate([d_qkv, d_pre], axis=1)
    bias_part = jnp.sum(d_qkv.astype(jnp.float32), axis=0).reshape(3, head_width)
    d_hidden = ring_reduce_scatter(
        jnp.einsum("tc,dc->td", d_both, cols, preferred_element_type=jnp.float32), ring, 3
    )
    weight_parts = jnp.einsum(
        "td,tc->dc", hidden_group, d_both, preferred_element_type=jnp.float32
    ).astype(jnp.bfloat16)
    owned_parts = lax.psum_scatter(weight_parts, "dp", scatter_dimension=0, tiled=True)
    split_qkv, split_fc1 = return_heads(owned_parts)
    d_hidden, split_qkv, split_fc1 = lax.optimization_barrier((d_hidden, split_qkv, split_fc1))
    grad_gain, grad_shift, d_inputs = norm_back(d_hidden, normed, scaled, gain32)
    grad_tokens = (grad_out32 + d_inputs).astype(jnp.bfloat16)
    owned_fc2 = lax.psum_scatter(
        grad_fc2_part.astype(jnp.bfloat16), "dp", scatter_dimension=0, tiled=True
    ).astype(jnp.float32)
    full_bqkv = lax.dynamic_update_slice_in_dim(
        jnp.zeros((3, D), jnp.float32), bias_part, here * head_width, 1
    )
    full_bfc1 = lax.dynamic_update_slice_in_dim(
        jnp.zeros((dp_count, ctx_count, unit), jnp.float32),
        grad_bfc1_part.reshape(dp_count, 1, unit),
        here,
        1,
    )
    small = jnp.concatenate(
        [
            full_bqkv.reshape(count, -1),
            grad_b_fc2.reshape(count, -1),
            grad_gain.reshape(count, -1),
            grad_shift.reshape(count, -1),
            full_bfc1.reshape(count, -1),
        ],
        axis=1,
    )
    owned_small = reduce_small(small)
    cuts = [0, 3 * D // count, D // count, D // count, D // count, FF // count]
    bounds = [sum(cuts[: i + 1]) for i in range(len(cuts))]
    owned_bqkv, owned_bout, owned_gain, owned_shift, owned_bfc1 = [
        owned_small[bounds[i] : bounds[i + 1]] for i in range(5)
    ]
    return (
        block_out,
        grad_tokens,
        split_qkv.reshape(rows_piece, 3 * D),
        owned_bqkv,
        owned_w_out,
        owned_bout,
        split_fc1.reshape(rows_piece, FF),
        owned_bfc1,
        owned_fc2,
        owned_bout,
        owned_gain,
        owned_shift,
    )


def body(
    ring,
    tokens,
    lengths,
    w_qkv,
    b_qkv,
    w_out,
    b_out,
    w_fc1,
    b_fc1,
    w_fc2,
    b_fc2,
    ln_gain,
    ln_shift,
    cotangent,
):
    return head_plan(
        ring,
        tokens,
        lengths,
        w_qkv,
        b_qkv,
        w_out,
        b_out,
        w_fc1,
        b_fc1,
        w_fc2,
        b_fc2,
        ln_gain,
        ln_shift,
        cotangent,
    )


def solution(mesh):
    in_specs = (
        P(("dp", "ctx"), None),
        P("dp", None),
        P(("dp", "ctx"), None),
        P(("dp", "ctx")),
        P(("dp", "ctx"), None),
        P(("dp", "ctx")),
        P(("dp", "ctx"), None),
        P(("dp", "ctx")),
        P(("dp", "ctx"), None),
        P(("dp", "ctx")),
        P(("dp", "ctx")),
        P(("dp", "ctx")),
        P(("dp", "ctx"), None),
    )
    out_specs = (
        P(("dp", "ctx"), None),
        P(("dp", "ctx"), None),
        P(("dp", "ctx"), None),
        P(("dp", "ctx")),
        P(("dp", "ctx"), None),
        P(("dp", "ctx")),
        P(("dp", "ctx"), None),
        P(("dp", "ctx")),
        P(("dp", "ctx"), None),
        P(("dp", "ctx")),
        P(("dp", "ctx")),
        P(("dp", "ctx")),
    )
    ring = ring_of(mesh)
    return jax.shard_map(functools.partial(body, ring), mesh=mesh, in_specs=in_specs, out_specs=out_specs, check_vma=False)
```

```python
import functools
import math

import jax
import jax.numpy as jnp
from jax import lax
from jax.experimental import pallas as pl
from jax.experimental.pallas import tpu as pltpu
from jax.sharding import PartitionSpec as P

D = 2048
HEADS = 32
HEAD_DIM = 64
ROT = 32
FF = 8192


EPS = 1e-05
GELU_COEF = math.sqrt(2.0 / math.pi)
NEGATIVE = -1e30


def norm_parts(inputs, gain, shift):
    mean = jnp.mean(inputs, axis=-1, keepdims=True)
    centred = inputs - mean
    var = jnp.mean(centred * centred, axis=-1, keepdims=True)
    scaled = lax.rsqrt(var + EPS)
    normed = centred * scaled
    return (normed, scaled, normed * gain + shift)


def norm_back(d_hidden, normed, scaled, gain32):
    grad_gain = jnp.sum(d_hidden * normed, axis=0)
    grad_shift = jnp.sum(d_hidden, axis=0)
    d_normed = d_hidden * gain32
    d_inputs = scaled * (
        d_normed
        - jnp.mean(d_normed, axis=-1, keepdims=True)
        - normed * jnp.mean(d_normed * normed, axis=-1, keepdims=True)
    )
    return (grad_gain, grad_shift, d_inputs)


def gelu_tanh(pre):
    return 0.5 * pre * (1.0 + jnp.tanh(GELU_COEF * (pre + 0.044715 * pre * pre * pre)))


def gelu_slope(pre):
    tangent = jnp.tanh(GELU_COEF * (pre + 0.044715 * pre * pre * pre))
    return 0.5 * (1.0 + tangent) + 0.5 * pre * (1.0 - tangent * tangent) * GELU_COEF * (
        1.0 + 3.0 * 0.044715 * pre * pre
    )


def rotary_tables(positions):
    half = ROT // 2
    freq = jnp.exp(jnp.arange(half, dtype=jnp.float32) * (-2.0 * math.log(10000.0) / ROT))
    angle = positions.astype(jnp.float32)[:, None] * freq[None, :]
    return (jnp.cos(angle)[:, None, :], jnp.sin(angle)[:, None, :])


def rotate(heads, cosine, sine):
    half = ROT // 2
    first = heads[..., :half]
    second = heads[..., half:ROT]
    return jnp.concatenate(
        [first * cosine - second * sine, second * cosine + first * sine, heads[..., ROT:]], axis=-1
    )


def rotate_back(grads, cosine, sine):
    half = ROT // 2
    first = grads[..., :half]
    second = grads[..., half:ROT]
    return jnp.concatenate(
        [first * cosine + second * sine, second * cosine - first * sine, grads[..., ROT:]], axis=-1
    )


def segment_info(lengths_row, rows):
    ends = jnp.cumsum(lengths_row)
    starts = ends - lengths_row
    seg = jnp.sum((rows[:, None] >= ends[None, :]).astype(jnp.int32), axis=1)
    onehot = seg[:, None] == jnp.arange(lengths_row.shape[0], dtype=jnp.int32)[None, :]
    first_rows = jnp.sum(jnp.where(onehot, starts[None, :], 0), axis=1)
    return (seg, rows - first_rows)


TRANS_B = (((1,), (1,)), ((), ()))


def _allowed(segq_ref, segk_ref, i, j, tq, tk, causal):
    same = segq_ref[...] == segk_ref[...]
    if not causal:
        return same
    rows = i * tq + lax.broadcasted_iota(jnp.int32, (tq, tk), 0)
    cols = j * tk + lax.broadcasted_iota(jnp.int32, (tq, tk), 1)
    return same & (cols <= rows)


def _fwd_kernel(qi_ref, kj_ref, q_ref, k_ref, v_ref, segq_ref, segk_ref, o_ref, lse_ref, m_sc, acc_sc, *, tq, tk, scale):
    t = pl.program_id(1)
    i = qi_ref[t]
    j = kj_ref[t]
    dim = o_ref.shape[2]

    @pl.when(j == 0)
    def _():
        m_sc[...] = jnp.full_like(m_sc, NEGATIVE)
        acc_sc[...] = jnp.zeros_like(acc_sc)

    def absorb(causal):
        q = q_ref[0]
        k = k_ref[0]
        s = lax.dot_general(q, k, TRANS_B, preferred_element_type=jnp.float32) * scale
        s = jnp.where(_allowed(segq_ref, segk_ref, i, j, tq, tk, causal), s, -jnp.inf)
        m_prev = m_sc[...]
        m_new = jnp.maximum(m_prev, jnp.max(s, axis=1, keepdims=True))
        factor = jnp.exp(m_prev - m_new)
        p = jnp.exp(s - m_new)
        acc_sc[...] = acc_sc[...] * factor + jnp.dot(
            p.astype(jnp.bfloat16), v_ref[0], preferred_element_type=jnp.float32
        )
        m_sc[...] = m_new

    @pl.when(j < i)
    def _():
        absorb(False)

    @pl.when(j == i)
    def _():
        absorb(True)
        acc = acc_sc[...]
        total = acc[:, dim : dim + 1]
        o_ref[0] = acc[:, :dim] / total
        lse_ref[0] = m_sc[...] + jnp.log(total)


def _schedule(count, queries_outer):
    if queries_outer:
        pairs = [(i, j) for i in range(count) for j in range(i + 1)]
    else:
        pairs = [(i, j) for j in range(count) for i in range(j, count)]
    return (
        jnp.asarray([p[0] for p in pairs], jnp.int32),
        jnp.asarray([p[1] for p in pairs], jnp.int32),
    )


def attention_forward(q, k, v, seg, block=512):
    heads, total, dim = q.shape
    count = total // block
    scale = 1.0 / math.sqrt(dim)
    segq = seg.reshape(total, 1)
    segk = seg.reshape(1, total)
    qi, kj = _schedule(count, True)
    steps = qi.shape[0]
    lanes = 2 * dim
    v_ext = jnp.concatenate(
        [v, jnp.ones((heads, total, 1), v.dtype), jnp.zeros((heads, total, lanes - dim - 1), v.dtype)],
        axis=2,
    )

    return pl.pallas_call(
        functools.partial(_fwd_kernel, tq=block, tk=block, scale=scale),
        out_shape=(
            jax.ShapeDtypeStruct((heads, total, dim), jnp.float32),
            jax.ShapeDtypeStruct((heads, total, 1), jnp.float32),
        ),
        grid_spec=pltpu.PrefetchScalarGridSpec(
            num_scalar_prefetch=2,
            grid=(heads, steps),
            in_specs=[
                pl.BlockSpec((1, block, dim), lambda h, t, qi, kj: (h, qi[t], 0)),
                pl.BlockSpec((1, block, dim), lambda h, t, qi, kj: (h, kj[t], 0)),
                pl.BlockSpec((1, block, lanes), lambda h, t, qi, kj: (h, kj[t], 0)),
                pl.BlockSpec((block, 1), lambda h, t, qi, kj: (qi[t], 0)),
                pl.BlockSpec((1, block), lambda h, t, qi, kj: (0, kj[t])),
            ],
            out_specs=[
                pl.BlockSpec((1, block, dim), lambda h, t, qi, kj: (h, qi[t], 0)),
                pl.BlockSpec((1, block, 1), lambda h, t, qi, kj: (h, qi[t], 0)),
            ],
            scratch_shapes=[
                pltpu.VMEM((block, 1), jnp.float32),
                pltpu.VMEM((block, lanes), jnp.float32),
            ],
        ),
        cost_estimate=pl.CostEstimate(
            flops=2 * heads * total * total * dim,
            transcendentals=heads * total * total // 2,
            bytes_accessed=heads * total * dim * 10,
        ),
    )(qi, kj, q, k, v_ext, segq, segk)


def _bwd_kernel(qi_ref, kj_ref, q_ref, k_ref, v_ref, do_ref, lse_ref, delta_ref, segq_ref, segk_ref, dq_ref, dk_ref, dv_ref, dk_sc, dv_sc, *, tq, tk, scale, count):
    t = pl.program_id(1)
    i = qi_ref[t]
    j = kj_ref[t]

    @pl.when(t == 0)
    def _():
        dq_ref[...] = jnp.zeros_like(dq_ref)

    @pl.when(i == j)
    def _():
        dk_sc[...] = jnp.zeros_like(dk_sc)
        dv_sc[...] = jnp.zeros_like(dv_sc)

    def absorb(causal):
        q = q_ref[0]
        k = k_ref[0]
        do = do_ref[0]
        s = lax.dot_general(q, k, TRANS_B, preferred_element_type=jnp.float32) * scale
        s = jnp.where(_allowed(segq_ref, segk_ref, i, j, tq, tk, causal), s, -jnp.inf)
        p = jnp.exp(s - lse_ref[0])
        dp = lax.dot_general(do, v_ref[0], TRANS_B, preferred_element_type=jnp.float32)
        ds = (p * (dp - delta_ref[0])).astype(jnp.bfloat16)
        dv_sc[...] += jnp.dot(do.T, p.astype(jnp.bfloat16), preferred_element_type=jnp.float32)
        dk_sc[...] += jnp.dot(q.T, ds, preferred_element_type=jnp.float32)
        rows = pl.ds(pl.multiple_of(i * tq, tq), tq)
        dq_ref[0, rows, :] += lax.dot(ds, k, preferred_element_type=jnp.float32) * scale

    @pl.when(j < i)
    def _():
        absorb(False)

    @pl.when(j == i)
    def _():
        absorb(True)

    @pl.when(i == count - 1)
    def _():
        dk_ref[0] = dk_sc[...].T * scale
        dv_ref[0] = dv_sc[...].T


def attention_backward(q, k, v, do, lse, delta, seg, block=512):
    heads, total, dim = q.shape
    count = total // block
    scale = 1.0 / math.sqrt(dim)
    segq = seg.reshape(total, 1)
    segk = seg.reshape(1, total)
    qi, kj = _schedule(count, False)
    steps = qi.shape[0]

    def q_map(h, t, qi, kj):
        return (h, qi[t], 0)

    def k_map(h, t, qi, kj):
        return (h, kj[t], 0)

    return pl.pallas_call(
        functools.partial(_bwd_kernel, tq=block, tk=block, scale=scale, count=count),
        out_shape=(
            jax.ShapeDtypeStruct((heads, total, dim), jnp.float32),
            jax.ShapeDtypeStruct((heads, total, dim), jnp.float32),
            jax.ShapeDtypeStruct((heads, total, dim), jnp.float32),
        ),
        grid_spec=pltpu.PrefetchScalarGridSpec(
            num_scalar_prefetch=2,
            grid=(heads, steps),
            in_specs=[
                pl.BlockSpec((1, block, dim), q_map),
                pl.BlockSpec((1, block, dim), k_map),
                pl.BlockSpec((1, block, dim), k_map),
                pl.BlockSpec((1, block, dim), q_map),
                pl.BlockSpec((1, block, 1), q_map),
                pl.BlockSpec((1, block, 1), q_map),
                pl.BlockSpec((block, 1), lambda h, t, qi, kj: (qi[t], 0)),
                pl.BlockSpec((1, block), lambda h, t, qi, kj: (0, kj[t])),
            ],
            out_specs=[
                pl.BlockSpec((1, total, dim), lambda h, t, qi, kj: (h, 0, 0)),
                pl.BlockSpec((1, block, dim), k_map),
                pl.BlockSpec((1, block, dim), k_map),
            ],
            scratch_shapes=[
                pltpu.VMEM((dim, block), jnp.float32),
                pltpu.VMEM((dim, block), jnp.float32),
            ],
        ),
        cost_estimate=pl.CostEstimate(
            flops=5 * heads * total * total * dim,
            transcendentals=heads * total * total // 2,
            bytes_accessed=heads * total * dim * 24,
        ),
    )(qi, kj, q, k, v, do, lse, delta, segq, segk)


MESH_ID = pl.DeviceIdType.MESH


class Ring:
    def __init__(self, size, a_stride, b_stride):
        self.size = size
        self.half = size // 2
        self.a_stride = a_stride
        self.b_stride = b_stride

    def position(self, c):
        a = (c // self.a_stride) % self.half
        b = (c // self.b_stride) % 2
        return a + b * (2 * self.half - 1 - 2 * a)

    def device(self, pos):
        pos = pos % self.size
        b = pos // self.half
        a = pos + b * (2 * self.half - 1 - 2 * pos)
        return a * self.a_stride + b * self.b_stride


def ring_of(mesh):
    size = mesh.shape["ctx"]
    devices = list(mesh.devices.reshape(-1, size)[0])
    try:
        coords = [tuple(d.coords) for d in devices]
    except AttributeError:
        coords = None
    if coords and size % 2 == 0 and size >= 4:
        for b_stride in range(1, size):
            for a_stride in range(1, size):
                ring = Ring(size, a_stride, b_stride)
                order = [ring.device(p) for p in range(size)]
                if sorted(order) != list(range(size)):
                    continue
                hops = [
                    sum(abs(x - y) for x, y in zip(coords[order[p]], coords[order[(p + 1) % size]]))
                    for p in range(size)
                ]
                if max(hops) == 1:
                    return ring
    return Ring(size, 2, 1) if size % 2 == 0 and size >= 4 else None


def _barrier(g, left, right):
    barrier = pltpu.get_barrier_semaphore()
    for other in (left, right):
        pl.semaphore_signal(barrier, 1, device_id=(g, other), device_id_type=MESH_ID)
    pl.semaphore_wait(barrier, 2)


def _gather_kernel(x_ref, y_ref, own_sem, send_sem, recv_sem, *, ring, rows):
    n = ring.size
    half = rows // 2
    g = lax.axis_index("dp")
    c = lax.axis_index("ctx")
    pos = ring.position(c)
    right = ring.device(pos + 1)
    left = ring.device(pos + n - 1)
    own = pltpu.make_async_copy(x_ref, y_ref.at[pl.ds(c * rows, rows)], own_sem)
    own.start()
    _barrier(g, left, right)

    def link(direction, step, origin, source):
        offset = origin * rows + direction * half
        return pltpu.make_async_remote_copy(
            src_ref=source,
            dst_ref=y_ref.at[pl.ds(offset, half)],
            send_sem=send_sem.at[direction, step],
            recv_sem=recv_sem.at[direction, step],
            device_id=(g, right if direction == 0 else left),
            device_id_type=MESH_ID,
        )

    sent = []
    for step in range(n - 1):
        origins = (ring.device(pos - step + n), ring.device(pos + step))
        for direction in (0, 1):
            origin = origins[direction]
            if step == 0:
                source = x_ref.at[pl.ds(direction * half, half)]
            else:
                link(direction, step - 1, origin, None if False else y_ref.at[pl.ds(origin * rows + direction * half, half)]).wait_recv()
                source = y_ref.at[pl.ds(origin * rows + direction * half, half)]
            copy = link(direction, step, origin, source)
            copy.start()
            sent.append(copy)
    last = n - 2
    for direction, origin in ((0, ring.device(pos - last - 1 + n)), (1, ring.device(pos + last + 1))):
        link(direction, last, origin, y_ref.at[pl.ds(origin * rows + direction * half, half)]).wait_recv()
    for copy in sent:
        copy.wait_send()
    own.wait()


def ring_all_gather(x, ring, collective_id):
    rows, cols = x.shape
    n = ring.size
    return pl.pallas_call(
        functools.partial(_gather_kernel, ring=ring, rows=rows),
        out_shape=jax.ShapeDtypeStruct((n * rows, cols), x.dtype),
        in_specs=[pl.BlockSpec(memory_space=pl.ANY)],
        out_specs=pl.BlockSpec(memory_space=pl.ANY),
        scratch_shapes=[
            pltpu.SemaphoreType.DMA(()),
            pltpu.SemaphoreType.DMA((2, n - 1)),
            pltpu.SemaphoreType.DMA((2, n - 1)),
        ],
        compiler_params=pltpu.CompilerParams(collective_id=collective_id, has_side_effects=True),
    )(x)


def _scatter_kernel(p_ref, out_ref, recv_buf, send_buf, send_sem, recv_sem, *, ring, rows, parts):
    n = ring.size
    half = rows // 2
    piece = half // parts
    g = lax.axis_index("dp")
    c = lax.axis_index("ctx")
    pos = ring.position(c)
    right = ring.device(pos + 1)
    left = ring.device(pos + n - 1)
    _barrier(g, left, right)

    def link(direction, step, part):
        window = pl.ds(part * piece, piece)
        return pltpu.make_async_remote_copy(
            src_ref=send_buf.at[direction, step, window],
            dst_ref=recv_buf.at[direction, step, window],
            send_sem=send_sem.at[direction, step, part],
            recv_sem=recv_sem.at[direction, step, part],
            device_id=(g, right if direction == 0 else left),
            device_id_type=MESH_ID,
        )

    sent = []
    for step in range(n - 1):
        targets = (ring.device(pos - 1 - step + 2 * n), ring.device(pos + 1 + step))
        for part in range(parts):
            for direction in (0, 1):
                start = pl.multiple_of(
                    targets[direction] * rows + direction * half + part * piece, piece
                )
                window = pl.ds(part * piece, piece)
                total = p_ref[pl.ds(start, piece), :].astype(jnp.float32)
                if step > 0:
                    link(direction, step - 1, part).wait_recv()
                    total = total + recv_buf[direction, step - 1, window].astype(jnp.float32)
                send_buf[direction, step, window] = total.astype(send_buf.dtype)
                copy = link(direction, step, part)
                copy.start()
                sent.append(copy)
    for part in range(parts):
        for direction in (0, 1):
            link(direction, n - 2, part).wait_recv()
            start = pl.multiple_of(c * rows + direction * half + part * piece, piece)
            window = pl.ds(part * piece, piece)
            out_ref[pl.ds(direction * half + part * piece, piece), :] = (
                p_ref[pl.ds(start, piece), :].astype(jnp.float32)
                + recv_buf[direction, n - 2, window].astype(jnp.float32)
            ).astype(out_ref.dtype)
    for copy in sent:
        copy.wait_send()


def ring_reduce_scatter(p, ring, collective_id, out_dtype=jnp.float32, wire=jnp.bfloat16, parts=2):
    total_rows, cols = p.shape
    n = ring.size
    rows = total_rows // n
    half = rows // 2
    return pl.pallas_call(
        functools.partial(_scatter_kernel, ring=ring, rows=rows, parts=parts),
        out_shape=jax.ShapeDtypeStruct((rows, cols), out_dtype),
        in_specs=[pl.BlockSpec(memory_space=pltpu.VMEM)],
        out_specs=pl.BlockSpec(memory_space=pltpu.VMEM),
        scratch_shapes=[
            pltpu.VMEM((2, n - 1, half, cols), wire),
            pltpu.VMEM((2, n - 1, half, cols), wire),
            pltpu.SemaphoreType.DMA((2, n - 1, parts)),
            pltpu.SemaphoreType.DMA((2, n - 1, parts)),
        ],
        compiler_params=pltpu.CompilerParams(
            collective_id=collective_id, has_side_effects=True, vmem_limit_bytes=60 * 1024 * 1024
        ),
    )(p)


def _exchange_kernel(x_ref, out_ref, own_sem, send_sem, recv_sem, *, group):
    n = x_ref.shape[0]
    g = lax.axis_index("dp")
    c = lax.axis_index("ctx")
    n_ctx = lax.axis_size("ctx")
    me = {"all": g * n_ctx + c, "ctx": c, "dp": g}[group]

    def address(member):
        if group == "all":
            return (member // n_ctx, member % n_ctx)
        if group == "ctx":
            return (g, member)
        return (member, c)

    own = pltpu.make_async_copy(x_ref.at[me], out_ref.at[me], own_sem)
    own.start()
    barrier = pltpu.get_barrier_semaphore()
    for offset in range(1, n):
        pl.semaphore_signal(
            barrier, 1, device_id=address((me + offset) % n), device_id_type=MESH_ID
        )
    pl.semaphore_wait(barrier, n - 1)

    def link(offset, source, target):
        return pltpu.make_async_remote_copy(
            src_ref=x_ref.at[target],
            dst_ref=out_ref.at[source],
            send_sem=send_sem.at[offset],
            recv_sem=recv_sem.at[offset],
            device_id=address(target),
            device_id_type=MESH_ID,
        )

    sent = []
    for offset in range(1, n):
        copy = link(offset, me, (me + offset) % n)
        copy.start()
        sent.append(copy)
    for offset in range(1, n):
        link(offset, (me + n - offset) % n, me).wait_recv()
    for copy in sent:
        copy.wait_send()
    own.wait()


def exchange(x, group, collective_id):
    n = x.shape[0]
    space = pltpu.VMEM
    return pl.pallas_call(
        functools.partial(_exchange_kernel, group=group),
        out_shape=jax.ShapeDtypeStruct(x.shape, x.dtype),
        in_specs=[pl.BlockSpec(memory_space=space)],
        out_specs=pl.BlockSpec(memory_space=space),
        scratch_shapes=[
            pltpu.SemaphoreType.DMA(()),
            pltpu.SemaphoreType.DMA((n,)),
            pltpu.SemaphoreType.DMA((n,)),
        ],
        compiler_params=pltpu.CompilerParams(collective_id=collective_id, has_side_effects=True),
    )(x)


def block_moves(n_dp, n_ctx):
    count = n_dp * n_ctx
    return [(f, (f % n_dp) * n_ctx + f // n_dp) for f in range(count)]


def fetch_out_rows(w_out):
    n_dp = lax.axis_size("dp")
    n_ctx = lax.axis_size("ctx")
    moved = lax.ppermute(w_out.astype(jnp.bfloat16), ("dp", "ctx"), perm=block_moves(n_dp, n_ctx))
    return lax.all_gather(moved, "dp", axis=0, tiled=True)


def return_out_rows(grad_out_rows):
    n_dp = lax.axis_size("dp")
    n_ctx = lax.axis_size("ctx")
    part = lax.psum_scatter(grad_out_rows, "dp", scatter_dimension=0, tiled=True)
    back = [(b, a) for a, b in block_moves(n_dp, n_ctx)]
    return lax.ppermute(part, ("dp", "ctx"), perm=back)


def pack_rows(vector, lanes):
    size = vector.shape[0]
    total = -(-size // (16 * lanes)) * 16 * lanes
    return jnp.pad(vector, (0, total - size)).reshape(-1, lanes)


def fetch_small(b_qkv, b_out, b_fc2, ln_gain, ln_shift, b_fc1):
    pieces = (b_qkv, b_out, b_fc2, ln_gain, ln_shift, b_fc1)
    n_dp = lax.axis_size("dp")
    n_ctx = lax.axis_size("ctx")
    packed = pack_rows(jnp.concatenate([p.astype(jnp.bfloat16) for p in pieces]), 128)
    over_dp = exchange(jnp.broadcast_to(packed[None], (n_dp,) + packed.shape), "dp", 4)
    over_all = exchange(jnp.broadcast_to(over_dp[None], (n_ctx,) + over_dp.shape), "ctx", 8)
    table = over_all.transpose(1, 0, 2, 3).reshape(n_dp * n_ctx, -1)
    result = []
    offset = 0
    for p in pieces:
        result.append(table[:, offset : offset + p.shape[0]])
        offset += p.shape[0]
    return result


def reduce_small(small):
    n_dp = lax.axis_size("dp")
    n_ctx = lax.axis_size("ctx")
    count, width = small.shape
    packed = jax.vmap(lambda row: pack_rows(row, 128))(small)
    packed = packed.reshape((n_dp, n_ctx) + packed.shape[1:]).transpose(1, 0, 2, 3)
    over_ctx = jnp.sum(exchange(packed, "ctx", 7), axis=0)
    over_dp = jnp.sum(exchange(over_ctx, "dp", 9), axis=0)
    return over_dp.reshape(-1)[:width]


def fetch_heads(w_qkv, w_fc1, w_fc2, tokens):
    dp_count = lax.axis_size("dp")
    ctx_count = lax.axis_size("ctx")
    rows_piece = w_qkv.shape[0]
    head_width = D // ctx_count
    unit = FF // (dp_count * ctx_count)
    qkv_piece = w_qkv.astype(jnp.bfloat16).reshape(rows_piece, 3, ctx_count, head_width)
    fc1_piece = w_fc1.astype(jnp.bfloat16).reshape(rows_piece, dp_count, ctx_count, unit)
    pieces = jnp.concatenate(
        [
            qkv_piece.transpose(2, 0, 1, 3).reshape(ctx_count, rows_piece, 3 * head_width),
            fc1_piece.transpose(2, 0, 1, 3).reshape(ctx_count, rows_piece, dp_count * unit),
        ],
        axis=2,
    )
    sent = exchange(pieces, "ctx", 5).reshape(ctx_count * rows_piece, -1)
    sent, tokens = lax.optimization_barrier((sent, tokens))
    cols, fc2_rows = (
        lax.all_gather(sent, "dp", axis=0, tiled=True),
        lax.all_gather(w_fc2.astype(jnp.bfloat16), "dp", axis=0, tiled=True),
    )
    return (cols, fc2_rows, tokens)


def return_heads(owned_parts):
    dp_count = lax.axis_size("dp")
    ctx_count = lax.axis_size("ctx")
    head_width = D // ctx_count
    unit = FF // (dp_count * ctx_count)
    rows_piece = owned_parts.shape[0] // ctx_count
    got = exchange(owned_parts.reshape(ctx_count, rows_piece, -1), "ctx", 6)
    qkv = got[:, :, : 3 * head_width].reshape(ctx_count, rows_piece, 3, head_width)
    fc1 = got[:, :, 3 * head_width :].reshape(ctx_count, rows_piece, dp_count, unit)
    return (
        qkv.transpose(1, 2, 0, 3).reshape(rows_piece, 3 * D).astype(jnp.float32),
        fc1.transpose(1, 2, 0, 3).reshape(rows_piece, FF).astype(jnp.float32),
    )


def head_plan(
    ring,
    tokens,
    lengths,
    w_qkv,
    b_qkv,
    w_out,
    b_out,
    w_fc1,
    b_fc1,
    w_fc2,
    b_fc2,
    ln_gain,
    ln_shift,
    cotangent,
):
    rows_here = tokens.shape[0]
    rows_piece = w_qkv.shape[0]
    dp_count = lax.axis_size("dp")
    ctx_count = lax.axis_size("ctx")
    count = dp_count * ctx_count
    group = rows_here * ctx_count
    head_width = D // ctx_count
    local_heads = HEADS // ctx_count
    unit = FF // (dp_count * ctx_count)
    here = lax.axis_index("ctx")
    group_rows = jnp.arange(group, dtype=jnp.int32)
    seg, positions = segment_info(lengths[0], group_rows)
    cosine, sine = rotary_tables(positions)
    qkv_bias, out_bias, fc2_bias, gain_low, shift_low, fc1_table = fetch_small(
        b_qkv, b_out, b_fc2, ln_gain, ln_shift, b_fc1
    )
    qkv_bias = qkv_bias.reshape(3 * D)
    out_bias = out_bias.reshape(D)
    fc2_bias = fc2_bias.reshape(D)
    gain_low = gain_low.reshape(D)
    shift_low = shift_low.reshape(D)
    fc1_bias = lax.dynamic_index_in_dim(
        fc1_table.reshape(dp_count, ctx_count, unit), here, 1, keepdims=False
    ).reshape(dp_count * unit)
    out_rows = fetch_out_rows(w_out)
    cols, fc2_rows, tokens = fetch_heads(w_qkv, w_fc1, w_fc2, tokens)
    gain32 = gain_low.astype(jnp.float32)
    shift32 = shift_low.astype(jnp.float32)
    inputs = tokens.astype(jnp.float32)
    normed, scaled, _ = norm_parts(inputs, gain32, shift32)
    tokens_group = ring_all_gather(tokens, ring, 0)
    late_dy, tokens_group = lax.optimization_barrier((cotangent, tokens_group))
    dy_group = lax.all_gather(late_dy, "ctx", axis=0, tiled=True)
    hidden_group = norm_parts(tokens_group.astype(jnp.float32), gain32, shift32)[2].astype(
        jnp.bfloat16
    )
    bias_cols = lax.dynamic_slice_in_dim(
        qkv_bias.reshape(3, D), here * head_width, head_width, 1
    ).reshape(3 * head_width)
    qkv_width = 3 * head_width
    head_count = 3 * local_heads
    qkv_weights = cols[:, :qkv_width].reshape(D, head_count, HEAD_DIM)
    fc1_weights = cols[:, qkv_width:]
    qkv_heads = jnp.einsum(
        "td,dhe->hte", hidden_group, qkv_weights, preferred_element_type=jnp.float32
    ) + bias_cols.astype(jnp.float32).reshape(head_count, 1, HEAD_DIM)
    pre = jnp.dot(hidden_group, fc1_weights, preferred_element_type=jnp.float32) + fc1_bias.astype(
        jnp.float32
    )
    cos_heads = cosine.reshape(1, group, -1)
    sin_heads = sine.reshape(1, group, -1)
    q_heads = rotate(qkv_heads[:local_heads], cos_heads, sin_heads).astype(jnp.bfloat16)
    k_heads = rotate(qkv_heads[local_heads : 2 * local_heads], cos_heads, sin_heads).astype(
        jnp.bfloat16
    )
    v_heads = qkv_heads[2 * local_heads :].astype(jnp.bfloat16)
    attended_heads, log_total = attention_forward(q_heads, k_heads, v_heads, seg)
    attended_low = attended_heads.astype(jnp.bfloat16)
    out_heads = out_rows.reshape(local_heads, HEAD_DIM, D)
    act = gelu_tanh(pre).astype(jnp.bfloat16)
    branches = ring_reduce_scatter(
        jnp.einsum("hte,hed->td", attended_low, out_heads, preferred_element_type=jnp.float32)
        + jnp.dot(act, fc2_rows, preferred_element_type=jnp.float32),
        ring,
        2,
    )
    block_out = (
        inputs + branches + out_bias.astype(jnp.float32) + fc2_bias.astype(jnp.float32)
    ).astype(jnp.bfloat16)
    grad_out32 = cotangent.astype(jnp.float32)
    grad_b_fc2 = jnp.sum(grad_out32, axis=0)
    grad_fc2_part = jnp.einsum("tf,td->fd", act, dy_group, preferred_element_type=jnp.float32)
    d_act = jnp.einsum("td,fd->tf", dy_group, fc2_rows, preferred_element_type=jnp.float32)
    d_pre = (d_act * gelu_slope(pre)).astype(jnp.bfloat16)
    grad_bfc1_part = jnp.sum(d_pre.astype(jnp.float32), axis=0)
    grad_out_rows = jnp.einsum(
        "hte,td->hed", attended_low, dy_group, preferred_element_type=jnp.float32
    ).reshape(head_width, D)
    owned_w_out = return_out_rows(grad_out_rows)
    d_heads = jnp.einsum(
        "td,hed->hte", dy_group, out_heads, preferred_element_type=jnp.float32
    ).astype(jnp.bfloat16)
    delta = jnp.sum(d_heads.astype(jnp.float32) * attended_heads, axis=2, keepdims=True)
    dq_heads, dk_heads, dv_heads = attention_backward(
        q_heads, k_heads, v_heads, d_heads, log_total, delta, seg
    )
    d_qkv_heads = jnp.concatenate(
        [
            rotate_back(dq_heads, cos_heads, sin_heads),
            rotate_back(dk_heads, cos_heads, sin_heads),
            dv_heads,
        ],
        axis=0,
    ).astype(jnp.bfloat16)
    bias_part = jnp.sum(d_qkv_heads.astype(jnp.float32), axis=1).reshape(3, head_width)
    d_hidden_part = jnp.einsum(
        "hte,dhe->td", d_qkv_heads, qkv_weights, preferred_element_type=jnp.float32
    ) + jnp.einsum("tf,df->td", d_pre, fc1_weights, preferred_element_type=jnp.float32)
    d_hidden = ring_reduce_scatter(d_hidden_part, ring, 3)
    weight_parts = jnp.concatenate(
        [
            jnp.einsum(
                "td,hte->dhe", hidden_group, d_qkv_heads, preferred_element_type=jnp.float32
            ).reshape(D, qkv_width),
            jnp.einsum("td,tf->df", hidden_group, d_pre, preferred_element_type=jnp.float32),
        ],
        axis=1,
    ).astype(jnp.bfloat16)
    owned_parts = lax.psum_scatter(weight_parts, "dp", scatter_dimension=0, tiled=True)
    split_qkv, split_fc1 = return_heads(owned_parts)
    d_hidden, split_qkv, split_fc1 = lax.optimization_barrier((d_hidden, split_qkv, split_fc1))
    grad_gain, grad_shift, d_inputs = norm_back(d_hidden, normed, scaled, gain32)
    grad_tokens = (grad_out32 + d_inputs).astype(jnp.bfloat16)
    owned_fc2 = lax.psum_scatter(
        grad_fc2_part.astype(jnp.bfloat16), "dp", scatter_dimension=0, tiled=True
    ).astype(jnp.float32)
    full_bqkv = lax.dynamic_update_slice_in_dim(
        jnp.zeros((3, D), jnp.float32), bias_part, here * head_width, 1
    )
    full_bfc1 = lax.dynamic_update_slice_in_dim(
        jnp.zeros((dp_count, ctx_count, unit), jnp.float32),
        grad_bfc1_part.reshape(dp_count, 1, unit),
        here,
        1,
    )
    small = jnp.concatenate(
        [
            full_bqkv.reshape(count, -1),
            grad_b_fc2.reshape(count, -1),
            grad_gain.reshape(count, -1),
            grad_shift.reshape(count, -1),
            full_bfc1.reshape(count, -1),
        ],
        axis=1,
    )
    owned_small = reduce_small(small)
    cuts = [0, 3 * D // count, D // count, D // count, D // count, FF // count]
    bounds = [sum(cuts[: i + 1]) for i in range(len(cuts))]
    owned_bqkv, owned_bout, owned_gain, owned_shift, owned_bfc1 = [
        owned_small[bounds[i] : bounds[i + 1]] for i in range(5)
    ]
    return (
        block_out,
        grad_tokens,
        split_qkv.reshape(rows_piece, 3 * D),
        owned_bqkv,
        owned_w_out,
        owned_bout,
        split_fc1.reshape(rows_piece, FF),
        owned_bfc1,
        owned_fc2,
        owned_bout,
        owned_gain,
        owned_shift,
    )


def body(
    ring,
    tokens,
    lengths,
    w_qkv,
    b_qkv,
    w_out,
    b_out,
    w_fc1,
    b_fc1,
    w_fc2,
    b_fc2,
    ln_gain,
    ln_shift,
    cotangent,
):
    return head_plan(
        ring,
        tokens,
        lengths,
        w_qkv,
        b_qkv,
        w_out,
        b_out,
        w_fc1,
        b_fc1,
        w_fc2,
        b_fc2,
        ln_gain,
        ln_shift,
        cotangent,
    )


def solution(mesh):
    in_specs = (
        P(("dp", "ctx"), None),
        P("dp", None),
        P(("dp", "ctx"), None),
        P(("dp", "ctx")),
        P(("dp", "ctx"), None),
        P(("dp", "ctx")),
        P(("dp", "ctx"), None),
        P(("dp", "ctx")),
        P(("dp", "ctx"), None),
        P(("dp", "ctx")),
        P(("dp", "ctx")),
        P(("dp", "ctx")),
        P(("dp", "ctx"), None),
    )
    out_specs = (
        P(("dp", "ctx"), None),
        P(("dp", "ctx"), None),
        P(("dp", "ctx"), None),
        P(("dp", "ctx")),
        P(("dp", "ctx"), None),
        P(("dp", "ctx")),
        P(("dp", "ctx"), None),
        P(("dp", "ctx")),
        P(("dp", "ctx"), None),
        P(("dp", "ctx")),
        P(("dp", "ctx")),
        P(("dp", "ctx")),
    )
    ring = ring_of(mesh)
    return jax.shard_map(functools.partial(body, ring), mesh=mesh, in_specs=in_specs, out_specs=out_specs, check_vma=False)
```

```python
import functools
import math

import jax
import jax.numpy as jnp
from jax import lax
from jax.experimental import pallas as pl
from jax.experimental.pallas import tpu as pltpu
from jax.sharding import PartitionSpec as P

D = 2048
HEADS = 32
HEAD_DIM = 64
ROT = 32
FF = 8192


EPS = 1e-05
GELU_COEF = math.sqrt(2.0 / math.pi)
NEGATIVE = -1e30


def norm_parts(inputs, gain, shift):
    mean = jnp.mean(inputs, axis=-1, keepdims=True)
    centred = inputs - mean
    var = jnp.mean(centred * centred, axis=-1, keepdims=True)
    scaled = lax.rsqrt(var + EPS)
    normed = centred * scaled
    return (normed, scaled, normed * gain + shift)


def norm_back(d_hidden, normed, scaled, gain32):
    grad_gain = jnp.sum(d_hidden * normed, axis=0)
    grad_shift = jnp.sum(d_hidden, axis=0)
    d_normed = d_hidden * gain32
    d_inputs = scaled * (
        d_normed
        - jnp.mean(d_normed, axis=-1, keepdims=True)
        - normed * jnp.mean(d_normed * normed, axis=-1, keepdims=True)
    )
    return (grad_gain, grad_shift, d_inputs)


def gelu_tanh(pre):
    return 0.5 * pre * (1.0 + jnp.tanh(GELU_COEF * (pre + 0.044715 * pre * pre * pre)))


def gelu_slope(pre):
    tangent = jnp.tanh(GELU_COEF * (pre + 0.044715 * pre * pre * pre))
    return 0.5 * (1.0 + tangent) + 0.5 * pre * (1.0 - tangent * tangent) * GELU_COEF * (
        1.0 + 3.0 * 0.044715 * pre * pre
    )


def rotary_tables(positions):
    half = ROT // 2
    freq = jnp.exp(jnp.arange(half, dtype=jnp.float32) * (-2.0 * math.log(10000.0) / ROT))
    angle = positions.astype(jnp.float32)[:, None] * freq[None, :]
    return (jnp.cos(angle)[:, None, :], jnp.sin(angle)[:, None, :])


def rotate(heads, cosine, sine):
    half = ROT // 2
    first = heads[..., :half]
    second = heads[..., half:ROT]
    return jnp.concatenate(
        [first * cosine - second * sine, second * cosine + first * sine, heads[..., ROT:]], axis=-1
    )


def rotate_back(grads, cosine, sine):
    half = ROT // 2
    first = grads[..., :half]
    second = grads[..., half:ROT]
    return jnp.concatenate(
        [first * cosine + second * sine, second * cosine - first * sine, grads[..., ROT:]], axis=-1
    )


def segment_info(lengths_row, rows):
    ends = jnp.cumsum(lengths_row)
    starts = ends - lengths_row
    seg = jnp.sum((rows[:, None] >= ends[None, :]).astype(jnp.int32), axis=1)
    onehot = seg[:, None] == jnp.arange(lengths_row.shape[0], dtype=jnp.int32)[None, :]
    first_rows = jnp.sum(jnp.where(onehot, starts[None, :], 0), axis=1)
    return (seg, rows - first_rows)


TRANS_B = (((1,), (1,)), ((), ()))


def _allowed(segq_ref, segk_ref, i, j, tq, tk, causal):
    same = segq_ref[...] == segk_ref[...]
    if not causal:
        return same
    rows = i * tq + lax.broadcasted_iota(jnp.int32, (tq, tk), 0)
    cols = j * tk + lax.broadcasted_iota(jnp.int32, (tq, tk), 1)
    return same & (cols <= rows)


def _fwd_kernel(qi_ref, kj_ref, q_ref, k_ref, v_ref, segq_ref, segk_ref, o_ref, lse_ref, m_sc, acc_sc, *, tq, tk, scale):
    t = pl.program_id(1)
    i = qi_ref[t]
    j = kj_ref[t]
    dim = o_ref.shape[2]

    @pl.when(j == 0)
    def _():
        m_sc[...] = jnp.full_like(m_sc, NEGATIVE)
        acc_sc[...] = jnp.zeros_like(acc_sc)

    def absorb(causal):
        q = q_ref[0]
        k = k_ref[0]
        s = lax.dot_general(q, k, TRANS_B, preferred_element_type=jnp.float32) * scale
        s = jnp.where(_allowed(segq_ref, segk_ref, i, j, tq, tk, causal), s, -jnp.inf)
        m_prev = m_sc[...]
        m_new = jnp.maximum(m_prev, jnp.max(s, axis=1, keepdims=True))
        factor = jnp.exp(m_prev - m_new)
        p = jnp.exp(s - m_new)
        acc_sc[...] = acc_sc[...] * factor + jnp.dot(
            p.astype(jnp.bfloat16), v_ref[0], preferred_element_type=jnp.float32
        )
        m_sc[...] = m_new

    @pl.when(j < i)
    def _():
        absorb(False)

    @pl.when(j == i)
    def _():
        absorb(True)
        acc = acc_sc[...]
        total = acc[:, dim : dim + 1]
        o_ref[0] = acc[:, :dim] / total
        lse_ref[0] = m_sc[...] + jnp.log(total)


def _schedule(count, queries_outer):
    if queries_outer:
        pairs = [(i, j) for i in range(count) for j in range(i + 1)]
    else:
        pairs = [(i, j) for j in range(count) for i in range(j, count)]
    return (
        jnp.asarray([p[0] for p in pairs], jnp.int32),
        jnp.asarray([p[1] for p in pairs], jnp.int32),
    )


def attention_forward(q, k, v, seg, block=512):
    heads, total, dim = q.shape
    count = total // block
    scale = 1.0 / math.sqrt(dim)
    segq = seg.reshape(total, 1)
    segk = seg.reshape(1, total)
    qi, kj = _schedule(count, True)
    steps = qi.shape[0]
    lanes = 2 * dim
    v_ext = jnp.concatenate(
        [v, jnp.ones((heads, total, 1), v.dtype), jnp.zeros((heads, total, lanes - dim - 1), v.dtype)],
        axis=2,
    )

    return pl.pallas_call(
        functools.partial(_fwd_kernel, tq=block, tk=block, scale=scale),
        out_shape=(
            jax.ShapeDtypeStruct((heads, total, dim), jnp.float32),
            jax.ShapeDtypeStruct((heads, total, 1), jnp.float32),
        ),
        grid_spec=pltpu.PrefetchScalarGridSpec(
            num_scalar_prefetch=2,
            grid=(heads, steps),
            in_specs=[
                pl.BlockSpec((1, block, dim), lambda h, t, qi, kj: (h, qi[t], 0)),
                pl.BlockSpec((1, block, dim), lambda h, t, qi, kj: (h, kj[t], 0)),
                pl.BlockSpec((1, block, lanes), lambda h, t, qi, kj: (h, kj[t], 0)),
                pl.BlockSpec((block, 1), lambda h, t, qi, kj: (qi[t], 0)),
                pl.BlockSpec((1, block), lambda h, t, qi, kj: (0, kj[t])),
            ],
            out_specs=[
                pl.BlockSpec((1, block, dim), lambda h, t, qi, kj: (h, qi[t], 0)),
                pl.BlockSpec((1, block, 1), lambda h, t, qi, kj: (h, qi[t], 0)),
            ],
            scratch_shapes=[
                pltpu.VMEM((block, 1), jnp.float32),
                pltpu.VMEM((block, lanes), jnp.float32),
            ],
        ),
        cost_estimate=pl.CostEstimate(
            flops=2 * heads * total * total * dim,
            transcendentals=heads * total * total // 2,
            bytes_accessed=heads * total * dim * 10,
        ),
    )(qi, kj, q, k, v_ext, segq, segk)


def _bwd_kernel(qi_ref, kj_ref, q_ref, k_ref, v_ref, do_ref, lse_ref, delta_ref, segq_ref, segk_ref, dq_ref, dk_ref, dv_ref, dk_sc, dv_sc, *, tq, tk, scale, count):
    t = pl.program_id(1)
    i = qi_ref[t]
    j = kj_ref[t]

    @pl.when(t == 0)
    def _():
        dq_ref[...] = jnp.zeros_like(dq_ref)

    @pl.when(i == j)
    def _():
        dk_sc[...] = jnp.zeros_like(dk_sc)
        dv_sc[...] = jnp.zeros_like(dv_sc)

    def absorb(causal):
        q = q_ref[0]
        k = k_ref[0]
        do = do_ref[0]
        s = lax.dot_general(q, k, TRANS_B, preferred_element_type=jnp.float32) * scale
        s = jnp.where(_allowed(segq_ref, segk_ref, i, j, tq, tk, causal), s, -jnp.inf)
        p = jnp.exp(s - lse_ref[0])
        dp = lax.dot_general(do, v_ref[0], TRANS_B, preferred_element_type=jnp.float32)
        ds = (p * (dp - delta_ref[0])).astype(jnp.bfloat16)
        dv_sc[...] += jnp.dot(do.T, p.astype(jnp.bfloat16), preferred_element_type=jnp.float32)
        dk_sc[...] += jnp.dot(q.T, ds, preferred_element_type=jnp.float32)
        rows = pl.ds(pl.multiple_of(i * tq, tq), tq)
        dq_ref[0, rows, :] += lax.dot(ds, k, preferred_element_type=jnp.float32) * scale

    @pl.when(j < i)
    def _():
        absorb(False)

    @pl.when(j == i)
    def _():
        absorb(True)

    @pl.when(i == count - 1)
    def _():
        dk_ref[0] = dk_sc[...].T * scale
        dv_ref[0] = dv_sc[...].T


def attention_backward(q, k, v, do, lse, delta, seg, block=512):
    heads, total, dim = q.shape
    count = total // block
    scale = 1.0 / math.sqrt(dim)
    segq = seg.reshape(total, 1)
    segk = seg.reshape(1, total)
    qi, kj = _schedule(count, False)
    steps = qi.shape[0]

    def q_map(h, t, qi, kj):
        return (h, qi[t], 0)

    def k_map(h, t, qi, kj):
        return (h, kj[t], 0)

    return pl.pallas_call(
        functools.partial(_bwd_kernel, tq=block, tk=block, scale=scale, count=count),
        out_shape=(
            jax.ShapeDtypeStruct((heads, total, dim), jnp.float32),
            jax.ShapeDtypeStruct((heads, total, dim), jnp.float32),
            jax.ShapeDtypeStruct((heads, total, dim), jnp.float32),
        ),
        grid_spec=pltpu.PrefetchScalarGridSpec(
            num_scalar_prefetch=2,
            grid=(heads, steps),
            in_specs=[
                pl.BlockSpec((1, block, dim), q_map),
                pl.BlockSpec((1, block, dim), k_map),
                pl.BlockSpec((1, block, dim), k_map),
                pl.BlockSpec((1, block, dim), q_map),
                pl.BlockSpec((1, block, 1), q_map),
                pl.BlockSpec((1, block, 1), q_map),
                pl.BlockSpec((block, 1), lambda h, t, qi, kj: (qi[t], 0)),
                pl.BlockSpec((1, block), lambda h, t, qi, kj: (0, kj[t])),
            ],
            out_specs=[
                pl.BlockSpec((1, total, dim), lambda h, t, qi, kj: (h, 0, 0)),
                pl.BlockSpec((1, block, dim), k_map),
                pl.BlockSpec((1, block, dim), k_map),
            ],
            scratch_shapes=[
                pltpu.VMEM((dim, block), jnp.float32),
                pltpu.VMEM((dim, block), jnp.float32),
            ],
        ),
        cost_estimate=pl.CostEstimate(
            flops=5 * heads * total * total * dim,
            transcendentals=heads * total * total // 2,
            bytes_accessed=heads * total * dim * 24,
        ),
    )(qi, kj, q, k, v, do, lse, delta, segq, segk)


MESH_ID = pl.DeviceIdType.MESH


class Ring:
    def __init__(self, size, a_stride, b_stride):
        self.size = size
        self.half = size // 2
        self.a_stride = a_stride
        self.b_stride = b_stride

    def position(self, c):
        a = (c // self.a_stride) % self.half
        b = (c // self.b_stride) % 2
        return a + b * (2 * self.half - 1 - 2 * a)

    def device(self, pos):
        pos = pos % self.size
        b = pos // self.half
        a = pos + b * (2 * self.half - 1 - 2 * pos)
        return a * self.a_stride + b * self.b_stride


def ring_of(mesh):
    size = mesh.shape["ctx"]
    devices = list(mesh.devices.reshape(-1, size)[0])
    try:
        coords = [tuple(d.coords) for d in devices]
    except AttributeError:
        coords = None
    if coords and size % 2 == 0 and size >= 4:
        for b_stride in range(1, size):
            for a_stride in range(1, size):
                ring = Ring(size, a_stride, b_stride)
                order = [ring.device(p) for p in range(size)]
                if sorted(order) != list(range(size)):
                    continue
                hops = [
                    sum(abs(x - y) for x, y in zip(coords[order[p]], coords[order[(p + 1) % size]]))
                    for p in range(size)
                ]
                if max(hops) == 1:
                    return ring
    return Ring(size, 2, 1) if size % 2 == 0 and size >= 4 else None


def _barrier(g, left, right):
    barrier = pltpu.get_barrier_semaphore()
    for other in (left, right):
        pl.semaphore_signal(barrier, 1, device_id=(g, other), device_id_type=MESH_ID)
    pl.semaphore_wait(barrier, 2)


def _gather_kernel(x_ref, y_ref, own_sem, send_sem, recv_sem, *, ring, rows):
    n = ring.size
    half = rows // 2
    g = lax.axis_index("dp")
    c = lax.axis_index("ctx")
    pos = ring.position(c)
    right = ring.device(pos + 1)
    left = ring.device(pos + n - 1)
    own = pltpu.make_async_copy(x_ref, y_ref.at[pl.ds(c * rows, rows)], own_sem)
    own.start()
    _barrier(g, left, right)

    def link(direction, step, origin, source):
        offset = origin * rows + direction * half
        return pltpu.make_async_remote_copy(
            src_ref=source,
            dst_ref=y_ref.at[pl.ds(offset, half)],
            send_sem=send_sem.at[direction, step],
            recv_sem=recv_sem.at[direction, step],
            device_id=(g, right if direction == 0 else left),
            device_id_type=MESH_ID,
        )

    sent = []
    for step in range(n - 1):
        origins = (ring.device(pos - step + n), ring.device(pos + step))
        for direction in (0, 1):
            origin = origins[direction]
            if step == 0:
                source = x_ref.at[pl.ds(direction * half, half)]
            else:
                link(direction, step - 1, origin, None if False else y_ref.at[pl.ds(origin * rows + direction * half, half)]).wait_recv()
                source = y_ref.at[pl.ds(origin * rows + direction * half, half)]
            copy = link(direction, step, origin, source)
            copy.start()
            sent.append(copy)
    last = n - 2
    for direction, origin in ((0, ring.device(pos - last - 1 + n)), (1, ring.device(pos + last + 1))):
        link(direction, last, origin, y_ref.at[pl.ds(origin * rows + direction * half, half)]).wait_recv()
    for copy in sent:
        copy.wait_send()
    own.wait()


def ring_all_gather(x, ring, collective_id):
    rows, cols = x.shape
    n = ring.size
    return pl.pallas_call(
        functools.partial(_gather_kernel, ring=ring, rows=rows),
        out_shape=jax.ShapeDtypeStruct((n * rows, cols), x.dtype),
        in_specs=[pl.BlockSpec(memory_space=pl.ANY)],
        out_specs=pl.BlockSpec(memory_space=pl.ANY),
        scratch_shapes=[
            pltpu.SemaphoreType.DMA(()),
            pltpu.SemaphoreType.DMA((2, n - 1)),
            pltpu.SemaphoreType.DMA((2, n - 1)),
        ],
        compiler_params=pltpu.CompilerParams(collective_id=collective_id, has_side_effects=True),
    )(x)


def _scatter_kernel(p_ref, out_ref, recv_buf, send_buf, send_sem, recv_sem, *, ring, rows, parts):
    n = ring.size
    half = rows // 2
    piece = half // parts
    g = lax.axis_index("dp")
    c = lax.axis_index("ctx")
    pos = ring.position(c)
    right = ring.device(pos + 1)
    left = ring.device(pos + n - 1)
    _barrier(g, left, right)

    def link(direction, step, part):
        window = pl.ds(part * piece, piece)
        return pltpu.make_async_remote_copy(
            src_ref=send_buf.at[direction, step, window],
            dst_ref=recv_buf.at[direction, step, window],
            send_sem=send_sem.at[direction, step, part],
            recv_sem=recv_sem.at[direction, step, part],
            device_id=(g, right if direction == 0 else left),
            device_id_type=MESH_ID,
        )

    sent = []
    for step in range(n - 1):
        targets = (ring.device(pos - 1 - step + 2 * n), ring.device(pos + 1 + step))
        for part in range(parts):
            for direction in (0, 1):
                start = pl.multiple_of(
                    targets[direction] * rows + direction * half + part * piece, piece
                )
                window = pl.ds(part * piece, piece)
                total = p_ref[pl.ds(start, piece), :].astype(jnp.float32)
                if step > 0:
                    link(direction, step - 1, part).wait_recv()
                    total = total + recv_buf[direction, step - 1, window].astype(jnp.float32)
                send_buf[direction, step, window] = total.astype(send_buf.dtype)
                copy = link(direction, step, part)
                copy.start()
                sent.append(copy)
    for part in range(parts):
        for direction in (0, 1):
            link(direction, n - 2, part).wait_recv()
            start = pl.multiple_of(c * rows + direction * half + part * piece, piece)
            window = pl.ds(part * piece, piece)
            out_ref[pl.ds(direction * half + part * piece, piece), :] = (
                p_ref[pl.ds(start, piece), :].astype(jnp.float32)
                + recv_buf[direction, n - 2, window].astype(jnp.float32)
            ).astype(out_ref.dtype)
    for copy in sent:
        copy.wait_send()


def ring_reduce_scatter(p, ring, collective_id, out_dtype=jnp.float32, wire=jnp.bfloat16, parts=2):
    total_rows, cols = p.shape
    n = ring.size
    rows = total_rows // n
    half = rows // 2
    return pl.pallas_call(
        functools.partial(_scatter_kernel, ring=ring, rows=rows, parts=parts),
        out_shape=jax.ShapeDtypeStruct((rows, cols), out_dtype),
        in_specs=[pl.BlockSpec(memory_space=pltpu.VMEM)],
        out_specs=pl.BlockSpec(memory_space=pltpu.VMEM),
        scratch_shapes=[
            pltpu.VMEM((2, n - 1, half, cols), wire),
            pltpu.VMEM((2, n - 1, half, cols), wire),
            pltpu.SemaphoreType.DMA((2, n - 1, parts)),
            pltpu.SemaphoreType.DMA((2, n - 1, parts)),
        ],
        compiler_params=pltpu.CompilerParams(
            collective_id=collective_id, has_side_effects=True, vmem_limit_bytes=60 * 1024 * 1024
        ),
    )(p)


def _exchange_kernel(x_ref, out_ref, own_sem, send_sem, recv_sem, *, group):
    n = x_ref.shape[0]
    g = lax.axis_index("dp")
    c = lax.axis_index("ctx")
    n_ctx = lax.axis_size("ctx")
    me = {"all": g * n_ctx + c, "ctx": c, "dp": g}[group]

    def address(member):
        if group == "all":
            return (member // n_ctx, member % n_ctx)
        if group == "ctx":
            return (g, member)
        return (member, c)

    own = pltpu.make_async_copy(x_ref.at[me], out_ref.at[me], own_sem)
    own.start()
    barrier = pltpu.get_barrier_semaphore()
    for offset in range(1, n):
        pl.semaphore_signal(
            barrier, 1, device_id=address((me + offset) % n), device_id_type=MESH_ID
        )
    pl.semaphore_wait(barrier, n - 1)

    def link(offset, source, target):
        return pltpu.make_async_remote_copy(
            src_ref=x_ref.at[target],
            dst_ref=out_ref.at[source],
            send_sem=send_sem.at[offset],
            recv_sem=recv_sem.at[offset],
            device_id=address(target),
            device_id_type=MESH_ID,
        )

    sent = []
    for offset in range(1, n):
        copy = link(offset, me, (me + offset) % n)
        copy.start()
        sent.append(copy)
    for offset in range(1, n):
        link(offset, (me + n - offset) % n, me).wait_recv()
    for copy in sent:
        copy.wait_send()
    own.wait()


def exchange(x, group, collective_id):
    n = x.shape[0]
    space = pltpu.VMEM
    return pl.pallas_call(
        functools.partial(_exchange_kernel, group=group),
        out_shape=jax.ShapeDtypeStruct(x.shape, x.dtype),
        in_specs=[pl.BlockSpec(memory_space=space)],
        out_specs=pl.BlockSpec(memory_space=space),
        scratch_shapes=[
            pltpu.SemaphoreType.DMA(()),
            pltpu.SemaphoreType.DMA((n,)),
            pltpu.SemaphoreType.DMA((n,)),
        ],
        compiler_params=pltpu.CompilerParams(collective_id=collective_id, has_side_effects=True),
    )(x)


def block_moves(n_dp, n_ctx):
    count = n_dp * n_ctx
    return [(f, (f % n_dp) * n_ctx + f // n_dp) for f in range(count)]


def fetch_out_rows(w_out):
    n_dp = lax.axis_size("dp")
    n_ctx = lax.axis_size("ctx")
    moved = lax.ppermute(w_out.astype(jnp.bfloat16), ("dp", "ctx"), perm=block_moves(n_dp, n_ctx))
    return lax.all_gather(moved, "dp", axis=0, tiled=True)


def return_out_rows(grad_out_rows):
    n_dp = lax.axis_size("dp")
    n_ctx = lax.axis_size("ctx")
    part = lax.psum_scatter(grad_out_rows, "dp", scatter_dimension=0, tiled=True)
    back = [(b, a) for a, b in block_moves(n_dp, n_ctx)]
    return lax.ppermute(part, ("dp", "ctx"), perm=back)


def pack_rows(vector, lanes):
    size = vector.shape[0]
    total = -(-size // (16 * lanes)) * 16 * lanes
    return jnp.pad(vector, (0, total - size)).reshape(-1, lanes)


def fetch_small(b_qkv, b_out, b_fc2, ln_gain, ln_shift, b_fc1):
    pieces = (b_qkv, b_out, b_fc2, ln_gain, ln_shift, b_fc1)
    n_dp = lax.axis_size("dp")
    n_ctx = lax.axis_size("ctx")
    packed = pack_rows(jnp.concatenate([p.astype(jnp.bfloat16) for p in pieces]), 128)
    over_dp = exchange(jnp.broadcast_to(packed[None], (n_dp,) + packed.shape), "dp", 4)
    over_all = exchange(jnp.broadcast_to(over_dp[None], (n_ctx,) + over_dp.shape), "ctx", 8)
    table = over_all.transpose(1, 0, 2, 3).reshape(n_dp * n_ctx, -1)
    result = []
    offset = 0
    for p in pieces:
        result.append(table[:, offset : offset + p.shape[0]])
        offset += p.shape[0]
    return result


def reduce_small(small):
    n_dp = lax.axis_size("dp")
    n_ctx = lax.axis_size("ctx")
    count, width = small.shape
    packed = jax.vmap(lambda row: pack_rows(row, 128))(small)
    packed = packed.reshape((n_dp, n_ctx) + packed.shape[1:]).transpose(1, 0, 2, 3)
    over_ctx = jnp.sum(exchange(packed, "ctx", 7), axis=0)
    over_dp = jnp.sum(exchange(over_ctx, "dp", 9), axis=0)
    return over_dp.reshape(-1)[:width]


def fetch_heads(w_qkv, w_fc1, w_fc2, tokens):
    dp_count = lax.axis_size("dp")
    ctx_count = lax.axis_size("ctx")
    rows_piece = w_qkv.shape[0]
    head_width = D // ctx_count
    unit = FF // (dp_count * ctx_count)
    qkv_piece = w_qkv.astype(jnp.bfloat16).reshape(rows_piece, 3, ctx_count, head_width)
    fc1_piece = w_fc1.astype(jnp.bfloat16).reshape(rows_piece, dp_count, ctx_count, unit)
    pieces = jnp.concatenate(
        [
            qkv_piece.transpose(2, 0, 1, 3).reshape(ctx_count, rows_piece, 3 * head_width),
            fc1_piece.transpose(2, 0, 1, 3).reshape(ctx_count, rows_piece, dp_count * unit),
        ],
        axis=2,
    )
    sent = exchange(pieces, "ctx", 5).reshape(ctx_count * rows_piece, -1)
    sent, tokens = lax.optimization_barrier((sent, tokens))
    cols, fc2_rows = (
        lax.all_gather(sent, "dp", axis=0, tiled=True),
        lax.all_gather(w_fc2.astype(jnp.bfloat16), "dp", axis=0, tiled=True),
    )
    return (cols, fc2_rows, tokens)


def return_heads(owned_parts):
    dp_count = lax.axis_size("dp")
    ctx_count = lax.axis_size("ctx")
    head_width = D // ctx_count
    unit = FF // (dp_count * ctx_count)
    rows_piece = owned_parts.shape[0] // ctx_count
    got = exchange(owned_parts.reshape(ctx_count, rows_piece, -1), "ctx", 6)
    qkv = got[:, :, : 3 * head_width].reshape(ctx_count, rows_piece, 3, head_width)
    fc1 = got[:, :, 3 * head_width :].reshape(ctx_count, rows_piece, dp_count, unit)
    return (
        qkv.transpose(1, 2, 0, 3).reshape(rows_piece, 3 * D).astype(jnp.float32),
        fc1.transpose(1, 2, 0, 3).reshape(rows_piece, FF).astype(jnp.float32),
    )


def head_plan(
    ring,
    tokens,
    lengths,
    w_qkv,
    b_qkv,
    w_out,
    b_out,
    w_fc1,
    b_fc1,
    w_fc2,
    b_fc2,
    ln_gain,
    ln_shift,
    cotangent,
):
    rows_here = tokens.shape[0]
    rows_piece = w_qkv.shape[0]
    dp_count = lax.axis_size("dp")
    ctx_count = lax.axis_size("ctx")
    count = dp_count * ctx_count
    group = rows_here * ctx_count
    head_width = D // ctx_count
    local_heads = HEADS // ctx_count
    unit = FF // (dp_count * ctx_count)
    here = lax.axis_index("ctx")
    group_rows = jnp.arange(group, dtype=jnp.int32)
    seg, positions = segment_info(lengths[0], group_rows)
    cosine, sine = rotary_tables(positions)
    qkv_bias, out_bias, fc2_bias, gain_low, shift_low, fc1_table = fetch_small(
        b_qkv, b_out, b_fc2, ln_gain, ln_shift, b_fc1
    )
    qkv_bias = qkv_bias.reshape(3 * D)
    out_bias = out_bias.reshape(D)
    fc2_bias = fc2_bias.reshape(D)
    gain_low = gain_low.reshape(D)
    shift_low = shift_low.reshape(D)
    fc1_bias = lax.dynamic_index_in_dim(
        fc1_table.reshape(dp_count, ctx_count, unit), here, 1, keepdims=False
    ).reshape(dp_count * unit)
    out_rows = fetch_out_rows(w_out)
    cols, fc2_rows, tokens = fetch_heads(w_qkv, w_fc1, w_fc2, tokens)
    gain32 = gain_low.astype(jnp.float32)
    shift32 = shift_low.astype(jnp.float32)
    inputs = tokens.astype(jnp.float32)
    normed, scaled, _ = norm_parts(inputs, gain32, shift32)
    tokens_group = ring_all_gather(tokens, ring, 0)
    late_dy, tokens_group = lax.optimization_barrier((cotangent, tokens_group))
    dy_group = lax.all_gather(late_dy, "ctx", axis=0, tiled=True)
    hidden_group = norm_parts(tokens_group.astype(jnp.float32), gain32, shift32)[2].astype(
        jnp.bfloat16
    )
    bias_cols = lax.dynamic_slice_in_dim(
        qkv_bias.reshape(3, D), here * head_width, head_width, 1
    ).reshape(3 * head_width)
    qkv_width = 3 * head_width
    head_count = 3 * local_heads
    qkv_weights = cols[:, :qkv_width].reshape(D, head_count, HEAD_DIM)
    fc1_weights = cols[:, qkv_width:]
    qkv_heads = jnp.einsum(
        "td,dhe->hte", hidden_group, qkv_weights, preferred_element_type=jnp.float32
    ) + bias_cols.astype(jnp.float32).reshape(head_count, 1, HEAD_DIM)
    pre = jnp.dot(hidden_group, fc1_weights, preferred_element_type=jnp.float32) + fc1_bias.astype(
        jnp.float32
    )
    cos_heads = cosine.reshape(1, group, -1)
    sin_heads = sine.reshape(1, group, -1)
    q_heads = rotate(qkv_heads[:local_heads], cos_heads, sin_heads).astype(jnp.bfloat16)
    k_heads = rotate(qkv_heads[local_heads : 2 * local_heads], cos_heads, sin_heads).astype(
        jnp.bfloat16
    )
    v_heads = qkv_heads[2 * local_heads :].astype(jnp.bfloat16)
    attended_heads, log_total = attention_forward(q_heads, k_heads, v_heads, seg)
    attended_low = attended_heads.astype(jnp.bfloat16)
    out_heads = out_rows.reshape(local_heads, HEAD_DIM, D)
    act = gelu_tanh(pre).astype(jnp.bfloat16)
    branches = ring_reduce_scatter(
        jnp.einsum("hte,hed->td", attended_low, out_heads, preferred_element_type=jnp.float32)
        + jnp.dot(act, fc2_rows, preferred_element_type=jnp.float32),
        ring,
        2,
    )
    block_out = (
        inputs + branches + out_bias.astype(jnp.float32) + fc2_bias.astype(jnp.float32)
    ).astype(jnp.bfloat16)
    grad_out32 = cotangent.astype(jnp.float32)
    grad_b_fc2 = jnp.sum(grad_out32, axis=0)
    grad_fc2_part = jnp.einsum("tf,td->fd", act, dy_group, preferred_element_type=jnp.float32)
    d_act = jnp.einsum("td,fd->tf", dy_group, fc2_rows, preferred_element_type=jnp.float32)
    d_pre = (d_act * gelu_slope(pre)).astype(jnp.bfloat16)
    grad_bfc1_part = jnp.sum(d_pre.astype(jnp.float32), axis=0)
    grad_out_rows = jnp.einsum(
        "hte,td->hed", attended_low, dy_group, preferred_element_type=jnp.float32
    ).reshape(head_width, D)
    owned_w_out = return_out_rows(grad_out_rows)
    d_heads = jnp.einsum(
        "td,hed->hte", dy_group, out_heads, preferred_element_type=jnp.float32
    ).astype(jnp.bfloat16)
    delta = jnp.sum(d_heads.astype(jnp.float32) * attended_heads, axis=2, keepdims=True)
    dq_heads, dk_heads, dv_heads = attention_backward(
        q_heads, k_heads, v_heads, d_heads, log_total, delta, seg
    )
    shape = (group, local_heads, HEAD_DIM)
    d_query = rotate_back(dq_heads.transpose(1, 0, 2), cosine, sine).reshape(group, head_width)
    d_keys = rotate_back(dk_heads.transpose(1, 0, 2), cosine, sine).reshape(group, head_width)
    d_values = dv_heads.transpose(1, 0, 2).reshape(group, head_width)
    d_qkv = jnp.concatenate([d_query, d_keys, d_values], axis=1).astype(jnp.bfloat16)
    d_both = jnp.concatenate([d_qkv, d_pre], axis=1)
    bias_part = jnp.sum(d_qkv.astype(jnp.float32), axis=0).reshape(3, head_width)
    d_hidden = ring_reduce_scatter(
        jnp.einsum("tc,dc->td", d_both, cols, preferred_element_type=jnp.float32), ring, 3
    )
    weight_parts = jnp.einsum(
        "td,tc->dc", hidden_group, d_both, preferred_element_type=jnp.float32
    ).astype(jnp.bfloat16)
    owned_parts = lax.psum_scatter(weight_parts, "dp", scatter_dimension=0, tiled=True)
    split_qkv, split_fc1 = return_heads(owned_parts)
    d_hidden, split_qkv, split_fc1 = lax.optimization_barrier((d_hidden, split_qkv, split_fc1))
    grad_gain, grad_shift, d_inputs = norm_back(d_hidden, normed, scaled, gain32)
    grad_tokens = (grad_out32 + d_inputs).astype(jnp.bfloat16)
    owned_fc2 = lax.psum_scatter(
        grad_fc2_part.astype(jnp.bfloat16), "dp", scatter_dimension=0, tiled=True
    ).astype(jnp.float32)
    full_bqkv = lax.dynamic_update_slice_in_dim(
        jnp.zeros((3, D), jnp.float32), bias_part, here * head_width, 1
    )
    full_bfc1 = lax.dynamic_update_slice_in_dim(
        jnp.zeros((dp_count, ctx_count, unit), jnp.float32),
        grad_bfc1_part.reshape(dp_count, 1, unit),
        here,
        1,
    )
    small = jnp.concatenate(
        [
            full_bqkv.reshape(count, -1),
            grad_b_fc2.reshape(count, -1),
            grad_gain.reshape(count, -1),
            grad_shift.reshape(count, -1),
            full_bfc1.reshape(count, -1),
        ],
        axis=1,
    )
    owned_small = reduce_small(small)
    cuts = [0, 3 * D // count, D // count, D // count, D // count, FF // count]
    bounds = [sum(cuts[: i + 1]) for i in range(len(cuts))]
    owned_bqkv, owned_bout, owned_gain, owned_shift, owned_bfc1 = [
        owned_small[bounds[i] : bounds[i + 1]] for i in range(5)
    ]
    return (
        block_out,
        grad_tokens,
        split_qkv.reshape(rows_piece, 3 * D),
        owned_bqkv,
        owned_w_out,
        owned_bout,
        split_fc1.reshape(rows_piece, FF),
        owned_bfc1,
        owned_fc2,
        owned_bout,
        owned_gain,
        owned_shift,
    )


def body(
    ring,
    tokens,
    lengths,
    w_qkv,
    b_qkv,
    w_out,
    b_out,
    w_fc1,
    b_fc1,
    w_fc2,
    b_fc2,
    ln_gain,
    ln_shift,
    cotangent,
):
    return head_plan(
        ring,
        tokens,
        lengths,
        w_qkv,
        b_qkv,
        w_out,
        b_out,
        w_fc1,
        b_fc1,
        w_fc2,
        b_fc2,
        ln_gain,
        ln_shift,
        cotangent,
    )


def solution(mesh):
    in_specs = (
        P(("dp", "ctx"), None),
        P("dp", None),
        P(("dp", "ctx"), None),
        P(("dp", "ctx")),
        P(("dp", "ctx"), None),
        P(("dp", "ctx")),
        P(("dp", "ctx"), None),
        P(("dp", "ctx")),
        P(("dp", "ctx"), None),
        P(("dp", "ctx")),
        P(("dp", "ctx")),
        P(("dp", "ctx")),
        P(("dp", "ctx"), None),
    )
    out_specs = (
        P(("dp", "ctx"), None),
        P(("dp", "ctx"), None),
        P(("dp", "ctx"), None),
        P(("dp", "ctx")),
        P(("dp", "ctx"), None),
        P(("dp", "ctx")),
        P(("dp", "ctx"), None),
        P(("dp", "ctx")),
        P(("dp", "ctx"), None),
        P(("dp", "ctx")),
        P(("dp", "ctx")),
        P(("dp", "ctx")),
    )
    ring = ring_of(mesh)
    return jax.shard_map(functools.partial(body, ring), mesh=mesh, in_specs=in_specs, out_specs=out_specs, check_vma=False)
```

```python
import functools
import math

import jax
import jax.numpy as jnp
from jax import lax
from jax.experimental import pallas as pl
from jax.experimental.pallas import tpu as pltpu
from jax.sharding import PartitionSpec as P

D = 2048
HEADS = 32
HEAD_DIM = 64
ROT = 32
FF = 8192


EPS = 1e-05
GELU_COEF = math.sqrt(2.0 / math.pi)
NEGATIVE = -1e30


def norm_parts(inputs, gain, shift):
    mean = jnp.mean(inputs, axis=-1, keepdims=True)
    centred = inputs - mean
    var = jnp.mean(centred * centred, axis=-1, keepdims=True)
    scaled = lax.rsqrt(var + EPS)
    normed = centred * scaled
    return (normed, scaled, normed * gain + shift)


def norm_back(d_hidden, normed, scaled, gain32):
    grad_gain = jnp.sum(d_hidden * normed, axis=0)
    grad_shift = jnp.sum(d_hidden, axis=0)
    d_normed = d_hidden * gain32
    d_inputs = scaled * (
        d_normed
        - jnp.mean(d_normed, axis=-1, keepdims=True)
        - normed * jnp.mean(d_normed * normed, axis=-1, keepdims=True)
    )
    return (grad_gain, grad_shift, d_inputs)


def gelu_tanh(pre):
    return 0.5 * pre * (1.0 + jnp.tanh(GELU_COEF * (pre + 0.044715 * pre * pre * pre)))


def gelu_slope(pre):
    tangent = jnp.tanh(GELU_COEF * (pre + 0.044715 * pre * pre * pre))
    return 0.5 * (1.0 + tangent) + 0.5 * pre * (1.0 - tangent * tangent) * GELU_COEF * (
        1.0 + 3.0 * 0.044715 * pre * pre
    )


def rotary_tables(positions):
    half = ROT // 2
    freq = jnp.exp(jnp.arange(half, dtype=jnp.float32) * (-2.0 * math.log(10000.0) / ROT))
    angle = positions.astype(jnp.float32)[:, None] * freq[None, :]
    return (jnp.cos(angle)[:, None, :], jnp.sin(angle)[:, None, :])


def rotate(heads, cosine, sine):
    half = ROT // 2
    first = heads[..., :half]
    second = heads[..., half:ROT]
    return jnp.concatenate(
        [first * cosine - second * sine, second * cosine + first * sine, heads[..., ROT:]], axis=-1
    )


def rotate_back(grads, cosine, sine):
    half = ROT // 2
    first = grads[..., :half]
    second = grads[..., half:ROT]
    return jnp.concatenate(
        [first * cosine + second * sine, second * cosine - first * sine, grads[..., ROT:]], axis=-1
    )


def segment_info(lengths_row, rows):
    ends = jnp.cumsum(lengths_row)
    starts = ends - lengths_row
    seg = jnp.sum((rows[:, None] >= ends[None, :]).astype(jnp.int32), axis=1)
    onehot = seg[:, None] == jnp.arange(lengths_row.shape[0], dtype=jnp.int32)[None, :]
    first_rows = jnp.sum(jnp.where(onehot, starts[None, :], 0), axis=1)
    return (seg, rows - first_rows)


TRANS_B = (((1,), (1,)), ((), ()))


def _allowed(segq_ref, segk_ref, i, j, tq, tk, causal):
    same = segq_ref[...] == segk_ref[...]
    if not causal:
        return same
    rows = i * tq + lax.broadcasted_iota(jnp.int32, (tq, tk), 0)
    cols = j * tk + lax.broadcasted_iota(jnp.int32, (tq, tk), 1)
    return same & (cols <= rows)


def _fwd_kernel(qi_ref, kj_ref, q_ref, k_ref, v_ref, segq_ref, segk_ref, o_ref, lse_ref, m_sc, acc_sc, *, tq, tk, scale):
    t = pl.program_id(1)
    i = qi_ref[t]
    j = kj_ref[t]
    dim = o_ref.shape[2]

    @pl.when(j == 0)
    def _():
        m_sc[...] = jnp.full_like(m_sc, NEGATIVE)
        acc_sc[...] = jnp.zeros_like(acc_sc)

    def absorb(causal):
        q = q_ref[0]
        k = k_ref[0]
        s = lax.dot_general(q, k, TRANS_B, preferred_element_type=jnp.float32) * scale
        s = jnp.where(_allowed(segq_ref, segk_ref, i, j, tq, tk, causal), s, -jnp.inf)
        m_prev = m_sc[...]
        lanes = s.shape[1]
        folded = s[:, :128]
        for start in range(128, lanes, 128):
            folded = jnp.maximum(folded, s[:, start : start + 128])
        m_new = jnp.maximum(m_prev, jnp.max(folded, axis=1, keepdims=True))
        factor = jnp.exp(m_prev - m_new)
        p = jnp.exp(s - m_new)
        acc_sc[...] = acc_sc[...] * factor + jnp.dot(
            p.astype(jnp.bfloat16), v_ref[0], preferred_element_type=jnp.float32
        )
        m_sc[...] = m_new

    @pl.when(j < i)
    def _():
        absorb(False)

    @pl.when(j == i)
    def _():
        absorb(True)
        acc = acc_sc[...]
        total = acc[:, dim : dim + 1]
        o_ref[0] = acc[:, :dim] / total
        lse_ref[0] = m_sc[...] + jnp.log(total)


def _schedule(count, queries_outer):
    if queries_outer:
        pairs = [(i, j) for i in range(count) for j in range(i + 1)]
    else:
        pairs = [(i, j) for j in range(count) for i in range(j, count)]
    return (
        jnp.asarray([p[0] for p in pairs], jnp.int32),
        jnp.asarray([p[1] for p in pairs], jnp.int32),
    )


def attention_forward(q, k, v, seg, block=512):
    heads, total, dim = q.shape
    count = total // block
    scale = 1.0 / math.sqrt(dim)
    segq = seg.reshape(total, 1)
    segk = seg.reshape(1, total)
    qi, kj = _schedule(count, True)
    steps = qi.shape[0]
    lanes = 2 * dim
    v_ext = jnp.concatenate(
        [v, jnp.ones((heads, total, 1), v.dtype), jnp.zeros((heads, total, lanes - dim - 1), v.dtype)],
        axis=2,
    )

    return pl.pallas_call(
        functools.partial(_fwd_kernel, tq=block, tk=block, scale=scale),
        out_shape=(
            jax.ShapeDtypeStruct((heads, total, dim), jnp.float32),
            jax.ShapeDtypeStruct((heads, total, 1), jnp.float32),
        ),
        grid_spec=pltpu.PrefetchScalarGridSpec(
            num_scalar_prefetch=2,
            grid=(heads, steps),
            in_specs=[
                pl.BlockSpec((1, block, dim), lambda h, t, qi, kj: (h, qi[t], 0)),
                pl.BlockSpec((1, block, dim), lambda h, t, qi, kj: (h, kj[t], 0)),
                pl.BlockSpec((1, block, lanes), lambda h, t, qi, kj: (h, kj[t], 0)),
                pl.BlockSpec((block, 1), lambda h, t, qi, kj: (qi[t], 0)),
                pl.BlockSpec((1, block), lambda h, t, qi, kj: (0, kj[t])),
            ],
            out_specs=[
                pl.BlockSpec((1, block, dim), lambda h, t, qi, kj: (h, qi[t], 0)),
                pl.BlockSpec((1, block, 1), lambda h, t, qi, kj: (h, qi[t], 0)),
            ],
            scratch_shapes=[
                pltpu.VMEM((block, 1), jnp.float32),
                pltpu.VMEM((block, lanes), jnp.float32),
            ],
        ),
        cost_estimate=pl.CostEstimate(
            flops=2 * heads * total * total * dim,
            transcendentals=heads * total * total // 2,
            bytes_accessed=heads * total * dim * 10,
        ),
    )(qi, kj, q, k, v_ext, segq, segk)


def _bwd_kernel(qi_ref, kj_ref, q_ref, k_ref, v_ref, do_ref, lse_ref, delta_ref, segq_ref, segk_ref, dq_ref, dk_ref, dv_ref, dk_sc, dv_sc, *, tq, tk, scale, count):
    t = pl.program_id(1)
    i = qi_ref[t]
    j = kj_ref[t]

    @pl.when(t == 0)
    def _():
        dq_ref[...] = jnp.zeros_like(dq_ref)

    @pl.when(i == j)
    def _():
        dk_sc[...] = jnp.zeros_like(dk_sc)
        dv_sc[...] = jnp.zeros_like(dv_sc)

    def absorb(causal):
        q = q_ref[0]
        k = k_ref[0]
        do = do_ref[0]
        s = lax.dot_general(q, k, TRANS_B, preferred_element_type=jnp.float32) * scale
        s = jnp.where(_allowed(segq_ref, segk_ref, i, j, tq, tk, causal), s, -jnp.inf)
        p = jnp.exp(s - lse_ref[0])
        dp = lax.dot_general(do, v_ref[0], TRANS_B, preferred_element_type=jnp.float32)
        ds = (p * (dp - delta_ref[0])).astype(jnp.bfloat16)
        dv_sc[...] += jnp.dot(do.T, p.astype(jnp.bfloat16), preferred_element_type=jnp.float32)
        dk_sc[...] += jnp.dot(q.T, ds, preferred_element_type=jnp.float32)
        rows = pl.ds(pl.multiple_of(i * tq, tq), tq)
        dq_ref[0, rows, :] += lax.dot(ds, k, preferred_element_type=jnp.float32) * scale

    @pl.when(j < i)
    def _():
        absorb(False)

    @pl.when(j == i)
    def _():
        absorb(True)

    @pl.when(i == count - 1)
    def _():
        dk_ref[0] = dk_sc[...].T * scale
        dv_ref[0] = dv_sc[...].T


def attention_backward(q, k, v, do, lse, delta, seg, block=512):
    heads, total, dim = q.shape
    count = total // block
    scale = 1.0 / math.sqrt(dim)
    segq = seg.reshape(total, 1)
    segk = seg.reshape(1, total)
    qi, kj = _schedule(count, False)
    steps = qi.shape[0]

    def q_map(h, t, qi, kj):
        return (h, qi[t], 0)

    def k_map(h, t, qi, kj):
        return (h, kj[t], 0)

    return pl.pallas_call(
        functools.partial(_bwd_kernel, tq=block, tk=block, scale=scale, count=count),
        out_shape=(
            jax.ShapeDtypeStruct((heads, total, dim), jnp.float32),
            jax.ShapeDtypeStruct((heads, total, dim), jnp.float32),
            jax.ShapeDtypeStruct((heads, total, dim), jnp.float32),
        ),
        grid_spec=pltpu.PrefetchScalarGridSpec(
            num_scalar_prefetch=2,
            grid=(heads, steps),
            in_specs=[
                pl.BlockSpec((1, block, dim), q_map),
                pl.BlockSpec((1, block, dim), k_map),
                pl.BlockSpec((1, block, dim), k_map),
                pl.BlockSpec((1, block, dim), q_map),
                pl.BlockSpec((1, block, 1), q_map),
                pl.BlockSpec((1, block, 1), q_map),
                pl.BlockSpec((block, 1), lambda h, t, qi, kj: (qi[t], 0)),
                pl.BlockSpec((1, block), lambda h, t, qi, kj: (0, kj[t])),
            ],
            out_specs=[
                pl.BlockSpec((1, total, dim), lambda h, t, qi, kj: (h, 0, 0)),
                pl.BlockSpec((1, block, dim), k_map),
                pl.BlockSpec((1, block, dim), k_map),
            ],
            scratch_shapes=[
                pltpu.VMEM((dim, block), jnp.float32),
                pltpu.VMEM((dim, block), jnp.float32),
            ],
        ),
        cost_estimate=pl.CostEstimate(
            flops=5 * heads * total * total * dim,
            transcendentals=heads * total * total // 2,
            bytes_accessed=heads * total * dim * 24,
        ),
    )(qi, kj, q, k, v, do, lse, delta, segq, segk)


MESH_ID = pl.DeviceIdType.MESH


class Ring:
    def __init__(self, size, a_stride, b_stride):
        self.size = size
        self.half = size // 2
        self.a_stride = a_stride
        self.b_stride = b_stride

    def position(self, c):
        a = (c // self.a_stride) % self.half
        b = (c // self.b_stride) % 2
        return a + b * (2 * self.half - 1 - 2 * a)

    def device(self, pos):
        pos = pos % self.size
        b = pos // self.half
        a = pos + b * (2 * self.half - 1 - 2 * pos)
        return a * self.a_stride + b * self.b_stride


def ring_of(mesh):
    size = mesh.shape["ctx"]
    devices = list(mesh.devices.reshape(-1, size)[0])
    try:
        coords = [tuple(d.coords) for d in devices]
    except AttributeError:
        coords = None
    if coords and size % 2 == 0 and size >= 4:
        for b_stride in range(1, size):
            for a_stride in range(1, size):
                ring = Ring(size, a_stride, b_stride)
                order = [ring.device(p) for p in range(size)]
                if sorted(order) != list(range(size)):
                    continue
                hops = [
                    sum(abs(x - y) for x, y in zip(coords[order[p]], coords[order[(p + 1) % size]]))
                    for p in range(size)
                ]
                if max(hops) == 1:
                    return ring
    return Ring(size, 2, 1) if size % 2 == 0 and size >= 4 else None


def _barrier(g, left, right):
    barrier = pltpu.get_barrier_semaphore()
    for other in (left, right):
        pl.semaphore_signal(barrier, 1, device_id=(g, other), device_id_type=MESH_ID)
    pl.semaphore_wait(barrier, 2)


def _gather_kernel(x_ref, y_ref, own_sem, send_sem, recv_sem, *, ring, rows):
    n = ring.size
    half = rows // 2
    g = lax.axis_index("dp")
    c = lax.axis_index("ctx")
    pos = ring.position(c)
    right = ring.device(pos + 1)
    left = ring.device(pos + n - 1)
    own = pltpu.make_async_copy(x_ref, y_ref.at[pl.ds(c * rows, rows)], own_sem)
    own.start()
    _barrier(g, left, right)

    def link(direction, step, origin, source):
        offset = origin * rows + direction * half
        return pltpu.make_async_remote_copy(
            src_ref=source,
            dst_ref=y_ref.at[pl.ds(offset, half)],
            send_sem=send_sem.at[direction, step],
            recv_sem=recv_sem.at[direction, step],
            device_id=(g, right if direction == 0 else left),
            device_id_type=MESH_ID,
        )

    sent = []
    for step in range(n - 1):
        origins = (ring.device(pos - step + n), ring.device(pos + step))
        for direction in (0, 1):
            origin = origins[direction]
            if step == 0:
                source = x_ref.at[pl.ds(direction * half, half)]
            else:
                link(direction, step - 1, origin, None if False else y_ref.at[pl.ds(origin * rows + direction * half, half)]).wait_recv()
                source = y_ref.at[pl.ds(origin * rows + direction * half, half)]
            copy = link(direction, step, origin, source)
            copy.start()
            sent.append(copy)
    last = n - 2
    for direction, origin in ((0, ring.device(pos - last - 1 + n)), (1, ring.device(pos + last + 1))):
        link(direction, last, origin, y_ref.at[pl.ds(origin * rows + direction * half, half)]).wait_recv()
    for copy in sent:
        copy.wait_send()
    own.wait()


def ring_all_gather(x, ring, collective_id):
    rows, cols = x.shape
    n = ring.size
    return pl.pallas_call(
        functools.partial(_gather_kernel, ring=ring, rows=rows),
        out_shape=jax.ShapeDtypeStruct((n * rows, cols), x.dtype),
        in_specs=[pl.BlockSpec(memory_space=pl.ANY)],
        out_specs=pl.BlockSpec(memory_space=pl.ANY),
        scratch_shapes=[
            pltpu.SemaphoreType.DMA(()),
            pltpu.SemaphoreType.DMA((2, n - 1)),
            pltpu.SemaphoreType.DMA((2, n - 1)),
        ],
        compiler_params=pltpu.CompilerParams(collective_id=collective_id, has_side_effects=True),
    )(x)


def _scatter_kernel(p_ref, out_ref, recv_buf, send_buf, send_sem, recv_sem, *, ring, rows, parts):
    n = ring.size
    half = rows // 2
    piece = half // parts
    g = lax.axis_index("dp")
    c = lax.axis_index("ctx")
    pos = ring.position(c)
    right = ring.device(pos + 1)
    left = ring.device(pos + n - 1)
    _barrier(g, left, right)

    def link(direction, step, part):
        window = pl.ds(part * piece, piece)
        return pltpu.make_async_remote_copy(
            src_ref=send_buf.at[direction, step, window],
            dst_ref=recv_buf.at[direction, step, window],
            send_sem=send_sem.at[direction, step, part],
            recv_sem=recv_sem.at[direction, step, part],
            device_id=(g, right if direction == 0 else left),
            device_id_type=MESH_ID,
        )

    sent = []
    for step in range(n - 1):
        targets = (ring.device(pos - 1 - step + 2 * n), ring.device(pos + 1 + step))
        for part in range(parts):
            for direction in (0, 1):
                start = pl.multiple_of(
                    targets[direction] * rows + direction * half + part * piece, piece
                )
                window = pl.ds(part * piece, piece)
                total = p_ref[pl.ds(start, piece), :].astype(jnp.float32)
                if step > 0:
                    link(direction, step - 1, part).wait_recv()
                    total = total + recv_buf[direction, step - 1, window].astype(jnp.float32)
                send_buf[direction, step, window] = total.astype(send_buf.dtype)
                copy = link(direction, step, part)
                copy.start()
                sent.append(copy)
    for part in range(parts):
        for direction in (0, 1):
            link(direction, n - 2, part).wait_recv()
            start = pl.multiple_of(c * rows + direction * half + part * piece, piece)
            window = pl.ds(part * piece, piece)
            out_ref[pl.ds(direction * half + part * piece, piece), :] = (
                p_ref[pl.ds(start, piece), :].astype(jnp.float32)
                + recv_buf[direction, n - 2, window].astype(jnp.float32)
            ).astype(out_ref.dtype)
    for copy in sent:
        copy.wait_send()


def ring_reduce_scatter(p, ring, collective_id, out_dtype=jnp.float32, wire=jnp.bfloat16, parts=2):
    total_rows, cols = p.shape
    n = ring.size
    rows = total_rows // n
    half = rows // 2
    return pl.pallas_call(
        functools.partial(_scatter_kernel, ring=ring, rows=rows, parts=parts),
        out_shape=jax.ShapeDtypeStruct((rows, cols), out_dtype),
        in_specs=[pl.BlockSpec(memory_space=pltpu.VMEM)],
        out_specs=pl.BlockSpec(memory_space=pltpu.VMEM),
        scratch_shapes=[
            pltpu.VMEM((2, n - 1, half, cols), wire),
            pltpu.VMEM((2, n - 1, half, cols), wire),
            pltpu.SemaphoreType.DMA((2, n - 1, parts)),
            pltpu.SemaphoreType.DMA((2, n - 1, parts)),
        ],
        compiler_params=pltpu.CompilerParams(
            collective_id=collective_id, has_side_effects=True, vmem_limit_bytes=60 * 1024 * 1024
        ),
    )(p)


def _exchange_kernel(x_ref, out_ref, own_sem, send_sem, recv_sem, *, group):
    n = x_ref.shape[0]
    g = lax.axis_index("dp")
    c = lax.axis_index("ctx")
    n_ctx = lax.axis_size("ctx")
    me = {"all": g * n_ctx + c, "ctx": c, "dp": g}[group]

    def address(member):
        if group == "all":
            return (member // n_ctx, member % n_ctx)
        if group == "ctx":
            return (g, member)
        return (member, c)

    own = pltpu.make_async_copy(x_ref.at[me], out_ref.at[me], own_sem)
    own.start()
    barrier = pltpu.get_barrier_semaphore()
    for offset in range(1, n):
        pl.semaphore_signal(
            barrier, 1, device_id=address((me + offset) % n), device_id_type=MESH_ID
        )
    pl.semaphore_wait(barrier, n - 1)

    def link(offset, source, target):
        return pltpu.make_async_remote_copy(
            src_ref=x_ref.at[target],
            dst_ref=out_ref.at[source],
            send_sem=send_sem.at[offset],
            recv_sem=recv_sem.at[offset],
            device_id=address(target),
            device_id_type=MESH_ID,
        )

    sent = []
    for offset in range(1, n):
        copy = link(offset, me, (me + offset) % n)
        copy.start()
        sent.append(copy)
    for offset in range(1, n):
        link(offset, (me + n - offset) % n, me).wait_recv()
    for copy in sent:
        copy.wait_send()
    own.wait()


def exchange(x, group, collective_id):
    n = x.shape[0]
    space = pltpu.VMEM
    return pl.pallas_call(
        functools.partial(_exchange_kernel, group=group),
        out_shape=jax.ShapeDtypeStruct(x.shape, x.dtype),
        in_specs=[pl.BlockSpec(memory_space=space)],
        out_specs=pl.BlockSpec(memory_space=space),
        scratch_shapes=[
            pltpu.SemaphoreType.DMA(()),
            pltpu.SemaphoreType.DMA((n,)),
            pltpu.SemaphoreType.DMA((n,)),
        ],
        compiler_params=pltpu.CompilerParams(collective_id=collective_id, has_side_effects=True),
    )(x)


def block_moves(n_dp, n_ctx):
    count = n_dp * n_ctx
    return [(f, (f % n_dp) * n_ctx + f // n_dp) for f in range(count)]


def fetch_out_rows(w_out):
    n_dp = lax.axis_size("dp")
    n_ctx = lax.axis_size("ctx")
    moved = lax.ppermute(w_out.astype(jnp.bfloat16), ("dp", "ctx"), perm=block_moves(n_dp, n_ctx))
    return lax.all_gather(moved, "dp", axis=0, tiled=True)


def return_out_rows(grad_out_rows):
    n_dp = lax.axis_size("dp")
    n_ctx = lax.axis_size("ctx")
    part = lax.psum_scatter(grad_out_rows, "dp", scatter_dimension=0, tiled=True)
    back = [(b, a) for a, b in block_moves(n_dp, n_ctx)]
    return lax.ppermute(part, ("dp", "ctx"), perm=back)


def pack_rows(vector, lanes):
    size = vector.shape[0]
    total = -(-size // (16 * lanes)) * 16 * lanes
    return jnp.pad(vector, (0, total - size)).reshape(-1, lanes)


def fetch_small(b_qkv, b_out, b_fc2, ln_gain, ln_shift, b_fc1):
    pieces = (b_qkv, b_out, b_fc2, ln_gain, ln_shift, b_fc1)
    n_dp = lax.axis_size("dp")
    n_ctx = lax.axis_size("ctx")
    packed = pack_rows(jnp.concatenate([p.astype(jnp.bfloat16) for p in pieces]), 128)
    over_dp = exchange(jnp.broadcast_to(packed[None], (n_dp,) + packed.shape), "dp", 4)
    over_all = exchange(jnp.broadcast_to(over_dp[None], (n_ctx,) + over_dp.shape), "ctx", 8)
    table = over_all.transpose(1, 0, 2, 3).reshape(n_dp * n_ctx, -1)
    result = []
    offset = 0
    for p in pieces:
        result.append(table[:, offset : offset + p.shape[0]])
        offset += p.shape[0]
    return result


def reduce_small(small):
    n_dp = lax.axis_size("dp")
    n_ctx = lax.axis_size("ctx")
    count, width = small.shape
    packed = jax.vmap(lambda row: pack_rows(row, 128))(small)
    packed = packed.reshape((n_dp, n_ctx) + packed.shape[1:]).transpose(1, 0, 2, 3)
    over_ctx = jnp.sum(exchange(packed, "ctx", 7), axis=0)
    over_dp = jnp.sum(exchange(over_ctx, "dp", 9), axis=0)
    return over_dp.reshape(-1)[:width]


def fetch_heads(w_qkv, w_fc1, w_fc2, tokens):
    dp_count = lax.axis_size("dp")
    ctx_count = lax.axis_size("ctx")
    rows_piece = w_qkv.shape[0]
    head_width = D // ctx_count
    unit = FF // (dp_count * ctx_count)
    qkv_piece = w_qkv.astype(jnp.bfloat16).reshape(rows_piece, 3, ctx_count, head_width)
    fc1_piece = w_fc1.astype(jnp.bfloat16).reshape(rows_piece, dp_count, ctx_count, unit)
    pieces = jnp.concatenate(
        [
            qkv_piece.transpose(2, 0, 1, 3).reshape(ctx_count, rows_piece, 3 * head_width),
            fc1_piece.transpose(2, 0, 1, 3).reshape(ctx_count, rows_piece, dp_count * unit),
        ],
        axis=2,
    )
    sent = exchange(pieces, "ctx", 5).reshape(ctx_count * rows_piece, -1)
    sent, tokens = lax.optimization_barrier((sent, tokens))
    cols, fc2_rows = (
        lax.all_gather(sent, "dp", axis=0, tiled=True),
        lax.all_gather(w_fc2.astype(jnp.bfloat16), "dp", axis=0, tiled=True),
    )
    return (cols, fc2_rows, tokens)


def return_heads(owned_parts):
    dp_count = lax.axis_size("dp")
    ctx_count = lax.axis_size("ctx")
    head_width = D // ctx_count
    unit = FF // (dp_count * ctx_count)
    rows_piece = owned_parts.shape[0] // ctx_count
    got = exchange(owned_parts.reshape(ctx_count, rows_piece, -1), "ctx", 6)
    qkv = got[:, :, : 3 * head_width].reshape(ctx_count, rows_piece, 3, head_width)
    fc1 = got[:, :, 3 * head_width :].reshape(ctx_count, rows_piece, dp_count, unit)
    return (
        qkv.transpose(1, 2, 0, 3).reshape(rows_piece, 3 * D).astype(jnp.float32),
        fc1.transpose(1, 2, 0, 3).reshape(rows_piece, FF).astype(jnp.float32),
    )


def head_plan(
    ring,
    tokens,
    lengths,
    w_qkv,
    b_qkv,
    w_out,
    b_out,
    w_fc1,
    b_fc1,
    w_fc2,
    b_fc2,
    ln_gain,
    ln_shift,
    cotangent,
):
    rows_here = tokens.shape[0]
    rows_piece = w_qkv.shape[0]
    dp_count = lax.axis_size("dp")
    ctx_count = lax.axis_size("ctx")
    count = dp_count * ctx_count
    group = rows_here * ctx_count
    head_width = D // ctx_count
    local_heads = HEADS // ctx_count
    unit = FF // (dp_count * ctx_count)
    here = lax.axis_index("ctx")
    group_rows = jnp.arange(group, dtype=jnp.int32)
    seg, positions = segment_info(lengths[0], group_rows)
    cosine, sine = rotary_tables(positions)
    qkv_bias, out_bias, fc2_bias, gain_low, shift_low, fc1_table = fetch_small(
        b_qkv, b_out, b_fc2, ln_gain, ln_shift, b_fc1
    )
    qkv_bias = qkv_bias.reshape(3 * D)
    out_bias = out_bias.reshape(D)
    fc2_bias = fc2_bias.reshape(D)
    gain_low = gain_low.reshape(D)
    shift_low = shift_low.reshape(D)
    fc1_bias = lax.dynamic_index_in_dim(
        fc1_table.reshape(dp_count, ctx_count, unit), here, 1, keepdims=False
    ).reshape(dp_count * unit)
    out_rows = fetch_out_rows(w_out)
    cols, fc2_rows, tokens = fetch_heads(w_qkv, w_fc1, w_fc2, tokens)
    gain32 = gain_low.astype(jnp.float32)
    shift32 = shift_low.astype(jnp.float32)
    inputs = tokens.astype(jnp.float32)
    normed, scaled, _ = norm_parts(inputs, gain32, shift32)
    tokens_group = ring_all_gather(tokens, ring, 0)
    late_dy, tokens_group = lax.optimization_barrier((cotangent, tokens_group))
    dy_group = lax.all_gather(late_dy, "ctx", axis=0, tiled=True)
    hidden_group = norm_parts(tokens_group.astype(jnp.float32), gain32, shift32)[2].astype(
        jnp.bfloat16
    )
    bias_cols = lax.dynamic_slice_in_dim(
        qkv_bias.reshape(3, D), here * head_width, head_width, 1
    ).reshape(3 * head_width)
    both = jnp.dot(hidden_group, cols, preferred_element_type=jnp.float32) + jnp.concatenate(
        [bias_cols, fc1_bias]
    ).astype(jnp.float32)
    qkv = both[:, : 3 * head_width]
    pre = both[:, 3 * head_width :]
    shape = (group, local_heads, HEAD_DIM)
    query = rotate(qkv[:, :head_width].reshape(shape), cosine, sine).astype(jnp.bfloat16)
    keys = rotate(qkv[:, head_width : 2 * head_width].reshape(shape), cosine, sine).astype(
        jnp.bfloat16
    )
    values = qkv[:, 2 * head_width :].reshape(shape).astype(jnp.bfloat16)
    q_heads = query.transpose(1, 0, 2)
    k_heads = keys.transpose(1, 0, 2)
    v_heads = values.transpose(1, 0, 2)
    attended_heads, log_total = attention_forward(q_heads, k_heads, v_heads, seg)
    attended = attended_heads.transpose(1, 0, 2).reshape(group, head_width).astype(jnp.bfloat16)
    act = gelu_tanh(pre).astype(jnp.bfloat16)
    branches = ring_reduce_scatter(
        jnp.dot(attended, out_rows, preferred_element_type=jnp.float32)
        + jnp.dot(act, fc2_rows, preferred_element_type=jnp.float32),
        ring,
        2,
    )
    block_out = (
        inputs + branches + out_bias.astype(jnp.float32) + fc2_bias.astype(jnp.float32)
    ).astype(jnp.bfloat16)
    grad_out32 = cotangent.astype(jnp.float32)
    grad_b_fc2 = jnp.sum(grad_out32, axis=0)
    grad_fc2_part = jnp.einsum("tf,td->fd", act, dy_group, preferred_element_type=jnp.float32)
    d_act = jnp.einsum("td,fd->tf", dy_group, fc2_rows, preferred_element_type=jnp.float32)
    d_pre = (d_act * gelu_slope(pre)).astype(jnp.bfloat16)
    grad_bfc1_part = jnp.sum(d_pre.astype(jnp.float32), axis=0)
    grad_out_rows = jnp.einsum("tc,td->cd", attended, dy_group, preferred_element_type=jnp.float32)
    owned_w_out = return_out_rows(grad_out_rows)
    d_attended = (
        jnp.einsum("td,cd->tc", dy_group, out_rows, preferred_element_type=jnp.float32)
        .astype(jnp.bfloat16)
        .reshape(shape)
    )
    d_heads = d_attended.transpose(1, 0, 2)
    delta = jnp.sum(d_heads.astype(jnp.float32) * attended_heads, axis=2, keepdims=True)
    dq_heads, dk_heads, dv_heads = attention_backward(
        q_heads, k_heads, v_heads, d_heads, log_total, delta, seg
    )
    d_query = dq_heads.transpose(1, 0, 2)
    d_keys = dk_heads.transpose(1, 0, 2)
    d_values = dv_heads.transpose(1, 0, 2)
    d_query = rotate_back(d_query, cosine, sine).reshape(group, head_width)
    d_keys = rotate_back(d_keys, cosine, sine).reshape(group, head_width)
    d_qkv = jnp.concatenate([d_query, d_keys, d_values.reshape(group, head_width)], axis=1).astype(
        jnp.bfloat16
    )
    d_both = jnp.concatenate([d_qkv, d_pre], axis=1)
    bias_part = jnp.sum(d_qkv.astype(jnp.float32), axis=0).reshape(3, head_width)
    d_hidden = ring_reduce_scatter(
        jnp.einsum("tc,dc->td", d_both, cols, preferred_element_type=jnp.float32), ring, 3
    )
    weight_parts = jnp.einsum(
        "td,tc->dc", hidden_group, d_both, preferred_element_type=jnp.float32
    ).astype(jnp.bfloat16)
    owned_parts = lax.psum_scatter(weight_parts, "dp", scatter_dimension=0, tiled=True)
    split_qkv, split_fc1 = return_heads(owned_parts)
    d_hidden, split_qkv, split_fc1 = lax.optimization_barrier((d_hidden, split_qkv, split_fc1))
    grad_gain, grad_shift, d_inputs = norm_back(d_hidden, normed, scaled, gain32)
    grad_tokens = (grad_out32 + d_inputs).astype(jnp.bfloat16)
    owned_fc2 = lax.psum_scatter(
        grad_fc2_part.astype(jnp.bfloat16), "dp", scatter_dimension=0, tiled=True
    ).astype(jnp.float32)
    full_bqkv = lax.dynamic_update_slice_in_dim(
        jnp.zeros((3, D), jnp.float32), bias_part, here * head_width, 1
    )
    full_bfc1 = lax.dynamic_update_slice_in_dim(
        jnp.zeros((dp_count, ctx_count, unit), jnp.float32),
        grad_bfc1_part.reshape(dp_count, 1, unit),
        here,
        1,
    )
    small = jnp.concatenate(
        [
            full_bqkv.reshape(count, -1),
            grad_b_fc2.reshape(count, -1),
            grad_gain.reshape(count, -1),
            grad_shift.reshape(count, -1),
            full_bfc1.reshape(count, -1),
        ],
        axis=1,
    )
    owned_small = reduce_small(small)
    cuts = [0, 3 * D // count, D // count, D // count, D // count, FF // count]
    bounds = [sum(cuts[: i + 1]) for i in range(len(cuts))]
    owned_bqkv, owned_bout, owned_gain, owned_shift, owned_bfc1 = [
        owned_small[bounds[i] : bounds[i + 1]] for i in range(5)
    ]
    return (
        block_out,
        grad_tokens,
        split_qkv.reshape(rows_piece, 3 * D),
        owned_bqkv,
        owned_w_out,
        owned_bout,
        split_fc1.reshape(rows_piece, FF),
        owned_bfc1,
        owned_fc2,
        owned_bout,
        owned_gain,
        owned_shift,
    )


def body(
    ring,
    tokens,
    lengths,
    w_qkv,
    b_qkv,
    w_out,
    b_out,
    w_fc1,
    b_fc1,
    w_fc2,
    b_fc2,
    ln_gain,
    ln_shift,
    cotangent,
):
    return head_plan(
        ring,
        tokens,
        lengths,
        w_qkv,
        b_qkv,
        w_out,
        b_out,
        w_fc1,
        b_fc1,
        w_fc2,
        b_fc2,
        ln_gain,
        ln_shift,
        cotangent,
    )


def solution(mesh):
    in_specs = (
        P(("dp", "ctx"), None),
        P("dp", None),
        P(("dp", "ctx"), None),
        P(("dp", "ctx")),
        P(("dp", "ctx"), None),
        P(("dp", "ctx")),
        P(("dp", "ctx"), None),
        P(("dp", "ctx")),
        P(("dp", "ctx"), None),
        P(("dp", "ctx")),
        P(("dp", "ctx")),
        P(("dp", "ctx")),
        P(("dp", "ctx"), None),
    )
    out_specs = (
        P(("dp", "ctx"), None),
        P(("dp", "ctx"), None),
        P(("dp", "ctx"), None),
        P(("dp", "ctx")),
        P(("dp", "ctx"), None),
        P(("dp", "ctx")),
        P(("dp", "ctx"), None),
        P(("dp", "ctx")),
        P(("dp", "ctx"), None),
        P(("dp", "ctx")),
        P(("dp", "ctx")),
        P(("dp", "ctx")),
    )
    ring = ring_of(mesh)
    return jax.shard_map(functools.partial(body, ring), mesh=mesh, in_specs=in_specs, out_specs=out_specs, check_vma=False)
```

```python
import functools
import math

import jax
import jax.numpy as jnp
from jax import lax
from jax.experimental import pallas as pl
from jax.experimental.pallas import tpu as pltpu
from jax.sharding import PartitionSpec as P

D = 2048
HEADS = 32
HEAD_DIM = 64
ROT = 32
FF = 8192


EPS = 1e-05
GELU_COEF = math.sqrt(2.0 / math.pi)
NEGATIVE = -1e30


def norm_parts(inputs, gain, shift):
    mean = jnp.mean(inputs, axis=-1, keepdims=True)
    centred = inputs - mean
    var = jnp.mean(centred * centred, axis=-1, keepdims=True)
    scaled = lax.rsqrt(var + EPS)
    normed = centred * scaled
    return (normed, scaled, normed * gain + shift)


def norm_back(d_hidden, normed, scaled, gain32):
    grad_gain = jnp.sum(d_hidden * normed, axis=0)
    grad_shift = jnp.sum(d_hidden, axis=0)
    d_normed = d_hidden * gain32
    d_inputs = scaled * (
        d_normed
        - jnp.mean(d_normed, axis=-1, keepdims=True)
        - normed * jnp.mean(d_normed * normed, axis=-1, keepdims=True)
    )
    return (grad_gain, grad_shift, d_inputs)


def gelu_tanh(pre):
    return 0.5 * pre * (1.0 + jnp.tanh(GELU_COEF * (pre + 0.044715 * pre * pre * pre)))


def gelu_slope(pre):
    tangent = jnp.tanh(GELU_COEF * (pre + 0.044715 * pre * pre * pre))
    return 0.5 * (1.0 + tangent) + 0.5 * pre * (1.0 - tangent * tangent) * GELU_COEF * (
        1.0 + 3.0 * 0.044715 * pre * pre
    )


def rotary_tables(positions):
    half = ROT // 2
    freq = jnp.exp(jnp.arange(half, dtype=jnp.float32) * (-2.0 * math.log(10000.0) / ROT))
    angle = positions.astype(jnp.float32)[:, None] * freq[None, :]
    return (jnp.cos(angle)[:, None, :], jnp.sin(angle)[:, None, :])


def rotate(heads, cosine, sine):
    half = ROT // 2
    first = heads[..., :half]
    second = heads[..., half:ROT]
    return jnp.concatenate(
        [first * cosine - second * sine, second * cosine + first * sine, heads[..., ROT:]], axis=-1
    )


def rotate_back(grads, cosine, sine):
    half = ROT // 2
    first = grads[..., :half]
    second = grads[..., half:ROT]
    return jnp.concatenate(
        [first * cosine + second * sine, second * cosine - first * sine, grads[..., ROT:]], axis=-1
    )


def segment_info(lengths_row, rows):
    ends = jnp.cumsum(lengths_row)
    starts = ends - lengths_row
    seg = jnp.sum((rows[:, None] >= ends[None, :]).astype(jnp.int32), axis=1)
    onehot = seg[:, None] == jnp.arange(lengths_row.shape[0], dtype=jnp.int32)[None, :]
    first_rows = jnp.sum(jnp.where(onehot, starts[None, :], 0), axis=1)
    return (seg, rows - first_rows)


TRANS_B = (((1,), (1,)), ((), ()))


def _allowed(segq_ref, segk_ref, i, j, tq, tk, causal):
    same = segq_ref[...] == segk_ref[...]
    if not causal:
        return same
    rows = i * tq + lax.broadcasted_iota(jnp.int32, (tq, tk), 0)
    cols = j * tk + lax.broadcasted_iota(jnp.int32, (tq, tk), 1)
    return same & (cols <= rows)


def _fwd_kernel(qi_ref, kj_ref, q_ref, k_ref, v_ref, segq_ref, segk_ref, o_ref, lse_ref, m_sc, acc_sc, *, tq, tk, scale):
    t = pl.program_id(1)
    i = qi_ref[t]
    j = kj_ref[t]
    dim = o_ref.shape[2]

    @pl.when(j == 0)
    def _():
        m_sc[...] = jnp.full_like(m_sc, NEGATIVE)
        acc_sc[...] = jnp.zeros_like(acc_sc)

    def absorb(causal):
        q = q_ref[0]
        k = k_ref[0]
        s = lax.dot_general(q, k, TRANS_B, preferred_element_type=jnp.float32) * scale
        s = jnp.where(_allowed(segq_ref, segk_ref, i, j, tq, tk, causal), s, -jnp.inf)
        m_prev = m_sc[...]
        lanes = s.shape[1]
        folded = s[:, :128]
        for start in range(128, lanes, 128):
            folded = jnp.maximum(folded, s[:, start : start + 128])
        m_new = jnp.maximum(m_prev, jnp.max(folded, axis=1, keepdims=True))
        factor = jnp.exp(m_prev - m_new)
        p = jnp.exp(s - m_new)
        acc_sc[...] = acc_sc[...] * factor + jnp.dot(
            p.astype(jnp.bfloat16), v_ref[0], preferred_element_type=jnp.float32
        )
        m_sc[...] = m_new

    @pl.when(j < i)
    def _():
        absorb(False)

    @pl.when(j == i)
    def _():
        absorb(True)
        acc = acc_sc[...]
        total = acc[:, dim : dim + 1]
        o_ref[0] = acc[:, :dim] / total
        lse_ref[0] = m_sc[...] + jnp.log(total)


def _schedule(count, queries_outer):
    if queries_outer:
        pairs = [(i, j) for i in range(count) for j in range(i + 1)]
    else:
        pairs = [(i, j) for j in range(count) for i in range(j, count)]
    return (
        jnp.asarray([p[0] for p in pairs], jnp.int32),
        jnp.asarray([p[1] for p in pairs], jnp.int32),
    )


def attention_forward(q, k, v, seg, block=512):
    heads, total, dim = q.shape
    count = total // block
    scale = 1.0 / math.sqrt(dim)
    segq = seg.reshape(total, 1)
    segk = seg.reshape(1, total)
    qi, kj = _schedule(count, True)
    steps = qi.shape[0]
    lanes = 2 * dim
    v_ext = jnp.concatenate(
        [v, jnp.ones((heads, total, 1), v.dtype), jnp.zeros((heads, total, lanes - dim - 1), v.dtype)],
        axis=2,
    )

    return pl.pallas_call(
        functools.partial(_fwd_kernel, tq=block, tk=block, scale=scale),
        out_shape=(
            jax.ShapeDtypeStruct((heads, total, dim), jnp.float32),
            jax.ShapeDtypeStruct((heads, total, 1), jnp.float32),
        ),
        grid_spec=pltpu.PrefetchScalarGridSpec(
            num_scalar_prefetch=2,
            grid=(heads, steps),
            in_specs=[
                pl.BlockSpec((1, block, dim), lambda h, t, qi, kj: (h, qi[t], 0)),
                pl.BlockSpec((1, block, dim), lambda h, t, qi, kj: (h, kj[t], 0)),
                pl.BlockSpec((1, block, lanes), lambda h, t, qi, kj: (h, kj[t], 0)),
                pl.BlockSpec((block, 1), lambda h, t, qi, kj: (qi[t], 0)),
                pl.BlockSpec((1, block), lambda h, t, qi, kj: (0, kj[t])),
            ],
            out_specs=[
                pl.BlockSpec((1, block, dim), lambda h, t, qi, kj: (h, qi[t], 0)),
                pl.BlockSpec((1, block, 1), lambda h, t, qi, kj: (h, qi[t], 0)),
            ],
            scratch_shapes=[
                pltpu.VMEM((block, 1), jnp.float32),
                pltpu.VMEM((block, lanes), jnp.float32),
            ],
        ),
        cost_estimate=pl.CostEstimate(
            flops=2 * heads * total * total * dim,
            transcendentals=heads * total * total // 2,
            bytes_accessed=heads * total * dim * 10,
        ),
    )(qi, kj, q, k, v_ext, segq, segk)


def _bwd_kernel(qi_ref, kj_ref, q_ref, k_ref, v_ref, do_ref, lse_ref, delta_ref, segq_ref, segk_ref, dq_ref, dk_ref, dv_ref, dk_sc, dv_sc, *, tq, tk, scale, count):
    t = pl.program_id(1)
    i = qi_ref[t]
    j = kj_ref[t]

    @pl.when(t == 0)
    def _():
        dq_ref[...] = jnp.zeros_like(dq_ref)

    @pl.when(i == j)
    def _():
        dk_sc[...] = jnp.zeros_like(dk_sc)
        dv_sc[...] = jnp.zeros_like(dv_sc)

    def absorb(causal):
        q = q_ref[0]
        k = k_ref[0]
        do = do_ref[0]
        s = lax.dot_general(q, k, TRANS_B, preferred_element_type=jnp.float32) * scale
        s = jnp.where(_allowed(segq_ref, segk_ref, i, j, tq, tk, causal), s, -jnp.inf)
        p = jnp.exp(s - lse_ref[0])
        dp = lax.dot_general(do, v_ref[0], TRANS_B, preferred_element_type=jnp.float32)
        ds = (p * (dp - delta_ref[0])).astype(jnp.bfloat16)
        dv_sc[...] += jnp.dot(do.T, p.astype(jnp.bfloat16), preferred_element_type=jnp.float32)
        dk_sc[...] += jnp.dot(q.T, ds, preferred_element_type=jnp.float32)
        rows = pl.ds(pl.multiple_of(i * tq, tq), tq)
        dq_ref[0, rows, :] += lax.dot(ds, k, preferred_element_type=jnp.float32) * scale

    @pl.when(j < i)
    def _():
        absorb(False)

    @pl.when(j == i)
    def _():
        absorb(True)

    @pl.when(i == count - 1)
    def _():
        dk_ref[0] = dk_sc[...].T * scale
        dv_ref[0] = dv_sc[...].T


def attention_backward(q, k, v, do, lse, delta, seg, block=512):
    heads, total, dim = q.shape
    count = total // block
    scale = 1.0 / math.sqrt(dim)
    segq = seg.reshape(total, 1)
    segk = seg.reshape(1, total)
    qi, kj = _schedule(count, False)
    steps = qi.shape[0]

    def q_map(h, t, qi, kj):
        return (h, qi[t], 0)

    def k_map(h, t, qi, kj):
        return (h, kj[t], 0)

    return pl.pallas_call(
        functools.partial(_bwd_kernel, tq=block, tk=block, scale=scale, count=count),
        out_shape=(
            jax.ShapeDtypeStruct((heads, total, dim), jnp.float32),
            jax.ShapeDtypeStruct((heads, total, dim), jnp.float32),
            jax.ShapeDtypeStruct((heads, total, dim), jnp.float32),
        ),
        grid_spec=pltpu.PrefetchScalarGridSpec(
            num_scalar_prefetch=2,
            grid=(heads, steps),
            in_specs=[
                pl.BlockSpec((1, block, dim), q_map),
                pl.BlockSpec((1, block, dim), k_map),
                pl.BlockSpec((1, block, dim), k_map),
                pl.BlockSpec((1, block, dim), q_map),
                pl.BlockSpec((1, block, 1), q_map),
                pl.BlockSpec((1, block, 1), q_map),
                pl.BlockSpec((block, 1), lambda h, t, qi, kj: (qi[t], 0)),
                pl.BlockSpec((1, block), lambda h, t, qi, kj: (0, kj[t])),
            ],
            out_specs=[
                pl.BlockSpec((1, total, dim), lambda h, t, qi, kj: (h, 0, 0)),
                pl.BlockSpec((1, block, dim), k_map),
                pl.BlockSpec((1, block, dim), k_map),
            ],
            scratch_shapes=[
                pltpu.VMEM((dim, block), jnp.float32),
                pltpu.VMEM((dim, block), jnp.float32),
            ],
        ),
        cost_estimate=pl.CostEstimate(
            flops=5 * heads * total * total * dim,
            transcendentals=heads * total * total // 2,
            bytes_accessed=heads * total * dim * 24,
        ),
    )(qi, kj, q, k, v, do, lse, delta, segq, segk)


MESH_ID = pl.DeviceIdType.MESH


class Ring:
    def __init__(self, size, a_stride, b_stride):
        self.size = size
        self.half = size // 2
        self.a_stride = a_stride
        self.b_stride = b_stride

    def position(self, c):
        a = (c // self.a_stride) % self.half
        b = (c // self.b_stride) % 2
        return a + b * (2 * self.half - 1 - 2 * a)

    def device(self, pos):
        pos = pos % self.size
        b = pos // self.half
        a = pos + b * (2 * self.half - 1 - 2 * pos)
        return a * self.a_stride + b * self.b_stride


def ring_of(mesh):
    size = mesh.shape["ctx"]
    devices = list(mesh.devices.reshape(-1, size)[0])
    try:
        coords = [tuple(d.coords) for d in devices]
    except AttributeError:
        coords = None
    if coords and size % 2 == 0 and size >= 4:
        for b_stride in range(1, size):
            for a_stride in range(1, size):
                ring = Ring(size, a_stride, b_stride)
                order = [ring.device(p) for p in range(size)]
                if sorted(order) != list(range(size)):
                    continue
                hops = [
                    sum(abs(x - y) for x, y in zip(coords[order[p]], coords[order[(p + 1) % size]]))
                    for p in range(size)
                ]
                if max(hops) == 1:
                    return ring
    return Ring(size, 2, 1) if size % 2 == 0 and size >= 4 else None


def _barrier(g, left, right):
    barrier = pltpu.get_barrier_semaphore()
    for other in (left, right):
        pl.semaphore_signal(barrier, 1, device_id=(g, other), device_id_type=MESH_ID)
    pl.semaphore_wait(barrier, 2)


def _gather_kernel(x_ref, y_ref, own_sem, send_sem, recv_sem, *, ring, rows):
    n = ring.size
    half = rows // 2
    g = lax.axis_index("dp")
    c = lax.axis_index("ctx")
    pos = ring.position(c)
    right = ring.device(pos + 1)
    left = ring.device(pos + n - 1)
    own = pltpu.make_async_copy(x_ref, y_ref.at[pl.ds(c * rows, rows)], own_sem)
    own.start()
    _barrier(g, left, right)

    def link(direction, step, origin, source):
        offset = origin * rows + direction * half
        return pltpu.make_async_remote_copy(
            src_ref=source,
            dst_ref=y_ref.at[pl.ds(offset, half)],
            send_sem=send_sem.at[direction, step],
            recv_sem=recv_sem.at[direction, step],
            device_id=(g, right if direction == 0 else left),
            device_id_type=MESH_ID,
        )

    sent = []
    for step in range(n - 1):
        origins = (ring.device(pos - step + n), ring.device(pos + step))
        for direction in (0, 1):
            origin = origins[direction]
            if step == 0:
                source = x_ref.at[pl.ds(direction * half, half)]
            else:
                link(direction, step - 1, origin, None if False else y_ref.at[pl.ds(origin * rows + direction * half, half)]).wait_recv()
                source = y_ref.at[pl.ds(origin * rows + direction * half, half)]
            copy = link(direction, step, origin, source)
            copy.start()
            sent.append(copy)
    last = n - 2
    for direction, origin in ((0, ring.device(pos - last - 1 + n)), (1, ring.device(pos + last + 1))):
        link(direction, last, origin, y_ref.at[pl.ds(origin * rows + direction * half, half)]).wait_recv()
    for copy in sent:
        copy.wait_send()
    own.wait()


def ring_all_gather(x, ring, collective_id):
    rows, cols = x.shape
    n = ring.size
    return pl.pallas_call(
        functools.partial(_gather_kernel, ring=ring, rows=rows),
        out_shape=jax.ShapeDtypeStruct((n * rows, cols), x.dtype),
        in_specs=[pl.BlockSpec(memory_space=pl.ANY)],
        out_specs=pl.BlockSpec(memory_space=pl.ANY),
        scratch_shapes=[
            pltpu.SemaphoreType.DMA(()),
            pltpu.SemaphoreType.DMA((2, n - 1)),
            pltpu.SemaphoreType.DMA((2, n - 1)),
        ],
        compiler_params=pltpu.CompilerParams(collective_id=collective_id, has_side_effects=True),
    )(x)


def _scatter_kernel(p_ref, out_ref, recv_buf, send_buf, send_sem, recv_sem, *, ring, rows, parts):
    n = ring.size
    half = rows // 2
    piece = half // parts
    g = lax.axis_index("dp")
    c = lax.axis_index("ctx")
    pos = ring.position(c)
    right = ring.device(pos + 1)
    left = ring.device(pos + n - 1)
    _barrier(g, left, right)

    def link(direction, step, part):
        window = pl.ds(part * piece, piece)
        return pltpu.make_async_remote_copy(
            src_ref=send_buf.at[direction, step, window],
            dst_ref=recv_buf.at[direction, step, window],
            send_sem=send_sem.at[direction, step, part],
            recv_sem=recv_sem.at[direction, step, part],
            device_id=(g, right if direction == 0 else left),
            device_id_type=MESH_ID,
        )

    sent = []
    for step in range(n - 1):
        targets = (ring.device(pos - 1 - step + 2 * n), ring.device(pos + 1 + step))
        for part in range(parts):
            for direction in (0, 1):
                start = pl.multiple_of(
                    targets[direction] * rows + direction * half + part * piece, piece
                )
                window = pl.ds(part * piece, piece)
                total = p_ref[pl.ds(start, piece), :].astype(jnp.float32)
                if step > 0:
                    link(direction, step - 1, part).wait_recv()
                    total = total + recv_buf[direction, step - 1, window].astype(jnp.float32)
                send_buf[direction, step, window] = total.astype(send_buf.dtype)
                copy = link(direction, step, part)
                copy.start()
                sent.append(copy)
    for part in range(parts):
        for direction in (0, 1):
            link(direction, n - 2, part).wait_recv()
            start = pl.multiple_of(c * rows + direction * half + part * piece, piece)
            window = pl.ds(part * piece, piece)
            out_ref[pl.ds(direction * half + part * piece, piece), :] = (
                p_ref[pl.ds(start, piece), :].astype(jnp.float32)
                + recv_buf[direction, n - 2, window].astype(jnp.float32)
            ).astype(out_ref.dtype)
    for copy in sent:
        copy.wait_send()


def ring_reduce_scatter(p, ring, collective_id, out_dtype=jnp.float32, wire=jnp.bfloat16, parts=4):
    total_rows, cols = p.shape
    n = ring.size
    rows = total_rows // n
    half = rows // 2
    return pl.pallas_call(
        functools.partial(_scatter_kernel, ring=ring, rows=rows, parts=parts),
        out_shape=jax.ShapeDtypeStruct((rows, cols), out_dtype),
        in_specs=[pl.BlockSpec(memory_space=pltpu.VMEM)],
        out_specs=pl.BlockSpec(memory_space=pltpu.VMEM),
        scratch_shapes=[
            pltpu.VMEM((2, n - 1, half, cols), wire),
            pltpu.VMEM((2, n - 1, half, cols), wire),
            pltpu.SemaphoreType.DMA((2, n - 1, parts)),
            pltpu.SemaphoreType.DMA((2, n - 1, parts)),
        ],
        compiler_params=pltpu.CompilerParams(
            collective_id=collective_id, has_side_effects=True, vmem_limit_bytes=60 * 1024 * 1024
        ),
    )(p)


def _exchange_kernel(x_ref, out_ref, own_sem, send_sem, recv_sem, *, group):
    n = x_ref.shape[0]
    g = lax.axis_index("dp")
    c = lax.axis_index("ctx")
    n_ctx = lax.axis_size("ctx")
    me = {"all": g * n_ctx + c, "ctx": c, "dp": g}[group]

    def address(member):
        if group == "all":
            return (member // n_ctx, member % n_ctx)
        if group == "ctx":
            return (g, member)
        return (member, c)

    own = pltpu.make_async_copy(x_ref.at[me], out_ref.at[me], own_sem)
    own.start()
    barrier = pltpu.get_barrier_semaphore()
    for offset in range(1, n):
        pl.semaphore_signal(
            barrier, 1, device_id=address((me + offset) % n), device_id_type=MESH_ID
        )
    pl.semaphore_wait(barrier, n - 1)

    def link(offset, source, target):
        return pltpu.make_async_remote_copy(
            src_ref=x_ref.at[target],
            dst_ref=out_ref.at[source],
            send_sem=send_sem.at[offset],
            recv_sem=recv_sem.at[offset],
            device_id=address(target),
            device_id_type=MESH_ID,
        )

    sent = []
    for offset in range(1, n):
        copy = link(offset, me, (me + offset) % n)
        copy.start()
        sent.append(copy)
    for offset in range(1, n):
        link(offset, (me + n - offset) % n, me).wait_recv()
    for copy in sent:
        copy.wait_send()
    own.wait()


def exchange(x, group, collective_id):
    n = x.shape[0]
    space = pltpu.VMEM
    return pl.pallas_call(
        functools.partial(_exchange_kernel, group=group),
        out_shape=jax.ShapeDtypeStruct(x.shape, x.dtype),
        in_specs=[pl.BlockSpec(memory_space=space)],
        out_specs=pl.BlockSpec(memory_space=space),
        scratch_shapes=[
            pltpu.SemaphoreType.DMA(()),
            pltpu.SemaphoreType.DMA((n,)),
            pltpu.SemaphoreType.DMA((n,)),
        ],
        compiler_params=pltpu.CompilerParams(collective_id=collective_id, has_side_effects=True),
    )(x)


def block_moves(n_dp, n_ctx):
    count = n_dp * n_ctx
    return [(f, (f % n_dp) * n_ctx + f // n_dp) for f in range(count)]


def fetch_out_rows(w_out):
    n_dp = lax.axis_size("dp")
    n_ctx = lax.axis_size("ctx")
    moved = lax.ppermute(w_out.astype(jnp.bfloat16), ("dp", "ctx"), perm=block_moves(n_dp, n_ctx))
    return lax.all_gather(moved, "dp", axis=0, tiled=True)


def return_out_rows(grad_out_rows):
    n_dp = lax.axis_size("dp")
    n_ctx = lax.axis_size("ctx")
    part = lax.psum_scatter(grad_out_rows, "dp", scatter_dimension=0, tiled=True)
    back = [(b, a) for a, b in block_moves(n_dp, n_ctx)]
    return lax.ppermute(part, ("dp", "ctx"), perm=back)


def pack_rows(vector, lanes):
    size = vector.shape[0]
    total = -(-size // (16 * lanes)) * 16 * lanes
    return jnp.pad(vector, (0, total - size)).reshape(-1, lanes)


def fetch_small(b_qkv, b_out, b_fc2, ln_gain, ln_shift, b_fc1):
    pieces = (b_qkv, b_out, b_fc2, ln_gain, ln_shift, b_fc1)
    n_dp = lax.axis_size("dp")
    n_ctx = lax.axis_size("ctx")
    packed = pack_rows(jnp.concatenate([p.astype(jnp.bfloat16) for p in pieces]), 128)
    over_dp = exchange(jnp.broadcast_to(packed[None], (n_dp,) + packed.shape), "dp", 4)
    over_all = exchange(jnp.broadcast_to(over_dp[None], (n_ctx,) + over_dp.shape), "ctx", 8)
    table = over_all.transpose(1, 0, 2, 3).reshape(n_dp * n_ctx, -1)
    result = []
    offset = 0
    for p in pieces:
        result.append(table[:, offset : offset + p.shape[0]])
        offset += p.shape[0]
    return result


def reduce_small(small):
    n_dp = lax.axis_size("dp")
    n_ctx = lax.axis_size("ctx")
    count, width = small.shape
    packed = jax.vmap(lambda row: pack_rows(row, 128))(small)
    packed = packed.reshape((n_dp, n_ctx) + packed.shape[1:]).transpose(1, 0, 2, 3)
    over_ctx = jnp.sum(exchange(packed, "ctx", 7), axis=0)
    over_dp = jnp.sum(exchange(over_ctx, "dp", 9), axis=0)
    return over_dp.reshape(-1)[:width]


def fetch_heads(w_qkv, w_fc1, w_fc2, tokens):
    dp_count = lax.axis_size("dp")
    ctx_count = lax.axis_size("ctx")
    rows_piece = w_qkv.shape[0]
    head_width = D // ctx_count
    unit = FF // (dp_count * ctx_count)
    qkv_piece = w_qkv.astype(jnp.bfloat16).reshape(rows_piece, 3, ctx_count, head_width)
    fc1_piece = w_fc1.astype(jnp.bfloat16).reshape(rows_piece, dp_count, ctx_count, unit)
    pieces = jnp.concatenate(
        [
            qkv_piece.transpose(2, 0, 1, 3).reshape(ctx_count, rows_piece, 3 * head_width),
            fc1_piece.transpose(2, 0, 1, 3).reshape(ctx_count, rows_piece, dp_count * unit),
        ],
        axis=2,
    )
    sent = exchange(pieces, "ctx", 5).reshape(ctx_count * rows_piece, -1)
    sent, tokens = lax.optimization_barrier((sent, tokens))
    cols, fc2_rows = (
        lax.all_gather(sent, "dp", axis=0, tiled=True),
        lax.all_gather(w_fc2.astype(jnp.bfloat16), "dp", axis=0, tiled=True),
    )
    return (cols, fc2_rows, tokens)


def return_heads(owned_parts):
    dp_count = lax.axis_size("dp")
    ctx_count = lax.axis_size("ctx")
    head_width = D // ctx_count
    unit = FF // (dp_count * ctx_count)
    rows_piece = owned_parts.shape[0] // ctx_count
    got = exchange(owned_parts.reshape(ctx_count, rows_piece, -1), "ctx", 6)
    qkv = got[:, :, : 3 * head_width].reshape(ctx_count, rows_piece, 3, head_width)
    fc1 = got[:, :, 3 * head_width :].reshape(ctx_count, rows_piece, dp_count, unit)
    return (
        qkv.transpose(1, 2, 0, 3).reshape(rows_piece, 3 * D).astype(jnp.float32),
        fc1.transpose(1, 2, 0, 3).reshape(rows_piece, FF).astype(jnp.float32),
    )


def head_plan(
    ring,
    tokens,
    lengths,
    w_qkv,
    b_qkv,
    w_out,
    b_out,
    w_fc1,
    b_fc1,
    w_fc2,
    b_fc2,
    ln_gain,
    ln_shift,
    cotangent,
):
    rows_here = tokens.shape[0]
    rows_piece = w_qkv.shape[0]
    dp_count = lax.axis_size("dp")
    ctx_count = lax.axis_size("ctx")
    count = dp_count * ctx_count
    group = rows_here * ctx_count
    head_width = D // ctx_count
    local_heads = HEADS // ctx_count
    unit = FF // (dp_count * ctx_count)
    here = lax.axis_index("ctx")
    group_rows = jnp.arange(group, dtype=jnp.int32)
    seg, positions = segment_info(lengths[0], group_rows)
    cosine, sine = rotary_tables(positions)
    qkv_bias, out_bias, fc2_bias, gain_low, shift_low, fc1_table = fetch_small(
        b_qkv, b_out, b_fc2, ln_gain, ln_shift, b_fc1
    )
    qkv_bias = qkv_bias.reshape(3 * D)
    out_bias = out_bias.reshape(D)
    fc2_bias = fc2_bias.reshape(D)
    gain_low = gain_low.reshape(D)
    shift_low = shift_low.reshape(D)
    fc1_bias = lax.dynamic_index_in_dim(
        fc1_table.reshape(dp_count, ctx_count, unit), here, 1, keepdims=False
    ).reshape(dp_count * unit)
    out_rows = fetch_out_rows(w_out)
    cols, fc2_rows, tokens = fetch_heads(w_qkv, w_fc1, w_fc2, tokens)
    gain32 = gain_low.astype(jnp.float32)
    shift32 = shift_low.astype(jnp.float32)
    inputs = tokens.astype(jnp.float32)
    normed, scaled, _ = norm_parts(inputs, gain32, shift32)
    tokens_group = ring_all_gather(tokens, ring, 0)
    late_dy, tokens_group = lax.optimization_barrier((cotangent, tokens_group))
    dy_group = lax.all_gather(late_dy, "ctx", axis=0, tiled=True)
    hidden_group = norm_parts(tokens_group.astype(jnp.float32), gain32, shift32)[2].astype(
        jnp.bfloat16
    )
    bias_cols = lax.dynamic_slice_in_dim(
        qkv_bias.reshape(3, D), here * head_width, head_width, 1
    ).reshape(3 * head_width)
    both = jnp.dot(hidden_group, cols, preferred_element_type=jnp.float32) + jnp.concatenate(
        [bias_cols, fc1_bias]
    ).astype(jnp.float32)
    qkv = both[:, : 3 * head_width]
    pre = both[:, 3 * head_width :]
    shape = (group, local_heads, HEAD_DIM)
    query = rotate(qkv[:, :head_width].reshape(shape), cosine, sine).astype(jnp.bfloat16)
    keys = rotate(qkv[:, head_width : 2 * head_width].reshape(shape), cosine, sine).astype(
        jnp.bfloat16
    )
    values = qkv[:, 2 * head_width :].reshape(shape).astype(jnp.bfloat16)
    q_heads = query.transpose(1, 0, 2)
    k_heads = keys.transpose(1, 0, 2)
    v_heads = values.transpose(1, 0, 2)
    attended_heads, log_total = attention_forward(q_heads, k_heads, v_heads, seg)
    attended = attended_heads.transpose(1, 0, 2).reshape(group, head_width).astype(jnp.bfloat16)
    act = gelu_tanh(pre).astype(jnp.bfloat16)
    branches = ring_reduce_scatter(
        jnp.dot(attended, out_rows, preferred_element_type=jnp.float32)
        + jnp.dot(act, fc2_rows, preferred_element_type=jnp.float32),
        ring,
        2,
    )
    block_out = (
        inputs + branches + out_bias.astype(jnp.float32) + fc2_bias.astype(jnp.float32)
    ).astype(jnp.bfloat16)
    grad_out32 = cotangent.astype(jnp.float32)
    grad_b_fc2 = jnp.sum(grad_out32, axis=0)
    grad_fc2_part = jnp.einsum("tf,td->fd", act, dy_group, preferred_element_type=jnp.float32)
    d_act = jnp.einsum("td,fd->tf", dy_group, fc2_rows, preferred_element_type=jnp.float32)
    d_pre = (d_act * gelu_slope(pre)).astype(jnp.bfloat16)
    grad_bfc1_part = jnp.sum(d_pre.astype(jnp.float32), axis=0)
    grad_out_rows = jnp.einsum("tc,td->cd", attended, dy_group, preferred_element_type=jnp.float32)
    owned_w_out = return_out_rows(grad_out_rows)
    d_attended = (
        jnp.einsum("td,cd->tc", dy_group, out_rows, preferred_element_type=jnp.float32)
        .astype(jnp.bfloat16)
        .reshape(shape)
    )
    d_heads = d_attended.transpose(1, 0, 2)
    delta = jnp.sum(d_heads.astype(jnp.float32) * attended_heads, axis=2, keepdims=True)
    dq_heads, dk_heads, dv_heads = attention_backward(
        q_heads, k_heads, v_heads, d_heads, log_total, delta, seg
    )
    d_query = dq_heads.transpose(1, 0, 2)
    d_keys = dk_heads.transpose(1, 0, 2)
    d_values = dv_heads.transpose(1, 0, 2)
    d_query = rotate_back(d_query, cosine, sine).reshape(group, head_width)
    d_keys = rotate_back(d_keys, cosine, sine).reshape(group, head_width)
    d_qkv = jnp.concatenate([d_query, d_keys, d_values.reshape(group, head_width)], axis=1).astype(
        jnp.bfloat16
    )
    d_both = jnp.concatenate([d_qkv, d_pre], axis=1)
    bias_part = jnp.sum(d_qkv.astype(jnp.float32), axis=0).reshape(3, head_width)
    d_hidden = ring_reduce_scatter(
        jnp.einsum("tc,dc->td", d_both, cols, preferred_element_type=jnp.float32), ring, 3
    )
    weight_parts = jnp.einsum(
        "td,tc->dc", hidden_group, d_both, preferred_element_type=jnp.float32
    ).astype(jnp.bfloat16)
    owned_parts = lax.psum_scatter(weight_parts, "dp", scatter_dimension=0, tiled=True)
    split_qkv, split_fc1 = return_heads(owned_parts)
    d_hidden, split_qkv, split_fc1 = lax.optimization_barrier((d_hidden, split_qkv, split_fc1))
    grad_gain, grad_shift, d_inputs = norm_back(d_hidden, normed, scaled, gain32)
    grad_tokens = (grad_out32 + d_inputs).astype(jnp.bfloat16)
    owned_fc2 = lax.psum_scatter(
        grad_fc2_part.astype(jnp.bfloat16), "dp", scatter_dimension=0, tiled=True
    ).astype(jnp.float32)
    full_bqkv = lax.dynamic_update_slice_in_dim(
        jnp.zeros((3, D), jnp.float32), bias_part, here * head_width, 1
    )
    full_bfc1 = lax.dynamic_update_slice_in_dim(
        jnp.zeros((dp_count, ctx_count, unit), jnp.float32),
        grad_bfc1_part.reshape(dp_count, 1, unit),
        here,
        1,
    )
    small = jnp.concatenate(
        [
            full_bqkv.reshape(count, -1),
            grad_b_fc2.reshape(count, -1),
            grad_gain.reshape(count, -1),
            grad_shift.reshape(count, -1),
            full_bfc1.reshape(count, -1),
        ],
        axis=1,
    )
    owned_small = reduce_small(small)
    cuts = [0, 3 * D // count, D // count, D // count, D // count, FF // count]
    bounds = [sum(cuts[: i + 1]) for i in range(len(cuts))]
    owned_bqkv, owned_bout, owned_gain, owned_shift, owned_bfc1 = [
        owned_small[bounds[i] : bounds[i + 1]] for i in range(5)
    ]
    return (
        block_out,
        grad_tokens,
        split_qkv.reshape(rows_piece, 3 * D),
        owned_bqkv,
        owned_w_out,
        owned_bout,
        split_fc1.reshape(rows_piece, FF),
        owned_bfc1,
        owned_fc2,
        owned_bout,
        owned_gain,
        owned_shift,
    )


def body(
    ring,
    tokens,
    lengths,
    w_qkv,
    b_qkv,
    w_out,
    b_out,
    w_fc1,
    b_fc1,
    w_fc2,
    b_fc2,
    ln_gain,
    ln_shift,
    cotangent,
):
    return head_plan(
        ring,
        tokens,
        lengths,
        w_qkv,
        b_qkv,
        w_out,
        b_out,
        w_fc1,
        b_fc1,
        w_fc2,
        b_fc2,
        ln_gain,
        ln_shift,
        cotangent,
    )


def solution(mesh):
    in_specs = (
        P(("dp", "ctx"), None),
        P("dp", None),
        P(("dp", "ctx"), None),
        P(("dp", "ctx")),
        P(("dp", "ctx"), None),
        P(("dp", "ctx")),
        P(("dp", "ctx"), None),
        P(("dp", "ctx")),
        P(("dp", "ctx"), None),
        P(("dp", "ctx")),
        P(("dp", "ctx")),
        P(("dp", "ctx")),
        P(("dp", "ctx"), None),
    )
    out_specs = (
        P(("dp", "ctx"), None),
        P(("dp", "ctx"), None),
        P(("dp", "ctx"), None),
        P(("dp", "ctx")),
        P(("dp", "ctx"), None),
        P(("dp", "ctx")),
        P(("dp", "ctx"), None),
        P(("dp", "ctx")),
        P(("dp", "ctx"), None),
        P(("dp", "ctx")),
        P(("dp", "ctx")),
        P(("dp", "ctx")),
    )
    ring = ring_of(mesh)
    return jax.shard_map(functools.partial(body, ring), mesh=mesh, in_specs=in_specs, out_specs=out_specs, check_vma=False)
```

```python
import functools
import math

import jax
import jax.numpy as jnp
from jax import lax
from jax.experimental import pallas as pl
from jax.experimental.pallas import tpu as pltpu
from jax.sharding import PartitionSpec as P

D = 2048
HEADS = 32
HEAD_DIM = 64
ROT = 32
FF = 8192


EPS = 1e-05
GELU_COEF = math.sqrt(2.0 / math.pi)
NEGATIVE = -1e30


def norm_parts(inputs, gain, shift):
    mean = jnp.mean(inputs, axis=-1, keepdims=True)
    centred = inputs - mean
    var = jnp.mean(centred * centred, axis=-1, keepdims=True)
    scaled = lax.rsqrt(var + EPS)
    normed = centred * scaled
    return (normed, scaled, normed * gain + shift)


def norm_back(d_hidden, normed, scaled, gain32):
    grad_gain = jnp.sum(d_hidden * normed, axis=0)
    grad_shift = jnp.sum(d_hidden, axis=0)
    d_normed = d_hidden * gain32
    d_inputs = scaled * (
        d_normed
        - jnp.mean(d_normed, axis=-1, keepdims=True)
        - normed * jnp.mean(d_normed * normed, axis=-1, keepdims=True)
    )
    return (grad_gain, grad_shift, d_inputs)


def gelu_tanh(pre):
    return 0.5 * pre * (1.0 + jnp.tanh(GELU_COEF * (pre + 0.044715 * pre * pre * pre)))


def gelu_slope(pre):
    tangent = jnp.tanh(GELU_COEF * (pre + 0.044715 * pre * pre * pre))
    return 0.5 * (1.0 + tangent) + 0.5 * pre * (1.0 - tangent * tangent) * GELU_COEF * (
        1.0 + 3.0 * 0.044715 * pre * pre
    )


def rotary_tables(positions):
    half = ROT // 2
    freq = jnp.exp(jnp.arange(half, dtype=jnp.float32) * (-2.0 * math.log(10000.0) / ROT))
    angle = positions.astype(jnp.float32)[:, None] * freq[None, :]
    return (jnp.cos(angle)[:, None, :], jnp.sin(angle)[:, None, :])


def rotate(heads, cosine, sine):
    half = ROT // 2
    first = heads[..., :half]
    second = heads[..., half:ROT]
    return jnp.concatenate(
        [first * cosine - second * sine, second * cosine + first * sine, heads[..., ROT:]], axis=-1
    )


def rotate_back(grads, cosine, sine):
    half = ROT // 2
    first = grads[..., :half]
    second = grads[..., half:ROT]
    return jnp.concatenate(
        [first * cosine + second * sine, second * cosine - first * sine, grads[..., ROT:]], axis=-1
    )


def segment_info(lengths_row, rows):
    ends = jnp.cumsum(lengths_row)
    starts = ends - lengths_row
    seg = jnp.sum((rows[:, None] >= ends[None, :]).astype(jnp.int32), axis=1)
    onehot = seg[:, None] == jnp.arange(lengths_row.shape[0], dtype=jnp.int32)[None, :]
    first_rows = jnp.sum(jnp.where(onehot, starts[None, :], 0), axis=1)
    return (seg, rows - first_rows)


TRANS_B = (((1,), (1,)), ((), ()))


def _allowed(segq_ref, segk_ref, i, j, tq, tk, causal):
    same = segq_ref[...] == segk_ref[...]
    if not causal:
        return same
    rows = i * tq + lax.broadcasted_iota(jnp.int32, (tq, tk), 0)
    cols = j * tk + lax.broadcasted_iota(jnp.int32, (tq, tk), 1)
    return same & (cols <= rows)


def _fwd_kernel(qi_ref, kj_ref, q_ref, k_ref, v_ref, segq_ref, segk_ref, o_ref, lse_ref, m_sc, acc_sc, *, tq, tk, scale):
    t = pl.program_id(1)
    i = qi_ref[t]
    j = kj_ref[t]
    dim = o_ref.shape[2]

    @pl.when(j == 0)
    def _():
        m_sc[...] = jnp.full_like(m_sc, NEGATIVE)
        acc_sc[...] = jnp.zeros_like(acc_sc)

    def absorb(causal):
        q = q_ref[0]
        k = k_ref[0]
        s = lax.dot_general(q, k, TRANS_B, preferred_element_type=jnp.float32) * scale
        s = jnp.where(_allowed(segq_ref, segk_ref, i, j, tq, tk, causal), s, -jnp.inf)
        m_prev = m_sc[...]
        lanes = s.shape[1]
        folded = s[:, :128]
        for start in range(128, lanes, 128):
            folded = jnp.maximum(folded, s[:, start : start + 128])
        m_new = jnp.maximum(m_prev, jnp.max(folded, axis=1, keepdims=True))
        factor = jnp.exp(m_prev - m_new)
        p = jnp.exp(s - m_new)
        acc_sc[...] = acc_sc[...] * factor + jnp.dot(
            p.astype(jnp.bfloat16), v_ref[0], preferred_element_type=jnp.float32
        )
        m_sc[...] = m_new

    @pl.when(j < i)
    def _():
        absorb(False)

    @pl.when(j == i)
    def _():
        absorb(True)
        acc = acc_sc[...]
        total = acc[:, dim : dim + 1]
        o_ref[0] = acc[:, :dim] / total
        lse_ref[0] = m_sc[...] + jnp.log(total)


def _schedule(count, queries_outer):
    if queries_outer:
        pairs = [(i, j) for i in range(count) for j in range(i + 1)]
    else:
        pairs = [(i, j) for j in range(count) for i in range(j, count)]
    return (
        jnp.asarray([p[0] for p in pairs], jnp.int32),
        jnp.asarray([p[1] for p in pairs], jnp.int32),
    )


def attention_forward(q, k, v, seg, block=512):
    heads, total, dim = q.shape
    count = total // block
    scale = 1.0 / math.sqrt(dim)
    segq = seg.reshape(total, 1)
    segk = seg.reshape(1, total)
    qi, kj = _schedule(count, True)
    steps = qi.shape[0]
    lanes = 2 * dim
    v_ext = jnp.concatenate(
        [v, jnp.ones((heads, total, 1), v.dtype), jnp.zeros((heads, total, lanes - dim - 1), v.dtype)],
        axis=2,
    )

    return pl.pallas_call(
        functools.partial(_fwd_kernel, tq=block, tk=block, scale=scale),
        out_shape=(
            jax.ShapeDtypeStruct((heads, total, dim), jnp.float32),
            jax.ShapeDtypeStruct((heads, total, 1), jnp.float32),
        ),
        grid_spec=pltpu.PrefetchScalarGridSpec(
            num_scalar_prefetch=2,
            grid=(heads, steps),
            in_specs=[
                pl.BlockSpec((1, block, dim), lambda h, t, qi, kj: (h, qi[t], 0)),
                pl.BlockSpec((1, block, dim), lambda h, t, qi, kj: (h, kj[t], 0)),
                pl.BlockSpec((1, block, lanes), lambda h, t, qi, kj: (h, kj[t], 0)),
                pl.BlockSpec((block, 1), lambda h, t, qi, kj: (qi[t], 0)),
                pl.BlockSpec((1, block), lambda h, t, qi, kj: (0, kj[t])),
            ],
            out_specs=[
                pl.BlockSpec((1, block, dim), lambda h, t, qi, kj: (h, qi[t], 0)),
                pl.BlockSpec((1, block, 1), lambda h, t, qi, kj: (h, qi[t], 0)),
            ],
            scratch_shapes=[
                pltpu.VMEM((block, 1), jnp.float32),
                pltpu.VMEM((block, lanes), jnp.float32),
            ],
        ),
        cost_estimate=pl.CostEstimate(
            flops=2 * heads * total * total * dim,
            transcendentals=heads * total * total // 2,
            bytes_accessed=heads * total * dim * 10,
        ),
    )(qi, kj, q, k, v_ext, segq, segk)


def _bwd_kernel(qi_ref, kj_ref, q_ref, k_ref, v_ref, do_ref, lse_ref, delta_ref, segq_ref, segk_ref, dq_ref, dk_ref, dv_ref, dk_sc, dv_sc, *, tq, tk, scale, count):
    t = pl.program_id(1)
    i = qi_ref[t]
    j = kj_ref[t]

    @pl.when(t == 0)
    def _():
        dq_ref[...] = jnp.zeros_like(dq_ref)

    @pl.when(i == j)
    def _():
        dk_sc[...] = jnp.zeros_like(dk_sc)
        dv_sc[...] = jnp.zeros_like(dv_sc)

    def absorb(causal):
        q = q_ref[0]
        k = k_ref[0]
        do = do_ref[0]
        s = lax.dot_general(q, k, TRANS_B, preferred_element_type=jnp.float32) * scale
        s = jnp.where(_allowed(segq_ref, segk_ref, i, j, tq, tk, causal), s, -jnp.inf)
        spread = tk // lse_ref.shape[2]
        p = jnp.exp(s - jnp.concatenate([lse_ref[0]] * spread, axis=1))
        dp = lax.dot_general(do, v_ref[0], TRANS_B, preferred_element_type=jnp.float32)
        ds = (p * (dp - jnp.concatenate([delta_ref[0]] * spread, axis=1))).astype(jnp.bfloat16)
        dv_sc[...] += jnp.dot(do.T, p.astype(jnp.bfloat16), preferred_element_type=jnp.float32)
        dk_sc[...] += jnp.dot(q.T, ds, preferred_element_type=jnp.float32)
        rows = pl.ds(pl.multiple_of(i * tq, tq), tq)
        dq_ref[0, rows, :] += lax.dot(ds, k, preferred_element_type=jnp.float32) * scale

    @pl.when(j < i)
    def _():
        absorb(False)

    @pl.when(j == i)
    def _():
        absorb(True)

    @pl.when(i == count - 1)
    def _():
        dk_ref[0] = dk_sc[...].T * scale
        dv_ref[0] = dv_sc[...].T


def attention_backward(q, k, v, do, lse, delta, seg, block=512):
    heads, total, dim = q.shape
    count = total // block
    scale = 1.0 / math.sqrt(dim)
    segq = seg.reshape(total, 1)
    segk = seg.reshape(1, total)
    qi, kj = _schedule(count, False)
    lse = jnp.broadcast_to(lse, (heads, total, 128))
    delta = jnp.broadcast_to(delta, (heads, total, 128))
    steps = qi.shape[0]

    def q_map(h, t, qi, kj):
        return (h, qi[t], 0)

    def k_map(h, t, qi, kj):
        return (h, kj[t], 0)

    return pl.pallas_call(
        functools.partial(_bwd_kernel, tq=block, tk=block, scale=scale, count=count),
        out_shape=(
            jax.ShapeDtypeStruct((heads, total, dim), jnp.float32),
            jax.ShapeDtypeStruct((heads, total, dim), jnp.float32),
            jax.ShapeDtypeStruct((heads, total, dim), jnp.float32),
        ),
        grid_spec=pltpu.PrefetchScalarGridSpec(
            num_scalar_prefetch=2,
            grid=(heads, steps),
            in_specs=[
                pl.BlockSpec((1, block, dim), q_map),
                pl.BlockSpec((1, block, dim), k_map),
                pl.BlockSpec((1, block, dim), k_map),
                pl.BlockSpec((1, block, dim), q_map),
                pl.BlockSpec((1, block, 128), q_map),
                pl.BlockSpec((1, block, 128), q_map),
                pl.BlockSpec((block, 1), lambda h, t, qi, kj: (qi[t], 0)),
                pl.BlockSpec((1, block), lambda h, t, qi, kj: (0, kj[t])),
            ],
            out_specs=[
                pl.BlockSpec((1, total, dim), lambda h, t, qi, kj: (h, 0, 0)),
                pl.BlockSpec((1, block, dim), k_map),
                pl.BlockSpec((1, block, dim), k_map),
            ],
            scratch_shapes=[
                pltpu.VMEM((dim, block), jnp.float32),
                pltpu.VMEM((dim, block), jnp.float32),
            ],
        ),
        cost_estimate=pl.CostEstimate(
            flops=5 * heads * total * total * dim,
            transcendentals=heads * total * total // 2,
            bytes_accessed=heads * total * dim * 24,
        ),
    )(qi, kj, q, k, v, do, lse, delta, segq, segk)


MESH_ID = pl.DeviceIdType.MESH


class Ring:
    def __init__(self, size, a_stride, b_stride):
        self.size = size
        self.half = size // 2
        self.a_stride = a_stride
        self.b_stride = b_stride

    def position(self, c):
        a = (c // self.a_stride) % self.half
        b = (c // self.b_stride) % 2
        return a + b * (2 * self.half - 1 - 2 * a)

    def device(self, pos):
        pos = pos % self.size
        b = pos // self.half
        a = pos + b * (2 * self.half - 1 - 2 * pos)
        return a * self.a_stride + b * self.b_stride


def ring_of(mesh):
    size = mesh.shape["ctx"]
    devices = list(mesh.devices.reshape(-1, size)[0])
    try:
        coords = [tuple(d.coords) for d in devices]
    except AttributeError:
        coords = None
    if coords and size % 2 == 0 and size >= 4:
        for b_stride in range(1, size):
            for a_stride in range(1, size):
                ring = Ring(size, a_stride, b_stride)
                order = [ring.device(p) for p in range(size)]
                if sorted(order) != list(range(size)):
                    continue
                hops = [
                    sum(abs(x - y) for x, y in zip(coords[order[p]], coords[order[(p + 1) % size]]))
                    for p in range(size)
                ]
                if max(hops) == 1:
                    return ring
    return Ring(size, 2, 1) if size % 2 == 0 and size >= 4 else None


def _barrier(g, left, right):
    barrier = pltpu.get_barrier_semaphore()
    for other in (left, right):
        pl.semaphore_signal(barrier, 1, device_id=(g, other), device_id_type=MESH_ID)
    pl.semaphore_wait(barrier, 2)


def _gather_kernel(x_ref, y_ref, own_sem, send_sem, recv_sem, *, ring, rows):
    n = ring.size
    half = rows // 2
    g = lax.axis_index("dp")
    c = lax.axis_index("ctx")
    pos = ring.position(c)
    right = ring.device(pos + 1)
    left = ring.device(pos + n - 1)
    own = pltpu.make_async_copy(x_ref, y_ref.at[pl.ds(c * rows, rows)], own_sem)
    own.start()
    _barrier(g, left, right)

    def link(direction, step, origin, source):
        offset = origin * rows + direction * half
        return pltpu.make_async_remote_copy(
            src_ref=source,
            dst_ref=y_ref.at[pl.ds(offset, half)],
            send_sem=send_sem.at[direction, step],
            recv_sem=recv_sem.at[direction, step],
            device_id=(g, right if direction == 0 else left),
            device_id_type=MESH_ID,
        )

    sent = []
    for step in range(n - 1):
        origins = (ring.device(pos - step + n), ring.device(pos + step))
        for direction in (0, 1):
            origin = origins[direction]
            if step == 0:
                source = x_ref.at[pl.ds(direction * half, half)]
            else:
                link(direction, step - 1, origin, None if False else y_ref.at[pl.ds(origin * rows + direction * half, half)]).wait_recv()
                source = y_ref.at[pl.ds(origin * rows + direction * half, half)]
            copy = link(direction, step, origin, source)
            copy.start()
            sent.append(copy)
    last = n - 2
    for direction, origin in ((0, ring.device(pos - last - 1 + n)), (1, ring.device(pos + last + 1))):
        link(direction, last, origin, y_ref.at[pl.ds(origin * rows + direction * half, half)]).wait_recv()
    for copy in sent:
        copy.wait_send()
    own.wait()


def ring_all_gather(x, ring, collective_id):
    rows, cols = x.shape
    n = ring.size
    return pl.pallas_call(
        functools.partial(_gather_kernel, ring=ring, rows=rows),
        out_shape=jax.ShapeDtypeStruct((n * rows, cols), x.dtype),
        in_specs=[pl.BlockSpec(memory_space=pl.ANY)],
        out_specs=pl.BlockSpec(memory_space=pl.ANY),
        scratch_shapes=[
            pltpu.SemaphoreType.DMA(()),
            pltpu.SemaphoreType.DMA((2, n - 1)),
            pltpu.SemaphoreType.DMA((2, n - 1)),
        ],
        compiler_params=pltpu.CompilerParams(collective_id=collective_id, has_side_effects=True),
    )(x)


def _scatter_kernel(p_ref, out_ref, recv_buf, send_buf, send_sem, recv_sem, *, ring, rows, parts):
    n = ring.size
    half = rows // 2
    piece = half // parts
    g = lax.axis_index("dp")
    c = lax.axis_index("ctx")
    pos = ring.position(c)
    right = ring.device(pos + 1)
    left = ring.device(pos + n - 1)
    _barrier(g, left, right)

    def link(direction, step, part):
        window = pl.ds(part * piece, piece)
        return pltpu.make_async_remote_copy(
            src_ref=send_buf.at[direction, step, window],
            dst_ref=recv_buf.at[direction, step, window],
            send_sem=send_sem.at[direction, step, part],
            recv_sem=recv_sem.at[direction, step, part],
            device_id=(g, right if direction == 0 else left),
            device_id_type=MESH_ID,
        )

    sent = []
    for step in range(n - 1):
        targets = (ring.device(pos - 1 - step + 2 * n), ring.device(pos + 1 + step))
        for part in range(parts):
            for direction in (0, 1):
                start = pl.multiple_of(
                    targets[direction] * rows + direction * half + part * piece, piece
                )
                window = pl.ds(part * piece, piece)
                total = p_ref[pl.ds(start, piece), :].astype(jnp.float32)
                if step > 0:
                    link(direction, step - 1, part).wait_recv()
                    total = total + recv_buf[direction, step - 1, window].astype(jnp.float32)
                send_buf[direction, step, window] = total.astype(send_buf.dtype)
                copy = link(direction, step, part)
                copy.start()
                sent.append(copy)
    for part in range(parts):
        for direction in (0, 1):
            link(direction, n - 2, part).wait_recv()
            start = pl.multiple_of(c * rows + direction * half + part * piece, piece)
            window = pl.ds(part * piece, piece)
            out_ref[pl.ds(direction * half + part * piece, piece), :] = (
                p_ref[pl.ds(start, piece), :].astype(jnp.float32)
                + recv_buf[direction, n - 2, window].astype(jnp.float32)
            ).astype(out_ref.dtype)
    for copy in sent:
        copy.wait_send()


def ring_reduce_scatter(p, ring, collective_id, out_dtype=jnp.float32, wire=jnp.bfloat16, parts=2):
    total_rows, cols = p.shape
    n = ring.size
    rows = total_rows // n
    half = rows // 2
    return pl.pallas_call(
        functools.partial(_scatter_kernel, ring=ring, rows=rows, parts=parts),
        out_shape=jax.ShapeDtypeStruct((rows, cols), out_dtype),
        in_specs=[pl.BlockSpec(memory_space=pltpu.VMEM)],
        out_specs=pl.BlockSpec(memory_space=pltpu.VMEM),
        scratch_shapes=[
            pltpu.VMEM((2, n - 1, half, cols), wire),
            pltpu.VMEM((2, n - 1, half, cols), wire),
            pltpu.SemaphoreType.DMA((2, n - 1, parts)),
            pltpu.SemaphoreType.DMA((2, n - 1, parts)),
        ],
        compiler_params=pltpu.CompilerParams(
            collective_id=collective_id, has_side_effects=True, vmem_limit_bytes=60 * 1024 * 1024
        ),
    )(p)


def _exchange_kernel(x_ref, out_ref, own_sem, send_sem, recv_sem, *, group):
    n = x_ref.shape[0]
    g = lax.axis_index("dp")
    c = lax.axis_index("ctx")
    n_ctx = lax.axis_size("ctx")
    me = {"all": g * n_ctx + c, "ctx": c, "dp": g}[group]

    def address(member):
        if group == "all":
            return (member // n_ctx, member % n_ctx)
        if group == "ctx":
            return (g, member)
        return (member, c)

    own = pltpu.make_async_copy(x_ref.at[me], out_ref.at[me], own_sem)
    own.start()
    barrier = pltpu.get_barrier_semaphore()
    for offset in range(1, n):
        pl.semaphore_signal(
            barrier, 1, device_id=address((me + offset) % n), device_id_type=MESH_ID
        )
    pl.semaphore_wait(barrier, n - 1)

    def link(offset, source, target):
        return pltpu.make_async_remote_copy(
            src_ref=x_ref.at[target],
            dst_ref=out_ref.at[source],
            send_sem=send_sem.at[offset],
            recv_sem=recv_sem.at[offset],
            device_id=address(target),
            device_id_type=MESH_ID,
        )

    sent = []
    for offset in range(1, n):
        copy = link(offset, me, (me + offset) % n)
        copy.start()
        sent.append(copy)
    for offset in range(1, n):
        link(offset, (me + n - offset) % n, me).wait_recv()
    for copy in sent:
        copy.wait_send()
    own.wait()


def exchange(x, group, collective_id):
    n = x.shape[0]
    space = pltpu.VMEM
    return pl.pallas_call(
        functools.partial(_exchange_kernel, group=group),
        out_shape=jax.ShapeDtypeStruct(x.shape, x.dtype),
        in_specs=[pl.BlockSpec(memory_space=space)],
        out_specs=pl.BlockSpec(memory_space=space),
        scratch_shapes=[
            pltpu.SemaphoreType.DMA(()),
            pltpu.SemaphoreType.DMA((n,)),
            pltpu.SemaphoreType.DMA((n,)),
        ],
        compiler_params=pltpu.CompilerParams(collective_id=collective_id, has_side_effects=True),
    )(x)


def block_moves(n_dp, n_ctx):
    count = n_dp * n_ctx
    return [(f, (f % n_dp) * n_ctx + f // n_dp) for f in range(count)]


def fetch_out_rows(w_out):
    n_dp = lax.axis_size("dp")
    n_ctx = lax.axis_size("ctx")
    moved = lax.ppermute(w_out.astype(jnp.bfloat16), ("dp", "ctx"), perm=block_moves(n_dp, n_ctx))
    return lax.all_gather(moved, "dp", axis=0, tiled=True)


def return_out_rows(grad_out_rows):
    n_dp = lax.axis_size("dp")
    n_ctx = lax.axis_size("ctx")
    part = lax.psum_scatter(grad_out_rows, "dp", scatter_dimension=0, tiled=True)
    back = [(b, a) for a, b in block_moves(n_dp, n_ctx)]
    return lax.ppermute(part, ("dp", "ctx"), perm=back)


def pack_rows(vector, lanes):
    size = vector.shape[0]
    total = -(-size // (16 * lanes)) * 16 * lanes
    return jnp.pad(vector, (0, total - size)).reshape(-1, lanes)


def fetch_small(b_qkv, b_out, b_fc2, ln_gain, ln_shift, b_fc1):
    pieces = (b_qkv, b_out, b_fc2, ln_gain, ln_shift, b_fc1)
    n_dp = lax.axis_size("dp")
    n_ctx = lax.axis_size("ctx")
    packed = pack_rows(jnp.concatenate([p.astype(jnp.bfloat16) for p in pieces]), 128)
    over_dp = exchange(jnp.broadcast_to(packed[None], (n_dp,) + packed.shape), "dp", 4)
    over_all = exchange(jnp.broadcast_to(over_dp[None], (n_ctx,) + over_dp.shape), "ctx", 8)
    table = over_all.transpose(1, 0, 2, 3).reshape(n_dp * n_ctx, -1)
    result = []
    offset = 0
    for p in pieces:
        result.append(table[:, offset : offset + p.shape[0]])
        offset += p.shape[0]
    return result


def reduce_small(small):
    n_dp = lax.axis_size("dp")
    n_ctx = lax.axis_size("ctx")
    count, width = small.shape
    packed = jax.vmap(lambda row: pack_rows(row, 128))(small)
    packed = packed.reshape((n_dp, n_ctx) + packed.shape[1:]).transpose(1, 0, 2, 3)
    over_ctx = jnp.sum(exchange(packed, "ctx", 7), axis=0)
    over_dp = jnp.sum(exchange(over_ctx, "dp", 9), axis=0)
    return over_dp.reshape(-1)[:width]


def fetch_heads(w_qkv, w_fc1, w_fc2, tokens):
    dp_count = lax.axis_size("dp")
    ctx_count = lax.axis_size("ctx")
    rows_piece = w_qkv.shape[0]
    head_width = D // ctx_count
    unit = FF // (dp_count * ctx_count)
    qkv_piece = w_qkv.astype(jnp.bfloat16).reshape(rows_piece, 3, ctx_count, head_width)
    fc1_piece = w_fc1.astype(jnp.bfloat16).reshape(rows_piece, dp_count, ctx_count, unit)
    pieces = jnp.concatenate(
        [
            qkv_piece.transpose(2, 0, 1, 3).reshape(ctx_count, rows_piece, 3 * head_width),
            fc1_piece.transpose(2, 0, 1, 3).reshape(ctx_count, rows_piece, dp_count * unit),
        ],
        axis=2,
    )
    sent = exchange(pieces, "ctx", 5).reshape(ctx_count * rows_piece, -1)
    sent, tokens = lax.optimization_barrier((sent, tokens))
    cols, fc2_rows = (
        lax.all_gather(sent, "dp", axis=0, tiled=True),
        lax.all_gather(w_fc2.astype(jnp.bfloat16), "dp", axis=0, tiled=True),
    )
    return (cols, fc2_rows, tokens)


def return_heads(owned_parts):
    dp_count = lax.axis_size("dp")
    ctx_count = lax.axis_size("ctx")
    head_width = D // ctx_count
    unit = FF // (dp_count * ctx_count)
    rows_piece = owned_parts.shape[0] // ctx_count
    got = exchange(owned_parts.reshape(ctx_count, rows_piece, -1), "ctx", 6)
    qkv = got[:, :, : 3 * head_width].reshape(ctx_count, rows_piece, 3, head_width)
    fc1 = got[:, :, 3 * head_width :].reshape(ctx_count, rows_piece, dp_count, unit)
    return (
        qkv.transpose(1, 2, 0, 3).reshape(rows_piece, 3 * D).astype(jnp.float32),
        fc1.transpose(1, 2, 0, 3).reshape(rows_piece, FF).astype(jnp.float32),
    )


def head_plan(
    ring,
    tokens,
    lengths,
    w_qkv,
    b_qkv,
    w_out,
    b_out,
    w_fc1,
    b_fc1,
    w_fc2,
    b_fc2,
    ln_gain,
    ln_shift,
    cotangent,
):
    rows_here = tokens.shape[0]
    rows_piece = w_qkv.shape[0]
    dp_count = lax.axis_size("dp")
    ctx_count = lax.axis_size("ctx")
    count = dp_count * ctx_count
    group = rows_here * ctx_count
    head_width = D // ctx_count
    local_heads = HEADS // ctx_count
    unit = FF // (dp_count * ctx_count)
    here = lax.axis_index("ctx")
    group_rows = jnp.arange(group, dtype=jnp.int32)
    seg, positions = segment_info(lengths[0], group_rows)
    cosine, sine = rotary_tables(positions)
    qkv_bias, out_bias, fc2_bias, gain_low, shift_low, fc1_table = fetch_small(
        b_qkv, b_out, b_fc2, ln_gain, ln_shift, b_fc1
    )
    qkv_bias = qkv_bias.reshape(3 * D)
    out_bias = out_bias.reshape(D)
    fc2_bias = fc2_bias.reshape(D)
    gain_low = gain_low.reshape(D)
    shift_low = shift_low.reshape(D)
    fc1_bias = lax.dynamic_index_in_dim(
        fc1_table.reshape(dp_count, ctx_count, unit), here, 1, keepdims=False
    ).reshape(dp_count * unit)
    out_rows = fetch_out_rows(w_out)
    cols, fc2_rows, tokens = fetch_heads(w_qkv, w_fc1, w_fc2, tokens)
    gain32 = gain_low.astype(jnp.float32)
    shift32 = shift_low.astype(jnp.float32)
    inputs = tokens.astype(jnp.float32)
    normed, scaled, _ = norm_parts(inputs, gain32, shift32)
    tokens_group = ring_all_gather(tokens, ring, 0)
    late_dy, tokens_group = lax.optimization_barrier((cotangent, tokens_group))
    dy_group = lax.all_gather(late_dy, "ctx", axis=0, tiled=True)
    hidden_group = norm_parts(tokens_group.astype(jnp.float32), gain32, shift32)[2].astype(
        jnp.bfloat16
    )
    bias_cols = lax.dynamic_slice_in_dim(
        qkv_bias.reshape(3, D), here * head_width, head_width, 1
    ).reshape(3 * head_width)
    both = jnp.dot(hidden_group, cols, preferred_element_type=jnp.float32) + jnp.concatenate(
        [bias_cols, fc1_bias]
    ).astype(jnp.float32)
    qkv = both[:, : 3 * head_width]
    pre = both[:, 3 * head_width :]
    shape = (group, local_heads, HEAD_DIM)
    query = rotate(qkv[:, :head_width].reshape(shape), cosine, sine).astype(jnp.bfloat16)
    keys = rotate(qkv[:, head_width : 2 * head_width].reshape(shape), cosine, sine).astype(
        jnp.bfloat16
    )
    values = qkv[:, 2 * head_width :].reshape(shape).astype(jnp.bfloat16)
    q_heads = query.transpose(1, 0, 2)
    k_heads = keys.transpose(1, 0, 2)
    v_heads = values.transpose(1, 0, 2)
    attended_heads, log_total = attention_forward(q_heads, k_heads, v_heads, seg)
    attended = attended_heads.transpose(1, 0, 2).reshape(group, head_width).astype(jnp.bfloat16)
    act = gelu_tanh(pre).astype(jnp.bfloat16)
    branches = ring_reduce_scatter(
        jnp.dot(attended, out_rows, preferred_element_type=jnp.float32)
        + jnp.dot(act, fc2_rows, preferred_element_type=jnp.float32),
        ring,
        2,
    )
    block_out = (
        inputs + branches + out_bias.astype(jnp.float32) + fc2_bias.astype(jnp.float32)
    ).astype(jnp.bfloat16)
    grad_out32 = cotangent.astype(jnp.float32)
    grad_b_fc2 = jnp.sum(grad_out32, axis=0)
    grad_fc2_part = jnp.einsum("tf,td->fd", act, dy_group, preferred_element_type=jnp.float32)
    d_act = jnp.einsum("td,fd->tf", dy_group, fc2_rows, preferred_element_type=jnp.float32)
    d_pre = (d_act * gelu_slope(pre)).astype(jnp.bfloat16)
    grad_bfc1_part = jnp.sum(d_pre.astype(jnp.float32), axis=0)
    grad_out_rows = jnp.einsum("tc,td->cd", attended, dy_group, preferred_element_type=jnp.float32)
    owned_w_out = return_out_rows(grad_out_rows)
    d_attended = (
        jnp.einsum("td,cd->tc", dy_group, out_rows, preferred_element_type=jnp.float32)
        .astype(jnp.bfloat16)
        .reshape(shape)
    )
    d_heads = d_attended.transpose(1, 0, 2)
    delta = jnp.sum(d_heads.astype(jnp.float32) * attended_heads, axis=2, keepdims=True)
    dq_heads, dk_heads, dv_heads = attention_backward(
        q_heads, k_heads, v_heads, d_heads, log_total, delta, seg
    )
    d_query = dq_heads.transpose(1, 0, 2)
    d_keys = dk_heads.transpose(1, 0, 2)
    d_values = dv_heads.transpose(1, 0, 2)
    d_query = rotate_back(d_query, cosine, sine).reshape(group, head_width)
    d_keys = rotate_back(d_keys, cosine, sine).reshape(group, head_width)
    d_qkv = jnp.concatenate([d_query, d_keys, d_values.reshape(group, head_width)], axis=1).astype(
        jnp.bfloat16
    )
    d_both = jnp.concatenate([d_qkv, d_pre], axis=1)
    bias_part = jnp.sum(d_qkv.astype(jnp.float32), axis=0).reshape(3, head_width)
    d_hidden = ring_reduce_scatter(
        jnp.einsum("tc,dc->td", d_both, cols, preferred_element_type=jnp.float32), ring, 3
    )
    weight_parts = jnp.einsum(
        "td,tc->dc", hidden_group, d_both, preferred_element_type=jnp.float32
    ).astype(jnp.bfloat16)
    owned_parts = lax.psum_scatter(weight_parts, "dp", scatter_dimension=0, tiled=True)
    split_qkv, split_fc1 = return_heads(owned_parts)
    d_hidden, split_qkv, split_fc1 = lax.optimization_barrier((d_hidden, split_qkv, split_fc1))
    grad_gain, grad_shift, d_inputs = norm_back(d_hidden, normed, scaled, gain32)
    grad_tokens = (grad_out32 + d_inputs).astype(jnp.bfloat16)
    owned_fc2 = lax.psum_scatter(
        grad_fc2_part.astype(jnp.bfloat16), "dp", scatter_dimension=0, tiled=True
    ).astype(jnp.float32)
    full_bqkv = lax.dynamic_update_slice_in_dim(
        jnp.zeros((3, D), jnp.float32), bias_part, here * head_width, 1
    )
    full_bfc1 = lax.dynamic_update_slice_in_dim(
        jnp.zeros((dp_count, ctx_count, unit), jnp.float32),
        grad_bfc1_part.reshape(dp_count, 1, unit),
        here,
        1,
    )
    small = jnp.concatenate(
        [
            full_bqkv.reshape(count, -1),
            grad_b_fc2.reshape(count, -1),
            grad_gain.reshape(count, -1),
            grad_shift.reshape(count, -1),
            full_bfc1.reshape(count, -1),
        ],
        axis=1,
    )
    owned_small = reduce_small(small)
    cuts = [0, 3 * D // count, D // count, D // count, D // count, FF // count]
    bounds = [sum(cuts[: i + 1]) for i in range(len(cuts))]
    owned_bqkv, owned_bout, owned_gain, owned_shift, owned_bfc1 = [
        owned_small[bounds[i] : bounds[i + 1]] for i in range(5)
    ]
    return (
        block_out,
        grad_tokens,
        split_qkv.reshape(rows_piece, 3 * D),
        owned_bqkv,
        owned_w_out,
        owned_bout,
        split_fc1.reshape(rows_piece, FF),
        owned_bfc1,
        owned_fc2,
        owned_bout,
        owned_gain,
        owned_shift,
    )


def body(
    ring,
    tokens,
    lengths,
    w_qkv,
    b_qkv,
    w_out,
    b_out,
    w_fc1,
    b_fc1,
    w_fc2,
    b_fc2,
    ln_gain,
    ln_shift,
    cotangent,
):
    return head_plan(
        ring,
        tokens,
        lengths,
        w_qkv,
        b_qkv,
        w_out,
        b_out,
        w_fc1,
        b_fc1,
        w_fc2,
        b_fc2,
        ln_gain,
        ln_shift,
        cotangent,
    )


def solution(mesh):
    in_specs = (
        P(("dp", "ctx"), None),
        P("dp", None),
        P(("dp", "ctx"), None),
        P(("dp", "ctx")),
        P(("dp", "ctx"), None),
        P(("dp", "ctx")),
        P(("dp", "ctx"), None),
        P(("dp", "ctx")),
        P(("dp", "ctx"), None),
        P(("dp", "ctx")),
        P(("dp", "ctx")),
        P(("dp", "ctx")),
        P(("dp", "ctx"), None),
    )
    out_specs = (
        P(("dp", "ctx"), None),
        P(("dp", "ctx"), None),
        P(("dp", "ctx"), None),
        P(("dp", "ctx")),
        P(("dp", "ctx"), None),
        P(("dp", "ctx")),
        P(("dp", "ctx"), None),
        P(("dp", "ctx")),
        P(("dp", "ctx"), None),
        P(("dp", "ctx")),
        P(("dp", "ctx")),
        P(("dp", "ctx")),
    )
    ring = ring_of(mesh)
    return jax.shard_map(functools.partial(body, ring), mesh=mesh, in_specs=in_specs, out_specs=out_specs, check_vma=False)
```

```python
import functools
import math

import jax
import jax.numpy as jnp
from jax import lax
from jax.experimental import pallas as pl
from jax.experimental.pallas import tpu as pltpu
from jax.sharding import PartitionSpec as P

D = 2048
HEADS = 32
HEAD_DIM = 64
ROT = 32
FF = 8192


EPS = 1e-05
GELU_COEF = math.sqrt(2.0 / math.pi)
NEGATIVE = -1e30


def norm_parts(inputs, gain, shift):
    mean = jnp.mean(inputs, axis=-1, keepdims=True)
    centred = inputs - mean
    var = jnp.mean(centred * centred, axis=-1, keepdims=True)
    scaled = lax.rsqrt(var + EPS)
    normed = centred * scaled
    return (normed, scaled, normed * gain + shift)


def norm_back(d_hidden, normed, scaled, gain32):
    grad_gain = jnp.sum(d_hidden * normed, axis=0)
    grad_shift = jnp.sum(d_hidden, axis=0)
    d_normed = d_hidden * gain32
    d_inputs = scaled * (
        d_normed
        - jnp.mean(d_normed, axis=-1, keepdims=True)
        - normed * jnp.mean(d_normed * normed, axis=-1, keepdims=True)
    )
    return (grad_gain, grad_shift, d_inputs)


def gelu_tanh(pre):
    return 0.5 * pre * (1.0 + jnp.tanh(GELU_COEF * (pre + 0.044715 * pre * pre * pre)))


def gelu_slope(pre):
    tangent = jnp.tanh(GELU_COEF * (pre + 0.044715 * pre * pre * pre))
    return 0.5 * (1.0 + tangent) + 0.5 * pre * (1.0 - tangent * tangent) * GELU_COEF * (
        1.0 + 3.0 * 0.044715 * pre * pre
    )


def rotary_tables(positions):
    half = ROT // 2
    freq = jnp.exp(jnp.arange(half, dtype=jnp.float32) * (-2.0 * math.log(10000.0) / ROT))
    angle = positions.astype(jnp.float32)[:, None] * freq[None, :]
    return (jnp.cos(angle)[:, None, :], jnp.sin(angle)[:, None, :])


def rotate(heads, cosine, sine):
    half = ROT // 2
    first = heads[..., :half]
    second = heads[..., half:ROT]
    return jnp.concatenate(
        [first * cosine - second * sine, second * cosine + first * sine, heads[..., ROT:]], axis=-1
    )


def rotate_back(grads, cosine, sine):
    half = ROT // 2
    first = grads[..., :half]
    second = grads[..., half:ROT]
    return jnp.concatenate(
        [first * cosine + second * sine, second * cosine - first * sine, grads[..., ROT:]], axis=-1
    )


def segment_info(lengths_row, rows):
    ends = jnp.cumsum(lengths_row)
    starts = ends - lengths_row
    seg = jnp.sum((rows[:, None] >= ends[None, :]).astype(jnp.int32), axis=1)
    onehot = seg[:, None] == jnp.arange(lengths_row.shape[0], dtype=jnp.int32)[None, :]
    first_rows = jnp.sum(jnp.where(onehot, starts[None, :], 0), axis=1)
    return (seg, rows - first_rows)


TRANS_B = (((1,), (1,)), ((), ()))


def _allowed(segq_ref, segk_ref, i, j, tq, tk, causal):
    same = segq_ref[...] == segk_ref[...]
    if not causal:
        return same
    rows = i * tq + lax.broadcasted_iota(jnp.int32, (tq, tk), 0)
    cols = j * tk + lax.broadcasted_iota(jnp.int32, (tq, tk), 1)
    return same & (cols <= rows)


def _fwd_kernel(qi_ref, kj_ref, q_ref, k_ref, v_ref, segq_ref, segk_ref, o_ref, lse_ref, m_sc, acc_sc, *, tq, tk, scale):
    t = pl.program_id(1)
    i = qi_ref[t]
    j = kj_ref[t]
    dim = o_ref.shape[2]

    @pl.when(j == 0)
    def _():
        m_sc[...] = jnp.full_like(m_sc, NEGATIVE)
        acc_sc[...] = jnp.zeros_like(acc_sc)

    def absorb(causal):
        q = q_ref[0]
        k = k_ref[0]
        s = lax.dot_general(q, k, TRANS_B, preferred_element_type=jnp.float32) * scale
        s = jnp.where(_allowed(segq_ref, segk_ref, i, j, tq, tk, causal), s, -jnp.inf)
        m_prev = m_sc[...]
        lanes = s.shape[1]
        folded = s[:, :128]
        for start in range(128, lanes, 128):
            folded = jnp.maximum(folded, s[:, start : start + 128])
        m_new = jnp.maximum(m_prev, jnp.max(folded, axis=1, keepdims=True))
        factor = jnp.exp(m_prev - m_new)
        p = jnp.exp(s - m_new)
        acc_sc[...] = acc_sc[...] * factor + jnp.dot(
            p.astype(jnp.bfloat16), v_ref[0], preferred_element_type=jnp.float32
        )
        m_sc[...] = m_new

    @pl.when(j < i)
    def _():
        absorb(False)

    @pl.when(j == i)
    def _():
        absorb(True)
        acc = acc_sc[...]
        total = acc[:, dim : dim + 1]
        o_ref[0] = acc[:, :dim] / total
        lse_ref[0] = m_sc[...] + jnp.log(total)


def _schedule(count, queries_outer):
    if queries_outer:
        pairs = [(i, j) for i in range(count) for j in range(i + 1)]
    else:
        pairs = [(i, j) for j in range(count) for i in range(j, count)]
    return (
        jnp.asarray([p[0] for p in pairs], jnp.int32),
        jnp.asarray([p[1] for p in pairs], jnp.int32),
    )


def attention_forward(q, k, v, seg, block=512):
    heads, total, dim = q.shape
    count = total // block
    scale = 1.0 / math.sqrt(dim)
    segq = seg.reshape(total, 1)
    segk = seg.reshape(1, total)
    qi, kj = _schedule(count, True)
    steps = qi.shape[0]
    lanes = 2 * dim
    v_ext = jnp.concatenate(
        [v, jnp.ones((heads, total, 1), v.dtype), jnp.zeros((heads, total, lanes - dim - 1), v.dtype)],
        axis=2,
    )

    return pl.pallas_call(
        functools.partial(_fwd_kernel, tq=block, tk=block, scale=scale),
        out_shape=(
            jax.ShapeDtypeStruct((heads, total, dim), jnp.float32),
            jax.ShapeDtypeStruct((heads, total, 1), jnp.float32),
        ),
        grid_spec=pltpu.PrefetchScalarGridSpec(
            num_scalar_prefetch=2,
            grid=(heads, steps),
            in_specs=[
                pl.BlockSpec((1, block, dim), lambda h, t, qi, kj: (h, qi[t], 0)),
                pl.BlockSpec((1, block, dim), lambda h, t, qi, kj: (h, kj[t], 0)),
                pl.BlockSpec((1, block, lanes), lambda h, t, qi, kj: (h, kj[t], 0)),
                pl.BlockSpec((block, 1), lambda h, t, qi, kj: (qi[t], 0)),
                pl.BlockSpec((1, block), lambda h, t, qi, kj: (0, kj[t])),
            ],
            out_specs=[
                pl.BlockSpec((1, block, dim), lambda h, t, qi, kj: (h, qi[t], 0)),
                pl.BlockSpec((1, block, 1), lambda h, t, qi, kj: (h, qi[t], 0)),
            ],
            scratch_shapes=[
                pltpu.VMEM((block, 1), jnp.float32),
                pltpu.VMEM((block, lanes), jnp.float32),
            ],
        ),
        cost_estimate=pl.CostEstimate(
            flops=2 * heads * total * total * dim,
            transcendentals=heads * total * total // 2,
            bytes_accessed=heads * total * dim * 10,
        ),
    )(qi, kj, q, k, v_ext, segq, segk)


def _bwd_kernel(qi_ref, kj_ref, q_ref, k_ref, v_ref, do_ref, lse_ref, delta_ref, segq_ref, segk_ref, dq_ref, dk_ref, dv_ref, dk_sc, dv_sc, *, tq, tk, scale, count):
    t = pl.program_id(1)
    i = qi_ref[t]
    j = kj_ref[t]

    @pl.when(t == 0)
    def _():
        dq_ref[...] = jnp.zeros_like(dq_ref)

    @pl.when(i == j)
    def _():
        dk_sc[...] = jnp.zeros_like(dk_sc)
        dv_sc[...] = jnp.zeros_like(dv_sc)

    def absorb(causal):
        q = q_ref[0]
        k = k_ref[0]
        do = do_ref[0]
        s = lax.dot_general(q, k, TRANS_B, preferred_element_type=jnp.float32) * scale
        s = jnp.where(_allowed(segq_ref, segk_ref, i, j, tq, tk, causal), s, -jnp.inf)
        p = jnp.exp(s - lse_ref[0])
        dp = lax.dot_general(do, v_ref[0], TRANS_B, preferred_element_type=jnp.float32)
        ds = (p * (dp - delta_ref[0])).astype(jnp.bfloat16)
        dv_sc[...] += jnp.dot(do.T, p.astype(jnp.bfloat16), preferred_element_type=jnp.float32)
        dk_sc[...] += jnp.dot(q.T, ds, preferred_element_type=jnp.float32)
        rows = pl.ds(pl.multiple_of(i * tq, tq), tq)
        dq_ref[0, rows, :] += lax.dot(ds, k, preferred_element_type=jnp.float32) * scale

    @pl.when(j < i)
    def _():
        absorb(False)

    @pl.when(j == i)
    def _():
        absorb(True)

    @pl.when(i == count - 1)
    def _():
        dk_ref[0] = dk_sc[...].T * scale
        dv_ref[0] = dv_sc[...].T


def attention_backward(q, k, v, do, lse, delta, seg, block=512):
    heads, total, dim = q.shape
    count = total // block
    scale = 1.0 / math.sqrt(dim)
    segq = seg.reshape(total, 1)
    segk = seg.reshape(1, total)
    qi, kj = _schedule(count, False)
    steps = qi.shape[0]

    def q_map(h, t, qi, kj):
        return (h, qi[t], 0)

    def k_map(h, t, qi, kj):
        return (h, kj[t], 0)

    return pl.pallas_call(
        functools.partial(_bwd_kernel, tq=block, tk=block, scale=scale, count=count),
        out_shape=(
            jax.ShapeDtypeStruct((heads, total, dim), jnp.float32),
            jax.ShapeDtypeStruct((heads, total, dim), jnp.float32),
            jax.ShapeDtypeStruct((heads, total, dim), jnp.float32),
        ),
        grid_spec=pltpu.PrefetchScalarGridSpec(
            num_scalar_prefetch=2,
            grid=(heads, steps),
            in_specs=[
                pl.BlockSpec((1, block, dim), q_map),
                pl.BlockSpec((1, block, dim), k_map),
                pl.BlockSpec((1, block, dim), k_map),
                pl.BlockSpec((1, block, dim), q_map),
                pl.BlockSpec((1, block, 1), q_map),
                pl.BlockSpec((1, block, 1), q_map),
                pl.BlockSpec((block, 1), lambda h, t, qi, kj: (qi[t], 0)),
                pl.BlockSpec((1, block), lambda h, t, qi, kj: (0, kj[t])),
            ],
            out_specs=[
                pl.BlockSpec((1, total, dim), lambda h, t, qi, kj: (h, 0, 0)),
                pl.BlockSpec((1, block, dim), k_map),
                pl.BlockSpec((1, block, dim), k_map),
            ],
            scratch_shapes=[
                pltpu.VMEM((dim, block), jnp.float32),
                pltpu.VMEM((dim, block), jnp.float32),
            ],
        ),
        cost_estimate=pl.CostEstimate(
            flops=5 * heads * total * total * dim,
            transcendentals=heads * total * total // 2,
            bytes_accessed=heads * total * dim * 24,
        ),
    )(qi, kj, q, k, v, do, lse, delta, segq, segk)


MESH_ID = pl.DeviceIdType.MESH


class Ring:
    def __init__(self, size, a_stride, b_stride):
        self.size = size
        self.half = size // 2
        self.a_stride = a_stride
        self.b_stride = b_stride

    def position(self, c):
        a = (c // self.a_stride) % self.half
        b = (c // self.b_stride) % 2
        return a + b * (2 * self.half - 1 - 2 * a)

    def device(self, pos):
        pos = pos % self.size
        b = pos // self.half
        a = pos + b * (2 * self.half - 1 - 2 * pos)
        return a * self.a_stride + b * self.b_stride


def ring_of(mesh):
    size = mesh.shape["ctx"]
    devices = list(mesh.devices.reshape(-1, size)[0])
    try:
        coords = [tuple(d.coords) for d in devices]
    except AttributeError:
        coords = None
    if coords and size % 2 == 0 and size >= 4:
        for b_stride in range(1, size):
            for a_stride in range(1, size):
                ring = Ring(size, a_stride, b_stride)
                order = [ring.device(p) for p in range(size)]
                if sorted(order) != list(range(size)):
                    continue
                hops = [
                    sum(abs(x - y) for x, y in zip(coords[order[p]], coords[order[(p + 1) % size]]))
                    for p in range(size)
                ]
                if max(hops) == 1:
                    return ring
    return Ring(size, 2, 1) if size % 2 == 0 and size >= 4 else None


def _barrier(g, left, right):
    barrier = pltpu.get_barrier_semaphore()
    for other in (left, right):
        pl.semaphore_signal(barrier, 1, device_id=(g, other), device_id_type=MESH_ID)
    pl.semaphore_wait(barrier, 2)


def _gather_kernel(x_ref, y_ref, own_sem, send_sem, recv_sem, *, ring, rows):
    n = ring.size
    half = rows // 2
    g = lax.axis_index("dp")
    c = lax.axis_index("ctx")
    pos = ring.position(c)
    right = ring.device(pos + 1)
    left = ring.device(pos + n - 1)
    own = pltpu.make_async_copy(x_ref, y_ref.at[pl.ds(c * rows, rows)], own_sem)
    own.start()
    _barrier(g, left, right)

    def link(direction, step, origin, source):
        offset = origin * rows + direction * half
        return pltpu.make_async_remote_copy(
            src_ref=source,
            dst_ref=y_ref.at[pl.ds(offset, half)],
            send_sem=send_sem.at[direction, step],
            recv_sem=recv_sem.at[direction, step],
            device_id=(g, right if direction == 0 else left),
            device_id_type=MESH_ID,
        )

    sent = []
    for step in range(n - 1):
        origins = (ring.device(pos - step + n), ring.device(pos + step))
        for direction in (0, 1):
            origin = origins[direction]
            if step == 0:
                source = x_ref.at[pl.ds(direction * half, half)]
            else:
                link(direction, step - 1, origin, None if False else y_ref.at[pl.ds(origin * rows + direction * half, half)]).wait_recv()
                source = y_ref.at[pl.ds(origin * rows + direction * half, half)]
            copy = link(direction, step, origin, source)
            copy.start()
            sent.append(copy)
    last = n - 2
    for direction, origin in ((0, ring.device(pos - last - 1 + n)), (1, ring.device(pos + last + 1))):
        link(direction, last, origin, y_ref.at[pl.ds(origin * rows + direction * half, half)]).wait_recv()
    for copy in sent:
        copy.wait_send()
    own.wait()


def ring_all_gather(x, ring, collective_id):
    rows, cols = x.shape
    n = ring.size
    return pl.pallas_call(
        functools.partial(_gather_kernel, ring=ring, rows=rows),
        out_shape=jax.ShapeDtypeStruct((n * rows, cols), x.dtype),
        in_specs=[pl.BlockSpec(memory_space=pl.ANY)],
        out_specs=pl.BlockSpec(memory_space=pl.ANY),
        scratch_shapes=[
            pltpu.SemaphoreType.DMA(()),
            pltpu.SemaphoreType.DMA((2, n - 1)),
            pltpu.SemaphoreType.DMA((2, n - 1)),
        ],
        compiler_params=pltpu.CompilerParams(collective_id=collective_id, has_side_effects=True),
    )(x)


def _scatter_kernel(p_ref, out_ref, recv_buf, send_buf, send_sem, recv_sem, *, ring, rows, parts):
    n = ring.size
    half = rows // 2
    piece = half // parts
    g = lax.axis_index("dp")
    c = lax.axis_index("ctx")
    pos = ring.position(c)
    right = ring.device(pos + 1)
    left = ring.device(pos + n - 1)
    _barrier(g, left, right)

    def link(direction, step, part):
        window = pl.ds(part * piece, piece)
        return pltpu.make_async_remote_copy(
            src_ref=send_buf.at[direction, step, window],
            dst_ref=recv_buf.at[direction, step, window],
            send_sem=send_sem.at[direction, step, part],
            recv_sem=recv_sem.at[direction, step, part],
            device_id=(g, right if direction == 0 else left),
            device_id_type=MESH_ID,
        )

    sent = []
    for step in range(n - 1):
        targets = (ring.device(pos - 1 - step + 2 * n), ring.device(pos + 1 + step))
        for part in range(parts):
            for direction in (0, 1):
                start = pl.multiple_of(
                    targets[direction] * rows + direction * half + part * piece, piece
                )
                window = pl.ds(part * piece, piece)
                total = p_ref[pl.ds(start, piece), :].astype(jnp.float32)
                if step > 0:
                    link(direction, step - 1, part).wait_recv()
                    total = total + recv_buf[direction, step - 1, window].astype(jnp.float32)
                send_buf[direction, step, window] = total.astype(send_buf.dtype)
                copy = link(direction, step, part)
                copy.start()
                sent.append(copy)
    for part in range(parts):
        for direction in (0, 1):
            link(direction, n - 2, part).wait_recv()
            start = pl.multiple_of(c * rows + direction * half + part * piece, piece)
            window = pl.ds(part * piece, piece)
            out_ref[pl.ds(direction * half + part * piece, piece), :] = (
                p_ref[pl.ds(start, piece), :].astype(jnp.float32)
                + recv_buf[direction, n - 2, window].astype(jnp.float32)
            ).astype(out_ref.dtype)
    for copy in sent:
        copy.wait_send()


def ring_reduce_scatter(p, ring, collective_id, out_dtype=jnp.float32, wire=jnp.bfloat16, parts=2):
    total_rows, cols = p.shape
    n = ring.size
    rows = total_rows // n
    half = rows // 2
    return pl.pallas_call(
        functools.partial(_scatter_kernel, ring=ring, rows=rows, parts=parts),
        out_shape=jax.ShapeDtypeStruct((rows, cols), out_dtype),
        in_specs=[pl.BlockSpec(memory_space=pltpu.VMEM)],
        out_specs=pl.BlockSpec(memory_space=pltpu.VMEM),
        scratch_shapes=[
            pltpu.VMEM((2, n - 1, half, cols), wire),
            pltpu.VMEM((2, n - 1, half, cols), wire),
            pltpu.SemaphoreType.DMA((2, n - 1, parts)),
            pltpu.SemaphoreType.DMA((2, n - 1, parts)),
        ],
        compiler_params=pltpu.CompilerParams(
            collective_id=collective_id, has_side_effects=True, vmem_limit_bytes=60 * 1024 * 1024
        ),
    )(p)


def _exchange_kernel(x_ref, out_ref, own_sem, send_sem, recv_sem, *, group):
    n = x_ref.shape[0]
    g = lax.axis_index("dp")
    c = lax.axis_index("ctx")
    n_ctx = lax.axis_size("ctx")
    me = {"all": g * n_ctx + c, "ctx": c, "dp": g}[group]

    def address(member):
        if group == "all":
            return (member // n_ctx, member % n_ctx)
        if group == "ctx":
            return (g, member)
        return (member, c)

    own = pltpu.make_async_copy(x_ref.at[me], out_ref.at[me], own_sem)
    own.start()
    barrier = pltpu.get_barrier_semaphore()
    for offset in range(1, n):
        pl.semaphore_signal(
            barrier, 1, device_id=address((me + offset) % n), device_id_type=MESH_ID
        )
    pl.semaphore_wait(barrier, n - 1)

    def link(offset, source, target):
        return pltpu.make_async_remote_copy(
            src_ref=x_ref.at[target],
            dst_ref=out_ref.at[source],
            send_sem=send_sem.at[offset],
            recv_sem=recv_sem.at[offset],
            device_id=address(target),
            device_id_type=MESH_ID,
        )

    sent = []
    for offset in range(1, n):
        copy = link(offset, me, (me + offset) % n)
        copy.start()
        sent.append(copy)
    for offset in range(1, n):
        link(offset, (me + n - offset) % n, me).wait_recv()
    for copy in sent:
        copy.wait_send()
    own.wait()


def exchange(x, group, collective_id):
    n = x.shape[0]
    space = pltpu.VMEM
    return pl.pallas_call(
        functools.partial(_exchange_kernel, group=group),
        out_shape=jax.ShapeDtypeStruct(x.shape, x.dtype),
        in_specs=[pl.BlockSpec(memory_space=space)],
        out_specs=pl.BlockSpec(memory_space=space),
        scratch_shapes=[
            pltpu.SemaphoreType.DMA(()),
            pltpu.SemaphoreType.DMA((n,)),
            pltpu.SemaphoreType.DMA((n,)),
        ],
        compiler_params=pltpu.CompilerParams(collective_id=collective_id, has_side_effects=True),
    )(x)


def block_moves(n_dp, n_ctx):
    count = n_dp * n_ctx
    return [(f, (f % n_dp) * n_ctx + f // n_dp) for f in range(count)]


def fetch_out_rows(w_out):
    n_dp = lax.axis_size("dp")
    n_ctx = lax.axis_size("ctx")
    moved = lax.ppermute(w_out.astype(jnp.bfloat16), ("dp", "ctx"), perm=block_moves(n_dp, n_ctx))
    return lax.all_gather(moved, "dp", axis=0, tiled=True)


def return_out_rows(grad_out_rows):
    n_dp = lax.axis_size("dp")
    n_ctx = lax.axis_size("ctx")
    part = lax.psum_scatter(grad_out_rows, "dp", scatter_dimension=0, tiled=True)
    back = [(b, a) for a, b in block_moves(n_dp, n_ctx)]
    return lax.ppermute(part, ("dp", "ctx"), perm=back)


def pack_rows(vector, lanes):
    size = vector.shape[0]
    total = -(-size // (16 * lanes)) * 16 * lanes
    return jnp.pad(vector, (0, total - size)).reshape(-1, lanes)


def pack_small(b_qkv, b_out, b_fc2, ln_gain, ln_shift, b_fc1):
    pieces = (b_qkv, b_out, b_fc2, ln_gain, ln_shift, b_fc1)
    return pack_rows(jnp.concatenate([p.astype(jnp.bfloat16) for p in pieces]), 128)


def fetch_small(over_ctx, sizes):
    n_dp = lax.axis_size("dp")
    n_ctx = lax.axis_size("ctx")
    over_all = exchange(jnp.broadcast_to(over_ctx[None], (n_dp,) + over_ctx.shape), "dp", 4)
    table = over_all.reshape(n_dp * n_ctx, -1)
    result = []
    offset = 0
    for size in sizes:
        result.append(table[:, offset : offset + size])
        offset += size
    return result


def reduce_small(small):
    n_dp = lax.axis_size("dp")
    n_ctx = lax.axis_size("ctx")
    count, width = small.shape
    packed = jax.vmap(lambda row: pack_rows(row, 128))(small)
    packed = packed.reshape((n_dp, n_ctx) + packed.shape[1:]).transpose(1, 0, 2, 3)
    over_ctx = jnp.sum(exchange(packed, "ctx", 7), axis=0)
    over_dp = jnp.sum(exchange(over_ctx, "dp", 9), axis=0)
    return over_dp.reshape(-1)[:width]


def fetch_heads(w_qkv, w_fc1, w_fc2, tokens, packed):
    dp_count = lax.axis_size("dp")
    ctx_count = lax.axis_size("ctx")
    rows_piece = w_qkv.shape[0]
    head_width = D // ctx_count
    unit = FF // (dp_count * ctx_count)
    qkv_piece = w_qkv.astype(jnp.bfloat16).reshape(rows_piece, 3, ctx_count, head_width)
    fc1_piece = w_fc1.astype(jnp.bfloat16).reshape(rows_piece, dp_count, ctx_count, unit)
    pieces = jnp.concatenate(
        [
            qkv_piece.transpose(2, 0, 1, 3).reshape(ctx_count, rows_piece, 3 * head_width),
            fc1_piece.transpose(2, 0, 1, 3).reshape(ctx_count, rows_piece, dp_count * unit),
        ],
        axis=2,
    )
    width = pieces.shape[2]
    flat = packed.reshape(-1)
    extra = -(-flat.shape[0] // (8 * width)) * 8
    flat = jnp.pad(flat, (0, extra * width - flat.shape[0])).reshape(extra, width)
    payload = jnp.concatenate(
        [pieces, jnp.broadcast_to(flat[None], (ctx_count, extra, width))], axis=1
    )
    got = exchange(payload, "ctx", 5)
    small = got[:, rows_piece:, :].reshape(ctx_count, -1)[:, : packed.size]
    small = small.reshape((ctx_count,) + packed.shape)
    sent = got[:, :rows_piece, :].reshape(ctx_count * rows_piece, -1)
    sent, tokens = lax.optimization_barrier((sent, tokens))
    cols, fc2_rows = (
        lax.all_gather(sent, "dp", axis=0, tiled=True),
        lax.all_gather(w_fc2.astype(jnp.bfloat16), "dp", axis=0, tiled=True),
    )
    return (cols, fc2_rows, tokens, small)


def return_heads(owned_parts):
    dp_count = lax.axis_size("dp")
    ctx_count = lax.axis_size("ctx")
    head_width = D // ctx_count
    unit = FF // (dp_count * ctx_count)
    rows_piece = owned_parts.shape[0] // ctx_count
    got = exchange(owned_parts.reshape(ctx_count, rows_piece, -1), "ctx", 6)
    qkv = got[:, :, : 3 * head_width].reshape(ctx_count, rows_piece, 3, head_width)
    fc1 = got[:, :, 3 * head_width :].reshape(ctx_count, rows_piece, dp_count, unit)
    return (
        qkv.transpose(1, 2, 0, 3).reshape(rows_piece, 3 * D).astype(jnp.float32),
        fc1.transpose(1, 2, 0, 3).reshape(rows_piece, FF).astype(jnp.float32),
    )


def head_plan(
    ring,
    tokens,
    lengths,
    w_qkv,
    b_qkv,
    w_out,
    b_out,
    w_fc1,
    b_fc1,
    w_fc2,
    b_fc2,
    ln_gain,
    ln_shift,
    cotangent,
):
    rows_here = tokens.shape[0]
    rows_piece = w_qkv.shape[0]
    dp_count = lax.axis_size("dp")
    ctx_count = lax.axis_size("ctx")
    count = dp_count * ctx_count
    group = rows_here * ctx_count
    head_width = D // ctx_count
    local_heads = HEADS // ctx_count
    unit = FF // (dp_count * ctx_count)
    here = lax.axis_index("ctx")
    group_rows = jnp.arange(group, dtype=jnp.int32)
    seg, positions = segment_info(lengths[0], group_rows)
    cosine, sine = rotary_tables(positions)
    packed = pack_small(b_qkv, b_out, b_fc2, ln_gain, ln_shift, b_fc1)
    cols, fc2_rows, tokens, small_ctx = fetch_heads(w_qkv, w_fc1, w_fc2, tokens, packed)
    qkv_bias, out_bias, fc2_bias, gain_low, shift_low, fc1_table = fetch_small(
        small_ctx, [p.shape[0] for p in (b_qkv, b_out, b_fc2, ln_gain, ln_shift, b_fc1)]
    )
    qkv_bias = qkv_bias.reshape(3 * D)
    out_bias = out_bias.reshape(D)
    fc2_bias = fc2_bias.reshape(D)
    gain_low = gain_low.reshape(D)
    shift_low = shift_low.reshape(D)
    fc1_bias = lax.dynamic_index_in_dim(
        fc1_table.reshape(dp_count, ctx_count, unit), here, 1, keepdims=False
    ).reshape(dp_count * unit)
    out_rows = fetch_out_rows(w_out)
    gain32 = gain_low.astype(jnp.float32)
    shift32 = shift_low.astype(jnp.float32)
    inputs = tokens.astype(jnp.float32)
    normed, scaled, _ = norm_parts(inputs, gain32, shift32)
    tokens_group = ring_all_gather(tokens, ring, 0)
    late_dy, tokens_group = lax.optimization_barrier((cotangent, tokens_group))
    dy_group = lax.all_gather(late_dy, "ctx", axis=0, tiled=True)
    hidden_group = norm_parts(tokens_group.astype(jnp.float32), gain32, shift32)[2].astype(
        jnp.bfloat16
    )
    bias_cols = lax.dynamic_slice_in_dim(
        qkv_bias.reshape(3, D), here * head_width, head_width, 1
    ).reshape(3 * head_width)
    both = jnp.dot(hidden_group, cols, preferred_element_type=jnp.float32) + jnp.concatenate(
        [bias_cols, fc1_bias]
    ).astype(jnp.float32)
    qkv = both[:, : 3 * head_width]
    pre = both[:, 3 * head_width :]
    shape = (group, local_heads, HEAD_DIM)
    query = rotate(qkv[:, :head_width].reshape(shape), cosine, sine).astype(jnp.bfloat16)
    keys = rotate(qkv[:, head_width : 2 * head_width].reshape(shape), cosine, sine).astype(
        jnp.bfloat16
    )
    values = qkv[:, 2 * head_width :].reshape(shape).astype(jnp.bfloat16)
    q_heads = query.transpose(1, 0, 2)
    k_heads = keys.transpose(1, 0, 2)
    v_heads = values.transpose(1, 0, 2)
    attended_heads, log_total = attention_forward(q_heads, k_heads, v_heads, seg)
    attended = attended_heads.transpose(1, 0, 2).reshape(group, head_width).astype(jnp.bfloat16)
    act = gelu_tanh(pre).astype(jnp.bfloat16)
    branches = ring_reduce_scatter(
        jnp.dot(attended, out_rows, preferred_element_type=jnp.float32)
        + jnp.dot(act, fc2_rows, preferred_element_type=jnp.float32),
        ring,
        2,
    )
    block_out = (
        inputs + branches + out_bias.astype(jnp.float32) + fc2_bias.astype(jnp.float32)
    ).astype(jnp.bfloat16)
    grad_out32 = cotangent.astype(jnp.float32)
    grad_b_fc2 = jnp.sum(grad_out32, axis=0)
    grad_fc2_part = jnp.einsum("tf,td->fd", act, dy_group, preferred_element_type=jnp.float32)
    d_act = jnp.einsum("td,fd->tf", dy_group, fc2_rows, preferred_element_type=jnp.float32)
    d_pre = (d_act * gelu_slope(pre)).astype(jnp.bfloat16)
    grad_bfc1_part = jnp.sum(d_pre.astype(jnp.float32), axis=0)
    grad_out_rows = jnp.einsum("tc,td->cd", attended, dy_group, preferred_element_type=jnp.float32)
    owned_w_out = return_out_rows(grad_out_rows)
    d_attended = (
        jnp.einsum("td,cd->tc", dy_group, out_rows, preferred_element_type=jnp.float32)
        .astype(jnp.bfloat16)
        .reshape(shape)
    )
    d_heads = d_attended.transpose(1, 0, 2)
    delta = jnp.sum(d_heads.astype(jnp.float32) * attended_heads, axis=2, keepdims=True)
    dq_heads, dk_heads, dv_heads = attention_backward(
        q_heads, k_heads, v_heads, d_heads, log_total, delta, seg
    )
    d_query = dq_heads.transpose(1, 0, 2)
    d_keys = dk_heads.transpose(1, 0, 2)
    d_values = dv_heads.transpose(1, 0, 2)
    d_query = rotate_back(d_query, cosine, sine).reshape(group, head_width)
    d_keys = rotate_back(d_keys, cosine, sine).reshape(group, head_width)
    d_qkv = jnp.concatenate([d_query, d_keys, d_values.reshape(group, head_width)], axis=1).astype(
        jnp.bfloat16
    )
    d_both = jnp.concatenate([d_qkv, d_pre], axis=1)
    bias_part = jnp.sum(d_qkv.astype(jnp.float32), axis=0).reshape(3, head_width)
    d_hidden = ring_reduce_scatter(
        jnp.einsum("tc,dc->td", d_both, cols, preferred_element_type=jnp.float32), ring, 3
    )
    weight_parts = jnp.einsum(
        "td,tc->dc", hidden_group, d_both, preferred_element_type=jnp.float32
    ).astype(jnp.bfloat16)
    owned_parts = lax.psum_scatter(weight_parts, "dp", scatter_dimension=0, tiled=True)
    split_qkv, split_fc1 = return_heads(owned_parts)
    d_hidden, split_qkv, split_fc1 = lax.optimization_barrier((d_hidden, split_qkv, split_fc1))
    grad_gain, grad_shift, d_inputs = norm_back(d_hidden, normed, scaled, gain32)
    grad_tokens = (grad_out32 + d_inputs).astype(jnp.bfloat16)
    owned_fc2 = lax.psum_scatter(
        grad_fc2_part.astype(jnp.bfloat16), "dp", scatter_dimension=0, tiled=True
    ).astype(jnp.float32)
    full_bqkv = lax.dynamic_update_slice_in_dim(
        jnp.zeros((3, D), jnp.float32), bias_part, here * head_width, 1
    )
    full_bfc1 = lax.dynamic_update_slice_in_dim(
        jnp.zeros((dp_count, ctx_count, unit), jnp.float32),
        grad_bfc1_part.reshape(dp_count, 1, unit),
        here,
        1,
    )
    small = jnp.concatenate(
        [
            full_bqkv.reshape(count, -1),
            grad_b_fc2.reshape(count, -1),
            grad_gain.reshape(count, -1),
            grad_shift.reshape(count, -1),
            full_bfc1.reshape(count, -1),
        ],
        axis=1,
    )
    owned_small = reduce_small(small)
    cuts = [0, 3 * D // count, D // count, D // count, D // count, FF // count]
    bounds = [sum(cuts[: i + 1]) for i in range(len(cuts))]
    owned_bqkv, owned_bout, owned_gain, owned_shift, owned_bfc1 = [
        owned_small[bounds[i] : bounds[i + 1]] for i in range(5)
    ]
    return (
        block_out,
        grad_tokens,
        split_qkv.reshape(rows_piece, 3 * D),
        owned_bqkv,
        owned_w_out,
        owned_bout,
        split_fc1.reshape(rows_piece, FF),
        owned_bfc1,
        owned_fc2,
        owned_bout,
        owned_gain,
        owned_shift,
    )


def body(
    ring,
    tokens,
    lengths,
    w_qkv,
    b_qkv,
    w_out,
    b_out,
    w_fc1,
    b_fc1,
    w_fc2,
    b_fc2,
    ln_gain,
    ln_shift,
    cotangent,
):
    return head_plan(
        ring,
        tokens,
        lengths,
        w_qkv,
        b_qkv,
        w_out,
        b_out,
        w_fc1,
        b_fc1,
        w_fc2,
        b_fc2,
        ln_gain,
        ln_shift,
        cotangent,
    )


def solution(mesh):
    in_specs = (
        P(("dp", "ctx"), None),
        P("dp", None),
        P(("dp", "ctx"), None),
        P(("dp", "ctx")),
        P(("dp", "ctx"), None),
        P(("dp", "ctx")),
        P(("dp", "ctx"), None),
        P(("dp", "ctx")),
        P(("dp", "ctx"), None),
        P(("dp", "ctx")),
        P(("dp", "ctx")),
        P(("dp", "ctx")),
        P(("dp", "ctx"), None),
    )
    out_specs = (
        P(("dp", "ctx"), None),
        P(("dp", "ctx"), None),
        P(("dp", "ctx"), None),
        P(("dp", "ctx")),
        P(("dp", "ctx"), None),
        P(("dp", "ctx")),
        P(("dp", "ctx"), None),
        P(("dp", "ctx")),
        P(("dp", "ctx"), None),
        P(("dp", "ctx")),
        P(("dp", "ctx")),
        P(("dp", "ctx")),
    )
    ring = ring_of(mesh)
    return jax.shard_map(functools.partial(body, ring), mesh=mesh, in_specs=in_specs, out_specs=out_specs, check_vma=False)
```

```python
import functools
import math

import jax
import jax.numpy as jnp
from jax import lax
from jax.experimental import pallas as pl
from jax.experimental.pallas import tpu as pltpu
from jax.sharding import PartitionSpec as P

D = 2048
HEADS = 32
HEAD_DIM = 64
ROT = 32
FF = 8192


EPS = 1e-05
GELU_COEF = math.sqrt(2.0 / math.pi)
NEGATIVE = -1e30


def norm_parts(inputs, gain, shift):
    mean = jnp.mean(inputs, axis=-1, keepdims=True)
    centred = inputs - mean
    var = jnp.mean(centred * centred, axis=-1, keepdims=True)
    scaled = lax.rsqrt(var + EPS)
    normed = centred * scaled
    return (normed, scaled, normed * gain + shift)


def norm_back(d_hidden, normed, scaled, gain32):
    grad_gain = jnp.sum(d_hidden * normed, axis=0)
    grad_shift = jnp.sum(d_hidden, axis=0)
    d_normed = d_hidden * gain32
    d_inputs = scaled * (
        d_normed
        - jnp.mean(d_normed, axis=-1, keepdims=True)
        - normed * jnp.mean(d_normed * normed, axis=-1, keepdims=True)
    )
    return (grad_gain, grad_shift, d_inputs)


def gelu_tanh(pre):
    return 0.5 * pre * (1.0 + jnp.tanh(GELU_COEF * (pre + 0.044715 * pre * pre * pre)))


def gelu_slope(pre):
    tangent = jnp.tanh(GELU_COEF * (pre + 0.044715 * pre * pre * pre))
    return 0.5 * (1.0 + tangent) + 0.5 * pre * (1.0 - tangent * tangent) * GELU_COEF * (
        1.0 + 3.0 * 0.044715 * pre * pre
    )


def rotary_tables(positions):
    half = ROT // 2
    freq = jnp.exp(jnp.arange(half, dtype=jnp.float32) * (-2.0 * math.log(10000.0) / ROT))
    angle = positions.astype(jnp.float32)[:, None] * freq[None, :]
    return (jnp.cos(angle)[:, None, :], jnp.sin(angle)[:, None, :])


def rotate(heads, cosine, sine):
    half = ROT // 2
    first = heads[..., :half]
    second = heads[..., half:ROT]
    return jnp.concatenate(
        [first * cosine - second * sine, second * cosine + first * sine, heads[..., ROT:]], axis=-1
    )


def rotate_back(grads, cosine, sine):
    half = ROT // 2
    first = grads[..., :half]
    second = grads[..., half:ROT]
    return jnp.concatenate(
        [first * cosine + second * sine, second * cosine - first * sine, grads[..., ROT:]], axis=-1
    )


def segment_info(lengths_row, rows):
    ends = jnp.cumsum(lengths_row)
    starts = ends - lengths_row
    seg = jnp.sum((rows[:, None] >= ends[None, :]).astype(jnp.int32), axis=1)
    onehot = seg[:, None] == jnp.arange(lengths_row.shape[0], dtype=jnp.int32)[None, :]
    first_rows = jnp.sum(jnp.where(onehot, starts[None, :], 0), axis=1)
    return (seg, rows - first_rows)


TRANS_B = (((1,), (1,)), ((), ()))


def _allowed(segq_ref, segk_ref, i, j, tq, tk, causal):
    same = segq_ref[...] == segk_ref[...]
    if not causal:
        return same
    rows = i * tq + lax.broadcasted_iota(jnp.int32, (tq, tk), 0)
    cols = j * tk + lax.broadcasted_iota(jnp.int32, (tq, tk), 1)
    return same & (cols <= rows)


def _fwd_kernel(qi_ref, kj_ref, q_ref, k_ref, v_ref, segq_ref, segk_ref, o_ref, lse_ref, m_sc, acc_sc, *, tq, tk, scale):
    t = pl.program_id(1)
    i = qi_ref[t]
    j = kj_ref[t]
    dim = o_ref.shape[2]

    @pl.when(j == 0)
    def _():
        m_sc[...] = jnp.full_like(m_sc, NEGATIVE)
        acc_sc[...] = jnp.zeros_like(acc_sc)

    def absorb(causal):
        q = q_ref[0]
        k = k_ref[0]
        s = lax.dot_general(q, k, TRANS_B, preferred_element_type=jnp.float32) * scale
        s = jnp.where(_allowed(segq_ref, segk_ref, i, j, tq, tk, causal), s, -jnp.inf)
        m_prev = m_sc[...]
        lanes = s.shape[1]
        folded = s[:, :128]
        for start in range(128, lanes, 128):
            folded = jnp.maximum(folded, s[:, start : start + 128])
        m_new = jnp.maximum(m_prev, jnp.max(folded, axis=1, keepdims=True))
        factor = jnp.exp(m_prev - m_new)
        p = jnp.exp(s - m_new)
        acc_sc[...] = acc_sc[...] * factor + jnp.dot(
            p.astype(jnp.bfloat16), v_ref[0], preferred_element_type=jnp.float32
        )
        m_sc[...] = m_new

    @pl.when(j < i)
    def _():
        absorb(False)

    @pl.when(j == i)
    def _():
        absorb(True)
        acc = acc_sc[...]
        total = acc[:, dim : dim + 1]
        o_ref[0] = acc[:, :dim] / total
        lse_ref[0] = m_sc[...] + jnp.log(total)


def _schedule(count, queries_outer):
    if queries_outer:
        pairs = [(i, j) for i in range(count) for j in range(i + 1)]
    else:
        pairs = [(i, j) for j in range(count) for i in range(j, count)]
    return (
        jnp.asarray([p[0] for p in pairs], jnp.int32),
        jnp.asarray([p[1] for p in pairs], jnp.int32),
    )


def attention_forward(q, k, v, seg, block=512):
    heads, total, dim = q.shape
    count = total // block
    scale = 1.0 / math.sqrt(dim)
    segq = seg.reshape(total, 1)
    segk = seg.reshape(1, total)
    qi, kj = _schedule(count, True)
    steps = qi.shape[0]
    lanes = 2 * dim
    v_ext = jnp.concatenate(
        [v, jnp.ones((heads, total, 1), v.dtype), jnp.zeros((heads, total, lanes - dim - 1), v.dtype)],
        axis=2,
    )

    return pl.pallas_call(
        functools.partial(_fwd_kernel, tq=block, tk=block, scale=scale),
        out_shape=(
            jax.ShapeDtypeStruct((heads, total, dim), jnp.float32),
            jax.ShapeDtypeStruct((heads, total, 1), jnp.float32),
        ),
        grid_spec=pltpu.PrefetchScalarGridSpec(
            num_scalar_prefetch=2,
            grid=(heads, steps),
            in_specs=[
                pl.BlockSpec((1, block, dim), lambda h, t, qi, kj: (h, qi[t], 0)),
                pl.BlockSpec((1, block, dim), lambda h, t, qi, kj: (h, kj[t], 0)),
                pl.BlockSpec((1, block, lanes), lambda h, t, qi, kj: (h, kj[t], 0)),
                pl.BlockSpec((block, 1), lambda h, t, qi, kj: (qi[t], 0)),
                pl.BlockSpec((1, block), lambda h, t, qi, kj: (0, kj[t])),
            ],
            out_specs=[
                pl.BlockSpec((1, block, dim), lambda h, t, qi, kj: (h, qi[t], 0)),
                pl.BlockSpec((1, block, 1), lambda h, t, qi, kj: (h, qi[t], 0)),
            ],
            scratch_shapes=[
                pltpu.VMEM((block, 1), jnp.float32),
                pltpu.VMEM((block, lanes), jnp.float32),
            ],
        ),
        cost_estimate=pl.CostEstimate(
            flops=2 * heads * total * total * dim,
            transcendentals=heads * total * total // 2,
            bytes_accessed=heads * total * dim * 10,
        ),
    )(qi, kj, q, k, v_ext, segq, segk)


def _bwd_kernel(qi_ref, kj_ref, q_ref, k_ref, v_ref, do_ref, lse_ref, delta_ref, segq_ref, segk_ref, dq_ref, dk_ref, dv_ref, dk_sc, dv_sc, *, tq, tk, scale, count):
    t = pl.program_id(1)
    i = qi_ref[t]
    j = kj_ref[t]

    @pl.when(t == 0)
    def _():
        dq_ref[...] = jnp.zeros_like(dq_ref)

    @pl.when(i == j)
    def _():
        dk_sc[...] = jnp.zeros_like(dk_sc)
        dv_sc[...] = jnp.zeros_like(dv_sc)

    def absorb(causal):
        q = q_ref[0]
        k = k_ref[0]
        do = do_ref[0]
        s = lax.dot_general(q, k, TRANS_B, preferred_element_type=jnp.float32) * scale
        s = jnp.where(_allowed(segq_ref, segk_ref, i, j, tq, tk, causal), s, -jnp.inf)
        p = jnp.exp(s - lse_ref[0])
        dp = lax.dot_general(do, v_ref[0], TRANS_B, preferred_element_type=jnp.float32)
        ds = (p * (dp - delta_ref[0])).astype(jnp.bfloat16)
        dv_sc[...] += jnp.dot(do.T, p.astype(jnp.bfloat16), preferred_element_type=jnp.float32)
        dk_sc[...] += jnp.dot(q.T, ds, preferred_element_type=jnp.float32)
        rows = pl.ds(pl.multiple_of(i * tq, tq), tq)
        dq_ref[0, rows, :] += lax.dot(ds, k, preferred_element_type=jnp.float32) * scale

    @pl.when(j < i)
    def _():
        absorb(False)

    @pl.when(j == i)
    def _():
        absorb(True)

    @pl.when(i == count - 1)
    def _():
        dk_ref[0] = dk_sc[...].T * scale
        dv_ref[0] = dv_sc[...].T


def attention_backward(q, k, v, do, lse, delta, seg, block=512):
    heads, total, dim = q.shape
    count = total // block
    scale = 1.0 / math.sqrt(dim)
    segq = seg.reshape(total, 1)
    segk = seg.reshape(1, total)
    qi, kj = _schedule(count, False)
    steps = qi.shape[0]

    def q_map(h, t, qi, kj):
        return (h, qi[t], 0)

    def k_map(h, t, qi, kj):
        return (h, kj[t], 0)

    return pl.pallas_call(
        functools.partial(_bwd_kernel, tq=block, tk=block, scale=scale, count=count),
        out_shape=(
            jax.ShapeDtypeStruct((heads, total, dim), jnp.float32),
            jax.ShapeDtypeStruct((heads, total, dim), jnp.float32),
            jax.ShapeDtypeStruct((heads, total, dim), jnp.float32),
        ),
        grid_spec=pltpu.PrefetchScalarGridSpec(
            num_scalar_prefetch=2,
            grid=(heads, steps),
            in_specs=[
                pl.BlockSpec((1, block, dim), q_map),
                pl.BlockSpec((1, block, dim), k_map),
                pl.BlockSpec((1, block, dim), k_map),
                pl.BlockSpec((1, block, dim), q_map),
                pl.BlockSpec((1, block, 1), q_map),
                pl.BlockSpec((1, block, 1), q_map),
                pl.BlockSpec((block, 1), lambda h, t, qi, kj: (qi[t], 0)),
                pl.BlockSpec((1, block), lambda h, t, qi, kj: (0, kj[t])),
            ],
            out_specs=[
                pl.BlockSpec((1, total, dim), lambda h, t, qi, kj: (h, 0, 0)),
                pl.BlockSpec((1, block, dim), k_map),
                pl.BlockSpec((1, block, dim), k_map),
            ],
            scratch_shapes=[
                pltpu.VMEM((dim, block), jnp.float32),
                pltpu.VMEM((dim, block), jnp.float32),
            ],
        ),
        cost_estimate=pl.CostEstimate(
            flops=5 * heads * total * total * dim,
            transcendentals=heads * total * total // 2,
            bytes_accessed=heads * total * dim * 24,
        ),
    )(qi, kj, q, k, v, do, lse, delta, segq, segk)


MESH_ID = pl.DeviceIdType.MESH


class Ring:
    def __init__(self, size, a_stride, b_stride):
        self.size = size
        self.half = size // 2
        self.a_stride = a_stride
        self.b_stride = b_stride

    def position(self, c):
        a = (c // self.a_stride) % self.half
        b = (c // self.b_stride) % 2
        return a + b * (2 * self.half - 1 - 2 * a)

    def device(self, pos):
        pos = pos % self.size
        b = pos // self.half
        a = pos + b * (2 * self.half - 1 - 2 * pos)
        return a * self.a_stride + b * self.b_stride


def ring_of(mesh):
    size = mesh.shape["ctx"]
    devices = list(mesh.devices.reshape(-1, size)[0])
    try:
        coords = [tuple(d.coords) for d in devices]
    except AttributeError:
        coords = None
    if coords and size % 2 == 0 and size >= 4:
        for b_stride in range(1, size):
            for a_stride in range(1, size):
                ring = Ring(size, a_stride, b_stride)
                order = [ring.device(p) for p in range(size)]
                if sorted(order) != list(range(size)):
                    continue
                hops = [
                    sum(abs(x - y) for x, y in zip(coords[order[p]], coords[order[(p + 1) % size]]))
                    for p in range(size)
                ]
                if max(hops) == 1:
                    return ring
    return Ring(size, 2, 1) if size % 2 == 0 and size >= 4 else None


def _barrier(g, left, right):
    barrier = pltpu.get_barrier_semaphore()
    for other in (left, right):
        pl.semaphore_signal(barrier, 1, device_id=(g, other), device_id_type=MESH_ID)
    pl.semaphore_wait(barrier, 2)


def _gather_kernel(x_ref, y_ref, own_sem, send_sem, recv_sem, *, ring, rows):
    n = ring.size
    half = rows // 2
    g = lax.axis_index("dp")
    c = lax.axis_index("ctx")
    pos = ring.position(c)
    right = ring.device(pos + 1)
    left = ring.device(pos + n - 1)
    own = pltpu.make_async_copy(x_ref, y_ref.at[pl.ds(c * rows, rows)], own_sem)
    own.start()
    _barrier(g, left, right)

    def link(direction, step, origin, source):
        offset = origin * rows + direction * half
        return pltpu.make_async_remote_copy(
            src_ref=source,
            dst_ref=y_ref.at[pl.ds(offset, half)],
            send_sem=send_sem.at[direction, step],
            recv_sem=recv_sem.at[direction, step],
            device_id=(g, right if direction == 0 else left),
            device_id_type=MESH_ID,
        )

    sent = []
    for step in range(n - 1):
        origins = (ring.device(pos - step + n), ring.device(pos + step))
        for direction in (0, 1):
            origin = origins[direction]
            if step == 0:
                source = x_ref.at[pl.ds(direction * half, half)]
            else:
                link(direction, step - 1, origin, None if False else y_ref.at[pl.ds(origin * rows + direction * half, half)]).wait_recv()
                source = y_ref.at[pl.ds(origin * rows + direction * half, half)]
            copy = link(direction, step, origin, source)
            copy.start()
            sent.append(copy)
    last = n - 2
    for direction, origin in ((0, ring.device(pos - last - 1 + n)), (1, ring.device(pos + last + 1))):
        link(direction, last, origin, y_ref.at[pl.ds(origin * rows + direction * half, half)]).wait_recv()
    for copy in sent:
        copy.wait_send()
    own.wait()


def ring_all_gather(x, ring, collective_id):
    rows, cols = x.shape
    n = ring.size
    return pl.pallas_call(
        functools.partial(_gather_kernel, ring=ring, rows=rows),
        out_shape=jax.ShapeDtypeStruct((n * rows, cols), x.dtype),
        in_specs=[pl.BlockSpec(memory_space=pl.ANY)],
        out_specs=pl.BlockSpec(memory_space=pl.ANY),
        scratch_shapes=[
            pltpu.SemaphoreType.DMA(()),
            pltpu.SemaphoreType.DMA((2, n - 1)),
            pltpu.SemaphoreType.DMA((2, n - 1)),
        ],
        compiler_params=pltpu.CompilerParams(collective_id=collective_id, has_side_effects=True),
    )(x)


def _scatter_kernel(p_ref, out_ref, recv_buf, send_buf, send_sem, recv_sem, *, ring, rows, parts):
    n = ring.size
    half = rows // 2
    piece = half // parts
    g = lax.axis_index("dp")
    c = lax.axis_index("ctx")
    pos = ring.position(c)
    right = ring.device(pos + 1)
    left = ring.device(pos + n - 1)
    _barrier(g, left, right)

    def link(direction, step, part):
        window = pl.ds(part * piece, piece)
        return pltpu.make_async_remote_copy(
            src_ref=send_buf.at[direction, step, window],
            dst_ref=recv_buf.at[direction, step, window],
            send_sem=send_sem.at[direction, step, part],
            recv_sem=recv_sem.at[direction, step, part],
            device_id=(g, right if direction == 0 else left),
            device_id_type=MESH_ID,
        )

    sent = []
    for step in range(n - 1):
        targets = (ring.device(pos - 1 - step + 2 * n), ring.device(pos + 1 + step))
        for part in range(parts):
            for direction in (0, 1):
                start = pl.multiple_of(
                    targets[direction] * rows + direction * half + part * piece, piece
                )
                window = pl.ds(part * piece, piece)
                total = p_ref[pl.ds(start, piece), :].astype(jnp.float32)
                if step > 0:
                    link(direction, step - 1, part).wait_recv()
                    total = total + recv_buf[direction, step - 1, window].astype(jnp.float32)
                send_buf[direction, step, window] = total.astype(send_buf.dtype)
                copy = link(direction, step, part)
                copy.start()
                sent.append(copy)
    for part in range(parts):
        for direction in (0, 1):
            link(direction, n - 2, part).wait_recv()
            start = pl.multiple_of(c * rows + direction * half + part * piece, piece)
            window = pl.ds(part * piece, piece)
            out_ref[pl.ds(direction * half + part * piece, piece), :] = (
                p_ref[pl.ds(start, piece), :].astype(jnp.float32)
                + recv_buf[direction, n - 2, window].astype(jnp.float32)
            ).astype(out_ref.dtype)
    for copy in sent:
        copy.wait_send()


def ring_reduce_scatter(p, ring, collective_id, out_dtype=jnp.float32, wire=jnp.bfloat16, parts=2):
    total_rows, cols = p.shape
    n = ring.size
    rows = total_rows // n
    half = rows // 2
    return pl.pallas_call(
        functools.partial(_scatter_kernel, ring=ring, rows=rows, parts=parts),
        out_shape=jax.ShapeDtypeStruct((rows, cols), out_dtype),
        in_specs=[pl.BlockSpec(memory_space=pltpu.VMEM)],
        out_specs=pl.BlockSpec(memory_space=pltpu.VMEM),
        scratch_shapes=[
            pltpu.VMEM((2, n - 1, half, cols), wire),
            pltpu.VMEM((2, n - 1, half, cols), wire),
            pltpu.SemaphoreType.DMA((2, n - 1, parts)),
            pltpu.SemaphoreType.DMA((2, n - 1, parts)),
        ],
        compiler_params=pltpu.CompilerParams(
            collective_id=collective_id, has_side_effects=True, vmem_limit_bytes=60 * 1024 * 1024
        ),
    )(p)


def _exchange_kernel(x_ref, out_ref, own_sem, send_sem, recv_sem, *, group):
    n = x_ref.shape[0]
    g = lax.axis_index("dp")
    c = lax.axis_index("ctx")
    n_ctx = lax.axis_size("ctx")
    me = {"all": g * n_ctx + c, "ctx": c, "dp": g}[group]

    def address(member):
        if group == "all":
            return (member // n_ctx, member % n_ctx)
        if group == "ctx":
            return (g, member)
        return (member, c)

    own = pltpu.make_async_copy(x_ref.at[me], out_ref.at[me], own_sem)
    own.start()
    barrier = pltpu.get_barrier_semaphore()
    for offset in range(1, n):
        pl.semaphore_signal(
            barrier, 1, device_id=address((me + offset) % n), device_id_type=MESH_ID
        )
    pl.semaphore_wait(barrier, n - 1)

    def link(offset, source, target):
        return pltpu.make_async_remote_copy(
            src_ref=x_ref.at[target],
            dst_ref=out_ref.at[source],
            send_sem=send_sem.at[offset],
            recv_sem=recv_sem.at[offset],
            device_id=address(target),
            device_id_type=MESH_ID,
        )

    sent = []
    for offset in range(1, n):
        copy = link(offset, me, (me + offset) % n)
        copy.start()
        sent.append(copy)
    for offset in range(1, n):
        link(offset, (me + n - offset) % n, me).wait_recv()
    for copy in sent:
        copy.wait_send()
    own.wait()


def exchange(x, group, collective_id):
    n = x.shape[0]
    space = pltpu.VMEM
    return pl.pallas_call(
        functools.partial(_exchange_kernel, group=group),
        out_shape=jax.ShapeDtypeStruct(x.shape, x.dtype),
        in_specs=[pl.BlockSpec(memory_space=space)],
        out_specs=pl.BlockSpec(memory_space=space),
        scratch_shapes=[
            pltpu.SemaphoreType.DMA(()),
            pltpu.SemaphoreType.DMA((n,)),
            pltpu.SemaphoreType.DMA((n,)),
        ],
        compiler_params=pltpu.CompilerParams(collective_id=collective_id, has_side_effects=True),
    )(x)


def block_moves(n_dp, n_ctx):
    count = n_dp * n_ctx
    return [(f, (f % n_dp) * n_ctx + f // n_dp) for f in range(count)]


def fetch_out_rows(w_out):
    n_dp = lax.axis_size("dp")
    n_ctx = lax.axis_size("ctx")
    moved = lax.ppermute(w_out.astype(jnp.bfloat16), ("dp", "ctx"), perm=block_moves(n_dp, n_ctx))
    return lax.all_gather(moved, "dp", axis=0, tiled=True)


def return_out_rows(grad_out_rows):
    n_dp = lax.axis_size("dp")
    n_ctx = lax.axis_size("ctx")
    part = lax.psum_scatter(grad_out_rows, "dp", scatter_dimension=0, tiled=True)
    back = [(b, a) for a, b in block_moves(n_dp, n_ctx)]
    return lax.ppermute(part, ("dp", "ctx"), perm=back)


def pack_rows(vector, lanes):
    size = vector.shape[0]
    total = -(-size // (16 * lanes)) * 16 * lanes
    return jnp.pad(vector, (0, total - size)).reshape(-1, lanes)


def fetch_small(b_qkv, b_out, b_fc2, ln_gain, ln_shift, b_fc1):
    pieces = (b_qkv, b_out, b_fc2, ln_gain, ln_shift, b_fc1)
    n_dp = lax.axis_size("dp")
    n_ctx = lax.axis_size("ctx")
    packed = pack_rows(jnp.concatenate([p.astype(jnp.bfloat16) for p in pieces]), 128)
    over_dp = exchange(jnp.broadcast_to(packed[None], (n_dp,) + packed.shape), "dp", 4)
    over_all = exchange(jnp.broadcast_to(over_dp[None], (n_ctx,) + over_dp.shape), "ctx", 8)
    table = over_all.transpose(1, 0, 2, 3).reshape(n_dp * n_ctx, -1)
    result = []
    offset = 0
    for p in pieces:
        result.append(table[:, offset : offset + p.shape[0]])
        offset += p.shape[0]
    return result


def reduce_small(over_ctx):
    width = over_ctx.shape[1]
    packed = jax.vmap(lambda row: pack_rows(row, 128))(over_ctx)
    over_dp = jnp.sum(exchange(packed, "dp", 9), axis=0)
    return over_dp.reshape(-1)[:width]


def fetch_heads(w_qkv, w_fc1, w_fc2, tokens):
    dp_count = lax.axis_size("dp")
    ctx_count = lax.axis_size("ctx")
    rows_piece = w_qkv.shape[0]
    head_width = D // ctx_count
    unit = FF // (dp_count * ctx_count)
    qkv_piece = w_qkv.astype(jnp.bfloat16).reshape(rows_piece, 3, ctx_count, head_width)
    fc1_piece = w_fc1.astype(jnp.bfloat16).reshape(rows_piece, dp_count, ctx_count, unit)
    pieces = jnp.concatenate(
        [
            qkv_piece.transpose(2, 0, 1, 3).reshape(ctx_count, rows_piece, 3 * head_width),
            fc1_piece.transpose(2, 0, 1, 3).reshape(ctx_count, rows_piece, dp_count * unit),
        ],
        axis=2,
    )
    sent = exchange(pieces, "ctx", 5).reshape(ctx_count * rows_piece, -1)
    sent, tokens = lax.optimization_barrier((sent, tokens))
    cols, fc2_rows = (
        lax.all_gather(sent, "dp", axis=0, tiled=True),
        lax.all_gather(w_fc2.astype(jnp.bfloat16), "dp", axis=0, tiled=True),
    )
    return (cols, fc2_rows, tokens)


def split_wide(values):
    high = values.astype(jnp.bfloat16)
    low_part = (values - high.astype(jnp.float32)).astype(jnp.bfloat16)
    return jnp.concatenate([high, low_part], axis=-1)


def join_wide(values):
    half = values.shape[-1] // 2
    return values[..., :half].astype(jnp.float32) + values[..., half:].astype(jnp.float32)


def return_heads(owned_parts, small):
    dp_count = lax.axis_size("dp")
    ctx_count = lax.axis_size("ctx")
    head_width = D // ctx_count
    unit = FF // (dp_count * ctx_count)
    rows_piece = owned_parts.shape[0] // ctx_count
    width = owned_parts.shape[1]
    small_width = small.shape[1]
    small_by_ctx = small.reshape(dp_count, ctx_count, small_width).transpose(1, 0, 2)
    coded = split_wide(small_by_ctx.reshape(ctx_count, -1))
    extra = -(-coded.shape[1] // (8 * width)) * 8
    coded = jnp.pad(coded, ((0, 0), (0, extra * width - coded.shape[1])))
    payload = jnp.concatenate(
        [owned_parts.reshape(ctx_count, rows_piece, width), coded.reshape(ctx_count, extra, width)],
        axis=1,
    )
    got = exchange(payload, "ctx", 6)
    small_got = got[:, rows_piece:, :].reshape(ctx_count, -1)[:, : 2 * dp_count * small_width]
    over_ctx = jnp.sum(join_wide(small_got), axis=0).reshape(dp_count, small_width)
    got = got[:, :rows_piece, :]
    qkv = got[:, :, : 3 * head_width].reshape(ctx_count, rows_piece, 3, head_width)
    fc1 = got[:, :, 3 * head_width :].reshape(ctx_count, rows_piece, dp_count, unit)
    return (
        qkv.transpose(1, 2, 0, 3).reshape(rows_piece, 3 * D).astype(jnp.float32),
        fc1.transpose(1, 2, 0, 3).reshape(rows_piece, FF).astype(jnp.float32),
        over_ctx,
    )


def head_plan(
    ring,
    tokens,
    lengths,
    w_qkv,
    b_qkv,
    w_out,
    b_out,
    w_fc1,
    b_fc1,
    w_fc2,
    b_fc2,
    ln_gain,
    ln_shift,
    cotangent,
):
    rows_here = tokens.shape[0]
    rows_piece = w_qkv.shape[0]
    dp_count = lax.axis_size("dp")
    ctx_count = lax.axis_size("ctx")
    count = dp_count * ctx_count
    group = rows_here * ctx_count
    head_width = D // ctx_count
    local_heads = HEADS // ctx_count
    unit = FF // (dp_count * ctx_count)
    here = lax.axis_index("ctx")
    group_rows = jnp.arange(group, dtype=jnp.int32)
    seg, positions = segment_info(lengths[0], group_rows)
    cosine, sine = rotary_tables(positions)
    qkv_bias, out_bias, fc2_bias, gain_low, shift_low, fc1_table = fetch_small(
        b_qkv, b_out, b_fc2, ln_gain, ln_shift, b_fc1
    )
    qkv_bias = qkv_bias.reshape(3 * D)
    out_bias = out_bias.reshape(D)
    fc2_bias = fc2_bias.reshape(D)
    gain_low = gain_low.reshape(D)
    shift_low = shift_low.reshape(D)
    fc1_bias = lax.dynamic_index_in_dim(
        fc1_table.reshape(dp_count, ctx_count, unit), here, 1, keepdims=False
    ).reshape(dp_count * unit)
    out_rows = fetch_out_rows(w_out)
    cols, fc2_rows, tokens = fetch_heads(w_qkv, w_fc1, w_fc2, tokens)
    gain32 = gain_low.astype(jnp.float32)
    shift32 = shift_low.astype(jnp.float32)
    inputs = tokens.astype(jnp.float32)
    normed, scaled, _ = norm_parts(inputs, gain32, shift32)
    tokens_group = ring_all_gather(tokens, ring, 0)
    late_dy, tokens_group = lax.optimization_barrier((cotangent, tokens_group))
    dy_group = lax.all_gather(late_dy, "ctx", axis=0, tiled=True)
    normed_group, _, hidden32_group = norm_parts(tokens_group.astype(jnp.float32), gain32, shift32)
    hidden_group = hidden32_group.astype(jnp.bfloat16)
    bias_cols = lax.dynamic_slice_in_dim(
        qkv_bias.reshape(3, D), here * head_width, head_width, 1
    ).reshape(3 * head_width)
    both = jnp.dot(hidden_group, cols, preferred_element_type=jnp.float32) + jnp.concatenate(
        [bias_cols, fc1_bias]
    ).astype(jnp.float32)
    qkv = both[:, : 3 * head_width]
    pre = both[:, 3 * head_width :]
    shape = (group, local_heads, HEAD_DIM)
    query = rotate(qkv[:, :head_width].reshape(shape), cosine, sine).astype(jnp.bfloat16)
    keys = rotate(qkv[:, head_width : 2 * head_width].reshape(shape), cosine, sine).astype(
        jnp.bfloat16
    )
    values = qkv[:, 2 * head_width :].reshape(shape).astype(jnp.bfloat16)
    q_heads = query.transpose(1, 0, 2)
    k_heads = keys.transpose(1, 0, 2)
    v_heads = values.transpose(1, 0, 2)
    attended_heads, log_total = attention_forward(q_heads, k_heads, v_heads, seg)
    attended = attended_heads.transpose(1, 0, 2).reshape(group, head_width).astype(jnp.bfloat16)
    act = gelu_tanh(pre).astype(jnp.bfloat16)
    branches = ring_reduce_scatter(
        jnp.dot(attended, out_rows, preferred_element_type=jnp.float32)
        + jnp.dot(act, fc2_rows, preferred_element_type=jnp.float32),
        ring,
        2,
    )
    block_out = (
        inputs + branches + out_bias.astype(jnp.float32) + fc2_bias.astype(jnp.float32)
    ).astype(jnp.bfloat16)
    grad_out32 = cotangent.astype(jnp.float32)
    grad_b_fc2 = jnp.sum(grad_out32, axis=0)
    grad_fc2_part = jnp.einsum("tf,td->fd", act, dy_group, preferred_element_type=jnp.float32)
    d_act = jnp.einsum("td,fd->tf", dy_group, fc2_rows, preferred_element_type=jnp.float32)
    d_pre = (d_act * gelu_slope(pre)).astype(jnp.bfloat16)
    grad_bfc1_part = jnp.sum(d_pre.astype(jnp.float32), axis=0)
    grad_out_rows = jnp.einsum("tc,td->cd", attended, dy_group, preferred_element_type=jnp.float32)
    owned_w_out = return_out_rows(grad_out_rows)
    d_attended = (
        jnp.einsum("td,cd->tc", dy_group, out_rows, preferred_element_type=jnp.float32)
        .astype(jnp.bfloat16)
        .reshape(shape)
    )
    d_heads = d_attended.transpose(1, 0, 2)
    delta = jnp.sum(d_heads.astype(jnp.float32) * attended_heads, axis=2, keepdims=True)
    dq_heads, dk_heads, dv_heads = attention_backward(
        q_heads, k_heads, v_heads, d_heads, log_total, delta, seg
    )
    d_query = dq_heads.transpose(1, 0, 2)
    d_keys = dk_heads.transpose(1, 0, 2)
    d_values = dv_heads.transpose(1, 0, 2)
    d_query = rotate_back(d_query, cosine, sine).reshape(group, head_width)
    d_keys = rotate_back(d_keys, cosine, sine).reshape(group, head_width)
    d_qkv = jnp.concatenate([d_query, d_keys, d_values.reshape(group, head_width)], axis=1).astype(
        jnp.bfloat16
    )
    d_both = jnp.concatenate([d_qkv, d_pre], axis=1)
    bias_part = jnp.sum(d_qkv.astype(jnp.float32), axis=0).reshape(3, head_width)
    d_hidden_part = jnp.einsum("tc,dc->td", d_both, cols, preferred_element_type=jnp.float32)
    gain_part = jnp.sum(d_hidden_part * normed_group, axis=0)
    shift_part = jnp.sum(d_hidden_part, axis=0)
    d_hidden = ring_reduce_scatter(d_hidden_part, ring, 3)
    weight_parts = jnp.einsum(
        "td,tc->dc", hidden_group, d_both, preferred_element_type=jnp.float32
    ).astype(jnp.bfloat16)
    owned_parts = lax.psum_scatter(weight_parts, "dp", scatter_dimension=0, tiled=True)
    owned_fc2 = lax.psum_scatter(
        grad_fc2_part.astype(jnp.bfloat16), "dp", scatter_dimension=0, tiled=True
    ).astype(jnp.float32)
    full_bqkv = lax.dynamic_update_slice_in_dim(
        jnp.zeros((3, D), jnp.float32), bias_part, here * head_width, 1
    )
    full_bfc1 = lax.dynamic_update_slice_in_dim(
        jnp.zeros((dp_count, ctx_count, unit), jnp.float32),
        grad_bfc1_part.reshape(dp_count, 1, unit),
        here,
        1,
    )
    small = jnp.concatenate(
        [
            full_bqkv.reshape(count, -1),
            grad_b_fc2.reshape(count, -1),
            gain_part.reshape(count, -1),
            shift_part.reshape(count, -1),
            full_bfc1.reshape(count, -1),
        ],
        axis=1,
    )
    split_qkv, split_fc1, over_ctx = return_heads(owned_parts, small)
    d_hidden, split_qkv, split_fc1, over_ctx = lax.optimization_barrier(
        (d_hidden, split_qkv, split_fc1, over_ctx)
    )
    _, _, d_inputs = norm_back(d_hidden, normed, scaled, gain32)
    grad_tokens = (grad_out32 + d_inputs).astype(jnp.bfloat16)
    owned_small = reduce_small(over_ctx)
    cuts = [0, 3 * D // count, D // count, D // count, D // count, FF // count]
    bounds = [sum(cuts[: i + 1]) for i in range(len(cuts))]
    owned_bqkv, owned_bout, owned_gain, owned_shift, owned_bfc1 = [
        owned_small[bounds[i] : bounds[i + 1]] for i in range(5)
    ]
    return (
        block_out,
        grad_tokens,
        split_qkv.reshape(rows_piece, 3 * D),
        owned_bqkv,
        owned_w_out,
        owned_bout,
        split_fc1.reshape(rows_piece, FF),
        owned_bfc1,
        owned_fc2,
        owned_bout,
        owned_gain,
        owned_shift,
    )


def body(
    ring,
    tokens,
    lengths,
    w_qkv,
    b_qkv,
    w_out,
    b_out,
    w_fc1,
    b_fc1,
    w_fc2,
    b_fc2,
    ln_gain,
    ln_shift,
    cotangent,
):
    return head_plan(
        ring,
        tokens,
        lengths,
        w_qkv,
        b_qkv,
        w_out,
        b_out,
        w_fc1,
        b_fc1,
        w_fc2,
        b_fc2,
        ln_gain,
        ln_shift,
        cotangent,
    )


def solution(mesh):
    in_specs = (
        P(("dp", "ctx"), None),
        P("dp", None),
        P(("dp", "ctx"), None),
        P(("dp", "ctx")),
        P(("dp", "ctx"), None),
        P(("dp", "ctx")),
        P(("dp", "ctx"), None),
        P(("dp", "ctx")),
        P(("dp", "ctx"), None),
        P(("dp", "ctx")),
        P(("dp", "ctx")),
        P(("dp", "ctx")),
        P(("dp", "ctx"), None),
    )
    out_specs = (
        P(("dp", "ctx"), None),
        P(("dp", "ctx"), None),
        P(("dp", "ctx"), None),
        P(("dp", "ctx")),
        P(("dp", "ctx"), None),
        P(("dp", "ctx")),
        P(("dp", "ctx"), None),
        P(("dp", "ctx")),
        P(("dp", "ctx"), None),
        P(("dp", "ctx")),
        P(("dp", "ctx")),
        P(("dp", "ctx")),
    )
    ring = ring_of(mesh)
    return jax.shard_map(functools.partial(body, ring), mesh=mesh, in_specs=in_specs, out_specs=out_specs, check_vma=False)
```

```python
import functools
import math

import jax
import jax.numpy as jnp
from jax import lax
from jax.experimental import pallas as pl
from jax.experimental.pallas import tpu as pltpu
from jax.sharding import PartitionSpec as P

D = 2048
HEADS = 32
HEAD_DIM = 64
ROT = 32
FF = 8192


EPS = 1e-05
GELU_COEF = math.sqrt(2.0 / math.pi)
NEGATIVE = -1e30


def norm_parts(inputs, gain, shift):
    mean = jnp.mean(inputs, axis=-1, keepdims=True)
    centred = inputs - mean
    var = jnp.mean(centred * centred, axis=-1, keepdims=True)
    scaled = lax.rsqrt(var + EPS)
    normed = centred * scaled
    return (normed, scaled, normed * gain + shift)


def norm_back(d_hidden, normed, scaled, gain32):
    grad_gain = jnp.sum(d_hidden * normed, axis=0)
    grad_shift = jnp.sum(d_hidden, axis=0)
    d_normed = d_hidden * gain32
    d_inputs = scaled * (
        d_normed
        - jnp.mean(d_normed, axis=-1, keepdims=True)
        - normed * jnp.mean(d_normed * normed, axis=-1, keepdims=True)
    )
    return (grad_gain, grad_shift, d_inputs)


def gelu_tanh(pre):
    return 0.5 * pre * (1.0 + jnp.tanh(GELU_COEF * (pre + 0.044715 * pre * pre * pre)))


def gelu_slope(pre):
    tangent = jnp.tanh(GELU_COEF * (pre + 0.044715 * pre * pre * pre))
    return 0.5 * (1.0 + tangent) + 0.5 * pre * (1.0 - tangent * tangent) * GELU_COEF * (
        1.0 + 3.0 * 0.044715 * pre * pre
    )


def rotary_tables(positions):
    half = ROT // 2
    freq = jnp.exp(jnp.arange(half, dtype=jnp.float32) * (-2.0 * math.log(10000.0) / ROT))
    angle = positions.astype(jnp.float32)[:, None] * freq[None, :]
    return (jnp.cos(angle)[:, None, :], jnp.sin(angle)[:, None, :])


def rotate(heads, cosine, sine):
    half = ROT // 2
    first = heads[..., :half]
    second = heads[..., half:ROT]
    return jnp.concatenate(
        [first * cosine - second * sine, second * cosine + first * sine, heads[..., ROT:]], axis=-1
    )


def rotate_back(grads, cosine, sine):
    half = ROT // 2
    first = grads[..., :half]
    second = grads[..., half:ROT]
    return jnp.concatenate(
        [first * cosine + second * sine, second * cosine - first * sine, grads[..., ROT:]], axis=-1
    )


def segment_info(lengths_row, rows):
    ends = jnp.cumsum(lengths_row)
    starts = ends - lengths_row
    seg = jnp.sum((rows[:, None] >= ends[None, :]).astype(jnp.int32), axis=1)
    onehot = seg[:, None] == jnp.arange(lengths_row.shape[0], dtype=jnp.int32)[None, :]
    first_rows = jnp.sum(jnp.where(onehot, starts[None, :], 0), axis=1)
    return (seg, rows - first_rows)


TRANS_B = (((1,), (1,)), ((), ()))


def _allowed(segq_ref, segk_ref, i, j, tq, tk, causal):
    same = segq_ref[...] == segk_ref[...]
    if not causal:
        return same
    rows = i * tq + lax.broadcasted_iota(jnp.int32, (tq, tk), 0)
    cols = j * tk + lax.broadcasted_iota(jnp.int32, (tq, tk), 1)
    return same & (cols <= rows)


def _fwd_kernel(qi_ref, kj_ref, q_ref, k_ref, v_ref, segq_ref, segk_ref, o_ref, lse_ref, m_sc, acc_sc, *, tq, tk, scale):
    t = pl.program_id(1)
    i = qi_ref[t]
    j = kj_ref[t]
    dim = o_ref.shape[2]

    @pl.when(j == 0)
    def _():
        m_sc[...] = jnp.full_like(m_sc, NEGATIVE)
        acc_sc[...] = jnp.zeros_like(acc_sc)

    def absorb(causal):
        q = q_ref[0]
        k = k_ref[0]
        s = lax.dot_general(q, k, TRANS_B, preferred_element_type=jnp.float32) * scale
        s = jnp.where(_allowed(segq_ref, segk_ref, i, j, tq, tk, causal), s, -jnp.inf)
        m_prev = m_sc[...]
        lanes = s.shape[1]
        folded = s[:, :128]
        for start in range(128, lanes, 128):
            folded = jnp.maximum(folded, s[:, start : start + 128])
        m_new = jnp.maximum(m_prev, jnp.max(folded, axis=1, keepdims=True))
        factor = jnp.exp(m_prev - m_new)
        p = jnp.exp(s - m_new)
        acc_sc[...] = acc_sc[...] * factor + jnp.dot(
            p.astype(jnp.bfloat16), v_ref[0], preferred_element_type=jnp.float32
        )
        m_sc[...] = m_new

    @pl.when(j < i)
    def _():
        absorb(False)

    @pl.when(j == i)
    def _():
        absorb(True)
        acc = acc_sc[...]
        total = acc[:, dim : dim + 1]
        o_ref[0] = acc[:, :dim] / total
        lse_ref[0] = m_sc[...] + jnp.log(total)


def _schedule(count, queries_outer):
    if queries_outer:
        pairs = [(i, j) for i in range(count) for j in range(i + 1)]
    else:
        pairs = [(i, j) for j in range(count) for i in range(j, count)]
    return (
        jnp.asarray([p[0] for p in pairs], jnp.int32),
        jnp.asarray([p[1] for p in pairs], jnp.int32),
    )


def attention_forward(q, k, v, seg, block=1024):
    heads, total, dim = q.shape
    count = total // block
    scale = 1.0 / math.sqrt(dim)
    segq = seg.reshape(total, 1)
    segk = seg.reshape(1, total)
    qi, kj = _schedule(count, True)
    steps = qi.shape[0]
    lanes = 2 * dim
    v_ext = jnp.concatenate(
        [v, jnp.ones((heads, total, 1), v.dtype), jnp.zeros((heads, total, lanes - dim - 1), v.dtype)],
        axis=2,
    )

    return pl.pallas_call(
        functools.partial(_fwd_kernel, tq=block, tk=block, scale=scale),
        out_shape=(
            jax.ShapeDtypeStruct((heads, total, dim), jnp.float32),
            jax.ShapeDtypeStruct((heads, total, 1), jnp.float32),
        ),
        grid_spec=pltpu.PrefetchScalarGridSpec(
            num_scalar_prefetch=2,
            grid=(heads, steps),
            in_specs=[
                pl.BlockSpec((1, block, dim), lambda h, t, qi, kj: (h, qi[t], 0)),
                pl.BlockSpec((1, block, dim), lambda h, t, qi, kj: (h, kj[t], 0)),
                pl.BlockSpec((1, block, lanes), lambda h, t, qi, kj: (h, kj[t], 0)),
                pl.BlockSpec((block, 1), lambda h, t, qi, kj: (qi[t], 0)),
                pl.BlockSpec((1, block), lambda h, t, qi, kj: (0, kj[t])),
            ],
            out_specs=[
                pl.BlockSpec((1, block, dim), lambda h, t, qi, kj: (h, qi[t], 0)),
                pl.BlockSpec((1, block, 1), lambda h, t, qi, kj: (h, qi[t], 0)),
            ],
            scratch_shapes=[
                pltpu.VMEM((block, 1), jnp.float32),
                pltpu.VMEM((block, lanes), jnp.float32),
            ],
        ),
        cost_estimate=pl.CostEstimate(
            flops=2 * heads * total * total * dim,
            transcendentals=heads * total * total // 2,
            bytes_accessed=heads * total * dim * 10,
        ),
    )(qi, kj, q, k, v_ext, segq, segk)


def _bwd_kernel(qi_ref, kj_ref, q_ref, k_ref, v_ref, do_ref, lse_ref, delta_ref, segq_ref, segk_ref, dq_ref, dk_ref, dv_ref, dk_sc, dv_sc, *, tq, tk, scale, count):
    t = pl.program_id(1)
    i = qi_ref[t]
    j = kj_ref[t]

    @pl.when(t == 0)
    def _():
        dq_ref[...] = jnp.zeros_like(dq_ref)

    @pl.when(i == j)
    def _():
        dk_sc[...] = jnp.zeros_like(dk_sc)
        dv_sc[...] = jnp.zeros_like(dv_sc)

    def absorb(causal):
        q = q_ref[0]
        k = k_ref[0]
        do = do_ref[0]
        s = lax.dot_general(q, k, TRANS_B, preferred_element_type=jnp.float32) * scale
        s = jnp.where(_allowed(segq_ref, segk_ref, i, j, tq, tk, causal), s, -jnp.inf)
        p = jnp.exp(s - lse_ref[0])
        dp = lax.dot_general(do, v_ref[0], TRANS_B, preferred_element_type=jnp.float32)
        ds = (p * (dp - delta_ref[0])).astype(jnp.bfloat16)
        dv_sc[...] += jnp.dot(do.T, p.astype(jnp.bfloat16), preferred_element_type=jnp.float32)
        dk_sc[...] += jnp.dot(q.T, ds, preferred_element_type=jnp.float32)
        rows = pl.ds(pl.multiple_of(i * tq, tq), tq)
        dq_ref[0, rows, :] += lax.dot(ds, k, preferred_element_type=jnp.float32) * scale

    @pl.when(j < i)
    def _():
        absorb(False)

    @pl.when(j == i)
    def _():
        absorb(True)

    @pl.when(i == count - 1)
    def _():
        dk_ref[0] = dk_sc[...].T * scale
        dv_ref[0] = dv_sc[...].T


def attention_backward(q, k, v, do, lse, delta, seg, block=1024):
    heads, total, dim = q.shape
    count = total // block
    scale = 1.0 / math.sqrt(dim)
    segq = seg.reshape(total, 1)
    segk = seg.reshape(1, total)
    qi, kj = _schedule(count, False)
    steps = qi.shape[0]

    def q_map(h, t, qi, kj):
        return (h, qi[t], 0)

    def k_map(h, t, qi, kj):
        return (h, kj[t], 0)

    return pl.pallas_call(
        functools.partial(_bwd_kernel, tq=block, tk=block, scale=scale, count=count),
        out_shape=(
            jax.ShapeDtypeStruct((heads, total, dim), jnp.float32),
            jax.ShapeDtypeStruct((heads, total, dim), jnp.float32),
            jax.ShapeDtypeStruct((heads, total, dim), jnp.float32),
        ),
        grid_spec=pltpu.PrefetchScalarGridSpec(
            num_scalar_prefetch=2,
            grid=(heads, steps),
            in_specs=[
                pl.BlockSpec((1, block, dim), q_map),
                pl.BlockSpec((1, block, dim), k_map),
                pl.BlockSpec((1, block, dim), k_map),
                pl.BlockSpec((1, block, dim), q_map),
                pl.BlockSpec((1, block, 1), q_map),
                pl.BlockSpec((1, block, 1), q_map),
                pl.BlockSpec((block, 1), lambda h, t, qi, kj: (qi[t], 0)),
                pl.BlockSpec((1, block), lambda h, t, qi, kj: (0, kj[t])),
            ],
            out_specs=[
                pl.BlockSpec((1, total, dim), lambda h, t, qi, kj: (h, 0, 0)),
                pl.BlockSpec((1, block, dim), k_map),
                pl.BlockSpec((1, block, dim), k_map),
            ],
            scratch_shapes=[
                pltpu.VMEM((dim, block), jnp.float32),
                pltpu.VMEM((dim, block), jnp.float32),
            ],
        ),
        cost_estimate=pl.CostEstimate(
            flops=5 * heads * total * total * dim,
            transcendentals=heads * total * total // 2,
            bytes_accessed=heads * total * dim * 24,
        ),
    )(qi, kj, q, k, v, do, lse, delta, segq, segk)


MESH_ID = pl.DeviceIdType.MESH


class Ring:
    def __init__(self, size, a_stride, b_stride):
        self.size = size
        self.half = size // 2
        self.a_stride = a_stride
        self.b_stride = b_stride

    def position(self, c):
        a = (c // self.a_stride) % self.half
        b = (c // self.b_stride) % 2
        return a + b * (2 * self.half - 1 - 2 * a)

    def device(self, pos):
        pos = pos % self.size
        b = pos // self.half
        a = pos + b * (2 * self.half - 1 - 2 * pos)
        return a * self.a_stride + b * self.b_stride


def ring_of(mesh):
    size = mesh.shape["ctx"]
    devices = list(mesh.devices.reshape(-1, size)[0])
    try:
        coords = [tuple(d.coords) for d in devices]
    except AttributeError:
        coords = None
    if coords and size % 2 == 0 and size >= 4:
        for b_stride in range(1, size):
            for a_stride in range(1, size):
                ring = Ring(size, a_stride, b_stride)
                order = [ring.device(p) for p in range(size)]
                if sorted(order) != list(range(size)):
                    continue
                hops = [
                    sum(abs(x - y) for x, y in zip(coords[order[p]], coords[order[(p + 1) % size]]))
                    for p in range(size)
                ]
                if max(hops) == 1:
                    return ring
    return Ring(size, 2, 1) if size % 2 == 0 and size >= 4 else None


def _barrier(g, left, right):
    barrier = pltpu.get_barrier_semaphore()
    for other in (left, right):
        pl.semaphore_signal(barrier, 1, device_id=(g, other), device_id_type=MESH_ID)
    pl.semaphore_wait(barrier, 2)


def _gather_kernel(x_ref, y_ref, own_sem, send_sem, recv_sem, *, ring, rows):
    n = ring.size
    half = rows // 2
    g = lax.axis_index("dp")
    c = lax.axis_index("ctx")
    pos = ring.position(c)
    right = ring.device(pos + 1)
    left = ring.device(pos + n - 1)
    own = pltpu.make_async_copy(x_ref, y_ref.at[pl.ds(c * rows, rows)], own_sem)
    own.start()
    _barrier(g, left, right)

    def link(direction, step, origin, source):
        offset = origin * rows + direction * half
        return pltpu.make_async_remote_copy(
            src_ref=source,
            dst_ref=y_ref.at[pl.ds(offset, half)],
            send_sem=send_sem.at[direction, step],
            recv_sem=recv_sem.at[direction, step],
            device_id=(g, right if direction == 0 else left),
            device_id_type=MESH_ID,
        )

    sent = []
    for step in range(n - 1):
        origins = (ring.device(pos - step + n), ring.device(pos + step))
        for direction in (0, 1):
            origin = origins[direction]
            if step == 0:
                source = x_ref.at[pl.ds(direction * half, half)]
            else:
                link(direction, step - 1, origin, None if False else y_ref.at[pl.ds(origin * rows + direction * half, half)]).wait_recv()
                source = y_ref.at[pl.ds(origin * rows + direction * half, half)]
            copy = link(direction, step, origin, source)
            copy.start()
            sent.append(copy)
    last = n - 2
    for direction, origin in ((0, ring.device(pos - last - 1 + n)), (1, ring.device(pos + last + 1))):
        link(direction, last, origin, y_ref.at[pl.ds(origin * rows + direction * half, half)]).wait_recv()
    for copy in sent:
        copy.wait_send()
    own.wait()


def ring_all_gather(x, ring, collective_id):
    rows, cols = x.shape
    n = ring.size
    return pl.pallas_call(
        functools.partial(_gather_kernel, ring=ring, rows=rows),
        out_shape=jax.ShapeDtypeStruct((n * rows, cols), x.dtype),
        in_specs=[pl.BlockSpec(memory_space=pl.ANY)],
        out_specs=pl.BlockSpec(memory_space=pl.ANY),
        scratch_shapes=[
            pltpu.SemaphoreType.DMA(()),
            pltpu.SemaphoreType.DMA((2, n - 1)),
            pltpu.SemaphoreType.DMA((2, n - 1)),
        ],
        compiler_params=pltpu.CompilerParams(collective_id=collective_id, has_side_effects=True),
    )(x)


def _scatter_kernel(p_ref, out_ref, recv_buf, send_buf, send_sem, recv_sem, *, ring, rows, parts):
    n = ring.size
    half = rows // 2
    piece = half // parts
    g = lax.axis_index("dp")
    c = lax.axis_index("ctx")
    pos = ring.position(c)
    right = ring.device(pos + 1)
    left = ring.device(pos + n - 1)
    _barrier(g, left, right)

    def link(direction, step, part):
        window = pl.ds(part * piece, piece)
        return pltpu.make_async_remote_copy(
            src_ref=send_buf.at[direction, step, window],
            dst_ref=recv_buf.at[direction, step, window],
            send_sem=send_sem.at[direction, step, part],
            recv_sem=recv_sem.at[direction, step, part],
            device_id=(g, right if direction == 0 else left),
            device_id_type=MESH_ID,
        )

    sent = []
    for step in range(n - 1):
        targets = (ring.device(pos - 1 - step + 2 * n), ring.device(pos + 1 + step))
        for part in range(parts):
            for direction in (0, 1):
                start = pl.multiple_of(
                    targets[direction] * rows + direction * half + part * piece, piece
                )
                window = pl.ds(part * piece, piece)
                total = p_ref[pl.ds(start, piece), :].astype(jnp.float32)
                if step > 0:
                    link(direction, step - 1, part).wait_recv()
                    total = total + recv_buf[direction, step - 1, window].astype(jnp.float32)
                send_buf[direction, step, window] = total.astype(send_buf.dtype)
                copy = link(direction, step, part)
                copy.start()
                sent.append(copy)
    for part in range(parts):
        for direction in (0, 1):
            link(direction, n - 2, part).wait_recv()
            start = pl.multiple_of(c * rows + direction * half + part * piece, piece)
            window = pl.ds(part * piece, piece)
            out_ref[pl.ds(direction * half + part * piece, piece), :] = (
                p_ref[pl.ds(start, piece), :].astype(jnp.float32)
                + recv_buf[direction, n - 2, window].astype(jnp.float32)
            ).astype(out_ref.dtype)
    for copy in sent:
        copy.wait_send()


def ring_reduce_scatter(p, ring, collective_id, out_dtype=jnp.float32, wire=jnp.bfloat16, parts=2):
    total_rows, cols = p.shape
    n = ring.size
    rows = total_rows // n
    half = rows // 2
    return pl.pallas_call(
        functools.partial(_scatter_kernel, ring=ring, rows=rows, parts=parts),
        out_shape=jax.ShapeDtypeStruct((rows, cols), out_dtype),
        in_specs=[pl.BlockSpec(memory_space=pltpu.VMEM)],
        out_specs=pl.BlockSpec(memory_space=pltpu.VMEM),
        scratch_shapes=[
            pltpu.VMEM((2, n - 1, half, cols), wire),
            pltpu.VMEM((2, n - 1, half, cols), wire),
            pltpu.SemaphoreType.DMA((2, n - 1, parts)),
            pltpu.SemaphoreType.DMA((2, n - 1, parts)),
        ],
        compiler_params=pltpu.CompilerParams(
            collective_id=collective_id, has_side_effects=True, vmem_limit_bytes=60 * 1024 * 1024
        ),
    )(p)


def _exchange_kernel(x_ref, out_ref, own_sem, send_sem, recv_sem, *, group):
    n = x_ref.shape[0]
    g = lax.axis_index("dp")
    c = lax.axis_index("ctx")
    n_ctx = lax.axis_size("ctx")
    me = {"all": g * n_ctx + c, "ctx": c, "dp": g}[group]

    def address(member):
        if group == "all":
            return (member // n_ctx, member % n_ctx)
        if group == "ctx":
            return (g, member)
        return (member, c)

    own = pltpu.make_async_copy(x_ref.at[me], out_ref.at[me], own_sem)
    own.start()
    barrier = pltpu.get_barrier_semaphore()
    for offset in range(1, n):
        pl.semaphore_signal(
            barrier, 1, device_id=address((me + offset) % n), device_id_type=MESH_ID
        )
    pl.semaphore_wait(barrier, n - 1)

    def link(offset, source, target):
        return pltpu.make_async_remote_copy(
            src_ref=x_ref.at[target],
            dst_ref=out_ref.at[source],
            send_sem=send_sem.at[offset],
            recv_sem=recv_sem.at[offset],
            device_id=address(target),
            device_id_type=MESH_ID,
        )

    sent = []
    for offset in range(1, n):
        copy = link(offset, me, (me + offset) % n)
        copy.start()
        sent.append(copy)
    for offset in range(1, n):
        link(offset, (me + n - offset) % n, me).wait_recv()
    for copy in sent:
        copy.wait_send()
    own.wait()


def exchange(x, group, collective_id):
    n = x.shape[0]
    space = pltpu.VMEM
    return pl.pallas_call(
        functools.partial(_exchange_kernel, group=group),
        out_shape=jax.ShapeDtypeStruct(x.shape, x.dtype),
        in_specs=[pl.BlockSpec(memory_space=space)],
        out_specs=pl.BlockSpec(memory_space=space),
        scratch_shapes=[
            pltpu.SemaphoreType.DMA(()),
            pltpu.SemaphoreType.DMA((n,)),
            pltpu.SemaphoreType.DMA((n,)),
        ],
        compiler_params=pltpu.CompilerParams(collective_id=collective_id, has_side_effects=True),
    )(x)


def block_moves(n_dp, n_ctx):
    count = n_dp * n_ctx
    return [(f, (f % n_dp) * n_ctx + f // n_dp) for f in range(count)]


def fetch_out_rows(w_out):
    n_dp = lax.axis_size("dp")
    n_ctx = lax.axis_size("ctx")
    moved = lax.ppermute(w_out.astype(jnp.bfloat16), ("dp", "ctx"), perm=block_moves(n_dp, n_ctx))
    return lax.all_gather(moved, "dp", axis=0, tiled=True)


def return_out_rows(grad_out_rows):
    n_dp = lax.axis_size("dp")
    n_ctx = lax.axis_size("ctx")
    part = lax.psum_scatter(grad_out_rows, "dp", scatter_dimension=0, tiled=True)
    back = [(b, a) for a, b in block_moves(n_dp, n_ctx)]
    return lax.ppermute(part, ("dp", "ctx"), perm=back)


def pack_rows(vector, lanes):
    size = vector.shape[0]
    total = -(-size // (16 * lanes)) * 16 * lanes
    return jnp.pad(vector, (0, total - size)).reshape(-1, lanes)


def fetch_small(b_qkv, b_out, b_fc2, ln_gain, ln_shift, b_fc1):
    pieces = (b_qkv, b_out, b_fc2, ln_gain, ln_shift, b_fc1)
    n_dp = lax.axis_size("dp")
    n_ctx = lax.axis_size("ctx")
    packed = pack_rows(jnp.concatenate([p.astype(jnp.bfloat16) for p in pieces]), 128)
    over_dp = exchange(jnp.broadcast_to(packed[None], (n_dp,) + packed.shape), "dp", 4)
    over_all = exchange(jnp.broadcast_to(over_dp[None], (n_ctx,) + over_dp.shape), "ctx", 8)
    table = over_all.transpose(1, 0, 2, 3).reshape(n_dp * n_ctx, -1)
    result = []
    offset = 0
    for p in pieces:
        result.append(table[:, offset : offset + p.shape[0]])
        offset += p.shape[0]
    return result


def reduce_small(small):
    n_dp = lax.axis_size("dp")
    n_ctx = lax.axis_size("ctx")
    count, width = small.shape
    packed = jax.vmap(lambda row: pack_rows(row, 128))(small)
    packed = packed.reshape((n_dp, n_ctx) + packed.shape[1:]).transpose(1, 0, 2, 3)
    over_ctx = jnp.sum(exchange(packed, "ctx", 7), axis=0)
    over_dp = jnp.sum(exchange(over_ctx, "dp", 9), axis=0)
    return over_dp.reshape(-1)[:width]


def fetch_heads(w_qkv, w_fc1, w_fc2, tokens):
    dp_count = lax.axis_size("dp")
    ctx_count = lax.axis_size("ctx")
    rows_piece = w_qkv.shape[0]
    head_width = D // ctx_count
    unit = FF // (dp_count * ctx_count)
    qkv_piece = w_qkv.astype(jnp.bfloat16).reshape(rows_piece, 3, ctx_count, head_width)
    fc1_piece = w_fc1.astype(jnp.bfloat16).reshape(rows_piece, dp_count, ctx_count, unit)
    pieces = jnp.concatenate(
        [
            qkv_piece.transpose(2, 0, 1, 3).reshape(ctx_count, rows_piece, 3 * head_width),
            fc1_piece.transpose(2, 0, 1, 3).reshape(ctx_count, rows_piece, dp_count * unit),
        ],
        axis=2,
    )
    sent = exchange(pieces, "ctx", 5).reshape(ctx_count * rows_piece, -1)
    sent, tokens = lax.optimization_barrier((sent, tokens))
    cols, fc2_rows = (
        lax.all_gather(sent, "dp", axis=0, tiled=True),
        lax.all_gather(w_fc2.astype(jnp.bfloat16), "dp", axis=0, tiled=True),
    )
    return (cols, fc2_rows, tokens)


def return_heads(owned_parts):
    dp_count = lax.axis_size("dp")
    ctx_count = lax.axis_size("ctx")
    head_width = D // ctx_count
    unit = FF // (dp_count * ctx_count)
    rows_piece = owned_parts.shape[0] // ctx_count
    got = exchange(owned_parts.reshape(ctx_count, rows_piece, -1), "ctx", 6)
    qkv = got[:, :, : 3 * head_width].reshape(ctx_count, rows_piece, 3, head_width)
    fc1 = got[:, :, 3 * head_width :].reshape(ctx_count, rows_piece, dp_count, unit)
    return (
        qkv.transpose(1, 2, 0, 3).reshape(rows_piece, 3 * D).astype(jnp.float32),
        fc1.transpose(1, 2, 0, 3).reshape(rows_piece, FF).astype(jnp.float32),
    )


def head_plan(
    ring,
    tokens,
    lengths,
    w_qkv,
    b_qkv,
    w_out,
    b_out,
    w_fc1,
    b_fc1,
    w_fc2,
    b_fc2,
    ln_gain,
    ln_shift,
    cotangent,
):
    rows_here = tokens.shape[0]
    rows_piece = w_qkv.shape[0]
    dp_count = lax.axis_size("dp")
    ctx_count = lax.axis_size("ctx")
    count = dp_count * ctx_count
    group = rows_here * ctx_count
    head_width = D // ctx_count
    local_heads = HEADS // ctx_count
    unit = FF // (dp_count * ctx_count)
    here = lax.axis_index("ctx")
    group_rows = jnp.arange(group, dtype=jnp.int32)
    seg, positions = segment_info(lengths[0], group_rows)
    cosine, sine = rotary_tables(positions)
    qkv_bias, out_bias, fc2_bias, gain_low, shift_low, fc1_table = fetch_small(
        b_qkv, b_out, b_fc2, ln_gain, ln_shift, b_fc1
    )
    qkv_bias = qkv_bias.reshape(3 * D)
    out_bias = out_bias.reshape(D)
    fc2_bias = fc2_bias.reshape(D)
    gain_low = gain_low.reshape(D)
    shift_low = shift_low.reshape(D)
    fc1_bias = lax.dynamic_index_in_dim(
        fc1_table.reshape(dp_count, ctx_count, unit), here, 1, keepdims=False
    ).reshape(dp_count * unit)
    out_rows = fetch_out_rows(w_out)
    cols, fc2_rows, tokens = fetch_heads(w_qkv, w_fc1, w_fc2, tokens)
    gain32 = gain_low.astype(jnp.float32)
    shift32 = shift_low.astype(jnp.float32)
    inputs = tokens.astype(jnp.float32)
    normed, scaled, _ = norm_parts(inputs, gain32, shift32)
    tokens_group = ring_all_gather(tokens, ring, 0)
    late_dy, tokens_group = lax.optimization_barrier((cotangent, tokens_group))
    dy_group = lax.all_gather(late_dy, "ctx", axis=0, tiled=True)
    hidden_group = norm_parts(tokens_group.astype(jnp.float32), gain32, shift32)[2].astype(
        jnp.bfloat16
    )
    bias_cols = lax.dynamic_slice_in_dim(
        qkv_bias.reshape(3, D), here * head_width, head_width, 1
    ).reshape(3 * head_width)
    both = jnp.dot(hidden_group, cols, preferred_element_type=jnp.float32) + jnp.concatenate(
        [bias_cols, fc1_bias]
    ).astype(jnp.float32)
    qkv = both[:, : 3 * head_width]
    pre = both[:, 3 * head_width :]
    shape = (group, local_heads, HEAD_DIM)
    query = rotate(qkv[:, :head_width].reshape(shape), cosine, sine).astype(jnp.bfloat16)
    keys = rotate(qkv[:, head_width : 2 * head_width].reshape(shape), cosine, sine).astype(
        jnp.bfloat16
    )
    values = qkv[:, 2 * head_width :].reshape(shape).astype(jnp.bfloat16)
    q_heads = query.transpose(1, 0, 2)
    k_heads = keys.transpose(1, 0, 2)
    v_heads = values.transpose(1, 0, 2)
    attended_heads, log_total = attention_forward(q_heads, k_heads, v_heads, seg)
    attended = attended_heads.transpose(1, 0, 2).reshape(group, head_width).astype(jnp.bfloat16)
    act = gelu_tanh(pre).astype(jnp.bfloat16)
    branches = ring_reduce_scatter(
        jnp.dot(attended, out_rows, preferred_element_type=jnp.float32)
        + jnp.dot(act, fc2_rows, preferred_element_type=jnp.float32),
        ring,
        2,
    )
    block_out = (
        inputs + branches + out_bias.astype(jnp.float32) + fc2_bias.astype(jnp.float32)
    ).astype(jnp.bfloat16)
    grad_out32 = cotangent.astype(jnp.float32)
    grad_b_fc2 = jnp.sum(grad_out32, axis=0)
    grad_fc2_part = jnp.einsum("tf,td->fd", act, dy_group, preferred_element_type=jnp.float32)
    d_act = jnp.einsum("td,fd->tf", dy_group, fc2_rows, preferred_element_type=jnp.float32)
    d_pre = (d_act * gelu_slope(pre)).astype(jnp.bfloat16)
    grad_bfc1_part = jnp.sum(d_pre.astype(jnp.float32), axis=0)
    grad_out_rows = jnp.einsum("tc,td->cd", attended, dy_group, preferred_element_type=jnp.float32)
    owned_w_out = return_out_rows(grad_out_rows)
    d_attended = (
        jnp.einsum("td,cd->tc", dy_group, out_rows, preferred_element_type=jnp.float32)
        .astype(jnp.bfloat16)
        .reshape(shape)
    )
    d_heads = d_attended.transpose(1, 0, 2)
    delta = jnp.sum(d_heads.astype(jnp.float32) * attended_heads, axis=2, keepdims=True)
    dq_heads, dk_heads, dv_heads = attention_backward(
        q_heads, k_heads, v_heads, d_heads, log_total, delta, seg
    )
    d_query = dq_heads.transpose(1, 0, 2)
    d_keys = dk_heads.transpose(1, 0, 2)
    d_values = dv_heads.transpose(1, 0, 2)
    d_query = rotate_back(d_query, cosine, sine).reshape(group, head_width)
    d_keys = rotate_back(d_keys, cosine, sine).reshape(group, head_width)
    d_qkv = jnp.concatenate([d_query, d_keys, d_values.reshape(group, head_width)], axis=1).astype(
        jnp.bfloat16
    )
    d_both = jnp.concatenate([d_qkv, d_pre], axis=1)
    bias_part = jnp.sum(d_qkv.astype(jnp.float32), axis=0).reshape(3, head_width)
    d_hidden = ring_reduce_scatter(
        jnp.einsum("tc,dc->td", d_both, cols, preferred_element_type=jnp.float32), ring, 3
    )
    weight_parts = jnp.einsum(
        "td,tc->dc", hidden_group, d_both, preferred_element_type=jnp.float32
    ).astype(jnp.bfloat16)
    owned_parts = lax.psum_scatter(weight_parts, "dp", scatter_dimension=0, tiled=True)
    split_qkv, split_fc1 = return_heads(owned_parts)
    d_hidden, split_qkv, split_fc1 = lax.optimization_barrier((d_hidden, split_qkv, split_fc1))
    grad_gain, grad_shift, d_inputs = norm_back(d_hidden, normed, scaled, gain32)
    grad_tokens = (grad_out32 + d_inputs).astype(jnp.bfloat16)
    owned_fc2 = lax.psum_scatter(
        grad_fc2_part.astype(jnp.bfloat16), "dp", scatter_dimension=0, tiled=True
    ).astype(jnp.float32)
    full_bqkv = lax.dynamic_update_slice_in_dim(
        jnp.zeros((3, D), jnp.float32), bias_part, here * head_width, 1
    )
    full_bfc1 = lax.dynamic_update_slice_in_dim(
        jnp.zeros((dp_count, ctx_count, unit), jnp.float32),
        grad_bfc1_part.reshape(dp_count, 1, unit),
        here,
        1,
    )
    small = jnp.concatenate(
        [
            full_bqkv.reshape(count, -1),
            grad_b_fc2.reshape(count, -1),
            grad_gain.reshape(count, -1),
            grad_shift.reshape(count, -1),
            full_bfc1.reshape(count, -1),
        ],
        axis=1,
    )
    owned_small = reduce_small(small)
    cuts = [0, 3 * D // count, D // count, D // count, D // count, FF // count]
    bounds = [sum(cuts[: i + 1]) for i in range(len(cuts))]
    owned_bqkv, owned_bout, owned_gain, owned_shift, owned_bfc1 = [
        owned_small[bounds[i] : bounds[i + 1]] for i in range(5)
    ]
    return (
        block_out,
        grad_tokens,
        split_qkv.reshape(rows_piece, 3 * D),
        owned_bqkv,
        owned_w_out,
        owned_bout,
        split_fc1.reshape(rows_piece, FF),
        owned_bfc1,
        owned_fc2,
        owned_bout,
        owned_gain,
        owned_shift,
    )


def body(
    ring,
    tokens,
    lengths,
    w_qkv,
    b_qkv,
    w_out,
    b_out,
    w_fc1,
    b_fc1,
    w_fc2,
    b_fc2,
    ln_gain,
    ln_shift,
    cotangent,
):
    return head_plan(
        ring,
        tokens,
        lengths,
        w_qkv,
        b_qkv,
        w_out,
        b_out,
        w_fc1,
        b_fc1,
        w_fc2,
        b_fc2,
        ln_gain,
        ln_shift,
        cotangent,
    )


def solution(mesh):
    in_specs = (
        P(("dp", "ctx"), None),
        P("dp", None),
        P(("dp", "ctx"), None),
        P(("dp", "ctx")),
        P(("dp", "ctx"), None),
        P(("dp", "ctx")),
        P(("dp", "ctx"), None),
        P(("dp", "ctx")),
        P(("dp", "ctx"), None),
        P(("dp", "ctx")),
        P(("dp", "ctx")),
        P(("dp", "ctx")),
        P(("dp", "ctx"), None),
    )
    out_specs = (
        P(("dp", "ctx"), None),
        P(("dp", "ctx"), None),
        P(("dp", "ctx"), None),
        P(("dp", "ctx")),
        P(("dp", "ctx"), None),
        P(("dp", "ctx")),
        P(("dp", "ctx"), None),
        P(("dp", "ctx")),
        P(("dp", "ctx"), None),
        P(("dp", "ctx")),
        P(("dp", "ctx")),
        P(("dp", "ctx")),
    )
    ring = ring_of(mesh)
    return jax.shard_map(functools.partial(body, ring), mesh=mesh, in_specs=in_specs, out_specs=out_specs, check_vma=False)
```

```python
import functools
import math

import jax
import jax.numpy as jnp
from jax import lax
from jax.experimental import pallas as pl
from jax.experimental.pallas import tpu as pltpu
from jax.sharding import PartitionSpec as P

D = 2048
HEADS = 32
HEAD_DIM = 64
ROT = 32
FF = 8192


EPS = 1e-05
GELU_COEF = math.sqrt(2.0 / math.pi)
NEGATIVE = -1e30


def norm_parts(inputs, gain, shift):
    mean = jnp.mean(inputs, axis=-1, keepdims=True)
    centred = inputs - mean
    var = jnp.mean(centred * centred, axis=-1, keepdims=True)
    scaled = lax.rsqrt(var + EPS)
    normed = centred * scaled
    return (normed, scaled, normed * gain + shift)


def norm_back(d_hidden, normed, scaled, gain32):
    grad_gain = jnp.sum(d_hidden * normed, axis=0)
    grad_shift = jnp.sum(d_hidden, axis=0)
    d_normed = d_hidden * gain32
    d_inputs = scaled * (
        d_normed
        - jnp.mean(d_normed, axis=-1, keepdims=True)
        - normed * jnp.mean(d_normed * normed, axis=-1, keepdims=True)
    )
    return (grad_gain, grad_shift, d_inputs)


def gelu_tanh(pre):
    return 0.5 * pre * (1.0 + jnp.tanh(GELU_COEF * (pre + 0.044715 * pre * pre * pre)))


def gelu_slope(pre):
    tangent = jnp.tanh(GELU_COEF * (pre + 0.044715 * pre * pre * pre))
    return 0.5 * (1.0 + tangent) + 0.5 * pre * (1.0 - tangent * tangent) * GELU_COEF * (
        1.0 + 3.0 * 0.044715 * pre * pre
    )


def rotary_tables(positions):
    half = ROT // 2
    freq = jnp.exp(jnp.arange(half, dtype=jnp.float32) * (-2.0 * math.log(10000.0) / ROT))
    angle = positions.astype(jnp.float32)[:, None] * freq[None, :]
    return (jnp.cos(angle)[:, None, :], jnp.sin(angle)[:, None, :])


def rotate(heads, cosine, sine):
    half = ROT // 2
    first = heads[..., :half]
    second = heads[..., half:ROT]
    return jnp.concatenate(
        [first * cosine - second * sine, second * cosine + first * sine, heads[..., ROT:]], axis=-1
    )


def rotate_back(grads, cosine, sine):
    half = ROT // 2
    first = grads[..., :half]
    second = grads[..., half:ROT]
    return jnp.concatenate(
        [first * cosine + second * sine, second * cosine - first * sine, grads[..., ROT:]], axis=-1
    )


def segment_info(lengths_row, rows):
    ends = jnp.cumsum(lengths_row)
    starts = ends - lengths_row
    seg = jnp.sum((rows[:, None] >= ends[None, :]).astype(jnp.int32), axis=1)
    onehot = seg[:, None] == jnp.arange(lengths_row.shape[0], dtype=jnp.int32)[None, :]
    first_rows = jnp.sum(jnp.where(onehot, starts[None, :], 0), axis=1)
    return (seg, rows - first_rows)


TRANS_B = (((1,), (1,)), ((), ()))


def _allowed(segq_ref, segk_ref, i, j, tq, tk, causal):
    same = segq_ref[...] == segk_ref[...]
    if not causal:
        return same
    rows = i * tq + lax.broadcasted_iota(jnp.int32, (tq, tk), 0)
    cols = j * tk + lax.broadcasted_iota(jnp.int32, (tq, tk), 1)
    return same & (cols <= rows)


def _fwd_kernel(qi_ref, kj_ref, q_ref, k_ref, v_ref, segq_ref, segk_ref, o_ref, lse_ref, m_sc, acc_sc, *, tq, tk, scale):
    t = pl.program_id(1)
    i = qi_ref[t]
    j = kj_ref[t]
    dim = o_ref.shape[2]

    @pl.when(j == 0)
    def _():
        m_sc[...] = jnp.full_like(m_sc, NEGATIVE)
        acc_sc[...] = jnp.zeros_like(acc_sc)

    def absorb(causal):
        q = q_ref[0]
        k = k_ref[0]
        s = lax.dot_general(q, k, TRANS_B, preferred_element_type=jnp.float32) * scale
        s = jnp.where(_allowed(segq_ref, segk_ref, i, j, tq, tk, causal), s, -jnp.inf)
        m_prev = m_sc[...]
        lanes = s.shape[1]
        folded = s[:, :128]
        for start in range(128, lanes, 128):
            folded = jnp.maximum(folded, s[:, start : start + 128])
        m_new = jnp.maximum(m_prev, jnp.max(folded, axis=1, keepdims=True))
        factor = jnp.exp(m_prev - m_new)
        p = jnp.exp(s - m_new)
        acc_sc[...] = acc_sc[...] * factor + jnp.dot(
            p.astype(jnp.bfloat16), v_ref[0], preferred_element_type=jnp.float32
        )
        m_sc[...] = m_new

    @pl.when(j < i)
    def _():
        absorb(False)

    @pl.when(j == i)
    def _():
        absorb(True)
        acc = acc_sc[...]
        total = acc[:, dim : dim + 1]
        o_ref[0] = acc[:, :dim] / total
        lse_ref[0] = m_sc[...] + jnp.log(total)


def _schedule(count, queries_outer):
    if queries_outer:
        pairs = [(i, j) for i in range(count) for j in range(i + 1)]
    else:
        pairs = [(i, j) for j in range(count) for i in range(j, count)]
    return (
        jnp.asarray([p[0] for p in pairs], jnp.int32),
        jnp.asarray([p[1] for p in pairs], jnp.int32),
    )


def attention_forward(q, k, v, seg, block=2048):
    heads, total, dim = q.shape
    count = total // block
    scale = 1.0 / math.sqrt(dim)
    segq = seg.reshape(total, 1)
    segk = seg.reshape(1, total)
    qi, kj = _schedule(count, True)
    steps = qi.shape[0]
    lanes = 2 * dim
    v_ext = jnp.concatenate(
        [v, jnp.ones((heads, total, 1), v.dtype), jnp.zeros((heads, total, lanes - dim - 1), v.dtype)],
        axis=2,
    )

    return pl.pallas_call(
        functools.partial(_fwd_kernel, tq=block, tk=block, scale=scale),
        out_shape=(
            jax.ShapeDtypeStruct((heads, total, dim), jnp.float32),
            jax.ShapeDtypeStruct((heads, total, 1), jnp.float32),
        ),
        grid_spec=pltpu.PrefetchScalarGridSpec(
            num_scalar_prefetch=2,
            grid=(heads, steps),
            in_specs=[
                pl.BlockSpec((1, block, dim), lambda h, t, qi, kj: (h, qi[t], 0)),
                pl.BlockSpec((1, block, dim), lambda h, t, qi, kj: (h, kj[t], 0)),
                pl.BlockSpec((1, block, lanes), lambda h, t, qi, kj: (h, kj[t], 0)),
                pl.BlockSpec((block, 1), lambda h, t, qi, kj: (qi[t], 0)),
                pl.BlockSpec((1, block), lambda h, t, qi, kj: (0, kj[t])),
            ],
            out_specs=[
                pl.BlockSpec((1, block, dim), lambda h, t, qi, kj: (h, qi[t], 0)),
                pl.BlockSpec((1, block, 1), lambda h, t, qi, kj: (h, qi[t], 0)),
            ],
            scratch_shapes=[
                pltpu.VMEM((block, 1), jnp.float32),
                pltpu.VMEM((block, lanes), jnp.float32),
            ],
        ),
        cost_estimate=pl.CostEstimate(
            flops=2 * heads * total * total * dim,
            transcendentals=heads * total * total // 2,
            bytes_accessed=heads * total * dim * 10,
        ),
    )(qi, kj, q, k, v_ext, segq, segk)


def _bwd_kernel(qi_ref, kj_ref, q_ref, k_ref, v_ref, do_ref, lse_ref, delta_ref, segq_ref, segk_ref, dq_ref, dk_ref, dv_ref, dk_sc, dv_sc, *, tq, tk, scale, count):
    t = pl.program_id(1)
    i = qi_ref[t]
    j = kj_ref[t]

    @pl.when(t == 0)
    def _():
        dq_ref[...] = jnp.zeros_like(dq_ref)

    @pl.when(i == j)
    def _():
        dk_sc[...] = jnp.zeros_like(dk_sc)
        dv_sc[...] = jnp.zeros_like(dv_sc)

    def absorb(causal):
        q = q_ref[0]
        k = k_ref[0]
        do = do_ref[0]
        s = lax.dot_general(q, k, TRANS_B, preferred_element_type=jnp.float32) * scale
        s = jnp.where(_allowed(segq_ref, segk_ref, i, j, tq, tk, causal), s, -jnp.inf)
        p = jnp.exp(s - lse_ref[0])
        dp = lax.dot_general(do, v_ref[0], TRANS_B, preferred_element_type=jnp.float32)
        ds = (p * (dp - delta_ref[0])).astype(jnp.bfloat16)
        dv_sc[...] += jnp.dot(do.T, p.astype(jnp.bfloat16), preferred_element_type=jnp.float32)
        dk_sc[...] += jnp.dot(q.T, ds, preferred_element_type=jnp.float32)
        rows = pl.ds(pl.multiple_of(i * tq, tq), tq)
        dq_ref[0, rows, :] += lax.dot(ds, k, preferred_element_type=jnp.float32) * scale

    @pl.when(j < i)
    def _():
        absorb(False)

    @pl.when(j == i)
    def _():
        absorb(True)

    @pl.when(i == count - 1)
    def _():
        dk_ref[0] = dk_sc[...].T * scale
        dv_ref[0] = dv_sc[...].T


def attention_backward(q, k, v, do, lse, delta, seg, block=2048):
    heads, total, dim = q.shape
    count = total // block
    scale = 1.0 / math.sqrt(dim)
    segq = seg.reshape(total, 1)
    segk = seg.reshape(1, total)
    qi, kj = _schedule(count, False)
    steps = qi.shape[0]

    def q_map(h, t, qi, kj):
        return (h, qi[t], 0)

    def k_map(h, t, qi, kj):
        return (h, kj[t], 0)

    return pl.pallas_call(
        functools.partial(_bwd_kernel, tq=block, tk=block, scale=scale, count=count),
        out_shape=(
            jax.ShapeDtypeStruct((heads, total, dim), jnp.float32),
            jax.ShapeDtypeStruct((heads, total, dim), jnp.float32),
            jax.ShapeDtypeStruct((heads, total, dim), jnp.float32),
        ),
        grid_spec=pltpu.PrefetchScalarGridSpec(
            num_scalar_prefetch=2,
            grid=(heads, steps),
            in_specs=[
                pl.BlockSpec((1, block, dim), q_map),
                pl.BlockSpec((1, block, dim), k_map),
                pl.BlockSpec((1, block, dim), k_map),
                pl.BlockSpec((1, block, dim), q_map),
                pl.BlockSpec((1, block, 1), q_map),
                pl.BlockSpec((1, block, 1), q_map),
                pl.BlockSpec((block, 1), lambda h, t, qi, kj: (qi[t], 0)),
                pl.BlockSpec((1, block), lambda h, t, qi, kj: (0, kj[t])),
            ],
            out_specs=[
                pl.BlockSpec((1, total, dim), lambda h, t, qi, kj: (h, 0, 0)),
                pl.BlockSpec((1, block, dim), k_map),
                pl.BlockSpec((1, block, dim), k_map),
            ],
            scratch_shapes=[
                pltpu.VMEM((dim, block), jnp.float32),
                pltpu.VMEM((dim, block), jnp.float32),
            ],
        ),
        cost_estimate=pl.CostEstimate(
            flops=5 * heads * total * total * dim,
            transcendentals=heads * total * total // 2,
            bytes_accessed=heads * total * dim * 24,
        ),
    )(qi, kj, q, k, v, do, lse, delta, segq, segk)


MESH_ID = pl.DeviceIdType.MESH


class Ring:
    def __init__(self, size, a_stride, b_stride):
        self.size = size
        self.half = size // 2
        self.a_stride = a_stride
        self.b_stride = b_stride

    def position(self, c):
        a = (c // self.a_stride) % self.half
        b = (c // self.b_stride) % 2
        return a + b * (2 * self.half - 1 - 2 * a)

    def device(self, pos):
        pos = pos % self.size
        b = pos // self.half
        a = pos + b * (2 * self.half - 1 - 2 * pos)
        return a * self.a_stride + b * self.b_stride


def ring_of(mesh):
    size = mesh.shape["ctx"]
    devices = list(mesh.devices.reshape(-1, size)[0])
    try:
        coords = [tuple(d.coords) for d in devices]
    except AttributeError:
        coords = None
    if coords and size % 2 == 0 and size >= 4:
        for b_stride in range(1, size):
            for a_stride in range(1, size):
                ring = Ring(size, a_stride, b_stride)
                order = [ring.device(p) for p in range(size)]
                if sorted(order) != list(range(size)):
                    continue
                hops = [
                    sum(abs(x - y) for x, y in zip(coords[order[p]], coords[order[(p + 1) % size]]))
                    for p in range(size)
                ]
                if max(hops) == 1:
                    return ring
    return Ring(size, 2, 1) if size % 2 == 0 and size >= 4 else None


def _barrier(g, left, right):
    barrier = pltpu.get_barrier_semaphore()
    for other in (left, right):
        pl.semaphore_signal(barrier, 1, device_id=(g, other), device_id_type=MESH_ID)
    pl.semaphore_wait(barrier, 2)


def _gather_kernel(x_ref, y_ref, own_sem, send_sem, recv_sem, *, ring, rows):
    n = ring.size
    half = rows // 2
    g = lax.axis_index("dp")
    c = lax.axis_index("ctx")
    pos = ring.position(c)
    right = ring.device(pos + 1)
    left = ring.device(pos + n - 1)
    own = pltpu.make_async_copy(x_ref, y_ref.at[pl.ds(c * rows, rows)], own_sem)
    own.start()
    _barrier(g, left, right)

    def link(direction, step, origin, source):
        offset = origin * rows + direction * half
        return pltpu.make_async_remote_copy(
            src_ref=source,
            dst_ref=y_ref.at[pl.ds(offset, half)],
            send_sem=send_sem.at[direction, step],
            recv_sem=recv_sem.at[direction, step],
            device_id=(g, right if direction == 0 else left),
            device_id_type=MESH_ID,
        )

    sent = []
    for step in range(n - 1):
        origins = (ring.device(pos - step + n), ring.device(pos + step))
        for direction in (0, 1):
            origin = origins[direction]
            if step == 0:
                source = x_ref.at[pl.ds(direction * half, half)]
            else:
                link(direction, step - 1, origin, None if False else y_ref.at[pl.ds(origin * rows + direction * half, half)]).wait_recv()
                source = y_ref.at[pl.ds(origin * rows + direction * half, half)]
            copy = link(direction, step, origin, source)
            copy.start()
            sent.append(copy)
    last = n - 2
    for direction, origin in ((0, ring.device(pos - last - 1 + n)), (1, ring.device(pos + last + 1))):
        link(direction, last, origin, y_ref.at[pl.ds(origin * rows + direction * half, half)]).wait_recv()
    for copy in sent:
        copy.wait_send()
    own.wait()


def ring_all_gather(x, ring, collective_id):
    rows, cols = x.shape
    n = ring.size
    return pl.pallas_call(
        functools.partial(_gather_kernel, ring=ring, rows=rows),
        out_shape=jax.ShapeDtypeStruct((n * rows, cols), x.dtype),
        in_specs=[pl.BlockSpec(memory_space=pl.ANY)],
        out_specs=pl.BlockSpec(memory_space=pl.ANY),
        scratch_shapes=[
            pltpu.SemaphoreType.DMA(()),
            pltpu.SemaphoreType.DMA((2, n - 1)),
            pltpu.SemaphoreType.DMA((2, n - 1)),
        ],
        compiler_params=pltpu.CompilerParams(collective_id=collective_id, has_side_effects=True),
    )(x)


def _scatter_kernel(p_ref, out_ref, recv_buf, send_buf, send_sem, recv_sem, *, ring, rows, parts):
    n = ring.size
    half = rows // 2
    piece = half // parts
    g = lax.axis_index("dp")
    c = lax.axis_index("ctx")
    pos = ring.position(c)
    right = ring.device(pos + 1)
    left = ring.device(pos + n - 1)
    _barrier(g, left, right)

    def link(direction, step, part):
        window = pl.ds(part * piece, piece)
        return pltpu.make_async_remote_copy(
            src_ref=send_buf.at[direction, step, window],
            dst_ref=recv_buf.at[direction, step, window],
            send_sem=send_sem.at[direction, step, part],
            recv_sem=recv_sem.at[direction, step, part],
            device_id=(g, right if direction == 0 else left),
            device_id_type=MESH_ID,
        )

    sent = []
    for step in range(n - 1):
        targets = (ring.device(pos - 1 - step + 2 * n), ring.device(pos + 1 + step))
        for part in range(parts):
            for direction in (0, 1):
                start = pl.multiple_of(
                    targets[direction] * rows + direction * half + part * piece, piece
                )
                window = pl.ds(part * piece, piece)
                total = p_ref[pl.ds(start, piece), :].astype(jnp.float32)
                if step > 0:
                    link(direction, step - 1, part).wait_recv()
                    total = total + recv_buf[direction, step - 1, window].astype(jnp.float32)
                send_buf[direction, step, window] = total.astype(send_buf.dtype)
                copy = link(direction, step, part)
                copy.start()
                sent.append(copy)
    for part in range(parts):
        for direction in (0, 1):
            link(direction, n - 2, part).wait_recv()
            start = pl.multiple_of(c * rows + direction * half + part * piece, piece)
            window = pl.ds(part * piece, piece)
            out_ref[pl.ds(direction * half + part * piece, piece), :] = (
                p_ref[pl.ds(start, piece), :].astype(jnp.float32)
                + recv_buf[direction, n - 2, window].astype(jnp.float32)
            ).astype(out_ref.dtype)
    for copy in sent:
        copy.wait_send()


def ring_reduce_scatter(p, ring, collective_id, out_dtype=jnp.float32, wire=jnp.bfloat16, parts=2):
    total_rows, cols = p.shape
    n = ring.size
    rows = total_rows // n
    half = rows // 2
    return pl.pallas_call(
        functools.partial(_scatter_kernel, ring=ring, rows=rows, parts=parts),
        out_shape=jax.ShapeDtypeStruct((rows, cols), out_dtype),
        in_specs=[pl.BlockSpec(memory_space=pltpu.VMEM)],
        out_specs=pl.BlockSpec(memory_space=pltpu.VMEM),
        scratch_shapes=[
            pltpu.VMEM((2, n - 1, half, cols), wire),
            pltpu.VMEM((2, n - 1, half, cols), wire),
            pltpu.SemaphoreType.DMA((2, n - 1, parts)),
            pltpu.SemaphoreType.DMA((2, n - 1, parts)),
        ],
        compiler_params=pltpu.CompilerParams(
            collective_id=collective_id, has_side_effects=True, vmem_limit_bytes=60 * 1024 * 1024
        ),
    )(p)


def _exchange_kernel(x_ref, out_ref, own_sem, send_sem, recv_sem, *, group):
    n = x_ref.shape[0]
    g = lax.axis_index("dp")
    c = lax.axis_index("ctx")
    n_ctx = lax.axis_size("ctx")
    me = {"all": g * n_ctx + c, "ctx": c, "dp": g}[group]

    def address(member):
        if group == "all":
            return (member // n_ctx, member % n_ctx)
        if group == "ctx":
            return (g, member)
        return (member, c)

    own = pltpu.make_async_copy(x_ref.at[me], out_ref.at[me], own_sem)
    own.start()
    barrier = pltpu.get_barrier_semaphore()
    for offset in range(1, n):
        pl.semaphore_signal(
            barrier, 1, device_id=address((me + offset) % n), device_id_type=MESH_ID
        )
    pl.semaphore_wait(barrier, n - 1)

    def link(offset, source, target):
        return pltpu.make_async_remote_copy(
            src_ref=x_ref.at[target],
            dst_ref=out_ref.at[source],
            send_sem=send_sem.at[offset],
            recv_sem=recv_sem.at[offset],
            device_id=address(target),
            device_id_type=MESH_ID,
        )

    sent = []
    for offset in range(1, n):
        copy = link(offset, me, (me + offset) % n)
        copy.start()
        sent.append(copy)
    for offset in range(1, n):
        link(offset, (me + n - offset) % n, me).wait_recv()
    for copy in sent:
        copy.wait_send()
    own.wait()


def exchange(x, group, collective_id):
    n = x.shape[0]
    space = pltpu.VMEM
    return pl.pallas_call(
        functools.partial(_exchange_kernel, group=group),
        out_shape=jax.ShapeDtypeStruct(x.shape, x.dtype),
        in_specs=[pl.BlockSpec(memory_space=space)],
        out_specs=pl.BlockSpec(memory_space=space),
        scratch_shapes=[
            pltpu.SemaphoreType.DMA(()),
            pltpu.SemaphoreType.DMA((n,)),
            pltpu.SemaphoreType.DMA((n,)),
        ],
        compiler_params=pltpu.CompilerParams(collective_id=collective_id, has_side_effects=True),
    )(x)


def block_moves(n_dp, n_ctx):
    count = n_dp * n_ctx
    return [(f, (f % n_dp) * n_ctx + f // n_dp) for f in range(count)]


def fetch_out_rows(w_out):
    n_dp = lax.axis_size("dp")
    n_ctx = lax.axis_size("ctx")
    moved = lax.ppermute(w_out.astype(jnp.bfloat16), ("dp", "ctx"), perm=block_moves(n_dp, n_ctx))
    return lax.all_gather(moved, "dp", axis=0, tiled=True)


def return_out_rows(grad_out_rows):
    n_dp = lax.axis_size("dp")
    n_ctx = lax.axis_size("ctx")
    part = lax.psum_scatter(grad_out_rows, "dp", scatter_dimension=0, tiled=True)
    back = [(b, a) for a, b in block_moves(n_dp, n_ctx)]
    return lax.ppermute(part, ("dp", "ctx"), perm=back)


def pack_rows(vector, lanes):
    size = vector.shape[0]
    total = -(-size // (16 * lanes)) * 16 * lanes
    return jnp.pad(vector, (0, total - size)).reshape(-1, lanes)


def fetch_small(b_qkv, b_out, b_fc2, ln_gain, ln_shift, b_fc1):
    pieces = (b_qkv, b_out, b_fc2, ln_gain, ln_shift, b_fc1)
    n_dp = lax.axis_size("dp")
    n_ctx = lax.axis_size("ctx")
    packed = pack_rows(jnp.concatenate([p.astype(jnp.bfloat16) for p in pieces]), 128)
    over_dp = exchange(jnp.broadcast_to(packed[None], (n_dp,) + packed.shape), "dp", 4)
    over_all = exchange(jnp.broadcast_to(over_dp[None], (n_ctx,) + over_dp.shape), "ctx", 8)
    table = over_all.transpose(1, 0, 2, 3).reshape(n_dp * n_ctx, -1)
    result = []
    offset = 0
    for p in pieces:
        result.append(table[:, offset : offset + p.shape[0]])
        offset += p.shape[0]
    return result


def reduce_small(small):
    n_dp = lax.axis_size("dp")
    n_ctx = lax.axis_size("ctx")
    count, width = small.shape
    packed = jax.vmap(lambda row: pack_rows(row, 128))(small)
    packed = packed.reshape((n_dp, n_ctx) + packed.shape[1:]).transpose(1, 0, 2, 3)
    over_ctx = jnp.sum(exchange(packed, "ctx", 7), axis=0)
    over_dp = jnp.sum(exchange(over_ctx, "dp", 9), axis=0)
    return over_dp.reshape(-1)[:width]


def fetch_heads(w_qkv, w_fc1, w_fc2, tokens):
    dp_count = lax.axis_size("dp")
    ctx_count = lax.axis_size("ctx")
    rows_piece = w_qkv.shape[0]
    head_width = D // ctx_count
    unit = FF // (dp_count * ctx_count)
    qkv_piece = w_qkv.astype(jnp.bfloat16).reshape(rows_piece, 3, ctx_count, head_width)
    fc1_piece = w_fc1.astype(jnp.bfloat16).reshape(rows_piece, dp_count, ctx_count, unit)
    pieces = jnp.concatenate(
        [
            qkv_piece.transpose(2, 0, 1, 3).reshape(ctx_count, rows_piece, 3 * head_width),
            fc1_piece.transpose(2, 0, 1, 3).reshape(ctx_count, rows_piece, dp_count * unit),
        ],
        axis=2,
    )
    sent = exchange(pieces, "ctx", 5).reshape(ctx_count * rows_piece, -1)
    sent, tokens = lax.optimization_barrier((sent, tokens))
    cols, fc2_rows = (
        lax.all_gather(sent, "dp", axis=0, tiled=True),
        lax.all_gather(w_fc2.astype(jnp.bfloat16), "dp", axis=0, tiled=True),
    )
    return (cols, fc2_rows, tokens)


def return_heads(owned_parts):
    dp_count = lax.axis_size("dp")
    ctx_count = lax.axis_size("ctx")
    head_width = D // ctx_count
    unit = FF // (dp_count * ctx_count)
    rows_piece = owned_parts.shape[0] // ctx_count
    got = exchange(owned_parts.reshape(ctx_count, rows_piece, -1), "ctx", 6)
    qkv = got[:, :, : 3 * head_width].reshape(ctx_count, rows_piece, 3, head_width)
    fc1 = got[:, :, 3 * head_width :].reshape(ctx_count, rows_piece, dp_count, unit)
    return (
        qkv.transpose(1, 2, 0, 3).reshape(rows_piece, 3 * D).astype(jnp.float32),
        fc1.transpose(1, 2, 0, 3).reshape(rows_piece, FF).astype(jnp.float32),
    )


def head_plan(
    ring,
    tokens,
    lengths,
    w_qkv,
    b_qkv,
    w_out,
    b_out,
    w_fc1,
    b_fc1,
    w_fc2,
    b_fc2,
    ln_gain,
    ln_shift,
    cotangent,
):
    rows_here = tokens.shape[0]
    rows_piece = w_qkv.shape[0]
    dp_count = lax.axis_size("dp")
    ctx_count = lax.axis_size("ctx")
    count = dp_count * ctx_count
    group = rows_here * ctx_count
    head_width = D // ctx_count
    local_heads = HEADS // ctx_count
    unit = FF // (dp_count * ctx_count)
    here = lax.axis_index("ctx")
    group_rows = jnp.arange(group, dtype=jnp.int32)
    seg, positions = segment_info(lengths[0], group_rows)
    cosine, sine = rotary_tables(positions)
    qkv_bias, out_bias, fc2_bias, gain_low, shift_low, fc1_table = fetch_small(
        b_qkv, b_out, b_fc2, ln_gain, ln_shift, b_fc1
    )
    qkv_bias = qkv_bias.reshape(3 * D)
    out_bias = out_bias.reshape(D)
    fc2_bias = fc2_bias.reshape(D)
    gain_low = gain_low.reshape(D)
    shift_low = shift_low.reshape(D)
    fc1_bias = lax.dynamic_index_in_dim(
        fc1_table.reshape(dp_count, ctx_count, unit), here, 1, keepdims=False
    ).reshape(dp_count * unit)
    out_rows = fetch_out_rows(w_out)
    cols, fc2_rows, tokens = fetch_heads(w_qkv, w_fc1, w_fc2, tokens)
    gain32 = gain_low.astype(jnp.float32)
    shift32 = shift_low.astype(jnp.float32)
    inputs = tokens.astype(jnp.float32)
    normed, scaled, _ = norm_parts(inputs, gain32, shift32)
    tokens_group = ring_all_gather(tokens, ring, 0)
    late_dy, tokens_group = lax.optimization_barrier((cotangent, tokens_group))
    dy_group = lax.all_gather(late_dy, "ctx", axis=0, tiled=True)
    hidden_group = norm_parts(tokens_group.astype(jnp.float32), gain32, shift32)[2].astype(
        jnp.bfloat16
    )
    bias_cols = lax.dynamic_slice_in_dim(
        qkv_bias.reshape(3, D), here * head_width, head_width, 1
    ).reshape(3 * head_width)
    both = jnp.dot(hidden_group, cols, preferred_element_type=jnp.float32) + jnp.concatenate(
        [bias_cols, fc1_bias]
    ).astype(jnp.float32)
    qkv = both[:, : 3 * head_width]
    pre = both[:, 3 * head_width :]
    shape = (group, local_heads, HEAD_DIM)
    query = rotate(qkv[:, :head_width].reshape(shape), cosine, sine).astype(jnp.bfloat16)
    keys = rotate(qkv[:, head_width : 2 * head_width].reshape(shape), cosine, sine).astype(
        jnp.bfloat16
    )
    values = qkv[:, 2 * head_width :].reshape(shape).astype(jnp.bfloat16)
    q_heads = query.transpose(1, 0, 2)
    k_heads = keys.transpose(1, 0, 2)
    v_heads = values.transpose(1, 0, 2)
    attended_heads, log_total = attention_forward(q_heads, k_heads, v_heads, seg)
    attended = attended_heads.transpose(1, 0, 2).reshape(group, head_width).astype(jnp.bfloat16)
    act = gelu_tanh(pre).astype(jnp.bfloat16)
    branches = ring_reduce_scatter(
        jnp.dot(attended, out_rows, preferred_element_type=jnp.float32)
        + jnp.dot(act, fc2_rows, preferred_element_type=jnp.float32),
        ring,
        2,
    )
    block_out = (
        inputs + branches + out_bias.astype(jnp.float32) + fc2_bias.astype(jnp.float32)
    ).astype(jnp.bfloat16)
    grad_out32 = cotangent.astype(jnp.float32)
    grad_b_fc2 = jnp.sum(grad_out32, axis=0)
    grad_fc2_part = jnp.einsum("tf,td->fd", act, dy_group, preferred_element_type=jnp.float32)
    d_act = jnp.einsum("td,fd->tf", dy_group, fc2_rows, preferred_element_type=jnp.float32)
    d_pre = (d_act * gelu_slope(pre)).astype(jnp.bfloat16)
    grad_bfc1_part = jnp.sum(d_pre.astype(jnp.float32), axis=0)
    grad_out_rows = jnp.einsum("tc,td->cd", attended, dy_group, preferred_element_type=jnp.float32)
    owned_w_out = return_out_rows(grad_out_rows)
    d_attended = (
        jnp.einsum("td,cd->tc", dy_group, out_rows, preferred_element_type=jnp.float32)
        .astype(jnp.bfloat16)
        .reshape(shape)
    )
    d_heads = d_attended.transpose(1, 0, 2)
    delta = jnp.sum(d_heads.astype(jnp.float32) * attended_heads, axis=2, keepdims=True)
    dq_heads, dk_heads, dv_heads = attention_backward(
        q_heads, k_heads, v_heads, d_heads, log_total, delta, seg
    )
    d_query = dq_heads.transpose(1, 0, 2)
    d_keys = dk_heads.transpose(1, 0, 2)
    d_values = dv_heads.transpose(1, 0, 2)
    d_query = rotate_back(d_query, cosine, sine).reshape(group, head_width)
    d_keys = rotate_back(d_keys, cosine, sine).reshape(group, head_width)
    d_qkv = jnp.concatenate([d_query, d_keys, d_values.reshape(group, head_width)], axis=1).astype(
        jnp.bfloat16
    )
    d_both = jnp.concatenate([d_qkv, d_pre], axis=1)
    bias_part = jnp.sum(d_qkv.astype(jnp.float32), axis=0).reshape(3, head_width)
    d_hidden = ring_reduce_scatter(
        jnp.einsum("tc,dc->td", d_both, cols, preferred_element_type=jnp.float32), ring, 3
    )
    weight_parts = jnp.einsum(
        "td,tc->dc", hidden_group, d_both, preferred_element_type=jnp.float32
    ).astype(jnp.bfloat16)
    owned_parts = lax.psum_scatter(weight_parts, "dp", scatter_dimension=0, tiled=True)
    split_qkv, split_fc1 = return_heads(owned_parts)
    d_hidden, split_qkv, split_fc1 = lax.optimization_barrier((d_hidden, split_qkv, split_fc1))
    grad_gain, grad_shift, d_inputs = norm_back(d_hidden, normed, scaled, gain32)
    grad_tokens = (grad_out32 + d_inputs).astype(jnp.bfloat16)
    owned_fc2 = lax.psum_scatter(
        grad_fc2_part.astype(jnp.bfloat16), "dp", scatter_dimension=0, tiled=True
    ).astype(jnp.float32)
    full_bqkv = lax.dynamic_update_slice_in_dim(
        jnp.zeros((3, D), jnp.float32), bias_part, here * head_width, 1
    )
    full_bfc1 = lax.dynamic_update_slice_in_dim(
        jnp.zeros((dp_count, ctx_count, unit), jnp.float32),
        grad_bfc1_part.reshape(dp_count, 1, unit),
        here,
        1,
    )
    small = jnp.concatenate(
        [
            full_bqkv.reshape(count, -1),
            grad_b_fc2.reshape(count, -1),
            grad_gain.reshape(count, -1),
            grad_shift.reshape(count, -1),
            full_bfc1.reshape(count, -1),
        ],
        axis=1,
    )
    owned_small = reduce_small(small)
    cuts = [0, 3 * D // count, D // count, D // count, D // count, FF // count]
    bounds = [sum(cuts[: i + 1]) for i in range(len(cuts))]
    owned_bqkv, owned_bout, owned_gain, owned_shift, owned_bfc1 = [
        owned_small[bounds[i] : bounds[i + 1]] for i in range(5)
    ]
    return (
        block_out,
        grad_tokens,
        split_qkv.reshape(rows_piece, 3 * D),
        owned_bqkv,
        owned_w_out,
        owned_bout,
        split_fc1.reshape(rows_piece, FF),
        owned_bfc1,
        owned_fc2,
        owned_bout,
        owned_gain,
        owned_shift,
    )


def body(
    ring,
    tokens,
    lengths,
    w_qkv,
    b_qkv,
    w_out,
    b_out,
    w_fc1,
    b_fc1,
    w_fc2,
    b_fc2,
    ln_gain,
    ln_shift,
    cotangent,
):
    return head_plan(
        ring,
        tokens,
        lengths,
        w_qkv,
        b_qkv,
        w_out,
        b_out,
        w_fc1,
        b_fc1,
        w_fc2,
        b_fc2,
        ln_gain,
        ln_shift,
        cotangent,
    )


def solution(mesh):
    in_specs = (
        P(("dp", "ctx"), None),
        P("dp", None),
        P(("dp", "ctx"), None),
        P(("dp", "ctx")),
        P(("dp", "ctx"), None),
        P(("dp", "ctx")),
        P(("dp", "ctx"), None),
        P(("dp", "ctx")),
        P(("dp", "ctx"), None),
        P(("dp", "ctx")),
        P(("dp", "ctx")),
        P(("dp", "ctx")),
        P(("dp", "ctx"), None),
    )
    out_specs = (
        P(("dp", "ctx"), None),
        P(("dp", "ctx"), None),
        P(("dp", "ctx"), None),
        P(("dp", "ctx")),
        P(("dp", "ctx"), None),
        P(("dp", "ctx")),
        P(("dp", "ctx"), None),
        P(("dp", "ctx")),
        P(("dp", "ctx"), None),
        P(("dp", "ctx")),
        P(("dp", "ctx")),
        P(("dp", "ctx")),
    )
    ring = ring_of(mesh)
    return jax.shard_map(functools.partial(body, ring), mesh=mesh, in_specs=in_specs, out_specs=out_specs, check_vma=False)
```

```python
import functools
import math

import jax
import jax.numpy as jnp
from jax import lax
from jax.experimental import pallas as pl
from jax.experimental.pallas import tpu as pltpu
from jax.sharding import PartitionSpec as P

D = 2048
HEADS = 32
HEAD_DIM = 64
ROT = 32
FF = 8192


EPS = 1e-05
GELU_COEF = math.sqrt(2.0 / math.pi)
NEGATIVE = -1e30


def norm_parts(inputs, gain, shift):
    mean = jnp.mean(inputs, axis=-1, keepdims=True)
    centred = inputs - mean
    var = jnp.mean(centred * centred, axis=-1, keepdims=True)
    scaled = lax.rsqrt(var + EPS)
    normed = centred * scaled
    return (normed, scaled, normed * gain + shift)


def norm_back(d_hidden, normed, scaled, gain32):
    grad_gain = jnp.sum(d_hidden * normed, axis=0)
    grad_shift = jnp.sum(d_hidden, axis=0)
    d_normed = d_hidden * gain32
    d_inputs = scaled * (
        d_normed
        - jnp.mean(d_normed, axis=-1, keepdims=True)
        - normed * jnp.mean(d_normed * normed, axis=-1, keepdims=True)
    )
    return (grad_gain, grad_shift, d_inputs)


def gelu_tanh(pre):
    return 0.5 * pre * (1.0 + jnp.tanh(GELU_COEF * (pre + 0.044715 * pre * pre * pre)))


def gelu_slope(pre):
    tangent = jnp.tanh(GELU_COEF * (pre + 0.044715 * pre * pre * pre))
    return 0.5 * (1.0 + tangent) + 0.5 * pre * (1.0 - tangent * tangent) * GELU_COEF * (
        1.0 + 3.0 * 0.044715 * pre * pre
    )


def rotary_tables(positions):
    half = ROT // 2
    freq = jnp.exp(jnp.arange(half, dtype=jnp.float32) * (-2.0 * math.log(10000.0) / ROT))
    angle = positions.astype(jnp.float32)[:, None] * freq[None, :]
    return (jnp.cos(angle)[:, None, :], jnp.sin(angle)[:, None, :])


def rotate(heads, cosine, sine):
    half = ROT // 2
    first = heads[..., :half]
    second = heads[..., half:ROT]
    return jnp.concatenate(
        [first * cosine - second * sine, second * cosine + first * sine, heads[..., ROT:]], axis=-1
    )


def rotate_back(grads, cosine, sine):
    half = ROT // 2
    first = grads[..., :half]
    second = grads[..., half:ROT]
    return jnp.concatenate(
        [first * cosine + second * sine, second * cosine - first * sine, grads[..., ROT:]], axis=-1
    )


def segment_info(lengths_row, rows):
    ends = jnp.cumsum(lengths_row)
    starts = ends - lengths_row
    seg = jnp.sum((rows[:, None] >= ends[None, :]).astype(jnp.int32), axis=1)
    onehot = seg[:, None] == jnp.arange(lengths_row.shape[0], dtype=jnp.int32)[None, :]
    first_rows = jnp.sum(jnp.where(onehot, starts[None, :], 0), axis=1)
    return (seg, rows - first_rows)


TRANS_B = (((1,), (1,)), ((), ()))


def _allowed(segq_ref, segk_ref, i, j, tq, tk, causal):
    same = segq_ref[...] == segk_ref[...]
    if not causal:
        return same
    rows = i * tq + lax.broadcasted_iota(jnp.int32, (tq, tk), 0)
    cols = j * tk + lax.broadcasted_iota(jnp.int32, (tq, tk), 1)
    return same & (cols <= rows)


def _fwd_kernel(qi_ref, kj_ref, q_ref, k_ref, v_ref, segq_ref, segk_ref, o_ref, lse_ref, m_sc, acc_sc, *, tq, tk, scale):
    t = pl.program_id(1)
    i = qi_ref[t]
    j = kj_ref[t]
    dim = o_ref.shape[2]

    @pl.when(j == 0)
    def _():
        m_sc[...] = jnp.full_like(m_sc, NEGATIVE)
        acc_sc[...] = jnp.zeros_like(acc_sc)

    def absorb(causal):
        q = q_ref[0]
        k = k_ref[0]
        s = lax.dot_general(q, k, TRANS_B, preferred_element_type=jnp.float32) * scale
        s = jnp.where(_allowed(segq_ref, segk_ref, i, j, tq, tk, causal), s, -jnp.inf)
        m_prev = m_sc[...]
        lanes = s.shape[1]
        folded = s[:, :128]
        for start in range(128, lanes, 128):
            folded = jnp.maximum(folded, s[:, start : start + 128])
        m_new = jnp.maximum(m_prev, jnp.max(folded, axis=1, keepdims=True))
        factor = jnp.exp(m_prev - m_new)
        p = jnp.exp(s - m_new)
        acc_sc[...] = acc_sc[...] * factor + jnp.dot(
            p.astype(jnp.bfloat16), v_ref[0], preferred_element_type=jnp.float32
        )
        m_sc[...] = m_new

    @pl.when(j < i)
    def _():
        absorb(False)

    @pl.when(j == i)
    def _():
        absorb(True)
        acc = acc_sc[...]
        total = acc[:, dim : dim + 1]
        o_ref[0] = acc[:, :dim] / total
        lse_ref[0] = m_sc[...] + jnp.log(total)


def _schedule(count, queries_outer):
    if queries_outer:
        pairs = [(i, j) for i in range(count) for j in range(i + 1)]
    else:
        pairs = [(i, j) for j in range(count) for i in range(j, count)]
    return (
        jnp.asarray([p[0] for p in pairs], jnp.int32),
        jnp.asarray([p[1] for p in pairs], jnp.int32),
    )


def attention_forward(q, k, v, seg, block=1024):
    heads, total, dim = q.shape
    count = total // block
    scale = 1.0 / math.sqrt(dim)
    segq = seg.reshape(total, 1)
    segk = seg.reshape(1, total)
    qi, kj = _schedule(count, True)
    steps = qi.shape[0]
    lanes = 2 * dim
    v_ext = jnp.concatenate(
        [v, jnp.ones((heads, total, 1), v.dtype), jnp.zeros((heads, total, lanes - dim - 1), v.dtype)],
        axis=2,
    )

    return pl.pallas_call(
        functools.partial(_fwd_kernel, tq=block, tk=block, scale=scale),
        out_shape=(
            jax.ShapeDtypeStruct((heads, total, dim), jnp.float32),
            jax.ShapeDtypeStruct((heads, total, 1), jnp.float32),
        ),
        grid_spec=pltpu.PrefetchScalarGridSpec(
            num_scalar_prefetch=2,
            grid=(heads, steps),
            in_specs=[
                pl.BlockSpec((1, block, dim), lambda h, t, qi, kj: (h, qi[t], 0)),
                pl.BlockSpec((1, block, dim), lambda h, t, qi, kj: (h, kj[t], 0)),
                pl.BlockSpec((1, block, lanes), lambda h, t, qi, kj: (h, kj[t], 0)),
                pl.BlockSpec((block, 1), lambda h, t, qi, kj: (qi[t], 0)),
                pl.BlockSpec((1, block), lambda h, t, qi, kj: (0, kj[t])),
            ],
            out_specs=[
                pl.BlockSpec((1, block, dim), lambda h, t, qi, kj: (h, qi[t], 0)),
                pl.BlockSpec((1, block, 1), lambda h, t, qi, kj: (h, qi[t], 0)),
            ],
            scratch_shapes=[
                pltpu.VMEM((block, 1), jnp.float32),
                pltpu.VMEM((block, lanes), jnp.float32),
            ],
        ),
        cost_estimate=pl.CostEstimate(
            flops=2 * heads * total * total * dim,
            transcendentals=heads * total * total // 2,
            bytes_accessed=heads * total * dim * 10,
        ),
    )(qi, kj, q, k, v_ext, segq, segk)


def _bwd_kernel(qi_ref, kj_ref, q_ref, k_ref, v_ref, do_ref, lse_ref, delta_ref, segq_ref, segk_ref, dq_ref, dk_ref, dv_ref, dk_sc, dv_sc, *, tq, tk, scale, count):
    t = pl.program_id(1)
    i = qi_ref[t]
    j = kj_ref[t]

    @pl.when(t == 0)
    def _():
        dq_ref[...] = jnp.zeros_like(dq_ref)

    @pl.when(i == j)
    def _():
        dk_sc[...] = jnp.zeros_like(dk_sc)
        dv_sc[...] = jnp.zeros_like(dv_sc)

    def absorb(causal):
        q = q_ref[0]
        k = k_ref[0]
        do = do_ref[0]
        s = lax.dot_general(q, k, TRANS_B, preferred_element_type=jnp.float32) * scale
        s = jnp.where(_allowed(segq_ref, segk_ref, i, j, tq, tk, causal), s, -jnp.inf)
        p = jnp.exp(s - lse_ref[0])
        dp = lax.dot_general(do, v_ref[0], TRANS_B, preferred_element_type=jnp.float32)
        ds = (p * (dp - delta_ref[0])).astype(jnp.bfloat16)
        dv_sc[...] += jnp.dot(do.T, p.astype(jnp.bfloat16), preferred_element_type=jnp.float32)
        dk_sc[...] += jnp.dot(q.T, ds, preferred_element_type=jnp.float32)
        rows = pl.ds(pl.multiple_of(i * tq, tq), tq)
        dq_ref[0, rows, :] += lax.dot(ds, k, preferred_element_type=jnp.float32) * scale

    @pl.when(j < i)
    def _():
        absorb(False)

    @pl.when(j == i)
    def _():
        absorb(True)

    @pl.when(i == count - 1)
    def _():
        dk_ref[0] = dk_sc[...].T * scale
        dv_ref[0] = dv_sc[...].T


def attention_backward(q, k, v, do, lse, delta, seg, block=1024):
    heads, total, dim = q.shape
    count = total // block
    scale = 1.0 / math.sqrt(dim)
    segq = seg.reshape(total, 1)
    segk = seg.reshape(1, total)
    qi, kj = _schedule(count, False)
    steps = qi.shape[0]

    def q_map(h, t, qi, kj):
        return (h, qi[t], 0)

    def k_map(h, t, qi, kj):
        return (h, kj[t], 0)

    return pl.pallas_call(
        functools.partial(_bwd_kernel, tq=block, tk=block, scale=scale, count=count),
        out_shape=(
            jax.ShapeDtypeStruct((heads, total, dim), jnp.float32),
            jax.ShapeDtypeStruct((heads, total, dim), jnp.float32),
            jax.ShapeDtypeStruct((heads, total, dim), jnp.float32),
        ),
        grid_spec=pltpu.PrefetchScalarGridSpec(
            num_scalar_prefetch=2,
            grid=(heads, steps),
            in_specs=[
                pl.BlockSpec((1, block, dim), q_map),
                pl.BlockSpec((1, block, dim), k_map),
                pl.BlockSpec((1, block, dim), k_map),
                pl.BlockSpec((1, block, dim), q_map),
                pl.BlockSpec((1, block, 1), q_map),
                pl.BlockSpec((1, block, 1), q_map),
                pl.BlockSpec((block, 1), lambda h, t, qi, kj: (qi[t], 0)),
                pl.BlockSpec((1, block), lambda h, t, qi, kj: (0, kj[t])),
            ],
            out_specs=[
                pl.BlockSpec((1, total, dim), lambda h, t, qi, kj: (h, 0, 0)),
                pl.BlockSpec((1, block, dim), k_map),
                pl.BlockSpec((1, block, dim), k_map),
            ],
            scratch_shapes=[
                pltpu.VMEM((dim, block), jnp.float32),
                pltpu.VMEM((dim, block), jnp.float32),
            ],
        ),
        cost_estimate=pl.CostEstimate(
            flops=5 * heads * total * total * dim,
            transcendentals=heads * total * total // 2,
            bytes_accessed=heads * total * dim * 24,
        ),
    )(qi, kj, q, k, v, do, lse, delta, segq, segk)


MESH_ID = pl.DeviceIdType.MESH


class Ring:
    def __init__(self, size, a_stride, b_stride):
        self.size = size
        self.half = size // 2
        self.a_stride = a_stride
        self.b_stride = b_stride

    def position(self, c):
        a = (c // self.a_stride) % self.half
        b = (c // self.b_stride) % 2
        return a + b * (2 * self.half - 1 - 2 * a)

    def device(self, pos):
        pos = pos % self.size
        b = pos // self.half
        a = pos + b * (2 * self.half - 1 - 2 * pos)
        return a * self.a_stride + b * self.b_stride


def ring_of(mesh):
    size = mesh.shape["ctx"]
    devices = list(mesh.devices.reshape(-1, size)[0])
    try:
        coords = [tuple(d.coords) for d in devices]
    except AttributeError:
        coords = None
    if coords and size % 2 == 0 and size >= 4:
        for b_stride in range(1, size):
            for a_stride in range(1, size):
                ring = Ring(size, a_stride, b_stride)
                order = [ring.device(p) for p in range(size)]
                if sorted(order) != list(range(size)):
                    continue
                hops = [
                    sum(abs(x - y) for x, y in zip(coords[order[p]], coords[order[(p + 1) % size]]))
                    for p in range(size)
                ]
                if max(hops) == 1:
                    return ring
    return Ring(size, 2, 1) if size % 2 == 0 and size >= 4 else None


def _barrier(g, left, right):
    barrier = pltpu.get_barrier_semaphore()
    for other in (left, right):
        pl.semaphore_signal(barrier, 1, device_id=(g, other), device_id_type=MESH_ID)
    pl.semaphore_wait(barrier, 2)


def _gather_kernel(x_ref, y_ref, own_sem, send_sem, recv_sem, *, ring, rows):
    n = ring.size
    half = rows // 2
    g = lax.axis_index("dp")
    c = lax.axis_index("ctx")
    pos = ring.position(c)
    right = ring.device(pos + 1)
    left = ring.device(pos + n - 1)
    own = pltpu.make_async_copy(x_ref, y_ref.at[pl.ds(c * rows, rows)], own_sem)
    own.start()
    _barrier(g, left, right)

    def link(direction, step, origin, source):
        offset = origin * rows + direction * half
        return pltpu.make_async_remote_copy(
            src_ref=source,
            dst_ref=y_ref.at[pl.ds(offset, half)],
            send_sem=send_sem.at[direction, step],
            recv_sem=recv_sem.at[direction, step],
            device_id=(g, right if direction == 0 else left),
            device_id_type=MESH_ID,
        )

    sent = []
    for step in range(n - 1):
        origins = (ring.device(pos - step + n), ring.device(pos + step))
        for direction in (0, 1):
            origin = origins[direction]
            if step == 0:
                source = x_ref.at[pl.ds(direction * half, half)]
            else:
                link(direction, step - 1, origin, None if False else y_ref.at[pl.ds(origin * rows + direction * half, half)]).wait_recv()
                source = y_ref.at[pl.ds(origin * rows + direction * half, half)]
            copy = link(direction, step, origin, source)
            copy.start()
            sent.append(copy)
    last = n - 2
    for direction, origin in ((0, ring.device(pos - last - 1 + n)), (1, ring.device(pos + last + 1))):
        link(direction, last, origin, y_ref.at[pl.ds(origin * rows + direction * half, half)]).wait_recv()
    for copy in sent:
        copy.wait_send()
    own.wait()


def ring_all_gather(x, ring, collective_id):
    rows, cols = x.shape
    n = ring.size
    return pl.pallas_call(
        functools.partial(_gather_kernel, ring=ring, rows=rows),
        out_shape=jax.ShapeDtypeStruct((n * rows, cols), x.dtype),
        in_specs=[pl.BlockSpec(memory_space=pl.ANY)],
        out_specs=pl.BlockSpec(memory_space=pl.ANY),
        scratch_shapes=[
            pltpu.SemaphoreType.DMA(()),
            pltpu.SemaphoreType.DMA((2, n - 1)),
            pltpu.SemaphoreType.DMA((2, n - 1)),
        ],
        compiler_params=pltpu.CompilerParams(collective_id=collective_id, has_side_effects=True),
    )(x)


def _scatter_kernel(p_ref, out_ref, recv_buf, send_buf, send_sem, recv_sem, *, ring, rows, parts):
    n = ring.size
    half = rows // 2
    piece = half // parts
    g = lax.axis_index("dp")
    c = lax.axis_index("ctx")
    pos = ring.position(c)
    right = ring.device(pos + 1)
    left = ring.device(pos + n - 1)
    _barrier(g, left, right)

    def link(direction, step, part):
        window = pl.ds(part * piece, piece)
        return pltpu.make_async_remote_copy(
            src_ref=send_buf.at[direction, step, window],
            dst_ref=recv_buf.at[direction, step, window],
            send_sem=send_sem.at[direction, step, part],
            recv_sem=recv_sem.at[direction, step, part],
            device_id=(g, right if direction == 0 else left),
            device_id_type=MESH_ID,
        )

    sent = []
    for step in range(n - 1):
        targets = (ring.device(pos - 1 - step + 2 * n), ring.device(pos + 1 + step))
        for part in range(parts):
            for direction in (0, 1):
                start = pl.multiple_of(
                    targets[direction] * rows + direction * half + part * piece, piece
                )
                window = pl.ds(part * piece, piece)
                total = p_ref[pl.ds(start, piece), :].astype(jnp.float32)
                if step > 0:
                    link(direction, step - 1, part).wait_recv()
                    total = total + recv_buf[direction, step - 1, window].astype(jnp.float32)
                send_buf[direction, step, window] = total.astype(send_buf.dtype)
                copy = link(direction, step, part)
                copy.start()
                sent.append(copy)
    for part in range(parts):
        for direction in (0, 1):
            link(direction, n - 2, part).wait_recv()
            start = pl.multiple_of(c * rows + direction * half + part * piece, piece)
            window = pl.ds(part * piece, piece)
            out_ref[pl.ds(direction * half + part * piece, piece), :] = (
                p_ref[pl.ds(start, piece), :].astype(jnp.float32)
                + recv_buf[direction, n - 2, window].astype(jnp.float32)
            ).astype(out_ref.dtype)
    for copy in sent:
        copy.wait_send()


def ring_reduce_scatter(p, ring, collective_id, out_dtype=jnp.float32, wire=jnp.bfloat16, parts=2):
    total_rows, cols = p.shape
    n = ring.size
    rows = total_rows // n
    half = rows // 2
    return pl.pallas_call(
        functools.partial(_scatter_kernel, ring=ring, rows=rows, parts=parts),
        out_shape=jax.ShapeDtypeStruct((rows, cols), out_dtype),
        in_specs=[pl.BlockSpec(memory_space=pltpu.VMEM)],
        out_specs=pl.BlockSpec(memory_space=pltpu.VMEM),
        scratch_shapes=[
            pltpu.VMEM((2, n - 1, half, cols), wire),
            pltpu.VMEM((2, n - 1, half, cols), wire),
            pltpu.SemaphoreType.DMA((2, n - 1, parts)),
            pltpu.SemaphoreType.DMA((2, n - 1, parts)),
        ],
        compiler_params=pltpu.CompilerParams(
            collective_id=collective_id, has_side_effects=True, vmem_limit_bytes=60 * 1024 * 1024
        ),
    )(p)


def _exchange_kernel(x_ref, out_ref, own_sem, send_sem, recv_sem, *, group):
    n = x_ref.shape[0]
    g = lax.axis_index("dp")
    c = lax.axis_index("ctx")
    n_ctx = lax.axis_size("ctx")
    me = {"all": g * n_ctx + c, "ctx": c, "dp": g}[group]

    def address(member):
        if group == "all":
            return (member // n_ctx, member % n_ctx)
        if group == "ctx":
            return (g, member)
        return (member, c)

    own = pltpu.make_async_copy(x_ref.at[me], out_ref.at[me], own_sem)
    own.start()
    barrier = pltpu.get_barrier_semaphore()
    for offset in range(1, n):
        pl.semaphore_signal(
            barrier, 1, device_id=address((me + offset) % n), device_id_type=MESH_ID
        )
    pl.semaphore_wait(barrier, n - 1)

    def link(offset, source, target):
        return pltpu.make_async_remote_copy(
            src_ref=x_ref.at[target],
            dst_ref=out_ref.at[source],
            send_sem=send_sem.at[offset],
            recv_sem=recv_sem.at[offset],
            device_id=address(target),
            device_id_type=MESH_ID,
        )

    sent = []
    for offset in range(1, n):
        copy = link(offset, me, (me + offset) % n)
        copy.start()
        sent.append(copy)
    for offset in range(1, n):
        link(offset, (me + n - offset) % n, me).wait_recv()
    for copy in sent:
        copy.wait_send()
    own.wait()


def exchange(x, group, collective_id):
    n = x.shape[0]
    space = pltpu.VMEM
    return pl.pallas_call(
        functools.partial(_exchange_kernel, group=group),
        out_shape=jax.ShapeDtypeStruct(x.shape, x.dtype),
        in_specs=[pl.BlockSpec(memory_space=space)],
        out_specs=pl.BlockSpec(memory_space=space),
        scratch_shapes=[
            pltpu.SemaphoreType.DMA(()),
            pltpu.SemaphoreType.DMA((n,)),
            pltpu.SemaphoreType.DMA((n,)),
        ],
        compiler_params=pltpu.CompilerParams(collective_id=collective_id, has_side_effects=True),
    )(x)


def block_moves(n_dp, n_ctx):
    count = n_dp * n_ctx
    return [(f, (f % n_dp) * n_ctx + f // n_dp) for f in range(count)]


def fetch_out_rows(w_out):
    n_dp = lax.axis_size("dp")
    n_ctx = lax.axis_size("ctx")
    moved = lax.ppermute(w_out.astype(jnp.bfloat16), ("dp", "ctx"), perm=block_moves(n_dp, n_ctx))
    return lax.all_gather(moved, "dp", axis=0, tiled=True)


def return_out_rows(grad_out_rows):
    n_dp = lax.axis_size("dp")
    n_ctx = lax.axis_size("ctx")
    part = lax.psum_scatter(grad_out_rows, "dp", scatter_dimension=0, tiled=True)
    back = [(b, a) for a, b in block_moves(n_dp, n_ctx)]
    return lax.ppermute(part, ("dp", "ctx"), perm=back)


def pack_rows(vector, lanes):
    size = vector.shape[0]
    total = -(-size // (16 * lanes)) * 16 * lanes
    return jnp.pad(vector, (0, total - size)).reshape(-1, lanes)


def fetch_small(b_qkv, b_out, b_fc2, ln_gain, ln_shift, b_fc1):
    pieces = (b_qkv, b_out, b_fc2, ln_gain, ln_shift, b_fc1)
    n_dp = lax.axis_size("dp")
    n_ctx = lax.axis_size("ctx")
    packed = pack_rows(jnp.concatenate([p.astype(jnp.bfloat16) for p in pieces]), 128)
    over_dp = exchange(jnp.broadcast_to(packed[None], (n_dp,) + packed.shape), "dp", 4)
    over_all = exchange(jnp.broadcast_to(over_dp[None], (n_ctx,) + over_dp.shape), "ctx", 8)
    table = over_all.transpose(1, 0, 2, 3).reshape(n_dp * n_ctx, -1)
    result = []
    offset = 0
    for p in pieces:
        result.append(table[:, offset : offset + p.shape[0]])
        offset += p.shape[0]
    return result


def reduce_small(small):
    n_dp = lax.axis_size("dp")
    n_ctx = lax.axis_size("ctx")
    count, width = small.shape
    packed = jax.vmap(lambda row: pack_rows(row, 128))(small)
    packed = packed.reshape((n_dp, n_ctx) + packed.shape[1:]).transpose(1, 0, 2, 3)
    over_ctx = jnp.sum(exchange(packed, "ctx", 7), axis=0)
    over_dp = jnp.sum(exchange(over_ctx, "dp", 9), axis=0)
    return over_dp.reshape(-1)[:width]


def fetch_heads(w_qkv, w_fc1, w_fc2, tokens):
    dp_count = lax.axis_size("dp")
    ctx_count = lax.axis_size("ctx")
    rows_piece = w_qkv.shape[0]
    head_width = D // ctx_count
    unit = FF // (dp_count * ctx_count)
    qkv_piece = w_qkv.astype(jnp.bfloat16).reshape(rows_piece, 3, ctx_count, head_width)
    fc1_piece = w_fc1.astype(jnp.bfloat16).reshape(rows_piece, dp_count, ctx_count, unit)
    pieces = jnp.concatenate(
        [
            qkv_piece.transpose(2, 0, 1, 3).reshape(ctx_count, rows_piece, 3 * head_width),
            fc1_piece.transpose(2, 0, 1, 3).reshape(ctx_count, rows_piece, dp_count * unit),
        ],
        axis=2,
    )
    sent = exchange(pieces, "ctx", 5).reshape(ctx_count * rows_piece, -1)
    sent, tokens = lax.optimization_barrier((sent, tokens))
    cols, fc2_rows = (
        lax.all_gather(sent, "dp", axis=0, tiled=True),
        lax.all_gather(w_fc2.astype(jnp.bfloat16), "dp", axis=0, tiled=True),
    )
    return (cols, fc2_rows, tokens)


def return_heads(owned_parts):
    dp_count = lax.axis_size("dp")
    ctx_count = lax.axis_size("ctx")
    head_width = D // ctx_count
    unit = FF // (dp_count * ctx_count)
    rows_piece = owned_parts.shape[0] // ctx_count
    got = exchange(owned_parts.reshape(ctx_count, rows_piece, -1), "ctx", 6)
    qkv = got[:, :, : 3 * head_width].reshape(ctx_count, rows_piece, 3, head_width)
    fc1 = got[:, :, 3 * head_width :].reshape(ctx_count, rows_piece, dp_count, unit)
    return (
        qkv.transpose(1, 2, 0, 3).reshape(rows_piece, 3 * D).astype(jnp.float32),
        fc1.transpose(1, 2, 0, 3).reshape(rows_piece, FF).astype(jnp.float32),
    )


def head_plan(
    ring,
    tokens,
    lengths,
    w_qkv,
    b_qkv,
    w_out,
    b_out,
    w_fc1,
    b_fc1,
    w_fc2,
    b_fc2,
    ln_gain,
    ln_shift,
    cotangent,
):
    rows_here = tokens.shape[0]
    rows_piece = w_qkv.shape[0]
    dp_count = lax.axis_size("dp")
    ctx_count = lax.axis_size("ctx")
    count = dp_count * ctx_count
    group = rows_here * ctx_count
    head_width = D // ctx_count
    local_heads = HEADS // ctx_count
    unit = FF // (dp_count * ctx_count)
    here = lax.axis_index("ctx")
    group_rows = jnp.arange(group, dtype=jnp.int32)
    seg, positions = segment_info(lengths[0], group_rows)
    cosine, sine = rotary_tables(positions)
    qkv_bias, out_bias, fc2_bias, gain_low, shift_low, fc1_table = fetch_small(
        b_qkv, b_out, b_fc2, ln_gain, ln_shift, b_fc1
    )
    qkv_bias = qkv_bias.reshape(3 * D)
    out_bias = out_bias.reshape(D)
    fc2_bias = fc2_bias.reshape(D)
    gain_low = gain_low.reshape(D)
    shift_low = shift_low.reshape(D)
    fc1_bias = lax.dynamic_index_in_dim(
        fc1_table.reshape(dp_count, ctx_count, unit), here, 1, keepdims=False
    ).reshape(dp_count * unit)
    out_rows = fetch_out_rows(w_out)
    cols, fc2_rows, tokens = fetch_heads(w_qkv, w_fc1, w_fc2, tokens)
    gain32 = gain_low.astype(jnp.float32)
    shift32 = shift_low.astype(jnp.float32)
    inputs = tokens.astype(jnp.float32)
    normed, scaled, _ = norm_parts(inputs, gain32, shift32)
    tokens_group = ring_all_gather(tokens, ring, 0)
    late_dy, tokens_group = lax.optimization_barrier((cotangent, tokens_group))
    dy_group = lax.all_gather(late_dy, "ctx", axis=0, tiled=True)
    hidden_group = norm_parts(tokens_group.astype(jnp.float32), gain32, shift32)[2].astype(
        jnp.bfloat16
    )
    bias_cols = lax.dynamic_slice_in_dim(
        qkv_bias.reshape(3, D), here * head_width, head_width, 1
    ).reshape(3 * head_width)
    qkv_width = 3 * head_width
    head_count = 3 * local_heads
    qkv_weights = cols[:, :qkv_width].reshape(D, head_count, HEAD_DIM)
    fc1_weights = cols[:, qkv_width:]
    qkv_heads = jnp.einsum(
        "td,dhe->hte", hidden_group, qkv_weights, preferred_element_type=jnp.float32
    ) + bias_cols.astype(jnp.float32).reshape(head_count, 1, HEAD_DIM)
    pre = jnp.dot(hidden_group, fc1_weights, preferred_element_type=jnp.float32) + fc1_bias.astype(
        jnp.float32
    )
    cos_heads = cosine.reshape(1, group, -1)
    sin_heads = sine.reshape(1, group, -1)
    q_heads = rotate(qkv_heads[:local_heads], cos_heads, sin_heads).astype(jnp.bfloat16)
    k_heads = rotate(qkv_heads[local_heads : 2 * local_heads], cos_heads, sin_heads).astype(
        jnp.bfloat16
    )
    v_heads = qkv_heads[2 * local_heads :].astype(jnp.bfloat16)
    attended_heads, log_total = attention_forward(q_heads, k_heads, v_heads, seg)
    attended_low = attended_heads.astype(jnp.bfloat16)
    out_heads = out_rows.reshape(local_heads, HEAD_DIM, D)
    act = gelu_tanh(pre).astype(jnp.bfloat16)
    branches = ring_reduce_scatter(
        jnp.einsum("hte,hed->td", attended_low, out_heads, preferred_element_type=jnp.float32)
        + jnp.dot(act, fc2_rows, preferred_element_type=jnp.float32),
        ring,
        2,
    )
    block_out = (
        inputs + branches + out_bias.astype(jnp.float32) + fc2_bias.astype(jnp.float32)
    ).astype(jnp.bfloat16)
    grad_out32 = cotangent.astype(jnp.float32)
    grad_b_fc2 = jnp.sum(grad_out32, axis=0)
    grad_fc2_part = jnp.einsum("tf,td->fd", act, dy_group, preferred_element_type=jnp.float32)
    d_act = jnp.einsum("td,fd->tf", dy_group, fc2_rows, preferred_element_type=jnp.float32)
    d_pre = (d_act * gelu_slope(pre)).astype(jnp.bfloat16)
    grad_bfc1_part = jnp.sum(d_pre.astype(jnp.float32), axis=0)
    grad_out_rows = jnp.einsum(
        "hte,td->hed", attended_low, dy_group, preferred_element_type=jnp.float32
    ).reshape(head_width, D)
    owned_w_out = return_out_rows(grad_out_rows)
    d_heads = jnp.einsum(
        "td,hed->hte", dy_group, out_heads, preferred_element_type=jnp.float32
    ).astype(jnp.bfloat16)
    delta = jnp.sum(d_heads.astype(jnp.float32) * attended_heads, axis=2, keepdims=True)
    dq_heads, dk_heads, dv_heads = attention_backward(
        q_heads, k_heads, v_heads, d_heads, log_total, delta, seg
    )
    shape = (group, local_heads, HEAD_DIM)
    d_query = rotate_back(dq_heads.transpose(1, 0, 2), cosine, sine).reshape(group, head_width)
    d_keys = rotate_back(dk_heads.transpose(1, 0, 2), cosine, sine).reshape(group, head_width)
    d_values = dv_heads.transpose(1, 0, 2).reshape(group, head_width)
    d_qkv = jnp.concatenate([d_query, d_keys, d_values], axis=1).astype(jnp.bfloat16)
    d_both = jnp.concatenate([d_qkv, d_pre], axis=1)
    bias_part = jnp.sum(d_qkv.astype(jnp.float32), axis=0).reshape(3, head_width)
    d_hidden = ring_reduce_scatter(
        jnp.einsum("tc,dc->td", d_both, cols, preferred_element_type=jnp.float32), ring, 3
    )
    weight_parts = jnp.einsum(
        "td,tc->dc", hidden_group, d_both, preferred_element_type=jnp.float32
    ).astype(jnp.bfloat16)
    owned_parts = lax.psum_scatter(weight_parts, "dp", scatter_dimension=0, tiled=True)
    split_qkv, split_fc1 = return_heads(owned_parts)
    d_hidden, split_qkv, split_fc1 = lax.optimization_barrier((d_hidden, split_qkv, split_fc1))
    grad_gain, grad_shift, d_inputs = norm_back(d_hidden, normed, scaled, gain32)
    grad_tokens = (grad_out32 + d_inputs).astype(jnp.bfloat16)
    owned_fc2 = lax.psum_scatter(
        grad_fc2_part.astype(jnp.bfloat16), "dp", scatter_dimension=0, tiled=True
    ).astype(jnp.float32)
    full_bqkv = lax.dynamic_update_slice_in_dim(
        jnp.zeros((3, D), jnp.float32), bias_part, here * head_width, 1
    )
    full_bfc1 = lax.dynamic_update_slice_in_dim(
        jnp.zeros((dp_count, ctx_count, unit), jnp.float32),
        grad_bfc1_part.reshape(dp_count, 1, unit),
        here,
        1,
    )
    small = jnp.concatenate(
        [
            full_bqkv.reshape(count, -1),
            grad_b_fc2.reshape(count, -1),
            grad_gain.reshape(count, -1),
            grad_shift.reshape(count, -1),
            full_bfc1.reshape(count, -1),
        ],
        axis=1,
    )
    owned_small = reduce_small(small)
    cuts = [0, 3 * D // count, D // count, D // count, D // count, FF // count]
    bounds = [sum(cuts[: i + 1]) for i in range(len(cuts))]
    owned_bqkv, owned_bout, owned_gain, owned_shift, owned_bfc1 = [
        owned_small[bounds[i] : bounds[i + 1]] for i in range(5)
    ]
    return (
        block_out,
        grad_tokens,
        split_qkv.reshape(rows_piece, 3 * D),
        owned_bqkv,
        owned_w_out,
        owned_bout,
        split_fc1.reshape(rows_piece, FF),
        owned_bfc1,
        owned_fc2,
        owned_bout,
        owned_gain,
        owned_shift,
    )


def body(
    ring,
    tokens,
    lengths,
    w_qkv,
    b_qkv,
    w_out,
    b_out,
    w_fc1,
    b_fc1,
    w_fc2,
    b_fc2,
    ln_gain,
    ln_shift,
    cotangent,
):
    return head_plan(
        ring,
        tokens,
        lengths,
        w_qkv,
        b_qkv,
        w_out,
        b_out,
        w_fc1,
        b_fc1,
        w_fc2,
        b_fc2,
        ln_gain,
        ln_shift,
        cotangent,
    )


def solution(mesh):
    in_specs = (
        P(("dp", "ctx"), None),
        P("dp", None),
        P(("dp", "ctx"), None),
        P(("dp", "ctx")),
        P(("dp", "ctx"), None),
        P(("dp", "ctx")),
        P(("dp", "ctx"), None),
        P(("dp", "ctx")),
        P(("dp", "ctx"), None),
        P(("dp", "ctx")),
        P(("dp", "ctx")),
        P(("dp", "ctx")),
        P(("dp", "ctx"), None),
    )
    out_specs = (
        P(("dp", "ctx"), None),
        P(("dp", "ctx"), None),
        P(("dp", "ctx"), None),
        P(("dp", "ctx")),
        P(("dp", "ctx"), None),
        P(("dp", "ctx")),
        P(("dp", "ctx"), None),
        P(("dp", "ctx")),
        P(("dp", "ctx"), None),
        P(("dp", "ctx")),
        P(("dp", "ctx")),
        P(("dp", "ctx")),
    )
    ring = ring_of(mesh)
    return jax.shard_map(functools.partial(body, ring), mesh=mesh, in_specs=in_specs, out_specs=out_specs, check_vma=False)
```

```python
import functools
import math

import jax
import jax.numpy as jnp
from jax import lax
from jax.experimental import pallas as pl
from jax.experimental.pallas import tpu as pltpu
from jax.sharding import PartitionSpec as P

D = 2048
HEADS = 32
HEAD_DIM = 64
ROT = 32
FF = 8192


EPS = 1e-05
GELU_COEF = math.sqrt(2.0 / math.pi)
NEGATIVE = -1e30


def norm_parts(inputs, gain, shift):
    mean = jnp.mean(inputs, axis=-1, keepdims=True)
    centred = inputs - mean
    var = jnp.mean(centred * centred, axis=-1, keepdims=True)
    scaled = lax.rsqrt(var + EPS)
    normed = centred * scaled
    return (normed, scaled, normed * gain + shift)


def norm_back(d_hidden, normed, scaled, gain32):
    grad_gain = jnp.sum(d_hidden * normed, axis=0)
    grad_shift = jnp.sum(d_hidden, axis=0)
    d_normed = d_hidden * gain32
    d_inputs = scaled * (
        d_normed
        - jnp.mean(d_normed, axis=-1, keepdims=True)
        - normed * jnp.mean(d_normed * normed, axis=-1, keepdims=True)
    )
    return (grad_gain, grad_shift, d_inputs)


def gelu_tanh(pre):
    return 0.5 * pre * (1.0 + jnp.tanh(GELU_COEF * (pre + 0.044715 * pre * pre * pre)))


def gelu_slope(pre):
    tangent = jnp.tanh(GELU_COEF * (pre + 0.044715 * pre * pre * pre))
    return 0.5 * (1.0 + tangent) + 0.5 * pre * (1.0 - tangent * tangent) * GELU_COEF * (
        1.0 + 3.0 * 0.044715 * pre * pre
    )


def rotary_tables(positions):
    half = ROT // 2
    freq = jnp.exp(jnp.arange(half, dtype=jnp.float32) * (-2.0 * math.log(10000.0) / ROT))
    angle = positions.astype(jnp.float32)[:, None] * freq[None, :]
    return (jnp.cos(angle)[:, None, :], jnp.sin(angle)[:, None, :])


def rotate(heads, cosine, sine):
    half = ROT // 2
    first = heads[..., :half]
    second = heads[..., half:ROT]
    return jnp.concatenate(
        [first * cosine - second * sine, second * cosine + first * sine, heads[..., ROT:]], axis=-1
    )


def rotate_back(grads, cosine, sine):
    half = ROT // 2
    first = grads[..., :half]
    second = grads[..., half:ROT]
    return jnp.concatenate(
        [first * cosine + second * sine, second * cosine - first * sine, grads[..., ROT:]], axis=-1
    )


def segment_info(lengths_row, rows):
    ends = jnp.cumsum(lengths_row)
    starts = ends - lengths_row
    seg = jnp.sum((rows[:, None] >= ends[None, :]).astype(jnp.int32), axis=1)
    onehot = seg[:, None] == jnp.arange(lengths_row.shape[0], dtype=jnp.int32)[None, :]
    first_rows = jnp.sum(jnp.where(onehot, starts[None, :], 0), axis=1)
    return (seg, rows - first_rows)


TRANS_B = (((1,), (1,)), ((), ()))


def _allowed(segq_ref, segk_ref, i, j, tq, tk, causal):
    same = segq_ref[...] == segk_ref[...]
    if not causal:
        return same
    rows = i * tq + lax.broadcasted_iota(jnp.int32, (tq, tk), 0)
    cols = j * tk + lax.broadcasted_iota(jnp.int32, (tq, tk), 1)
    return same & (cols <= rows)


def _fwd_kernel(qi_ref, kj_ref, q_ref, k_ref, v_ref, segq_ref, segk_ref, o_ref, lse_ref, m_sc, acc_sc, *, tq, tk, scale):
    t = pl.program_id(1)
    i = qi_ref[t]
    j = kj_ref[t]
    dim = o_ref.shape[2]

    @pl.when(j == 0)
    def _():
        m_sc[...] = jnp.full_like(m_sc, NEGATIVE)
        acc_sc[...] = jnp.zeros_like(acc_sc)

    def absorb(causal):
        q = q_ref[0]
        k = k_ref[0]
        s = lax.dot_general(q, k, TRANS_B, preferred_element_type=jnp.float32) * scale
        s = jnp.where(_allowed(segq_ref, segk_ref, i, j, tq, tk, causal), s, -jnp.inf)
        m_prev = m_sc[...]
        lanes = s.shape[1]
        folded = s[:, :128]
        for start in range(128, lanes, 128):
            folded = jnp.maximum(folded, s[:, start : start + 128])
        m_new = jnp.maximum(m_prev, jnp.max(folded, axis=1, keepdims=True))
        factor = jnp.exp(m_prev - m_new)
        p = jnp.exp(s - m_new)
        acc_sc[...] = acc_sc[...] * factor + jnp.dot(
            p.astype(jnp.bfloat16), v_ref[0], preferred_element_type=jnp.float32
        )
        m_sc[...] = m_new

    @pl.when(j < i)
    def _():
        absorb(False)

    @pl.when(j == i)
    def _():
        absorb(True)
        acc = acc_sc[...]
        total = acc[:, dim : dim + 1]
        o_ref[0] = acc[:, :dim] / total
        lse_ref[0] = m_sc[...] + jnp.log(total)


def _schedule(count, queries_outer):
    if queries_outer:
        pairs = [(i, j) for i in range(count) for j in range(i + 1)]
    else:
        pairs = [(i, j) for j in range(count) for i in range(j, count)]
    return (
        jnp.asarray([p[0] for p in pairs], jnp.int32),
        jnp.asarray([p[1] for p in pairs], jnp.int32),
    )


def attention_forward(q, k, v, seg, block=1024):
    heads, total, dim = q.shape
    count = total // block
    scale = 1.0 / math.sqrt(dim)
    segq = seg.reshape(total, 1)
    segk = seg.reshape(1, total)
    qi, kj = _schedule(count, True)
    steps = qi.shape[0]
    lanes = 2 * dim
    v_ext = jnp.concatenate(
        [v, jnp.ones((heads, total, 1), v.dtype), jnp.zeros((heads, total, lanes - dim - 1), v.dtype)],
        axis=2,
    )

    return pl.pallas_call(
        functools.partial(_fwd_kernel, tq=block, tk=block, scale=scale),
        out_shape=(
            jax.ShapeDtypeStruct((heads, total, dim), jnp.float32),
            jax.ShapeDtypeStruct((heads, total, 1), jnp.float32),
        ),
        grid_spec=pltpu.PrefetchScalarGridSpec(
            num_scalar_prefetch=2,
            grid=(heads, steps),
            in_specs=[
                pl.BlockSpec((1, block, dim), lambda h, t, qi, kj: (h, qi[t], 0)),
                pl.BlockSpec((1, block, dim), lambda h, t, qi, kj: (h, kj[t], 0)),
                pl.BlockSpec((1, block, lanes), lambda h, t, qi, kj: (h, kj[t], 0)),
                pl.BlockSpec((block, 1), lambda h, t, qi, kj: (qi[t], 0)),
                pl.BlockSpec((1, block), lambda h, t, qi, kj: (0, kj[t])),
            ],
            out_specs=[
                pl.BlockSpec((1, block, dim), lambda h, t, qi, kj: (h, qi[t], 0)),
                pl.BlockSpec((1, block, 1), lambda h, t, qi, kj: (h, qi[t], 0)),
            ],
            scratch_shapes=[
                pltpu.VMEM((block, 1), jnp.float32),
                pltpu.VMEM((block, lanes), jnp.float32),
            ],
        ),
        cost_estimate=pl.CostEstimate(
            flops=2 * heads * total * total * dim,
            transcendentals=heads * total * total // 2,
            bytes_accessed=heads * total * dim * 10,
        ),
    )(qi, kj, q, k, v_ext, segq, segk)


def _bwd_kernel(qi_ref, kj_ref, q_ref, k_ref, v_ref, do_ref, lse_ref, delta_ref, segq_ref, segk_ref, dq_ref, dk_ref, dv_ref, dk_sc, dv_sc, *, tq, tk, scale, count):
    t = pl.program_id(1)
    i = qi_ref[t]
    j = kj_ref[t]

    @pl.when(t == 0)
    def _():
        dq_ref[...] = jnp.zeros_like(dq_ref)

    @pl.when(i == j)
    def _():
        dk_sc[...] = jnp.zeros_like(dk_sc)
        dv_sc[...] = jnp.zeros_like(dv_sc)

    def absorb(causal):
        q = q_ref[0]
        k = k_ref[0]
        do = do_ref[0]
        s = lax.dot_general(q, k, TRANS_B, preferred_element_type=jnp.float32) * scale
        s = jnp.where(_allowed(segq_ref, segk_ref, i, j, tq, tk, causal), s, -jnp.inf)
        p = jnp.exp(s - lse_ref[0])
        dp = lax.dot_general(do, v_ref[0], TRANS_B, preferred_element_type=jnp.float32)
        ds = (p * (dp - delta_ref[0])).astype(jnp.bfloat16)
        dv_sc[...] += jnp.dot(do.T, p.astype(jnp.bfloat16), preferred_element_type=jnp.float32)
        dk_sc[...] += jnp.dot(q.T, ds, preferred_element_type=jnp.float32)
        rows = pl.ds(pl.multiple_of(i * tq, tq), tq)
        dq_ref[0, rows, :] += lax.dot(ds, k, preferred_element_type=jnp.float32) * scale

    @pl.when(j < i)
    def _():
        absorb(False)

    @pl.when(j == i)
    def _():
        absorb(True)

    @pl.when(i == count - 1)
    def _():
        dk_ref[0] = dk_sc[...].T * scale
        dv_ref[0] = dv_sc[...].T


def attention_backward(q, k, v, do, lse, delta, seg, block=1024):
    heads, total, dim = q.shape
    count = total // block
    scale = 1.0 / math.sqrt(dim)
    segq = seg.reshape(total, 1)
    segk = seg.reshape(1, total)
    qi, kj = _schedule(count, False)
    steps = qi.shape[0]

    def q_map(h, t, qi, kj):
        return (h, qi[t], 0)

    def k_map(h, t, qi, kj):
        return (h, kj[t], 0)

    return pl.pallas_call(
        functools.partial(_bwd_kernel, tq=block, tk=block, scale=scale, count=count),
        out_shape=(
            jax.ShapeDtypeStruct((heads, total, dim), jnp.float32),
            jax.ShapeDtypeStruct((heads, total, dim), jnp.float32),
            jax.ShapeDtypeStruct((heads, total, dim), jnp.float32),
        ),
        grid_spec=pltpu.PrefetchScalarGridSpec(
            num_scalar_prefetch=2,
            grid=(heads, steps),
            in_specs=[
                pl.BlockSpec((1, block, dim), q_map),
                pl.BlockSpec((1, block, dim), k_map),
                pl.BlockSpec((1, block, dim), k_map),
                pl.BlockSpec((1, block, dim), q_map),
                pl.BlockSpec((1, block, 1), q_map),
                pl.BlockSpec((1, block, 1), q_map),
                pl.BlockSpec((block, 1), lambda h, t, qi, kj: (qi[t], 0)),
                pl.BlockSpec((1, block), lambda h, t, qi, kj: (0, kj[t])),
            ],
            out_specs=[
                pl.BlockSpec((1, total, dim), lambda h, t, qi, kj: (h, 0, 0)),
                pl.BlockSpec((1, block, dim), k_map),
                pl.BlockSpec((1, block, dim), k_map),
            ],
            scratch_shapes=[
                pltpu.VMEM((dim, block), jnp.float32),
                pltpu.VMEM((dim, block), jnp.float32),
            ],
        ),
        cost_estimate=pl.CostEstimate(
            flops=5 * heads * total * total * dim,
            transcendentals=heads * total * total // 2,
            bytes_accessed=heads * total * dim * 24,
        ),
    )(qi, kj, q, k, v, do, lse, delta, segq, segk)


MESH_ID = pl.DeviceIdType.MESH


class Ring:
    def __init__(self, size, a_stride, b_stride):
        self.size = size
        self.half = size // 2
        self.a_stride = a_stride
        self.b_stride = b_stride

    def position(self, c):
        a = (c // self.a_stride) % self.half
        b = (c // self.b_stride) % 2
        return a + b * (2 * self.half - 1 - 2 * a)

    def device(self, pos):
        pos = pos % self.size
        b = pos // self.half
        a = pos + b * (2 * self.half - 1 - 2 * pos)
        return a * self.a_stride + b * self.b_stride


def ring_of(mesh):
    size = mesh.shape["ctx"]
    devices = list(mesh.devices.reshape(-1, size)[0])
    try:
        coords = [tuple(d.coords) for d in devices]
    except AttributeError:
        coords = None
    if coords and size % 2 == 0 and size >= 4:
        for b_stride in range(1, size):
            for a_stride in range(1, size):
                ring = Ring(size, a_stride, b_stride)
                order = [ring.device(p) for p in range(size)]
                if sorted(order) != list(range(size)):
                    continue
                hops = [
                    sum(abs(x - y) for x, y in zip(coords[order[p]], coords[order[(p + 1) % size]]))
                    for p in range(size)
                ]
                if max(hops) == 1:
                    return ring
    return Ring(size, 2, 1) if size % 2 == 0 and size >= 4 else None


def _barrier(g, left, right):
    barrier = pltpu.get_barrier_semaphore()
    for other in (left, right):
        pl.semaphore_signal(barrier, 1, device_id=(g, other), device_id_type=MESH_ID)
    pl.semaphore_wait(barrier, 2)


def _gather_kernel(x_ref, y_ref, own_sem, send_sem, recv_sem, *, ring, rows, parts):
    n = ring.size
    half = rows // 2
    piece = half // parts
    g = lax.axis_index("dp")
    c = lax.axis_index("ctx")
    pos = ring.position(c)
    right = ring.device(pos + 1)
    left = ring.device(pos + n - 1)
    own = pltpu.make_async_copy(x_ref, y_ref.at[pl.ds(c * rows, rows)], own_sem)
    own.start()
    _barrier(g, left, right)

    def link(direction, step, part, origin, source):
        offset = origin * rows + direction * half + part * piece
        return pltpu.make_async_remote_copy(
            src_ref=source,
            dst_ref=y_ref.at[pl.ds(offset, piece)],
            send_sem=send_sem.at[direction, step, part],
            recv_sem=recv_sem.at[direction, step, part],
            device_id=(g, right if direction == 0 else left),
            device_id_type=MESH_ID,
        )

    sent = []
    for step in range(n - 1):
        origins = (ring.device(pos - step + n), ring.device(pos + step))
        for part in range(parts):
            for direction in (0, 1):
                origin = origins[direction]
                here_rows = y_ref.at[pl.ds(origin * rows + direction * half + part * piece, piece)]
                if step == 0:
                    source = x_ref.at[pl.ds(direction * half + part * piece, piece)]
                else:
                    link(direction, step - 1, part, origin, here_rows).wait_recv()
                    source = here_rows
                copy = link(direction, step, part, origin, source)
                copy.start()
                sent.append(copy)
    last = n - 2
    for part in range(parts):
        for direction, origin in ((0, ring.device(pos - last - 1 + n)), (1, ring.device(pos + last + 1))):
            rows_at = y_ref.at[pl.ds(origin * rows + direction * half + part * piece, piece)]
            link(direction, last, part, origin, rows_at).wait_recv()
    for copy in sent:
        copy.wait_send()
    own.wait()


def ring_all_gather(x, ring, collective_id):
    rows, cols = x.shape
    n = ring.size
    return pl.pallas_call(
        functools.partial(_gather_kernel, ring=ring, rows=rows, parts=2),
        out_shape=jax.ShapeDtypeStruct((n * rows, cols), x.dtype),
        in_specs=[pl.BlockSpec(memory_space=pl.ANY)],
        out_specs=pl.BlockSpec(memory_space=pl.ANY),
        scratch_shapes=[
            pltpu.SemaphoreType.DMA(()),
            pltpu.SemaphoreType.DMA((2, n - 1, 2)),
            pltpu.SemaphoreType.DMA((2, n - 1, 2)),
        ],
        compiler_params=pltpu.CompilerParams(collective_id=collective_id, has_side_effects=True),
    )(x)


def _scatter_kernel(p_ref, out_ref, recv_buf, send_buf, send_sem, recv_sem, *, ring, rows, parts):
    n = ring.size
    half = rows // 2
    piece = half // parts
    g = lax.axis_index("dp")
    c = lax.axis_index("ctx")
    pos = ring.position(c)
    right = ring.device(pos + 1)
    left = ring.device(pos + n - 1)
    _barrier(g, left, right)

    def link(direction, step, part):
        window = pl.ds(part * piece, piece)
        return pltpu.make_async_remote_copy(
            src_ref=send_buf.at[direction, step, window],
            dst_ref=recv_buf.at[direction, step, window],
            send_sem=send_sem.at[direction, step, part],
            recv_sem=recv_sem.at[direction, step, part],
            device_id=(g, right if direction == 0 else left),
            device_id_type=MESH_ID,
        )

    sent = []
    for step in range(n - 1):
        targets = (ring.device(pos - 1 - step + 2 * n), ring.device(pos + 1 + step))
        for part in range(parts):
            for direction in (0, 1):
                start = pl.multiple_of(
                    targets[direction] * rows + direction * half + part * piece, piece
                )
                window = pl.ds(part * piece, piece)
                total = p_ref[pl.ds(start, piece), :].astype(jnp.float32)
                if step > 0:
                    link(direction, step - 1, part).wait_recv()
                    total = total + recv_buf[direction, step - 1, window].astype(jnp.float32)
                send_buf[direction, step, window] = total.astype(send_buf.dtype)
                copy = link(direction, step, part)
                copy.start()
                sent.append(copy)
    for part in range(parts):
        for direction in (0, 1):
            link(direction, n - 2, part).wait_recv()
            start = pl.multiple_of(c * rows + direction * half + part * piece, piece)
            window = pl.ds(part * piece, piece)
            out_ref[pl.ds(direction * half + part * piece, piece), :] = (
                p_ref[pl.ds(start, piece), :].astype(jnp.float32)
                + recv_buf[direction, n - 2, window].astype(jnp.float32)
            ).astype(out_ref.dtype)
    for copy in sent:
        copy.wait_send()


def ring_reduce_scatter(p, ring, collective_id, out_dtype=jnp.float32, wire=jnp.bfloat16, parts=2):
    total_rows, cols = p.shape
    n = ring.size
    rows = total_rows // n
    half = rows // 2
    return pl.pallas_call(
        functools.partial(_scatter_kernel, ring=ring, rows=rows, parts=parts),
        out_shape=jax.ShapeDtypeStruct((rows, cols), out_dtype),
        in_specs=[pl.BlockSpec(memory_space=pltpu.VMEM)],
        out_specs=pl.BlockSpec(memory_space=pltpu.VMEM),
        scratch_shapes=[
            pltpu.VMEM((2, n - 1, half, cols), wire),
            pltpu.VMEM((2, n - 1, half, cols), wire),
            pltpu.SemaphoreType.DMA((2, n - 1, parts)),
            pltpu.SemaphoreType.DMA((2, n - 1, parts)),
        ],
        compiler_params=pltpu.CompilerParams(
            collective_id=collective_id, has_side_effects=True, vmem_limit_bytes=60 * 1024 * 1024
        ),
    )(p)


def _exchange_kernel(x_ref, out_ref, own_sem, send_sem, recv_sem, *, group):
    n = x_ref.shape[0]
    g = lax.axis_index("dp")
    c = lax.axis_index("ctx")
    n_ctx = lax.axis_size("ctx")
    me = {"all": g * n_ctx + c, "ctx": c, "dp": g}[group]

    def address(member):
        if group == "all":
            return (member // n_ctx, member % n_ctx)
        if group == "ctx":
            return (g, member)
        return (member, c)

    own = pltpu.make_async_copy(x_ref.at[me], out_ref.at[me], own_sem)
    own.start()
    barrier = pltpu.get_barrier_semaphore()
    for offset in range(1, n):
        pl.semaphore_signal(
            barrier, 1, device_id=address((me + offset) % n), device_id_type=MESH_ID
        )
    pl.semaphore_wait(barrier, n - 1)

    def link(offset, source, target):
        return pltpu.make_async_remote_copy(
            src_ref=x_ref.at[target],
            dst_ref=out_ref.at[source],
            send_sem=send_sem.at[offset],
            recv_sem=recv_sem.at[offset],
            device_id=address(target),
            device_id_type=MESH_ID,
        )

    sent = []
    for offset in range(1, n):
        copy = link(offset, me, (me + offset) % n)
        copy.start()
        sent.append(copy)
    for offset in range(1, n):
        link(offset, (me + n - offset) % n, me).wait_recv()
    for copy in sent:
        copy.wait_send()
    own.wait()


def exchange(x, group, collective_id):
    n = x.shape[0]
    space = pltpu.VMEM
    return pl.pallas_call(
        functools.partial(_exchange_kernel, group=group),
        out_shape=jax.ShapeDtypeStruct(x.shape, x.dtype),
        in_specs=[pl.BlockSpec(memory_space=space)],
        out_specs=pl.BlockSpec(memory_space=space),
        scratch_shapes=[
            pltpu.SemaphoreType.DMA(()),
            pltpu.SemaphoreType.DMA((n,)),
            pltpu.SemaphoreType.DMA((n,)),
        ],
        compiler_params=pltpu.CompilerParams(collective_id=collective_id, has_side_effects=True),
    )(x)


def block_moves(n_dp, n_ctx):
    count = n_dp * n_ctx
    return [(f, (f % n_dp) * n_ctx + f // n_dp) for f in range(count)]


def fetch_out_rows(w_out):
    n_dp = lax.axis_size("dp")
    n_ctx = lax.axis_size("ctx")
    moved = lax.ppermute(w_out.astype(jnp.bfloat16), ("dp", "ctx"), perm=block_moves(n_dp, n_ctx))
    return lax.all_gather(moved, "dp", axis=0, tiled=True)


def return_out_rows(grad_out_rows):
    n_dp = lax.axis_size("dp")
    n_ctx = lax.axis_size("ctx")
    part = lax.psum_scatter(grad_out_rows, "dp", scatter_dimension=0, tiled=True)
    back = [(b, a) for a, b in block_moves(n_dp, n_ctx)]
    return lax.ppermute(part, ("dp", "ctx"), perm=back)


def pack_rows(vector, lanes):
    size = vector.shape[0]
    total = -(-size // (16 * lanes)) * 16 * lanes
    return jnp.pad(vector, (0, total - size)).reshape(-1, lanes)


def fetch_small(b_qkv, b_out, b_fc2, ln_gain, ln_shift, b_fc1):
    pieces = (b_qkv, b_out, b_fc2, ln_gain, ln_shift, b_fc1)
    n_dp = lax.axis_size("dp")
    n_ctx = lax.axis_size("ctx")
    packed = pack_rows(jnp.concatenate([p.astype(jnp.bfloat16) for p in pieces]), 128)
    over_dp = exchange(jnp.broadcast_to(packed[None], (n_dp,) + packed.shape), "dp", 4)
    over_all = exchange(jnp.broadcast_to(over_dp[None], (n_ctx,) + over_dp.shape), "ctx", 8)
    table = over_all.transpose(1, 0, 2, 3).reshape(n_dp * n_ctx, -1)
    result = []
    offset = 0
    for p in pieces:
        result.append(table[:, offset : offset + p.shape[0]])
        offset += p.shape[0]
    return result


def reduce_small(small):
    n_dp = lax.axis_size("dp")
    n_ctx = lax.axis_size("ctx")
    count, width = small.shape
    packed = jax.vmap(lambda row: pack_rows(row, 128))(small)
    packed = packed.reshape((n_dp, n_ctx) + packed.shape[1:]).transpose(1, 0, 2, 3)
    over_ctx = jnp.sum(exchange(packed, "ctx", 7), axis=0)
    over_dp = jnp.sum(exchange(over_ctx, "dp", 9), axis=0)
    return over_dp.reshape(-1)[:width]


def fetch_heads(w_qkv, w_fc1, w_fc2, tokens):
    dp_count = lax.axis_size("dp")
    ctx_count = lax.axis_size("ctx")
    rows_piece = w_qkv.shape[0]
    head_width = D // ctx_count
    unit = FF // (dp_count * ctx_count)
    qkv_piece = w_qkv.astype(jnp.bfloat16).reshape(rows_piece, 3, ctx_count, head_width)
    fc1_piece = w_fc1.astype(jnp.bfloat16).reshape(rows_piece, dp_count, ctx_count, unit)
    pieces = jnp.concatenate(
        [
            qkv_piece.transpose(2, 0, 1, 3).reshape(ctx_count, rows_piece, 3 * head_width),
            fc1_piece.transpose(2, 0, 1, 3).reshape(ctx_count, rows_piece, dp_count * unit),
        ],
        axis=2,
    )
    sent = exchange(pieces, "ctx", 5).reshape(ctx_count * rows_piece, -1)
    sent, tokens = lax.optimization_barrier((sent, tokens))
    cols, fc2_rows = (
        lax.all_gather(sent, "dp", axis=0, tiled=True),
        lax.all_gather(w_fc2.astype(jnp.bfloat16), "dp", axis=0, tiled=True),
    )
    return (cols, fc2_rows, tokens)


def return_heads(owned_parts):
    dp_count = lax.axis_size("dp")
    ctx_count = lax.axis_size("ctx")
    head_width = D // ctx_count
    unit = FF // (dp_count * ctx_count)
    rows_piece = owned_parts.shape[0] // ctx_count
    got = exchange(owned_parts.reshape(ctx_count, rows_piece, -1), "ctx", 6)
    qkv = got[:, :, : 3 * head_width].reshape(ctx_count, rows_piece, 3, head_width)
    fc1 = got[:, :, 3 * head_width :].reshape(ctx_count, rows_piece, dp_count, unit)
    return (
        qkv.transpose(1, 2, 0, 3).reshape(rows_piece, 3 * D).astype(jnp.float32),
        fc1.transpose(1, 2, 0, 3).reshape(rows_piece, FF).astype(jnp.float32),
    )


def head_plan(
    ring,
    tokens,
    lengths,
    w_qkv,
    b_qkv,
    w_out,
    b_out,
    w_fc1,
    b_fc1,
    w_fc2,
    b_fc2,
    ln_gain,
    ln_shift,
    cotangent,
):
    rows_here = tokens.shape[0]
    rows_piece = w_qkv.shape[0]
    dp_count = lax.axis_size("dp")
    ctx_count = lax.axis_size("ctx")
    count = dp_count * ctx_count
    group = rows_here * ctx_count
    head_width = D // ctx_count
    local_heads = HEADS // ctx_count
    unit = FF // (dp_count * ctx_count)
    here = lax.axis_index("ctx")
    group_rows = jnp.arange(group, dtype=jnp.int32)
    seg, positions = segment_info(lengths[0], group_rows)
    cosine, sine = rotary_tables(positions)
    qkv_bias, out_bias, fc2_bias, gain_low, shift_low, fc1_table = fetch_small(
        b_qkv, b_out, b_fc2, ln_gain, ln_shift, b_fc1
    )
    qkv_bias = qkv_bias.reshape(3 * D)
    out_bias = out_bias.reshape(D)
    fc2_bias = fc2_bias.reshape(D)
    gain_low = gain_low.reshape(D)
    shift_low = shift_low.reshape(D)
    fc1_bias = lax.dynamic_index_in_dim(
        fc1_table.reshape(dp_count, ctx_count, unit), here, 1, keepdims=False
    ).reshape(dp_count * unit)
    out_rows = fetch_out_rows(w_out)
    cols, fc2_rows, tokens = fetch_heads(w_qkv, w_fc1, w_fc2, tokens)
    gain32 = gain_low.astype(jnp.float32)
    shift32 = shift_low.astype(jnp.float32)
    inputs = tokens.astype(jnp.float32)
    normed, scaled, _ = norm_parts(inputs, gain32, shift32)
    tokens_group = ring_all_gather(tokens, ring, 0)
    late_dy, tokens_group = lax.optimization_barrier((cotangent, tokens_group))
    dy_group = lax.all_gather(late_dy, "ctx", axis=0, tiled=True)
    hidden_group = norm_parts(tokens_group.astype(jnp.float32), gain32, shift32)[2].astype(
        jnp.bfloat16
    )
    bias_cols = lax.dynamic_slice_in_dim(
        qkv_bias.reshape(3, D), here * head_width, head_width, 1
    ).reshape(3 * head_width)
    both = jnp.dot(hidden_group, cols, preferred_element_type=jnp.float32) + jnp.concatenate(
        [bias_cols, fc1_bias]
    ).astype(jnp.float32)
    qkv = both[:, : 3 * head_width]
    pre = both[:, 3 * head_width :]
    shape = (group, local_heads, HEAD_DIM)
    query = rotate(qkv[:, :head_width].reshape(shape), cosine, sine).astype(jnp.bfloat16)
    keys = rotate(qkv[:, head_width : 2 * head_width].reshape(shape), cosine, sine).astype(
        jnp.bfloat16
    )
    values = qkv[:, 2 * head_width :].reshape(shape).astype(jnp.bfloat16)
    q_heads = query.transpose(1, 0, 2)
    k_heads = keys.transpose(1, 0, 2)
    v_heads = values.transpose(1, 0, 2)
    attended_heads, log_total = attention_forward(q_heads, k_heads, v_heads, seg)
    attended = attended_heads.transpose(1, 0, 2).reshape(group, head_width).astype(jnp.bfloat16)
    act = gelu_tanh(pre).astype(jnp.bfloat16)
    branches = ring_reduce_scatter(
        jnp.dot(attended, out_rows, preferred_element_type=jnp.float32)
        + jnp.dot(act, fc2_rows, preferred_element_type=jnp.float32),
        ring,
        2,
    )
    block_out = (
        inputs + branches + out_bias.astype(jnp.float32) + fc2_bias.astype(jnp.float32)
    ).astype(jnp.bfloat16)
    grad_out32 = cotangent.astype(jnp.float32)
    grad_b_fc2 = jnp.sum(grad_out32, axis=0)
    grad_fc2_part = jnp.einsum("tf,td->fd", act, dy_group, preferred_element_type=jnp.float32)
    d_act = jnp.einsum("td,fd->tf", dy_group, fc2_rows, preferred_element_type=jnp.float32)
    d_pre = (d_act * gelu_slope(pre)).astype(jnp.bfloat16)
    grad_bfc1_part = jnp.sum(d_pre.astype(jnp.float32), axis=0)
    grad_out_rows = jnp.einsum("tc,td->cd", attended, dy_group, preferred_element_type=jnp.float32)
    owned_w_out = return_out_rows(grad_out_rows)
    d_attended = (
        jnp.einsum("td,cd->tc", dy_group, out_rows, preferred_element_type=jnp.float32)
        .astype(jnp.bfloat16)
        .reshape(shape)
    )
    d_heads = d_attended.transpose(1, 0, 2)
    delta = jnp.sum(d_heads.astype(jnp.float32) * attended_heads, axis=2, keepdims=True)
    dq_heads, dk_heads, dv_heads = attention_backward(
        q_heads, k_heads, v_heads, d_heads, log_total, delta, seg
    )
    d_query = dq_heads.transpose(1, 0, 2)
    d_keys = dk_heads.transpose(1, 0, 2)
    d_values = dv_heads.transpose(1, 0, 2)
    d_query = rotate_back(d_query, cosine, sine).reshape(group, head_width)
    d_keys = rotate_back(d_keys, cosine, sine).reshape(group, head_width)
    d_qkv = jnp.concatenate([d_query, d_keys, d_values.reshape(group, head_width)], axis=1).astype(
        jnp.bfloat16
    )
    d_both = jnp.concatenate([d_qkv, d_pre], axis=1)
    bias_part = jnp.sum(d_qkv.astype(jnp.float32), axis=0).reshape(3, head_width)
    d_hidden = ring_reduce_scatter(
        jnp.einsum("tc,dc->td", d_both, cols, preferred_element_type=jnp.float32), ring, 3
    )
    weight_parts = jnp.einsum(
        "td,tc->dc", hidden_group, d_both, preferred_element_type=jnp.float32
    ).astype(jnp.bfloat16)
    owned_parts = lax.psum_scatter(weight_parts, "dp", scatter_dimension=0, tiled=True)
    split_qkv, split_fc1 = return_heads(owned_parts)
    d_hidden, split_qkv, split_fc1 = lax.optimization_barrier((d_hidden, split_qkv, split_fc1))
    grad_gain, grad_shift, d_inputs = norm_back(d_hidden, normed, scaled, gain32)
    grad_tokens = (grad_out32 + d_inputs).astype(jnp.bfloat16)
    owned_fc2 = lax.psum_scatter(
        grad_fc2_part.astype(jnp.bfloat16), "dp", scatter_dimension=0, tiled=True
    ).astype(jnp.float32)
    full_bqkv = lax.dynamic_update_slice_in_dim(
        jnp.zeros((3, D), jnp.float32), bias_part, here * head_width, 1
    )
    full_bfc1 = lax.dynamic_update_slice_in_dim(
        jnp.zeros((dp_count, ctx_count, unit), jnp.float32),
        grad_bfc1_part.reshape(dp_count, 1, unit),
        here,
        1,
    )
    small = jnp.concatenate(
        [
            full_bqkv.reshape(count, -1),
            grad_b_fc2.reshape(count, -1),
            grad_gain.reshape(count, -1),
            grad_shift.reshape(count, -1),
            full_bfc1.reshape(count, -1),
        ],
        axis=1,
    )
    owned_small = reduce_small(small)
    cuts = [0, 3 * D // count, D // count, D // count, D // count, FF // count]
    bounds = [sum(cuts[: i + 1]) for i in range(len(cuts))]
    owned_bqkv, owned_bout, owned_gain, owned_shift, owned_bfc1 = [
        owned_small[bounds[i] : bounds[i + 1]] for i in range(5)
    ]
    return (
        block_out,
        grad_tokens,
        split_qkv.reshape(rows_piece, 3 * D),
        owned_bqkv,
        owned_w_out,
        owned_bout,
        split_fc1.reshape(rows_piece, FF),
        owned_bfc1,
        owned_fc2,
        owned_bout,
        owned_gain,
        owned_shift,
    )


def body(
    ring,
    tokens,
    lengths,
    w_qkv,
    b_qkv,
    w_out,
    b_out,
    w_fc1,
    b_fc1,
    w_fc2,
    b_fc2,
    ln_gain,
    ln_shift,
    cotangent,
):
    return head_plan(
        ring,
        tokens,
        lengths,
        w_qkv,
        b_qkv,
        w_out,
        b_out,
        w_fc1,
        b_fc1,
        w_fc2,
        b_fc2,
        ln_gain,
        ln_shift,
        cotangent,
    )


def solution(mesh):
    in_specs = (
        P(("dp", "ctx"), None),
        P("dp", None),
        P(("dp", "ctx"), None),
        P(("dp", "ctx")),
        P(("dp", "ctx"), None),
        P(("dp", "ctx")),
        P(("dp", "ctx"), None),
        P(("dp", "ctx")),
        P(("dp", "ctx"), None),
        P(("dp", "ctx")),
        P(("dp", "ctx")),
        P(("dp", "ctx")),
        P(("dp", "ctx"), None),
    )
    out_specs = (
        P(("dp", "ctx"), None),
        P(("dp", "ctx"), None),
        P(("dp", "ctx"), None),
        P(("dp", "ctx")),
        P(("dp", "ctx"), None),
        P(("dp", "ctx")),
        P(("dp", "ctx"), None),
        P(("dp", "ctx")),
        P(("dp", "ctx"), None),
        P(("dp", "ctx")),
        P(("dp", "ctx")),
        P(("dp", "ctx")),
    )
    ring = ring_of(mesh)
    return jax.shard_map(functools.partial(body, ring), mesh=mesh, in_specs=in_specs, out_specs=out_specs, check_vma=False)
```

```python
import functools
import math

import jax
import jax.numpy as jnp
from jax import lax
from jax.experimental import pallas as pl
from jax.experimental.pallas import tpu as pltpu
from jax.sharding import PartitionSpec as P

D = 2048
HEADS = 32
HEAD_DIM = 64
ROT = 32
FF = 8192


EPS = 1e-05
GELU_COEF = math.sqrt(2.0 / math.pi)
NEGATIVE = -1e30


def norm_parts(inputs, gain, shift):
    mean = jnp.mean(inputs, axis=-1, keepdims=True)
    centred = inputs - mean
    var = jnp.mean(centred * centred, axis=-1, keepdims=True)
    scaled = lax.rsqrt(var + EPS)
    normed = centred * scaled
    return (normed, scaled, normed * gain + shift)


def norm_back(d_hidden, normed, scaled, gain32):
    grad_gain = jnp.sum(d_hidden * normed, axis=0)
    grad_shift = jnp.sum(d_hidden, axis=0)
    d_normed = d_hidden * gain32
    d_inputs = scaled * (
        d_normed
        - jnp.mean(d_normed, axis=-1, keepdims=True)
        - normed * jnp.mean(d_normed * normed, axis=-1, keepdims=True)
    )
    return (grad_gain, grad_shift, d_inputs)


def gelu_tanh(pre):
    return 0.5 * pre * (1.0 + jnp.tanh(GELU_COEF * (pre + 0.044715 * pre * pre * pre)))


def gelu_slope(pre):
    tangent = jnp.tanh(GELU_COEF * (pre + 0.044715 * pre * pre * pre))
    return 0.5 * (1.0 + tangent) + 0.5 * pre * (1.0 - tangent * tangent) * GELU_COEF * (
        1.0 + 3.0 * 0.044715 * pre * pre
    )


def rotary_tables(positions):
    half = ROT // 2
    freq = jnp.exp(jnp.arange(half, dtype=jnp.float32) * (-2.0 * math.log(10000.0) / ROT))
    angle = positions.astype(jnp.float32)[:, None] * freq[None, :]
    return (jnp.cos(angle)[:, None, :], jnp.sin(angle)[:, None, :])


def rotate(heads, cosine, sine):
    half = ROT // 2
    first = heads[..., :half]
    second = heads[..., half:ROT]
    return jnp.concatenate(
        [first * cosine - second * sine, second * cosine + first * sine, heads[..., ROT:]], axis=-1
    )


def rotate_back(grads, cosine, sine):
    half = ROT // 2
    first = grads[..., :half]
    second = grads[..., half:ROT]
    return jnp.concatenate(
        [first * cosine + second * sine, second * cosine - first * sine, grads[..., ROT:]], axis=-1
    )


def segment_info(lengths_row, rows):
    ends = jnp.cumsum(lengths_row)
    starts = ends - lengths_row
    seg = jnp.sum((rows[:, None] >= ends[None, :]).astype(jnp.int32), axis=1)
    onehot = seg[:, None] == jnp.arange(lengths_row.shape[0], dtype=jnp.int32)[None, :]
    first_rows = jnp.sum(jnp.where(onehot, starts[None, :], 0), axis=1)
    return (seg, rows - first_rows)


TRANS_B = (((1,), (1,)), ((), ()))


def _allowed(segq_ref, segk_ref, i, j, tq, tk, causal):
    same = segq_ref[...] == segk_ref[...]
    if not causal:
        return same
    rows = i * tq + lax.broadcasted_iota(jnp.int32, (tq, tk), 0)
    cols = j * tk + lax.broadcasted_iota(jnp.int32, (tq, tk), 1)
    return same & (cols <= rows)


def _fwd_kernel(qi_ref, kj_ref, q_ref, k_ref, v_ref, segq_ref, segk_ref, o_ref, lse_ref, m_sc, acc_sc, *, tq, tk, scale):
    t = pl.program_id(1)
    i = qi_ref[t]
    j = kj_ref[t]
    dim = o_ref.shape[2]

    @pl.when(j == 0)
    def _():
        m_sc[...] = jnp.full_like(m_sc, NEGATIVE)
        acc_sc[...] = jnp.zeros_like(acc_sc)

    def absorb(causal):
        q = q_ref[0]
        k = k_ref[0]
        s = lax.dot_general(q, k, TRANS_B, preferred_element_type=jnp.float32) * scale
        s = jnp.where(_allowed(segq_ref, segk_ref, i, j, tq, tk, causal), s, -jnp.inf)
        m_prev = m_sc[...]
        lanes = s.shape[1]
        folded = s[:, :128]
        for start in range(128, lanes, 128):
            folded = jnp.maximum(folded, s[:, start : start + 128])
        m_new = jnp.maximum(m_prev, jnp.max(folded, axis=1, keepdims=True))
        factor = jnp.exp(m_prev - m_new)
        p = jnp.exp(s - m_new)
        acc_sc[...] = acc_sc[...] * factor + jnp.dot(
            p.astype(jnp.bfloat16), v_ref[0], preferred_element_type=jnp.float32
        )
        m_sc[...] = m_new

    @pl.when(j < i)
    def _():
        absorb(False)

    @pl.when(j == i)
    def _():
        absorb(True)
        acc = acc_sc[...]
        total = acc[:, dim : dim + 1]
        o_ref[0] = acc[:, :dim] / total
        lse_ref[0] = m_sc[...] + jnp.log(total)


def _schedule(count, queries_outer):
    if queries_outer:
        pairs = [(i, j) for i in range(count) for j in range(i + 1)]
    else:
        pairs = [(i, j) for j in range(count) for i in range(j, count)]
    return (
        jnp.asarray([p[0] for p in pairs], jnp.int32),
        jnp.asarray([p[1] for p in pairs], jnp.int32),
    )


def attention_forward(q, k, v, seg, block=1024):
    heads, total, dim = q.shape
    count = total // block
    scale = 1.0 / math.sqrt(dim)
    segq = seg.reshape(total, 1)
    segk = seg.reshape(1, total)
    qi, kj = _schedule(count, True)
    steps = qi.shape[0]
    lanes = 2 * dim
    v_ext = jnp.concatenate(
        [v, jnp.ones((heads, total, 1), v.dtype), jnp.zeros((heads, total, lanes - dim - 1), v.dtype)],
        axis=2,
    )

    return pl.pallas_call(
        functools.partial(_fwd_kernel, tq=block, tk=block, scale=scale),
        out_shape=(
            jax.ShapeDtypeStruct((heads, total, dim), jnp.float32),
            jax.ShapeDtypeStruct((heads, total, 1), jnp.float32),
        ),
        grid_spec=pltpu.PrefetchScalarGridSpec(
            num_scalar_prefetch=2,
            grid=(heads, steps),
            in_specs=[
                pl.BlockSpec((1, block, dim), lambda h, t, qi, kj: (h, qi[t], 0)),
                pl.BlockSpec((1, block, dim), lambda h, t, qi, kj: (h, kj[t], 0)),
                pl.BlockSpec((1, block, lanes), lambda h, t, qi, kj: (h, kj[t], 0)),
                pl.BlockSpec((block, 1), lambda h, t, qi, kj: (qi[t], 0)),
                pl.BlockSpec((1, block), lambda h, t, qi, kj: (0, kj[t])),
            ],
            out_specs=[
                pl.BlockSpec((1, block, dim), lambda h, t, qi, kj: (h, qi[t], 0)),
                pl.BlockSpec((1, block, 1), lambda h, t, qi, kj: (h, qi[t], 0)),
            ],
            scratch_shapes=[
                pltpu.VMEM((block, 1), jnp.float32),
                pltpu.VMEM((block, lanes), jnp.float32),
            ],
        ),
        cost_estimate=pl.CostEstimate(
            flops=2 * heads * total * total * dim,
            transcendentals=heads * total * total // 2,
            bytes_accessed=heads * total * dim * 10,
        ),
    )(qi, kj, q, k, v_ext, segq, segk)


def _bwd_kernel(qi_ref, kj_ref, q_ref, k_ref, v_ref, do_ref, lse_ref, delta_ref, segq_ref, segk_ref, dq_ref, dk_ref, dv_ref, dk_sc, dv_sc, *, tq, tk, scale, count):
    t = pl.program_id(1)
    i = qi_ref[t]
    j = kj_ref[t]

    @pl.when(t == 0)
    def _():
        dq_ref[...] = jnp.zeros_like(dq_ref)

    @pl.when(i == j)
    def _():
        dk_sc[...] = jnp.zeros_like(dk_sc)
        dv_sc[...] = jnp.zeros_like(dv_sc)

    def absorb(causal):
        q = q_ref[0]
        k = k_ref[0]
        do = do_ref[0]
        s = lax.dot_general(q, k, TRANS_B, preferred_element_type=jnp.float32) * scale
        s = jnp.where(_allowed(segq_ref, segk_ref, i, j, tq, tk, causal), s, -jnp.inf)
        p = jnp.exp(s - lse_ref[0])
        dp = lax.dot_general(do, v_ref[0], TRANS_B, preferred_element_type=jnp.float32)
        ds = (p * (dp - delta_ref[0])).astype(jnp.bfloat16)
        dv_sc[...] += jnp.dot(do.T, p.astype(jnp.bfloat16), preferred_element_type=jnp.float32)
        dk_sc[...] += jnp.dot(q.T, ds, preferred_element_type=jnp.float32)
        rows = pl.ds(pl.multiple_of(i * tq, tq), tq)
        dq_ref[0, rows, :] += lax.dot(ds, k, preferred_element_type=jnp.float32) * scale

    @pl.when(j < i)
    def _():
        absorb(False)

    @pl.when(j == i)
    def _():
        absorb(True)

    @pl.when(i == count - 1)
    def _():
        dk_ref[0] = dk_sc[...].T * scale
        dv_ref[0] = dv_sc[...].T


def attention_backward(q, k, v, do, lse, delta, seg, block=1024):
    heads, total, dim = q.shape
    count = total // block
    scale = 1.0 / math.sqrt(dim)
    segq = seg.reshape(total, 1)
    segk = seg.reshape(1, total)
    qi, kj = _schedule(count, False)
    steps = qi.shape[0]

    def q_map(h, t, qi, kj):
        return (h, qi[t], 0)

    def k_map(h, t, qi, kj):
        return (h, kj[t], 0)

    return pl.pallas_call(
        functools.partial(_bwd_kernel, tq=block, tk=block, scale=scale, count=count),
        out_shape=(
            jax.ShapeDtypeStruct((heads, total, dim), jnp.float32),
            jax.ShapeDtypeStruct((heads, total, dim), jnp.float32),
            jax.ShapeDtypeStruct((heads, total, dim), jnp.float32),
        ),
        grid_spec=pltpu.PrefetchScalarGridSpec(
            num_scalar_prefetch=2,
            grid=(heads, steps),
            in_specs=[
                pl.BlockSpec((1, block, dim), q_map),
                pl.BlockSpec((1, block, dim), k_map),
                pl.BlockSpec((1, block, dim), k_map),
                pl.BlockSpec((1, block, dim), q_map),
                pl.BlockSpec((1, block, 1), q_map),
                pl.BlockSpec((1, block, 1), q_map),
                pl.BlockSpec((block, 1), lambda h, t, qi, kj: (qi[t], 0)),
                pl.BlockSpec((1, block), lambda h, t, qi, kj: (0, kj[t])),
            ],
            out_specs=[
                pl.BlockSpec((1, total, dim), lambda h, t, qi, kj: (h, 0, 0)),
                pl.BlockSpec((1, block, dim), k_map),
                pl.BlockSpec((1, block, dim), k_map),
            ],
            scratch_shapes=[
                pltpu.VMEM((dim, block), jnp.float32),
                pltpu.VMEM((dim, block), jnp.float32),
            ],
        ),
        cost_estimate=pl.CostEstimate(
            flops=5 * heads * total * total * dim,
            transcendentals=heads * total * total // 2,
            bytes_accessed=heads * total * dim * 24,
        ),
    )(qi, kj, q, k, v, do, lse, delta, segq, segk)


MESH_ID = pl.DeviceIdType.MESH


class Ring:
    def __init__(self, size, a_stride, b_stride):
        self.size = size
        self.half = size // 2
        self.a_stride = a_stride
        self.b_stride = b_stride

    def position(self, c):
        a = (c // self.a_stride) % self.half
        b = (c // self.b_stride) % 2
        return a + b * (2 * self.half - 1 - 2 * a)

    def device(self, pos):
        pos = pos % self.size
        b = pos // self.half
        a = pos + b * (2 * self.half - 1 - 2 * pos)
        return a * self.a_stride + b * self.b_stride


def ring_of(mesh):
    size = mesh.shape["ctx"]
    devices = list(mesh.devices.reshape(-1, size)[0])
    try:
        coords = [tuple(d.coords) for d in devices]
    except AttributeError:
        coords = None
    if coords and size % 2 == 0 and size >= 4:
        for b_stride in range(1, size):
            for a_stride in range(1, size):
                ring = Ring(size, a_stride, b_stride)
                order = [ring.device(p) for p in range(size)]
                if sorted(order) != list(range(size)):
                    continue
                hops = [
                    sum(abs(x - y) for x, y in zip(coords[order[p]], coords[order[(p + 1) % size]]))
                    for p in range(size)
                ]
                if max(hops) == 1:
                    return ring
    return Ring(size, 2, 1) if size % 2 == 0 and size >= 4 else None


def _barrier(g, left, right):
    barrier = pltpu.get_barrier_semaphore()
    for other in (left, right):
        pl.semaphore_signal(barrier, 1, device_id=(g, other), device_id_type=MESH_ID)
    pl.semaphore_wait(barrier, 2)


def _gather_kernel(x_ref, y_ref, own_sem, send_sem, recv_sem, *, ring, rows, parts):
    n = ring.size
    half = rows // 2
    piece = half // parts
    g = lax.axis_index("dp")
    c = lax.axis_index("ctx")
    pos = ring.position(c)
    right = ring.device(pos + 1)
    left = ring.device(pos + n - 1)
    own = pltpu.make_async_copy(x_ref, y_ref.at[pl.ds(c * rows, rows)], own_sem)
    own.start()
    _barrier(g, left, right)

    def link(direction, step, part, origin, source):
        offset = origin * rows + direction * half + part * piece
        return pltpu.make_async_remote_copy(
            src_ref=source,
            dst_ref=y_ref.at[pl.ds(offset, piece)],
            send_sem=send_sem.at[direction, step, part],
            recv_sem=recv_sem.at[direction, step, part],
            device_id=(g, right if direction == 0 else left),
            device_id_type=MESH_ID,
        )

    sent = []
    for step in range(n - 1):
        origins = (ring.device(pos - step + n), ring.device(pos + step))
        for part in range(parts):
            for direction in (0, 1):
                origin = origins[direction]
                here_rows = y_ref.at[pl.ds(origin * rows + direction * half + part * piece, piece)]
                if step == 0:
                    source = x_ref.at[pl.ds(direction * half + part * piece, piece)]
                else:
                    link(direction, step - 1, part, origin, here_rows).wait_recv()
                    source = here_rows
                copy = link(direction, step, part, origin, source)
                copy.start()
                sent.append(copy)
    last = n - 2
    for part in range(parts):
        for direction, origin in ((0, ring.device(pos - last - 1 + n)), (1, ring.device(pos + last + 1))):
            rows_at = y_ref.at[pl.ds(origin * rows + direction * half + part * piece, piece)]
            link(direction, last, part, origin, rows_at).wait_recv()
    for copy in sent:
        copy.wait_send()
    own.wait()


def ring_all_gather(x, ring, collective_id):
    rows, cols = x.shape
    n = ring.size
    return pl.pallas_call(
        functools.partial(_gather_kernel, ring=ring, rows=rows, parts=4),
        out_shape=jax.ShapeDtypeStruct((n * rows, cols), x.dtype),
        in_specs=[pl.BlockSpec(memory_space=pl.ANY)],
        out_specs=pl.BlockSpec(memory_space=pl.ANY),
        scratch_shapes=[
            pltpu.SemaphoreType.DMA(()),
            pltpu.SemaphoreType.DMA((2, n - 1, 4)),
            pltpu.SemaphoreType.DMA((2, n - 1, 4)),
        ],
        compiler_params=pltpu.CompilerParams(collective_id=collective_id, has_side_effects=True),
    )(x)


def _scatter_kernel(p_ref, out_ref, recv_buf, send_buf, send_sem, recv_sem, *, ring, rows, parts):
    n = ring.size
    half = rows // 2
    piece = half // parts
    g = lax.axis_index("dp")
    c = lax.axis_index("ctx")
    pos = ring.position(c)
    right = ring.device(pos + 1)
    left = ring.device(pos + n - 1)
    _barrier(g, left, right)

    def link(direction, step, part):
        window = pl.ds(part * piece, piece)
        return pltpu.make_async_remote_copy(
            src_ref=send_buf.at[direction, step, window],
            dst_ref=recv_buf.at[direction, step, window],
            send_sem=send_sem.at[direction, step, part],
            recv_sem=recv_sem.at[direction, step, part],
            device_id=(g, right if direction == 0 else left),
            device_id_type=MESH_ID,
        )

    sent = []
    for step in range(n - 1):
        targets = (ring.device(pos - 1 - step + 2 * n), ring.device(pos + 1 + step))
        for part in range(parts):
            for direction in (0, 1):
                start = pl.multiple_of(
                    targets[direction] * rows + direction * half + part * piece, piece
                )
                window = pl.ds(part * piece, piece)
                total = p_ref[pl.ds(start, piece), :].astype(jnp.float32)
                if step > 0:
                    link(direction, step - 1, part).wait_recv()
                    total = total + recv_buf[direction, step - 1, window].astype(jnp.float32)
                send_buf[direction, step, window] = total.astype(send_buf.dtype)
                copy = link(direction, step, part)
                copy.start()
                sent.append(copy)
    for part in range(parts):
        for direction in (0, 1):
            link(direction, n - 2, part).wait_recv()
            start = pl.multiple_of(c * rows + direction * half + part * piece, piece)
            window = pl.ds(part * piece, piece)
            out_ref[pl.ds(direction * half + part * piece, piece), :] = (
                p_ref[pl.ds(start, piece), :].astype(jnp.float32)
                + recv_buf[direction, n - 2, window].astype(jnp.float32)
            ).astype(out_ref.dtype)
    for copy in sent:
        copy.wait_send()


def ring_reduce_scatter(p, ring, collective_id, out_dtype=jnp.float32, wire=jnp.bfloat16, parts=2):
    total_rows, cols = p.shape
    n = ring.size
    rows = total_rows // n
    half = rows // 2
    return pl.pallas_call(
        functools.partial(_scatter_kernel, ring=ring, rows=rows, parts=parts),
        out_shape=jax.ShapeDtypeStruct((rows, cols), out_dtype),
        in_specs=[pl.BlockSpec(memory_space=pltpu.VMEM)],
        out_specs=pl.BlockSpec(memory_space=pltpu.VMEM),
        scratch_shapes=[
            pltpu.VMEM((2, n - 1, half, cols), wire),
            pltpu.VMEM((2, n - 1, half, cols), wire),
            pltpu.SemaphoreType.DMA((2, n - 1, parts)),
            pltpu.SemaphoreType.DMA((2, n - 1, parts)),
        ],
        compiler_params=pltpu.CompilerParams(
            collective_id=collective_id, has_side_effects=True, vmem_limit_bytes=60 * 1024 * 1024
        ),
    )(p)


def _exchange_kernel(x_ref, out_ref, own_sem, send_sem, recv_sem, *, group):
    n = x_ref.shape[0]
    g = lax.axis_index("dp")
    c = lax.axis_index("ctx")
    n_ctx = lax.axis_size("ctx")
    me = {"all": g * n_ctx + c, "ctx": c, "dp": g}[group]

    def address(member):
        if group == "all":
            return (member // n_ctx, member % n_ctx)
        if group == "ctx":
            return (g, member)
        return (member, c)

    own = pltpu.make_async_copy(x_ref.at[me], out_ref.at[me], own_sem)
    own.start()
    barrier = pltpu.get_barrier_semaphore()
    for offset in range(1, n):
        pl.semaphore_signal(
            barrier, 1, device_id=address((me + offset) % n), device_id_type=MESH_ID
        )
    pl.semaphore_wait(barrier, n - 1)

    def link(offset, source, target):
        return pltpu.make_async_remote_copy(
            src_ref=x_ref.at[target],
            dst_ref=out_ref.at[source],
            send_sem=send_sem.at[offset],
            recv_sem=recv_sem.at[offset],
            device_id=address(target),
            device_id_type=MESH_ID,
        )

    sent = []
    for offset in range(1, n):
        copy = link(offset, me, (me + offset) % n)
        copy.start()
        sent.append(copy)
    for offset in range(1, n):
        link(offset, (me + n - offset) % n, me).wait_recv()
    for copy in sent:
        copy.wait_send()
    own.wait()


def exchange(x, group, collective_id):
    n = x.shape[0]
    space = pltpu.VMEM
    return pl.pallas_call(
        functools.partial(_exchange_kernel, group=group),
        out_shape=jax.ShapeDtypeStruct(x.shape, x.dtype),
        in_specs=[pl.BlockSpec(memory_space=space)],
        out_specs=pl.BlockSpec(memory_space=space),
        scratch_shapes=[
            pltpu.SemaphoreType.DMA(()),
            pltpu.SemaphoreType.DMA((n,)),
            pltpu.SemaphoreType.DMA((n,)),
        ],
        compiler_params=pltpu.CompilerParams(collective_id=collective_id, has_side_effects=True),
    )(x)


def block_moves(n_dp, n_ctx):
    count = n_dp * n_ctx
    return [(f, (f % n_dp) * n_ctx + f // n_dp) for f in range(count)]


def fetch_out_rows(w_out):
    n_dp = lax.axis_size("dp")
    n_ctx = lax.axis_size("ctx")
    moved = lax.ppermute(w_out.astype(jnp.bfloat16), ("dp", "ctx"), perm=block_moves(n_dp, n_ctx))
    return lax.all_gather(moved, "dp", axis=0, tiled=True)


def return_out_rows(grad_out_rows):
    n_dp = lax.axis_size("dp")
    n_ctx = lax.axis_size("ctx")
    part = lax.psum_scatter(grad_out_rows, "dp", scatter_dimension=0, tiled=True)
    back = [(b, a) for a, b in block_moves(n_dp, n_ctx)]
    return lax.ppermute(part, ("dp", "ctx"), perm=back)


def pack_rows(vector, lanes):
    size = vector.shape[0]
    total = -(-size // (16 * lanes)) * 16 * lanes
    return jnp.pad(vector, (0, total - size)).reshape(-1, lanes)


def fetch_small(b_qkv, b_out, b_fc2, ln_gain, ln_shift, b_fc1):
    pieces = (b_qkv, b_out, b_fc2, ln_gain, ln_shift, b_fc1)
    n_dp = lax.axis_size("dp")
    n_ctx = lax.axis_size("ctx")
    packed = pack_rows(jnp.concatenate([p.astype(jnp.bfloat16) for p in pieces]), 128)
    over_dp = exchange(jnp.broadcast_to(packed[None], (n_dp,) + packed.shape), "dp", 4)
    over_all = exchange(jnp.broadcast_to(over_dp[None], (n_ctx,) + over_dp.shape), "ctx", 8)
    table = over_all.transpose(1, 0, 2, 3).reshape(n_dp * n_ctx, -1)
    result = []
    offset = 0
    for p in pieces:
        result.append(table[:, offset : offset + p.shape[0]])
        offset += p.shape[0]
    return result


def reduce_small(small):
    n_dp = lax.axis_size("dp")
    n_ctx = lax.axis_size("ctx")
    count, width = small.shape
    packed = jax.vmap(lambda row: pack_rows(row, 128))(small)
    packed = packed.reshape((n_dp, n_ctx) + packed.shape[1:]).transpose(1, 0, 2, 3)
    over_ctx = jnp.sum(exchange(packed, "ctx", 7), axis=0)
    over_dp = jnp.sum(exchange(over_ctx, "dp", 9), axis=0)
    return over_dp.reshape(-1)[:width]


def fetch_heads(w_qkv, w_fc1, w_fc2, tokens):
    dp_count = lax.axis_size("dp")
    ctx_count = lax.axis_size("ctx")
    rows_piece = w_qkv.shape[0]
    head_width = D // ctx_count
    unit = FF // (dp_count * ctx_count)
    qkv_piece = w_qkv.astype(jnp.bfloat16).reshape(rows_piece, 3, ctx_count, head_width)
    fc1_piece = w_fc1.astype(jnp.bfloat16).reshape(rows_piece, dp_count, ctx_count, unit)
    pieces = jnp.concatenate(
        [
            qkv_piece.transpose(2, 0, 1, 3).reshape(ctx_count, rows_piece, 3 * head_width),
            fc1_piece.transpose(2, 0, 1, 3).reshape(ctx_count, rows_piece, dp_count * unit),
        ],
        axis=2,
    )
    sent = exchange(pieces, "ctx", 5).reshape(ctx_count * rows_piece, -1)
    sent, tokens = lax.optimization_barrier((sent, tokens))
    cols, fc2_rows = (
        lax.all_gather(sent, "dp", axis=0, tiled=True),
        lax.all_gather(w_fc2.astype(jnp.bfloat16), "dp", axis=0, tiled=True),
    )
    return (cols, fc2_rows, tokens)


def return_heads(owned_parts):
    dp_count = lax.axis_size("dp")
    ctx_count = lax.axis_size("ctx")
    head_width = D // ctx_count
    unit = FF // (dp_count * ctx_count)
    rows_piece = owned_parts.shape[0] // ctx_count
    got = exchange(owned_parts.reshape(ctx_count, rows_piece, -1), "ctx", 6)
    qkv = got[:, :, : 3 * head_width].reshape(ctx_count, rows_piece, 3, head_width)
    fc1 = got[:, :, 3 * head_width :].reshape(ctx_count, rows_piece, dp_count, unit)
    return (
        qkv.transpose(1, 2, 0, 3).reshape(rows_piece, 3 * D).astype(jnp.float32),
        fc1.transpose(1, 2, 0, 3).reshape(rows_piece, FF).astype(jnp.float32),
    )


def head_plan(
    ring,
    tokens,
    lengths,
    w_qkv,
    b_qkv,
    w_out,
    b_out,
    w_fc1,
    b_fc1,
    w_fc2,
    b_fc2,
    ln_gain,
    ln_shift,
    cotangent,
):
    rows_here = tokens.shape[0]
    rows_piece = w_qkv.shape[0]
    dp_count = lax.axis_size("dp")
    ctx_count = lax.axis_size("ctx")
    count = dp_count * ctx_count
    group = rows_here * ctx_count
    head_width = D // ctx_count
    local_heads = HEADS // ctx_count
    unit = FF // (dp_count * ctx_count)
    here = lax.axis_index("ctx")
    group_rows = jnp.arange(group, dtype=jnp.int32)
    seg, positions = segment_info(lengths[0], group_rows)
    cosine, sine = rotary_tables(positions)
    qkv_bias, out_bias, fc2_bias, gain_low, shift_low, fc1_table = fetch_small(
        b_qkv, b_out, b_fc2, ln_gain, ln_shift, b_fc1
    )
    qkv_bias = qkv_bias.reshape(3 * D)
    out_bias = out_bias.reshape(D)
    fc2_bias = fc2_bias.reshape(D)
    gain_low = gain_low.reshape(D)
    shift_low = shift_low.reshape(D)
    fc1_bias = lax.dynamic_index_in_dim(
        fc1_table.reshape(dp_count, ctx_count, unit), here, 1, keepdims=False
    ).reshape(dp_count * unit)
    out_rows = fetch_out_rows(w_out)
    cols, fc2_rows, tokens = fetch_heads(w_qkv, w_fc1, w_fc2, tokens)
    gain32 = gain_low.astype(jnp.float32)
    shift32 = shift_low.astype(jnp.float32)
    inputs = tokens.astype(jnp.float32)
    normed, scaled, _ = norm_parts(inputs, gain32, shift32)
    tokens_group = ring_all_gather(tokens, ring, 0)
    late_dy, tokens_group = lax.optimization_barrier((cotangent, tokens_group))
    dy_group = lax.all_gather(late_dy, "ctx", axis=0, tiled=True)
    hidden_group = norm_parts(tokens_group.astype(jnp.float32), gain32, shift32)[2].astype(
        jnp.bfloat16
    )
    bias_cols = lax.dynamic_slice_in_dim(
        qkv_bias.reshape(3, D), here * head_width, head_width, 1
    ).reshape(3 * head_width)
    both = jnp.dot(hidden_group, cols, preferred_element_type=jnp.float32) + jnp.concatenate(
        [bias_cols, fc1_bias]
    ).astype(jnp.float32)
    qkv = both[:, : 3 * head_width]
    pre = both[:, 3 * head_width :]
    shape = (group, local_heads, HEAD_DIM)
    query = rotate(qkv[:, :head_width].reshape(shape), cosine, sine).astype(jnp.bfloat16)
    keys = rotate(qkv[:, head_width : 2 * head_width].reshape(shape), cosine, sine).astype(
        jnp.bfloat16
    )
    values = qkv[:, 2 * head_width :].reshape(shape).astype(jnp.bfloat16)
    q_heads = query.transpose(1, 0, 2)
    k_heads = keys.transpose(1, 0, 2)
    v_heads = values.transpose(1, 0, 2)
    attended_heads, log_total = attention_forward(q_heads, k_heads, v_heads, seg)
    attended = attended_heads.transpose(1, 0, 2).reshape(group, head_width).astype(jnp.bfloat16)
    act = gelu_tanh(pre).astype(jnp.bfloat16)
    branches = ring_reduce_scatter(
        jnp.dot(attended, out_rows, preferred_element_type=jnp.float32)
        + jnp.dot(act, fc2_rows, preferred_element_type=jnp.float32),
        ring,
        2,
    )
    block_out = (
        inputs + branches + out_bias.astype(jnp.float32) + fc2_bias.astype(jnp.float32)
    ).astype(jnp.bfloat16)
    grad_out32 = cotangent.astype(jnp.float32)
    grad_b_fc2 = jnp.sum(grad_out32, axis=0)
    grad_fc2_part = jnp.einsum("tf,td->fd", act, dy_group, preferred_element_type=jnp.float32)
    d_act = jnp.einsum("td,fd->tf", dy_group, fc2_rows, preferred_element_type=jnp.float32)
    d_pre = (d_act * gelu_slope(pre)).astype(jnp.bfloat16)
    grad_bfc1_part = jnp.sum(d_pre.astype(jnp.float32), axis=0)
    grad_out_rows = jnp.einsum("tc,td->cd", attended, dy_group, preferred_element_type=jnp.float32)
    owned_w_out = return_out_rows(grad_out_rows)
    d_attended = (
        jnp.einsum("td,cd->tc", dy_group, out_rows, preferred_element_type=jnp.float32)
        .astype(jnp.bfloat16)
        .reshape(shape)
    )
    d_heads = d_attended.transpose(1, 0, 2)
    delta = jnp.sum(d_heads.astype(jnp.float32) * attended_heads, axis=2, keepdims=True)
    dq_heads, dk_heads, dv_heads = attention_backward(
        q_heads, k_heads, v_heads, d_heads, log_total, delta, seg
    )
    d_query = dq_heads.transpose(1, 0, 2)
    d_keys = dk_heads.transpose(1, 0, 2)
    d_values = dv_heads.transpose(1, 0, 2)
    d_query = rotate_back(d_query, cosine, sine).reshape(group, head_width)
    d_keys = rotate_back(d_keys, cosine, sine).reshape(group, head_width)
    d_qkv = jnp.concatenate([d_query, d_keys, d_values.reshape(group, head_width)], axis=1).astype(
        jnp.bfloat16
    )
    d_both = jnp.concatenate([d_qkv, d_pre], axis=1)
    bias_part = jnp.sum(d_qkv.astype(jnp.float32), axis=0).reshape(3, head_width)
    d_hidden = ring_reduce_scatter(
        jnp.einsum("tc,dc->td", d_both, cols, preferred_element_type=jnp.float32), ring, 3
    )
    weight_parts = jnp.einsum(
        "td,tc->dc", hidden_group, d_both, preferred_element_type=jnp.float32
    ).astype(jnp.bfloat16)
    owned_parts = lax.psum_scatter(weight_parts, "dp", scatter_dimension=0, tiled=True)
    split_qkv, split_fc1 = return_heads(owned_parts)
    d_hidden, split_qkv, split_fc1 = lax.optimization_barrier((d_hidden, split_qkv, split_fc1))
    grad_gain, grad_shift, d_inputs = norm_back(d_hidden, normed, scaled, gain32)
    grad_tokens = (grad_out32 + d_inputs).astype(jnp.bfloat16)
    owned_fc2 = lax.psum_scatter(
        grad_fc2_part.astype(jnp.bfloat16), "dp", scatter_dimension=0, tiled=True
    ).astype(jnp.float32)
    full_bqkv = lax.dynamic_update_slice_in_dim(
        jnp.zeros((3, D), jnp.float32), bias_part, here * head_width, 1
    )
    full_bfc1 = lax.dynamic_update_slice_in_dim(
        jnp.zeros((dp_count, ctx_count, unit), jnp.float32),
        grad_bfc1_part.reshape(dp_count, 1, unit),
        here,
        1,
    )
    small = jnp.concatenate(
        [
            full_bqkv.reshape(count, -1),
            grad_b_fc2.reshape(count, -1),
            grad_gain.reshape(count, -1),
            grad_shift.reshape(count, -1),
            full_bfc1.reshape(count, -1),
        ],
        axis=1,
    )
    owned_small = reduce_small(small)
    cuts = [0, 3 * D // count, D // count, D // count, D // count, FF // count]
    bounds = [sum(cuts[: i + 1]) for i in range(len(cuts))]
    owned_bqkv, owned_bout, owned_gain, owned_shift, owned_bfc1 = [
        owned_small[bounds[i] : bounds[i + 1]] for i in range(5)
    ]
    return (
        block_out,
        grad_tokens,
        split_qkv.reshape(rows_piece, 3 * D),
        owned_bqkv,
        owned_w_out,
        owned_bout,
        split_fc1.reshape(rows_piece, FF),
        owned_bfc1,
        owned_fc2,
        owned_bout,
        owned_gain,
        owned_shift,
    )


def body(
    ring,
    tokens,
    lengths,
    w_qkv,
    b_qkv,
    w_out,
    b_out,
    w_fc1,
    b_fc1,
    w_fc2,
    b_fc2,
    ln_gain,
    ln_shift,
    cotangent,
):
    return head_plan(
        ring,
        tokens,
        lengths,
        w_qkv,
        b_qkv,
        w_out,
        b_out,
        w_fc1,
        b_fc1,
        w_fc2,
        b_fc2,
        ln_gain,
        ln_shift,
        cotangent,
    )


def solution(mesh):
    in_specs = (
        P(("dp", "ctx"), None),
        P("dp", None),
        P(("dp", "ctx"), None),
        P(("dp", "ctx")),
        P(("dp", "ctx"), None),
        P(("dp", "ctx")),
        P(("dp", "ctx"), None),
        P(("dp", "ctx")),
        P(("dp", "ctx"), None),
        P(("dp", "ctx")),
        P(("dp", "ctx")),
        P(("dp", "ctx")),
        P(("dp", "ctx"), None),
    )
    out_specs = (
        P(("dp", "ctx"), None),
        P(("dp", "ctx"), None),
        P(("dp", "ctx"), None),
        P(("dp", "ctx")),
        P(("dp", "ctx"), None),
        P(("dp", "ctx")),
        P(("dp", "ctx"), None),
        P(("dp", "ctx")),
        P(("dp", "ctx"), None),
        P(("dp", "ctx")),
        P(("dp", "ctx")),
        P(("dp", "ctx")),
    )
    ring = ring_of(mesh)
    return jax.shard_map(functools.partial(body, ring), mesh=mesh, in_specs=in_specs, out_specs=out_specs, check_vma=False)
```
